32 devices in a mesh: dp: 16 (over z, y, core), tensor: 2 (over x).
Axes of the slice: x: 2, y: 2, z: 4, core: 2. Of those that a mesh axis runs over, the one named last changes fastest.
Arguments:
- tokens_in: bfloat16 [2, 4096, 768], P(None, ('dp', 'tensor')), may hold values from -6 to 6
- positions: int32 [3, 2, 4096], P(None, None, ('dp', 'tensor')), may hold values from 0 to 15
- segment_ids: int32 [2, 16, 256], P(None, 'dp'), may hold values from 0 to 2, never falling along the last dimension, each value on 1 to 128 neighbouring positions
- owners: int32 [10368, 1], replicated, may hold values from 0 to 15; in each aligned block of 10368 rows (0 to 10367, 10368 to 20735, ...) at most 1296 rows name the same one
- master: float32 [20736, 1024], P('dp', 'tensor'), may hold values from -0.21875 to 0.21875
- first_moment: float32 [20736, 1024], P('dp', 'tensor'), may hold values from -112 to 112
- second_moment: float32 [20736, 1024], P('dp', 'tensor'), may hold values from 81.92 to 1638.4
- norm_gains: float32 [2, 1280], replicated, may hold values from 0.5 to 1.5
- norm_biases: float32 [2, 1280], replicated, may hold values from -4 to 4
- norm_first: float32 [4, 1280], replicated, may hold values from -256 to 256
- norm_second: float32 [4, 1280], replicated, may hold values from 2048 to 8192
- cotangent: float32 [2, 4096, 512], P(None, ('dp', 'tensor')), may hold values from -6 to 6
Outputs:
- decoded: float32 [2, 4096, 512], P(None, ('dp', 'tensor'))
- tokens_grad: float32 [2, 4096, 768], P(None, ('dp', 'tensor'))
- new_master: float32 [20736, 1024], P('dp', 'tensor')
- new_first: float32 [20736, 1024], P('dp', 'tensor')
- new_second: float32 [20736, 1024], P('dp', 'tensor')
- new_norms: float32 [4, 1280], replicated
- new_norm_first: float32 [4, 1280], replicated
- new_norm_second: float32 [4, 1280], replicated
The draws below stay inside these ranges and needn't reach their ends.
Inputs may be any that keep to these rules, and one draw needn't show every extreme that they name: `owners`: every dp index owns at most 1296 blocks, and some index owns exactly 1296. `segment_ids`: along each sequence the tile ids never fall; each tile has 1 to 128 tokens, and some tile has exactly 128.
All inputs are finite; a program needn't handle non-finite values.
Results may differ from the reference program's by a relative error of at most 0.024.
Values may be sent and summed in bfloat16 or wider, within the bound.
A program may use at most 192 MiB of HBM per device.

```python
import math
from functools import reduce
import jax
import jax.numpy as jnp
import numpy as np
from jax import lax

DE = 768
HE = 12
HDE = 64
FFE = 3072
DD = 512
HD = 16
HDD = 32
FFD = 2048
SEQ = 256
MICRO = 2
SEGS = 3
UNIT = 512
STEP = 10
TOKENS = 8192
NUNIT = 10368
CAP = 1296
N_DP = 16
N_TENSOR = 2


def set_ends(result, own_key, least, top_value):
    dims = result.shape
    place = [jax.random.randint(jax.random.fold_in(own_key, axis), (), 0, dims[axis]) for axis in range(len(dims))]
    result = result.at[tuple(place)].set(least)
    longest = dims.index(max(dims))
    place[longest] = (place[longest] + 1) % dims[longest]
    return result.at[tuple(place)].set(top_value)


def level_of(stream_key, dims, split, smallest, high):
    factor_of = 1.0
    for axis_at, parts in split:
        steps = jax.random.uniform(jax.random.fold_in(jax.random.fold_in(stream_key, 6), axis_at), (parts,), jnp.float32, smallest / len(split), high / len(split))
        factor_of = factor_of * jnp.repeat(jnp.exp(steps), dims[axis_at] // parts).reshape((-1,) + (1,) * (len(dims) - 1 - axis_at))
    return factor_of


def profile(amount, total, limit, skew):
    portions = [(1 << 20) // math.isqrt(rank ** skew) + 1 for rank in range(2, amount + 1)]
    surplus, holding = total - limit - (amount - 1), [1] * (amount - 1)
    while surplus > 0:
        candidates = [i for i in range(amount - 1) if holding[i] < limit]
        pool, left = sum([portions[i] for i in candidates]), surplus
        for i in candidates:
            extra = min(limit - holding[i], max(1, left * portions[i] // pool), surplus)
            holding[i] = holding[i] + extra
            surplus = surplus - extra
    return np.array([limit] + holding)


def uneven_parts(key, count, total, reach, slope):
    if count == 2:
        one = jax.random.randint(key, (), max(1, total - reach), min(reach, total - 1) + 1)
        return jnp.stack([one, total - one])
    lengths = jnp.asarray(profile(count, total, reach, slope), jnp.int32)
    couples = (count - 1) // 2
    source_of, taker = lengths[1:1 + 2 * couples:2], lengths[2:2 + 2 * couples:2]
    slack = jnp.minimum(source_of - 1, reach - taker)
    shifted = jax.random.randint(jax.random.fold_in(key, 1), (couples,), 0, 1 << 20) % (slack + 1)
    lengths = lengths.at[1:1 + 2 * couples:2].set(source_of - shifted).at[2:2 + 2 * couples:2].set(taker + shifted)
    return lengths[jax.random.permutation(jax.random.fold_in(key, 2), count)]


def assign_block(own_key, own, number, rows, count, top, reach, skew):
    order = jax.random.permutation(own_key, count)
    crowded, ordinary = portions_of(count, rows * top, reach, skew, True), portions_of(count, rows * top, reach, skew, False)
    places = jnp.arange(count)

    def named(lengths, rotation):
        used = int((lengths > 0).sum())
        fixed = max(1, used // 4)
        shifted = fixed + (places - fixed + rotation * (used - fixed)) % max(1, count - fixed)
        return jnp.zeros((count,), jnp.int32).at[order[jnp.where(places < fixed, places, shifted)]].set(jnp.asarray(lengths, jnp.int32))

    lengths = jnp.where(number % 4 == 0, named(crowded, number // 4), named(ordinary, number - number // 4 - 1))
    mixed = jax.random.permutation(jax.random.fold_in(own, 3), count)
    donor, sink = mixed[0:count // 2 * 2:2], mixed[1:count // 2 * 2:2]
    room = jnp.minimum(lengths[donor] - 1, reach - lengths[sink]) // 2
    room = jnp.where((donor == order[0]) | (sink == order[0]) | (lengths[sink] == 0), 0, jnp.maximum(room, 0))
    shifted = jax.random.randint(jax.random.fold_in(own, 4), (count // 2,), 0, 1 << 20) % (room + 1)
    lengths = lengths.at[donor].add(-shifted).at[sink].add(shifted)
    members = jnp.searchsorted(jnp.cumsum(lengths), jnp.arange(rows * top), side="right").astype(jnp.int32)
    table = members.reshape(top, rows).T
    table = table[jax.random.permutation(jax.random.fold_in(own, 1), rows)]
    rotation = jax.random.randint(jax.random.fold_in(own, 2), (rows, 1), 0, top)
    return jnp.take_along_axis(table, (jnp.arange(top)[None, :] + rotation) % top, axis=1)


def portions_of(number_of, total, reach, slope, full):
    loads = [(1 << 20) // math.isqrt(standing ** slope) + 1 for standing in range(1, number_of + 1)]
    largest = reach if full else min(reach, max(-(-total // number_of), total * loads[0] // sum(loads)))
    least = 1 if total - largest >= number_of - 1 else 0
    given, rest = [largest] + [least] * (number_of - 1), total - largest - least * (number_of - 1)
    while rest > 0:
        free = [i for i in range(1, number_of) if given[i] < largest] or [i for i in range(1, number_of) if given[i] < reach]
        mass, budget = sum([loads[i] for i in free]), rest
        for i in free:
            extra = min(reach - given[i], max(1, budget * loads[i] // mass), rest)
            given[i] = given[i] + extra
            rest = rest - extra
    return np.array(given)


def gaussian(own_key, extent, scale, reach, cuts=(), kind=jnp.bfloat16):
    array = jax.random.normal(own_key, extent, jnp.float32) * scale
    if len(cuts) > 0:
        array = level_of(own_key, extent, cuts, -0.22, 0.18) * array
    return jnp.clip(array, min=-reach, max=reach).astype(kind)


def setup_inputs(seed: int = 0) -> dict:
    key_of = jax.random.split(jax.random.key(seed), 13)
    tokens_in = gaussian(key_of[0], (MICRO, N_DP * SEQ, DE), 1.0, 6.0, ((1, 32),))
    positions = set_ends(jax.random.randint(key_of[1], (3, MICRO, N_DP * SEQ), 0, 16), jax.random.fold_in(key_of[1], 1), 0, 15).astype(jnp.int32)
    segment_ids = jax.vmap(lambda own: jnp.searchsorted(jnp.cumsum(uneven_parts(own, SEGS, SEQ, SEQ // 2, 2)), jnp.arange(SEQ), side="right"))(jax.random.split(key_of[2], MICRO * N_DP)).reshape((MICRO, N_DP, SEQ)).astype(jnp.int32)
    owners_keys = jax.random.split(jax.random.fold_in(key_of[3], 1), NUNIT // NUNIT)
    owners_turns = jax.random.permutation(jax.random.fold_in(key_of[3], 3), NUNIT // NUNIT)
    owners = jax.vmap(lambda own, number: assign_block(jax.random.fold_in(key_of[3], 2), own, number, NUNIT, N_DP, 1, CAP, 2))(owners_keys, owners_turns).reshape((NUNIT, 1))
    master = gaussian(key_of[4], (N_DP * CAP, N_TENSOR * UNIT), DE ** -0.5, 0.21875, ((0, 16), (1, 2)), jnp.float32)
    first_moment = gaussian(key_of[5], (N_DP * CAP, N_TENSOR * UNIT), (0.2 * TOKENS ** 0.5), 112.0, ((0, 16), (1, 2)), jnp.float32)
    second_moment = jnp.clip(jnp.exp(math.log(1638.4) - 2.9957323 * jax.random.uniform(key_of[6], (N_DP * CAP, N_TENSOR * UNIT), jnp.float32) ** level_of(key_of[6], (N_DP * CAP, N_TENSOR * UNIT), ((0, 16), (1, 2)), -0.2, 0.2)), 81.92, 1638.4)
    norm_gains = jnp.clip(1.0 + 0.1 * jax.random.normal(key_of[7], (2, DE + DD), jnp.float32), 0.5, 1.5)
    norm_biases = gaussian(key_of[8], (2, DE + DD), 0.3, 4.0, (), jnp.float32)
    norm_first = gaussian(key_of[9], (4, DE + DD), (0.5 * TOKENS ** 0.5), 256.0, (), jnp.float32)
    norm_second = jnp.clip(jnp.exp(jax.random.uniform(key_of[10], (4, DE + DD), jnp.float32, math.log(2048.0), math.log(8192.0))), 2048.0, 8192.0)
    cotangent = gaussian(key_of[11], (MICRO, N_DP * SEQ, DD), 1.0, 6.0, ((1, 32),), jnp.float32)
    return {"tokens_in": tokens_in, "positions": positions, "segment_ids": segment_ids, "owners": owners, "master": master, "first_moment": first_moment, "second_moment": second_moment, "norm_gains": norm_gains, "norm_biases": norm_biases, "norm_first": norm_first, "norm_second": norm_second, "cotangent": cotangent}


@jax.custom_vjp
def low(v):
    return lax.optimization_barrier(v.astype(jnp.bfloat16)).astype(jnp.float32)

@jax.custom_vjp
def low_back(v):
    return v

def low_keep(v):
    return (low(v), None)

def low_pass(kept, grad):
    return (grad,)

def back_keep(v):
    return (v, None)

def back_low(kept, grad):
    return (low(grad),)
low.defvjp(low_keep, low_pass)
low_back.defvjp(back_keep, back_low)
NORM_EPS = 1e-06
BETA_ONE = 0.5
BETA_TWO = 0.5
LEARN_RATE = 0.03
NORM_RATE = 0.3
WEIGHT_DECAY = 0.05
ADAM_EPS = 1e-08
MASK_FILL = -1000000000.0
HIGHEST = lax.Precision.HIGHEST

def sincos_part(coordinate, part_width):
    halfway = part_width // 2
    frequency = 1.0 / 10000.0 ** (jnp.arange(halfway, dtype=jnp.float32) / halfway)
    angles = coordinate.astype(jnp.float32)[:, None] * frequency[None, :]
    return jnp.concatenate([jnp.sin(angles), jnp.cos(angles)], axis=1)

def sincos_embed(positions, model_width):
    side_width = model_width // 16 * 6
    first_width = model_width - 2 * side_width
    return jnp.concatenate([sincos_part(positions[0], first_width), sincos_part(positions[1], side_width), sincos_part(positions[2], side_width)], axis=1)

def layer_norm(values, gain_row, bias_row):
    center = values - lax.optimization_barrier(jnp.mean(values, axis=-1, keepdims=True))
    spread = lax.optimization_barrier(jnp.mean(center * center, axis=-1, keepdims=True))
    return center * lax.rsqrt(spread + NORM_EPS) * gain_row + bias_row

def slot_table(owners, devices, capacity):
    owner_ids = owners[:, 0]
    onehot = (owner_ids[:, None] == jnp.arange(devices, dtype=jnp.int32)[None, :]).astype(jnp.int32)
    before = jnp.cumsum(onehot, axis=0) - onehot
    owner_rank = lax.optimization_barrier(jnp.sum(before * onehot, axis=1))
    return (owner_ids * capacity + owner_rank).astype(jnp.int32)

def weight_shapes(tensor_count):
    enc_heads = HE // tensor_count
    dec_heads = HD // tensor_count
    return [(DE, 3 * enc_heads * HDE), (enc_heads * HDE, DE), (DE, FFE // tensor_count), (FFE // tensor_count, DE), (DE, DD // tensor_count), (DD, 3 * dec_heads * HDD), (dec_heads * HDD, DD), (DD, FFD // tensor_count), (FFD // tensor_count, DD)]

def split_flat(flat_vector, shapes):
    pieces = []
    offset = 0
    for matrix_shape in shapes:
        length = matrix_shape[0] * matrix_shape[1]
        pieces.append(flat_vector[offset:offset + length].reshape(matrix_shape))
        offset += length
    return pieces

def adamw(weights, gradient, moment_one, moment_two, decay_rate, step_rate):
    one_new = BETA_ONE * moment_one + (1.0 - BETA_ONE) * gradient
    two_new = BETA_TWO * moment_two + (1.0 - BETA_TWO) * gradient * gradient
    one_hat = one_new / (1.0 - BETA_ONE ** STEP)
    two_hat = two_new / (1.0 - BETA_TWO ** STEP)
    weights_new = weights - step_rate * (one_hat / (jnp.sqrt(two_hat) + ADAM_EPS) + decay_rate * weights)
    return (weights_new, one_new, two_new)

def attention_half(normed, w_qkv, w_out, head_count, head_size, same_tile):
    length = normed.shape[0]
    projected = jnp.dot(normed, w_qkv, precision=HIGHEST, preferred_element_type=jnp.float32)
    projected = low(low_back(projected)).reshape(length, 3, head_count, head_size)
    queries = projected[:, 0]
    key_rows = projected[:, 1]
    value_rows = projected[:, 2]
    scores = jnp.einsum('qhd,khd->hqk', queries, key_rows, precision=HIGHEST) * head_size ** (-0.5)
    scores = low_back(scores + jnp.where(same_tile, 0.0, MASK_FILL)[None])
    weights = jax.nn.softmax(scores, axis=-1)
    attended = jnp.einsum('hqk,khd->qhd', low(weights), value_rows, precision=HIGHEST)
    attended = low(low_back(attended.reshape(length, head_count * head_size)))
    return low(jnp.dot(attended, w_out, precision=HIGHEST, preferred_element_type=jnp.float32))

def feed_half(normed, w_in, w_down):
    hidden = low_back(jnp.dot(normed, w_in, precision=HIGHEST, preferred_element_type=jnp.float32))
    active = low(jax.nn.gelu(hidden, approximate=False))
    return low(jnp.dot(active, w_down, precision=HIGHEST, preferred_element_type=jnp.float32))

def residual_block(residual, halves, gain_rows, bias_rows, head_count, head_size, same_tile):
    normed = low(layer_norm(residual, gain_rows[0], bias_rows[0]))
    branch = reduce(jnp.add, [attention_half(normed, tensor_half[0], tensor_half[1], head_count, head_size, same_tile) for tensor_half in halves])
    residual = residual + low_back(branch)
    normed_two = low(layer_norm(residual, gain_rows[1], bias_rows[1]))
    branch_two = reduce(jnp.add, [feed_half(normed_two, tensor_half[2], tensor_half[3]) for tensor_half in halves])
    return residual + low_back(branch_two)

def sequence_forward(tokens, positions, segments, enc_halves, embed_halves, dec_halves, gain_rows, bias_rows):
    same_tile = segments[:, None] == segments[None, :]
    residual = tokens + sincos_embed(positions, DE)
    residual = residual_block(residual, enc_halves, gain_rows[:, :DE], bias_rows[:, :DE], HE // N_TENSOR, HDE, same_tile)
    residual_low = low(residual)
    columns = [low(low_back(jnp.dot(residual_low, w_embed, precision=HIGHEST, preferred_element_type=jnp.float32))) for w_embed in embed_halves]
    residual = jnp.concatenate(columns, axis=1) + sincos_embed(positions, DD)
    return residual_block(residual, dec_halves, gain_rows[:, DE:], bias_rows[:, DE:], HD // N_TENSOR, HDD, same_tile)

def full_forward(tokens, master, gain_rows, bias_rows, positions, segments, slot_index):
    copies = low(master)
    halves = []
    for tensor_pos in range(N_TENSOR):
        flat_vector = jnp.take(copies[:, tensor_pos * UNIT:(tensor_pos + 1) * UNIT], slot_index, axis=0).reshape(-1)
        halves.append(split_flat(flat_vector, weight_shapes(N_TENSOR)))
    enc_halves = [matrices[0:4] for matrices in halves]
    embed_halves = [matrices[4] for matrices in halves]
    dec_halves = [matrices[5:9] for matrices in halves]

    def one_sequence(inputs):
        seq_tokens, seq_positions, seq_segments = inputs
        return sequence_forward(seq_tokens, seq_positions, seq_segments, enc_halves, embed_halves, dec_halves, gain_rows, bias_rows)
    return lax.map(jax.checkpoint(one_sequence), (tokens, positions, segments))

def reference(tokens_in, positions, segment_ids, owners, master, first_moment, second_moment, norm_gains, norm_biases, norm_first, norm_second, cotangent):
    slot_index = slot_table(owners, N_DP, CAP)
    sequences = MICRO * N_DP
    seq_tokens = tokens_in.astype(jnp.float32).reshape(sequences, SEQ, DE)
    seq_positions = positions.reshape(3, sequences, SEQ).transpose(1, 0, 2)
    seq_segments = segment_ids.reshape(sequences, SEQ)

    def forward(tokens, weights, gain_rows, bias_rows):
        return full_forward(tokens, weights, gain_rows, bias_rows, seq_positions, seq_segments, slot_index)
    decoded, pullback = jax.vjp(forward, seq_tokens, master, norm_gains, norm_biases)
    token_grad, master_grad, gain_grad, bias_grad = pullback(cotangent.reshape(sequences, SEQ, DD))
    new_master, new_first, new_second = adamw(master, master_grad, first_moment, second_moment, WEIGHT_DECAY, LEARN_RATE)
    norm_params = jnp.concatenate([norm_gains, norm_biases], axis=0)
    norm_grad = jnp.concatenate([gain_grad, bias_grad], axis=0)
    new_norms, norm_one_new, norm_two_new = adamw(norm_params, norm_grad, norm_first, norm_second, 0.0, NORM_RATE)
    return (decoded.reshape(MICRO, N_DP * SEQ, DD), token_grad.reshape(MICRO, N_DP * SEQ, DE), new_master, new_first, new_second, new_norms, norm_one_new, norm_two_new)
```

```python
from functools import partial

import jax
import jax.numpy as jnp
from jax import lax
from jax.experimental import pallas as pl
from jax.experimental.pallas import tpu as pltpu
from jax.sharding import PartitionSpec as P

DE = 768
HE = 12
HDE = 64
FFE = 3072
DD = 512
HD = 16
HDD = 32
FFD = 2048
STEP = 10


NORM_EPS = 1e-06
BETA_ONE = 0.5
BETA_TWO = 0.5
LEARN_RATE = 0.03
NORM_RATE = 0.3
WEIGHT_DECAY = 0.05
ADAM_EPS = 1e-08
MASK_FILL = -1000000000.0


def sincos_part(coordinate, part_width):
    halfway = part_width // 2
    frequency = 1.0 / 10000.0 ** (jnp.arange(halfway, dtype=jnp.float32) / halfway)
    angles = coordinate.astype(jnp.float32)[:, None] * frequency[None, :]
    return jnp.concatenate([jnp.sin(angles), jnp.cos(angles)], axis=1)


def sincos_embed(positions, model_width):
    side_width = model_width // 16 * 6
    first_width = model_width - 2 * side_width
    return jnp.concatenate(
        [
            sincos_part(positions[0], first_width),
            sincos_part(positions[1], side_width),
            sincos_part(positions[2], side_width),
        ],
        axis=1,
    )


def slot_table(owners, devices, capacity):
    owner_ids = owners[:, 0]
    onehot = (owner_ids[:, None] == jnp.arange(devices, dtype=jnp.int32)[None, :]).astype(jnp.int32)
    before = jnp.cumsum(onehot, axis=0) - onehot
    owner_rank = jnp.sum(before * onehot, axis=1)
    return owner_ids * capacity + owner_rank


def weight_shapes(tensor_count):
    enc_heads = HE // tensor_count
    dec_heads = HD // tensor_count
    return [
        (DE, 3 * enc_heads * HDE),
        (enc_heads * HDE, DE),
        (DE, FFE // tensor_count),
        (FFE // tensor_count, DE),
        (DE, DD // tensor_count),
        (DD, 3 * dec_heads * HDD),
        (dec_heads * HDD, DD),
        (DD, FFD // tensor_count),
        (FFD // tensor_count, DD),
    ]


def split_flat(flat_vector, shapes):
    pieces = []
    offset = 0
    for matrix_shape in shapes:
        length = matrix_shape[0] * matrix_shape[1]
        pieces.append(flat_vector[offset : offset + length].reshape(matrix_shape))
        offset += length
    return pieces


def adamw(weights, gradient, moment_one, moment_two, decay_rate, step_rate):
    one_new = BETA_ONE * moment_one + (1.0 - BETA_ONE) * gradient
    two_new = BETA_TWO * moment_two + (1.0 - BETA_TWO) * gradient * gradient
    one_hat = one_new / (1.0 - BETA_ONE**STEP)
    two_hat = two_new / (1.0 - BETA_TWO**STEP)
    weights_new = weights - step_rate * (
        one_hat / (jnp.sqrt(two_hat) + ADAM_EPS) + decay_rate * weights
    )
    return (weights_new, one_new, two_new)


def norm_forward(values, gain_row, bias_row):
    center = values - jnp.mean(values, axis=-1, keepdims=True)
    spread = jnp.mean(center * center, axis=-1, keepdims=True)
    inverse = lax.rsqrt(spread + NORM_EPS)
    normed = center * inverse
    return (normed * gain_row + bias_row, (normed, inverse))


def norm_backward(upstream, stored, gain_row):
    normed, inverse = stored
    scaled = upstream * gain_row
    mean_one = jnp.mean(scaled, axis=-1, keepdims=True)
    mean_two = jnp.mean(scaled * normed, axis=-1, keepdims=True)
    return (
        inverse * (scaled - mean_one - normed * mean_two),
        jnp.sum(upstream * normed, axis=0),
        jnp.sum(upstream, axis=0),
    )


def inner_rows(left_side, right_side):
    return lax.dot_general(
        left_side, right_side, (((0,), (0,)), ((), ())), preferred_element_type=jnp.float32
    )


def times_transpose(left_side, right_side):
    return lax.dot_general(
        left_side, right_side, (((1,), (1,)), ((), ())), preferred_element_type=jnp.float32
    )


def gather_rows(values):
    return lax.all_gather(values, "tensor", axis=0, tiled=True)


def gather_grads(values):
    return lax.all_gather(values, "tensor", axis=0, tiled=True)


def branch_rows(values, weight):
    return lax.psum_scatter(
        jnp.dot(values, weight, preferred_element_type=jnp.float32).astype(jnp.bfloat16),
        "tensor",
        scatter_dimension=0,
        tiled=True,
    ).astype(jnp.float32)


def input_rows(values, weight):
    return lax.psum_scatter(
        times_transpose(values, weight).astype(jnp.bfloat16),
        "tensor",
        scatter_dimension=0,
        tiled=True,
    ).astype(jnp.float32)


def block_scores(queries, key_rows, mask_bias, block_start, block_rows, head_size):
    scores = jnp.einsum(
        "qhd,khd->hqk", queries, key_rows, preferred_element_type=jnp.float32
    ) * head_size ** (-0.5)
    return scores + mask_bias[None, block_start : block_start + block_rows]


def attention_forward(gathered, w_qkv, head_count, head_size, mask_bias):
    length = gathered.shape[0]
    projected = jnp.dot(gathered, w_qkv, preferred_element_type=jnp.float32).astype(jnp.bfloat16)
    projected = projected.reshape(length, 3, head_count, head_size)
    queries = projected[:, 0]
    key_rows = projected[:, 1]
    value_rows = projected[:, 2]
    block_rows = min(512, length)
    scores = block_scores(queries, key_rows, mask_bias, 0, block_rows, head_size)
    row_peak = jnp.max(scores, axis=-1, keepdims=True)
    row_total = row_peak + jnp.log(jnp.sum(jnp.exp(scores - row_peak), axis=-1, keepdims=True))
    weights = jnp.exp(scores - row_total).astype(jnp.bfloat16)
    outputs = jnp.einsum("hqk,khd->qhd", weights, value_rows, preferred_element_type=jnp.float32)
    totals = [row_total]
    attended = outputs.astype(jnp.bfloat16).reshape(length, head_count * head_size)
    return (attended, (queries, key_rows, value_rows, totals))


def attention_backward(upstream, w_out, attended, stored, head_count, head_size, mask_bias):
    queries, key_rows, value_rows, totals = stored
    length = upstream.shape[0]
    score_scale = head_size ** (-0.5)
    grad_out = inner_rows(attended, upstream)
    attended_grad = (
        times_transpose(upstream, w_out).astype(jnp.bfloat16).reshape(length, head_count, head_size)
    )
    block_rows = min(512, length)
    key_grads = jnp.zeros((length, head_count, head_size), jnp.float32)
    value_grads = jnp.zeros((length, head_count, head_size), jnp.float32)
    query_grads = []
    for number, block_start in enumerate(range(0, length, block_rows)):
        scores = block_scores(queries, key_rows, mask_bias, block_start, block_rows, head_size)
        weights = jnp.exp(scores - totals[number])
        value_grads = jnp.einsum(
            "hqk,qhd->khd",
            weights.astype(jnp.bfloat16),
            attended_grad,
            preferred_element_type=jnp.float32,
        )
        weight_grads = jnp.einsum(
            "qhd,khd->hqk", attended_grad, value_rows, preferred_element_type=jnp.float32
        )
        score_grads = (
            weights * (weight_grads - jnp.sum(weights * weight_grads, axis=-1, keepdims=True))
        ).astype(jnp.bfloat16)
        query_grads.append(
            jnp.einsum("hqk,khd->qhd", score_grads, key_rows, preferred_element_type=jnp.float32)
            * score_scale
        )
        key_grads = (
            jnp.einsum("hqk,qhd->khd", score_grads, queries, preferred_element_type=jnp.float32)
            * score_scale
        )
    projected_grad = jnp.stack([query_grads[0], key_grads, value_grads], axis=1)
    return (
        projected_grad.astype(jnp.bfloat16).reshape(length, 3 * head_count * head_size),
        grad_out,
    )


def block_forward(residual, matrices, gain_rows, bias_rows, head_count, head_size, mask_bias):
    w_qkv, w_out, w_in, w_down = matrices
    normed, norm_one = norm_forward(residual, gain_rows[0], bias_rows[0])
    gathered = gather_rows(normed.astype(jnp.bfloat16))
    attended, stored = attention_forward(gathered, w_qkv, head_count, head_size, mask_bias)
    middle = residual + branch_rows(attended, w_out)
    normed_two, norm_two = norm_forward(middle, gain_rows[1], bias_rows[1])
    gathered_two = gather_rows(normed_two.astype(jnp.bfloat16))
    hidden = jnp.dot(gathered_two, w_in, preferred_element_type=jnp.float32)
    active = jax.nn.gelu(hidden, approximate=False).astype(jnp.bfloat16)
    result = middle + branch_rows(active, w_down)
    return (result, (gathered, norm_one, attended, stored, gathered_two, norm_two, hidden, active))


def block_backward(upstream, matrices, gain_rows, saved_values, head_count, head_size, mask_bias):
    w_qkv, w_out, w_in, w_down = matrices
    gathered, norm_one, attended, stored, gathered_two, norm_two, hidden, active = saved_values
    down_full = gather_grads(upstream.astype(jnp.bfloat16))
    grad_down = inner_rows(active, down_full)
    active_grad = times_transpose(down_full, w_down)
    gelu_pull = jax.vjp(partial(jax.nn.gelu, approximate=False), hidden)[1]
    hidden_grad = gelu_pull(active_grad)[0].astype(jnp.bfloat16)
    grad_in = inner_rows(gathered_two, hidden_grad)
    normed_two_grad = input_rows(hidden_grad, w_in)
    middle_grad, gain_two, bias_two = norm_backward(normed_two_grad, norm_two, gain_rows[1])
    middle_grad = upstream + middle_grad
    middle_full = gather_grads(middle_grad.astype(jnp.bfloat16))
    projected_grad, grad_out = attention_backward(
        middle_full, w_out, attended, stored, head_count, head_size, mask_bias
    )
    grad_qkv = inner_rows(gathered, projected_grad)
    normed_grad = input_rows(projected_grad, w_qkv)
    input_grad, gain_one, bias_one = norm_backward(normed_grad, norm_one, gain_rows[0])
    return (
        middle_grad + input_grad,
        [grad_qkv, grad_out, grad_in, grad_down],
        (gain_one, gain_two, bias_one, bias_two),
    )


def embed_forward(residual, w_embed):
    residual_low = gather_rows(residual.astype(jnp.bfloat16))
    columns = jnp.dot(residual_low, w_embed, preferred_element_type=jnp.float32).astype(
        jnp.bfloat16
    )
    own_columns = lax.all_to_all(columns, "tensor", split_axis=0, concat_axis=1, tiled=True)
    return (own_columns.astype(jnp.float32), residual_low)


def embed_backward(upstream, residual_low, w_embed):
    columns = lax.all_to_all(
        upstream.astype(jnp.bfloat16), "tensor", split_axis=1, concat_axis=0, tiled=True
    )
    grad_embed = inner_rows(residual_low, columns)
    return (input_rows(columns, w_embed), grad_embed)


def slot_builder(gradients, unit_of_slot, unit_width):
    flat_units = jnp.concatenate([gradient.reshape(-1) for gradient in gradients]).reshape(
        -1, unit_width
    )
    unit_total = flat_units.shape[0]
    source = jnp.take(flat_units, jnp.clip(unit_of_slot, 0, unit_total - 1), axis=0)
    return jnp.where((unit_of_slot >= 0)[:, None], source, 0.0)


def per_device(
    tokens_in,
    positions,
    segment_ids,
    owners,
    master,
    first_moment,
    second_moment,
    norm_gains,
    norm_biases,
    norm_first,
    norm_second,
    cotangent,
):
    devices = lax.axis_size("dp")
    tensor_count = lax.axis_size("tensor")
    capacity = master.shape[0]
    unit_width = master.shape[1]
    unit_count = owners.shape[0]
    slot_index = slot_table(owners, devices, capacity)
    unit_of_slot = (
        jnp.full((devices * capacity,), -1, jnp.int32)
        .at[slot_index]
        .set(jnp.arange(unit_count, dtype=jnp.int32))
    )
    targets = unit_of_slot
    targets = jnp.where(targets < 0, unit_count, targets)
    placed = (
        jnp.zeros((unit_count, unit_width), jnp.bfloat16)
        .at[targets]
        .set(lax.all_gather(master.astype(jnp.bfloat16), "dp", axis=0, tiled=True), mode="drop")
    )
    shapes = weight_shapes(tensor_count)
    matrices = split_flat(placed.reshape(-1), shapes)
    encoder = matrices[0:4]
    w_embed = matrices[4]
    decoder = matrices[5:9]
    enc_heads = HE // tensor_count
    dec_heads = HD // tensor_count
    micro_count = tokens_in.shape[0]
    grad_sums = [jnp.zeros(matrix_shape, jnp.float32) for matrix_shape in shapes]
    norm_sums = jnp.zeros((4, DE + DD), jnp.float32)
    decoded_rows = []
    token_grads = []
    for micro_step in range(micro_count):
        tile_ids = segment_ids[micro_step, 0]
        mask_bias = jnp.where(tile_ids[:, None] == tile_ids[None, :], 0.0, MASK_FILL).astype(
            jnp.float32
        )
        position_now = positions[:, micro_step]
        residual = tokens_in[micro_step].astype(jnp.float32) + sincos_embed(position_now, DE)
        residual, enc_saved = block_forward(
            residual, encoder, norm_gains[:, :DE], norm_biases[:, :DE], enc_heads, HDE, mask_bias
        )
        residual, embed_low = embed_forward(residual, w_embed)
        residual = residual + sincos_embed(position_now, DD)
        residual, dec_saved = block_forward(
            residual, decoder, norm_gains[:, DE:], norm_biases[:, DE:], dec_heads, HDD, mask_bias
        )
        decoded_rows.append(residual)
        upstream, dec_grads, dec_norm = block_backward(
            cotangent[micro_step], decoder, norm_gains[:, DE:], dec_saved, dec_heads, HDD, mask_bias
        )
        upstream, grad_embed = embed_backward(upstream, embed_low, w_embed)
        upstream, enc_grads, enc_norm = block_backward(
            upstream, encoder, norm_gains[:, :DE], enc_saved, enc_heads, HDE, mask_bias
        )
        token_grads.append(upstream)
        step_grads = enc_grads + [grad_embed] + dec_grads
        step_norm = jnp.concatenate([jnp.stack(enc_norm), jnp.stack(dec_norm)], axis=1)
        grad_sums = [total_grad + new_grad for total_grad, new_grad in zip(grad_sums, step_grads)]
        norm_sums = norm_sums + step_norm
    reduced = lax.psum_scatter(
        slot_builder(grad_sums, unit_of_slot, unit_width), "dp", scatter_dimension=0, tiled=True
    )
    norm_total = lax.psum(norm_sums, ("dp", "tensor"))
    new_master, new_first, new_second = adamw(
        master, reduced, first_moment, second_moment, WEIGHT_DECAY, LEARN_RATE
    )
    norm_params = jnp.concatenate([norm_gains, norm_biases], axis=0)
    new_norms, norm_one_new, norm_two_new = adamw(
        norm_params, norm_total, norm_first, norm_second, 0.0, NORM_RATE
    )
    return (
        jnp.stack(decoded_rows),
        jnp.stack(token_grads),
        new_master,
        new_first,
        new_second,
        new_norms,
        norm_one_new,
        norm_two_new,
    )


MESH = pl.DeviceIdType.MESH
ALL = slice(None)


class Place:
    def __init__(self):
        self.d = lax.axis_index("dp")
        self.x = lax.axis_index("tensor")
        self.z = self.d // 4
        self.y = (self.d // 2) % 2
        self.c = self.d % 2
        self.ids = {
            "c": (self.d + 1 - 2 * self.c, self.x),
            "y": (self.d + 2 - 4 * self.y, self.x),
            "x": (self.d, 1 - self.x),
            "z+": (self.d + 4, self.x),
            "z-": (self.d - 4, self.x),
        }

    def greet(self, kinds):
        bar = pltpu.get_barrier_semaphore()
        for k in kinds:
            pl.semaphore_signal(bar, inc=1, device_id=self.ids[k], device_id_type=MESH)

        @pl.when(self.z < 3)
        def _():
            pl.semaphore_signal(bar, inc=1, device_id=self.ids["z+"], device_id_type=MESH)

        @pl.when(self.z > 0)
        def _():
            pl.semaphore_signal(bar, inc=1, device_id=self.ids["z-"], device_id_type=MESH)

        inner = jnp.where(jnp.logical_and(self.z > 0, self.z < 3), 1, 0)
        pl.semaphore_wait(bar, len(kinds) + 1 + inner)

    def there(self, disp):
        dz = disp[0]
        if dz == 0:
            return None
        return self.z + dz <= 3 if dz > 0 else self.z + dz >= 0

    def at(self, disp):
        dz, fy, fx = disp
        return (1 - self.x if fx else self.x, self.z + dz, 1 - self.y if fy else self.y)


def when(cond, f):
    if cond is None:
        f()
    else:
        pl.when(cond)(f)


def both(a, b):
    if a is None:
        return b
    if b is None:
        return a
    return jnp.logical_and(a, b)


def spread(order):
    out = {}
    todo = [((0, 0, 0), -1, 0)]
    while todo:
        (dz, fy, fx), last, way = todo.pop(0)
        nxt = []
        for i, a in enumerate(order):
            if i < last:
                continue
            if a == "z":
                for s in (1, -1):
                    if i == last and s != way:
                        continue
                    n = (dz - s, fy, fx)
                    if abs(n[0]) <= 3:
                        nxt.append((n, "z+" if s > 0 else "z-", i, s))
            elif i > last:
                n = (dz, 1, fx) if a == "y" else (dz, fy, 1)
                nxt.append((n, a, i, 0))
        out[(dz, fy, fx)] = [(n, w) for n, w, _, _ in nxt]
        todo += [(n, i, s) for n, _, i, s in nxt]
    return out


def hops(d):
    return abs(d[0]) + d[1] + d[2]


BACK = {"z+": "z-", "z-": "z+", "x": "x", "y": "y"}


def gather_kernel(plan, with_x, mine, out, send, recv, sib_send, sib_recv, own_sem):
    p = Place()
    p.greet(["c", "y", "x"] if with_x else ["c", "y"])
    trees = [spread(o) for o, _, _ in plan]
    ids = [{d: i + 32 * g for i, d in enumerate(sorted(t))} for g, t in enumerate(trees)]
    waits = []

    def at(disp, core, g):
        t, z, y = p.at(disp)
        return out.at[((t,) if with_x else ()) + (z, y, core, pl.ds(plan[g][1], plan[g][2]))]

    def push(src, g, nd, way, cond):
        k = ids[g][nd]
        od = None
        cp = pltpu.make_async_remote_copy(src_ref=src[0], dst_ref=src[1], send_sem=send.at[k], recv_sem=recv.at[k],
                                          device_id=p.ids[way], device_id_type=MESH)
        c2 = cond
        if way == "z+":
            c2 = both(cond, p.z < 3)
        elif way == "z-":
            c2 = both(cond, p.z > 0)
        when(c2, cp.start)
        waits.append((c2, cp))

    def share(src, g, disp, cond):
        k = ids[g][disp]
        cp = pltpu.make_async_remote_copy(src_ref=src, dst_ref=at(disp, p.c, g), send_sem=sib_send.at[k], recv_sem=sib_recv.at[k],
                                          device_id=p.ids["c"], device_id_type=MESH)
        when(cond, cp.start)
        waits.append((cond, cp))

    zero = (0, 0, 0)
    for g, tree in enumerate(trees):
        src = mine.at[pl.ds(plan[g][1], plan[g][2])]
        for nd, way in tree[zero]:
            push((src, at(zero, p.c, g)), g, nd, way, None)
    own = pltpu.make_async_copy(mine, out.at[((p.x,) if with_x else ()) + (p.z, p.y, p.c)], own_sem)
    own.start()
    for g in range(len(plan)):
        share(mine.at[pl.ds(plan[g][1], plan[g][2])], g, zero, None)
    events = sorted((hops(d), g, d) for g, t in enumerate(trees) for d in t if d != zero)
    for _, g, d in events:
        cond = p.there(d)
        blk = at(d, p.c, g)
        got = pltpu.make_async_remote_copy(src_ref=blk, dst_ref=blk, send_sem=send.at[ids[g][d]], recv_sem=recv.at[ids[g][d]],
                                           device_id=p.ids["c"], device_id_type=MESH)
        when(cond, got.wait_recv)
        for nd, way in trees[g][d]:
            push((blk, blk), g, nd, way, cond)
        share(blk, g, d, cond)
    for g, t in enumerate(trees):
        for d in t:
            blk = at(d, 1 - p.c, g)
            got = pltpu.make_async_remote_copy(src_ref=blk, dst_ref=blk, send_sem=sib_send.at[ids[g][d]], recv_sem=sib_recv.at[ids[g][d]],
                                               device_id=p.ids["c"], device_id_type=MESH)
            when(p.there(d), got.wait_recv)
    own.wait()
    for c, cp in waits:
        when(c, cp.wait_send)


def gather(shard, plan, with_x, ident, space=pl.ANY):
    rows, width = shard.shape
    lead = (2, 4, 2, 2) if with_x else (4, 2, 2)
    sems = pltpu.SemaphoreType.DMA((32 * len(plan),))
    return pl.pallas_call(
        partial(gather_kernel, plan, with_x),
        out_shape=jax.ShapeDtypeStruct(lead + (rows, width), shard.dtype),
        in_specs=[pl.BlockSpec(memory_space=space)],
        out_specs=pl.BlockSpec(memory_space=space),
        scratch_shapes=[sems, sems, sems, sems, pltpu.SemaphoreType.DMA],
        compiler_params=pltpu.CompilerParams(collective_id=ident, has_side_effects=True, vmem_limit_bytes=60 << 20),
        name=f"gather_{ident}",
    )(shard)


def add_rows(acc, got, step=80):
    n = acc.shape[0]
    while n % step:
        step -= 16

    def body(i, _):
        r = pl.ds(pl.multiple_of(i * step, step), step)
        acc[r, :] = acc[r, :] + got[r, :]
        return 0

    lax.fori_loop(0, n // step, body, 0)


def reduce_kernel(plan, with_x, src, out, *rest):
    n = len(plan)
    accs, halves, bufs = rest[:n], rest[n:2 * n], rest[2 * n:3 * n]
    send, recv, sib_send, sib_recv, loads = rest[3 * n:]
    p = Place()
    p.greet(["c", "y", "x"] if with_x else ["c", "y"])
    trees = [spread(o) for o, _, _ in plan]
    ids = [{d: i + 32 * g for i, d in enumerate(sorted(t))} for g, t in enumerate(trees)]
    waits = []
    zero = (0, 0, 0)

    def ix(disp):
        t, z, y = p.at(disp)
        return ((t,) if with_x else ()) + (z, y)

    events = sorted((-hops(d), g, d) for g, t in enumerate(trees) for d in t)
    for _, g, d in events:
        cond = p.there(d)
        k = ids[g][d]
        rows = pl.ds(plan[g][1], plan[g][2])
        cp = pltpu.make_async_remote_copy(
            src_ref=src.at[ix(d) + (1 - p.c, rows)], dst_ref=halves[g].at[ix(d)], send_sem=sib_send.at[k],
            recv_sem=sib_recv.at[k], device_id=p.ids["c"], device_id_type=MESH)
        ld = pltpu.make_async_copy(src.at[ix(d) + (p.c, rows)], accs[g].at[ix(d)], loads.at[k])

        def go(cp=cp, ld=ld):
            cp.start()
            ld.start()
        when(cond, go)
        waits.append((cond, cp))
    for _, g, d in events:
        k = ids[g][d]
        rows = pl.ds(plan[g][1], plan[g][2])
        base = k - ids[g][min(trees[g])]

        def step(g=g, d=d, k=k, rows=rows):
            acc = accs[g].at[ix(d)]
            pltpu.make_async_copy(src.at[ix(d) + (p.c, rows)], acc, loads.at[k]).wait()
            half = halves[g].at[ix(d)]
            pltpu.make_async_remote_copy(src_ref=half, dst_ref=half, send_sem=sib_send.at[k], recv_sem=sib_recv.at[k],
                                         device_id=p.ids["c"], device_id_type=MESH).wait_recv()
            add_rows(acc, half)
            for nd, way in trees[g][d]:
                kk = ids[g][nd]
                buf = bufs[g].at[kk - 32 * g]

                def take(acc=acc, buf=buf, kk=kk):
                    pltpu.make_async_remote_copy(src_ref=buf, dst_ref=buf, send_sem=send.at[kk], recv_sem=recv.at[kk],
                                                 device_id=p.ids["c"], device_id_type=MESH).wait_recv()
                    add_rows(acc, buf)
                if way == "z+":
                    when(p.z < 3, take)
                elif way == "z-":
                    when(p.z > 0, take)
                else:
                    take()
        cond = p.there(d)
        when(cond, step)
        if d != zero:
            way = [w for t in trees[g].values() for nd, w in t if nd == d][0]
            acc = accs[g].at[ix(d)]
            cp = pltpu.make_async_remote_copy(src_ref=acc, dst_ref=bufs[g].at[k - 32 * g], send_sem=send.at[k], recv_sem=recv.at[k],
                                              device_id=p.ids[BACK[way]], device_id_type=MESH)
            when(cond, cp.start)
            waits.append((cond, cp))
        else:
            out[rows, :] = accs[g][ix(d)]
    for c, cp in waits:
        when(c, cp.wait_send)


def reduce_scatter(whole, plan, with_x, ident, limit=62 << 20):
    rows, width = whole.shape[-2:]
    dt = whole.dtype
    lead = (2, 4, 2) if with_x else (4, 2)
    blocks = [pltpu.VMEM(lead + (num, width), dt) for _, _, num in plan]
    bufs = [pltpu.VMEM((len(spread(o)), num, width), dt) for o, _, num in plan]
    sems = pltpu.SemaphoreType.DMA((32 * len(plan),))
    return pl.pallas_call(
        partial(reduce_kernel, plan, with_x),
        out_shape=jax.ShapeDtypeStruct((rows, width), dt),
        in_specs=[pl.BlockSpec(memory_space=pl.ANY)],
        out_specs=pl.BlockSpec(memory_space=pltpu.VMEM),
        scratch_shapes=blocks + blocks + bufs + [sems] * 5,
        compiler_params=pltpu.CompilerParams(collective_id=ident, has_side_effects=True, vmem_limit_bytes=limit),
        name=f"reduce_{ident}",
    )(whole)


PLAN_ALL = [("zxy", 0, 640), ("zyx", 640, 640), ("xzy", 1280, 640), ("yzx", 1920, 720)]
PLAN_DP = [("zy", 0, 656)]
SHARD_UNITS = 656
PANEL = 128


def layout(shapes, shards):
    table = []
    unit_at, row_at = 0, 0
    for rows, cols in shapes:
        rb, panels = rows // shards, cols // PANEL
        units = rb * cols // 512
        padded = -(-rb // 16) * 16
        table.append((rb, panels, units, unit_at, row_at, padded))
        unit_at += units
        row_at += padded * panels
    return table, unit_at, row_at


def unit_places(units, table, shards):
    place = jnp.zeros_like(units)
    for rb, panels, n, first, _, _ in table:
        lo = first * shards
        v = units - lo
        here = (v // n) * SHARD_UNITS + first + v % n
        place = jnp.where(v >= 0, here, place)
    return place


def own_units(owners, mine, capacity):
    count = owners.shape[0] // 128
    hit = (owners[:, 0] == mine).reshape(count, 128)
    lane = jnp.arange(128)
    tri = (lane[:, None] <= lane[None, :]).astype(jnp.bfloat16)
    within = jnp.dot(hit.astype(jnp.bfloat16), tri, preferred_element_type=jnp.float32)
    totals = within[:, 127].astype(jnp.int32)
    upto = jnp.sum(jnp.where(jnp.arange(count)[:, None] >= jnp.arange(count)[None, :], totals[None, :], 0), axis=1)
    slot = jnp.arange(capacity, dtype=jnp.int32)
    block = jnp.sum((upto[None, :] <= slot[:, None]).astype(jnp.int32), axis=1)
    pick = block[:, None] == jnp.arange(count)[None, :]
    before = jnp.sum(jnp.where(pick, (upto - totals)[None, :], 0), axis=1)
    row = jnp.dot(pick.astype(jnp.bfloat16), within.astype(jnp.bfloat16), preferred_element_type=jnp.float32)
    rank = (slot - before).astype(jnp.float32)
    at = jnp.sum((row <= rank[:, None]).astype(jnp.int32), axis=1)
    return block * 128 + at, slot < upto[count - 1]


def to_panels(shard, table):
    out = []
    for rb, panels, n, first, _, padded in table:
        m = shard[first:first + n].reshape(rb, panels, PANEL).transpose(1, 0, 2)
        if padded > rb:
            m = jnp.pad(m, ((0, 0), (0, padded - rb), (0, 0)))
        out.append(m.reshape(panels * padded, PANEL))
    return jnp.concatenate(out, axis=0)


def from_panels(rows, table):
    out = []
    for rb, panels, n, first, at, padded in table:
        m = rows[at:at + panels * padded].reshape(panels, padded, PANEL)[:, :rb]
        out.append(m.transpose(1, 0, 2).reshape(n, 512))
    out = jnp.concatenate(out, axis=0)
    return jnp.pad(out, ((0, SHARD_UNITS - out.shape[0]), (0, 0)))


BY_ROWS = (1, 3, 6, 8)


def unpack(full, table):
    full = full.reshape(2, 16, full.shape[-2], PANEL)
    mats = []
    for i, (rb, panels, n, _, at, padded) in enumerate(table):
        m = full[:, :, at:at + panels * padded].reshape(2, 16, panels, padded, PANEL)[:, :, :, :rb]
        if i in BY_ROWS:
            m = m.transpose(0, 1, 3, 2, 4).reshape(2 * 16 * rb, panels * PANEL)
        else:
            m = m.transpose(1, 3, 0, 2, 4).reshape(16 * rb, 2 * panels * PANEL)
        mats.append(m)
    return mats


def pack(mats, table):
    out = []
    for i, (rb, panels, n, _, at, padded) in enumerate(table):
        m = mats[i].astype(jnp.bfloat16)
        if i in BY_ROWS:
            m = m.reshape(2, 16, rb, panels, PANEL).transpose(0, 1, 3, 2, 4)
        else:
            m = m.reshape(16, rb, 2, panels, PANEL).transpose(2, 0, 3, 1, 4)
        if padded > rb:
            m = jnp.pad(m, ((0, 0), (0, 0), (0, 0), (0, padded - rb), (0, 0)))
        out.append(m.reshape(2, 16, panels * padded, PANEL))
    out = jnp.concatenate(out, axis=2)
    return out.reshape(2, 4, 2, 2, out.shape[2], PANEL)


def whole_attention(n1, w_qkv, heads, size, mask):
    length = n1.shape[0]
    proj = jnp.dot(n1, w_qkv, preferred_element_type=jnp.float32).astype(jnp.bfloat16)
    proj = proj.reshape(length, 2, 3, heads // 2, size)
    q, k, v = (proj[:, :, i].reshape(length, heads, size) for i in range(3))
    z = jnp.einsum("qhd,khd->hqk", q, k, preferred_element_type=jnp.float32) * size ** (-0.5) + mask[None]
    e = jnp.exp(z - jnp.max(z, axis=-1, keepdims=True))
    p = e / jnp.sum(e, axis=-1, keepdims=True)
    a = jnp.einsum("hqk,khd->qhd", p.astype(jnp.bfloat16), v, preferred_element_type=jnp.float32)
    return a.astype(jnp.bfloat16).reshape(length, heads * size), (q, k, v, p)


def whole_forward(x, mats, gains, biases, heads, size, mask):
    w_qkv, w_out, w_in, w_down = mats
    n1, s1 = norm_forward(x, gains[0], biases[0])
    n1 = n1.astype(jnp.bfloat16)
    a, att = whole_attention(n1, w_qkv, heads, size, mask)
    x1 = x + jnp.dot(a, w_out, preferred_element_type=jnp.float32)
    n2, s2 = norm_forward(x1, gains[1], biases[1])
    n2 = n2.astype(jnp.bfloat16)
    h = jnp.dot(n2, w_in, preferred_element_type=jnp.float32)
    u = jax.nn.gelu(h, approximate=False).astype(jnp.bfloat16)
    return x1 + jnp.dot(u, w_down, preferred_element_type=jnp.float32), (n1, s1, a, att, n2, s2, h, u)


def whole_backward(dr, mats, gains, saved, heads, size):
    w_qkv, w_out, w_in, w_down = mats
    n1, s1, a, (q, k, v, p), n2, s2, h, u = saved
    length = dr.shape[0]
    r = dr.astype(jnp.bfloat16)
    d_down = inner_rows(u, r)
    du = times_transpose(r, w_down)
    dh = jax.vjp(partial(jax.nn.gelu, approximate=False), h)[1](du)[0].astype(jnp.bfloat16)
    d_in = inner_rows(n2, dh)
    dn2 = times_transpose(dh, w_in)
    dx1, dg2, db2 = norm_backward(dn2, s2, gains[1])
    dx1 = dr + dx1
    r1 = dx1.astype(jnp.bfloat16)
    d_out = inner_rows(a, r1)
    da = times_transpose(r1, w_out).astype(jnp.bfloat16).reshape(length, heads, size)
    dp = jnp.einsum("qhd,khd->hqk", da, v, preferred_element_type=jnp.float32)
    dv = jnp.einsum("hqk,qhd->khd", p.astype(jnp.bfloat16), da, preferred_element_type=jnp.float32)
    dz = (p * (dp - jnp.sum(p * dp, axis=-1, keepdims=True))).astype(jnp.bfloat16)
    dq = jnp.einsum("hqk,khd->qhd", dz, k, preferred_element_type=jnp.float32) * size ** (-0.5)
    dk = jnp.einsum("hqk,qhd->khd", dz, q, preferred_element_type=jnp.float32) * size ** (-0.5)
    half = heads // 2
    dproj = jnp.stack([g.reshape(length, 2, half, size) for g in (dq, dk, dv)], axis=2)
    dproj = dproj.astype(jnp.bfloat16).reshape(length, 3 * heads * size)
    d_qkv = inner_rows(n1, dproj)
    dn1 = times_transpose(dproj, w_qkv)
    dx, dg1, db1 = norm_backward(dn1, s1, gains[0])
    return dx1 + dx, [d_qkv, d_out, d_in, d_down], (dg1, dg2, db1, db2)


def swap(v):
    return lax.ppermute(v, "tensor", [(0, 1), (1, 0)])


def sequence_device(tokens_in, positions, segment_ids, owners, master, first_moment, second_moment, norm_gains,
                    norm_biases, norm_first, norm_second, cotangent):
    t = lax.axis_index("tensor")
    shapes = weight_shapes(2)
    table, _, _ = layout(shapes, 16)

    def whole(v, axis):
        own = lax.dynamic_index_in_dim(v, t, axis, keepdims=False)
        other = swap(lax.dynamic_index_in_dim(v, 1 - t, axis, keepdims=False))
        at = 1 if axis == 1 else 0
        return jnp.concatenate([jnp.where(t == 0, own, other), jnp.where(t == 0, other, own)], axis=at)

    def halves(v):
        half = v.shape[0] // 2
        own = lax.dynamic_slice_in_dim(v, t * half, half, 0)
        other = swap(lax.dynamic_slice_in_dim(v, (1 - t) * half, half, 0))
        return jnp.stack([jnp.where(t == 0, own, other), jnp.where(t == 0, other, own)])

    tokens, cot, pos = whole(tokens_in, 0), whole(cotangent, 0), whole(positions, 1)
    tile = lax.dynamic_index_in_dim(segment_ids, t, 0, keepdims=False)[0]

    unit, used = own_units(owners, lax.axis_index("dp"), master.shape[0])
    place = unit_places(unit, table, 16)
    parts = jnp.zeros((16 * SHARD_UNITS, 512), jnp.bfloat16)
    parts = parts.at[jnp.where(used, place, 16 * SHARD_UNITS)].set(master.astype(jnp.bfloat16), mode="drop", unique_indices=True)
    shard = reduce_scatter(parts.reshape(4, 2, 2, SHARD_UNITS, 512), PLAN_DP, False, 1)
    full = gather(to_panels(shard, table), PLAN_ALL, True, 2)
    mats = unpack(full, table)

    mask = jnp.where(tile[:, None] == tile[None, :], 0.0, MASK_FILL).astype(jnp.float32)
    x0 = tokens.astype(jnp.float32) + sincos_embed(pos, DE)
    x2, enc = whole_forward(x0, mats[0:4], norm_gains[:, :DE], norm_biases[:, :DE], HE, HDE, mask)
    e = x2.astype(jnp.bfloat16)
    y0 = jnp.dot(e, mats[4], preferred_element_type=jnp.float32).astype(jnp.bfloat16).astype(jnp.float32) + sincos_embed(pos, DD)
    decoded, dec = whole_forward(y0, mats[5:9], norm_gains[:, DE:], norm_biases[:, DE:], HD, HDD, mask)
    dy0, dec_grads, dec_norm = whole_backward(cot, mats[5:9], norm_gains[:, DE:], dec, HD, HDD)
    de = dy0.astype(jnp.bfloat16)
    d_embed = inner_rows(e, de)
    dx2 = times_transpose(de, mats[4])
    dx0, enc_grads, enc_norm = whole_backward(dx2, mats[0:4], norm_gains[:, :DE], enc, HE, HDE)

    grads = pack(enc_grads + [d_embed] + dec_grads, table)
    summed = reduce_scatter(grads, PLAN_ALL, True, 3)
    spread_out = gather(from_panels(summed, table), PLAN_DP, False, 4).reshape(16 * SHARD_UNITS, 512)
    reduced = jnp.where(used[:, None], jnp.take(spread_out, jnp.clip(place, 0, 16 * SHARD_UNITS - 1), axis=0).astype(jnp.float32), 0.0)
    norm_total = lax.psum(jnp.concatenate([jnp.stack(enc_norm), jnp.stack(dec_norm)], axis=1), ("dp", "tensor"))
    new_master, new_first, new_second = adamw(master, reduced, first_moment, second_moment, WEIGHT_DECAY, LEARN_RATE)
    norm_params = jnp.concatenate([norm_gains, norm_biases], axis=0)
    new_norms, norm_one_new, norm_two_new = adamw(norm_params, norm_total, norm_first, norm_second, 0.0, NORM_RATE)
    return (halves(decoded), halves(dx0), new_master, new_first, new_second, new_norms, norm_one_new, norm_two_new)


def solution(mesh):
    step = sequence_device if (mesh.shape["dp"], mesh.shape["tensor"]) == (16, 2) else per_device
    return jax.shard_map(
        step,
        mesh=mesh,
        in_specs=(
            P(None, ("dp", "tensor"), None),
            P(None, None, ("dp", "tensor")),
            P(None, "dp", None),
            P(),
            P("dp", "tensor"),
            P("dp", "tensor"),
            P("dp", "tensor"),
            P(),
            P(),
            P(),
            P(),
            P(None, ("dp", "tensor"), None),
        ),
        out_specs=(
            P(None, ("dp", "tensor"), None),
            P(None, ("dp", "tensor"), None),
            P("dp", "tensor"),
            P("dp", "tensor"),
            P("dp", "tensor"),
            P(),
            P(),
            P(),
        ),
        check_vma=False,
    )
```

```python
from functools import partial

import jax
import jax.numpy as jnp
import ml_dtypes
import numpy as np
from jax import lax
from jax.experimental import pallas as pl
from jax.experimental.pallas import tpu as pltpu
from jax.sharding import PartitionSpec as P

DE = 768
HE = 12
HDE = 64
FFE = 3072
DD = 512
HD = 16
HDD = 32
FFD = 2048
STEP = 10


NORM_EPS = 1e-06
BETA_ONE = 0.5
BETA_TWO = 0.5
LEARN_RATE = 0.03
NORM_RATE = 0.3
WEIGHT_DECAY = 0.05
ADAM_EPS = 1e-08
MASK_FILL = -1000000000.0


def sincos_part(coordinate, part_width):
    halfway = part_width // 2
    frequency = 1.0 / 10000.0 ** (jnp.arange(halfway, dtype=jnp.float32) / halfway)
    angles = coordinate.astype(jnp.float32)[:, None] * frequency[None, :]
    return jnp.concatenate([jnp.sin(angles), jnp.cos(angles)], axis=1)


def sincos_embed(positions, model_width):
    side_width = model_width // 16 * 6
    first_width = model_width - 2 * side_width
    return jnp.concatenate(
        [
            sincos_part(positions[0], first_width),
            sincos_part(positions[1], side_width),
            sincos_part(positions[2], side_width),
        ],
        axis=1,
    )


def slot_table(owners, devices, capacity):
    owner_ids = owners[:, 0]
    onehot = (owner_ids[:, None] == jnp.arange(devices, dtype=jnp.int32)[None, :]).astype(jnp.int32)
    before = jnp.cumsum(onehot, axis=0) - onehot
    owner_rank = jnp.sum(before * onehot, axis=1)
    return owner_ids * capacity + owner_rank


def weight_shapes(tensor_count):
    enc_heads = HE // tensor_count
    dec_heads = HD // tensor_count
    return [
        (DE, 3 * enc_heads * HDE),
        (enc_heads * HDE, DE),
        (DE, FFE // tensor_count),
        (FFE // tensor_count, DE),
        (DE, DD // tensor_count),
        (DD, 3 * dec_heads * HDD),
        (dec_heads * HDD, DD),
        (DD, FFD // tensor_count),
        (FFD // tensor_count, DD),
    ]


def split_flat(flat_vector, shapes):
    pieces = []
    offset = 0
    for matrix_shape in shapes:
        length = matrix_shape[0] * matrix_shape[1]
        pieces.append(flat_vector[offset : offset + length].reshape(matrix_shape))
        offset += length
    return pieces


def adamw(weights, gradient, moment_one, moment_two, decay_rate, step_rate):
    one_new = BETA_ONE * moment_one + (1.0 - BETA_ONE) * gradient
    two_new = BETA_TWO * moment_two + (1.0 - BETA_TWO) * gradient * gradient
    one_hat = one_new / (1.0 - BETA_ONE**STEP)
    two_hat = two_new / (1.0 - BETA_TWO**STEP)
    weights_new = weights - step_rate * (
        one_hat / (jnp.sqrt(two_hat) + ADAM_EPS) + decay_rate * weights
    )
    return (weights_new, one_new, two_new)


def norm_forward(values, gain_row, bias_row):
    center = values - jnp.mean(values, axis=-1, keepdims=True)
    spread = jnp.mean(center * center, axis=-1, keepdims=True)
    inverse = lax.rsqrt(spread + NORM_EPS)
    normed = center * inverse
    return (normed * gain_row + bias_row, (normed, inverse))


def norm_backward(upstream, stored, gain_row):
    normed, inverse = stored
    scaled = upstream * gain_row
    mean_one = jnp.mean(scaled, axis=-1, keepdims=True)
    mean_two = jnp.mean(scaled * normed, axis=-1, keepdims=True)
    return (
        inverse * (scaled - mean_one - normed * mean_two),
        jnp.sum(upstream * normed, axis=0),
        jnp.sum(upstream, axis=0),
    )


def inner_rows(left_side, right_side):
    return lax.dot_general(
        left_side, right_side, (((0,), (0,)), ((), ())), preferred_element_type=jnp.float32
    )


def times_transpose(left_side, right_side):
    return lax.dot_general(
        left_side, right_side, (((1,), (1,)), ((), ())), preferred_element_type=jnp.float32
    )


def gather_rows(values):
    return lax.all_gather(values, "tensor", axis=0, tiled=True)


def gather_grads(values):
    return lax.all_gather(values, "tensor", axis=0, tiled=True)


def branch_rows(values, weight):
    return lax.psum_scatter(
        jnp.dot(values, weight, preferred_element_type=jnp.float32).astype(jnp.bfloat16),
        "tensor",
        scatter_dimension=0,
        tiled=True,
    ).astype(jnp.float32)


def input_rows(values, weight):
    return lax.psum_scatter(
        times_transpose(values, weight).astype(jnp.bfloat16),
        "tensor",
        scatter_dimension=0,
        tiled=True,
    ).astype(jnp.float32)


def block_scores(queries, key_rows, mask_bias, block_start, block_rows, head_size):
    scores = jnp.einsum(
        "qhd,khd->hqk", queries, key_rows, preferred_element_type=jnp.float32
    ) * head_size ** (-0.5)
    return scores + mask_bias[None, block_start : block_start + block_rows]


def attention_forward(gathered, w_qkv, head_count, head_size, mask_bias):
    length = gathered.shape[0]
    projected = jnp.dot(gathered, w_qkv, preferred_element_type=jnp.float32).astype(jnp.bfloat16)
    projected = projected.reshape(length, 3, head_count, head_size)
    queries = projected[:, 0]
    key_rows = projected[:, 1]
    value_rows = projected[:, 2]
    block_rows = min(512, length)
    scores = block_scores(queries, key_rows, mask_bias, 0, block_rows, head_size)
    row_peak = jnp.max(scores, axis=-1, keepdims=True)
    row_total = row_peak + jnp.log(jnp.sum(jnp.exp(scores - row_peak), axis=-1, keepdims=True))
    weights = jnp.exp(scores - row_total).astype(jnp.bfloat16)
    outputs = jnp.einsum("hqk,khd->qhd", weights, value_rows, preferred_element_type=jnp.float32)
    totals = [row_total]
    attended = outputs.astype(jnp.bfloat16).reshape(length, head_count * head_size)
    return (attended, (queries, key_rows, value_rows, totals))


def attention_backward(upstream, w_out, attended, stored, head_count, head_size, mask_bias):
    queries, key_rows, value_rows, totals = stored
    length = upstream.shape[0]
    score_scale = head_size ** (-0.5)
    grad_out = inner_rows(attended, upstream)
    attended_grad = (
        times_transpose(upstream, w_out).astype(jnp.bfloat16).reshape(length, head_count, head_size)
    )
    block_rows = min(512, length)
    key_grads = jnp.zeros((length, head_count, head_size), jnp.float32)
    value_grads = jnp.zeros((length, head_count, head_size), jnp.float32)
    query_grads = []
    for number, block_start in enumerate(range(0, length, block_rows)):
        scores = block_scores(queries, key_rows, mask_bias, block_start, block_rows, head_size)
        weights = jnp.exp(scores - totals[number])
        value_grads = jnp.einsum(
            "hqk,qhd->khd",
            weights.astype(jnp.bfloat16),
            attended_grad,
            preferred_element_type=jnp.float32,
        )
        weight_grads = jnp.einsum(
            "qhd,khd->hqk", attended_grad, value_rows, preferred_element_type=jnp.float32
        )
        score_grads = (
            weights * (weight_grads - jnp.sum(weights * weight_grads, axis=-1, keepdims=True))
        ).astype(jnp.bfloat16)
        query_grads.append(
            jnp.einsum("hqk,khd->qhd", score_grads, key_rows, preferred_element_type=jnp.float32)
            * score_scale
        )
        key_grads = (
            jnp.einsum("hqk,qhd->khd", score_grads, queries, preferred_element_type=jnp.float32)
            * score_scale
        )
    projected_grad = jnp.stack([query_grads[0], key_grads, value_grads], axis=1)
    return (
        projected_grad.astype(jnp.bfloat16).reshape(length, 3 * head_count * head_size),
        grad_out,
    )


def block_forward(residual, matrices, gain_rows, bias_rows, head_count, head_size, mask_bias):
    w_qkv, w_out, w_in, w_down = matrices
    normed, norm_one = norm_forward(residual, gain_rows[0], bias_rows[0])
    gathered = gather_rows(normed.astype(jnp.bfloat16))
    attended, stored = attention_forward(gathered, w_qkv, head_count, head_size, mask_bias)
    middle = residual + branch_rows(attended, w_out)
    normed_two, norm_two = norm_forward(middle, gain_rows[1], bias_rows[1])
    gathered_two = gather_rows(normed_two.astype(jnp.bfloat16))
    hidden = jnp.dot(gathered_two, w_in, preferred_element_type=jnp.float32)
    active = jax.nn.gelu(hidden, approximate=False).astype(jnp.bfloat16)
    result = middle + branch_rows(active, w_down)
    return (result, (gathered, norm_one, attended, stored, gathered_two, norm_two, hidden, active))


def block_backward(upstream, matrices, gain_rows, saved_values, head_count, head_size, mask_bias):
    w_qkv, w_out, w_in, w_down = matrices
    gathered, norm_one, attended, stored, gathered_two, norm_two, hidden, active = saved_values
    down_full = gather_grads(upstream.astype(jnp.bfloat16))
    grad_down = inner_rows(active, down_full)
    active_grad = times_transpose(down_full, w_down)
    gelu_pull = jax.vjp(partial(jax.nn.gelu, approximate=False), hidden)[1]
    hidden_grad = gelu_pull(active_grad)[0].astype(jnp.bfloat16)
    grad_in = inner_rows(gathered_two, hidden_grad)
    normed_two_grad = input_rows(hidden_grad, w_in)
    middle_grad, gain_two, bias_two = norm_backward(normed_two_grad, norm_two, gain_rows[1])
    middle_grad = upstream + middle_grad
    middle_full = gather_grads(middle_grad.astype(jnp.bfloat16))
    projected_grad, grad_out = attention_backward(
        middle_full, w_out, attended, stored, head_count, head_size, mask_bias
    )
    grad_qkv = inner_rows(gathered, projected_grad)
    normed_grad = input_rows(projected_grad, w_qkv)
    input_grad, gain_one, bias_one = norm_backward(normed_grad, norm_one, gain_rows[0])
    return (
        middle_grad + input_grad,
        [grad_qkv, grad_out, grad_in, grad_down],
        (gain_one, gain_two, bias_one, bias_two),
    )


def embed_forward(residual, w_embed):
    residual_low = gather_rows(residual.astype(jnp.bfloat16))
    columns = jnp.dot(residual_low, w_embed, preferred_element_type=jnp.float32).astype(
        jnp.bfloat16
    )
    own_columns = lax.all_to_all(columns, "tensor", split_axis=0, concat_axis=1, tiled=True)
    return (own_columns.astype(jnp.float32), residual_low)


def embed_backward(upstream, residual_low, w_embed):
    columns = lax.all_to_all(
        upstream.astype(jnp.bfloat16), "tensor", split_axis=1, concat_axis=0, tiled=True
    )
    grad_embed = inner_rows(residual_low, columns)
    return (input_rows(columns, w_embed), grad_embed)


def slot_builder(gradients, unit_of_slot, unit_width):
    flat_units = jnp.concatenate([gradient.reshape(-1) for gradient in gradients]).reshape(
        -1, unit_width
    )
    unit_total = flat_units.shape[0]
    source = jnp.take(flat_units, jnp.clip(unit_of_slot, 0, unit_total - 1), axis=0)
    return jnp.where((unit_of_slot >= 0)[:, None], source, 0.0)


def per_device(
    tokens_in,
    positions,
    segment_ids,
    owners,
    master,
    first_moment,
    second_moment,
    norm_gains,
    norm_biases,
    norm_first,
    norm_second,
    cotangent,
):
    devices = lax.axis_size("dp")
    tensor_count = lax.axis_size("tensor")
    capacity = master.shape[0]
    unit_width = master.shape[1]
    unit_count = owners.shape[0]
    slot_index = slot_table(owners, devices, capacity)
    unit_of_slot = (
        jnp.full((devices * capacity,), -1, jnp.int32)
        .at[slot_index]
        .set(jnp.arange(unit_count, dtype=jnp.int32))
    )
    targets = unit_of_slot
    targets = jnp.where(targets < 0, unit_count, targets)
    placed = (
        jnp.zeros((unit_count, unit_width), jnp.bfloat16)
        .at[targets]
        .set(lax.all_gather(master.astype(jnp.bfloat16), "dp", axis=0, tiled=True), mode="drop")
    )
    shapes = weight_shapes(tensor_count)
    matrices = split_flat(placed.reshape(-1), shapes)
    encoder = matrices[0:4]
    w_embed = matrices[4]
    decoder = matrices[5:9]
    enc_heads = HE // tensor_count
    dec_heads = HD // tensor_count
    micro_count = tokens_in.shape[0]
    grad_sums = [jnp.zeros(matrix_shape, jnp.float32) for matrix_shape in shapes]
    norm_sums = jnp.zeros((4, DE + DD), jnp.float32)
    decoded_rows = []
    token_grads = []
    for micro_step in range(micro_count):
        tile_ids = segment_ids[micro_step, 0]
        mask_bias = jnp.where(tile_ids[:, None] == tile_ids[None, :], 0.0, MASK_FILL).astype(
            jnp.float32
        )
        position_now = positions[:, micro_step]
        residual = tokens_in[micro_step].astype(jnp.float32) + sincos_embed(position_now, DE)
        residual, enc_saved = block_forward(
            residual, encoder, norm_gains[:, :DE], norm_biases[:, :DE], enc_heads, HDE, mask_bias
        )
        residual, embed_low = embed_forward(residual, w_embed)
        residual = residual + sincos_embed(position_now, DD)
        residual, dec_saved = block_forward(
            residual, decoder, norm_gains[:, DE:], norm_biases[:, DE:], dec_heads, HDD, mask_bias
        )
        decoded_rows.append(residual)
        upstream, dec_grads, dec_norm = block_backward(
            cotangent[micro_step], decoder, norm_gains[:, DE:], dec_saved, dec_heads, HDD, mask_bias
        )
        upstream, grad_embed = embed_backward(upstream, embed_low, w_embed)
        upstream, enc_grads, enc_norm = block_backward(
            upstream, encoder, norm_gains[:, :DE], enc_saved, enc_heads, HDE, mask_bias
        )
        token_grads.append(upstream)
        step_grads = enc_grads + [grad_embed] + dec_grads
        step_norm = jnp.concatenate([jnp.stack(enc_norm), jnp.stack(dec_norm)], axis=1)
        grad_sums = [total_grad + new_grad for total_grad, new_grad in zip(grad_sums, step_grads)]
        norm_sums = norm_sums + step_norm
    reduced = lax.psum_scatter(
        slot_builder(grad_sums, unit_of_slot, unit_width), "dp", scatter_dimension=0, tiled=True
    )
    norm_total = lax.psum(norm_sums, ("dp", "tensor"))
    new_master, new_first, new_second = adamw(
        master, reduced, first_moment, second_moment, WEIGHT_DECAY, LEARN_RATE
    )
    norm_params = jnp.concatenate([norm_gains, norm_biases], axis=0)
    new_norms, norm_one_new, norm_two_new = adamw(
        norm_params, norm_total, norm_first, norm_second, 0.0, NORM_RATE
    )
    return (
        jnp.stack(decoded_rows),
        jnp.stack(token_grads),
        new_master,
        new_first,
        new_second,
        new_norms,
        norm_one_new,
        norm_two_new,
    )


MESH = pl.DeviceIdType.MESH
ALL = slice(None)


class Place:
    def __init__(self):
        self.d = lax.axis_index("dp")
        self.x = lax.axis_index("tensor")
        self.z = self.d // 4
        self.y = (self.d // 2) % 2
        self.c = self.d % 2
        self.ids = {
            "c": (self.d + 1 - 2 * self.c, self.x),
            "y": (self.d + 2 - 4 * self.y, self.x),
            "x": (self.d, 1 - self.x),
            "z+": (self.d + 4, self.x),
            "z-": (self.d - 4, self.x),
        }

    def greet(self, kinds):
        bar = pltpu.get_barrier_semaphore()
        for k in kinds:
            pl.semaphore_signal(bar, inc=1, device_id=self.ids[k], device_id_type=MESH)

        @pl.when(self.z < 3)
        def _():
            pl.semaphore_signal(bar, inc=1, device_id=self.ids["z+"], device_id_type=MESH)

        @pl.when(self.z > 0)
        def _():
            pl.semaphore_signal(bar, inc=1, device_id=self.ids["z-"], device_id_type=MESH)

        inner = jnp.where(jnp.logical_and(self.z > 0, self.z < 3), 1, 0)
        pl.semaphore_wait(bar, len(kinds) + 1 + inner)

    def there(self, disp):
        dz = disp[0]
        if dz == 0:
            return None
        return self.z + dz <= 3 if dz > 0 else self.z + dz >= 0

    def at(self, disp):
        dz, fy, fx = disp
        return (1 - self.x if fx else self.x, self.z + dz, 1 - self.y if fy else self.y)


def when(cond, f):
    if cond is None:
        f()
    else:
        pl.when(cond)(f)


def both(a, b):
    if a is None:
        return b
    if b is None:
        return a
    return jnp.logical_and(a, b)


def spread(order):
    out = {}
    todo = [((0, 0, 0), -1, 0)]
    while todo:
        (dz, fy, fx), last, way = todo.pop(0)
        nxt = []
        for i, a in enumerate(order):
            if i < last:
                continue
            if a == "z":
                for s in (1, -1):
                    if i == last and s != way:
                        continue
                    n = (dz - s, fy, fx)
                    if abs(n[0]) <= 3:
                        nxt.append((n, "z+" if s > 0 else "z-", i, s))
            elif i > last:
                n = (dz, 1, fx) if a == "y" else (dz, fy, 1)
                nxt.append((n, a, i, 0))
        out[(dz, fy, fx)] = [(n, w) for n, w, _, _ in nxt]
        todo += [(n, i, s) for n, _, i, s in nxt]
    return out


def hops(d):
    return abs(d[0]) + d[1] + d[2]


BACK = {"z+": "z-", "z-": "z+", "x": "x", "y": "y"}


def gather_kernel(plan, with_x, mine, out, send, recv, sib_send, sib_recv, own_sem):
    p = Place()
    p.greet(["c", "y", "x"] if with_x else ["c", "y"])
    trees = [spread(o) for o, _, _ in plan]
    ids = [{d: i + 32 * g for i, d in enumerate(sorted(t))} for g, t in enumerate(trees)]
    waits = []

    def at(disp, core, g):
        t, z, y = p.at(disp)
        return out.at[((t,) if with_x else ()) + (z, y, core, pl.ds(plan[g][1], plan[g][2]))]

    def push(src, g, nd, way, cond):
        k = ids[g][nd]
        od = None
        cp = pltpu.make_async_remote_copy(src_ref=src[0], dst_ref=src[1], send_sem=send.at[k], recv_sem=recv.at[k],
                                          device_id=p.ids[way], device_id_type=MESH)
        c2 = cond
        if way == "z+":
            c2 = both(cond, p.z < 3)
        elif way == "z-":
            c2 = both(cond, p.z > 0)
        when(c2, cp.start)
        waits.append((c2, cp))

    def share(src, g, disp, cond):
        k = ids[g][disp]
        cp = pltpu.make_async_remote_copy(src_ref=src, dst_ref=at(disp, p.c, g), send_sem=sib_send.at[k], recv_sem=sib_recv.at[k],
                                          device_id=p.ids["c"], device_id_type=MESH)
        when(cond, cp.start)
        waits.append((cond, cp))

    zero = (0, 0, 0)
    for g, tree in enumerate(trees):
        src = mine.at[pl.ds(plan[g][1], plan[g][2])]
        for nd, way in tree[zero]:
            push((src, at(zero, p.c, g)), g, nd, way, None)
    own = pltpu.make_async_copy(mine, out.at[((p.x,) if with_x else ()) + (p.z, p.y, p.c)], own_sem)
    own.start()
    for g in range(len(plan)):
        share(mine.at[pl.ds(plan[g][1], plan[g][2])], g, zero, None)
    events = sorted((hops(d), g, d) for g, t in enumerate(trees) for d in t if d != zero)
    for _, g, d in events:
        cond = p.there(d)
        blk = at(d, p.c, g)
        got = pltpu.make_async_remote_copy(src_ref=blk, dst_ref=blk, send_sem=send.at[ids[g][d]], recv_sem=recv.at[ids[g][d]],
                                           device_id=p.ids["c"], device_id_type=MESH)
        when(cond, got.wait_recv)
        for nd, way in trees[g][d]:
            push((blk, blk), g, nd, way, cond)
        share(blk, g, d, cond)
    for g, t in enumerate(trees):
        for d in t:
            blk = at(d, 1 - p.c, g)
            got = pltpu.make_async_remote_copy(src_ref=blk, dst_ref=blk, send_sem=sib_send.at[ids[g][d]], recv_sem=sib_recv.at[ids[g][d]],
                                               device_id=p.ids["c"], device_id_type=MESH)
            when(p.there(d), got.wait_recv)
    own.wait()
    for c, cp in waits:
        when(c, cp.wait_send)


def gather(shard, plan, with_x, ident, space=pl.ANY):
    rows, width = shard.shape
    lead = (2, 4, 2, 2) if with_x else (4, 2, 2)
    sems = pltpu.SemaphoreType.DMA((32 * len(plan),))
    return pl.pallas_call(
        partial(gather_kernel, plan, with_x),
        out_shape=jax.ShapeDtypeStruct(lead + (rows, width), shard.dtype),
        in_specs=[pl.BlockSpec(memory_space=space)],
        out_specs=pl.BlockSpec(memory_space=space),
        scratch_shapes=[sems, sems, sems, sems, pltpu.SemaphoreType.DMA],
        compiler_params=pltpu.CompilerParams(collective_id=ident, has_side_effects=True, vmem_limit_bytes=60 << 20),
        name=f"gather_{ident}",
    )(shard)


def add_rows(acc, got, step=80):
    n = acc.shape[0]
    while n % step:
        step -= 16

    def body(i, _):
        r = pl.ds(pl.multiple_of(i * step, step), step)
        acc[r, :] = acc[r, :] + got[r, :]
        return 0

    lax.fori_loop(0, n // step, body, 0)


def total_steps(p, src, out, mid, line, send, recv):
    waits = []

    def move(k, a, b, way, cond=None):
        cp = pltpu.make_async_remote_copy(src_ref=a, dst_ref=b, send_sem=send.at[k], recv_sem=recv.at[k],
                                          device_id=p.ids[way], device_id_type=MESH)
        when(cond, cp.start)
        waits.append((cond, cp))

    def land(k, b, cond=None):
        when(cond, pltpu.make_async_remote_copy(src_ref=b, dst_ref=b, send_sem=send.at[k], recv_sem=recv.at[k],
                                                device_id=p.ids["c"], device_id_type=MESH).wait_recv)

    now = src
    for k, way in enumerate(("c", "x", "y")):
        move(k, now, mid.at[k], way)
        yield
        land(k, mid.at[k])
        nxt = mid.at[3 + k] if k < 2 else line.at[p.z]
        nxt[...] = now[...] + mid[k]
        now = nxt
    for k in range(3):
        lo, hi = jnp.maximum(p.z - k, 0), jnp.minimum(p.z + k, 3)
        if k > 0:
            land(2 + k, line.at[lo], p.z >= k)
            land(5 + k, line.at[hi], p.z + k <= 3)
        move(3 + k, line.at[lo], line.at[lo], "z+", jnp.logical_and(p.z >= k, p.z < 3))
        move(6 + k, line.at[hi], line.at[hi], "z-", jnp.logical_and(p.z + k <= 3, p.z > 0))
        yield
    land(5, line.at[jnp.maximum(p.z - 3, 0)], p.z >= 3)
    land(8, line.at[jnp.minimum(p.z + 3, 3)], p.z <= 0)
    out[...] = (line[0] + line[1]) + (line[2] + line[3])
    for c, cp in waits:
        when(c, cp.wait_send)


def reduce_kernel(plan, with_x, small, src, *rest):
    n = len(plan)
    steps = iter(())
    if small:
        small_src, out, small_out = rest[:3]
        mid, line, small_send, small_recv = rest[-4:]
        rest = rest[3:-4]
    else:
        out, rest = rest[0], rest[1:]
    accs, halves, bufs = rest[:n], rest[n:2 * n], rest[2 * n:3 * n]
    send, recv, sib_send, sib_recv, loads = rest[3 * n:]
    p = Place()
    p.greet(["c", "y", "x"] if with_x else ["c", "y"])
    if small:
        steps = total_steps(p, small_src, small_out, mid, line, small_send, small_recv)
    trees = [spread(o) for o, _, _ in plan]
    ids = [{d: i + 32 * g for i, d in enumerate(sorted(t))} for g, t in enumerate(trees)]
    waits = []
    zero = (0, 0, 0)

    def ix(disp):
        t, z, y = p.at(disp)
        return ((t,) if with_x else ()) + (z, y)

    events = sorted((-hops(d), g, d) for g, t in enumerate(trees) for d in t)
    for _, g, d in events:
        cond = p.there(d)
        k = ids[g][d]
        rows = pl.ds(plan[g][1], plan[g][2])
        cp = pltpu.make_async_remote_copy(
            src_ref=src.at[ix(d) + (1 - p.c, rows)], dst_ref=halves[g].at[ix(d)], send_sem=sib_send.at[k],
            recv_sem=sib_recv.at[k], device_id=p.ids["c"], device_id_type=MESH)
        ld = pltpu.make_async_copy(src.at[ix(d) + (p.c, rows)], accs[g].at[ix(d)], loads.at[k])

        def go(cp=cp, ld=ld):
            cp.start()
            ld.start()
        when(cond, go)
        waits.append((cond, cp))
    for number, (_, g, d) in enumerate(events):
        k = ids[g][d]
        rows = pl.ds(plan[g][1], plan[g][2])
        if number % 8 == 0:
            next(steps, None)

        def step(g=g, d=d, k=k, rows=rows):
            acc = accs[g].at[ix(d)]
            pltpu.make_async_copy(src.at[ix(d) + (p.c, rows)], acc, loads.at[k]).wait()
            half = halves[g].at[ix(d)]
            pltpu.make_async_remote_copy(src_ref=half, dst_ref=half, send_sem=sib_send.at[k], recv_sem=sib_recv.at[k],
                                         device_id=p.ids["c"], device_id_type=MESH).wait_recv()
            add_rows(acc, half)
            for nd, way in trees[g][d]:
                kk = ids[g][nd]
                buf = bufs[g].at[kk - 32 * g]

                def take(acc=acc, buf=buf, kk=kk):
                    pltpu.make_async_remote_copy(src_ref=buf, dst_ref=buf, send_sem=send.at[kk], recv_sem=recv.at[kk],
                                                 device_id=p.ids["c"], device_id_type=MESH).wait_recv()
                    add_rows(acc, buf)
                if way == "z+":
                    when(p.z < 3, take)
                elif way == "z-":
                    when(p.z > 0, take)
                else:
                    take()
        cond = p.there(d)
        when(cond, step)
        if d != zero:
            way = [w for t in trees[g].values() for nd, w in t if nd == d][0]
            acc = accs[g].at[ix(d)]
            cp = pltpu.make_async_remote_copy(src_ref=acc, dst_ref=bufs[g].at[k - 32 * g], send_sem=send.at[k], recv_sem=recv.at[k],
                                              device_id=p.ids[BACK[way]], device_id_type=MESH)
            when(cond, cp.start)
            waits.append((cond, cp))
        else:
            out[rows, :] = accs[g][ix(d)]
    for _ in steps:
        pass
    for c, cp in waits:
        when(c, cp.wait_send)


def reduce_scatter(whole, plan, with_x, ident, small=None):
    rows, width = whole.shape[-2:]
    dt = whole.dtype
    lead = (2, 4, 2) if with_x else (4, 2)
    blocks = [pltpu.VMEM(lead + (num, width), dt) for _, _, num in plan]
    bufs = [pltpu.VMEM((len(spread(o)), num, width), dt) for o, _, num in plan]
    sems = pltpu.SemaphoreType.DMA((32 * len(plan),))
    vmem = pl.BlockSpec(memory_space=pltpu.VMEM)
    out = jax.ShapeDtypeStruct((rows, width), dt)
    scratch = blocks + blocks + bufs + [sems] * 5
    if small is not None:
        out = (out, jax.ShapeDtypeStruct(small.shape, small.dtype))
        scratch += [pltpu.VMEM((5,) + small.shape, small.dtype), pltpu.VMEM((4,) + small.shape, small.dtype)]
        scratch += [pltpu.SemaphoreType.DMA((9,))] * 2
    return pl.pallas_call(
        partial(reduce_kernel, plan, with_x, small is not None),
        out_shape=out,
        in_specs=[pl.BlockSpec(memory_space=pl.ANY)] + ([] if small is None else [vmem]),
        out_specs=vmem if small is None else (vmem, vmem),
        scratch_shapes=scratch,
        compiler_params=pltpu.CompilerParams(collective_id=ident, has_side_effects=True, vmem_limit_bytes=62 << 20),
        name=f"reduce_{ident}",
    )(*((whole,) if small is None else (whole, small)))


PLAN_ALL = [("zxy", 0, 640), ("zyx", 640, 640), ("xzy", 1280, 640), ("yzx", 1920, 720)]
PLAN_DP = [("zy", 0, 656)]
SHARD_UNITS = 656
PANEL = 128


def layout(shapes, shards):
    table = []
    unit_at, row_at = 0, 0
    for rows, cols in shapes:
        rb, panels = rows // shards, cols // PANEL
        units = rb * cols // 512
        padded = -(-rb // 16) * 16
        table.append((rb, panels, units, unit_at, row_at, padded))
        unit_at += units
        row_at += padded * panels
    return table, unit_at, row_at


def unit_places(units, table, shards):
    place = jnp.zeros_like(units)
    for rb, panels, n, first, _, _ in table:
        lo = first * shards
        v = units - lo
        here = (v // n) * SHARD_UNITS + first + v % n
        place = jnp.where(v >= 0, here, place)
    return place


def own_units(owners, mine, capacity):
    count = owners.shape[0] // 128
    hit = (owners[:, 0] == mine).reshape(count, 128)
    lane = jnp.arange(128)
    tri = (lane[:, None] <= lane[None, :]).astype(jnp.bfloat16)
    within = jnp.dot(hit.astype(jnp.bfloat16), tri, preferred_element_type=jnp.float32)
    totals = within[:, 127].astype(jnp.int32)
    upto = jnp.sum(jnp.where(jnp.arange(count)[:, None] >= jnp.arange(count)[None, :], totals[None, :], 0), axis=1)
    slot = jnp.arange(capacity, dtype=jnp.int32)
    block = jnp.sum((upto[None, :] <= slot[:, None]).astype(jnp.int32), axis=1)
    pick = block[:, None] == jnp.arange(count)[None, :]
    before = jnp.sum(jnp.where(pick, (upto - totals)[None, :], 0), axis=1)
    row = jnp.dot(pick.astype(jnp.bfloat16), within.astype(jnp.bfloat16), preferred_element_type=jnp.float32)
    rank = (slot - before).astype(jnp.float32)
    at = jnp.sum((row <= rank[:, None]).astype(jnp.int32), axis=1)
    return block * 128 + at, slot < upto[count - 1]


def to_panels(shard, table):
    out = []
    for rb, panels, n, first, _, padded in table:
        m = shard[first:first + n].reshape(rb, panels, PANEL).transpose(1, 0, 2)
        if padded > rb:
            m = jnp.pad(m, ((0, 0), (0, padded - rb), (0, 0)))
        out.append(m.reshape(panels * padded, PANEL))
    return jnp.concatenate(out, axis=0)


def from_panels(rows, table):
    out = []
    for rb, panels, n, first, at, padded in table:
        m = rows[at:at + panels * padded].reshape(panels, padded, PANEL)[:, :rb]
        out.append(m.transpose(1, 0, 2).reshape(n, 512))
    out = jnp.concatenate(out, axis=0)
    return jnp.pad(out, ((0, SHARD_UNITS - out.shape[0]), (0, 0)))


BY_ROWS = (1, 3, 6, 8)


def position_table():
    cols = []
    for width in (DE, DD):
        side = width // 16 * 6
        parts = (width - 2 * side, side, side)
        tab = np.zeros((48, width), np.float64)
        col = 0
        for i, n in enumerate(parts):
            half = n // 2
            freq = 1.0 / 10000.0 ** (np.arange(half) / half)
            ang = np.arange(16)[:, None] * freq[None, :]
            tab[16 * i:16 * i + 16, col:col + n] = np.concatenate([np.sin(ang), np.cos(ang)], axis=1)
            col += n
        cols.append(tab)
    left = np.concatenate(cols, axis=1).astype(np.float32)
    terms = []
    for _ in range(3):
        terms.append(left.astype(ml_dtypes.bfloat16))
        left = left - terms[-1].astype(np.float32)
    return np.stack(terms)


def dot(a, b):
    return jnp.dot(a, b, preferred_element_type=jnp.float32)


def dot_nt(a, b):
    return lax.dot_general(a, b, (((1,), (1,)), ((), ())), preferred_element_type=jnp.float32)


def dot_tn(a, b):
    return lax.dot_general(a, b, (((0,), (0,)), ((), ())), preferred_element_type=jnp.float32)


def lanes(i, n=128):
    return pl.ds(pl.multiple_of(i * n, n), n)


def ln_parts(x):
    c = x - jnp.mean(x, axis=-1, keepdims=True)
    inv = lax.rsqrt(jnp.mean(c * c, axis=-1, keepdims=True) + NORM_EPS)
    return c * inv, inv


def ln_back(up, m, inv, gain):
    s = up * gain
    a = jnp.mean(s, axis=-1, keepdims=True)
    b = jnp.mean(s * m, axis=-1, keepdims=True)
    return inv * (s - a - m * b), jnp.sum(up * m, axis=0, keepdims=True), jnp.sum(up, axis=0, keepdims=True)


class Block:
    def __init__(self, width, heads, size, hidden, first, table, col):
        self.width, self.heads, self.size, self.hidden, self.col = width, heads, size, hidden, col
        self.q, self.o, self.a, self.b = table[first:first + 4]
        self.part = heads // 2 * size
        self.per = 128 // size


def panel(w, t, mat, g, lo=0, num=16):
    rb, _, _, _, at, padded = mat
    rows = pl.ds(pl.multiple_of(at + g * padded, 16), padded)
    v = w[t, lo:lo + num, rows, :] if isinstance(lo, int) else w[t, pl.ds(lo, num), rows, :]
    if padded > rb:
        v = v.astype(jnp.float32)[:, :rb].reshape(num * rb, 128).astype(jnp.bfloat16)
        return v
    return v.reshape(num * rb, 128)


def pair(w, mat, g):
    return jnp.concatenate([panel(w, 0, mat, g), panel(w, 1, mat, g)], axis=1)


def block_fwd(b, x, xo, w, gains, biases, same, n1, proj, p, att, ow, m1, i1, n2, m2, i2, act, slope):
    cols = slice(b.col, b.col + b.width)
    m, inv = ln_parts(x[...])
    m1[...] = m
    i1[...] = inv
    n1[...] = (m * gains[0:1, cols] + biases[0:1, cols]).astype(jnp.bfloat16)
    gq = b.q[1]

    def qkv(g, _):
        r = dot(n1[...], pair(w, b.q, g)).astype(jnp.bfloat16)
        proj[:, lanes(g)] = r[:, :128]
        proj[:, lanes(gq + g)] = r[:, 128:]
        return 0

    lax.fori_loop(0, gq, qkv, 0)
    np_ = b.part // 128
    lane = lax.broadcasted_iota(jnp.int32, (256, 128), 1)
    masks = [lane // b.size == i for i in range(b.per)]

    def heads(i, _):
        t, j = i // np_, i % np_
        q = proj[:, lanes(t * gq + j)]
        k = proj[:, lanes(t * gq + np_ + j)]
        v = proj[:, lanes(t * gq + 2 * np_ + j)]
        total = jnp.zeros((256, 128), jnp.float32)
        for h in range(b.per):
            z = dot_nt(jnp.where(masks[h], q, 0), k) * b.size ** (-0.5) + same
            e = jnp.exp(z - jnp.max(z, axis=-1, keepdims=True))
            s = e / jnp.sum(e, axis=-1, keepdims=True)
            p[i * b.per + h] = s
            total = total + dot(s.astype(jnp.bfloat16), jnp.where(masks[h], v, 0))
        att[:, lanes(i)] = total.astype(jnp.bfloat16)
        return 0

    lax.fori_loop(0, 2 * np_, heads, 0)
    for t in range(2):
        for g in range(b.width // 128):
            ow[t, :, g * 128:(g + 1) * 128] = panel(w, t, b.o, g)
    x1 = x[...] + dot(att[:, :b.part], ow[0]) + dot(att[:, b.part:], ow[1])
    xo[...] = x1
    m, inv = ln_parts(x1)
    m2[...] = m
    i2[...] = inv
    n2[...] = (m * gains[1:2, cols] + biases[1:2, cols]).astype(jnp.bfloat16)
    ga = b.a[1]

    def up(g, _):
        h = dot(n2[...], pair(w, b.a, g))
        big = 0.5 * (1.0 + lax.erf(h * 0.7071067811865476))
        act_v = (h * big).astype(jnp.bfloat16)
        dens = big + h * (0.3989422804014327 * jnp.exp(-0.5 * h * h))
        act[:, lanes(g)] = act_v[:, :128]
        act[:, lanes(ga + g)] = act_v[:, 128:]
        slope[:, lanes(g)] = dens[:, :128]
        slope[:, lanes(ga + g)] = dens[:, 128:]
        return 0

    lax.fori_loop(0, ga, up, 0)
    half = b.hidden // 2

    def down(g, _):
        w0 = jnp.concatenate([panel(w, 0, b.b, 2 * g), panel(w, 0, b.b, 2 * g + 1)], axis=1)
        w1 = jnp.concatenate([panel(w, 1, b.b, 2 * g), panel(w, 1, b.b, 2 * g + 1)], axis=1)
        xo[:, lanes(g, 256)] += dot(act[:, :half], w0) + dot(act[:, half:], w1)
        return 0

    lax.fori_loop(0, b.width // 256, down, 0)


def block_bwd(b, dr, w, gains, same, n1, proj, p, att, ow, m1, i1, n2, m2, i2, act, slope,
              r, dh, r1, dp_out, acc, da, norm_out):
    cols = slice(b.col, b.col + b.width)
    r[...] = dr[...].astype(jnp.bfloat16)
    half = b.hidden // 2
    rb = b.b[0]
    gb = b.width // 128
    num = 4

    def hidden(i, _):
        t, lo = i // (16 // num), (i % (16 // num)) * num
        wc = jnp.concatenate([panel(w, t, b.b, g, lo, num) for g in range(gb)], axis=1)
        at = lanes(i, num * rb)
        dh[:, at] = (dot_nt(r[...], wc) * slope[:, at]).astype(jnp.bfloat16)
        return 0

    lax.fori_loop(0, 2 * (16 // num), hidden, 0)
    ga = b.a[1]
    acc[...] = jnp.zeros_like(acc)

    def up(g, _):
        d = jnp.concatenate([dh[:, lanes(g)], dh[:, lanes(ga + g)]], axis=1)
        acc[...] += dot_nt(d, pair(w, b.a, g))
        return 0

    lax.fori_loop(0, ga, up, 0)
    dx, dg, db = ln_back(acc[...], m2[...], i2[...], gains[1:2, cols])
    norm_out[1:2, cols] = dg
    norm_out[3:4, cols] = db
    dx1 = dr[...] + dx
    dr[...] = dx1
    r1[...] = dx1.astype(jnp.bfloat16)
    for t in range(2):
        da[:, t * b.part:(t + 1) * b.part] = dot_nt(r1[...], ow[t]).astype(jnp.bfloat16)
    gq = b.q[1]
    np_ = b.part // 128
    lane = lax.broadcasted_iota(jnp.int32, (256, 128), 1)
    masks = [lane // b.size == i for i in range(b.per)]
    scale = b.size ** (-0.5)

    def heads(i, _):
        t, j = i // np_, i % np_
        q = proj[:, lanes(t * gq + j)]
        k = proj[:, lanes(t * gq + np_ + j)]
        v = proj[:, lanes(t * gq + 2 * np_ + j)]
        up_ = da[:, lanes(i)]
        dq = jnp.zeros((256, 128), jnp.float32)
        dk = jnp.zeros((256, 128), jnp.float32)
        dv = jnp.zeros((256, 128), jnp.float32)
        for h in range(b.per):
            s = p[i * b.per + h]
            u = jnp.where(masks[h], up_, 0)
            dp = dot_nt(u, v)
            dv = dv + dot_tn(s.astype(jnp.bfloat16), u)
            t1 = s * dp
            dz = (t1 - s * jnp.sum(t1, axis=-1, keepdims=True)).astype(jnp.bfloat16)
            dq = dq + dot(dz, jnp.where(masks[h], k, 0))
            dk = dk + dot_tn(dz, jnp.where(masks[h], q, 0))
        dp_out[:, lanes(t * gq + j)] = (dq * scale).astype(jnp.bfloat16)
        dp_out[:, lanes(t * gq + np_ + j)] = (dk * scale).astype(jnp.bfloat16)
        dp_out[:, lanes(t * gq + 2 * np_ + j)] = dv.astype(jnp.bfloat16)
        return 0

    lax.fori_loop(0, 2 * np_, heads, 0)
    acc[...] = jnp.zeros_like(acc)

    def qkv(g, _):
        d = jnp.concatenate([dp_out[:, lanes(g)], dp_out[:, lanes(gq + g)]], axis=1)
        acc[...] += dot_nt(d, pair(w, b.q, g))
        return 0

    lax.fori_loop(0, gq, qkv, 0)
    dx, dg, db = ln_back(acc[...], m1[...], i1[...], gains[0:1, cols])
    norm_out[0:1, cols] = dg
    norm_out[2:3, cols] = db
    dr[...] = dr[...] + dx


ACTS = (("n1", DE), ("att", DE), ("n2", DE), ("act", FFE), ("low", DE), ("n1", DD), ("att", DD), ("n2", DD), ("act", FFD))
GRADS = (3 * DE, DE, FFE, DE, DD, 3 * DD, DD, FFD, DD)


def chain_kernel(table, tok, pos, tile_r, tile_c, gains, biases, cot, tab, w, *refs):
    dec, dx0, norm_out = refs[:3]
    acts, grads = refs[3:12], refs[12:21]
    (pe, pd, se, sd, proj_e, proj_d, da_e, da_d, ow_e, ow_d, m1e, m2e, m1d, m2d, i1e, i2e, i1d, i2d,
     x, y, acc_e, acc_d) = refs[21:]
    enc_b = Block(DE, HE, HDE, FFE, 0, table, 0)
    dec_b = Block(DD, HD, HDD, FFD, 5, table, DE)
    em = table[4]
    lane = lax.broadcasted_iota(jnp.int32, (256, 48), 1)
    hot = jnp.logical_or(jnp.logical_or(lane == pos[:, 0:1], lane == pos[:, 1:2] + 16), lane == pos[:, 2:3] + 32)
    hot = jnp.where(hot, 1.0, 0.0).astype(jnp.bfloat16)
    same = jnp.where(tile_c[...] == tile_r[...], 0.0, MASK_FILL)
    x[...] = tok[...].astype(jnp.float32) + (dot(hot, tab[0, :, :DE]) + dot(hot, tab[1, :, :DE]) + dot(hot, tab[2, :, :DE]))
    n1e, ae, n2e, ue, low, n1d, ad, n2d, ud = acts
    dpe, r1e, dhe, re, dlow, dpd, r1d, dhd, rd = grads
    block_fwd(enc_b, x, dx0, w, gains, biases, same, n1e, proj_e, pe, ae, ow_e, m1e, i1e, n2e, m2e, i2e, ue, se)
    low[...] = dx0[...].astype(jnp.bfloat16)
    for g in range(2):
        v = dot(low[...], pair(w, em, g)).astype(jnp.bfloat16).astype(jnp.float32)
        y[:, g * 128:(g + 1) * 128] = v[:, :128]
        y[:, 256 + g * 128:256 + (g + 1) * 128] = v[:, 128:]
    y[...] += dot(hot, tab[0, :, DE:]) + dot(hot, tab[1, :, DE:]) + dot(hot, tab[2, :, DE:])
    block_fwd(dec_b, y, dec, w, gains, biases, same, n1d, proj_d, pd, ad, ow_d, m1d, i1d, n2d, m2d, i2d, ud, sd)
    y[...] = cot[...]
    block_bwd(dec_b, y, w, gains, same, n1d, proj_d, pd, ad, ow_d, m1d, i1d, n2d, m2d, i2d, ud, sd,
              rd, dhd, r1d, dpd, acc_d, da_d, norm_out)
    dlow[...] = y[...].astype(jnp.bfloat16)
    for g in range(2):
        d = jnp.concatenate([dlow[:, g * 128:(g + 1) * 128], dlow[:, 256 + g * 128:256 + (g + 1) * 128]], axis=1)
        v = dot_nt(d, pair(w, em, g))
        if g == 0:
            dx0[...] = v
        else:
            dx0[...] += v
    block_bwd(enc_b, dx0, w, gains, same, n1e, proj_e, pe, ae, ow_e, m1e, i1e, n2e, m2e, i2e, ue, se,
              re, dhe, r1e, dpe, acc_e, da_e, norm_out)


def chain(tokens, pos, tile, gains, biases, cot, full, table):
    f32, bf16 = jnp.float32, jnp.bfloat16
    S = jax.ShapeDtypeStruct
    outs = [S((256, DD), f32), S((256, DE), f32), S((4, DE + DD), f32)]
    outs += [S((256, n), bf16) for _, n in ACTS] + [S((256, n), bf16) for n in GRADS]
    V = pltpu.VMEM
    scratch = [V((HE, 256, 256), f32), V((HD, 256, 256), f32), V((256, FFE), f32), V((256, FFD), f32),
               V((256, 3 * DE), bf16), V((256, 3 * DD), bf16), V((256, DE), bf16), V((256, DD), bf16),
               V((2, DE // 2, DE), bf16), V((2, DD // 2, DD), bf16),
               V((256, DE), f32), V((256, DE), f32), V((256, DD), f32), V((256, DD), f32)] + [V((256, 1), f32)] * 4 + [
               V((256, DE), f32), V((256, DD), f32), V((256, DE), f32), V((256, DD), f32)]
    spec = pl.BlockSpec(memory_space=pltpu.VMEM)
    args = (tokens, pos.T, tile[None, :], tile[:, None], gains, biases, cot, jnp.asarray(position_table()),
            full.reshape(2, 16, full.shape[-2], 128))
    return pl.pallas_call(
        partial(chain_kernel, table), out_shape=outs, in_specs=[spec] * len(args), out_specs=[spec] * len(outs),
        scratch_shapes=scratch, compiler_params=pltpu.CompilerParams(vmem_limit_bytes=62 << 20), name="chain",
        cost_estimate=pl.CostEstimate(flops=11_000_000_000, bytes_accessed=40_000_000, transcendentals=5_000_000),
    )(*args)


def grad_panels(table, m, act, grad, turned, put):
    mat = table[m]
    rb, panels, padded = mat[0], mat[1], mat[5]
    count = act.shape[1]

    def turn(i, _):
        turned[pl.ds(pl.multiple_of(i * 128, 128), 128), :] = act[:, lanes(i)].T
        return 0

    lax.fori_loop(0, count // 128, turn, 0)

    def place(t, g, v):
        if padded > rb:
            v = v.reshape(16, rb, 128)
            v = jnp.concatenate([v, jnp.zeros((16, padded - rb, 128), jnp.float32)], axis=1).astype(jnp.bfloat16)
        else:
            v = v.astype(jnp.bfloat16).reshape(16, rb, 128)
        put(t, g, v)

    if m in BY_ROWS:
        half = count // 2

        def body(i, _):
            t, g = i // (panels // 2), i % (panels // 2)
            v = dot(turned[pl.ds(pl.multiple_of(t * half, 128), half), :], grad[:, lanes(g, 256)])
            place(t, 2 * g, v[:, :128])
            place(t, 2 * g + 1, v[:, 128:])
            return 0

        lax.fori_loop(0, panels, body, 0)
    else:
        def body(g, _):
            d = jnp.concatenate([grad[:, lanes(g)], grad[:, lanes(panels + g)]], axis=1)
            v = dot(turned[:count, :], d)
            place(0, g, v[:, :128])
            place(1, g, v[:, 128:])
            return 0

        lax.fori_loop(0, panels, body, 0)


def grads_kernel(table, *refs):
    acts, grads, out, turned = refs[:9], refs[9:18], refs[18], refs[19]
    for m in range(9):
        at, padded = table[m][4], table[m][5]

        def put(t, g, v):
            out[t, :, pl.ds(pl.multiple_of(at + g * padded, 16), padded), :] = v

        grad_panels(table, m, acts[m], grads[m], turned, put)


def weight_grads(acts, grads, table, rows):
    spec = pl.BlockSpec(memory_space=pltpu.VMEM)
    return pl.pallas_call(
        partial(grads_kernel, table), out_shape=jax.ShapeDtypeStruct((2, 16, rows, 128), jnp.bfloat16),
        in_specs=[spec] * 18, out_specs=spec, scratch_shapes=[pltpu.VMEM((FFE, 256), jnp.bfloat16)],
        compiler_params=pltpu.CompilerParams(vmem_limit_bytes=62 << 20), name="weight_grads",
        cost_estimate=pl.CostEstimate(flops=5_500_000_000, bytes_accessed=32_000_000, transcendentals=0),
    )(*acts, *grads)


def swap(v):
    return lax.ppermute(v, "tensor", [(0, 1), (1, 0)])


def sequence_device(tokens_in, positions, segment_ids, owners, master, first_moment, second_moment, norm_gains,
                    norm_biases, norm_first, norm_second, cotangent):
    t = lax.axis_index("tensor")
    shapes = weight_shapes(2)
    table, _, _ = layout(shapes, 16)

    def whole(v, axis):
        own = lax.dynamic_index_in_dim(v, t, axis, keepdims=False)
        other = swap(lax.dynamic_index_in_dim(v, 1 - t, axis, keepdims=False))
        at = 1 if axis == 1 else 0
        return jnp.concatenate([jnp.where(t == 0, own, other), jnp.where(t == 0, other, own)], axis=at)

    def halves(v):
        half = v.shape[0] // 2
        own = lax.dynamic_slice_in_dim(v, t * half, half, 0)
        other = swap(lax.dynamic_slice_in_dim(v, (1 - t) * half, half, 0))
        return jnp.stack([jnp.where(t == 0, own, other), jnp.where(t == 0, other, own)])

    tokens, cot, pos = whole(tokens_in, 0), whole(cotangent, 0), whole(positions, 1)
    tile = lax.dynamic_index_in_dim(segment_ids, t, 0, keepdims=False)[0]

    unit, used = own_units(owners, lax.axis_index("dp"), master.shape[0])
    place = unit_places(unit, table, 16)
    parts = jnp.zeros((16 * SHARD_UNITS, 512), jnp.bfloat16)
    parts = parts.at[jnp.where(used, place, 16 * SHARD_UNITS)].set(master.astype(jnp.bfloat16), mode="drop", unique_indices=True)
    shard = reduce_scatter(parts.reshape(4, 2, 2, SHARD_UNITS, 512), PLAN_DP, False, 1)
    full = gather(to_panels(shard, table), PLAN_ALL, True, 2)
    kept = chain(tokens, pos, tile, norm_gains, norm_biases, cot, full, table)
    decoded, dx0, norms = kept[:3]
    grads = weight_grads(kept[3:12], kept[12:21], table, full.shape[-2])
    summed, norm_total = reduce_scatter(grads.reshape(full.shape), PLAN_ALL, True, 3, norms)
    spread_out = gather(from_panels(summed, table), PLAN_DP, False, 4).reshape(16 * SHARD_UNITS, 512)
    reduced = jnp.where(used[:, None], jnp.take(spread_out, jnp.clip(place, 0, 16 * SHARD_UNITS - 1), axis=0).astype(jnp.float32), 0.0)
    new_master, new_first, new_second = adamw(master, reduced, first_moment, second_moment, WEIGHT_DECAY, LEARN_RATE)
    norm_params = jnp.concatenate([norm_gains, norm_biases], axis=0)
    new_norms, norm_one_new, norm_two_new = adamw(norm_params, norm_total, norm_first, norm_second, 0.0, NORM_RATE)
    return (halves(decoded), halves(dx0), new_master, new_first, new_second, new_norms, norm_one_new, norm_two_new)


def solution(mesh):
    step = sequence_device if (mesh.shape["dp"], mesh.shape["tensor"]) == (16, 2) else per_device
    return jax.shard_map(
        step,
        mesh=mesh,
        in_specs=(
            P(None, ("dp", "tensor"), None),
            P(None, None, ("dp", "tensor")),
            P(None, "dp", None),
            P(),
            P("dp", "tensor"),
            P("dp", "tensor"),
            P("dp", "tensor"),
            P(),
            P(),
            P(),
            P(),
            P(None, ("dp", "tensor"), None),
        ),
        out_specs=(
            P(None, ("dp", "tensor"), None),
            P(None, ("dp", "tensor"), None),
            P("dp", "tensor"),
            P("dp", "tensor"),
            P("dp", "tensor"),
            P(),
            P(),
            P(),
        ),
        check_vma=False,
    )
```

```python
from functools import partial

import jax
import jax.numpy as jnp
import ml_dtypes
import numpy as np
from jax import lax
from jax.experimental import pallas as pl
from jax.experimental.pallas import tpu as pltpu
from jax.sharding import PartitionSpec as P

DE = 768
HE = 12
HDE = 64
FFE = 3072
DD = 512
HD = 16
HDD = 32
FFD = 2048
STEP = 10


NORM_EPS = 1e-06
BETA_ONE = 0.5
BETA_TWO = 0.5
LEARN_RATE = 0.03
NORM_RATE = 0.3
WEIGHT_DECAY = 0.05
ADAM_EPS = 1e-08
MASK_FILL = -1000000000.0


def sincos_part(coordinate, part_width):
    halfway = part_width // 2
    frequency = 1.0 / 10000.0 ** (jnp.arange(halfway, dtype=jnp.float32) / halfway)
    angles = coordinate.astype(jnp.float32)[:, None] * frequency[None, :]
    return jnp.concatenate([jnp.sin(angles), jnp.cos(angles)], axis=1)


def sincos_embed(positions, model_width):
    side_width = model_width // 16 * 6
    first_width = model_width - 2 * side_width
    return jnp.concatenate(
        [
            sincos_part(positions[0], first_width),
            sincos_part(positions[1], side_width),
            sincos_part(positions[2], side_width),
        ],
        axis=1,
    )


def slot_table(owners, devices, capacity):
    owner_ids = owners[:, 0]
    onehot = (owner_ids[:, None] == jnp.arange(devices, dtype=jnp.int32)[None, :]).astype(jnp.int32)
    before = jnp.cumsum(onehot, axis=0) - onehot
    owner_rank = jnp.sum(before * onehot, axis=1)
    return owner_ids * capacity + owner_rank


def weight_shapes(tensor_count):
    enc_heads = HE // tensor_count
    dec_heads = HD // tensor_count
    return [
        (DE, 3 * enc_heads * HDE),
        (enc_heads * HDE, DE),
        (DE, FFE // tensor_count),
        (FFE // tensor_count, DE),
        (DE, DD // tensor_count),
        (DD, 3 * dec_heads * HDD),
        (dec_heads * HDD, DD),
        (DD, FFD // tensor_count),
        (FFD // tensor_count, DD),
    ]


def split_flat(flat_vector, shapes):
    pieces = []
    offset = 0
    for matrix_shape in shapes:
        length = matrix_shape[0] * matrix_shape[1]
        pieces.append(flat_vector[offset : offset + length].reshape(matrix_shape))
        offset += length
    return pieces


def adamw(weights, gradient, moment_one, moment_two, decay_rate, step_rate):
    one_new = BETA_ONE * moment_one + (1.0 - BETA_ONE) * gradient
    two_new = BETA_TWO * moment_two + (1.0 - BETA_TWO) * gradient * gradient
    one_hat = one_new / (1.0 - BETA_ONE**STEP)
    two_hat = two_new / (1.0 - BETA_TWO**STEP)
    weights_new = weights - step_rate * (
        one_hat / (jnp.sqrt(two_hat) + ADAM_EPS) + decay_rate * weights
    )
    return (weights_new, one_new, two_new)


def norm_forward(values, gain_row, bias_row):
    center = values - jnp.mean(values, axis=-1, keepdims=True)
    spread = jnp.mean(center * center, axis=-1, keepdims=True)
    inverse = lax.rsqrt(spread + NORM_EPS)
    normed = center * inverse
    return (normed * gain_row + bias_row, (normed, inverse))


def norm_backward(upstream, stored, gain_row):
    normed, inverse = stored
    scaled = upstream * gain_row
    mean_one = jnp.mean(scaled, axis=-1, keepdims=True)
    mean_two = jnp.mean(scaled * normed, axis=-1, keepdims=True)
    return (
        inverse * (scaled - mean_one - normed * mean_two),
        jnp.sum(upstream * normed, axis=0),
        jnp.sum(upstream, axis=0),
    )


def inner_rows(left_side, right_side):
    return lax.dot_general(
        left_side, right_side, (((0,), (0,)), ((), ())), preferred_element_type=jnp.float32
    )


def times_transpose(left_side, right_side):
    return lax.dot_general(
        left_side, right_side, (((1,), (1,)), ((), ())), preferred_element_type=jnp.float32
    )


def gather_rows(values):
    return lax.all_gather(values, "tensor", axis=0, tiled=True)


def gather_grads(values):
    return lax.all_gather(values, "tensor", axis=0, tiled=True)


def branch_rows(values, weight):
    return lax.psum_scatter(
        jnp.dot(values, weight, preferred_element_type=jnp.float32).astype(jnp.bfloat16),
        "tensor",
        scatter_dimension=0,
        tiled=True,
    ).astype(jnp.float32)


def input_rows(values, weight):
    return lax.psum_scatter(
        times_transpose(values, weight).astype(jnp.bfloat16),
        "tensor",
        scatter_dimension=0,
        tiled=True,
    ).astype(jnp.float32)


def block_scores(queries, key_rows, mask_bias, block_start, block_rows, head_size):
    scores = jnp.einsum(
        "qhd,khd->hqk", queries, key_rows, preferred_element_type=jnp.float32
    ) * head_size ** (-0.5)
    return scores + mask_bias[None, block_start : block_start + block_rows]


def attention_forward(gathered, w_qkv, head_count, head_size, mask_bias):
    length = gathered.shape[0]
    projected = jnp.dot(gathered, w_qkv, preferred_element_type=jnp.float32).astype(jnp.bfloat16)
    projected = projected.reshape(length, 3, head_count, head_size)
    queries = projected[:, 0]
    key_rows = projected[:, 1]
    value_rows = projected[:, 2]
    block_rows = min(512, length)
    scores = block_scores(queries, key_rows, mask_bias, 0, block_rows, head_size)
    row_peak = jnp.max(scores, axis=-1, keepdims=True)
    row_total = row_peak + jnp.log(jnp.sum(jnp.exp(scores - row_peak), axis=-1, keepdims=True))
    weights = jnp.exp(scores - row_total).astype(jnp.bfloat16)
    outputs = jnp.einsum("hqk,khd->qhd", weights, value_rows, preferred_element_type=jnp.float32)
    totals = [row_total]
    attended = outputs.astype(jnp.bfloat16).reshape(length, head_count * head_size)
    return (attended, (queries, key_rows, value_rows, totals))


def attention_backward(upstream, w_out, attended, stored, head_count, head_size, mask_bias):
    queries, key_rows, value_rows, totals = stored
    length = upstream.shape[0]
    score_scale = head_size ** (-0.5)
    grad_out = inner_rows(attended, upstream)
    attended_grad = (
        times_transpose(upstream, w_out).astype(jnp.bfloat16).reshape(length, head_count, head_size)
    )
    block_rows = min(512, length)
    key_grads = jnp.zeros((length, head_count, head_size), jnp.float32)
    value_grads = jnp.zeros((length, head_count, head_size), jnp.float32)
    query_grads = []
    for number, block_start in enumerate(range(0, length, block_rows)):
        scores = block_scores(queries, key_rows, mask_bias, block_start, block_rows, head_size)
        weights = jnp.exp(scores - totals[number])
        value_grads = jnp.einsum(
            "hqk,qhd->khd",
            weights.astype(jnp.bfloat16),
            attended_grad,
            preferred_element_type=jnp.float32,
        )
        weight_grads = jnp.einsum(
            "qhd,khd->hqk", attended_grad, value_rows, preferred_element_type=jnp.float32
        )
        score_grads = (
            weights * (weight_grads - jnp.sum(weights * weight_grads, axis=-1, keepdims=True))
        ).astype(jnp.bfloat16)
        query_grads.append(
            jnp.einsum("hqk,khd->qhd", score_grads, key_rows, preferred_element_type=jnp.float32)
            * score_scale
        )
        key_grads = (
            jnp.einsum("hqk,qhd->khd", score_grads, queries, preferred_element_type=jnp.float32)
            * score_scale
        )
    projected_grad = jnp.stack([query_grads[0], key_grads, value_grads], axis=1)
    return (
        projected_grad.astype(jnp.bfloat16).reshape(length, 3 * head_count * head_size),
        grad_out,
    )


def block_forward(residual, matrices, gain_rows, bias_rows, head_count, head_size, mask_bias):
    w_qkv, w_out, w_in, w_down = matrices
    normed, norm_one = norm_forward(residual, gain_rows[0], bias_rows[0])
    gathered = gather_rows(normed.astype(jnp.bfloat16))
    attended, stored = attention_forward(gathered, w_qkv, head_count, head_size, mask_bias)
    middle = residual + branch_rows(attended, w_out)
    normed_two, norm_two = norm_forward(middle, gain_rows[1], bias_rows[1])
    gathered_two = gather_rows(normed_two.astype(jnp.bfloat16))
    hidden = jnp.dot(gathered_two, w_in, preferred_element_type=jnp.float32)
    active = jax.nn.gelu(hidden, approximate=False).astype(jnp.bfloat16)
    result = middle + branch_rows(active, w_down)
    return (result, (gathered, norm_one, attended, stored, gathered_two, norm_two, hidden, active))


def block_backward(upstream, matrices, gain_rows, saved_values, head_count, head_size, mask_bias):
    w_qkv, w_out, w_in, w_down = matrices
    gathered, norm_one, attended, stored, gathered_two, norm_two, hidden, active = saved_values
    down_full = gather_grads(upstream.astype(jnp.bfloat16))
    grad_down = inner_rows(active, down_full)
    active_grad = times_transpose(down_full, w_down)
    gelu_pull = jax.vjp(partial(jax.nn.gelu, approximate=False), hidden)[1]
    hidden_grad = gelu_pull(active_grad)[0].astype(jnp.bfloat16)
    grad_in = inner_rows(gathered_two, hidden_grad)
    normed_two_grad = input_rows(hidden_grad, w_in)
    middle_grad, gain_two, bias_two = norm_backward(normed_two_grad, norm_two, gain_rows[1])
    middle_grad = upstream + middle_grad
    middle_full = gather_grads(middle_grad.astype(jnp.bfloat16))
    projected_grad, grad_out = attention_backward(
        middle_full, w_out, attended, stored, head_count, head_size, mask_bias
    )
    grad_qkv = inner_rows(gathered, projected_grad)
    normed_grad = input_rows(projected_grad, w_qkv)
    input_grad, gain_one, bias_one = norm_backward(normed_grad, norm_one, gain_rows[0])
    return (
        middle_grad + input_grad,
        [grad_qkv, grad_out, grad_in, grad_down],
        (gain_one, gain_two, bias_one, bias_two),
    )


def embed_forward(residual, w_embed):
    residual_low = gather_rows(residual.astype(jnp.bfloat16))
    columns = jnp.dot(residual_low, w_embed, preferred_element_type=jnp.float32).astype(
        jnp.bfloat16
    )
    own_columns = lax.all_to_all(columns, "tensor", split_axis=0, concat_axis=1, tiled=True)
    return (own_columns.astype(jnp.float32), residual_low)


def embed_backward(upstream, residual_low, w_embed):
    columns = lax.all_to_all(
        upstream.astype(jnp.bfloat16), "tensor", split_axis=1, concat_axis=0, tiled=True
    )
    grad_embed = inner_rows(residual_low, columns)
    return (input_rows(columns, w_embed), grad_embed)


def slot_builder(gradients, unit_of_slot, unit_width):
    flat_units = jnp.concatenate([gradient.reshape(-1) for gradient in gradients]).reshape(
        -1, unit_width
    )
    unit_total = flat_units.shape[0]
    source = jnp.take(flat_units, jnp.clip(unit_of_slot, 0, unit_total - 1), axis=0)
    return jnp.where((unit_of_slot >= 0)[:, None], source, 0.0)


def per_device(
    tokens_in,
    positions,
    segment_ids,
    owners,
    master,
    first_moment,
    second_moment,
    norm_gains,
    norm_biases,
    norm_first,
    norm_second,
    cotangent,
):
    devices = lax.axis_size("dp")
    tensor_count = lax.axis_size("tensor")
    capacity = master.shape[0]
    unit_width = master.shape[1]
    unit_count = owners.shape[0]
    slot_index = slot_table(owners, devices, capacity)
    unit_of_slot = (
        jnp.full((devices * capacity,), -1, jnp.int32)
        .at[slot_index]
        .set(jnp.arange(unit_count, dtype=jnp.int32))
    )
    targets = unit_of_slot
    targets = jnp.where(targets < 0, unit_count, targets)
    placed = (
        jnp.zeros((unit_count, unit_width), jnp.bfloat16)
        .at[targets]
        .set(lax.all_gather(master.astype(jnp.bfloat16), "dp", axis=0, tiled=True), mode="drop")
    )
    shapes = weight_shapes(tensor_count)
    matrices = split_flat(placed.reshape(-1), shapes)
    encoder = matrices[0:4]
    w_embed = matrices[4]
    decoder = matrices[5:9]
    enc_heads = HE // tensor_count
    dec_heads = HD // tensor_count
    micro_count = tokens_in.shape[0]
    grad_sums = [jnp.zeros(matrix_shape, jnp.float32) for matrix_shape in shapes]
    norm_sums = jnp.zeros((4, DE + DD), jnp.float32)
    decoded_rows = []
    token_grads = []
    for micro_step in range(micro_count):
        tile_ids = segment_ids[micro_step, 0]
        mask_bias = jnp.where(tile_ids[:, None] == tile_ids[None, :], 0.0, MASK_FILL).astype(
            jnp.float32
        )
        position_now = positions[:, micro_step]
        residual = tokens_in[micro_step].astype(jnp.float32) + sincos_embed(position_now, DE)
        residual, enc_saved = block_forward(
            residual, encoder, norm_gains[:, :DE], norm_biases[:, :DE], enc_heads, HDE, mask_bias
        )
        residual, embed_low = embed_forward(residual, w_embed)
        residual = residual + sincos_embed(position_now, DD)
        residual, dec_saved = block_forward(
            residual, decoder, norm_gains[:, DE:], norm_biases[:, DE:], dec_heads, HDD, mask_bias
        )
        decoded_rows.append(residual)
        upstream, dec_grads, dec_norm = block_backward(
            cotangent[micro_step], decoder, norm_gains[:, DE:], dec_saved, dec_heads, HDD, mask_bias
        )
        upstream, grad_embed = embed_backward(upstream, embed_low, w_embed)
        upstream, enc_grads, enc_norm = block_backward(
            upstream, encoder, norm_gains[:, :DE], enc_saved, enc_heads, HDE, mask_bias
        )
        token_grads.append(upstream)
        step_grads = enc_grads + [grad_embed] + dec_grads
        step_norm = jnp.concatenate([jnp.stack(enc_norm), jnp.stack(dec_norm)], axis=1)
        grad_sums = [total_grad + new_grad for total_grad, new_grad in zip(grad_sums, step_grads)]
        norm_sums = norm_sums + step_norm
    reduced = lax.psum_scatter(
        slot_builder(grad_sums, unit_of_slot, unit_width), "dp", scatter_dimension=0, tiled=True
    )
    norm_total = lax.psum(norm_sums, ("dp", "tensor"))
    new_master, new_first, new_second = adamw(
        master, reduced, first_moment, second_moment, WEIGHT_DECAY, LEARN_RATE
    )
    norm_params = jnp.concatenate([norm_gains, norm_biases], axis=0)
    new_norms, norm_one_new, norm_two_new = adamw(
        norm_params, norm_total, norm_first, norm_second, 0.0, NORM_RATE
    )
    return (
        jnp.stack(decoded_rows),
        jnp.stack(token_grads),
        new_master,
        new_first,
        new_second,
        new_norms,
        norm_one_new,
        norm_two_new,
    )


MESH = pl.DeviceIdType.MESH
ALL = slice(None)


class Place:
    def __init__(self):
        self.d = lax.axis_index("dp")
        self.x = lax.axis_index("tensor")
        self.z = self.d // 4
        self.y = (self.d // 2) % 2
        self.c = self.d % 2
        self.ids = {
            "c": (self.d + 1 - 2 * self.c, self.x),
            "y": (self.d + 2 - 4 * self.y, self.x),
            "x": (self.d, 1 - self.x),
            "z+": (self.d + 4, self.x),
            "z-": (self.d - 4, self.x),
        }

    def greet(self, kinds):
        bar = pltpu.get_barrier_semaphore()
        for k in kinds:
            pl.semaphore_signal(bar, inc=1, device_id=self.ids[k], device_id_type=MESH)

        @pl.when(self.z < 3)
        def _():
            pl.semaphore_signal(bar, inc=1, device_id=self.ids["z+"], device_id_type=MESH)

        @pl.when(self.z > 0)
        def _():
            pl.semaphore_signal(bar, inc=1, device_id=self.ids["z-"], device_id_type=MESH)

        inner = jnp.where(jnp.logical_and(self.z > 0, self.z < 3), 1, 0)
        pl.semaphore_wait(bar, len(kinds) + 1 + inner)

    def there(self, disp):
        dz = disp[0]
        if dz == 0:
            return None
        return self.z + dz <= 3 if dz > 0 else self.z + dz >= 0

    def at(self, disp):
        dz, fy, fx = disp
        return (1 - self.x if fx else self.x, self.z + dz, 1 - self.y if fy else self.y)


def when(cond, f):
    if cond is None:
        f()
    else:
        pl.when(cond)(f)


def both(a, b):
    if a is None:
        return b
    if b is None:
        return a
    return jnp.logical_and(a, b)


def spread(order):
    out = {}
    todo = [((0, 0, 0), -1, 0)]
    while todo:
        (dz, fy, fx), last, way = todo.pop(0)
        nxt = []
        for i, a in enumerate(order):
            if i < last:
                continue
            if a == "z":
                for s in (1, -1):
                    if i == last and s != way:
                        continue
                    n = (dz - s, fy, fx)
                    if abs(n[0]) <= 3:
                        nxt.append((n, "z+" if s > 0 else "z-", i, s))
            elif i > last:
                n = (dz, 1, fx) if a == "y" else (dz, fy, 1)
                nxt.append((n, a, i, 0))
        out[(dz, fy, fx)] = [(n, w) for n, w, _, _ in nxt]
        todo += [(n, i, s) for n, _, i, s in nxt]
    return out


def hops(d):
    return abs(d[0]) + d[1] + d[2]


BACK = {"z+": "z-", "z-": "z+", "x": "x", "y": "y"}


def add_rows(acc, got, step=80):
    n = acc.shape[0]
    while n % step:
        step -= 16

    def body(i, _):
        r = pl.ds(pl.multiple_of(i * step, step), step)
        acc[r, :] = acc[r, :] + got[r, :]
        return 0

    lax.fori_loop(0, n // step, body, 0)


SHARD_UNITS = 656
PANEL = 128
GROUPS = ((0, 1), (2,), (3,), (4, 5, 6), (7, 8))


def layout(shapes, shards):
    table = []
    unit_at, row_at, flat_at = 0, 0, 0
    starts = [g[0] for g in GROUPS]
    for i, (rows, cols) in enumerate(shapes):
        if i in starts:
            unit_at = -(-unit_at // 16) * 16
        rb, panels = rows // shards, cols // PANEL
        units = rb * cols // 512
        padded = -(-rb // 16) * 16
        table.append((rb, panels, units, unit_at, row_at, padded, flat_at))
        unit_at += units
        row_at += padded * panels
        flat_at += units * shards
    return table, unit_at, row_at


def unit_places(units, table, shards):
    place = jnp.zeros_like(units)
    for _, _, n, first, _, _, lo in table:
        v = units - lo
        here = (v // n) * SHARD_UNITS + first + v % n
        place = jnp.where(v >= 0, here, place)
    return place


def own_units(owners, mine, capacity):
    count = owners.shape[0] // 128
    hit = (owners[:, 0] == mine).reshape(count, 128)
    lane = jnp.arange(128)
    tri = (lane[:, None] <= lane[None, :]).astype(jnp.bfloat16)
    within = jnp.dot(hit.astype(jnp.bfloat16), tri, preferred_element_type=jnp.float32)
    totals = within[:, 127].astype(jnp.int32)
    upto = jnp.sum(jnp.where(jnp.arange(count)[:, None] >= jnp.arange(count)[None, :], totals[None, :], 0), axis=1)
    slot = jnp.arange(capacity, dtype=jnp.int32)
    block = jnp.sum((upto[None, :] <= slot[:, None]).astype(jnp.int32), axis=1)
    pick = block[:, None] == jnp.arange(count)[None, :]
    before = jnp.sum(jnp.where(pick, (upto - totals)[None, :], 0), axis=1)
    row = jnp.dot(pick.astype(jnp.bfloat16), within.astype(jnp.bfloat16), preferred_element_type=jnp.float32)
    rank = (slot - before).astype(jnp.float32)
    at = jnp.sum((row <= rank[:, None]).astype(jnp.int32), axis=1)
    return block * 128 + at, slot < upto[count - 1]


BY_ROWS = (1, 3, 6, 8)


def position_table():
    cols = []
    for width in (DE, DD):
        side = width // 16 * 6
        parts = (width - 2 * side, side, side)
        tab = np.zeros((48, width), np.float64)
        col = 0
        for i, n in enumerate(parts):
            half = n // 2
            freq = 1.0 / 10000.0 ** (np.arange(half) / half)
            ang = np.arange(16)[:, None] * freq[None, :]
            tab[16 * i:16 * i + 16, col:col + n] = np.concatenate([np.sin(ang), np.cos(ang)], axis=1)
            col += n
        cols.append(tab)
    left = np.concatenate(cols, axis=1).astype(np.float32)
    terms = []
    for _ in range(3):
        terms.append(left.astype(ml_dtypes.bfloat16))
        left = left - terms[-1].astype(np.float32)
    return np.stack(terms)


def dot(a, b):
    return jnp.dot(a, b, preferred_element_type=jnp.float32)


def dot_nt(a, b):
    return lax.dot_general(a, b, (((1,), (1,)), ((), ())), preferred_element_type=jnp.float32)


def dot_tn(a, b):
    return lax.dot_general(a, b, (((0,), (0,)), ((), ())), preferred_element_type=jnp.float32)


def lanes(i, n=128):
    return pl.ds(pl.multiple_of(i * n, n), n)


def ln_parts(x):
    c = x - jnp.mean(x, axis=-1, keepdims=True)
    inv = lax.rsqrt(jnp.mean(c * c, axis=-1, keepdims=True) + NORM_EPS)
    return c * inv, inv


def ln_back(up, m, inv, gain):
    s = up * gain
    a = jnp.mean(s, axis=-1, keepdims=True)
    b = jnp.mean(s * m, axis=-1, keepdims=True)
    return inv * (s - a - m * b), jnp.sum(up * m, axis=0, keepdims=True), jnp.sum(up, axis=0, keepdims=True)


class Block:
    def __init__(self, width, heads, size, hidden, first, table, col):
        self.width, self.heads, self.size, self.hidden, self.col = width, heads, size, hidden, col
        self.q, self.o, self.a, self.b = table[first:first + 4]
        self.part = heads // 2 * size
        self.per = 128 // size


def panel(w, t, mat, g, lo=0, num=16):
    rb, _, _, _, at, padded, _ = mat
    rows = pl.ds(pl.multiple_of(at + g * padded, 16), padded)
    v = w[t, lo:lo + num, rows, :] if isinstance(lo, int) else w[t, pl.ds(lo, num), rows, :]
    if padded > rb:
        v = v.astype(jnp.float32)[:, :rb].reshape(num * rb, 128).astype(jnp.bfloat16)
        return v
    return v.reshape(num * rb, 128)


def pair(w, mat, g):
    return jnp.concatenate([panel(w, 0, mat, g), panel(w, 1, mat, g)], axis=1)


def block_fwd(b, x, xo, w, gains, biases, same, n1, proj, p, att, ow, m1, i1, n2, m2, i2, act, slope):
    cols = slice(b.col, b.col + b.width)
    m, inv = ln_parts(x[...])
    m1[...] = m
    i1[...] = inv
    n1[...] = (m * gains[0:1, cols] + biases[0:1, cols]).astype(jnp.bfloat16)
    gq = b.q[1]

    def qkv(g, _):
        r = dot(n1[...], pair(w, b.q, g)).astype(jnp.bfloat16)
        proj[:, lanes(g)] = r[:, :128]
        proj[:, lanes(gq + g)] = r[:, 128:]
        return 0

    lax.fori_loop(0, gq, qkv, 0)
    np_ = b.part // 128
    lane = lax.broadcasted_iota(jnp.int32, (256, 128), 1)
    masks = [lane // b.size == i for i in range(b.per)]

    def heads(i, _):
        t, j = i // np_, i % np_
        q = proj[:, lanes(t * gq + j)]
        k = proj[:, lanes(t * gq + np_ + j)]
        v = proj[:, lanes(t * gq + 2 * np_ + j)]
        total = jnp.zeros((256, 128), jnp.float32)
        for h in range(b.per):
            z = dot_nt(jnp.where(masks[h], q, 0), k) * b.size ** (-0.5) + same
            e = jnp.exp(z - jnp.max(z, axis=-1, keepdims=True))
            s = e / jnp.sum(e, axis=-1, keepdims=True)
            p[i * b.per + h] = s
            total = total + dot(s.astype(jnp.bfloat16), jnp.where(masks[h], v, 0))
        att[:, lanes(i)] = total.astype(jnp.bfloat16)
        return 0

    lax.fori_loop(0, 2 * np_, heads, 0)
    for t in range(2):
        for g in range(b.width // 128):
            ow[t, :, g * 128:(g + 1) * 128] = panel(w, t, b.o, g)
    x1 = x[...] + dot(att[:, :b.part], ow[0]) + dot(att[:, b.part:], ow[1])
    xo[...] = x1
    m, inv = ln_parts(x1)
    m2[...] = m
    i2[...] = inv
    n2[...] = (m * gains[1:2, cols] + biases[1:2, cols]).astype(jnp.bfloat16)
    ga = b.a[1]

    def up(g, _):
        h = dot(n2[...], pair(w, b.a, g))
        big = 0.5 * (1.0 + lax.erf(h * 0.7071067811865476))
        act_v = (h * big).astype(jnp.bfloat16)
        dens = big + h * (0.3989422804014327 * jnp.exp(-0.5 * h * h))
        act[:, lanes(g)] = act_v[:, :128]
        act[:, lanes(ga + g)] = act_v[:, 128:]
        slope[:, lanes(g)] = dens[:, :128]
        slope[:, lanes(ga + g)] = dens[:, 128:]
        return 0

    lax.fori_loop(0, ga, up, 0)
    half = b.hidden // 2

    def down(g, _):
        w0 = jnp.concatenate([panel(w, 0, b.b, 2 * g), panel(w, 0, b.b, 2 * g + 1)], axis=1)
        w1 = jnp.concatenate([panel(w, 1, b.b, 2 * g), panel(w, 1, b.b, 2 * g + 1)], axis=1)
        xo[:, lanes(g, 256)] += dot(act[:, :half], w0) + dot(act[:, half:], w1)
        return 0

    lax.fori_loop(0, b.width // 256, down, 0)


def block_bwd(b, dr, w, gains, same, n1, proj, p, att, ow, m1, i1, n2, m2, i2, act, slope,
              r, dh, r1, dp_out, acc, da, norm_out):
    cols = slice(b.col, b.col + b.width)
    r[...] = dr[...].astype(jnp.bfloat16)
    half = b.hidden // 2
    rb = b.b[0]
    gb = b.width // 128
    num = 4

    def hidden(i, _):
        t, lo = i // (16 // num), (i % (16 // num)) * num
        wc = jnp.concatenate([panel(w, t, b.b, g, lo, num) for g in range(gb)], axis=1)
        at = lanes(i, num * rb)
        dh[:, at] = (dot_nt(r[...], wc) * slope[:, at]).astype(jnp.bfloat16)
        return 0

    lax.fori_loop(0, 2 * (16 // num), hidden, 0)
    ga = b.a[1]
    acc[...] = jnp.zeros_like(acc)

    def up(g, _):
        d = jnp.concatenate([dh[:, lanes(g)], dh[:, lanes(ga + g)]], axis=1)
        acc[...] += dot_nt(d, pair(w, b.a, g))
        return 0

    lax.fori_loop(0, ga, up, 0)
    dx, dg, db = ln_back(acc[...], m2[...], i2[...], gains[1:2, cols])
    norm_out[1:2, cols] = dg
    norm_out[3:4, cols] = db
    dx1 = dr[...] + dx
    dr[...] = dx1
    r1[...] = dx1.astype(jnp.bfloat16)
    for t in range(2):
        da[:, t * b.part:(t + 1) * b.part] = dot_nt(r1[...], ow[t]).astype(jnp.bfloat16)
    gq = b.q[1]
    np_ = b.part // 128
    lane = lax.broadcasted_iota(jnp.int32, (256, 128), 1)
    masks = [lane // b.size == i for i in range(b.per)]
    scale = b.size ** (-0.5)

    def heads(i, _):
        t, j = i // np_, i % np_
        q = proj[:, lanes(t * gq + j)]
        k = proj[:, lanes(t * gq + np_ + j)]
        v = proj[:, lanes(t * gq + 2 * np_ + j)]
        up_ = da[:, lanes(i)]
        dq = jnp.zeros((256, 128), jnp.float32)
        dk = jnp.zeros((256, 128), jnp.float32)
        dv = jnp.zeros((256, 128), jnp.float32)
        for h in range(b.per):
            s = p[i * b.per + h]
            u = jnp.where(masks[h], up_, 0)
            dp = dot_nt(u, v)
            dv = dv + dot_tn(s.astype(jnp.bfloat16), u)
            t1 = s * dp
            dz = (t1 - s * jnp.sum(t1, axis=-1, keepdims=True)).astype(jnp.bfloat16)
            dq = dq + dot(dz, jnp.where(masks[h], k, 0))
            dk = dk + dot_tn(dz, jnp.where(masks[h], q, 0))
        dp_out[:, lanes(t * gq + j)] = (dq * scale).astype(jnp.bfloat16)
        dp_out[:, lanes(t * gq + np_ + j)] = (dk * scale).astype(jnp.bfloat16)
        dp_out[:, lanes(t * gq + 2 * np_ + j)] = dv.astype(jnp.bfloat16)
        return 0

    lax.fori_loop(0, 2 * np_, heads, 0)
    acc[...] = jnp.zeros_like(acc)

    def qkv(g, _):
        d = jnp.concatenate([dp_out[:, lanes(g)], dp_out[:, lanes(gq + g)]], axis=1)
        acc[...] += dot_nt(d, pair(w, b.q, g))
        return 0

    lax.fori_loop(0, gq, qkv, 0)
    dx, dg, db = ln_back(acc[...], m1[...], i1[...], gains[0:1, cols])
    norm_out[0:1, cols] = dg
    norm_out[2:3, cols] = db
    dr[...] = dr[...] + dx


ACTS = (("n1", DE), ("att", DE), ("n2", DE), ("act", FFE), ("low", DE), ("n1", DD), ("att", DD), ("n2", DD), ("act", FFD))
GRADS = (3 * DE, DE, FFE, DE, DD, 3 * DD, DD, FFD, DD)


def chain_kernel(table, tok, pos, tile_r, tile_c, gains, biases, cot, tab, w, *refs):
    dec, dx0, norm_out = refs[:3]
    acts, grads = refs[3:12], refs[12:21]
    (pe, pd, se, sd, proj_e, proj_d, da_e, da_d, ow_e, ow_d, m1e, m2e, m1d, m2d, i1e, i2e, i1d, i2d,
     x, y, acc_e, acc_d) = refs[21:]
    enc_b = Block(DE, HE, HDE, FFE, 0, table, 0)
    dec_b = Block(DD, HD, HDD, FFD, 5, table, DE)
    em = table[4]
    lane = lax.broadcasted_iota(jnp.int32, (256, 48), 1)
    hot = jnp.logical_or(jnp.logical_or(lane == pos[:, 0:1], lane == pos[:, 1:2] + 16), lane == pos[:, 2:3] + 32)
    hot = jnp.where(hot, 1.0, 0.0).astype(jnp.bfloat16)
    same = jnp.where(tile_c[...] == tile_r[...], 0.0, MASK_FILL)
    x[...] = tok[...].astype(jnp.float32) + (dot(hot, tab[0, :, :DE]) + dot(hot, tab[1, :, :DE]) + dot(hot, tab[2, :, :DE]))
    n1e, ae, n2e, ue, low, n1d, ad, n2d, ud = acts
    dpe, r1e, dhe, re, dlow, dpd, r1d, dhd, rd = grads
    block_fwd(enc_b, x, dx0, w, gains, biases, same, n1e, proj_e, pe, ae, ow_e, m1e, i1e, n2e, m2e, i2e, ue, se)
    low[...] = dx0[...].astype(jnp.bfloat16)
    for g in range(2):
        v = dot(low[...], pair(w, em, g)).astype(jnp.bfloat16).astype(jnp.float32)
        y[:, g * 128:(g + 1) * 128] = v[:, :128]
        y[:, 256 + g * 128:256 + (g + 1) * 128] = v[:, 128:]
    y[...] += dot(hot, tab[0, :, DE:]) + dot(hot, tab[1, :, DE:]) + dot(hot, tab[2, :, DE:])
    block_fwd(dec_b, y, dec, w, gains, biases, same, n1d, proj_d, pd, ad, ow_d, m1d, i1d, n2d, m2d, i2d, ud, sd)
    y[...] = cot[...]
    block_bwd(dec_b, y, w, gains, same, n1d, proj_d, pd, ad, ow_d, m1d, i1d, n2d, m2d, i2d, ud, sd,
              rd, dhd, r1d, dpd, acc_d, da_d, norm_out)
    dlow[...] = y[...].astype(jnp.bfloat16)
    for g in range(2):
        d = jnp.concatenate([dlow[:, g * 128:(g + 1) * 128], dlow[:, 256 + g * 128:256 + (g + 1) * 128]], axis=1)
        v = dot_nt(d, pair(w, em, g))
        if g == 0:
            dx0[...] = v
        else:
            dx0[...] += v
    block_bwd(enc_b, dx0, w, gains, same, n1e, proj_e, pe, ae, ow_e, m1e, i1e, n2e, m2e, i2e, ue, se,
              re, dhe, r1e, dpe, acc_e, da_e, norm_out)


def chain(tokens, pos, tile, gains, biases, cot, full, table):
    f32, bf16 = jnp.float32, jnp.bfloat16
    S = jax.ShapeDtypeStruct
    outs = [S((256, DD), f32), S((256, DE), f32), S((4, DE + DD), f32)]
    outs += [S((256, n), bf16) for _, n in ACTS] + [S((256, n), bf16) for n in GRADS]
    V = pltpu.VMEM
    scratch = [V((HE, 256, 256), f32), V((HD, 256, 256), f32), V((256, FFE), f32), V((256, FFD), f32),
               V((256, 3 * DE), bf16), V((256, 3 * DD), bf16), V((256, DE), bf16), V((256, DD), bf16),
               V((2, DE // 2, DE), bf16), V((2, DD // 2, DD), bf16),
               V((256, DE), f32), V((256, DE), f32), V((256, DD), f32), V((256, DD), f32)] + [V((256, 1), f32)] * 4 + [
               V((256, DE), f32), V((256, DD), f32), V((256, DE), f32), V((256, DD), f32)]
    spec = pl.BlockSpec(memory_space=pltpu.VMEM)
    args = (tokens, pos.T, tile[None, :], tile[:, None], gains, biases, cot, jnp.asarray(position_table()),
            full.reshape(2, 16, full.shape[-2], 128))
    return pl.pallas_call(
        partial(chain_kernel, table), out_shape=outs, in_specs=[spec] * len(args), out_specs=[spec] * len(outs),
        scratch_shapes=scratch, compiler_params=pltpu.CompilerParams(vmem_limit_bytes=62 << 20), name="chain",
        cost_estimate=pl.CostEstimate(flops=11_000_000_000, bytes_accessed=40_000_000, transcendentals=5_000_000),
    )(*args)


def grad_panels(table, m, act, grad, turned, put):
    mat = table[m]
    rb, panels, padded = mat[0], mat[1], mat[5]
    count = act.shape[1]

    def turn(i, _):
        turned[pl.ds(pl.multiple_of(i * 128, 128), 128), :] = act[:, lanes(i)].T
        return 0

    lax.fori_loop(0, count // 128, turn, 0)

    def place(t, g, v):
        if padded > rb:
            v = v.reshape(16, rb, 128)
            v = jnp.concatenate([v, jnp.zeros((16, padded - rb, 128), jnp.float32)], axis=1).astype(jnp.bfloat16)
        else:
            v = v.astype(jnp.bfloat16).reshape(16, rb, 128)
        put(t, g, v)

    if m in BY_ROWS:
        half = count // 2

        def body(i, _):
            t, g = i // (panels // 2), i % (panels // 2)
            v = dot(turned[pl.ds(pl.multiple_of(t * half, 128), half), :], grad[:, lanes(g, 256)])
            place(t, 2 * g, v[:, :128])
            place(t, 2 * g + 1, v[:, 128:])
            return 0

        lax.fori_loop(0, panels, body, 0)
    else:
        def body(g, _):
            d = jnp.concatenate([grad[:, lanes(g)], grad[:, lanes(panels + g)]], axis=1)
            v = dot(turned[:count, :], d)
            place(0, g, v[:, :128])
            place(1, g, v[:, 128:])
            return 0

        lax.fori_loop(0, panels, body, 0)


class Wires:
    def __init__(self, place, sem):
        self.place, self.sem, self.used, self.waits = place, sem, 0, []

    def new(self, n=1):
        self.used += n
        assert self.used <= self.sem.shape[0], self.used
        return self.used - n

    def copy(self, k, src, dst, way):
        return pltpu.make_async_remote_copy(src_ref=src, dst_ref=dst, send_sem=self.sem.at[k], recv_sem=self.sem.at[k + 1],
                                            device_id=self.place.ids[way], device_id_type=MESH)

    def send(self, k, src, dst, way, cond=None):
        cp = self.copy(k, src, dst, way)
        when(cond, cp.start)
        self.waits.append((cond, cp))

    def land(self, k, dst, cond=None):
        when(cond, self.copy(k, dst, dst, "c").wait_recv)

    def drain(self):
        for cond, cp in self.waits:
            when(cond, cp.wait_send)


def edge_slot(p, parent, way):
    dz, fy, _ = parent
    if way == "z+":
        return -dz
    if way == "z-":
        return 3 + dz
    return 6 + p.z + dz if way == "y" else 10 + 4 * fy + p.z + dz


def edge_slots(order):
    return 18 if "x" in order else 10


def beyond(p, way):
    return p.z < 3 if way == "z+" else p.z > 0 if way == "z-" else None


def reduce_events(p, w, order, own, half, bufs, done):
    tree = spread(order)
    top = max(hops(d) for d in tree)
    with_x = "x" in order
    pair = {d: w.new(2) for d in tree}
    wire = {d: w.new(2) for d in tree}
    parent = {nd: (d, way) for d, t in tree.items() for nd, way in t}
    events = []
    for d in sorted(tree, key=lambda d: (-hops(d), d)):
        def act(d=d):
            cond = p.there(d)

            def step():
                acc = own(d)
                w.land(pair[d], half(d))
                add_rows(acc, half(d))
                for nd, way in tree[d]:
                    buf = bufs.at[edge_slot(p, d, way)]

                    def take(buf=buf, nd=nd):
                        w.land(wire[nd], buf)
                        add_rows(acc, buf)
                    when(beyond(p, way), take)
            when(cond, step)
            if hops(d) == 0:
                done()
            else:
                up, way = parent[d]
                w.send(wire[d], own(d), bufs.at[edge_slot(p, up, way) if way[0] == "z" else edge_slot(p, d, way) if way == "y" else edge_slot(p, (d[0], d[1], 0), way)],
                       BACK[way], cond)
        events.append((top - hops(d), act))

    def share(give):
        for d in sorted(tree, key=lambda d: (-hops(d), d)):
            w.send(pair[d], give(d), half(d), "c", p.there(d))

    return events, share, top


def gather_events(p, w, order, first, at):
    tree = spread(order)
    pair = {d: w.new(2) for d in tree}
    wire = {d: w.new(2) for d in tree}
    events = []
    for d in sorted(tree, key=lambda d: (hops(d), d)):
        def act(d=d):
            cond = p.there(d)
            blk = at(d, p.c)
            if hops(d):
                w.land(wire[d], blk, cond)
                src = blk
            else:
                src = first
            for nd, way in tree[d]:
                w.send(wire[nd], src, blk, way, both(cond, beyond(p, way)))
            w.send(pair[d], src, blk, "c", cond)
        events.append((hops(d), act))

    def finish():
        for d in tree:
            w.land(pair[d], at(d, 1 - p.c), p.there(d))

    return events, finish


def run_events(lists, stride, extra=iter(()), every=8):
    todo = sorted(((level + stride * g, g, i), act) for g, evs in enumerate(lists) for i, (level, act) in enumerate(evs))
    for n, (_, act) in enumerate(todo):
        if n % every == 0:
            next(extra, None)
        act()
    for _ in extra:
        pass


def group_span(table, mats):
    first, last = table[mats[0]], table[mats[-1]]
    units = last[3] + last[2] - first[3]
    return first[3], -(-units // 16) * 16, first[4], last[4] + last[1] * last[5] - first[4]


def units_to_panels(table, mats, units, flat, put):
    base, count = table[mats[0]][3], units.shape[0]
    for k in range(4):
        flat[pl.ds(k, count, stride=4), :] = units[:, 128 * k:128 * (k + 1)].astype(jnp.float32)
    for m in mats:
        rb, panels, n, first, _, padded, _ = table[m]
        for g in range(panels):
            v = flat[pl.ds(4 * (first - base) + g, rb, stride=panels), :]
            if padded > rb:
                v = jnp.concatenate([v, jnp.zeros((padded - rb, 128), jnp.float32)], axis=0)
            put(m, g, v.astype(jnp.bfloat16))


def panels_to_units(table, mats, take, flat, units):
    base, count = table[mats[0]][3], units.shape[0]
    used = 0
    for m in mats:
        rb, panels, n, first, _, padded, _ = table[m]
        for g in range(panels):
            flat[pl.ds(4 * (first - base) + g, rb, stride=panels), :] = take(m, g)[:rb]
        used = 4 * (first - base + n)
    if used < 4 * count:
        flat[used:4 * count, :] = jnp.zeros((4 * count - used, 128), jnp.float32)
    for k in range(4):
        units[:, 128 * k:128 * (k + 1)] = flat[pl.ds(k, count, stride=4), :].astype(jnp.bfloat16)


def weights_kernel(table, groups, stride, parts, out, *rest):
    n = len(groups)
    accs, halves, bufs, shards = (rest[i * n:(i + 1) * n] for i in range(4))
    flat, sem = rest[4 * n:]
    p = Place()
    p.greet(["c", "y", "x"])
    w = Wires(p, sem)
    lists, finishes = [], []
    for g, mats in enumerate(groups):
        u0, un, r0, rn = group_span(table, mats)
        acc, half, buf, shard = accs[g], halves[g], bufs[g], shards[g]
        load = w.new()
        own_sem = w.new()

        def start(u0=u0, un=un, acc=acc, load=load):
            pltpu.make_async_copy(parts.at[:, :, p.c, pl.ds(u0, un)], acc, sem.at[load]).start()

        def own(d, acc=acc):
            return acc.at[p.at(d)[1:]]

        def other(d, half=half):
            return half.at[p.at(d)[1:]]

        def done(g=g, mats=mats, acc=acc, shard=shard, r0=r0, rn=rn, own_sem=own_sem):
            def put(m, i, v):
                lo = table[m][4] - r0 + i * table[m][5]
                shard[lo:lo + table[m][5], :] = v
            units_to_panels(table, mats, acc.at[p.z, p.y], flat, put)
            pltpu.make_async_copy(shard, out.at[p.x, p.z, p.y, p.c, pl.ds(r0, rn)], sem.at[own_sem]).start()

        ev, share, top = reduce_events(p, w, "zy", own, other, buf, done)

        def begin(start=start, share=share, u0=u0, un=un, acc=acc, load=load):
            start()
            share(lambda d: parts.at[p.at(d)[1:] + (1 - p.c, pl.ds(u0, un))])

        def loaded(u0=u0, un=un, acc=acc, load=load):
            pltpu.make_async_copy(parts.at[:, :, p.c, pl.ds(u0, un)], acc, sem.at[load]).wait()

        def at(d, core, r0=r0, rn=rn):
            t, z, y = p.at(d)
            return out.at[t, z, y, core, pl.ds(r0, rn)]

        ag, finish = gather_events(p, w, "zyx", shard, at)
        evs = [(-1, begin), (-0.5, loaded)] + ev + [(top + 1 + lv, a) for lv, a in ag]
        lists.append(evs)

        def end(finish=finish, shard=shard, r0=r0, rn=rn, own_sem=own_sem):
            finish()
            pltpu.make_async_copy(shard, out.at[p.x, p.z, p.y, p.c, pl.ds(r0, rn)], sem.at[own_sem]).wait()

        finishes.append(end)
    run_events(lists, stride)
    for f in finishes:
        f()
    w.drain()


def spread_weights(parts, table, rows, groups, stride, ident):
    spans = [group_span(table, m) for m in groups]
    bf16 = jnp.bfloat16
    scratch = [pltpu.VMEM((4, 2, s[1], 512), bf16) for s in spans] * 2
    scratch += [pltpu.VMEM((edge_slots("zy"), s[1], 512), bf16) for s in spans]
    scratch += [pltpu.VMEM((s[3], 128), bf16) for s in spans]
    scratch += [pltpu.VMEM((4 * max(s[1] for s in spans), 128), jnp.float32), pltpu.SemaphoreType.DMA((len(groups) * (2 + 4 * 14 + 4 * 28),))]
    return pl.pallas_call(
        partial(weights_kernel, table, groups, stride),
        out_shape=jax.ShapeDtypeStruct((2, 4, 2, 2, rows, 128), bf16),
        in_specs=[pl.BlockSpec(memory_space=pl.ANY)], out_specs=pl.BlockSpec(memory_space=pl.ANY),
        scratch_shapes=scratch,
        compiler_params=pltpu.CompilerParams(collective_id=ident, has_side_effects=True, vmem_limit_bytes=62 << 20),
        name="spread_weights",
    )(parts)


def return_kernel(table, groups, stride, *refs):
    n = len(groups)
    acts, grads, small_src, out, small_out = refs[:9], refs[9:18], refs[18], refs[19], refs[20]
    rest = refs[21:]
    sides, halves, bufs, units = (rest[i * n:(i + 1) * n] for i in range(4))
    flat, turned, mid, line, sem = rest[4 * n:]
    p = Place()
    p.greet(["c", "y", "x"])
    w = Wires(p, sem)
    lists, finishes = [], []
    for g, mats in enumerate(groups):
        u0, un, r0, rn = group_span(table, mats)
        side, half, buf, unit = sides[g], halves[g], bufs[g], units[g]
        own_sem = w.new()

        def own(d, side=side):
            return side.at[(p.c,) + p.at(d)]

        def other(d, half=half):
            return half.at[p.at(d)]

        def done(mats=mats, side=side, unit=unit, r0=r0, u0=u0, un=un, own_sem=own_sem):
            mine = side.at[p.c, p.x, p.z, p.y]

            def take(m, i):
                lo = table[m][4] - r0 + i * table[m][5]
                return mine[lo:lo + table[m][5], :].astype(jnp.float32)
            panels_to_units(table, mats, take, flat, unit)
            pltpu.make_async_copy(unit, out.at[p.z, p.y, p.c, pl.ds(u0, un)], sem.at[own_sem]).start()

        ev, share, top = reduce_events(p, w, "zyx", own, other, buf, done)

        def begin(mats=mats, side=side, share=share, r0=r0):
            for m in mats:
                lo, padded = table[m][4] - r0, table[m][5]

                def put(t, i, v, lo=lo, padded=padded):
                    v = v.reshape(4, 2, 2, padded, 128)
                    rows = pl.ds(pl.multiple_of(lo + i * padded, 16), padded)
                    side[0, t, :, :, rows, :] = v[:, :, 0]
                    side[1, t, :, :, rows, :] = v[:, :, 1]
                grad_panels(table, m, acts[m], grads[m], turned, put)
            share(lambda d: side.at[(1 - p.c,) + p.at(d)])

        def at(d, core, u0=u0, un=un):
            _, z, y = p.at(d)
            return out.at[z, y, core, pl.ds(u0, un)]

        ag, finish = gather_events(p, w, "zy", unit, at)
        lists.append([(-1, begin)] + ev + [(top + 1 + lv, a) for lv, a in ag])

        def end(finish=finish, unit=unit, u0=u0, un=un, own_sem=own_sem):
            finish()
            pltpu.make_async_copy(unit, out.at[p.z, p.y, p.c, pl.ds(u0, un)], sem.at[own_sem]).wait()

        finishes.append(end)
    run_events(lists, stride, total_steps(p, w, small_src, small_out, mid, line))
    for f in finishes:
        f()
    w.drain()


def total_steps(p, w, src, out, mid, line):
    k = [w.new(2) for _ in range(9)]
    now = src
    for i, way in enumerate(("c", "x", "y")):
        w.send(k[i], now, mid.at[i], way)
        yield
        w.land(k[i], mid.at[i])
        nxt = mid.at[3 + i] if i < 2 else line.at[p.z]
        nxt[...] = now[...] + mid[i]
        now = nxt
    for i in range(4):
        lo, hi = jnp.maximum(p.z - i, 0), jnp.minimum(p.z + i, 3)
        if i > 0:
            w.land(k[2 + i], line.at[lo], p.z >= i)
            w.land(k[5 + i], line.at[hi], p.z + i <= 3)
        if i < 3:
            w.send(k[3 + i], line.at[lo], line.at[lo], "z+", jnp.logical_and(p.z >= i, p.z < 3))
            w.send(k[6 + i], line.at[hi], line.at[hi], "z-", jnp.logical_and(p.z + i <= 3, p.z > 0))
            yield
    out[...] = (line[0] + line[1]) + (line[2] + line[3])


def return_grads(acts, grads, small, table, total_units, groups, stride, ident):
    spans = [group_span(table, m) for m in groups]
    bf16 = jnp.bfloat16
    scratch = [pltpu.VMEM((2, 2, 4, 2, s[3], 128), bf16) for s in spans]
    scratch += [pltpu.VMEM((2, 4, 2, s[3], 128), bf16) for s in spans]
    scratch += [pltpu.VMEM((edge_slots("zyx"), s[3], 128), bf16) for s in spans]
    scratch += [pltpu.VMEM((s[1], 512), bf16) for s in spans]
    scratch += [pltpu.VMEM((4 * max(s[1] for s in spans), 128), jnp.float32), pltpu.VMEM((FFE, 256), bf16),
                pltpu.VMEM((5,) + small.shape, small.dtype), pltpu.VMEM((4,) + small.shape, small.dtype),
                pltpu.SemaphoreType.DMA((len(groups) * (1 + 4 * 14 + 4 * 28) + 18,))]
    vmem = pl.BlockSpec(memory_space=pltpu.VMEM)
    return pl.pallas_call(
        partial(return_kernel, table, groups, stride),
        out_shape=(jax.ShapeDtypeStruct((4, 2, 2, total_units, 512), bf16), jax.ShapeDtypeStruct(small.shape, small.dtype)),
        in_specs=[vmem] * 19, out_specs=(pl.BlockSpec(memory_space=pl.ANY), vmem),
        scratch_shapes=scratch,
        compiler_params=pltpu.CompilerParams(collective_id=ident, has_side_effects=True, vmem_limit_bytes=63 << 20),
        name="return_grads",
    )(*acts, *grads, small)


def swap(v):
    return lax.ppermute(v, "tensor", [(0, 1), (1, 0)])


def sequence_device(tokens_in, positions, segment_ids, owners, master, first_moment, second_moment, norm_gains,
                    norm_biases, norm_first, norm_second, cotangent):
    t = lax.axis_index("tensor")
    shapes = weight_shapes(2)
    table, _, rows = layout(shapes, 16)

    def whole(v, axis):
        own = lax.dynamic_index_in_dim(v, t, axis, keepdims=False)
        other = swap(lax.dynamic_index_in_dim(v, 1 - t, axis, keepdims=False))
        at = 1 if axis == 1 else 0
        return jnp.concatenate([jnp.where(t == 0, own, other), jnp.where(t == 0, other, own)], axis=at)

    def halves(v):
        half = v.shape[0] // 2
        own = lax.dynamic_slice_in_dim(v, t * half, half, 0)
        other = swap(lax.dynamic_slice_in_dim(v, (1 - t) * half, half, 0))
        return jnp.stack([jnp.where(t == 0, own, other), jnp.where(t == 0, other, own)])

    tokens, cot, pos = whole(tokens_in, 0), whole(cotangent, 0), whole(positions, 1)
    tile = lax.dynamic_index_in_dim(segment_ids, t, 0, keepdims=False)[0]

    unit, used = own_units(owners, lax.axis_index("dp"), master.shape[0])
    place = unit_places(unit, table, 16)
    parts = jnp.zeros((16 * SHARD_UNITS, 512), jnp.bfloat16)
    parts = parts.at[jnp.where(used, place, 16 * SHARD_UNITS)].set(master.astype(jnp.bfloat16), mode="drop", unique_indices=True)
    full = spread_weights(parts.reshape(4, 2, 2, SHARD_UNITS, 512), table, rows, GROUPS, 2, 1)
    kept = chain(tokens, pos, tile, norm_gains, norm_biases, cot, full, table)
    decoded, dx0, norms = kept[:3]
    spread_out, norm_total = return_grads(kept[3:12], kept[12:21], norms, table, SHARD_UNITS, GROUPS, 3, 2)
    spread_out = spread_out.reshape(16 * SHARD_UNITS, 512)
    reduced = jnp.where(used[:, None], jnp.take(spread_out, jnp.clip(place, 0, 16 * SHARD_UNITS - 1), axis=0).astype(jnp.float32), 0.0)
    new_master, new_first, new_second = adamw(master, reduced, first_moment, second_moment, WEIGHT_DECAY, LEARN_RATE)
    norm_params = jnp.concatenate([norm_gains, norm_biases], axis=0)
    new_norms, norm_one_new, norm_two_new = adamw(norm_params, norm_total, norm_first, norm_second, 0.0, NORM_RATE)
    return (halves(decoded), halves(dx0), new_master, new_first, new_second, new_norms, norm_one_new, norm_two_new)


def solution(mesh):
    step = sequence_device if (mesh.shape["dp"], mesh.shape["tensor"]) == (16, 2) else per_device
    return jax.shard_map(
        step,
        mesh=mesh,
        in_specs=(
            P(None, ("dp", "tensor"), None),
            P(None, None, ("dp", "tensor")),
            P(None, "dp", None),
            P(),
            P("dp", "tensor"),
            P("dp", "tensor"),
            P("dp", "tensor"),
            P(),
            P(),
            P(),
            P(),
            P(None, ("dp", "tensor"), None),
        ),
        out_specs=(
            P(None, ("dp", "tensor"), None),
            P(None, ("dp", "tensor"), None),
            P("dp", "tensor"),
            P("dp", "tensor"),
            P("dp", "tensor"),
            P(),
            P(),
            P(),
        ),
        check_vma=False,
    )
```

```python
from functools import partial

import jax
import jax.numpy as jnp
import ml_dtypes
import numpy as np
from jax import lax
from jax.experimental import pallas as pl
from jax.experimental.pallas import tpu as pltpu
from jax.sharding import PartitionSpec as P

DE = 768
HE = 12
HDE = 64
FFE = 3072
DD = 512
HD = 16
HDD = 32
FFD = 2048
STEP = 10


NORM_EPS = 1e-06
BETA_ONE = 0.5
BETA_TWO = 0.5
LEARN_RATE = 0.03
NORM_RATE = 0.3
WEIGHT_DECAY = 0.05
ADAM_EPS = 1e-08
MASK_FILL = -1000000000.0


def sincos_part(coordinate, part_width):
    halfway = part_width // 2
    frequency = 1.0 / 10000.0 ** (jnp.arange(halfway, dtype=jnp.float32) / halfway)
    angles = coordinate.astype(jnp.float32)[:, None] * frequency[None, :]
    return jnp.concatenate([jnp.sin(angles), jnp.cos(angles)], axis=1)


def sincos_embed(positions, model_width):
    side_width = model_width // 16 * 6
    first_width = model_width - 2 * side_width
    return jnp.concatenate(
        [
            sincos_part(positions[0], first_width),
            sincos_part(positions[1], side_width),
            sincos_part(positions[2], side_width),
        ],
        axis=1,
    )


def slot_table(owners, devices, capacity):
    owner_ids = owners[:, 0]
    onehot = (owner_ids[:, None] == jnp.arange(devices, dtype=jnp.int32)[None, :]).astype(jnp.int32)
    before = jnp.cumsum(onehot, axis=0) - onehot
    owner_rank = jnp.sum(before * onehot, axis=1)
    return owner_ids * capacity + owner_rank


def weight_shapes(tensor_count):
    enc_heads = HE // tensor_count
    dec_heads = HD // tensor_count
    return [
        (DE, 3 * enc_heads * HDE),
        (enc_heads * HDE, DE),
        (DE, FFE // tensor_count),
        (FFE // tensor_count, DE),
        (DE, DD // tensor_count),
        (DD, 3 * dec_heads * HDD),
        (dec_heads * HDD, DD),
        (DD, FFD // tensor_count),
        (FFD // tensor_count, DD),
    ]


def split_flat(flat_vector, shapes):
    pieces = []
    offset = 0
    for matrix_shape in shapes:
        length = matrix_shape[0] * matrix_shape[1]
        pieces.append(flat_vector[offset : offset + length].reshape(matrix_shape))
        offset += length
    return pieces


def adamw(weights, gradient, moment_one, moment_two, decay_rate, step_rate):
    one_new = BETA_ONE * moment_one + (1.0 - BETA_ONE) * gradient
    two_new = BETA_TWO * moment_two + (1.0 - BETA_TWO) * gradient * gradient
    one_hat = one_new / (1.0 - BETA_ONE**STEP)
    two_hat = two_new / (1.0 - BETA_TWO**STEP)
    weights_new = weights - step_rate * (
        one_hat / (jnp.sqrt(two_hat) + ADAM_EPS) + decay_rate * weights
    )
    return (weights_new, one_new, two_new)


def norm_forward(values, gain_row, bias_row):
    center = values - jnp.mean(values, axis=-1, keepdims=True)
    spread = jnp.mean(center * center, axis=-1, keepdims=True)
    inverse = lax.rsqrt(spread + NORM_EPS)
    normed = center * inverse
    return (normed * gain_row + bias_row, (normed, inverse))


def norm_backward(upstream, stored, gain_row):
    normed, inverse = stored
    scaled = upstream * gain_row
    mean_one = jnp.mean(scaled, axis=-1, keepdims=True)
    mean_two = jnp.mean(scaled * normed, axis=-1, keepdims=True)
    return (
        inverse * (scaled - mean_one - normed * mean_two),
        jnp.sum(upstream * normed, axis=0),
        jnp.sum(upstream, axis=0),
    )


def inner_rows(left_side, right_side):
    return lax.dot_general(
        left_side, right_side, (((0,), (0,)), ((), ())), preferred_element_type=jnp.float32
    )


def times_transpose(left_side, right_side):
    return lax.dot_general(
        left_side, right_side, (((1,), (1,)), ((), ())), preferred_element_type=jnp.float32
    )


def gather_rows(values):
    return lax.all_gather(values, "tensor", axis=0, tiled=True)


def gather_grads(values):
    return lax.all_gather(values, "tensor", axis=0, tiled=True)


def branch_rows(values, weight):
    return lax.psum_scatter(
        jnp.dot(values, weight, preferred_element_type=jnp.float32).astype(jnp.bfloat16),
        "tensor",
        scatter_dimension=0,
        tiled=True,
    ).astype(jnp.float32)


def input_rows(values, weight):
    return lax.psum_scatter(
        times_transpose(values, weight).astype(jnp.bfloat16),
        "tensor",
        scatter_dimension=0,
        tiled=True,
    ).astype(jnp.float32)


def block_scores(queries, key_rows, mask_bias, block_start, block_rows, head_size):
    scores = jnp.einsum(
        "qhd,khd->hqk", queries, key_rows, preferred_element_type=jnp.float32
    ) * head_size ** (-0.5)
    return scores + mask_bias[None, block_start : block_start + block_rows]


def attention_forward(gathered, w_qkv, head_count, head_size, mask_bias):
    length = gathered.shape[0]
    projected = jnp.dot(gathered, w_qkv, preferred_element_type=jnp.float32).astype(jnp.bfloat16)
    projected = projected.reshape(length, 3, head_count, head_size)
    queries = projected[:, 0]
    key_rows = projected[:, 1]
    value_rows = projected[:, 2]
    block_rows = min(512, length)
    scores = block_scores(queries, key_rows, mask_bias, 0, block_rows, head_size)
    row_peak = jnp.max(scores, axis=-1, keepdims=True)
    row_total = row_peak + jnp.log(jnp.sum(jnp.exp(scores - row_peak), axis=-1, keepdims=True))
    weights = jnp.exp(scores - row_total).astype(jnp.bfloat16)
    outputs = jnp.einsum("hqk,khd->qhd", weights, value_rows, preferred_element_type=jnp.float32)
    totals = [row_total]
    attended = outputs.astype(jnp.bfloat16).reshape(length, head_count * head_size)
    return (attended, (queries, key_rows, value_rows, totals))


def attention_backward(upstream, w_out, attended, stored, head_count, head_size, mask_bias):
    queries, key_rows, value_rows, totals = stored
    length = upstream.shape[0]
    score_scale = head_size ** (-0.5)
    grad_out = inner_rows(attended, upstream)
    attended_grad = (
        times_transpose(upstream, w_out).astype(jnp.bfloat16).reshape(length, head_count, head_size)
    )
    block_rows = min(512, length)
    key_grads = jnp.zeros((length, head_count, head_size), jnp.float32)
    value_grads = jnp.zeros((length, head_count, head_size), jnp.float32)
    query_grads = []
    for number, block_start in enumerate(range(0, length, block_rows)):
        scores = block_scores(queries, key_rows, mask_bias, block_start, block_rows, head_size)
        weights = jnp.exp(scores - totals[number])
        value_grads = jnp.einsum(
            "hqk,qhd->khd",
            weights.astype(jnp.bfloat16),
            attended_grad,
            preferred_element_type=jnp.float32,
        )
        weight_grads = jnp.einsum(
            "qhd,khd->hqk", attended_grad, value_rows, preferred_element_type=jnp.float32
        )
        score_grads = (
            weights * (weight_grads - jnp.sum(weights * weight_grads, axis=-1, keepdims=True))
        ).astype(jnp.bfloat16)
        query_grads.append(
            jnp.einsum("hqk,khd->qhd", score_grads, key_rows, preferred_element_type=jnp.float32)
            * score_scale
        )
        key_grads = (
            jnp.einsum("hqk,qhd->khd", score_grads, queries, preferred_element_type=jnp.float32)
            * score_scale
        )
    projected_grad = jnp.stack([query_grads[0], key_grads, value_grads], axis=1)
    return (
        projected_grad.astype(jnp.bfloat16).reshape(length, 3 * head_count * head_size),
        grad_out,
    )


def block_forward(residual, matrices, gain_rows, bias_rows, head_count, head_size, mask_bias):
    w_qkv, w_out, w_in, w_down = matrices
    normed, norm_one = norm_forward(residual, gain_rows[0], bias_rows[0])
    gathered = gather_rows(normed.astype(jnp.bfloat16))
    attended, stored = attention_forward(gathered, w_qkv, head_count, head_size, mask_bias)
    middle = residual + branch_rows(attended, w_out)
    normed_two, norm_two = norm_forward(middle, gain_rows[1], bias_rows[1])
    gathered_two = gather_rows(normed_two.astype(jnp.bfloat16))
    hidden = jnp.dot(gathered_two, w_in, preferred_element_type=jnp.float32)
    active = jax.nn.gelu(hidden, approximate=False).astype(jnp.bfloat16)
    result = middle + branch_rows(active, w_down)
    return (result, (gathered, norm_one, attended, stored, gathered_two, norm_two, hidden, active))


def block_backward(upstream, matrices, gain_rows, saved_values, head_count, head_size, mask_bias):
    w_qkv, w_out, w_in, w_down = matrices
    gathered, norm_one, attended, stored, gathered_two, norm_two, hidden, active = saved_values
    down_full = gather_grads(upstream.astype(jnp.bfloat16))
    grad_down = inner_rows(active, down_full)
    active_grad = times_transpose(down_full, w_down)
    gelu_pull = jax.vjp(partial(jax.nn.gelu, approximate=False), hidden)[1]
    hidden_grad = gelu_pull(active_grad)[0].astype(jnp.bfloat16)
    grad_in = inner_rows(gathered_two, hidden_grad)
    normed_two_grad = input_rows(hidden_grad, w_in)
    middle_grad, gain_two, bias_two = norm_backward(normed_two_grad, norm_two, gain_rows[1])
    middle_grad = upstream + middle_grad
    middle_full = gather_grads(middle_grad.astype(jnp.bfloat16))
    projected_grad, grad_out = attention_backward(
        middle_full, w_out, attended, stored, head_count, head_size, mask_bias
    )
    grad_qkv = inner_rows(gathered, projected_grad)
    normed_grad = input_rows(projected_grad, w_qkv)
    input_grad, gain_one, bias_one = norm_backward(normed_grad, norm_one, gain_rows[0])
    return (
        middle_grad + input_grad,
        [grad_qkv, grad_out, grad_in, grad_down],
        (gain_one, gain_two, bias_one, bias_two),
    )


def embed_forward(residual, w_embed):
    residual_low = gather_rows(residual.astype(jnp.bfloat16))
    columns = jnp.dot(residual_low, w_embed, preferred_element_type=jnp.float32).astype(
        jnp.bfloat16
    )
    own_columns = lax.all_to_all(columns, "tensor", split_axis=0, concat_axis=1, tiled=True)
    return (own_columns.astype(jnp.float32), residual_low)


def embed_backward(upstream, residual_low, w_embed):
    columns = lax.all_to_all(
        upstream.astype(jnp.bfloat16), "tensor", split_axis=1, concat_axis=0, tiled=True
    )
    grad_embed = inner_rows(residual_low, columns)
    return (input_rows(columns, w_embed), grad_embed)


def slot_builder(gradients, unit_of_slot, unit_width):
    flat_units = jnp.concatenate([gradient.reshape(-1) for gradient in gradients]).reshape(
        -1, unit_width
    )
    unit_total = flat_units.shape[0]
    source = jnp.take(flat_units, jnp.clip(unit_of_slot, 0, unit_total - 1), axis=0)
    return jnp.where((unit_of_slot >= 0)[:, None], source, 0.0)


def per_device(
    tokens_in,
    positions,
    segment_ids,
    owners,
    master,
    first_moment,
    second_moment,
    norm_gains,
    norm_biases,
    norm_first,
    norm_second,
    cotangent,
):
    devices = lax.axis_size("dp")
    tensor_count = lax.axis_size("tensor")
    capacity = master.shape[0]
    unit_width = master.shape[1]
    unit_count = owners.shape[0]
    slot_index = slot_table(owners, devices, capacity)
    unit_of_slot = (
        jnp.full((devices * capacity,), -1, jnp.int32)
        .at[slot_index]
        .set(jnp.arange(unit_count, dtype=jnp.int32))
    )
    targets = unit_of_slot
    targets = jnp.where(targets < 0, unit_count, targets)
    placed = (
        jnp.zeros((unit_count, unit_width), jnp.bfloat16)
        .at[targets]
        .set(lax.all_gather(master.astype(jnp.bfloat16), "dp", axis=0, tiled=True), mode="drop")
    )
    shapes = weight_shapes(tensor_count)
    matrices = split_flat(placed.reshape(-1), shapes)
    encoder = matrices[0:4]
    w_embed = matrices[4]
    decoder = matrices[5:9]
    enc_heads = HE // tensor_count
    dec_heads = HD // tensor_count
    micro_count = tokens_in.shape[0]
    grad_sums = [jnp.zeros(matrix_shape, jnp.float32) for matrix_shape in shapes]
    norm_sums = jnp.zeros((4, DE + DD), jnp.float32)
    decoded_rows = []
    token_grads = []
    for micro_step in range(micro_count):
        tile_ids = segment_ids[micro_step, 0]
        mask_bias = jnp.where(tile_ids[:, None] == tile_ids[None, :], 0.0, MASK_FILL).astype(
            jnp.float32
        )
        position_now = positions[:, micro_step]
        residual = tokens_in[micro_step].astype(jnp.float32) + sincos_embed(position_now, DE)
        residual, enc_saved = block_forward(
            residual, encoder, norm_gains[:, :DE], norm_biases[:, :DE], enc_heads, HDE, mask_bias
        )
        residual, embed_low = embed_forward(residual, w_embed)
        residual = residual + sincos_embed(position_now, DD)
        residual, dec_saved = block_forward(
            residual, decoder, norm_gains[:, DE:], norm_biases[:, DE:], dec_heads, HDD, mask_bias
        )
        decoded_rows.append(residual)
        upstream, dec_grads, dec_norm = block_backward(
            cotangent[micro_step], decoder, norm_gains[:, DE:], dec_saved, dec_heads, HDD, mask_bias
        )
        upstream, grad_embed = embed_backward(upstream, embed_low, w_embed)
        upstream, enc_grads, enc_norm = block_backward(
            upstream, encoder, norm_gains[:, :DE], enc_saved, enc_heads, HDE, mask_bias
        )
        token_grads.append(upstream)
        step_grads = enc_grads + [grad_embed] + dec_grads
        step_norm = jnp.concatenate([jnp.stack(enc_norm), jnp.stack(dec_norm)], axis=1)
        grad_sums = [total_grad + new_grad for total_grad, new_grad in zip(grad_sums, step_grads)]
        norm_sums = norm_sums + step_norm
    reduced = lax.psum_scatter(
        slot_builder(grad_sums, unit_of_slot, unit_width), "dp", scatter_dimension=0, tiled=True
    )
    norm_total = lax.psum(norm_sums, ("dp", "tensor"))
    new_master, new_first, new_second = adamw(
        master, reduced, first_moment, second_moment, WEIGHT_DECAY, LEARN_RATE
    )
    norm_params = jnp.concatenate([norm_gains, norm_biases], axis=0)
    new_norms, norm_one_new, norm_two_new = adamw(
        norm_params, norm_total, norm_first, norm_second, 0.0, NORM_RATE
    )
    return (
        jnp.stack(decoded_rows),
        jnp.stack(token_grads),
        new_master,
        new_first,
        new_second,
        new_norms,
        norm_one_new,
        norm_two_new,
    )


MESH = pl.DeviceIdType.MESH
ALL = slice(None)


class Place:
    def __init__(self):
        self.d = lax.axis_index("dp")
        self.x = lax.axis_index("tensor")
        self.z = self.d // 4
        self.y = (self.d // 2) % 2
        self.c = self.d % 2
        self.ids = {
            "c": (self.d + 1 - 2 * self.c, self.x),
            "y": (self.d + 2 - 4 * self.y, self.x),
            "x": (self.d, 1 - self.x),
            "z+": (self.d + 4, self.x),
            "z-": (self.d - 4, self.x),
        }

    def greet(self, kinds):
        bar = pltpu.get_barrier_semaphore()
        for k in kinds:
            pl.semaphore_signal(bar, inc=1, device_id=self.ids[k], device_id_type=MESH)

        @pl.when(self.z < 3)
        def _():
            pl.semaphore_signal(bar, inc=1, device_id=self.ids["z+"], device_id_type=MESH)

        @pl.when(self.z > 0)
        def _():
            pl.semaphore_signal(bar, inc=1, device_id=self.ids["z-"], device_id_type=MESH)

        inner = jnp.where(jnp.logical_and(self.z > 0, self.z < 3), 1, 0)
        pl.semaphore_wait(bar, len(kinds) + 1 + inner)

    def there(self, disp):
        dz = disp[0]
        if dz == 0:
            return None
        return self.z + dz <= 3 if dz > 0 else self.z + dz >= 0

    def at(self, disp):
        dz, fy, fx = disp
        return (1 - self.x if fx else self.x, self.z + dz, 1 - self.y if fy else self.y)


def when(cond, f):
    if cond is None:
        f()
    else:
        pl.when(cond)(f)


def both(a, b):
    if a is None:
        return b
    if b is None:
        return a
    return jnp.logical_and(a, b)


def spread(order):
    out = {}
    todo = [((0, 0, 0), -1, 0)]
    while todo:
        (dz, fy, fx), last, way = todo.pop(0)
        nxt = []
        for i, a in enumerate(order):
            if i < last:
                continue
            if a == "z":
                for s in (1, -1):
                    if i == last and s != way:
                        continue
                    n = (dz - s, fy, fx)
                    if abs(n[0]) <= 3:
                        nxt.append((n, "z+" if s > 0 else "z-", i, s))
            elif i > last:
                n = (dz, 1, fx) if a == "y" else (dz, fy, 1)
                nxt.append((n, a, i, 0))
        out[(dz, fy, fx)] = [(n, w) for n, w, _, _ in nxt]
        todo += [(n, i, s) for n, _, i, s in nxt]
    return out


def hops(d):
    return abs(d[0]) + d[1] + d[2]


BACK = {"z+": "z-", "z-": "z+", "x": "x", "y": "y"}


def add_rows(acc, got, step=80):
    n = acc.shape[0]
    while n % step:
        step -= 16

    def body(i, _):
        r = pl.ds(pl.multiple_of(i * step, step), step)
        acc[r, :] = acc[r, :] + got[r, :]
        return 0

    lax.fori_loop(0, n // step, body, 0)


SHARD_UNITS = 656
PANEL = 128
GROUPS = ((0, 1), (2,), (3,), (4, 5, 6), (7, 8))

PLAN_OUT = (
    ("zy", "yz", "zy", "zy", "zy"),
    ("yzx", "xzy", "yzx", "zxy", "zyx"),
    (
        0, 192, 2, 5, 6, 1, 4, 8, 12, 10, 256, 3, 64, 9, 257, 66, 7, 260, 65, 11, 68, 259, 261, 13, 128, 268, 258, 69,
        14, 15, 265, 264, 196, 193, 72, 262, 194, 129, 136, 18, 201, 197, 19, 266, 137, 16, 204, 263, 73, 269, 198,
        24, 26, 22, 267, 34, 23, 133, 20, 21, 195, 25, 200, 70, 67, 270, 271, 29, 202, 130, 131, 199, 74, 76, 132, 33,
        140, 71, 134, 275, 272, 203, 205, 27, 77, 75, 138, 40, 276, 36, 135, 282, 274, 206, 207, 78, 79, 290, 283,
        141, 139, 292, 80, 81, 278, 281, 39, 210, 211, 41, 84, 142, 143, 277, 208, 82, 289, 91, 88, 218, 144, 35, 209,
        296, 147, 216, 37, 96, 28, 212, 294, 226, 38, 146, 213, 224, 85, 217, 285, 150, 153, 32, 161, 83, 154, 168,
        231, 95, 222, 298, 219, 145, 148, 232, 220, 92, 228, 87, 288, 157, 291, 286, 103, 284, 221, 234, 159, 17, 86,
        156, 152, 106, 273, 227, 155, 90, 42, 230, 293, 30, 31, 297, 229, 162, 214, 93, 165, 99, 233, 166, 100, 225,
        295, 94, 223, 98, 215, 280, 158, 164, 101, 287, 160, 279, 163, 102, 170, 105, 151, 167, 169, 89, 97, 104, 149,
    ),
)
PLAN_BACK = (
    ("zxy", "zxy", "yzx", "yzx", "yzx"),
    ("zy", "zy", "zy", "yz", "yz"),
    (
        256, 259, 258, 257, 268, 263, 270, 261, 128, 260, 262, 264, 130, 129, 277, 135, 265, 272, 266, 0, 269, 1, 5,
        6, 267, 12, 271, 2, 131, 132, 134, 279, 274, 192, 142, 136, 138, 276, 11, 133, 146, 194, 8, 141, 15, 273, 3,
        20, 281, 275, 278, 137, 4, 144, 10, 283, 26, 7, 199, 149, 198, 64, 282, 79, 140, 280, 197, 66, 145, 143, 206,
        139, 83, 22, 69, 193, 148, 9, 200, 150, 205, 284, 151, 285, 202, 84, 13, 17, 19, 208, 147, 77, 287, 16, 195,
        152, 65, 70, 14, 286, 155, 18, 290, 154, 288, 153, 291, 75, 201, 71, 204, 196, 72, 207, 213, 217, 215, 86,
        212, 24, 21, 210, 23, 76, 78, 25, 289, 67, 156, 294, 292, 90, 214, 85, 203, 68, 157, 80, 219, 209, 295, 74,
        82, 27, 160, 298, 211, 158, 216, 73, 218, 159, 164, 87, 28, 297, 29, 161, 89, 81, 91, 32, 30, 88, 220, 221,
        36, 92, 168, 163, 167, 33, 93, 296, 223, 165, 96, 37, 94, 40, 224, 166, 100, 35, 222, 97, 104, 293, 226, 228,
        227, 99, 31, 95, 101, 162, 34, 232, 38, 170, 169, 231, 225, 230, 41, 39, 106, 42, 102, 103, 105, 98, 229, 233,
        234,
    ),
)


def layout(shapes, shards):
    table = []
    unit_at, row_at, flat_at = 0, 0, 0
    starts = [g[0] for g in GROUPS]
    for i, (rows, cols) in enumerate(shapes):
        if i in starts:
            unit_at = -(-unit_at // 16) * 16
        rb, panels = rows // shards, cols // PANEL
        units = rb * cols // 512
        padded = -(-rb // 16) * 16
        table.append((rb, panels, units, unit_at, row_at, padded, flat_at))
        unit_at += units
        row_at += padded * panels
        flat_at += units * shards
    return table, unit_at, row_at


def unit_places(units, table, shards):
    place = jnp.zeros_like(units)
    for _, _, n, first, _, _, lo in table:
        v = units - lo
        here = (v // n) * SHARD_UNITS + first + v % n
        place = jnp.where(v >= 0, here, place)
    return place


def own_units(owners, mine, capacity):
    count = owners.shape[0] // 128
    hit = (owners[:, 0] == mine).reshape(count, 128)
    lane = jnp.arange(128)
    tri = (lane[:, None] <= lane[None, :]).astype(jnp.bfloat16)
    within = jnp.dot(hit.astype(jnp.bfloat16), tri, preferred_element_type=jnp.float32)
    totals = within[:, 127].astype(jnp.int32)
    upto = jnp.sum(jnp.where(jnp.arange(count)[:, None] >= jnp.arange(count)[None, :], totals[None, :], 0), axis=1)
    slot = jnp.arange(capacity, dtype=jnp.int32)
    block = jnp.sum((upto[None, :] <= slot[:, None]).astype(jnp.int32), axis=1)
    pick = block[:, None] == jnp.arange(count)[None, :]
    before = jnp.sum(jnp.where(pick, (upto - totals)[None, :], 0), axis=1)
    row = jnp.dot(pick.astype(jnp.bfloat16), within.astype(jnp.bfloat16), preferred_element_type=jnp.float32)
    rank = (slot - before).astype(jnp.float32)
    at = jnp.sum((row <= rank[:, None]).astype(jnp.int32), axis=1)
    return block * 128 + at, slot < upto[count - 1]


BY_ROWS = (1, 3, 6, 8)


def position_table():
    cols = []
    for width in (DE, DD):
        side = width // 16 * 6
        parts = (width - 2 * side, side, side)
        tab = np.zeros((48, width), np.float64)
        col = 0
        for i, n in enumerate(parts):
            half = n // 2
            freq = 1.0 / 10000.0 ** (np.arange(half) / half)
            ang = np.arange(16)[:, None] * freq[None, :]
            tab[16 * i:16 * i + 16, col:col + n] = np.concatenate([np.sin(ang), np.cos(ang)], axis=1)
            col += n
        cols.append(tab)
    left = np.concatenate(cols, axis=1).astype(np.float32)
    terms = []
    for _ in range(3):
        terms.append(left.astype(ml_dtypes.bfloat16))
        left = left - terms[-1].astype(np.float32)
    return np.stack(terms)


def dot(a, b):
    return jnp.dot(a, b, preferred_element_type=jnp.float32)


def dot_nt(a, b):
    return lax.dot_general(a, b, (((1,), (1,)), ((), ())), preferred_element_type=jnp.float32)


def dot_tn(a, b):
    return lax.dot_general(a, b, (((0,), (0,)), ((), ())), preferred_element_type=jnp.float32)


def lanes(i, n=128):
    return pl.ds(pl.multiple_of(i * n, n), n)


def ln_parts(x):
    c = x - jnp.mean(x, axis=-1, keepdims=True)
    inv = lax.rsqrt(jnp.mean(c * c, axis=-1, keepdims=True) + NORM_EPS)
    return c * inv, inv


def ln_back(up, m, inv, gain):
    s = up * gain
    a = jnp.mean(s, axis=-1, keepdims=True)
    b = jnp.mean(s * m, axis=-1, keepdims=True)
    return inv * (s - a - m * b), jnp.sum(up * m, axis=0, keepdims=True), jnp.sum(up, axis=0, keepdims=True)


class Block:
    def __init__(self, width, heads, size, hidden, first, table, col):
        self.width, self.heads, self.size, self.hidden, self.col = width, heads, size, hidden, col
        self.q, self.o, self.a, self.b = table[first:first + 4]
        self.part = heads // 2 * size
        self.per = 128 // size


def panel(w, t, mat, g, lo=0, num=16):
    rb, _, _, _, at, padded, _ = mat
    rows = pl.ds(pl.multiple_of(at + g * padded, 16), padded)
    v = w[t, lo:lo + num, rows, :] if isinstance(lo, int) else w[t, pl.ds(lo, num), rows, :]
    if padded > rb:
        v = v.astype(jnp.float32)[:, :rb].reshape(num * rb, 128).astype(jnp.bfloat16)
        return v
    return v.reshape(num * rb, 128)


def pair(w, mat, g):
    return jnp.concatenate([panel(w, 0, mat, g), panel(w, 1, mat, g)], axis=1)


def block_fwd(b, x, xo, w, gains, biases, same, n1, proj, p, att, ow, m1, i1, n2, m2, i2, act, slope,
              need, keep):
    cols = slice(b.col, b.col + b.width)
    m, inv = ln_parts(x[...])
    m1[...] = m
    i1[...] = inv
    n1[...] = (m * gains[0:1, cols] + biases[0:1, cols]).astype(jnp.bfloat16)
    keep(0)
    need(0)
    gq = b.q[1]

    def qkv(g, _):
        r = dot(n1[...], pair(w, b.q, g)).astype(jnp.bfloat16)
        proj[:, lanes(g)] = r[:, :128]
        proj[:, lanes(gq + g)] = r[:, 128:]
        return 0

    lax.fori_loop(0, gq, qkv, 0)
    np_ = b.part // 128
    lane = lax.broadcasted_iota(jnp.int32, (256, 128), 1)
    masks = [lane // b.size == i for i in range(b.per)]

    def heads(i, _):
        t, j = i // np_, i % np_
        q = proj[:, lanes(t * gq + j)]
        k = proj[:, lanes(t * gq + np_ + j)]
        v = proj[:, lanes(t * gq + 2 * np_ + j)]
        total = jnp.zeros((256, 128), jnp.float32)
        for h in range(b.per):
            z = dot_nt(jnp.where(masks[h], q, 0), k) * b.size ** (-0.5) + same
            e = jnp.exp(z - jnp.max(z, axis=-1, keepdims=True))
            s = e * (1.0 / jnp.sum(e, axis=-1, keepdims=True))
            p[i * b.per + h] = s
            total = total + dot(s.astype(jnp.bfloat16), jnp.where(masks[h], v, 0))
        att[:, lanes(i)] = total.astype(jnp.bfloat16)
        return 0

    lax.fori_loop(0, 2 * np_, heads, 0)
    keep(1)
    need(1)
    for t in range(2):
        for g in range(b.width // 128):
            ow[t, :, g * 128:(g + 1) * 128] = panel(w, t, b.o, g)
    x1 = x[...] + dot(att[:, :b.part], ow[0]) + dot(att[:, b.part:], ow[1])
    xo[...] = x1
    m, inv = ln_parts(x1)
    m2[...] = m
    i2[...] = inv
    n2[...] = (m * gains[1:2, cols] + biases[1:2, cols]).astype(jnp.bfloat16)
    keep(2)
    need(2)
    ga = b.a[1]

    def up(g, _):
        h = dot(n2[...], pair(w, b.a, g))
        big = 0.5 * (1.0 + lax.erf(h * 0.7071067811865476))
        act_v = (h * big).astype(jnp.bfloat16)
        dens = big + h * (0.3989422804014327 * jnp.exp(-0.5 * h * h))
        act[:, lanes(g)] = act_v[:, :128]
        act[:, lanes(ga + g)] = act_v[:, 128:]
        slope[:, lanes(g)] = dens[:, :128]
        slope[:, lanes(ga + g)] = dens[:, 128:]
        return 0

    lax.fori_loop(0, ga, up, 0)
    keep(3)
    need(3)
    half = b.hidden // 2

    def down(g, _):
        w0 = jnp.concatenate([panel(w, 0, b.b, 2 * g), panel(w, 0, b.b, 2 * g + 1)], axis=1)
        w1 = jnp.concatenate([panel(w, 1, b.b, 2 * g), panel(w, 1, b.b, 2 * g + 1)], axis=1)
        xo[:, lanes(g, 256)] += dot(act[:, :half], w0) + dot(act[:, half:], w1)
        return 0

    lax.fori_loop(0, b.width // 256, down, 0)


def block_bwd(b, dr, w, gains, same, n1, proj, p, att, ow, m1, i1, n2, m2, i2, act, slope,
              r, dh, r1, dp_out, acc, da, norm_out, keep):
    cols = slice(b.col, b.col + b.width)
    r[...] = dr[...].astype(jnp.bfloat16)
    keep(3)
    half = b.hidden // 2
    rb = b.b[0]
    gb = b.width // 128
    num = 4

    def hidden(i, _):
        t, lo = i // (16 // num), (i % (16 // num)) * num
        wc = jnp.concatenate([panel(w, t, b.b, g, lo, num) for g in range(gb)], axis=1)
        at = lanes(i, num * rb)
        dh[:, at] = (dot_nt(r[...], wc) * slope[:, at]).astype(jnp.bfloat16)
        return 0

    lax.fori_loop(0, 2 * (16 // num), hidden, 0)
    keep(2)
    ga = b.a[1]
    acc[...] = jnp.zeros_like(acc)

    def up(g, _):
        d = jnp.concatenate([dh[:, lanes(g)], dh[:, lanes(ga + g)]], axis=1)
        acc[...] += dot_nt(d, pair(w, b.a, g))
        return 0

    lax.fori_loop(0, ga, up, 0)
    dx, dg, db = ln_back(acc[...], m2[...], i2[...], gains[1:2, cols])
    norm_out[1:2, cols] = dg
    norm_out[3:4, cols] = db
    dx1 = dr[...] + dx
    dr[...] = dx1
    r1[...] = dx1.astype(jnp.bfloat16)
    keep(1)
    for t in range(2):
        da[:, t * b.part:(t + 1) * b.part] = dot_nt(r1[...], ow[t]).astype(jnp.bfloat16)
    gq = b.q[1]
    np_ = b.part // 128
    lane = lax.broadcasted_iota(jnp.int32, (256, 128), 1)
    masks = [lane // b.size == i for i in range(b.per)]
    scale = b.size ** (-0.5)

    def heads(i, _):
        t, j = i // np_, i % np_
        q = proj[:, lanes(t * gq + j)]
        k = proj[:, lanes(t * gq + np_ + j)]
        v = proj[:, lanes(t * gq + 2 * np_ + j)]
        up_ = da[:, lanes(i)]
        dq = jnp.zeros((256, 128), jnp.float32)
        dk = jnp.zeros((256, 128), jnp.float32)
        dv = jnp.zeros((256, 128), jnp.float32)
        for h in range(b.per):
            s = p[i * b.per + h]
            u = jnp.where(masks[h], up_, 0)
            dp = dot_nt(u, v)
            dv = dv + dot_tn(s.astype(jnp.bfloat16), u)
            t1 = s * dp
            dz = (t1 - s * jnp.sum(t1, axis=-1, keepdims=True)).astype(jnp.bfloat16)
            dq = dq + dot(dz, jnp.where(masks[h], k, 0))
            dk = dk + dot_tn(dz, jnp.where(masks[h], q, 0))
        dp_out[:, lanes(t * gq + j)] = (dq * scale).astype(jnp.bfloat16)
        dp_out[:, lanes(t * gq + np_ + j)] = (dk * scale).astype(jnp.bfloat16)
        dp_out[:, lanes(t * gq + 2 * np_ + j)] = dv.astype(jnp.bfloat16)
        return 0

    lax.fori_loop(0, 2 * np_, heads, 0)
    keep(0)
    acc[...] = jnp.zeros_like(acc)

    def qkv(g, _):
        d = jnp.concatenate([dp_out[:, lanes(g)], dp_out[:, lanes(gq + g)]], axis=1)
        acc[...] += dot_nt(d, pair(w, b.q, g))
        return 0

    lax.fori_loop(0, gq, qkv, 0)
    dx, dg, db = ln_back(acc[...], m1[...], i1[...], gains[0:1, cols])
    norm_out[0:1, cols] = dg
    norm_out[2:3, cols] = db
    dr[...] = dr[...] + dx


ACTS = (DE, DE, DE, FFE, DE, DD, DD, DD, FFD)
GRADS = (3 * DE, DE, FFE, DE, DD, 3 * DD, DD, FFD, DD)


def chain_kernel(table, tok, pos, tile, gains, biases, cot, tab, w_hbm, *refs):
    dec, dx0, norm_out = refs[:3]
    kept_out = refs[3:21]
    kept = refs[21:39]
    acts, grads = kept[:9], kept[9:]
    (w, pe, pd, se, sd, proj_e, proj_d, da_e, da_d, ow_e, ow_d, m1e, m2e, m1d, m2d, i1e, i2e, i1d, i2d,
     x, y, acc_e, acc_d, w_sem, out_sem) = refs[39:]
    enc_b = Block(DE, HE, HDE, FFE, 0, table, 0)
    dec_b = Block(DD, HD, HDD, FFD, 5, table, DE)
    em = table[4]

    def load(m):
        rows = pl.ds(table[m][4], table[m][1] * table[m][5])
        return pltpu.make_async_copy(w_hbm.at[:, :, rows], w.at[:, :, rows], w_sem.at[m])

    def store(i):
        return pltpu.make_async_copy(kept[i], kept_out[i], out_sem.at[i])

    for m in range(9):
        load(m).start()
    row = lax.broadcasted_iota(jnp.int32, (48, 256), 0)
    spots = [jnp.concatenate([pos[0, i:i + 1, :], pos[1, i:i + 1, :]], axis=1) for i in range(3)]
    hot = jnp.logical_or(jnp.logical_or(row == spots[0], row == spots[1] + 16), row == spots[2] + 32)
    hot = jnp.where(hot, 1.0, 0.0).astype(jnp.bfloat16)
    ids = tile[lax.axis_index("tensor")]
    tiles = jnp.where(lax.broadcasted_iota(jnp.int32, (16, 256), 0) == ids, 1.0, 0.0).astype(jnp.bfloat16)
    same = (1.0 - dot_tn(tiles, tiles)) * MASK_FILL
    x[...] = tok[...].astype(jnp.float32) + sum(dot_tn(hot, tab[i, :, :DE]) for i in range(3))
    n1e, ae, n2e, ue, low, n1d, ad, n2d, ud = acts
    dpe, r1e, dhe, re, dlow, dpd, r1d, dhd, rd = grads
    block_fwd(enc_b, x, dx0, w, gains, biases, same, n1e, proj_e, pe, ae, ow_e, m1e, i1e, n2e, m2e, i2e, ue, se,
              lambda k: load(k).wait(), lambda k: store(k).start())
    low[...] = dx0[...].astype(jnp.bfloat16)
    store(4).start()
    load(4).wait()
    for g in range(2):
        v = dot(low[...], pair(w, em, g)).astype(jnp.bfloat16).astype(jnp.float32)
        y[:, g * 128:(g + 1) * 128] = v[:, :128]
        y[:, 256 + g * 128:256 + (g + 1) * 128] = v[:, 128:]
    y[...] += sum(dot_tn(hot, tab[i, :, DE:]) for i in range(3))
    block_fwd(dec_b, y, dec, w, gains, biases, same, n1d, proj_d, pd, ad, ow_d, m1d, i1d, n2d, m2d, i2d, ud, sd,
              lambda k: load(5 + k).wait(), lambda k: store(5 + k).start())
    y[...] = cot[...]
    block_bwd(dec_b, y, w, gains, same, n1d, proj_d, pd, ad, ow_d, m1d, i1d, n2d, m2d, i2d, ud, sd,
              rd, dhd, r1d, dpd, acc_d, da_d, norm_out, lambda k: store(14 + k).start())
    dlow[...] = y[...].astype(jnp.bfloat16)
    store(13).start()
    for g in range(2):
        d = jnp.concatenate([dlow[:, g * 128:(g + 1) * 128], dlow[:, 256 + g * 128:256 + (g + 1) * 128]], axis=1)
        v = dot_nt(d, pair(w, em, g))
        if g == 0:
            dx0[...] = v
        else:
            dx0[...] += v
    block_bwd(enc_b, dx0, w, gains, same, n1e, proj_e, pe, ae, ow_e, m1e, i1e, n2e, m2e, i2e, ue, se,
              re, dhe, r1e, dpe, acc_e, da_e, norm_out, lambda k: store(9 + k).start())
    for i in range(18):
        store(i).wait()


def chain(tokens, pos, tile, gains, biases, cot, full, table):
    f32, bf16 = jnp.float32, jnp.bfloat16
    S = jax.ShapeDtypeStruct
    outs = [S((256, DD), f32), S((256, DE), f32), S((4, DE + DD), f32)]
    kept = [(256, n) for n in ACTS + GRADS]
    outs += [S(k, bf16) for k in kept]
    V = pltpu.VMEM
    scratch = [V(k, bf16) for k in kept] + [
        V((2, 16) + full.shape[-2:], bf16),
        V((HE, 256, 256), f32), V((HD, 256, 256), f32), V((256, FFE), f32), V((256, FFD), f32),
        V((256, 3 * DE), bf16), V((256, 3 * DD), bf16), V((256, DE), bf16), V((256, DD), bf16),
        V((2, DE // 2, DE), bf16), V((2, DD // 2, DD), bf16),
        V((256, DE), f32), V((256, DE), f32), V((256, DD), f32), V((256, DD), f32)] + [V((256, 1), f32)] * 4 + [
        V((256, DE), f32), V((256, DD), f32), V((256, DE), f32), V((256, DD), f32),
        pltpu.SemaphoreType.DMA((9,)), pltpu.SemaphoreType.DMA((18,))]
    vmem = pl.BlockSpec(memory_space=pltpu.VMEM)
    hbm = pl.BlockSpec(memory_space=pl.ANY)
    args = (tokens, pos, tile, gains, biases, cot, jnp.asarray(position_table()),
            full.reshape(2, 16, full.shape[-2], 128))
    return pl.pallas_call(
        partial(chain_kernel, table), out_shape=outs, in_specs=[vmem] * 7 + [hbm], out_specs=[vmem] * 3 + [hbm] * 18,
        scratch_shapes=scratch, compiler_params=pltpu.CompilerParams(vmem_limit_bytes=63 << 20), name="chain",
        cost_estimate=pl.CostEstimate(flops=11_000_000_000, bytes_accessed=40_000_000, transcendentals=5_000_000),
    )(*args)


def grad_panels(table, m, act, grad, turned, put):
    mat = table[m]
    rb, panels, padded = mat[0], mat[1], mat[5]
    count = act.shape[1]

    def turn(i, _):
        turned[pl.ds(pl.multiple_of(i * 128, 128), 128), :] = act[:, lanes(i)].T
        return 0

    lax.fori_loop(0, count // 128, turn, 0)

    def place(t, g, v):
        if padded > rb:
            v = v.reshape(16, rb, 128)
            v = jnp.concatenate([v, jnp.zeros((16, padded - rb, 128), jnp.float32)], axis=1).astype(jnp.bfloat16)
        else:
            v = v.astype(jnp.bfloat16).reshape(16, rb, 128)
        put(t, g, v)

    if m in BY_ROWS:
        half = count // 2

        def body(i, _):
            t, g = i // (panels // 2), i % (panels // 2)
            v = dot(turned[pl.ds(pl.multiple_of(t * half, 128), half), :], grad[:, lanes(g, 256)])
            place(t, 2 * g, v[:, :128])
            place(t, 2 * g + 1, v[:, 128:])
            return 0

        lax.fori_loop(0, panels, body, 0)
    else:
        def body(g, _):
            d = jnp.concatenate([grad[:, lanes(g)], grad[:, lanes(panels + g)]], axis=1)
            v = dot(turned[:count, :], d)
            place(0, g, v[:, :128])
            place(1, g, v[:, 128:])
            return 0

        lax.fori_loop(0, panels, body, 0)


class Wires:
    def __init__(self, place, sem):
        self.place, self.sem, self.used, self.waits = place, sem, 0, []

    def new(self, n=1):
        self.used += n
        assert self.used <= self.sem.shape[0], self.used
        return self.used - n

    def copy(self, k, src, dst, way):
        return pltpu.make_async_remote_copy(src_ref=src, dst_ref=dst, send_sem=self.sem.at[k], recv_sem=self.sem.at[k + 1],
                                            device_id=self.place.ids[way], device_id_type=MESH)

    def send(self, k, src, dst, way, cond=None):
        cp = self.copy(k, src, dst, way)
        when(cond, cp.start)
        self.waits.append((cond, cp))

    def land(self, k, dst, cond=None):
        when(cond, self.copy(k, dst, dst, "c").wait_recv)

    def drain(self):
        for cond, cp in self.waits:
            when(cond, cp.wait_send)


def edge_slots(order):
    slots, used, shared = {}, 0, {}
    for d, kids in sorted(spread(order).items()):
        for _, way in kids:
            if way in "xy" and order.index("z") < order.index(way):
                key = (way, d[1], d[2])
                if key not in shared:
                    shared[key] = used
                    used += 4
                slots[d, way] = (shared[key], 4)
            else:
                slots[d, way] = (used, 1)
                used += 1
    return slots, used


def beyond(p, way):
    return p.z < 3 if way == "z+" else p.z > 0 if way == "z-" else None


def reduce_events(p, w, order, own, half, bufs, ready, done):
    tree = spread(order)
    pair = {d: w.new(2) for d in tree}
    wire = {d: w.new(2) for d in tree}
    parent = {nd: (d, way) for d, t in tree.items() for nd, way in t}
    slots, _ = edge_slots(order)

    def buffer(up, way):
        first, n = slots[up, way]
        return bufs.at[first + p.z + up[0] if n > 1 else first]

    events = []
    far = sorted(tree, key=lambda d: (-hops(d), d))
    for d in far:
        def act(d=d):
            cond = p.there(d)

            def step():
                acc = own(d)
                ready(d)
                w.land(pair[d], half(d))
                add_rows(acc, half(d))
                for nd, way in tree[d]:
                    buf = buffer(d, way)

                    def take(buf=buf, nd=nd):
                        w.land(wire[nd], buf)
                        add_rows(acc, buf)
                    when(beyond(p, way), take)
            when(cond, step)
            if hops(d) == 0:
                done()
            else:
                up, way = parent[d]
                w.send(wire[d], own(d), buffer(up, way), BACK[way], cond)
        events.append(act)

    def share(give):
        for d in far:
            w.send(pair[d], give(d), half(d), "c", p.there(d))

    return events, share, far


def gather_events(p, w, order, first, at):
    tree = spread(order)
    pair = {d: w.new(2) for d in tree}
    wire = {d: w.new(2) for d in tree}
    events = []
    for d in sorted(tree, key=lambda d: (hops(d), d)):
        def act(d=d):
            cond = p.there(d)
            blk = at(d, p.c)
            if hops(d):
                w.land(wire[d], blk, cond)
                src = blk
            else:
                src = first
            for nd, way in tree[d]:
                w.send(wire[nd], src, blk, way, both(cond, beyond(p, way)))
            w.send(pair[d], src, blk, "c", cond)
        events.append(act)

    def finish():
        for d in tree:
            w.land(pair[d], at(d, 1 - p.c), p.there(d))

    return events, finish


def run_events(lists, order, extra=iter(()), every=8):
    assert sorted(order) == sorted(64 * g + i for g, acts in enumerate(lists) for i in range(len(acts)))
    for n, k in enumerate(order):
        if n % every == 0:
            next(extra, None)
        lists[k // 64][k % 64]()
    for _ in extra:
        pass


def group_span(table, mats):
    first, last = table[mats[0]], table[mats[-1]]
    units = last[3] + last[2] - first[3]
    return first[3], -(-units // 16) * 16, first[4], last[4] + last[1] * last[5] - first[4]


def units_to_panels(table, mats, units, flat, put):
    base, count = table[mats[0]][3], units.shape[0]
    for k in range(4):
        flat[pl.ds(k, count, stride=4), :] = units[:, 128 * k:128 * (k + 1)].astype(jnp.float32)
    for m in mats:
        rb, panels, n, first, _, padded, _ = table[m]
        for g in range(panels):
            v = flat[pl.ds(4 * (first - base) + g, rb, stride=panels), :]
            if padded > rb:
                v = jnp.concatenate([v, jnp.zeros((padded - rb, 128), jnp.float32)], axis=0)
            put(m, g, v.astype(jnp.bfloat16))


def panels_to_units(table, mats, take, flat, units):
    base, count = table[mats[0]][3], units.shape[0]
    used = 0
    for m in mats:
        rb, panels, n, first, _, padded, _ = table[m]
        for g in range(panels):
            flat[pl.ds(4 * (first - base) + g, rb, stride=panels), :] = take(m, g)[:rb]
        used = 4 * (first - base + n)
    if used < 4 * count:
        flat[used:4 * count, :] = jnp.zeros((4 * count - used, 128), jnp.float32)
    for k in range(4):
        units[:, 128 * k:128 * (k + 1)] = flat[pl.ds(k, count, stride=4), :].astype(jnp.bfloat16)


class Swap:
    def __init__(self, p, w, src, out, give, keep):
        self.p, self.w, self.src, self.out, self.give, self.keep = p, w, src, out, give, keep
        self.k, self.own = w.new(2), w.new()

    def local(self):
        return pltpu.make_async_copy(self.src.at[self.keep], self.out.at[self.p.x], self.w.sem.at[self.own])

    def start(self):
        self.w.send(self.k, self.src.at[self.give], self.out.at[self.p.x], "x")
        self.local().start()

    def finish(self):
        self.w.land(self.k, self.out.at[1 - self.p.x])
        self.local().wait()


def weights_kernel(table, groups, plan, parts, tok_in, pos_in, cot_in, out, tok, pos, cot, *rest):
    n = len(groups)
    accs, halves, bufs, shards = (rest[i * n:(i + 1) * n] for i in range(4))
    flat, sem = rest[4 * n:]
    p = Place()
    p.greet(["c", "y", "x"])
    w = Wires(p, sem)
    swaps = [Swap(p, w, a, b, 1 - p.x, p.x) for a, b in ((tok_in, tok), (pos_in, pos), (cot_in, cot))]
    for s in swaps:
        s.start()
    lists, finishes = [], []
    for g, mats in enumerate(groups):
        u0, un, r0, rn = group_span(table, mats)
        acc, half, buf, shard = accs[g], halves[g], bufs[g], shards[g]
        own_sem = w.new()
        loads = {d: w.new() for d in spread(plan[0][g])}

        def own(d, acc=acc):
            return acc.at[p.at(d)[1:]]

        def other(d, half=half):
            return half.at[p.at(d)[1:]]

        def load(d, u0=u0, un=un, own=own, loads=loads):
            return pltpu.make_async_copy(parts.at[p.at(d)[1:] + (p.c, pl.ds(u0, un))], own(d), sem.at[loads[d]])

        def ready(d, load=load):
            load(d).wait()

        def done(mats=mats, acc=acc, shard=shard, r0=r0):
            def put(m, i, v):
                lo = table[m][4] - r0 + i * table[m][5]
                shard[lo:lo + table[m][5], :] = v
            units_to_panels(table, mats, acc.at[p.z, p.y], flat, put)

        ev, share, far = reduce_events(p, w, plan[0][g], own, other, buf, ready, done)

        def begin(load=load, share=share, far=far, u0=u0, un=un):
            share(lambda d: parts.at[p.at(d)[1:] + (1 - p.c, pl.ds(u0, un))])
            for d in far:
                when(p.there(d), load(d).start)

        def at(d, core, r0=r0, rn=rn):
            t, z, y = p.at(d)
            return out.at[t, z, y, core, pl.ds(r0, rn)]

        def local(shard=shard, r0=r0, rn=rn, own_sem=own_sem):
            return pltpu.make_async_copy(shard, out.at[p.x, p.z, p.y, p.c, pl.ds(r0, rn)], sem.at[own_sem])

        ag, finish = gather_events(p, w, plan[1][g], shard, at)

        def send_first(act=ag[0], local=local):
            act()
            local().start()

        lists.append([begin] + ev + [send_first] + ag[1:])
        finishes += [finish, lambda local=local: local().wait()]
    run_events(lists, plan[2])
    for f in finishes + [s.finish for s in swaps]:
        f()
    w.drain()


def spread_weights(parts, tokens, pos, cot, table, rows, groups, plan, ident):
    spans = [group_span(table, m) for m in groups]
    bf16 = jnp.bfloat16
    S = jax.ShapeDtypeStruct
    scratch = [pltpu.VMEM((4, 2, s[1], 512), bf16) for s in spans] * 2
    scratch += [pltpu.VMEM((edge_slots(o)[1], s[1], 512), bf16) for s, o in zip(spans, plan[0])]
    scratch += [pltpu.VMEM((s[3], 128), bf16) for s in spans]
    scratch += [pltpu.VMEM((4 * max(s[1] for s in spans), 128), jnp.float32),
                pltpu.SemaphoreType.DMA((len(groups) * (1 + 5 * 14 + 4 * 28) + 9,))]
    hbm = pl.BlockSpec(memory_space=pl.ANY)
    return pl.pallas_call(
        partial(weights_kernel, table, groups, plan),
        out_shape=[S((2, 4, 2, 2, rows, 128), bf16)] + [S(v.shape, v.dtype) for v in (tokens, pos, cot)],
        in_specs=[hbm] * 4, out_specs=[hbm] * 4,
        scratch_shapes=scratch,
        compiler_params=pltpu.CompilerParams(collective_id=ident, has_side_effects=True, vmem_limit_bytes=62 << 20),
        name="spread_weights",
    )(parts, tokens, pos, cot)


def return_kernel(table, groups, plan, *refs):
    n = len(groups)
    kept_in, small_src, dec_in, dx_in, out, small_out, dec, dx = refs[:18], *refs[18:25]
    rest = refs[25:]
    kept, rest = rest[:18], rest[18:]
    acts, grads = kept[:9], kept[9:]
    sides, halves, bufs, units = (rest[i * n:(i + 1) * n] for i in range(4))
    flat, turned, mid, line, load_sem, sem = rest[4 * n:]

    def load(i):
        return pltpu.make_async_copy(kept_in[i], kept[i], load_sem.at[i])

    first = sorted(range(n), key=lambda g: plan[2].index(64 * g))
    for g in first:
        for m in groups[g]:
            load(m).start()
            load(9 + m).start()
    p = Place()
    p.greet(["c", "y", "x"])
    w = Wires(p, sem)
    swaps = [Swap(p, w, a, b, 1 - p.x, p.x) for a, b in ((dec_in, dec), (dx_in, dx))]
    lists, finishes = [], []
    for g, mats in enumerate(groups):
        u0, un, r0, rn = group_span(table, mats)
        side, half, buf, unit = sides[g], halves[g], bufs[g], units[g]
        own_sem = w.new()

        def own(d, side=side):
            return side.at[(p.c,) + p.at(d)]

        def other(d, half=half):
            return half.at[p.at(d)]

        def done(mats=mats, side=side, unit=unit, r0=r0):
            mine = side.at[p.c, p.x, p.z, p.y]

            def take(m, i):
                lo = table[m][4] - r0 + i * table[m][5]
                return mine[lo:lo + table[m][5], :].astype(jnp.float32)
            panels_to_units(table, mats, take, flat, unit)

        ev, share, far = reduce_events(p, w, plan[0][g], own, other, buf, lambda d: None, done)

        def begin(mats=mats, side=side, share=share, r0=r0):
            for m in mats:
                lo, padded = table[m][4] - r0, table[m][5]

                def put(t, i, v, lo=lo, padded=padded):
                    v = v.reshape(4, 2, 2, padded, 128)
                    rows = pl.ds(pl.multiple_of(lo + i * padded, 16), padded)
                    side[0, t, :, :, rows, :] = v[:, :, 0]
                    side[1, t, :, :, rows, :] = v[:, :, 1]
                load(m).wait()
                load(9 + m).wait()
                grad_panels(table, m, acts[m], grads[m], turned, put)
            share(lambda d: side.at[(1 - p.c,) + p.at(d)])

        def at(d, core, u0=u0, un=un):
            _, z, y = p.at(d)
            return out.at[z, y, core, pl.ds(u0, un)]

        def local(unit=unit, u0=u0, un=un, own_sem=own_sem):
            return pltpu.make_async_copy(unit, out.at[p.z, p.y, p.c, pl.ds(u0, un)], sem.at[own_sem])

        ag, finish = gather_events(p, w, plan[1][g], unit, at)

        def send_first(act=ag[0], local=local):
            act()
            local().start()

        lists.append([begin] + ev + [send_first] + ag[1:])
        finishes += [finish, lambda local=local: local().wait()]
    last = max(plan[2].index(64 * g + len(spread(plan[0][g]))) for g in range(n))
    g, i = plan[2][last] // 64, plan[2][last] % 64
    act = lists[g][i]

    def with_swaps():
        act()
        for s in swaps:
            s.start()

    lists[g][i] = with_swaps
    run_events(lists, plan[2], total_steps(p, w, small_src, small_out, mid, line))
    for f in finishes + [s.finish for s in swaps]:
        f()
    w.drain()


def total_steps(p, w, src, out, mid, line):
    k = [w.new(2) for _ in range(9)]
    now = src
    for i, way in enumerate(("c", "x", "y")):
        w.send(k[i], now, mid.at[i], way)
        yield
        w.land(k[i], mid.at[i])
        nxt = mid.at[3 + i] if i < 2 else line.at[p.z]
        nxt[...] = now[...] + mid[i]
        now = nxt
    for i in range(4):
        lo, hi = jnp.maximum(p.z - i, 0), jnp.minimum(p.z + i, 3)
        if i > 0:
            w.land(k[2 + i], line.at[lo], p.z >= i)
            w.land(k[5 + i], line.at[hi], p.z + i <= 3)
        if i < 3:
            w.send(k[3 + i], line.at[lo], line.at[lo], "z+", jnp.logical_and(p.z >= i, p.z < 3))
            w.send(k[6 + i], line.at[hi], line.at[hi], "z-", jnp.logical_and(p.z + i <= 3, p.z > 0))
            yield
    out[...] = (line[0] + line[1]) + (line[2] + line[3])


def return_grads(kept, small, dec, dx, table, total_units, groups, plan, ident):
    spans = [group_span(table, m) for m in groups]
    bf16 = jnp.bfloat16
    S = jax.ShapeDtypeStruct
    V = pltpu.VMEM
    scratch = [V(v.shape, v.dtype) for v in kept]
    scratch += [V((2, 2, 4, 2, s[3], 128), bf16) for s in spans]
    scratch += [V((2, 4, 2, s[3], 128), bf16) for s in spans]
    scratch += [V((edge_slots(o)[1], s[3], 128), bf16) for s, o in zip(spans, plan[0])]
    scratch += [V((s[1], 512), bf16) for s in spans]
    scratch += [V((4 * max(s[1] for s in spans), 128), jnp.float32), V((FFE, 256), bf16),
                V((5,) + small.shape, small.dtype), V((4,) + small.shape, small.dtype), pltpu.SemaphoreType.DMA((18,)),
                pltpu.SemaphoreType.DMA((len(groups) * (1 + 4 * 14 + 4 * 28) + 24,))]
    vmem = pl.BlockSpec(memory_space=pltpu.VMEM)
    hbm = pl.BlockSpec(memory_space=pl.ANY)
    return pl.pallas_call(
        partial(return_kernel, table, groups, plan),
        out_shape=(S((4, 2, 2, total_units, 512), bf16), S(small.shape, small.dtype), S(dec.shape, dec.dtype), S(dx.shape, dx.dtype)),
        in_specs=[hbm] * 18 + [vmem, hbm, hbm], out_specs=(hbm, vmem, hbm, hbm),
        scratch_shapes=scratch,
        compiler_params=pltpu.CompilerParams(collective_id=ident, has_side_effects=True, vmem_limit_bytes=63 << 20),
        name="return_grads",
    )(*kept, small, dec, dx)


def sequence_device(tokens_in, positions, segment_ids, owners, master, first_moment, second_moment, norm_gains,
                    norm_biases, norm_first, norm_second, cotangent):
    shapes = weight_shapes(2)
    table, _, rows = layout(shapes, 16)
    unit, used = own_units(owners, lax.axis_index("dp"), master.shape[0])
    place = unit_places(unit, table, 16)
    parts = jnp.zeros((16 * SHARD_UNITS, 512), jnp.bfloat16)
    parts = parts.at[jnp.where(used, place, 16 * SHARD_UNITS)].set(master.astype(jnp.bfloat16), mode="drop", unique_indices=True)
    full, tok, pos, cot = spread_weights(parts.reshape(4, 2, 2, SHARD_UNITS, 512), tokens_in, positions.transpose(1, 0, 2),
                                         cotangent, table, rows, GROUPS, PLAN_OUT, 1)
    kept = chain(tok.reshape(256, DE), pos, segment_ids, norm_gains, norm_biases, cot.reshape(256, DD), full, table)
    decoded, dx0, norms = kept[:3]
    spread_out, norm_total, decoded, dx0 = return_grads(kept[3:], norms, decoded.reshape(2, 128, DD), dx0.reshape(2, 128, DE), table,
                                                        SHARD_UNITS, GROUPS, PLAN_BACK, 2)
    spread_out = spread_out.reshape(16 * SHARD_UNITS, 512)
    reduced = jnp.where(used[:, None], jnp.take(spread_out, jnp.clip(place, 0, 16 * SHARD_UNITS - 1), axis=0).astype(jnp.float32), 0.0)
    new_master, new_first, new_second = adamw(master, reduced, first_moment, second_moment, WEIGHT_DECAY, LEARN_RATE)
    norm_params = jnp.concatenate([norm_gains, norm_biases], axis=0)
    new_norms, norm_one_new, norm_two_new = adamw(norm_params, norm_total, norm_first, norm_second, 0.0, NORM_RATE)
    return (decoded, dx0, new_master, new_first, new_second, new_norms, norm_one_new, norm_two_new)


def solution(mesh):
    step = sequence_device if (mesh.shape["dp"], mesh.shape["tensor"]) == (16, 2) else per_device
    return jax.shard_map(
        step,
        mesh=mesh,
        in_specs=(
            P(None, ("dp", "tensor"), None),
            P(None, None, ("dp", "tensor")),
            P(None, "dp", None),
            P(),
            P("dp", "tensor"),
            P("dp", "tensor"),
            P("dp", "tensor"),
            P(),
            P(),
            P(),
            P(),
            P(None, ("dp", "tensor"), None),
        ),
        out_specs=(
            P(None, ("dp", "tensor"), None),
            P(None, ("dp", "tensor"), None),
            P("dp", "tensor"),
            P("dp", "tensor"),
            P("dp", "tensor"),
            P(),
            P(),
            P(),
        ),
        check_vma=False,
    )
```

```python
from functools import partial

import jax
import jax.numpy as jnp
import ml_dtypes
import numpy as np
from jax import lax
from jax.experimental import pallas as pl
from jax.experimental.pallas import tpu as pltpu
from jax.sharding import PartitionSpec as P

DE = 768
HE = 12
HDE = 64
FFE = 3072
DD = 512
HD = 16
HDD = 32
FFD = 2048
STEP = 10


NORM_EPS = 1e-06
BETA_ONE = 0.5
BETA_TWO = 0.5
LEARN_RATE = 0.03
NORM_RATE = 0.3
WEIGHT_DECAY = 0.05
ADAM_EPS = 1e-08
MASK_FILL = -1000000000.0


def sincos_part(coordinate, part_width):
    halfway = part_width // 2
    frequency = 1.0 / 10000.0 ** (jnp.arange(halfway, dtype=jnp.float32) / halfway)
    angles = coordinate.astype(jnp.float32)[:, None] * frequency[None, :]
    return jnp.concatenate([jnp.sin(angles), jnp.cos(angles)], axis=1)


def sincos_embed(positions, model_width):
    side_width = model_width // 16 * 6
    first_width = model_width - 2 * side_width
    return jnp.concatenate(
        [
            sincos_part(positions[0], first_width),
            sincos_part(positions[1], side_width),
            sincos_part(positions[2], side_width),
        ],
        axis=1,
    )


def slot_table(owners, devices, capacity):
    owner_ids = owners[:, 0]
    onehot = (owner_ids[:, None] == jnp.arange(devices, dtype=jnp.int32)[None, :]).astype(jnp.int32)
    before = jnp.cumsum(onehot, axis=0) - onehot
    owner_rank = jnp.sum(before * onehot, axis=1)
    return owner_ids * capacity + owner_rank


def weight_shapes(tensor_count):
    enc_heads = HE // tensor_count
    dec_heads = HD // tensor_count
    return [
        (DE, 3 * enc_heads * HDE),
        (enc_heads * HDE, DE),
        (DE, FFE // tensor_count),
        (FFE // tensor_count, DE),
        (DE, DD // tensor_count),
        (DD, 3 * dec_heads * HDD),
        (dec_heads * HDD, DD),
        (DD, FFD // tensor_count),
        (FFD // tensor_count, DD),
    ]


def split_flat(flat_vector, shapes):
    pieces = []
    offset = 0
    for matrix_shape in shapes:
        length = matrix_shape[0] * matrix_shape[1]
        pieces.append(flat_vector[offset : offset + length].reshape(matrix_shape))
        offset += length
    return pieces


def adamw(weights, gradient, moment_one, moment_two, decay_rate, step_rate):
    one_new = BETA_ONE * moment_one + (1.0 - BETA_ONE) * gradient
    two_new = BETA_TWO * moment_two + (1.0 - BETA_TWO) * gradient * gradient
    one_hat = one_new / (1.0 - BETA_ONE**STEP)
    two_hat = two_new / (1.0 - BETA_TWO**STEP)
    weights_new = weights - step_rate * (
        one_hat / (jnp.sqrt(two_hat) + ADAM_EPS) + decay_rate * weights
    )
    return (weights_new, one_new, two_new)


def norm_forward(values, gain_row, bias_row):
    center = values - jnp.mean(values, axis=-1, keepdims=True)
    spread = jnp.mean(center * center, axis=-1, keepdims=True)
    inverse = lax.rsqrt(spread + NORM_EPS)
    normed = center * inverse
    return (normed * gain_row + bias_row, (normed, inverse))


def norm_backward(upstream, stored, gain_row):
    normed, inverse = stored
    scaled = upstream * gain_row
    mean_one = jnp.mean(scaled, axis=-1, keepdims=True)
    mean_two = jnp.mean(scaled * normed, axis=-1, keepdims=True)
    return (
        inverse * (scaled - mean_one - normed * mean_two),
        jnp.sum(upstream * normed, axis=0),
        jnp.sum(upstream, axis=0),
    )


def inner_rows(left_side, right_side):
    return lax.dot_general(
        left_side, right_side, (((0,), (0,)), ((), ())), preferred_element_type=jnp.float32
    )


def times_transpose(left_side, right_side):
    return lax.dot_general(
        left_side, right_side, (((1,), (1,)), ((), ())), preferred_element_type=jnp.float32
    )


def gather_rows(values):
    return lax.all_gather(values, "tensor", axis=0, tiled=True)


def gather_grads(values):
    return lax.all_gather(values, "tensor", axis=0, tiled=True)


def branch_rows(values, weight):
    return lax.psum_scatter(
        jnp.dot(values, weight, preferred_element_type=jnp.float32).astype(jnp.bfloat16),
        "tensor",
        scatter_dimension=0,
        tiled=True,
    ).astype(jnp.float32)


def input_rows(values, weight):
    return lax.psum_scatter(
        times_transpose(values, weight).astype(jnp.bfloat16),
        "tensor",
        scatter_dimension=0,
        tiled=True,
    ).astype(jnp.float32)


def block_scores(queries, key_rows, mask_bias, block_start, block_rows, head_size):
    scores = jnp.einsum(
        "qhd,khd->hqk", queries, key_rows, preferred_element_type=jnp.float32
    ) * head_size ** (-0.5)
    return scores + mask_bias[None, block_start : block_start + block_rows]


def attention_forward(gathered, w_qkv, head_count, head_size, mask_bias):
    length = gathered.shape[0]
    projected = jnp.dot(gathered, w_qkv, preferred_element_type=jnp.float32).astype(jnp.bfloat16)
    projected = projected.reshape(length, 3, head_count, head_size)
    queries = projected[:, 0]
    key_rows = projected[:, 1]
    value_rows = projected[:, 2]
    block_rows = min(512, length)
    scores = block_scores(queries, key_rows, mask_bias, 0, block_rows, head_size)
    row_peak = jnp.max(scores, axis=-1, keepdims=True)
    row_total = row_peak + jnp.log(jnp.sum(jnp.exp(scores - row_peak), axis=-1, keepdims=True))
    weights = jnp.exp(scores - row_total).astype(jnp.bfloat16)
    outputs = jnp.einsum("hqk,khd->qhd", weights, value_rows, preferred_element_type=jnp.float32)
    totals = [row_total]
    attended = outputs.astype(jnp.bfloat16).reshape(length, head_count * head_size)
    return (attended, (queries, key_rows, value_rows, totals))


def attention_backward(upstream, w_out, attended, stored, head_count, head_size, mask_bias):
    queries, key_rows, value_rows, totals = stored
    length = upstream.shape[0]
    score_scale = head_size ** (-0.5)
    grad_out = inner_rows(attended, upstream)
    attended_grad = (
        times_transpose(upstream, w_out).astype(jnp.bfloat16).reshape(length, head_count, head_size)
    )
    block_rows = min(512, length)
    key_grads = jnp.zeros((length, head_count, head_size), jnp.float32)
    value_grads = jnp.zeros((length, head_count, head_size), jnp.float32)
    query_grads = []
    for number, block_start in enumerate(range(0, length, block_rows)):
        scores = block_scores(queries, key_rows, mask_bias, block_start, block_rows, head_size)
        weights = jnp.exp(scores - totals[number])
        value_grads = jnp.einsum(
            "hqk,qhd->khd",
            weights.astype(jnp.bfloat16),
            attended_grad,
            preferred_element_type=jnp.float32,
        )
        weight_grads = jnp.einsum(
            "qhd,khd->hqk", attended_grad, value_rows, preferred_element_type=jnp.float32
        )
        score_grads = (
            weights * (weight_grads - jnp.sum(weights * weight_grads, axis=-1, keepdims=True))
        ).astype(jnp.bfloat16)
        query_grads.append(
            jnp.einsum("hqk,khd->qhd", score_grads, key_rows, preferred_element_type=jnp.float32)
            * score_scale
        )
        key_grads = (
            jnp.einsum("hqk,qhd->khd", score_grads, queries, preferred_element_type=jnp.float32)
            * score_scale
        )
    projected_grad = jnp.stack([query_grads[0], key_grads, value_grads], axis=1)
    return (
        projected_grad.astype(jnp.bfloat16).reshape(length, 3 * head_count * head_size),
        grad_out,
    )


def block_forward(residual, matrices, gain_rows, bias_rows, head_count, head_size, mask_bias):
    w_qkv, w_out, w_in, w_down = matrices
    normed, norm_one = norm_forward(residual, gain_rows[0], bias_rows[0])
    gathered = gather_rows(normed.astype(jnp.bfloat16))
    attended, stored = attention_forward(gathered, w_qkv, head_count, head_size, mask_bias)
    middle = residual + branch_rows(attended, w_out)
    normed_two, norm_two = norm_forward(middle, gain_rows[1], bias_rows[1])
    gathered_two = gather_rows(normed_two.astype(jnp.bfloat16))
    hidden = jnp.dot(gathered_two, w_in, preferred_element_type=jnp.float32)
    active = jax.nn.gelu(hidden, approximate=False).astype(jnp.bfloat16)
    result = middle + branch_rows(active, w_down)
    return (result, (gathered, norm_one, attended, stored, gathered_two, norm_two, hidden, active))


def block_backward(upstream, matrices, gain_rows, saved_values, head_count, head_size, mask_bias):
    w_qkv, w_out, w_in, w_down = matrices
    gathered, norm_one, attended, stored, gathered_two, norm_two, hidden, active = saved_values
    down_full = gather_grads(upstream.astype(jnp.bfloat16))
    grad_down = inner_rows(active, down_full)
    active_grad = times_transpose(down_full, w_down)
    gelu_pull = jax.vjp(partial(jax.nn.gelu, approximate=False), hidden)[1]
    hidden_grad = gelu_pull(active_grad)[0].astype(jnp.bfloat16)
    grad_in = inner_rows(gathered_two, hidden_grad)
    normed_two_grad = input_rows(hidden_grad, w_in)
    middle_grad, gain_two, bias_two = norm_backward(normed_two_grad, norm_two, gain_rows[1])
    middle_grad = upstream + middle_grad
    middle_full = gather_grads(middle_grad.astype(jnp.bfloat16))
    projected_grad, grad_out = attention_backward(
        middle_full, w_out, attended, stored, head_count, head_size, mask_bias
    )
    grad_qkv = inner_rows(gathered, projected_grad)
    normed_grad = input_rows(projected_grad, w_qkv)
    input_grad, gain_one, bias_one = norm_backward(normed_grad, norm_one, gain_rows[0])
    return (
        middle_grad + input_grad,
        [grad_qkv, grad_out, grad_in, grad_down],
        (gain_one, gain_two, bias_one, bias_two),
    )


def embed_forward(residual, w_embed):
    residual_low = gather_rows(residual.astype(jnp.bfloat16))
    columns = jnp.dot(residual_low, w_embed, preferred_element_type=jnp.float32).astype(
        jnp.bfloat16
    )
    own_columns = lax.all_to_all(columns, "tensor", split_axis=0, concat_axis=1, tiled=True)
    return (own_columns.astype(jnp.float32), residual_low)


def embed_backward(upstream, residual_low, w_embed):
    columns = lax.all_to_all(
        upstream.astype(jnp.bfloat16), "tensor", split_axis=1, concat_axis=0, tiled=True
    )
    grad_embed = inner_rows(residual_low, columns)
    return (input_rows(columns, w_embed), grad_embed)


def slot_builder(gradients, unit_of_slot, unit_width):
    flat_units = jnp.concatenate([gradient.reshape(-1) for gradient in gradients]).reshape(
        -1, unit_width
    )
    unit_total = flat_units.shape[0]
    source = jnp.take(flat_units, jnp.clip(unit_of_slot, 0, unit_total - 1), axis=0)
    return jnp.where((unit_of_slot >= 0)[:, None], source, 0.0)


def per_device(
    tokens_in,
    positions,
    segment_ids,
    owners,
    master,
    first_moment,
    second_moment,
    norm_gains,
    norm_biases,
    norm_first,
    norm_second,
    cotangent,
):
    devices = lax.axis_size("dp")
    tensor_count = lax.axis_size("tensor")
    capacity = master.shape[0]
    unit_width = master.shape[1]
    unit_count = owners.shape[0]
    slot_index = slot_table(owners, devices, capacity)
    unit_of_slot = (
        jnp.full((devices * capacity,), -1, jnp.int32)
        .at[slot_index]
        .set(jnp.arange(unit_count, dtype=jnp.int32))
    )
    targets = unit_of_slot
    targets = jnp.where(targets < 0, unit_count, targets)
    placed = (
        jnp.zeros((unit_count, unit_width), jnp.bfloat16)
        .at[targets]
        .set(lax.all_gather(master.astype(jnp.bfloat16), "dp", axis=0, tiled=True), mode="drop")
    )
    shapes = weight_shapes(tensor_count)
    matrices = split_flat(placed.reshape(-1), shapes)
    encoder = matrices[0:4]
    w_embed = matrices[4]
    decoder = matrices[5:9]
    enc_heads = HE // tensor_count
    dec_heads = HD // tensor_count
    micro_count = tokens_in.shape[0]
    grad_sums = [jnp.zeros(matrix_shape, jnp.float32) for matrix_shape in shapes]
    norm_sums = jnp.zeros((4, DE + DD), jnp.float32)
    decoded_rows = []
    token_grads = []
    for micro_step in range(micro_count):
        tile_ids = segment_ids[micro_step, 0]
        mask_bias = jnp.where(tile_ids[:, None] == tile_ids[None, :], 0.0, MASK_FILL).astype(
            jnp.float32
        )
        position_now = positions[:, micro_step]
        residual = tokens_in[micro_step].astype(jnp.float32) + sincos_embed(position_now, DE)
        residual, enc_saved = block_forward(
            residual, encoder, norm_gains[:, :DE], norm_biases[:, :DE], enc_heads, HDE, mask_bias
        )
        residual, embed_low = embed_forward(residual, w_embed)
        residual = residual + sincos_embed(position_now, DD)
        residual, dec_saved = block_forward(
            residual, decoder, norm_gains[:, DE:], norm_biases[:, DE:], dec_heads, HDD, mask_bias
        )
        decoded_rows.append(residual)
        upstream, dec_grads, dec_norm = block_backward(
            cotangent[micro_step], decoder, norm_gains[:, DE:], dec_saved, dec_heads, HDD, mask_bias
        )
        upstream, grad_embed = embed_backward(upstream, embed_low, w_embed)
        upstream, enc_grads, enc_norm = block_backward(
            upstream, encoder, norm_gains[:, :DE], enc_saved, enc_heads, HDE, mask_bias
        )
        token_grads.append(upstream)
        step_grads = enc_grads + [grad_embed] + dec_grads
        step_norm = jnp.concatenate([jnp.stack(enc_norm), jnp.stack(dec_norm)], axis=1)
        grad_sums = [total_grad + new_grad for total_grad, new_grad in zip(grad_sums, step_grads)]
        norm_sums = norm_sums + step_norm
    reduced = lax.psum_scatter(
        slot_builder(grad_sums, unit_of_slot, unit_width), "dp", scatter_dimension=0, tiled=True
    )
    norm_total = lax.psum(norm_sums, ("dp", "tensor"))
    new_master, new_first, new_second = adamw(
        master, reduced, first_moment, second_moment, WEIGHT_DECAY, LEARN_RATE
    )
    norm_params = jnp.concatenate([norm_gains, norm_biases], axis=0)
    new_norms, norm_one_new, norm_two_new = adamw(
        norm_params, norm_total, norm_first, norm_second, 0.0, NORM_RATE
    )
    return (
        jnp.stack(decoded_rows),
        jnp.stack(token_grads),
        new_master,
        new_first,
        new_second,
        new_norms,
        norm_one_new,
        norm_two_new,
    )


MESH = pl.DeviceIdType.MESH
ALL = slice(None)


class Place:
    def __init__(self):
        self.d = lax.axis_index("dp")
        self.x = lax.axis_index("tensor")
        self.z = self.d // 4
        self.y = (self.d // 2) % 2
        self.c = self.d % 2
        self.ids = {
            "c": (self.d + 1 - 2 * self.c, self.x),
            "y": (self.d + 2 - 4 * self.y, self.x),
            "x": (self.d, 1 - self.x),
            "z+": (self.d + 4, self.x),
            "z-": (self.d - 4, self.x),
        }

    def greet(self, kinds):
        bar = pltpu.get_barrier_semaphore()
        for k in kinds:
            pl.semaphore_signal(bar, inc=1, device_id=self.ids[k], device_id_type=MESH)

        @pl.when(self.z < 3)
        def _():
            pl.semaphore_signal(bar, inc=1, device_id=self.ids["z+"], device_id_type=MESH)

        @pl.when(self.z > 0)
        def _():
            pl.semaphore_signal(bar, inc=1, device_id=self.ids["z-"], device_id_type=MESH)

        inner = jnp.where(jnp.logical_and(self.z > 0, self.z < 3), 1, 0)
        pl.semaphore_wait(bar, len(kinds) + 1 + inner)

    def there(self, disp):
        dz = disp[0]
        if dz == 0:
            return None
        return self.z + dz <= 3 if dz > 0 else self.z + dz >= 0

    def at(self, disp):
        dz, fy, fx = disp
        return (1 - self.x if fx else self.x, self.z + dz, 1 - self.y if fy else self.y)


def when(cond, f):
    if cond is None:
        f()
    else:
        pl.when(cond)(f)


def both(a, b):
    if a is None:
        return b
    if b is None:
        return a
    return jnp.logical_and(a, b)


def spread(order):
    out = {}
    todo = [((0, 0, 0), -1, 0)]
    while todo:
        (dz, fy, fx), last, way = todo.pop(0)
        nxt = []
        for i, a in enumerate(order):
            if i < last:
                continue
            if a == "z":
                for s in (1, -1):
                    if i == last and s != way:
                        continue
                    n = (dz - s, fy, fx)
                    if abs(n[0]) <= 3:
                        nxt.append((n, "z+" if s > 0 else "z-", i, s))
            elif i > last:
                n = (dz, 1, fx) if a == "y" else (dz, fy, 1)
                nxt.append((n, a, i, 0))
        out[(dz, fy, fx)] = [(n, w) for n, w, _, _ in nxt]
        todo += [(n, i, s) for n, _, i, s in nxt]
    return out


def hops(d):
    return abs(d[0]) + d[1] + d[2]


BACK = {"z+": "z-", "z-": "z+", "x": "x", "y": "y"}


def add_rows(acc, got, step=80):
    n = acc.shape[0]
    while n % step:
        step -= 16

    def body(i, _):
        r = pl.ds(pl.multiple_of(i * step, step), step)
        acc[r, :] = acc[r, :] + got[r, :]
        return 0

    lax.fori_loop(0, n // step, body, 0)


SHARD_UNITS = 656
PANEL = 128
GROUPS = ((0, 1), (2,), (3,), (4, 5, 6), (7, 8))

PLAN_OUT = (
    ("zy", "yz", "zy", "yz", "zy"),
    ("zyx", "yzx", "yzx", "zxy", "xzy"),
    (
        192, 194, 128, 0, 193, 130, 198, 195, 133, 197, 134, 129, 132, 137, 201, 1, 199, 136, 131, 9, 196, 138, 202,
        135, 140, 8, 200, 141, 2, 139, 205, 203, 204, 142, 143, 3, 206, 5, 4, 12, 207, 147, 144, 6, 64, 256, 208, 7,
        211, 10, 146, 212, 11, 65, 13, 265, 261, 268, 150, 257, 221, 148, 260, 154, 219, 67, 66, 153, 258, 218, 68,
        14, 264, 69, 15, 161, 259, 262, 156, 70, 157, 226, 71, 16, 19, 266, 263, 73, 227, 18, 17, 72, 74, 26, 168,
        224, 162, 269, 20, 267, 76, 149, 152, 77, 34, 155, 75, 270, 29, 27, 271, 78, 79, 36, 272, 35, 275, 83, 80, 40,
        166, 282, 273, 90, 216, 39, 290, 25, 209, 233, 217, 82, 296, 42, 84, 276, 24, 21, 281, 22, 31, 164, 98, 231,
        285, 91, 96, 86, 280, 151, 88, 37, 33, 232, 32, 277, 89, 213, 23, 28, 278, 41, 283, 93, 289, 228, 85, 215, 92,
        97, 220, 145, 230, 170, 284, 160, 279, 288, 87, 165, 104, 225, 222, 169, 100, 295, 103, 286, 81, 274, 30, 163,
        293, 294, 292, 159, 167, 229, 95, 210, 94, 287, 99, 38, 223, 158, 291, 102, 106, 214, 101, 105, 298, 234, 297,
    ),
)
PLAN_BACK = (
    ("zxy", "yzx", "zyx", "yzx", "xzy"),
    ("zy", "zy", "zy", "yz", "yz"),
    (
        256, 257, 258, 262, 261, 269, 64, 259, 67, 260, 65, 69, 263, 66, 78, 264, 271, 278, 276, 77, 270, 268, 267,
        71, 70, 275, 282, 85, 72, 266, 76, 265, 192, 82, 68, 199, 277, 73, 0, 84, 274, 74, 272, 5, 273, 80, 75, 279,
        6, 79, 13, 128, 204, 1, 281, 2, 12, 89, 283, 280, 11, 141, 129, 19, 8, 83, 4, 195, 86, 193, 87, 3, 134, 15, 7,
        81, 284, 285, 133, 88, 91, 14, 10, 197, 194, 90, 22, 196, 132, 286, 131, 201, 288, 287, 130, 16, 18, 21, 198,
        9, 92, 20, 205, 93, 291, 202, 200, 290, 136, 289, 143, 292, 26, 140, 208, 150, 206, 17, 94, 23, 135, 25, 212,
        213, 294, 95, 142, 203, 96, 24, 138, 148, 139, 207, 137, 211, 27, 214, 210, 100, 97, 295, 144, 215, 149, 104,
        146, 209, 147, 28, 29, 151, 218, 219, 217, 145, 154, 32, 101, 153, 106, 30, 216, 36, 155, 152, 296, 33, 220,
        105, 221, 293, 98, 156, 40, 157, 224, 31, 103, 298, 222, 160, 158, 223, 164, 102, 99, 228, 37, 161, 227, 165,
        41, 225, 168, 159, 226, 35, 42, 34, 229, 163, 297, 39, 231, 230, 232, 162, 167, 170, 234, 38, 166, 169, 233,
    ),
)


def layout(shapes, shards):
    table = []
    unit_at, row_at, flat_at = 0, 0, 0
    starts = [g[0] for g in GROUPS]
    for i, (rows, cols) in enumerate(shapes):
        if i in starts:
            unit_at = -(-unit_at // 16) * 16
        rb, panels = rows // shards, cols // PANEL
        units = rb * cols // 512
        padded = -(-rb // 16) * 16
        table.append((rb, panels, units, unit_at, row_at, padded, flat_at))
        unit_at += units
        row_at += padded * panels
        flat_at += units * shards
    return table, unit_at, row_at


def unit_places(units, table, shards):
    place = jnp.zeros_like(units)
    for _, _, n, first, _, _, lo in table:
        v = units - lo
        here = (v // n) * SHARD_UNITS + first + v % n
        place = jnp.where(v >= 0, here, place)
    return place


def own_units(owners, mine, capacity):
    count = owners.shape[0] // 128
    hit = (owners[:, 0] == mine).reshape(count, 128)
    lane = jnp.arange(128)
    tri = (lane[:, None] <= lane[None, :]).astype(jnp.bfloat16)
    within = jnp.dot(hit.astype(jnp.bfloat16), tri, preferred_element_type=jnp.float32)
    totals = within[:, 127].astype(jnp.int32)
    upto = jnp.sum(jnp.where(jnp.arange(count)[:, None] >= jnp.arange(count)[None, :], totals[None, :], 0), axis=1)
    slot = jnp.arange(capacity, dtype=jnp.int32)
    block = jnp.sum((upto[None, :] <= slot[:, None]).astype(jnp.int32), axis=1)
    pick = block[:, None] == jnp.arange(count)[None, :]
    before = jnp.sum(jnp.where(pick, (upto - totals)[None, :], 0), axis=1)
    row = jnp.dot(pick.astype(jnp.bfloat16), within.astype(jnp.bfloat16), preferred_element_type=jnp.float32)
    rank = (slot - before).astype(jnp.float32)
    at = jnp.sum((row <= rank[:, None]).astype(jnp.int32), axis=1)
    return block * 128 + at, slot < upto[count - 1]


BY_ROWS = (1, 3, 6, 8)


def position_table():
    cols = []
    for width in (DE, DD):
        side = width // 16 * 6
        parts = (width - 2 * side, side, side)
        tab = np.zeros((48, width), np.float64)
        col = 0
        for i, n in enumerate(parts):
            half = n // 2
            freq = 1.0 / 10000.0 ** (np.arange(half) / half)
            ang = np.arange(16)[:, None] * freq[None, :]
            tab[16 * i:16 * i + 16, col:col + n] = np.concatenate([np.sin(ang), np.cos(ang)], axis=1)
            col += n
        cols.append(tab)
    left = np.concatenate(cols, axis=1).astype(np.float32)
    terms = []
    for _ in range(3):
        terms.append(left.astype(ml_dtypes.bfloat16))
        left = left - terms[-1].astype(np.float32)
    return np.stack(terms)


def dot(a, b):
    return jnp.dot(a, b, preferred_element_type=jnp.float32)


def dot_nt(a, b):
    return lax.dot_general(a, b, (((1,), (1,)), ((), ())), preferred_element_type=jnp.float32)


def dot_tn(a, b):
    return lax.dot_general(a, b, (((0,), (0,)), ((), ())), preferred_element_type=jnp.float32)


def lanes(i, n=128):
    return pl.ds(pl.multiple_of(i * n, n), n)


def ln_parts(x):
    c = x - jnp.mean(x, axis=-1, keepdims=True)
    inv = lax.rsqrt(jnp.mean(c * c, axis=-1, keepdims=True) + NORM_EPS)
    return c * inv, inv


def ln_back(up, m, inv, gain):
    s = up * gain
    a = jnp.mean(s, axis=-1, keepdims=True)
    b = jnp.mean(s * m, axis=-1, keepdims=True)
    return inv * (s - a - m * b), jnp.sum(up * m, axis=0, keepdims=True), jnp.sum(up, axis=0, keepdims=True)


class Block:
    def __init__(self, width, heads, size, hidden, first, table, col):
        self.width, self.heads, self.size, self.hidden, self.col = width, heads, size, hidden, col
        self.q, self.o, self.a, self.b = table[first:first + 4]
        self.part = heads // 2 * size
        self.per = 128 // size


def panel(w, t, mat, g, lo=0, num=16):
    rb, _, _, _, at, padded, _ = mat
    rows = pl.ds(pl.multiple_of(at + g * padded, 16), padded)
    v = w[t, lo:lo + num, rows, :] if isinstance(lo, int) else w[t, pl.ds(lo, num), rows, :]
    if padded > rb:
        v = v.astype(jnp.float32)[:, :rb].reshape(num * rb, 128).astype(jnp.bfloat16)
        return v
    return v.reshape(num * rb, 128)


def pair(w, mat, g):
    return jnp.concatenate([panel(w, 0, mat, g), panel(w, 1, mat, g)], axis=1)


def repeat(count, step, f):
    step = max(k for k in range(1, step + 1) if count % k == 0)

    def turn(i, _):
        for k in range(step):
            f(i * step + k)
        return 0

    if step == count:
        turn(0, 0)
    else:
        lax.fori_loop(0, count // step, turn, 0)


def pull(acc, up, w, mat, step):
    count = mat[1]
    step = max(k for k in range(1, step + 1) if count % k == 0)

    def part(i):
        gs = [i * step + k for k in range(step)]
        d = jnp.concatenate([up[:, lanes(o + g)] for g in gs for o in (0, count)], axis=1)
        return dot_nt(d, jnp.concatenate([pair(w, mat, g) for g in gs], axis=1))

    acc[...] = part(0)

    def turn(i, _):
        acc[...] += part(i)
        return 0

    lax.fori_loop(1, count // step, turn, 0)


def block_fwd(b, x, xo, w, gains, biases, same, n1, proj, p, att, ow, m1, i1, n2, m2, i2, act, slope,
              need, keep):
    cols = slice(b.col, b.col + b.width)
    m, inv = ln_parts(x[...])
    m1[...] = m
    i1[...] = inv
    n1[...] = (m * gains[0:1, cols] + biases[0:1, cols]).astype(jnp.bfloat16)
    keep(0)
    need(0)
    gq = b.q[1]

    def qkv(g):
        r = dot(n1[...], pair(w, b.q, g)).astype(jnp.bfloat16)
        proj[:, lanes(g)] = r[:, :128]
        proj[:, lanes(gq + g)] = r[:, 128:]

    repeat(gq, 9, qkv)
    np_ = b.part // 128
    lane = lax.broadcasted_iota(jnp.int32, (256, 128), 1)
    masks = [lane // b.size == i for i in range(b.per)]

    def heads(i, _):
        t, j = i // np_, i % np_
        q = proj[:, lanes(t * gq + j)]
        k = proj[:, lanes(t * gq + np_ + j)]
        v = proj[:, lanes(t * gq + 2 * np_ + j)]
        total = jnp.zeros((256, 128), jnp.float32)
        for h in range(b.per):
            z = dot_nt(jnp.where(masks[h], q, 0), k) * b.size ** (-0.5) + same
            e = jnp.exp(z - jnp.max(z, axis=-1, keepdims=True))
            s = e * (1.0 / jnp.sum(e, axis=-1, keepdims=True))
            p[i * b.per + h] = s
            total = total + dot(s.astype(jnp.bfloat16), jnp.where(masks[h], v, 0))
        att[:, lanes(i)] = total.astype(jnp.bfloat16)
        return 0

    lax.fori_loop(0, 2 * np_, heads, 0)
    keep(1)
    need(1)
    for t in range(2):
        for g in range(b.width // 128):
            ow[t, :, g * 128:(g + 1) * 128] = panel(w, t, b.o, g)
    x1 = x[...] + dot(att[:, :b.part], ow[0]) + dot(att[:, b.part:], ow[1])
    xo[...] = x1
    m, inv = ln_parts(x1)
    m2[...] = m
    i2[...] = inv
    n2[...] = (m * gains[1:2, cols] + biases[1:2, cols]).astype(jnp.bfloat16)
    keep(2)
    need(2)
    ga = b.a[1]

    def up(g):
        h = dot(n2[...], pair(w, b.a, g))
        big = 0.5 * (1.0 + lax.erf(h * 0.7071067811865476))
        act_v = (h * big).astype(jnp.bfloat16)
        dens = big + h * (0.3989422804014327 * jnp.exp(-0.5 * h * h))
        act[:, lanes(g)] = act_v[:, :128]
        act[:, lanes(ga + g)] = act_v[:, 128:]
        slope[:, lanes(g)] = dens[:, :128]
        slope[:, lanes(ga + g)] = dens[:, 128:]

    repeat(ga, 12, up)
    keep(3)
    need(3)
    half = b.hidden // 2

    def down(g):
        w0 = jnp.concatenate([panel(w, 0, b.b, 2 * g), panel(w, 0, b.b, 2 * g + 1)], axis=1)
        w1 = jnp.concatenate([panel(w, 1, b.b, 2 * g), panel(w, 1, b.b, 2 * g + 1)], axis=1)
        xo[:, lanes(g, 256)] += dot(act[:, :half], w0) + dot(act[:, half:], w1)

    repeat(b.width // 256, 1, down)


def block_bwd(b, dr, w, gains, same, n1, proj, p, att, ow, m1, i1, n2, m2, i2, act, slope,
              r, dh, r1, dp_out, acc, da, norm_out, keep):
    cols = slice(b.col, b.col + b.width)
    r[...] = dr[...].astype(jnp.bfloat16)
    keep(3)
    half = b.hidden // 2
    rb = b.b[0]
    gb = b.width // 128
    num = 16

    def hidden(i, _):
        t, lo = i // (16 // num), (i % (16 // num)) * num
        wc = jnp.concatenate([panel(w, t, b.b, g, lo, num) for g in range(gb)], axis=1)
        at = lanes(i, num * rb)
        dh[:, at] = (dot_nt(r[...], wc) * slope[:, at]).astype(jnp.bfloat16)
        return 0

    lax.fori_loop(0, 2 * (16 // num), hidden, 0)
    keep(2)
    ga = b.a[1]
    pull(acc, dh, w, b.a, 12)
    dx, dg, db = ln_back(acc[...], m2[...], i2[...], gains[1:2, cols])
    norm_out[1:2, cols] = dg
    norm_out[3:4, cols] = db
    dx1 = dr[...] + dx
    dr[...] = dx1
    r1[...] = dx1.astype(jnp.bfloat16)
    keep(1)
    for t in range(2):
        da[:, t * b.part:(t + 1) * b.part] = dot_nt(r1[...], ow[t]).astype(jnp.bfloat16)
    gq = b.q[1]
    np_ = b.part // 128
    lane = lax.broadcasted_iota(jnp.int32, (256, 128), 1)
    masks = [lane // b.size == i for i in range(b.per)]
    scale = b.size ** (-0.5)

    def heads(i, _):
        t, j = i // np_, i % np_
        q = proj[:, lanes(t * gq + j)]
        k = proj[:, lanes(t * gq + np_ + j)]
        v = proj[:, lanes(t * gq + 2 * np_ + j)]
        up_ = da[:, lanes(i)]
        dq = jnp.zeros((256, 128), jnp.float32)
        dk = jnp.zeros((256, 128), jnp.float32)
        dv = jnp.zeros((256, 128), jnp.float32)
        for h in range(b.per):
            s = p[i * b.per + h]
            u = jnp.where(masks[h], up_, 0)
            dp = dot_nt(u, v)
            dv = dv + dot_tn(s.astype(jnp.bfloat16), u)
            t1 = s * dp
            dz = (t1 - s * jnp.sum(t1, axis=-1, keepdims=True)).astype(jnp.bfloat16)
            dq = dq + dot(dz, jnp.where(masks[h], k, 0))
            dk = dk + dot_tn(dz, jnp.where(masks[h], q, 0))
        dp_out[:, lanes(t * gq + j)] = (dq * scale).astype(jnp.bfloat16)
        dp_out[:, lanes(t * gq + np_ + j)] = (dk * scale).astype(jnp.bfloat16)
        dp_out[:, lanes(t * gq + 2 * np_ + j)] = dv.astype(jnp.bfloat16)
        return 0

    lax.fori_loop(0, 2 * np_, heads, 0)
    keep(0)
    pull(acc, dp_out, w, b.q, 9)
    dx, dg, db = ln_back(acc[...], m1[...], i1[...], gains[0:1, cols])
    norm_out[0:1, cols] = dg
    norm_out[2:3, cols] = db
    dr[...] = dr[...] + dx


ACTS = (DE, DE, DE, FFE, DE, DD, DD, DD, FFD)
GRADS = (3 * DE, DE, FFE, DE, DD, 3 * DD, DD, FFD, DD)


def chain_kernel(table, tok, pos, tile, gains, biases, cot, tab, w_hbm, *refs):
    dec, dx0, norm_out = refs[:3]
    kept_out = refs[3:21]
    kept = refs[21:39]
    acts, grads = kept[:9], kept[9:]
    (w, pe, pd, se, sd, proj_e, proj_d, da_e, da_d, ow_e, ow_d, m1e, m2e, m1d, m2d, i1e, i2e, i1d, i2d,
     x, y, acc_e, acc_d, w_sem, out_sem) = refs[39:]
    enc_b = Block(DE, HE, HDE, FFE, 0, table, 0)
    dec_b = Block(DD, HD, HDD, FFD, 5, table, DE)
    em = table[4]

    def load(m):
        rows = pl.ds(table[m][4], table[m][1] * table[m][5])
        return pltpu.make_async_copy(w_hbm.at[:, :, rows], w.at[:, :, rows], w_sem.at[m])

    def store(i):
        return pltpu.make_async_copy(kept[i], kept_out[i], out_sem.at[i])

    for m in range(9):
        load(m).start()
    row = lax.broadcasted_iota(jnp.int32, (48, 256), 0)
    spots = [jnp.concatenate([pos[0, i:i + 1, :], pos[1, i:i + 1, :]], axis=1) for i in range(3)]
    hot = jnp.logical_or(jnp.logical_or(row == spots[0], row == spots[1] + 16), row == spots[2] + 32)
    hot = jnp.where(hot, 1.0, 0.0).astype(jnp.bfloat16)
    ids = tile[lax.axis_index("tensor")]
    tiles = jnp.where(lax.broadcasted_iota(jnp.int32, (16, 256), 0) == ids, 1.0, 0.0).astype(jnp.bfloat16)
    same = (1.0 - dot_tn(tiles, tiles)) * MASK_FILL
    x[...] = tok[...].astype(jnp.float32) + sum(dot_tn(hot, tab[i, :, :DE]) for i in range(3))
    n1e, ae, n2e, ue, low, n1d, ad, n2d, ud = acts
    dpe, r1e, dhe, re, dlow, dpd, r1d, dhd, rd = grads
    block_fwd(enc_b, x, dx0, w, gains, biases, same, n1e, proj_e, pe, ae, ow_e, m1e, i1e, n2e, m2e, i2e, ue, se,
              lambda k: load(k).wait(), lambda k: store(k).start())
    low[...] = dx0[...].astype(jnp.bfloat16)
    store(4).start()
    load(4).wait()
    for g in range(2):
        v = dot(low[...], pair(w, em, g)).astype(jnp.bfloat16).astype(jnp.float32)
        y[:, g * 128:(g + 1) * 128] = v[:, :128]
        y[:, 256 + g * 128:256 + (g + 1) * 128] = v[:, 128:]
    y[...] += sum(dot_tn(hot, tab[i, :, DE:]) for i in range(3))
    block_fwd(dec_b, y, dec, w, gains, biases, same, n1d, proj_d, pd, ad, ow_d, m1d, i1d, n2d, m2d, i2d, ud, sd,
              lambda k: load(5 + k).wait(), lambda k: store(5 + k).start())
    y[...] = cot[...]
    block_bwd(dec_b, y, w, gains, same, n1d, proj_d, pd, ad, ow_d, m1d, i1d, n2d, m2d, i2d, ud, sd,
              rd, dhd, r1d, dpd, acc_d, da_d, norm_out, lambda k: store(14 + k).start())
    dlow[...] = y[...].astype(jnp.bfloat16)
    store(13).start()
    for g in range(2):
        d = jnp.concatenate([dlow[:, g * 128:(g + 1) * 128], dlow[:, 256 + g * 128:256 + (g + 1) * 128]], axis=1)
        v = dot_nt(d, pair(w, em, g))
        if g == 0:
            dx0[...] = v
        else:
            dx0[...] += v
    block_bwd(enc_b, dx0, w, gains, same, n1e, proj_e, pe, ae, ow_e, m1e, i1e, n2e, m2e, i2e, ue, se,
              re, dhe, r1e, dpe, acc_e, da_e, norm_out, lambda k: store(9 + k).start())
    for i in range(18):
        store(i).wait()


def chain(tokens, pos, tile, gains, biases, cot, full, table):
    f32, bf16 = jnp.float32, jnp.bfloat16
    S = jax.ShapeDtypeStruct
    outs = [S((256, DD), f32), S((256, DE), f32), S((4, DE + DD), f32)]
    kept = [(256, n) for n in ACTS + GRADS]
    outs += [S(k, bf16) for k in kept]
    V = pltpu.VMEM
    scratch = [V(k, bf16) for k in kept] + [
        V((2, 16) + full.shape[-2:], bf16),
        V((HE, 256, 256), f32), V((HD, 256, 256), f32), V((256, FFE), f32), V((256, FFD), f32),
        V((256, 3 * DE), bf16), V((256, 3 * DD), bf16), V((256, DE), bf16), V((256, DD), bf16),
        V((2, DE // 2, DE), bf16), V((2, DD // 2, DD), bf16),
        V((256, DE), f32), V((256, DE), f32), V((256, DD), f32), V((256, DD), f32)] + [V((256, 1), f32)] * 4 + [
        V((256, DE), f32), V((256, DD), f32), V((256, DE), f32), V((256, DD), f32),
        pltpu.SemaphoreType.DMA((9,)), pltpu.SemaphoreType.DMA((18,))]
    vmem = pl.BlockSpec(memory_space=pltpu.VMEM)
    hbm = pl.BlockSpec(memory_space=pl.ANY)
    args = (tokens, pos, tile, gains, biases, cot, jnp.asarray(position_table()),
            full.reshape(2, 16, full.shape[-2], 128))
    return pl.pallas_call(
        partial(chain_kernel, table), out_shape=outs, in_specs=[vmem] * 7 + [hbm], out_specs=[vmem] * 3 + [hbm] * 18,
        scratch_shapes=scratch, compiler_params=pltpu.CompilerParams(vmem_limit_bytes=63 << 20), name="chain",
        cost_estimate=pl.CostEstimate(flops=11_000_000_000, bytes_accessed=40_000_000, transcendentals=5_000_000),
    )(*args)


def grad_panels(table, m, act, grad, turned, put):
    mat = table[m]
    rb, panels, padded = mat[0], mat[1], mat[5]
    count = act.shape[1]

    def turn(i):
        turned[pl.ds(pl.multiple_of(i * 128, 128), 128), :] = act[:, lanes(i)].T

    repeat(count // 128, 6, turn)

    def place(t, g, v):
        if padded > rb:
            v = v.reshape(16, rb, 128)
            v = jnp.concatenate([v, jnp.zeros((16, padded - rb, 128), jnp.float32)], axis=1).astype(jnp.bfloat16)
        else:
            v = v.astype(jnp.bfloat16).reshape(16, rb, 128)
        put(t, g, v)

    if m in BY_ROWS:
        half = count // 2

        def body(i):
            t, g = i // (panels // 2), i % (panels // 2)
            v = dot(turned[pl.ds(pl.multiple_of(t * half, 128), half), :], grad[:, lanes(g, 256)])
            place(t, 2 * g, v[:, :128])
            place(t, 2 * g + 1, v[:, 128:])

        repeat(panels, 6, body)
    else:
        def body(g):
            d = jnp.concatenate([grad[:, lanes(g)], grad[:, lanes(panels + g)]], axis=1)
            v = dot(turned[:count, :], d)
            place(0, g, v[:, :128])
            place(1, g, v[:, 128:])

        repeat(panels, 6, body)


class Wires:
    def __init__(self, place, sem):
        self.place, self.sem, self.used, self.waits = place, sem, 0, []

    def new(self, n=1):
        self.used += n
        assert self.used <= self.sem.shape[0], self.used
        return self.used - n

    def copy(self, k, src, dst, way):
        return pltpu.make_async_remote_copy(src_ref=src, dst_ref=dst, send_sem=self.sem.at[k], recv_sem=self.sem.at[k + 1],
                                            device_id=self.place.ids[way], device_id_type=MESH)

    def send(self, k, src, dst, way, cond=None):
        cp = self.copy(k, src, dst, way)
        when(cond, cp.start)
        self.waits.append((cond, cp))

    def land(self, k, dst, cond=None):
        when(cond, self.copy(k, dst, dst, "c").wait_recv)

    def drain(self):
        for cond, cp in self.waits:
            when(cond, cp.wait_send)


def edge_slots(order):
    slots, used, shared = {}, 0, {}
    for d, kids in sorted(spread(order).items()):
        for _, way in kids:
            if way in "xy" and order.index("z") < order.index(way):
                key = (way, d[1], d[2])
                if key not in shared:
                    shared[key] = used
                    used += 4
                slots[d, way] = (shared[key], 4)
            else:
                slots[d, way] = (used, 1)
                used += 1
    return slots, used


def beyond(p, way):
    return p.z < 3 if way == "z+" else p.z > 0 if way == "z-" else None


def reduce_events(p, w, order, own, half, bufs, ready, done):
    tree = spread(order)
    pair = {d: w.new(2) for d in tree}
    wire = {d: w.new(2) for d in tree}
    parent = {nd: (d, way) for d, t in tree.items() for nd, way in t}
    slots, _ = edge_slots(order)

    def buffer(up, way):
        first, n = slots[up, way]
        return bufs.at[first + p.z + up[0] if n > 1 else first]

    events = []
    far = sorted(tree, key=lambda d: (-hops(d), d))
    for d in far:
        def act(d=d):
            cond = p.there(d)

            def step():
                acc = own(d)
                ready(d)
                w.land(pair[d], half(d))
                add_rows(acc, half(d))
                for nd, way in tree[d]:
                    buf = buffer(d, way)

                    def take(buf=buf, nd=nd):
                        w.land(wire[nd], buf)
                        add_rows(acc, buf)
                    when(beyond(p, way), take)
            when(cond, step)
            if hops(d) == 0:
                done()
            else:
                up, way = parent[d]
                w.send(wire[d], own(d), buffer(up, way), BACK[way], cond)
        events.append(act)

    def share(give):
        for d in far:
            w.send(pair[d], give(d), half(d), "c", p.there(d))

    return events, share, far


def gather_events(p, w, order, first, at):
    tree = spread(order)
    pair = {d: w.new(2) for d in tree}
    wire = {d: w.new(2) for d in tree}
    events = []
    for d in sorted(tree, key=lambda d: (hops(d), d)):
        def act(d=d):
            cond = p.there(d)
            blk = at(d, p.c)
            if hops(d):
                w.land(wire[d], blk, cond)
                src = blk
            else:
                src = first
            for nd, way in tree[d]:
                w.send(wire[nd], src, blk, way, both(cond, beyond(p, way)))
            w.send(pair[d], src, blk, "c", cond)
        events.append(act)

    def finish():
        for d in tree:
            w.land(pair[d], at(d, 1 - p.c), p.there(d))

    return events, finish


def run_events(lists, order, extra=iter(()), every=8):
    assert sorted(order) == sorted(64 * g + i for g, acts in enumerate(lists) for i in range(len(acts)))
    for n, k in enumerate(order):
        if n % every == 0:
            next(extra, None)
        lists[k // 64][k % 64]()
    for _ in extra:
        pass


def group_span(table, mats):
    first, last = table[mats[0]], table[mats[-1]]
    units = last[3] + last[2] - first[3]
    return first[3], -(-units // 16) * 16, first[4], last[4] + last[1] * last[5] - first[4]


def units_to_panels(table, mats, units, flat, put):
    base, count = table[mats[0]][3], units.shape[0]
    for k in range(4):
        flat[pl.ds(k, count, stride=4), :] = units[:, 128 * k:128 * (k + 1)].astype(jnp.float32)
    for m in mats:
        rb, panels, n, first, _, padded, _ = table[m]
        for g in range(panels):
            v = flat[pl.ds(4 * (first - base) + g, rb, stride=panels), :]
            if padded > rb:
                v = jnp.concatenate([v, jnp.zeros((padded - rb, 128), jnp.float32)], axis=0)
            put(m, g, v.astype(jnp.bfloat16))


def panels_to_units(table, mats, take, flat, units):
    base, count = table[mats[0]][3], units.shape[0]
    used = 0
    for m in mats:
        rb, panels, n, first, _, padded, _ = table[m]
        for g in range(panels):
            flat[pl.ds(4 * (first - base) + g, rb, stride=panels), :] = take(m, g)[:rb]
        used = 4 * (first - base + n)
    if used < 4 * count:
        flat[used:4 * count, :] = jnp.zeros((4 * count - used, 128), jnp.float32)
    for k in range(4):
        units[:, 128 * k:128 * (k + 1)] = flat[pl.ds(k, count, stride=4), :].astype(jnp.bfloat16)


class Swap:
    def __init__(self, p, w, src, out, give, keep):
        self.p, self.w, self.src, self.out, self.give, self.keep = p, w, src, out, give, keep
        self.k, self.own = w.new(2), w.new()

    def local(self):
        return pltpu.make_async_copy(self.src.at[self.keep], self.out.at[self.p.x], self.w.sem.at[self.own])

    def start(self):
        self.w.send(self.k, self.src.at[self.give], self.out.at[self.p.x], "x")
        self.local().start()

    def finish(self):
        self.w.land(self.k, self.out.at[1 - self.p.x])
        self.local().wait()


def weights_kernel(table, groups, plan, parts, tok_in, pos_in, cot_in, out, tok, pos, cot, *rest):
    n = len(groups)
    accs, halves, bufs, shards = (rest[i * n:(i + 1) * n] for i in range(4))
    flat, sem = rest[4 * n:]
    p = Place()
    p.greet(["c", "y", "x"])
    w = Wires(p, sem)
    swaps = [Swap(p, w, a, b, 1 - p.x, p.x) for a, b in ((tok_in, tok), (pos_in, pos), (cot_in, cot))]
    for s in swaps:
        s.start()
    lists, finishes = [], []
    for g, mats in enumerate(groups):
        u0, un, r0, rn = group_span(table, mats)
        acc, half, buf, shard = accs[g], halves[g], bufs[g], shards[g]
        own_sem = w.new()
        loads = {d: w.new() for d in spread(plan[0][g])}

        def own(d, acc=acc):
            return acc.at[p.at(d)[1:]]

        def other(d, half=half):
            return half.at[p.at(d)[1:]]

        def load(d, u0=u0, un=un, own=own, loads=loads):
            return pltpu.make_async_copy(parts.at[p.at(d)[1:] + (p.c, pl.ds(u0, un))], own(d), sem.at[loads[d]])

        def ready(d, load=load):
            load(d).wait()

        def done(mats=mats, acc=acc, shard=shard, r0=r0):
            def put(m, i, v):
                lo = table[m][4] - r0 + i * table[m][5]
                shard[lo:lo + table[m][5], :] = v
            units_to_panels(table, mats, acc.at[p.z, p.y], flat, put)

        ev, share, far = reduce_events(p, w, plan[0][g], own, other, buf, ready, done)

        def begin(load=load, share=share, far=far, u0=u0, un=un):
            share(lambda d: parts.at[p.at(d)[1:] + (1 - p.c, pl.ds(u0, un))])
            for d in far:
                when(p.there(d), load(d).start)

        def at(d, core, r0=r0, rn=rn):
            t, z, y = p.at(d)
            return out.at[t, z, y, core, pl.ds(r0, rn)]

        def local(shard=shard, r0=r0, rn=rn, own_sem=own_sem):
            return pltpu.make_async_copy(shard, out.at[p.x, p.z, p.y, p.c, pl.ds(r0, rn)], sem.at[own_sem])

        ag, finish = gather_events(p, w, plan[1][g], shard, at)

        def send_first(act=ag[0], local=local):
            act()
            local().start()

        lists.append([begin] + ev + [send_first] + ag[1:])
        finishes += [finish, lambda local=local: local().wait()]
    run_events(lists, plan[2])
    for f in finishes + [s.finish for s in swaps]:
        f()
    w.drain()


def spread_weights(parts, tokens, pos, cot, table, rows, groups, plan, ident):
    spans = [group_span(table, m) for m in groups]
    bf16 = jnp.bfloat16
    S = jax.ShapeDtypeStruct
    scratch = [pltpu.VMEM((4, 2, s[1], 512), bf16) for s in spans] * 2
    scratch += [pltpu.VMEM((edge_slots(o)[1], s[1], 512), bf16) for s, o in zip(spans, plan[0])]
    scratch += [pltpu.VMEM((s[3], 128), bf16) for s in spans]
    scratch += [pltpu.VMEM((4 * max(s[1] for s in spans), 128), jnp.float32),
                pltpu.SemaphoreType.DMA((len(groups) * (1 + 5 * 14 + 4 * 28) + 9,))]
    hbm = pl.BlockSpec(memory_space=pl.ANY)
    return pl.pallas_call(
        partial(weights_kernel, table, groups, plan),
        out_shape=[S((2, 4, 2, 2, rows, 128), bf16)] + [S(v.shape, v.dtype) for v in (tokens, pos, cot)],
        in_specs=[hbm] * 4, out_specs=[hbm] * 4,
        scratch_shapes=scratch,
        compiler_params=pltpu.CompilerParams(collective_id=ident, has_side_effects=True, vmem_limit_bytes=62 << 20),
        name="spread_weights",
    )(parts, tokens, pos, cot)


def return_kernel(table, groups, plan, *refs):
    n = len(groups)
    kept_in, small_src, dec_in, dx_in, out, small_out, dec, dx = refs[:18], *refs[18:25]
    rest = refs[25:]
    kept, rest = rest[:18], rest[18:]
    acts, grads = kept[:9], kept[9:]
    sides, halves, bufs, units = (rest[i * n:(i + 1) * n] for i in range(4))
    flat, turned, mid, line, load_sem, sem = rest[4 * n:]

    def load(i):
        return pltpu.make_async_copy(kept_in[i], kept[i], load_sem.at[i])

    first = sorted(range(n), key=lambda g: plan[2].index(64 * g))
    for g in first:
        for m in groups[g]:
            load(m).start()
            load(9 + m).start()
    p = Place()
    p.greet(["c", "y", "x"])
    w = Wires(p, sem)
    swaps = [Swap(p, w, a, b, 1 - p.x, p.x) for a, b in ((dec_in, dec), (dx_in, dx))]
    swaps[0].start()
    lists, finishes = [], []
    for g, mats in enumerate(groups):
        u0, un, r0, rn = group_span(table, mats)
        side, half, buf, unit = sides[g], halves[g], bufs[g], units[g]
        own_sem = w.new()

        def own(d, side=side):
            return side.at[(p.c,) + p.at(d)]

        def other(d, half=half):
            return half.at[p.at(d)]

        def done(mats=mats, side=side, unit=unit, r0=r0):
            mine = side.at[p.c, p.x, p.z, p.y]

            def take(m, i):
                lo = table[m][4] - r0 + i * table[m][5]
                return mine[lo:lo + table[m][5], :].astype(jnp.float32)
            panels_to_units(table, mats, take, flat, unit)

        ev, share, far = reduce_events(p, w, plan[0][g], own, other, buf, lambda d: None, done)

        def begin(mats=mats, side=side, share=share, r0=r0):
            for m in mats:
                lo, padded = table[m][4] - r0, table[m][5]

                def put(t, i, v, lo=lo, padded=padded):
                    v = v.reshape(4, 2, 2, padded, 128)
                    rows = pl.ds(pl.multiple_of(lo + i * padded, 16), padded)
                    side[0, t, :, :, rows, :] = v[:, :, 0]
                    side[1, t, :, :, rows, :] = v[:, :, 1]
                load(m).wait()
                load(9 + m).wait()
                grad_panels(table, m, acts[m], grads[m], turned, put)
            share(lambda d: side.at[(1 - p.c,) + p.at(d)])

        def at(d, core, u0=u0, un=un):
            _, z, y = p.at(d)
            return out.at[z, y, core, pl.ds(u0, un)]

        def local(unit=unit, u0=u0, un=un, own_sem=own_sem):
            return pltpu.make_async_copy(unit, out.at[p.z, p.y, p.c, pl.ds(u0, un)], sem.at[own_sem])

        ag, finish = gather_events(p, w, plan[1][g], unit, at)

        def send_first(act=ag[0], local=local):
            act()
            local().start()

        lists.append([begin] + ev + [send_first] + ag[1:])
        finishes += [finish, lambda local=local: local().wait()]
    last = max(plan[2].index(64 * g + len(spread(plan[0][g]))) for g in range(n))
    g, i = plan[2][last] // 64, plan[2][last] % 64
    act = lists[g][i]

    def with_swaps():
        act()
        swaps[1].start()

    lists[g][i] = with_swaps
    run_events(lists, plan[2], total_steps(p, w, small_src, small_out, mid, line))
    for f in finishes + [s.finish for s in swaps]:
        f()
    w.drain()


def total_steps(p, w, src, out, mid, line):
    k = [w.new(2) for _ in range(9)]
    now = src
    for i, way in enumerate(("c", "x", "y")):
        w.send(k[i], now, mid.at[i], way)
        yield
        w.land(k[i], mid.at[i])
        nxt = mid.at[3 + i] if i < 2 else line.at[p.z]
        nxt[...] = now[...] + mid[i]
        now = nxt
    for i in range(4):
        lo, hi = jnp.maximum(p.z - i, 0), jnp.minimum(p.z + i, 3)
        if i > 0:
            w.land(k[2 + i], line.at[lo], p.z >= i)
            w.land(k[5 + i], line.at[hi], p.z + i <= 3)
        if i < 3:
            w.send(k[3 + i], line.at[lo], line.at[lo], "z+", jnp.logical_and(p.z >= i, p.z < 3))
            w.send(k[6 + i], line.at[hi], line.at[hi], "z-", jnp.logical_and(p.z + i <= 3, p.z > 0))
            yield
    out[...] = (line[0] + line[1]) + (line[2] + line[3])


def return_grads(kept, small, dec, dx, table, total_units, groups, plan, ident):
    spans = [group_span(table, m) for m in groups]
    bf16 = jnp.bfloat16
    S = jax.ShapeDtypeStruct
    V = pltpu.VMEM
    scratch = [V(v.shape, v.dtype) for v in kept]
    scratch += [V((2, 2, 4, 2, s[3], 128), bf16) for s in spans]
    scratch += [V((2, 4, 2, s[3], 128), bf16) for s in spans]
    scratch += [V((edge_slots(o)[1], s[3], 128), bf16) for s, o in zip(spans, plan[0])]
    scratch += [V((s[1], 512), bf16) for s in spans]
    scratch += [V((4 * max(s[1] for s in spans), 128), jnp.float32), V((FFE, 256), bf16),
                V((5,) + small.shape, small.dtype), V((4,) + small.shape, small.dtype), pltpu.SemaphoreType.DMA((18,)),
                pltpu.SemaphoreType.DMA((len(groups) * (1 + 4 * 14 + 4 * 28) + 24,))]
    vmem = pl.BlockSpec(memory_space=pltpu.VMEM)
    hbm = pl.BlockSpec(memory_space=pl.ANY)
    return pl.pallas_call(
        partial(return_kernel, table, groups, plan),
        out_shape=(S((4, 2, 2, total_units, 512), bf16), S(small.shape, small.dtype), S(dec.shape, dec.dtype), S(dx.shape, dx.dtype)),
        in_specs=[hbm] * 18 + [vmem, hbm, hbm], out_specs=(hbm, vmem, hbm, hbm),
        scratch_shapes=scratch,
        compiler_params=pltpu.CompilerParams(collective_id=ident, has_side_effects=True, vmem_limit_bytes=63 << 20),
        name="return_grads",
    )(*kept, small, dec, dx)


STEP_ROWS = 48


def update_kernel(place_s, place, spread, master, first, second, total, params, norm_first, norm_second,
                  new_master, new_first, new_second, new_norms, new_nf, new_ns):
    i = pl.program_id(0)

    @pl.when(i == 0)
    def _():
        new_norms[...], new_nf[...], new_ns[...] = adamw(params[...], total[...], norm_first[...], norm_second[...], 0.0, NORM_RATE)

    lane = lax.broadcasted_iota(jnp.int32, (16, 256), 1)
    row = lax.broadcasted_iota(jnp.int32, (16, 256), 0)
    for k in range(STEP_ROWS // 16):
        tiles = []
        for j in range(16):
            at = jnp.minimum(place_s[i * STEP_ROWS + 16 * k + j] >> 4, spread.shape[0] // 16 - 1)
            tiles.append(spread[pl.ds(pl.multiple_of(at * 16, 16), 16), :])
        here = slice(16 * k, 16 * k + 16)
        spot = place[here, :]
        used = jnp.logical_and(lane == row * 16 + (spot & 15), spot < spread.shape[0])
        grad = dot(jnp.where(used, 1.0, 0.0).astype(jnp.bfloat16), jnp.concatenate(tiles, axis=0))
        new_master[here, :], new_first[here, :], new_second[here, :] = adamw(
            master[here, :], grad, first[here, :], second[here, :], WEIGHT_DECAY, LEARN_RATE)


def update(place, spread, master, first, second, total, params, norm_first, norm_second):
    slots = master.shape[0]
    S = jax.ShapeDtypeStruct
    rows = pl.BlockSpec((STEP_ROWS, 512), lambda i, s: (i, 0))
    whole = lambda v: pl.BlockSpec(v.shape, lambda i, s: (0, 0), pipeline_mode=pl.Buffered(1))
    small = pl.BlockSpec(params.shape, lambda i, s: (0, 0))
    out = [S(master.shape, jnp.float32)] * 3 + [S(params.shape, jnp.float32)] * 3
    return pl.pallas_call(
        update_kernel, out_shape=out,
        grid_spec=pltpu.PrefetchScalarGridSpec(
            num_scalar_prefetch=1, grid=(slots // STEP_ROWS,),
            in_specs=[pl.BlockSpec((STEP_ROWS, 1), lambda i, s: (i, 0)), whole(spread), rows, rows, rows, small, small, small, small],
            out_specs=[rows] * 3 + [small] * 3),
        compiler_params=pltpu.CompilerParams(vmem_limit_bytes=40 << 20), name="update",
    )(place, place[:, None], spread, master, first, second, total, params, norm_first, norm_second)


def sequence_device(tokens_in, positions, segment_ids, owners, master, first_moment, second_moment, norm_gains,
                    norm_biases, norm_first, norm_second, cotangent):
    shapes = weight_shapes(2)
    table, _, rows = layout(shapes, 16)
    unit, used = own_units(owners, lax.axis_index("dp"), master.shape[0])
    place = jnp.where(used, unit_places(unit, table, 16), 16 * SHARD_UNITS)
    parts = jnp.zeros((16 * SHARD_UNITS, 512), jnp.bfloat16)
    parts = parts.at[place].set(master.astype(jnp.bfloat16), mode="drop", unique_indices=True)
    full, tok, pos, cot = spread_weights(parts.reshape(4, 2, 2, SHARD_UNITS, 512), tokens_in, positions.transpose(1, 0, 2),
                                         cotangent, table, rows, GROUPS, PLAN_OUT, 1)
    kept = chain(tok.reshape(256, DE), pos, segment_ids, norm_gains, norm_biases, cot.reshape(256, DD), full, table)
    decoded, dx0, norms = kept[:3]
    spread_out, norm_total, decoded, dx0 = return_grads(kept[3:], norms, decoded.reshape(2, 128, DD), dx0.reshape(2, 128, DE), table,
                                                        SHARD_UNITS, GROUPS, PLAN_BACK, 2)
    norm_params = jnp.concatenate([norm_gains, norm_biases], axis=0)
    new_master, new_first, new_second, new_norms, norm_one_new, norm_two_new = update(
        place, spread_out.reshape(16 * SHARD_UNITS, 512), master, first_moment, second_moment, norm_total, norm_params, norm_first, norm_second)
    return (decoded, dx0, new_master, new_first, new_second, new_norms, norm_one_new, norm_two_new)


def solution(mesh):
    step = sequence_device if (mesh.shape["dp"], mesh.shape["tensor"]) == (16, 2) else per_device
    return jax.shard_map(
        step,
        mesh=mesh,
        in_specs=(
            P(None, ("dp", "tensor"), None),
            P(None, None, ("dp", "tensor")),
            P(None, "dp", None),
            P(),
            P("dp", "tensor"),
            P("dp", "tensor"),
            P("dp", "tensor"),
            P(),
            P(),
            P(),
            P(),
            P(None, ("dp", "tensor"), None),
        ),
        out_specs=(
            P(None, ("dp", "tensor"), None),
            P(None, ("dp", "tensor"), None),
            P("dp", "tensor"),
            P("dp", "tensor"),
            P("dp", "tensor"),
            P(),
            P(),
            P(),
        ),
        check_vma=False,
    )
```

```python
from functools import partial

import jax
import jax.numpy as jnp
import ml_dtypes
import numpy as np
from jax import lax
from jax.experimental import pallas as pl
from jax.experimental.pallas import tpu as pltpu
from jax.sharding import PartitionSpec as P

DE = 768
HE = 12
HDE = 64
FFE = 3072
DD = 512
HD = 16
HDD = 32
FFD = 2048
STEP = 10


NORM_EPS = 1e-06
BETA_ONE = 0.5
BETA_TWO = 0.5
LEARN_RATE = 0.03
NORM_RATE = 0.3
WEIGHT_DECAY = 0.05
ADAM_EPS = 1e-08
MASK_FILL = -1000000000.0


def sincos_part(coordinate, part_width):
    halfway = part_width // 2
    frequency = 1.0 / 10000.0 ** (jnp.arange(halfway, dtype=jnp.float32) / halfway)
    angles = coordinate.astype(jnp.float32)[:, None] * frequency[None, :]
    return jnp.concatenate([jnp.sin(angles), jnp.cos(angles)], axis=1)


def sincos_embed(positions, model_width):
    side_width = model_width // 16 * 6
    first_width = model_width - 2 * side_width
    return jnp.concatenate(
        [
            sincos_part(positions[0], first_width),
            sincos_part(positions[1], side_width),
            sincos_part(positions[2], side_width),
        ],
        axis=1,
    )


def slot_table(owners, devices, capacity):
    owner_ids = owners[:, 0]
    onehot = (owner_ids[:, None] == jnp.arange(devices, dtype=jnp.int32)[None, :]).astype(jnp.int32)
    before = jnp.cumsum(onehot, axis=0) - onehot
    owner_rank = jnp.sum(before * onehot, axis=1)
    return owner_ids * capacity + owner_rank


def weight_shapes(tensor_count):
    enc_heads = HE // tensor_count
    dec_heads = HD // tensor_count
    return [
        (DE, 3 * enc_heads * HDE),
        (enc_heads * HDE, DE),
        (DE, FFE // tensor_count),
        (FFE // tensor_count, DE),
        (DE, DD // tensor_count),
        (DD, 3 * dec_heads * HDD),
        (dec_heads * HDD, DD),
        (DD, FFD // tensor_count),
        (FFD // tensor_count, DD),
    ]


def split_flat(flat_vector, shapes):
    pieces = []
    offset = 0
    for matrix_shape in shapes:
        length = matrix_shape[0] * matrix_shape[1]
        pieces.append(flat_vector[offset : offset + length].reshape(matrix_shape))
        offset += length
    return pieces


def adamw(weights, gradient, moment_one, moment_two, decay_rate, step_rate):
    one_new = BETA_ONE * moment_one + (1.0 - BETA_ONE) * gradient
    two_new = BETA_TWO * moment_two + (1.0 - BETA_TWO) * gradient * gradient
    one_hat = one_new / (1.0 - BETA_ONE**STEP)
    two_hat = two_new / (1.0 - BETA_TWO**STEP)
    weights_new = weights - step_rate * (
        one_hat / (jnp.sqrt(two_hat) + ADAM_EPS) + decay_rate * weights
    )
    return (weights_new, one_new, two_new)


def norm_forward(values, gain_row, bias_row):
    center = values - jnp.mean(values, axis=-1, keepdims=True)
    spread = jnp.mean(center * center, axis=-1, keepdims=True)
    inverse = lax.rsqrt(spread + NORM_EPS)
    normed = center * inverse
    return (normed * gain_row + bias_row, (normed, inverse))


def norm_backward(upstream, stored, gain_row):
    normed, inverse = stored
    scaled = upstream * gain_row
    mean_one = jnp.mean(scaled, axis=-1, keepdims=True)
    mean_two = jnp.mean(scaled * normed, axis=-1, keepdims=True)
    return (
        inverse * (scaled - mean_one - normed * mean_two),
        jnp.sum(upstream * normed, axis=0),
        jnp.sum(upstream, axis=0),
    )


def inner_rows(left_side, right_side):
    return lax.dot_general(
        left_side, right_side, (((0,), (0,)), ((), ())), preferred_element_type=jnp.float32
    )


def times_transpose(left_side, right_side):
    return lax.dot_general(
        left_side, right_side, (((1,), (1,)), ((), ())), preferred_element_type=jnp.float32
    )


def gather_rows(values):
    return lax.all_gather(values, "tensor", axis=0, tiled=True)


def gather_grads(values):
    return lax.all_gather(values, "tensor", axis=0, tiled=True)


def branch_rows(values, weight):
    return lax.psum_scatter(
        jnp.dot(values, weight, preferred_element_type=jnp.float32).astype(jnp.bfloat16),
        "tensor",
        scatter_dimension=0,
        tiled=True,
    ).astype(jnp.float32)


def input_rows(values, weight):
    return lax.psum_scatter(
        times_transpose(values, weight).astype(jnp.bfloat16),
        "tensor",
        scatter_dimension=0,
        tiled=True,
    ).astype(jnp.float32)


def block_scores(queries, key_rows, mask_bias, block_start, block_rows, head_size):
    scores = jnp.einsum(
        "qhd,khd->hqk", queries, key_rows, preferred_element_type=jnp.float32
    ) * head_size ** (-0.5)
    return scores + mask_bias[None, block_start : block_start + block_rows]


def attention_forward(gathered, w_qkv, head_count, head_size, mask_bias):
    length = gathered.shape[0]
    projected = jnp.dot(gathered, w_qkv, preferred_element_type=jnp.float32).astype(jnp.bfloat16)
    projected = projected.reshape(length, 3, head_count, head_size)
    queries = projected[:, 0]
    key_rows = projected[:, 1]
    value_rows = projected[:, 2]
    block_rows = min(512, length)
    scores = block_scores(queries, key_rows, mask_bias, 0, block_rows, head_size)
    row_peak = jnp.max(scores, axis=-1, keepdims=True)
    row_total = row_peak + jnp.log(jnp.sum(jnp.exp(scores - row_peak), axis=-1, keepdims=True))
    weights = jnp.exp(scores - row_total).astype(jnp.bfloat16)
    outputs = jnp.einsum("hqk,khd->qhd", weights, value_rows, preferred_element_type=jnp.float32)
    totals = [row_total]
    attended = outputs.astype(jnp.bfloat16).reshape(length, head_count * head_size)
    return (attended, (queries, key_rows, value_rows, totals))


def attention_backward(upstream, w_out, attended, stored, head_count, head_size, mask_bias):
    queries, key_rows, value_rows, totals = stored
    length = upstream.shape[0]
    score_scale = head_size ** (-0.5)
    grad_out = inner_rows(attended, upstream)
    attended_grad = (
        times_transpose(upstream, w_out).astype(jnp.bfloat16).reshape(length, head_count, head_size)
    )
    block_rows = min(512, length)
    key_grads = jnp.zeros((length, head_count, head_size), jnp.float32)
    value_grads = jnp.zeros((length, head_count, head_size), jnp.float32)
    query_grads = []
    for number, block_start in enumerate(range(0, length, block_rows)):
        scores = block_scores(queries, key_rows, mask_bias, block_start, block_rows, head_size)
        weights = jnp.exp(scores - totals[number])
        value_grads = jnp.einsum(
            "hqk,qhd->khd",
            weights.astype(jnp.bfloat16),
            attended_grad,
            preferred_element_type=jnp.float32,
        )
        weight_grads = jnp.einsum(
            "qhd,khd->hqk", attended_grad, value_rows, preferred_element_type=jnp.float32
        )
        score_grads = (
            weights * (weight_grads - jnp.sum(weights * weight_grads, axis=-1, keepdims=True))
        ).astype(jnp.bfloat16)
        query_grads.append(
            jnp.einsum("hqk,khd->qhd", score_grads, key_rows, preferred_element_type=jnp.float32)
            * score_scale
        )
        key_grads = (
            jnp.einsum("hqk,qhd->khd", score_grads, queries, preferred_element_type=jnp.float32)
            * score_scale
        )
    projected_grad = jnp.stack([query_grads[0], key_grads, value_grads], axis=1)
    return (
        projected_grad.astype(jnp.bfloat16).reshape(length, 3 * head_count * head_size),
        grad_out,
    )


def block_forward(residual, matrices, gain_rows, bias_rows, head_count, head_size, mask_bias):
    w_qkv, w_out, w_in, w_down = matrices
    normed, norm_one = norm_forward(residual, gain_rows[0], bias_rows[0])
    gathered = gather_rows(normed.astype(jnp.bfloat16))
    attended, stored = attention_forward(gathered, w_qkv, head_count, head_size, mask_bias)
    middle = residual + branch_rows(attended, w_out)
    normed_two, norm_two = norm_forward(middle, gain_rows[1], bias_rows[1])
    gathered_two = gather_rows(normed_two.astype(jnp.bfloat16))
    hidden = jnp.dot(gathered_two, w_in, preferred_element_type=jnp.float32)
    active = jax.nn.gelu(hidden, approximate=False).astype(jnp.bfloat16)
    result = middle + branch_rows(active, w_down)
    return (result, (gathered, norm_one, attended, stored, gathered_two, norm_two, hidden, active))


def block_backward(upstream, matrices, gain_rows, saved_values, head_count, head_size, mask_bias):
    w_qkv, w_out, w_in, w_down = matrices
    gathered, norm_one, attended, stored, gathered_two, norm_two, hidden, active = saved_values
    down_full = gather_grads(upstream.astype(jnp.bfloat16))
    grad_down = inner_rows(active, down_full)
    active_grad = times_transpose(down_full, w_down)
    gelu_pull = jax.vjp(partial(jax.nn.gelu, approximate=False), hidden)[1]
    hidden_grad = gelu_pull(active_grad)[0].astype(jnp.bfloat16)
    grad_in = inner_rows(gathered_two, hidden_grad)
    normed_two_grad = input_rows(hidden_grad, w_in)
    middle_grad, gain_two, bias_two = norm_backward(normed_two_grad, norm_two, gain_rows[1])
    middle_grad = upstream + middle_grad
    middle_full = gather_grads(middle_grad.astype(jnp.bfloat16))
    projected_grad, grad_out = attention_backward(
        middle_full, w_out, attended, stored, head_count, head_size, mask_bias
    )
    grad_qkv = inner_rows(gathered, projected_grad)
    normed_grad = input_rows(projected_grad, w_qkv)
    input_grad, gain_one, bias_one = norm_backward(normed_grad, norm_one, gain_rows[0])
    return (
        middle_grad + input_grad,
        [grad_qkv, grad_out, grad_in, grad_down],
        (gain_one, gain_two, bias_one, bias_two),
    )


def embed_forward(residual, w_embed):
    residual_low = gather_rows(residual.astype(jnp.bfloat16))
    columns = jnp.dot(residual_low, w_embed, preferred_element_type=jnp.float32).astype(
        jnp.bfloat16
    )
    own_columns = lax.all_to_all(columns, "tensor", split_axis=0, concat_axis=1, tiled=True)
    return (own_columns.astype(jnp.float32), residual_low)


def embed_backward(upstream, residual_low, w_embed):
    columns = lax.all_to_all(
        upstream.astype(jnp.bfloat16), "tensor", split_axis=1, concat_axis=0, tiled=True
    )
    grad_embed = inner_rows(residual_low, columns)
    return (input_rows(columns, w_embed), grad_embed)


def slot_builder(gradients, unit_of_slot, unit_width):
    flat_units = jnp.concatenate([gradient.reshape(-1) for gradient in gradients]).reshape(
        -1, unit_width
    )
    unit_total = flat_units.shape[0]
    source = jnp.take(flat_units, jnp.clip(unit_of_slot, 0, unit_total - 1), axis=0)
    return jnp.where((unit_of_slot >= 0)[:, None], source, 0.0)


def per_device(
    tokens_in,
    positions,
    segment_ids,
    owners,
    master,
    first_moment,
    second_moment,
    norm_gains,
    norm_biases,
    norm_first,
    norm_second,
    cotangent,
):
    devices = lax.axis_size("dp")
    tensor_count = lax.axis_size("tensor")
    capacity = master.shape[0]
    unit_width = master.shape[1]
    unit_count = owners.shape[0]
    slot_index = slot_table(owners, devices, capacity)
    unit_of_slot = (
        jnp.full((devices * capacity,), -1, jnp.int32)
        .at[slot_index]
        .set(jnp.arange(unit_count, dtype=jnp.int32))
    )
    targets = unit_of_slot
    targets = jnp.where(targets < 0, unit_count, targets)
    placed = (
        jnp.zeros((unit_count, unit_width), jnp.bfloat16)
        .at[targets]
        .set(lax.all_gather(master.astype(jnp.bfloat16), "dp", axis=0, tiled=True), mode="drop")
    )
    shapes = weight_shapes(tensor_count)
    matrices = split_flat(placed.reshape(-1), shapes)
    encoder = matrices[0:4]
    w_embed = matrices[4]
    decoder = matrices[5:9]
    enc_heads = HE // tensor_count
    dec_heads = HD // tensor_count
    micro_count = tokens_in.shape[0]
    grad_sums = [jnp.zeros(matrix_shape, jnp.float32) for matrix_shape in shapes]
    norm_sums = jnp.zeros((4, DE + DD), jnp.float32)
    decoded_rows = []
    token_grads = []
    for micro_step in range(micro_count):
        tile_ids = segment_ids[micro_step, 0]
        mask_bias = jnp.where(tile_ids[:, None] == tile_ids[None, :], 0.0, MASK_FILL).astype(
            jnp.float32
        )
        position_now = positions[:, micro_step]
        residual = tokens_in[micro_step].astype(jnp.float32) + sincos_embed(position_now, DE)
        residual, enc_saved = block_forward(
            residual, encoder, norm_gains[:, :DE], norm_biases[:, :DE], enc_heads, HDE, mask_bias
        )
        residual, embed_low = embed_forward(residual, w_embed)
        residual = residual + sincos_embed(position_now, DD)
        residual, dec_saved = block_forward(
            residual, decoder, norm_gains[:, DE:], norm_biases[:, DE:], dec_heads, HDD, mask_bias
        )
        decoded_rows.append(residual)
        upstream, dec_grads, dec_norm = block_backward(
            cotangent[micro_step], decoder, norm_gains[:, DE:], dec_saved, dec_heads, HDD, mask_bias
        )
        upstream, grad_embed = embed_backward(upstream, embed_low, w_embed)
        upstream, enc_grads, enc_norm = block_backward(
            upstream, encoder, norm_gains[:, :DE], enc_saved, enc_heads, HDE, mask_bias
        )
        token_grads.append(upstream)
        step_grads = enc_grads + [grad_embed] + dec_grads
        step_norm = jnp.concatenate([jnp.stack(enc_norm), jnp.stack(dec_norm)], axis=1)
        grad_sums = [total_grad + new_grad for total_grad, new_grad in zip(grad_sums, step_grads)]
        norm_sums = norm_sums + step_norm
    reduced = lax.psum_scatter(
        slot_builder(grad_sums, unit_of_slot, unit_width), "dp", scatter_dimension=0, tiled=True
    )
    norm_total = lax.psum(norm_sums, ("dp", "tensor"))
    new_master, new_first, new_second = adamw(
        master, reduced, first_moment, second_moment, WEIGHT_DECAY, LEARN_RATE
    )
    norm_params = jnp.concatenate([norm_gains, norm_biases], axis=0)
    new_norms, norm_one_new, norm_two_new = adamw(
        norm_params, norm_total, norm_first, norm_second, 0.0, NORM_RATE
    )
    return (
        jnp.stack(decoded_rows),
        jnp.stack(token_grads),
        new_master,
        new_first,
        new_second,
        new_norms,
        norm_one_new,
        norm_two_new,
    )


MESH = pl.DeviceIdType.MESH
ALL = slice(None)


class Place:
    def __init__(self):
        self.d = lax.axis_index("dp")
        self.x = lax.axis_index("tensor")
        self.z = self.d // 4
        self.y = (self.d // 2) % 2
        self.c = self.d % 2
        self.ids = {
            "c": (self.d + 1 - 2 * self.c, self.x),
            "y": (self.d + 2 - 4 * self.y, self.x),
            "x": (self.d, 1 - self.x),
            "z+": (self.d + 4, self.x),
            "z-": (self.d - 4, self.x),
        }

    def greet(self, kinds):
        bar = pltpu.get_barrier_semaphore()
        for k in kinds:
            pl.semaphore_signal(bar, inc=1, device_id=self.ids[k], device_id_type=MESH)

        @pl.when(self.z < 3)
        def _():
            pl.semaphore_signal(bar, inc=1, device_id=self.ids["z+"], device_id_type=MESH)

        @pl.when(self.z > 0)
        def _():
            pl.semaphore_signal(bar, inc=1, device_id=self.ids["z-"], device_id_type=MESH)

        inner = jnp.where(jnp.logical_and(self.z > 0, self.z < 3), 1, 0)
        pl.semaphore_wait(bar, len(kinds) + 1 + inner)

    def there(self, disp):
        dz = disp[0]
        if dz == 0:
            return None
        return self.z + dz <= 3 if dz > 0 else self.z + dz >= 0

    def at(self, disp):
        dz, fy, fx = disp
        return (1 - self.x if fx else self.x, self.z + dz, 1 - self.y if fy else self.y)


def when(cond, f):
    if cond is None:
        f()
    else:
        pl.when(cond)(f)


def both(a, b):
    if a is None:
        return b
    if b is None:
        return a
    return jnp.logical_and(a, b)


def spread(order):
    out = {}
    todo = [((0, 0, 0), -1, 0)]
    while todo:
        (dz, fy, fx), last, way = todo.pop(0)
        nxt = []
        for i, a in enumerate(order):
            if i < last:
                continue
            if a == "z":
                for s in (1, -1):
                    if i == last and s != way:
                        continue
                    n = (dz - s, fy, fx)
                    if abs(n[0]) <= 3:
                        nxt.append((n, "z+" if s > 0 else "z-", i, s))
            elif i > last:
                n = (dz, 1, fx) if a == "y" else (dz, fy, 1)
                nxt.append((n, a, i, 0))
        out[(dz, fy, fx)] = [(n, w) for n, w, _, _ in nxt]
        todo += [(n, i, s) for n, _, i, s in nxt]
    return out


def hops(d):
    return abs(d[0]) + d[1] + d[2]


BACK = {"z+": "z-", "z-": "z+", "x": "x", "y": "y"}


def add_rows(acc, got, step=80):
    n = acc.shape[0]
    while n % step:
        step -= 16

    def body(i, _):
        r = pl.ds(pl.multiple_of(i * step, step), step)
        acc[r, :] = acc[r, :] + got[r, :]
        return 0

    lax.fori_loop(0, n // step, body, 0)


SHARD_UNITS = 656
PANEL = 128
GROUPS = ((0, 1), (2,), (3,), (4, 5, 6), (7, 8))

PLAN_OUT = (
    ("zy", "yz", "zy", "yz", "zy"),
    ("zyx", "yzx", "yzx", "zxy", "xzy"),
    (
        192, 194, 128, 0, 193, 130, 198, 195, 133, 197, 134, 129, 132, 137, 201, 1, 199, 136, 131, 9, 196, 138, 202,
        135, 140, 8, 200, 141, 2, 139, 205, 203, 204, 142, 143, 3, 206, 5, 4, 12, 207, 147, 144, 6, 64, 256, 208, 7,
        211, 10, 146, 212, 11, 65, 13, 265, 261, 268, 150, 257, 221, 148, 260, 154, 219, 67, 66, 153, 258, 218, 68,
        14, 264, 69, 15, 161, 259, 262, 156, 70, 157, 226, 71, 16, 19, 266, 263, 73, 227, 18, 17, 72, 74, 26, 168,
        224, 162, 269, 20, 267, 76, 149, 152, 77, 34, 155, 75, 270, 29, 27, 271, 78, 79, 36, 272, 35, 275, 83, 80, 40,
        166, 282, 273, 90, 216, 39, 290, 25, 209, 233, 217, 82, 296, 42, 84, 276, 24, 21, 281, 22, 31, 164, 98, 231,
        285, 91, 96, 86, 280, 151, 88, 37, 33, 232, 32, 277, 89, 213, 23, 28, 278, 41, 283, 93, 289, 228, 85, 215, 92,
        97, 220, 145, 230, 170, 284, 160, 279, 288, 87, 165, 104, 225, 222, 169, 100, 295, 103, 286, 81, 274, 30, 163,
        293, 294, 292, 159, 167, 229, 95, 210, 94, 287, 99, 38, 223, 158, 291, 102, 106, 214, 101, 105, 298, 234, 297,
    ),
)
PLAN_BACK = (
    ("zxy", "yzx", "zyx", "yzx", "xzy"),
    ("zy", "zy", "zy", "yz", "yz"),
    (
        256, 257, 258, 262, 261, 269, 64, 259, 67, 260, 65, 69, 263, 66, 78, 264, 271, 278, 276, 77, 270, 268, 267,
        71, 70, 275, 282, 85, 72, 266, 76, 265, 192, 82, 68, 199, 277, 73, 0, 84, 274, 74, 272, 5, 273, 80, 75, 279,
        6, 79, 13, 128, 204, 1, 281, 2, 12, 89, 283, 280, 11, 141, 129, 19, 8, 83, 4, 195, 86, 193, 87, 3, 134, 15, 7,
        81, 284, 285, 133, 88, 91, 14, 10, 197, 194, 90, 22, 196, 132, 286, 131, 201, 288, 287, 130, 16, 18, 21, 198,
        9, 92, 20, 205, 93, 291, 202, 200, 290, 136, 289, 143, 292, 26, 140, 208, 150, 206, 17, 94, 23, 135, 25, 212,
        213, 294, 95, 142, 203, 96, 24, 138, 148, 139, 207, 137, 211, 27, 214, 210, 100, 97, 295, 144, 215, 149, 104,
        146, 209, 147, 28, 29, 151, 218, 219, 217, 145, 154, 32, 101, 153, 106, 30, 216, 36, 155, 152, 296, 33, 220,
        105, 221, 293, 98, 156, 40, 157, 224, 31, 103, 298, 222, 160, 158, 223, 164, 102, 99, 228, 37, 161, 227, 165,
        41, 225, 168, 159, 226, 35, 42, 34, 229, 163, 297, 39, 231, 230, 232, 162, 167, 170, 234, 38, 166, 169, 233,
    ),
)


def layout(shapes, shards):
    table = []
    unit_at, row_at, flat_at = 0, 0, 0
    starts = [g[0] for g in GROUPS]
    for i, (rows, cols) in enumerate(shapes):
        if i in starts:
            unit_at = -(-unit_at // 16) * 16
        rb, panels = rows // shards, cols // PANEL
        units = rb * cols // 512
        padded = -(-rb // 16) * 16
        table.append((rb, panels, units, unit_at, row_at, padded, flat_at))
        unit_at += units
        row_at += padded * panels
        flat_at += units * shards
    return table, unit_at, row_at


def unit_places(units, table, shards):
    place = jnp.zeros_like(units)
    for _, _, n, first, _, _, lo in table:
        v = units - lo
        here = (v // n) * SHARD_UNITS + first + v % n
        place = jnp.where(v >= 0, here, place)
    return place


def own_units(owners, mine, capacity):
    count = owners.shape[0] // 128
    hit = (owners[:, 0] == mine).reshape(count, 128)
    lane = jnp.arange(128)
    tri = (lane[:, None] <= lane[None, :]).astype(jnp.bfloat16)
    within = jnp.dot(hit.astype(jnp.bfloat16), tri, preferred_element_type=jnp.float32)
    totals = within[:, 127].astype(jnp.int32)
    upto = jnp.sum(jnp.where(jnp.arange(count)[:, None] >= jnp.arange(count)[None, :], totals[None, :], 0), axis=1)
    slot = jnp.arange(capacity, dtype=jnp.int32)
    block = jnp.sum((upto[None, :] <= slot[:, None]).astype(jnp.int32), axis=1)
    pick = block[:, None] == jnp.arange(count)[None, :]
    before = jnp.sum(jnp.where(pick, (upto - totals)[None, :], 0), axis=1)
    row = jnp.dot(pick.astype(jnp.bfloat16), within.astype(jnp.bfloat16), preferred_element_type=jnp.float32)
    rank = (slot - before).astype(jnp.float32)
    at = jnp.sum((row <= rank[:, None]).astype(jnp.int32), axis=1)
    return block * 128 + at, slot < upto[count - 1]


BY_ROWS = (1, 3, 6, 8)


def position_table():
    cols = []
    for width in (DE, DD):
        side = width // 16 * 6
        parts = (width - 2 * side, side, side)
        tab = np.zeros((48, width), np.float64)
        col = 0
        for i, n in enumerate(parts):
            half = n // 2
            freq = 1.0 / 10000.0 ** (np.arange(half) / half)
            ang = np.arange(16)[:, None] * freq[None, :]
            tab[16 * i:16 * i + 16, col:col + n] = np.concatenate([np.sin(ang), np.cos(ang)], axis=1)
            col += n
        cols.append(tab)
    left = np.concatenate(cols, axis=1).astype(np.float32)
    terms = []
    for _ in range(3):
        terms.append(left.astype(ml_dtypes.bfloat16))
        left = left - terms[-1].astype(np.float32)
    return np.stack(terms)


def dot(a, b):
    return jnp.dot(a, b, preferred_element_type=jnp.float32)


def dot_nt(a, b):
    return lax.dot_general(a, b, (((1,), (1,)), ((), ())), preferred_element_type=jnp.float32)


def dot_tn(a, b):
    return lax.dot_general(a, b, (((0,), (0,)), ((), ())), preferred_element_type=jnp.float32)


def lanes(i, n=128):
    return pl.ds(pl.multiple_of(i * n, n), n)


def ln_parts(x):
    c = x - jnp.mean(x, axis=-1, keepdims=True)
    inv = lax.rsqrt(jnp.mean(c * c, axis=-1, keepdims=True) + NORM_EPS)
    return c * inv, inv


def ln_back(up, m, inv, gain):
    s = up * gain
    a = jnp.mean(s, axis=-1, keepdims=True)
    b = jnp.mean(s * m, axis=-1, keepdims=True)
    return inv * (s - a - m * b), jnp.sum(up * m, axis=0, keepdims=True), jnp.sum(up, axis=0, keepdims=True)


class Block:
    def __init__(self, width, heads, size, hidden, first, table, col):
        self.width, self.heads, self.size, self.hidden, self.col = width, heads, size, hidden, col
        self.q, self.o, self.a, self.b = table[first:first + 4]
        self.part = heads // 2 * size
        self.per = 128 // size


def panel(w, t, mat, g, lo=0, num=16):
    rb, _, _, _, at, padded, _ = mat
    rows = pl.ds(pl.multiple_of(at + g * padded, 16), padded)
    v = w[t, lo:lo + num, rows, :] if isinstance(lo, int) else w[t, pl.ds(lo, num), rows, :]
    if padded > rb:
        v = v.astype(jnp.float32)[:, :rb].reshape(num * rb, 128).astype(jnp.bfloat16)
        return v
    return v.reshape(num * rb, 128)


def pair(w, mat, g):
    return jnp.concatenate([panel(w, 0, mat, g), panel(w, 1, mat, g)], axis=1)


def repeat(count, step, f):
    step = max(k for k in range(1, step + 1) if count % k == 0)

    def turn(i, _):
        for k in range(step):
            f(i * step + k)
        return 0

    if step == count:
        turn(0, 0)
    else:
        lax.fori_loop(0, count // step, turn, 0)


def pull(acc, up, w, mat, step):
    count = mat[1]
    step = max(k for k in range(1, step + 1) if count % k == 0)

    def part(i):
        gs = [i * step + k for k in range(step)]
        d = jnp.concatenate([up[:, lanes(o + g)] for g in gs for o in (0, count)], axis=1)
        return dot_nt(d, jnp.concatenate([pair(w, mat, g) for g in gs], axis=1))

    acc[...] = part(0)

    def turn(i, _):
        acc[...] += part(i)
        return 0

    lax.fori_loop(1, count // step, turn, 0)


def block_fwd(b, x, xo, w, gains, biases, same, n1, proj, p, att, ow, m1, i1, n2, m2, i2, act, slope,
              need, keep):
    cols = slice(b.col, b.col + b.width)
    m, inv = ln_parts(x[...])
    m1[...] = m
    i1[...] = inv
    n1[...] = (m * gains[0:1, cols] + biases[0:1, cols]).astype(jnp.bfloat16)
    keep(0)
    need(0)
    gq = b.q[1]

    def qkv(g):
        r = dot(n1[...], pair(w, b.q, g)).astype(jnp.bfloat16)
        proj[:, lanes(g)] = r[:, :128]
        proj[:, lanes(gq + g)] = r[:, 128:]

    repeat(gq, 9, qkv)
    np_ = b.part // 128
    lane = lax.broadcasted_iota(jnp.int32, (256, 128), 1)
    masks = [lane // b.size == i for i in range(b.per)]

    def heads(i, _):
        t, j = i // np_, i % np_
        q = proj[:, lanes(t * gq + j)]
        k = proj[:, lanes(t * gq + np_ + j)]
        v = proj[:, lanes(t * gq + 2 * np_ + j)]
        total = jnp.zeros((256, 128), jnp.float32)
        for h in range(b.per):
            z = dot_nt(jnp.where(masks[h], q, 0), k) * b.size ** (-0.5) + same
            e = jnp.exp(z - jnp.max(z, axis=-1, keepdims=True))
            s = e * (1.0 / jnp.sum(e, axis=-1, keepdims=True))
            p[i * b.per + h] = s
            total = total + dot(s.astype(jnp.bfloat16), jnp.where(masks[h], v, 0))
        att[:, lanes(i)] = total.astype(jnp.bfloat16)
        return 0

    lax.fori_loop(0, 2 * np_, heads, 0)
    keep(1)
    need(1)
    for t in range(2):
        for g in range(b.width // 128):
            ow[t, :, g * 128:(g + 1) * 128] = panel(w, t, b.o, g)
    x1 = x[...] + dot(att[:, :b.part], ow[0]) + dot(att[:, b.part:], ow[1])
    xo[...] = x1
    m, inv = ln_parts(x1)
    m2[...] = m
    i2[...] = inv
    n2[...] = (m * gains[1:2, cols] + biases[1:2, cols]).astype(jnp.bfloat16)
    keep(2)
    need(2)
    ga = b.a[1]

    def up(g):
        h = dot(n2[...], pair(w, b.a, g))
        big = 0.5 * (1.0 + lax.erf(h * 0.7071067811865476))
        act_v = (h * big).astype(jnp.bfloat16)
        dens = big + h * (0.3989422804014327 * jnp.exp(-0.5 * h * h))
        act[:, lanes(g)] = act_v[:, :128]
        act[:, lanes(ga + g)] = act_v[:, 128:]
        slope[:, lanes(g)] = dens[:, :128]
        slope[:, lanes(ga + g)] = dens[:, 128:]

    repeat(ga, 12, up)
    keep(3)
    need(3)
    half = b.hidden // 2

    def down(g):
        w0 = jnp.concatenate([panel(w, 0, b.b, 2 * g), panel(w, 0, b.b, 2 * g + 1)], axis=1)
        w1 = jnp.concatenate([panel(w, 1, b.b, 2 * g), panel(w, 1, b.b, 2 * g + 1)], axis=1)
        xo[:, lanes(g, 256)] += dot(act[:, :half], w0) + dot(act[:, half:], w1)

    repeat(b.width // 256, 1, down)


def block_bwd(b, dr, w, gains, same, n1, proj, p, att, ow, m1, i1, n2, m2, i2, act, slope,
              r, dh, r1, dp_out, acc, da, norm_out, keep):
    cols = slice(b.col, b.col + b.width)
    r[...] = dr[...].astype(jnp.bfloat16)
    keep(3)
    half = b.hidden // 2
    rb = b.b[0]
    gb = b.width // 128
    num = 16

    def hidden(i, _):
        t, lo = i // (16 // num), (i % (16 // num)) * num
        wc = jnp.concatenate([panel(w, t, b.b, g, lo, num) for g in range(gb)], axis=1)
        at = lanes(i, num * rb)
        dh[:, at] = (dot_nt(r[...], wc) * slope[:, at]).astype(jnp.bfloat16)
        return 0

    lax.fori_loop(0, 2 * (16 // num), hidden, 0)
    keep(2)
    ga = b.a[1]
    pull(acc, dh, w, b.a, 12)
    dx, dg, db = ln_back(acc[...], m2[...], i2[...], gains[1:2, cols])
    norm_out[1:2, cols] = dg
    norm_out[3:4, cols] = db
    dx1 = dr[...] + dx
    dr[...] = dx1
    r1[...] = dx1.astype(jnp.bfloat16)
    keep(1)
    for t in range(2):
        da[:, t * b.part:(t + 1) * b.part] = dot_nt(r1[...], ow[t]).astype(jnp.bfloat16)
    gq = b.q[1]
    np_ = b.part // 128
    lane = lax.broadcasted_iota(jnp.int32, (256, 128), 1)
    masks = [lane // b.size == i for i in range(b.per)]
    scale = b.size ** (-0.5)

    def heads(i, _):
        t, j = i // np_, i % np_
        q = proj[:, lanes(t * gq + j)]
        k = proj[:, lanes(t * gq + np_ + j)]
        v = proj[:, lanes(t * gq + 2 * np_ + j)]
        up_ = da[:, lanes(i)]
        dq = jnp.zeros((256, 128), jnp.float32)
        dk = jnp.zeros((256, 128), jnp.float32)
        dv = jnp.zeros((256, 128), jnp.float32)
        for h in range(b.per):
            s = p[i * b.per + h]
            u = jnp.where(masks[h], up_, 0)
            dp = dot_nt(u, v)
            dv = dv + dot_tn(s.astype(jnp.bfloat16), u)
            t1 = s * dp
            dz = (t1 - s * jnp.sum(t1, axis=-1, keepdims=True)).astype(jnp.bfloat16)
            dq = dq + dot(dz, jnp.where(masks[h], k, 0))
            dk = dk + dot_tn(dz, jnp.where(masks[h], q, 0))
        dp_out[:, lanes(t * gq + j)] = (dq * scale).astype(jnp.bfloat16)
        dp_out[:, lanes(t * gq + np_ + j)] = (dk * scale).astype(jnp.bfloat16)
        dp_out[:, lanes(t * gq + 2 * np_ + j)] = dv.astype(jnp.bfloat16)
        return 0

    lax.fori_loop(0, 2 * np_, heads, 0)
    keep(0)
    pull(acc, dp_out, w, b.q, 9)
    dx, dg, db = ln_back(acc[...], m1[...], i1[...], gains[0:1, cols])
    norm_out[0:1, cols] = dg
    norm_out[2:3, cols] = db
    dr[...] = dr[...] + dx


ACTS = (DE, DE, DE, FFE, DE, DD, DD, DD, FFD)
GRADS = (3 * DE, DE, FFE, DE, DD, 3 * DD, DD, FFD, DD)


def chain_kernel(table, tok, pos, tile, gains, biases, cot, tab, w_hbm, *refs):
    dec, dx0, norm_out = refs[:3]
    kept_out = refs[3:21]
    kept = refs[21:39]
    acts, grads = kept[:9], kept[9:]
    (w, pe, pd, se, sd, proj_e, proj_d, da_e, da_d, ow_e, ow_d, m1e, m2e, m1d, m2d, i1e, i2e, i1d, i2d,
     x, y, acc_e, acc_d, w_sem, out_sem) = refs[39:]
    enc_b = Block(DE, HE, HDE, FFE, 0, table, 0)
    dec_b = Block(DD, HD, HDD, FFD, 5, table, DE)
    em = table[4]

    def load(m):
        rows = pl.ds(table[m][4], table[m][1] * table[m][5])
        return pltpu.make_async_copy(w_hbm.at[:, :, rows], w.at[:, :, rows], w_sem.at[m])

    def store(i):
        return pltpu.make_async_copy(kept[i], kept_out[i], out_sem.at[i])

    for m in range(9):
        load(m).start()
    row = lax.broadcasted_iota(jnp.int32, (48, 256), 0)
    spots = [jnp.concatenate([pos[0, i:i + 1, :], pos[1, i:i + 1, :]], axis=1) for i in range(3)]
    hot = jnp.logical_or(jnp.logical_or(row == spots[0], row == spots[1] + 16), row == spots[2] + 32)
    hot = jnp.where(hot, 1.0, 0.0).astype(jnp.bfloat16)
    ids = tile[lax.axis_index("tensor")]
    tiles = jnp.where(lax.broadcasted_iota(jnp.int32, (16, 256), 0) == ids, 1.0, 0.0).astype(jnp.bfloat16)
    same = (1.0 - dot_tn(tiles, tiles)) * MASK_FILL
    x[...] = tok[...].astype(jnp.float32) + sum(dot_tn(hot, tab[i, :, :DE]) for i in range(3))
    n1e, ae, n2e, ue, low, n1d, ad, n2d, ud = acts
    dpe, r1e, dhe, re, dlow, dpd, r1d, dhd, rd = grads
    block_fwd(enc_b, x, dx0, w, gains, biases, same, n1e, proj_e, pe, ae, ow_e, m1e, i1e, n2e, m2e, i2e, ue, se,
              lambda k: load(k).wait(), lambda k: store(k).start())
    low[...] = dx0[...].astype(jnp.bfloat16)
    store(4).start()
    load(4).wait()
    for g in range(2):
        v = dot(low[...], pair(w, em, g)).astype(jnp.bfloat16).astype(jnp.float32)
        y[:, g * 128:(g + 1) * 128] = v[:, :128]
        y[:, 256 + g * 128:256 + (g + 1) * 128] = v[:, 128:]
    y[...] += sum(dot_tn(hot, tab[i, :, DE:]) for i in range(3))
    block_fwd(dec_b, y, dec, w, gains, biases, same, n1d, proj_d, pd, ad, ow_d, m1d, i1d, n2d, m2d, i2d, ud, sd,
              lambda k: load(5 + k).wait(), lambda k: store(5 + k).start())
    y[...] = cot[...]
    block_bwd(dec_b, y, w, gains, same, n1d, proj_d, pd, ad, ow_d, m1d, i1d, n2d, m2d, i2d, ud, sd,
              rd, dhd, r1d, dpd, acc_d, da_d, norm_out, lambda k: store(14 + k).start())
    dlow[...] = y[...].astype(jnp.bfloat16)
    store(13).start()
    for g in range(2):
        d = jnp.concatenate([dlow[:, g * 128:(g + 1) * 128], dlow[:, 256 + g * 128:256 + (g + 1) * 128]], axis=1)
        v = dot_nt(d, pair(w, em, g))
        if g == 0:
            dx0[...] = v
        else:
            dx0[...] += v
    block_bwd(enc_b, dx0, w, gains, same, n1e, proj_e, pe, ae, ow_e, m1e, i1e, n2e, m2e, i2e, ue, se,
              re, dhe, r1e, dpe, acc_e, da_e, norm_out, lambda k: store(9 + k).start())
    for i in range(18):
        store(i).wait()


def chain(tokens, pos, tile, gains, biases, cot, full, table):
    f32, bf16 = jnp.float32, jnp.bfloat16
    S = jax.ShapeDtypeStruct
    outs = [S((256, DD), f32), S((256, DE), f32), S((4, DE + DD), f32)]
    kept = [(256, n) for n in ACTS + GRADS]
    outs += [S(k, bf16) for k in kept]
    V = pltpu.VMEM
    scratch = [V(k, bf16) for k in kept] + [
        V((2, 16) + full.shape[-2:], bf16),
        V((HE, 256, 256), f32), V((HD, 256, 256), f32), V((256, FFE), f32), V((256, FFD), f32),
        V((256, 3 * DE), bf16), V((256, 3 * DD), bf16), V((256, DE), bf16), V((256, DD), bf16),
        V((2, DE // 2, DE), bf16), V((2, DD // 2, DD), bf16),
        V((256, DE), f32), V((256, DE), f32), V((256, DD), f32), V((256, DD), f32)] + [V((256, 1), f32)] * 4 + [
        V((256, DE), f32), V((256, DD), f32), V((256, DE), f32), V((256, DD), f32),
        pltpu.SemaphoreType.DMA((9,)), pltpu.SemaphoreType.DMA((18,))]
    vmem = pl.BlockSpec(memory_space=pltpu.VMEM)
    hbm = pl.BlockSpec(memory_space=pl.ANY)
    args = (tokens, pos, tile, gains, biases, cot, jnp.asarray(position_table()),
            full.reshape(2, 16, full.shape[-2], 128))
    return pl.pallas_call(
        partial(chain_kernel, table), out_shape=outs, in_specs=[vmem] * 7 + [hbm], out_specs=[vmem] * 3 + [hbm] * 18,
        scratch_shapes=scratch, compiler_params=pltpu.CompilerParams(vmem_limit_bytes=63 << 20), name="chain",
        cost_estimate=pl.CostEstimate(flops=11_000_000_000, bytes_accessed=40_000_000, transcendentals=5_000_000),
    )(*args)


def grad_panels(table, m, act, grad, turned, put):
    mat = table[m]
    rb, panels, padded = mat[0], mat[1], mat[5]
    count = act.shape[1]

    def turn(i):
        turned[pl.ds(pl.multiple_of(i * 128, 128), 128), :] = act[:, lanes(i)].T

    repeat(count // 128, 6, turn)

    def place(t, g, v):
        if padded > rb:
            v = v.reshape(16, rb, 128)
            v = jnp.concatenate([v, jnp.zeros((16, padded - rb, 128), jnp.float32)], axis=1).astype(jnp.bfloat16)
        else:
            v = v.astype(jnp.bfloat16).reshape(16, rb, 128)
        put(t, g, v)

    if m in BY_ROWS:
        half = count // 2

        def body(i):
            t, g = i // (panels // 2), i % (panels // 2)
            v = dot(turned[pl.ds(pl.multiple_of(t * half, 128), half), :], grad[:, lanes(g, 256)])
            place(t, 2 * g, v[:, :128])
            place(t, 2 * g + 1, v[:, 128:])

        repeat(panels, 6, body)
    else:
        def body(g):
            d = jnp.concatenate([grad[:, lanes(g)], grad[:, lanes(panels + g)]], axis=1)
            v = dot(turned[:count, :], d)
            place(0, g, v[:, :128])
            place(1, g, v[:, 128:])

        repeat(panels, 6, body)


class Wires:
    def __init__(self, place, sem):
        self.place, self.sem, self.used, self.waits = place, sem, 0, []

    def new(self, n=1):
        self.used += n
        assert self.used <= self.sem.shape[0], self.used
        return self.used - n

    def copy(self, k, src, dst, way):
        return pltpu.make_async_remote_copy(src_ref=src, dst_ref=dst, send_sem=self.sem.at[k], recv_sem=self.sem.at[k + 1],
                                            device_id=self.place.ids[way], device_id_type=MESH)

    def send(self, k, src, dst, way, cond=None):
        cp = self.copy(k, src, dst, way)
        when(cond, cp.start)
        self.waits.append((cond, cp))

    def land(self, k, dst, cond=None):
        when(cond, self.copy(k, dst, dst, "c").wait_recv)

    def drain(self):
        for cond, cp in self.waits:
            when(cond, cp.wait_send)


def edge_slots(order):
    slots, used, shared = {}, 0, {}
    for d, kids in sorted(spread(order).items()):
        for _, way in kids:
            if way in "xy" and order.index("z") < order.index(way):
                key = (way, d[1], d[2])
                if key not in shared:
                    shared[key] = used
                    used += 4
                slots[d, way] = (shared[key], 4)
            else:
                slots[d, way] = (used, 1)
                used += 1
    return slots, used


def beyond(p, way):
    return p.z < 3 if way == "z+" else p.z > 0 if way == "z-" else None


def reduce_events(p, w, order, own, half, bufs, ready, done):
    tree = spread(order)
    pair = {d: w.new(2) for d in tree}
    wire = {d: w.new(2) for d in tree}
    parent = {nd: (d, way) for d, t in tree.items() for nd, way in t}
    slots, _ = edge_slots(order)

    def buffer(up, way):
        first, n = slots[up, way]
        return bufs.at[first + p.z + up[0] if n > 1 else first]

    events = []
    far = sorted(tree, key=lambda d: (-hops(d), d))
    for d in far:
        def act(d=d):
            cond = p.there(d)

            def step():
                acc = own(d)
                ready(d)
                w.land(pair[d], half(d))
                add_rows(acc, half(d))
                for nd, way in tree[d]:
                    buf = buffer(d, way)

                    def take(buf=buf, nd=nd):
                        w.land(wire[nd], buf)
                        add_rows(acc, buf)
                    when(beyond(p, way), take)
            when(cond, step)
            if hops(d) == 0:
                done()
            else:
                up, way = parent[d]
                w.send(wire[d], own(d), buffer(up, way), BACK[way], cond)
        events.append(act)

    def share(give):
        for d in far:
            w.send(pair[d], give(d), half(d), "c", p.there(d))

    return events, share, far


def gather_events(p, w, order, first, at):
    tree = spread(order)
    pair = {d: w.new(2) for d in tree}
    wire = {d: w.new(2) for d in tree}
    events = []
    for d in sorted(tree, key=lambda d: (hops(d), d)):
        def act(d=d):
            cond = p.there(d)
            blk = at(d, p.c)
            if hops(d):
                w.land(wire[d], blk, cond)
                src = blk
            else:
                src = first
            for nd, way in tree[d]:
                w.send(wire[nd], src, blk, way, both(cond, beyond(p, way)))
            w.send(pair[d], src, blk, "c", cond)
        events.append(act)

    def finish():
        for d in tree:
            w.land(pair[d], at(d, 1 - p.c), p.there(d))

    return events, finish


def run_events(lists, order, extra=iter(()), every=8):
    assert sorted(order) == sorted(64 * g + i for g, acts in enumerate(lists) for i in range(len(acts)))
    for n, k in enumerate(order):
        if n % every == 0:
            next(extra, None)
        lists[k // 64][k % 64]()
    for _ in extra:
        pass


def group_span(table, mats):
    first, last = table[mats[0]], table[mats[-1]]
    units = last[3] + last[2] - first[3]
    return first[3], -(-units // 16) * 16, first[4], last[4] + last[1] * last[5] - first[4]


def units_to_panels(table, mats, units, flat, put):
    base, count = table[mats[0]][3], units.shape[0]
    for k in range(4):
        flat[pl.ds(k, count, stride=4), :] = units[:, 128 * k:128 * (k + 1)].astype(jnp.float32)
    for m in mats:
        rb, panels, n, first, _, padded, _ = table[m]
        for g in range(panels):
            v = flat[pl.ds(4 * (first - base) + g, rb, stride=panels), :]
            if padded > rb:
                v = jnp.concatenate([v, jnp.zeros((padded - rb, 128), jnp.float32)], axis=0)
            put(m, g, v.astype(jnp.bfloat16))


def panels_to_units(table, mats, take, flat, units):
    base, count = table[mats[0]][3], units.shape[0]
    used = 0
    for m in mats:
        rb, panels, n, first, _, padded, _ = table[m]
        for g in range(panels):
            flat[pl.ds(4 * (first - base) + g, rb, stride=panels), :] = take(m, g)[:rb]
        used = 4 * (first - base + n)
    if used < 4 * count:
        flat[used:4 * count, :] = jnp.zeros((4 * count - used, 128), jnp.float32)
    for k in range(4):
        units[:, 128 * k:128 * (k + 1)] = flat[pl.ds(k, count, stride=4), :].astype(jnp.bfloat16)


class Swap:
    def __init__(self, p, w, src, out, give, keep):
        self.p, self.w, self.src, self.out, self.give, self.keep = p, w, src, out, give, keep
        self.k, self.own = w.new(2), w.new()

    def local(self):
        return pltpu.make_async_copy(self.src.at[self.keep], self.out.at[self.p.x], self.w.sem.at[self.own])

    def start(self):
        self.w.send(self.k, self.src.at[self.give], self.out.at[self.p.x], "x")
        self.local().start()

    def finish(self):
        self.w.land(self.k, self.out.at[1 - self.p.x])
        self.local().wait()


def weights_kernel(table, groups, plan, parts, tok_in, pos_in, cot_in, out, tok, pos, cot, *rest):
    n = len(groups)
    accs, halves, bufs, shards = (rest[i * n:(i + 1) * n] for i in range(4))
    flat, sem = rest[4 * n:]
    p = Place()
    p.greet(["c", "y", "x"])
    w = Wires(p, sem)
    swaps = [Swap(p, w, a, b, 1 - p.x, p.x) for a, b in ((tok_in, tok), (pos_in, pos), (cot_in, cot))]
    for s in swaps:
        s.start()
    lists, finishes = [], []
    for g, mats in enumerate(groups):
        u0, un, r0, rn = group_span(table, mats)
        acc, half, buf, shard = accs[g], halves[g], bufs[g], shards[g]
        own_sem = w.new()
        loads = {d: w.new() for d in spread(plan[0][g])}

        def own(d, acc=acc):
            return acc.at[p.at(d)[1:]]

        def other(d, half=half):
            return half.at[p.at(d)[1:]]

        def load(d, u0=u0, un=un, own=own, loads=loads):
            return pltpu.make_async_copy(parts.at[p.at(d)[1:] + (p.c, pl.ds(u0, un))], own(d), sem.at[loads[d]])

        def ready(d, load=load):
            load(d).wait()

        def done(mats=mats, acc=acc, shard=shard, r0=r0):
            def put(m, i, v):
                lo = table[m][4] - r0 + i * table[m][5]
                shard[lo:lo + table[m][5], :] = v
            units_to_panels(table, mats, acc.at[p.z, p.y], flat, put)

        ev, share, far = reduce_events(p, w, plan[0][g], own, other, buf, ready, done)

        def begin(load=load, share=share, far=far, u0=u0, un=un):
            share(lambda d: parts.at[p.at(d)[1:] + (1 - p.c, pl.ds(u0, un))])
            for d in far:
                when(p.there(d), load(d).start)

        def at(d, core, r0=r0, rn=rn):
            t, z, y = p.at(d)
            return out.at[t, z, y, core, pl.ds(r0, rn)]

        def local(shard=shard, r0=r0, rn=rn, own_sem=own_sem):
            return pltpu.make_async_copy(shard, out.at[p.x, p.z, p.y, p.c, pl.ds(r0, rn)], sem.at[own_sem])

        ag, finish = gather_events(p, w, plan[1][g], shard, at)

        def send_first(act=ag[0], local=local):
            act()
            local().start()

        lists.append([begin] + ev + [send_first] + ag[1:])
        finishes += [finish, lambda local=local: local().wait()]
    run_events(lists, plan[2])
    for f in finishes + [s.finish for s in swaps]:
        f()
    w.drain()


def spread_weights(parts, tokens, pos, cot, table, rows, groups, plan, ident):
    spans = [group_span(table, m) for m in groups]
    bf16 = jnp.bfloat16
    S = jax.ShapeDtypeStruct
    scratch = [pltpu.VMEM((4, 2, s[1], 512), bf16) for s in spans] * 2
    scratch += [pltpu.VMEM((edge_slots(o)[1], s[1], 512), bf16) for s, o in zip(spans, plan[0])]
    scratch += [pltpu.VMEM((s[3], 128), bf16) for s in spans]
    scratch += [pltpu.VMEM((4 * max(s[1] for s in spans), 128), jnp.float32),
                pltpu.SemaphoreType.DMA((len(groups) * (1 + 5 * 14 + 4 * 28) + 9,))]
    hbm = pl.BlockSpec(memory_space=pl.ANY)
    return pl.pallas_call(
        partial(weights_kernel, table, groups, plan),
        out_shape=[S((2, 4, 2, 2, rows, 128), bf16)] + [S(v.shape, v.dtype) for v in (tokens, pos, cot)],
        in_specs=[hbm] * 4, out_specs=[hbm] * 4,
        scratch_shapes=scratch,
        compiler_params=pltpu.CompilerParams(collective_id=ident, has_side_effects=True, vmem_limit_bytes=62 << 20),
        name="spread_weights",
    )(parts, tokens, pos, cot)


def return_kernel(table, groups, plan, *refs):
    n = len(groups)
    kept_in, small_src, dec_in, dx_in, out, small_out, dec, dx = refs[:18], *refs[18:25]
    rest = refs[25:]
    kept, rest = rest[:18], rest[18:]
    acts, grads = kept[:9], kept[9:]
    sides, halves, bufs, units = (rest[i * n:(i + 1) * n] for i in range(4))
    flat, turned, mid, line, load_sem, sem = rest[4 * n:]

    def load(i):
        return pltpu.make_async_copy(kept_in[i], kept[i], load_sem.at[i])

    first = sorted(range(n), key=lambda g: plan[2].index(64 * g))
    for g in first:
        for m in groups[g]:
            load(m).start()
            load(9 + m).start()
    p = Place()
    p.greet(["c", "y", "x"])
    w = Wires(p, sem)
    swaps = [Swap(p, w, a, b, 1 - p.x, p.x) for a, b in ((dec_in, dec), (dx_in, dx))]
    swaps[0].start()
    lists, finishes = [], []
    for g, mats in enumerate(groups):
        u0, un, r0, rn = group_span(table, mats)
        side, half, buf, unit = sides[g], halves[g], bufs[g], units[g]
        own_sem = w.new()

        def own(d, side=side):
            return side.at[(p.c,) + p.at(d)]

        def other(d, half=half):
            return half.at[p.at(d)]

        def done(mats=mats, side=side, unit=unit, r0=r0):
            mine = side.at[p.c, p.x, p.z, p.y]

            def take(m, i):
                lo = table[m][4] - r0 + i * table[m][5]
                return mine[lo:lo + table[m][5], :].astype(jnp.float32)
            panels_to_units(table, mats, take, flat, unit)

        ev, share, far = reduce_events(p, w, plan[0][g], own, other, buf, lambda d: None, done)

        def begin(mats=mats, side=side, share=share, r0=r0):
            for m in mats:
                lo, padded = table[m][4] - r0, table[m][5]

                def put(t, i, v, lo=lo, padded=padded):
                    v = v.reshape(4, 2, 2, padded, 128)
                    rows = pl.ds(pl.multiple_of(lo + i * padded, 16), padded)
                    side[0, t, :, :, rows, :] = v[:, :, 0]
                    side[1, t, :, :, rows, :] = v[:, :, 1]
                load(m).wait()
                load(9 + m).wait()
                grad_panels(table, m, acts[m], grads[m], turned, put)
            share(lambda d: side.at[(1 - p.c,) + p.at(d)])

        def at(d, core, u0=u0, un=un):
            _, z, y = p.at(d)
            return out.at[z, y, core, pl.ds(u0, un)]

        def local(unit=unit, u0=u0, un=un, own_sem=own_sem):
            return pltpu.make_async_copy(unit, out.at[p.z, p.y, p.c, pl.ds(u0, un)], sem.at[own_sem])

        ag, finish = gather_events(p, w, plan[1][g], unit, at)

        def send_first(act=ag[0], local=local):
            act()
            local().start()

        lists.append([begin] + ev + [send_first] + ag[1:])
        finishes += [finish, lambda local=local: local().wait()]
    last = max(plan[2].index(64 * g + len(spread(plan[0][g]))) for g in range(n))
    g, i = plan[2][last] // 64, plan[2][last] % 64
    act = lists[g][i]

    def with_swaps():
        act()
        swaps[1].start()

    lists[g][i] = with_swaps
    run_events(lists, plan[2], total_steps(p, w, small_src, small_out, mid, line))
    for f in finishes + [s.finish for s in swaps]:
        f()
    w.drain()


def total_steps(p, w, src, out, mid, line):
    k = [w.new(2) for _ in range(9)]
    now = src
    for i, way in enumerate(("c", "x", "y")):
        w.send(k[i], now, mid.at[i], way)
        yield
        w.land(k[i], mid.at[i])
        nxt = mid.at[3 + i] if i < 2 else line.at[p.z]
        nxt[...] = now[...] + mid[i]
        now = nxt
    for i in range(4):
        lo, hi = jnp.maximum(p.z - i, 0), jnp.minimum(p.z + i, 3)
        if i > 0:
            w.land(k[2 + i], line.at[lo], p.z >= i)
            w.land(k[5 + i], line.at[hi], p.z + i <= 3)
        if i < 3:
            w.send(k[3 + i], line.at[lo], line.at[lo], "z+", jnp.logical_and(p.z >= i, p.z < 3))
            w.send(k[6 + i], line.at[hi], line.at[hi], "z-", jnp.logical_and(p.z + i <= 3, p.z > 0))
            yield
    out[...] = (line[0] + line[1]) + (line[2] + line[3])


def return_grads(kept, small, dec, dx, table, total_units, groups, plan, ident):
    spans = [group_span(table, m) for m in groups]
    bf16 = jnp.bfloat16
    S = jax.ShapeDtypeStruct
    V = pltpu.VMEM
    scratch = [V(v.shape, v.dtype) for v in kept]
    scratch += [V((2, 2, 4, 2, s[3], 128), bf16) for s in spans]
    scratch += [V((2, 4, 2, s[3], 128), bf16) for s in spans]
    scratch += [V((edge_slots(o)[1], s[3], 128), bf16) for s, o in zip(spans, plan[0])]
    scratch += [V((s[1], 512), bf16) for s in spans]
    scratch += [V((4 * max(s[1] for s in spans), 128), jnp.float32), V((FFE, 256), bf16),
                V((5,) + small.shape, small.dtype), V((4,) + small.shape, small.dtype), pltpu.SemaphoreType.DMA((18,)),
                pltpu.SemaphoreType.DMA((len(groups) * (1 + 4 * 14 + 4 * 28) + 24,))]
    vmem = pl.BlockSpec(memory_space=pltpu.VMEM)
    hbm = pl.BlockSpec(memory_space=pl.ANY)
    return pl.pallas_call(
        partial(return_kernel, table, groups, plan),
        out_shape=(S((4, 2, 2, total_units, 512), bf16), S(small.shape, small.dtype), S(dec.shape, dec.dtype), S(dx.shape, dx.dtype)),
        in_specs=[hbm] * 18 + [vmem, hbm, hbm], out_specs=(hbm, vmem, hbm, hbm),
        scratch_shapes=scratch,
        compiler_params=pltpu.CompilerParams(collective_id=ident, has_side_effects=True, vmem_limit_bytes=63 << 20),
        name="return_grads",
    )(*kept, small, dec, dx)


STEP_ROWS = 432


def update_kernel(place_s, place, spread, master, first, second, total, params, norm_first, norm_second,
                  new_master, new_first, new_second, new_norms, new_nf, new_ns):
    i = pl.program_id(0)

    @pl.when(i == 0)
    def _():
        new_norms[...], new_nf[...], new_ns[...] = adamw(params[...], total[...], norm_first[...], norm_second[...], 0.0, NORM_RATE)

    lane = lax.broadcasted_iota(jnp.int32, (16, 256), 1)
    row = lax.broadcasted_iota(jnp.int32, (16, 256), 0)
    for k in range(STEP_ROWS // 16):
        tiles = []
        for j in range(16):
            at = jnp.minimum(place_s[i * STEP_ROWS + 16 * k + j] >> 4, spread.shape[0] // 16 - 1)
            tiles.append(spread[pl.ds(pl.multiple_of(at * 16, 16), 16), :])
        here = slice(16 * k, 16 * k + 16)
        spot = place[here, :]
        used = jnp.logical_and(lane == row * 16 + (spot & 15), spot < spread.shape[0])
        grad = dot(jnp.where(used, 1.0, 0.0).astype(jnp.bfloat16), jnp.concatenate(tiles, axis=0))
        new_master[here, :], new_first[here, :], new_second[here, :] = adamw(
            master[here, :], grad, first[here, :], second[here, :], WEIGHT_DECAY, LEARN_RATE)


def update(place, spread, master, first, second, total, params, norm_first, norm_second):
    slots = master.shape[0]
    S = jax.ShapeDtypeStruct
    rows = pl.BlockSpec((STEP_ROWS, 512), lambda i, s: (i, 0))
    whole = lambda v: pl.BlockSpec(v.shape, lambda i, s: (0, 0), pipeline_mode=pl.Buffered(1))
    small = pl.BlockSpec(params.shape, lambda i, s: (0, 0))
    out = [S(master.shape, jnp.float32)] * 3 + [S(params.shape, jnp.float32)] * 3
    return pl.pallas_call(
        update_kernel, out_shape=out,
        grid_spec=pltpu.PrefetchScalarGridSpec(
            num_scalar_prefetch=1, grid=(slots // STEP_ROWS,),
            in_specs=[pl.BlockSpec((STEP_ROWS, 1), lambda i, s: (i, 0)), whole(spread), rows, rows, rows, small, small, small, small],
            out_specs=[rows] * 3 + [small] * 3),
        compiler_params=pltpu.CompilerParams(vmem_limit_bytes=62 << 20), name="update",
    )(place, lax.optimization_barrier(place)[:, None], spread, master, first, second, total, params, norm_first, norm_second)


def sequence_device(tokens_in, positions, segment_ids, owners, master, first_moment, second_moment, norm_gains,
                    norm_biases, norm_first, norm_second, cotangent):
    shapes = weight_shapes(2)
    table, _, rows = layout(shapes, 16)
    unit, used = own_units(owners, lax.axis_index("dp"), master.shape[0])
    place = jnp.where(used, unit_places(unit, table, 16), 16 * SHARD_UNITS)
    parts = jnp.zeros((16 * SHARD_UNITS, 512), jnp.bfloat16)
    parts = parts.at[place].set(master.astype(jnp.bfloat16), mode="drop", unique_indices=True)
    full, tok, pos, cot = spread_weights(parts.reshape(4, 2, 2, SHARD_UNITS, 512), tokens_in, positions.transpose(1, 0, 2),
                                         cotangent, table, rows, GROUPS, PLAN_OUT, 1)
    kept = chain(tok.reshape(256, DE), pos, segment_ids, norm_gains, norm_biases, cot.reshape(256, DD), full, table)
    decoded, dx0, norms = kept[:3]
    spread_out, norm_total, decoded, dx0 = return_grads(kept[3:], norms, decoded.reshape(2, 128, DD), dx0.reshape(2, 128, DE), table,
                                                        SHARD_UNITS, GROUPS, PLAN_BACK, 2)
    norm_params = jnp.concatenate([norm_gains, norm_biases], axis=0)
    new_master, new_first, new_second, new_norms, norm_one_new, norm_two_new = update(
        place, spread_out.reshape(16 * SHARD_UNITS, 512), master, first_moment, second_moment, norm_total, norm_params, norm_first, norm_second)
    return (decoded, dx0, new_master, new_first, new_second, new_norms, norm_one_new, norm_two_new)


def solution(mesh):
    step = sequence_device if (mesh.shape["dp"], mesh.shape["tensor"]) == (16, 2) else per_device
    return jax.shard_map(
        step,
        mesh=mesh,
        in_specs=(
            P(None, ("dp", "tensor"), None),
            P(None, None, ("dp", "tensor")),
            P(None, "dp", None),
            P(),
            P("dp", "tensor"),
            P("dp", "tensor"),
            P("dp", "tensor"),
            P(),
            P(),
            P(),
            P(),
            P(None, ("dp", "tensor"), None),
        ),
        out_specs=(
            P(None, ("dp", "tensor"), None),
            P(None, ("dp", "tensor"), None),
            P("dp", "tensor"),
            P("dp", "tensor"),
            P("dp", "tensor"),
            P(),
            P(),
            P(),
        ),
        check_vma=False,
    )
```

```python
from functools import partial

import jax
import jax.numpy as jnp
import ml_dtypes
import numpy as np
from jax import lax
from jax.experimental import pallas as pl
from jax.experimental.pallas import tpu as pltpu
from jax.sharding import PartitionSpec as P

DE = 768
HE = 12
HDE = 64
FFE = 3072
DD = 512
HD = 16
HDD = 32
FFD = 2048
STEP = 10


NORM_EPS = 1e-06
BETA_ONE = 0.5
BETA_TWO = 0.5
LEARN_RATE = 0.03
NORM_RATE = 0.3
WEIGHT_DECAY = 0.05
ADAM_EPS = 1e-08
MASK_FILL = -1000000000.0


def sincos_part(coordinate, part_width):
    halfway = part_width // 2
    frequency = 1.0 / 10000.0 ** (jnp.arange(halfway, dtype=jnp.float32) / halfway)
    angles = coordinate.astype(jnp.float32)[:, None] * frequency[None, :]
    return jnp.concatenate([jnp.sin(angles), jnp.cos(angles)], axis=1)


def sincos_embed(positions, model_width):
    side_width = model_width // 16 * 6
    first_width = model_width - 2 * side_width
    return jnp.concatenate(
        [
            sincos_part(positions[0], first_width),
            sincos_part(positions[1], side_width),
            sincos_part(positions[2], side_width),
        ],
        axis=1,
    )


def slot_table(owners, devices, capacity):
    owner_ids = owners[:, 0]
    onehot = (owner_ids[:, None] == jnp.arange(devices, dtype=jnp.int32)[None, :]).astype(jnp.int32)
    before = jnp.cumsum(onehot, axis=0) - onehot
    owner_rank = jnp.sum(before * onehot, axis=1)
    return owner_ids * capacity + owner_rank


def weight_shapes(tensor_count):
    enc_heads = HE // tensor_count
    dec_heads = HD // tensor_count
    return [
        (DE, 3 * enc_heads * HDE),
        (enc_heads * HDE, DE),
        (DE, FFE // tensor_count),
        (FFE // tensor_count, DE),
        (DE, DD // tensor_count),
        (DD, 3 * dec_heads * HDD),
        (dec_heads * HDD, DD),
        (DD, FFD // tensor_count),
        (FFD // tensor_count, DD),
    ]


def split_flat(flat_vector, shapes):
    pieces = []
    offset = 0
    for matrix_shape in shapes:
        length = matrix_shape[0] * matrix_shape[1]
        pieces.append(flat_vector[offset : offset + length].reshape(matrix_shape))
        offset += length
    return pieces


def adamw(weights, gradient, moment_one, moment_two, decay_rate, step_rate):
    one_new = BETA_ONE * moment_one + (1.0 - BETA_ONE) * gradient
    two_new = BETA_TWO * moment_two + (1.0 - BETA_TWO) * gradient * gradient
    one_hat = one_new / (1.0 - BETA_ONE**STEP)
    two_hat = two_new / (1.0 - BETA_TWO**STEP)
    weights_new = weights - step_rate * (
        one_hat / (jnp.sqrt(two_hat) + ADAM_EPS) + decay_rate * weights
    )
    return (weights_new, one_new, two_new)


def norm_forward(values, gain_row, bias_row):
    center = values - jnp.mean(values, axis=-1, keepdims=True)
    spread = jnp.mean(center * center, axis=-1, keepdims=True)
    inverse = lax.rsqrt(spread + NORM_EPS)
    normed = center * inverse
    return (normed * gain_row + bias_row, (normed, inverse))


def norm_backward(upstream, stored, gain_row):
    normed, inverse = stored
    scaled = upstream * gain_row
    mean_one = jnp.mean(scaled, axis=-1, keepdims=True)
    mean_two = jnp.mean(scaled * normed, axis=-1, keepdims=True)
    return (
        inverse * (scaled - mean_one - normed * mean_two),
        jnp.sum(upstream * normed, axis=0),
        jnp.sum(upstream, axis=0),
    )


def inner_rows(left_side, right_side):
    return lax.dot_general(
        left_side, right_side, (((0,), (0,)), ((), ())), preferred_element_type=jnp.float32
    )


def times_transpose(left_side, right_side):
    return lax.dot_general(
        left_side, right_side, (((1,), (1,)), ((), ())), preferred_element_type=jnp.float32
    )


def gather_rows(values):
    return lax.all_gather(values, "tensor", axis=0, tiled=True)


def gather_grads(values):
    return lax.all_gather(values, "tensor", axis=0, tiled=True)


def branch_rows(values, weight):
    return lax.psum_scatter(
        jnp.dot(values, weight, preferred_element_type=jnp.float32).astype(jnp.bfloat16),
        "tensor",
        scatter_dimension=0,
        tiled=True,
    ).astype(jnp.float32)


def input_rows(values, weight):
    return lax.psum_scatter(
        times_transpose(values, weight).astype(jnp.bfloat16),
        "tensor",
        scatter_dimension=0,
        tiled=True,
    ).astype(jnp.float32)


def block_scores(queries, key_rows, mask_bias, block_start, block_rows, head_size):
    scores = jnp.einsum(
        "qhd,khd->hqk", queries, key_rows, preferred_element_type=jnp.float32
    ) * head_size ** (-0.5)
    return scores + mask_bias[None, block_start : block_start + block_rows]


def attention_forward(gathered, w_qkv, head_count, head_size, mask_bias):
    length = gathered.shape[0]
    projected = jnp.dot(gathered, w_qkv, preferred_element_type=jnp.float32).astype(jnp.bfloat16)
    projected = projected.reshape(length, 3, head_count, head_size)
    queries = projected[:, 0]
    key_rows = projected[:, 1]
    value_rows = projected[:, 2]
    block_rows = min(512, length)
    scores = block_scores(queries, key_rows, mask_bias, 0, block_rows, head_size)
    row_peak = jnp.max(scores, axis=-1, keepdims=True)
    row_total = row_peak + jnp.log(jnp.sum(jnp.exp(scores - row_peak), axis=-1, keepdims=True))
    weights = jnp.exp(scores - row_total).astype(jnp.bfloat16)
    outputs = jnp.einsum("hqk,khd->qhd", weights, value_rows, preferred_element_type=jnp.float32)
    totals = [row_total]
    attended = outputs.astype(jnp.bfloat16).reshape(length, head_count * head_size)
    return (attended, (queries, key_rows, value_rows, totals))


def attention_backward(upstream, w_out, attended, stored, head_count, head_size, mask_bias):
    queries, key_rows, value_rows, totals = stored
    length = upstream.shape[0]
    score_scale = head_size ** (-0.5)
    grad_out = inner_rows(attended, upstream)
    attended_grad = (
        times_transpose(upstream, w_out).astype(jnp.bfloat16).reshape(length, head_count, head_size)
    )
    block_rows = min(512, length)
    key_grads = jnp.zeros((length, head_count, head_size), jnp.float32)
    value_grads = jnp.zeros((length, head_count, head_size), jnp.float32)
    query_grads = []
    for number, block_start in enumerate(range(0, length, block_rows)):
        scores = block_scores(queries, key_rows, mask_bias, block_start, block_rows, head_size)
        weights = jnp.exp(scores - totals[number])
        value_grads = jnp.einsum(
            "hqk,qhd->khd",
            weights.astype(jnp.bfloat16),
            attended_grad,
            preferred_element_type=jnp.float32,
        )
        weight_grads = jnp.einsum(
            "qhd,khd->hqk", attended_grad, value_rows, preferred_element_type=jnp.float32
        )
        score_grads = (
            weights * (weight_grads - jnp.sum(weights * weight_grads, axis=-1, keepdims=True))
        ).astype(jnp.bfloat16)
        query_grads.append(
            jnp.einsum("hqk,khd->qhd", score_grads, key_rows, preferred_element_type=jnp.float32)
            * score_scale
        )
        key_grads = (
            jnp.einsum("hqk,qhd->khd", score_grads, queries, preferred_element_type=jnp.float32)
            * score_scale
        )
    projected_grad = jnp.stack([query_grads[0], key_grads, value_grads], axis=1)
    return (
        projected_grad.astype(jnp.bfloat16).reshape(length, 3 * head_count * head_size),
        grad_out,
    )


def block_forward(residual, matrices, gain_rows, bias_rows, head_count, head_size, mask_bias):
    w_qkv, w_out, w_in, w_down = matrices
    normed, norm_one = norm_forward(residual, gain_rows[0], bias_rows[0])
    gathered = gather_rows(normed.astype(jnp.bfloat16))
    attended, stored = attention_forward(gathered, w_qkv, head_count, head_size, mask_bias)
    middle = residual + branch_rows(attended, w_out)
    normed_two, norm_two = norm_forward(middle, gain_rows[1], bias_rows[1])
    gathered_two = gather_rows(normed_two.astype(jnp.bfloat16))
    hidden = jnp.dot(gathered_two, w_in, preferred_element_type=jnp.float32)
    active = jax.nn.gelu(hidden, approximate=False).astype(jnp.bfloat16)
    result = middle + branch_rows(active, w_down)
    return (result, (gathered, norm_one, attended, stored, gathered_two, norm_two, hidden, active))


def block_backward(upstream, matrices, gain_rows, saved_values, head_count, head_size, mask_bias):
    w_qkv, w_out, w_in, w_down = matrices
    gathered, norm_one, attended, stored, gathered_two, norm_two, hidden, active = saved_values
    down_full = gather_grads(upstream.astype(jnp.bfloat16))
    grad_down = inner_rows(active, down_full)
    active_grad = times_transpose(down_full, w_down)
    gelu_pull = jax.vjp(partial(jax.nn.gelu, approximate=False), hidden)[1]
    hidden_grad = gelu_pull(active_grad)[0].astype(jnp.bfloat16)
    grad_in = inner_rows(gathered_two, hidden_grad)
    normed_two_grad = input_rows(hidden_grad, w_in)
    middle_grad, gain_two, bias_two = norm_backward(normed_two_grad, norm_two, gain_rows[1])
    middle_grad = upstream + middle_grad
    middle_full = gather_grads(middle_grad.astype(jnp.bfloat16))
    projected_grad, grad_out = attention_backward(
        middle_full, w_out, attended, stored, head_count, head_size, mask_bias
    )
    grad_qkv = inner_rows(gathered, projected_grad)
    normed_grad = input_rows(projected_grad, w_qkv)
    input_grad, gain_one, bias_one = norm_backward(normed_grad, norm_one, gain_rows[0])
    return (
        middle_grad + input_grad,
        [grad_qkv, grad_out, grad_in, grad_down],
        (gain_one, gain_two, bias_one, bias_two),
    )


def embed_forward(residual, w_embed):
    residual_low = gather_rows(residual.astype(jnp.bfloat16))
    columns = jnp.dot(residual_low, w_embed, preferred_element_type=jnp.float32).astype(
        jnp.bfloat16
    )
    own_columns = lax.all_to_all(columns, "tensor", split_axis=0, concat_axis=1, tiled=True)
    return (own_columns.astype(jnp.float32), residual_low)


def embed_backward(upstream, residual_low, w_embed):
    columns = lax.all_to_all(
        upstream.astype(jnp.bfloat16), "tensor", split_axis=1, concat_axis=0, tiled=True
    )
    grad_embed = inner_rows(residual_low, columns)
    return (input_rows(columns, w_embed), grad_embed)


def slot_builder(gradients, unit_of_slot, unit_width):
    flat_units = jnp.concatenate([gradient.reshape(-1) for gradient in gradients]).reshape(
        -1, unit_width
    )
    unit_total = flat_units.shape[0]
    source = jnp.take(flat_units, jnp.clip(unit_of_slot, 0, unit_total - 1), axis=0)
    return jnp.where((unit_of_slot >= 0)[:, None], source, 0.0)


def per_device(
    tokens_in,
    positions,
    segment_ids,
    owners,
    master,
    first_moment,
    second_moment,
    norm_gains,
    norm_biases,
    norm_first,
    norm_second,
    cotangent,
):
    devices = lax.axis_size("dp")
    tensor_count = lax.axis_size("tensor")
    capacity = master.shape[0]
    unit_width = master.shape[1]
    unit_count = owners.shape[0]
    slot_index = slot_table(owners, devices, capacity)
    unit_of_slot = (
        jnp.full((devices * capacity,), -1, jnp.int32)
        .at[slot_index]
        .set(jnp.arange(unit_count, dtype=jnp.int32))
    )
    targets = unit_of_slot
    targets = jnp.where(targets < 0, unit_count, targets)
    placed = (
        jnp.zeros((unit_count, unit_width), jnp.bfloat16)
        .at[targets]
        .set(lax.all_gather(master.astype(jnp.bfloat16), "dp", axis=0, tiled=True), mode="drop")
    )
    shapes = weight_shapes(tensor_count)
    matrices = split_flat(placed.reshape(-1), shapes)
    encoder = matrices[0:4]
    w_embed = matrices[4]
    decoder = matrices[5:9]
    enc_heads = HE // tensor_count
    dec_heads = HD // tensor_count
    micro_count = tokens_in.shape[0]
    grad_sums = [jnp.zeros(matrix_shape, jnp.float32) for matrix_shape in shapes]
    norm_sums = jnp.zeros((4, DE + DD), jnp.float32)
    decoded_rows = []
    token_grads = []
    for micro_step in range(micro_count):
        tile_ids = segment_ids[micro_step, 0]
        mask_bias = jnp.where(tile_ids[:, None] == tile_ids[None, :], 0.0, MASK_FILL).astype(
            jnp.float32
        )
        position_now = positions[:, micro_step]
        residual = tokens_in[micro_step].astype(jnp.float32) + sincos_embed(position_now, DE)
        residual, enc_saved = block_forward(
            residual, encoder, norm_gains[:, :DE], norm_biases[:, :DE], enc_heads, HDE, mask_bias
        )
        residual, embed_low = embed_forward(residual, w_embed)
        residual = residual + sincos_embed(position_now, DD)
        residual, dec_saved = block_forward(
            residual, decoder, norm_gains[:, DE:], norm_biases[:, DE:], dec_heads, HDD, mask_bias
        )
        decoded_rows.append(residual)
        upstream, dec_grads, dec_norm = block_backward(
            cotangent[micro_step], decoder, norm_gains[:, DE:], dec_saved, dec_heads, HDD, mask_bias
        )
        upstream, grad_embed = embed_backward(upstream, embed_low, w_embed)
        upstream, enc_grads, enc_norm = block_backward(
            upstream, encoder, norm_gains[:, :DE], enc_saved, enc_heads, HDE, mask_bias
        )
        token_grads.append(upstream)
        step_grads = enc_grads + [grad_embed] + dec_grads
        step_norm = jnp.concatenate([jnp.stack(enc_norm), jnp.stack(dec_norm)], axis=1)
        grad_sums = [total_grad + new_grad for total_grad, new_grad in zip(grad_sums, step_grads)]
        norm_sums = norm_sums + step_norm
    reduced = lax.psum_scatter(
        slot_builder(grad_sums, unit_of_slot, unit_width), "dp", scatter_dimension=0, tiled=True
    )
    norm_total = lax.psum(norm_sums, ("dp", "tensor"))
    new_master, new_first, new_second = adamw(
        master, reduced, first_moment, second_moment, WEIGHT_DECAY, LEARN_RATE
    )
    norm_params = jnp.concatenate([norm_gains, norm_biases], axis=0)
    new_norms, norm_one_new, norm_two_new = adamw(
        norm_params, norm_total, norm_first, norm_second, 0.0, NORM_RATE
    )
    return (
        jnp.stack(decoded_rows),
        jnp.stack(token_grads),
        new_master,
        new_first,
        new_second,
        new_norms,
        norm_one_new,
        norm_two_new,
    )


MESH = pl.DeviceIdType.MESH
ALL = slice(None)


class Place:
    def __init__(self):
        self.d = lax.axis_index("dp")
        self.x = lax.axis_index("tensor")
        self.z = self.d // 4
        self.y = (self.d // 2) % 2
        self.c = self.d % 2
        self.ids = {
            "c": (self.d + 1 - 2 * self.c, self.x),
            "y": (self.d + 2 - 4 * self.y, self.x),
            "x": (self.d, 1 - self.x),
            "z+": (self.d + 4, self.x),
            "z-": (self.d - 4, self.x),
        }

    def greet(self, kinds):
        bar = pltpu.get_barrier_semaphore()
        for k in kinds:
            pl.semaphore_signal(bar, inc=1, device_id=self.ids[k], device_id_type=MESH)

        @pl.when(self.z < 3)
        def _():
            pl.semaphore_signal(bar, inc=1, device_id=self.ids["z+"], device_id_type=MESH)

        @pl.when(self.z > 0)
        def _():
            pl.semaphore_signal(bar, inc=1, device_id=self.ids["z-"], device_id_type=MESH)

        inner = jnp.where(jnp.logical_and(self.z > 0, self.z < 3), 1, 0)
        pl.semaphore_wait(bar, len(kinds) + 1 + inner)

    def there(self, disp):
        dz = disp[0]
        if dz == 0:
            return None
        return self.z + dz <= 3 if dz > 0 else self.z + dz >= 0

    def at(self, disp):
        dz, fy, fx = disp
        return (1 - self.x if fx else self.x, self.z + dz, 1 - self.y if fy else self.y)


def when(cond, f):
    if cond is None:
        f()
    else:
        pl.when(cond)(f)


def both(a, b):
    if a is None:
        return b
    if b is None:
        return a
    return jnp.logical_and(a, b)


def spread(order):
    out = {}
    todo = [((0, 0, 0), -1, 0)]
    while todo:
        (dz, fy, fx), last, way = todo.pop(0)
        nxt = []
        for i, a in enumerate(order):
            if i < last:
                continue
            if a == "z":
                for s in (1, -1):
                    if i == last and s != way:
                        continue
                    n = (dz - s, fy, fx)
                    if abs(n[0]) <= 3:
                        nxt.append((n, "z+" if s > 0 else "z-", i, s))
            elif i > last:
                n = (dz, 1, fx) if a == "y" else (dz, fy, 1)
                nxt.append((n, a, i, 0))
        out[(dz, fy, fx)] = [(n, w) for n, w, _, _ in nxt]
        todo += [(n, i, s) for n, _, i, s in nxt]
    return out


def hops(d):
    return abs(d[0]) + d[1] + d[2]


BACK = {"z+": "z-", "z-": "z+", "x": "x", "y": "y"}


def add_rows(acc, got, step=80):
    n = acc.shape[0]
    while n % step:
        step -= 16

    def body(i, _):
        r = pl.ds(pl.multiple_of(i * step, step), step)
        acc[r, :] = acc[r, :] + got[r, :]
        return 0

    lax.fori_loop(0, n // step, body, 0)


SHARD_UNITS = 656
PANEL = 128
GROUPS = ((0, 1), (2,), (3,), (4, 5, 6), (7, 8))

PLAN_OUT = (
    ("zy", "zy", "yz", "yz", "yz"),
    ("zxy", "yzx", "zyx", "yzx", "xzy"),
    (
        128, 129, 0, 4, 131, 130, 132, 8, 134, 64, 135, 133, 1, 9, 2, 68, 69, 5, 138, 137, 73, 256, 6, 136, 3, 192,
        65, 140, 141, 66, 139, 7, 72, 10, 142, 143, 70, 12, 13, 67, 11, 147, 146, 144, 76, 71, 148, 74, 154, 14, 15,
        75, 77, 16, 193, 257, 162, 258, 19, 78, 194, 79, 320, 259, 168, 260, 196, 26, 197, 261, 20, 156, 80, 83, 82,
        262, 265, 198, 170, 155, 27, 145, 17, 151, 32, 84, 264, 86, 34, 200, 24, 157, 163, 266, 22, 90, 195, 28, 89,
        160, 40, 29, 268, 202, 36, 201, 152, 85, 88, 263, 91, 21, 93, 269, 97, 199, 267, 92, 35, 33, 25, 104, 205, 81,
        204, 203, 39, 270, 271, 167, 150, 206, 207, 23, 272, 31, 273, 101, 276, 37, 98, 210, 41, 100, 38, 42, 275,
        278, 103, 18, 211, 161, 96, 149, 165, 30, 95, 164, 280, 208, 277, 321, 215, 322, 102, 282, 153, 212, 323, 290,
        283, 94, 217, 106, 169, 279, 285, 209, 324, 87, 105, 158, 218, 216, 288, 289, 166, 99, 214, 159, 325, 225,
        284, 219, 326, 226, 220, 292, 327, 227, 221, 291, 224, 213, 294, 295, 328, 230, 296, 228, 293, 281, 274, 232,
        287, 223, 286, 329, 231, 222, 298, 297, 330, 233, 229, 234,
    ),
)
PLAN_BACK = (
    ("zxy", "yzx", "zyx", "yzx", "xzy"),
    ("zy", "zy", "zy", "yz", "yz"),
    (
        256, 257, 258, 262, 261, 269, 64, 259, 67, 260, 65, 69, 263, 66, 78, 264, 271, 278, 276, 77, 270, 268, 267,
        71, 70, 275, 282, 85, 72, 266, 76, 265, 192, 82, 68, 199, 277, 73, 0, 84, 274, 74, 272, 5, 273, 80, 75, 279,
        6, 79, 13, 128, 204, 1, 281, 2, 12, 89, 283, 280, 11, 141, 129, 19, 8, 83, 4, 195, 86, 193, 87, 3, 134, 15, 7,
        81, 284, 285, 133, 88, 91, 14, 10, 197, 194, 90, 22, 196, 132, 286, 131, 201, 288, 287, 130, 16, 18, 21, 198,
        9, 92, 20, 205, 93, 291, 202, 200, 290, 136, 289, 143, 292, 26, 140, 208, 150, 206, 17, 94, 23, 135, 25, 212,
        213, 294, 95, 142, 203, 96, 24, 138, 148, 139, 207, 137, 211, 27, 214, 210, 100, 97, 295, 144, 215, 149, 104,
        146, 209, 147, 28, 29, 151, 218, 219, 217, 145, 154, 32, 101, 153, 106, 30, 216, 36, 155, 152, 296, 33, 220,
        105, 221, 293, 98, 156, 40, 157, 224, 31, 103, 298, 222, 160, 158, 223, 164, 102, 99, 228, 37, 161, 227, 165,
        41, 225, 168, 159, 226, 35, 42, 34, 229, 163, 297, 39, 231, 230, 232, 162, 167, 170, 234, 38, 166, 169, 233,
    ),
)


def layout(shapes, shards):
    table = []
    unit_at, row_at, flat_at = 0, 0, 0
    starts = [g[0] for g in GROUPS]
    for i, (rows, cols) in enumerate(shapes):
        if i in starts:
            unit_at = -(-unit_at // 16) * 16
        rb, panels = rows // shards, cols // PANEL
        units = rb * cols // 512
        padded = -(-rb // 16) * 16
        table.append((rb, panels, units, unit_at, row_at, padded, flat_at))
        unit_at += units
        row_at += padded * panels
        flat_at += units * shards
    return table, unit_at, row_at


def unit_places(units, table, shards):
    place = jnp.zeros_like(units)
    for _, _, n, first, _, _, lo in table:
        v = units - lo
        here = (v // n) * SHARD_UNITS + first + v % n
        place = jnp.where(v >= 0, here, place)
    return place


def own_units(owners, mine, capacity):
    count = owners.shape[0] // 128
    hit = (owners[:, 0] == mine).reshape(count, 128)
    lane = jnp.arange(128)
    tri = (lane[:, None] <= lane[None, :]).astype(jnp.bfloat16)
    within = jnp.dot(hit.astype(jnp.bfloat16), tri, preferred_element_type=jnp.float32)
    totals = within[:, 127].astype(jnp.int32)
    upto = jnp.sum(jnp.where(jnp.arange(count)[:, None] >= jnp.arange(count)[None, :], totals[None, :], 0), axis=1)
    slot = jnp.arange(capacity, dtype=jnp.int32)
    block = jnp.sum((upto[None, :] <= slot[:, None]).astype(jnp.int32), axis=1)
    pick = block[:, None] == jnp.arange(count)[None, :]
    before = jnp.sum(jnp.where(pick, (upto - totals)[None, :], 0), axis=1)
    row = jnp.dot(pick.astype(jnp.bfloat16), within.astype(jnp.bfloat16), preferred_element_type=jnp.float32)
    rank = (slot - before).astype(jnp.float32)
    at = jnp.sum((row <= rank[:, None]).astype(jnp.int32), axis=1)
    return block * 128 + at, slot < upto[count - 1]


BY_ROWS = (1, 3, 6, 8)


def position_table():
    cols = []
    for width in (DE, DD):
        side = width // 16 * 6
        parts = (width - 2 * side, side, side)
        tab = np.zeros((48, width), np.float64)
        col = 0
        for i, n in enumerate(parts):
            half = n // 2
            freq = 1.0 / 10000.0 ** (np.arange(half) / half)
            ang = np.arange(16)[:, None] * freq[None, :]
            tab[16 * i:16 * i + 16, col:col + n] = np.concatenate([np.sin(ang), np.cos(ang)], axis=1)
            col += n
        cols.append(tab)
    left = np.concatenate(cols, axis=1).astype(np.float32)
    terms = []
    for _ in range(3):
        terms.append(left.astype(ml_dtypes.bfloat16))
        left = left - terms[-1].astype(np.float32)
    return np.stack(terms)


def dot(a, b):
    return jnp.dot(a, b, preferred_element_type=jnp.float32)


def dot_nt(a, b):
    return lax.dot_general(a, b, (((1,), (1,)), ((), ())), preferred_element_type=jnp.float32)


def dot_tn(a, b):
    return lax.dot_general(a, b, (((0,), (0,)), ((), ())), preferred_element_type=jnp.float32)


def lanes(i, n=128):
    return pl.ds(pl.multiple_of(i * n, n), n)


def ln_parts(x):
    c = x - jnp.mean(x, axis=-1, keepdims=True)
    inv = lax.rsqrt(jnp.mean(c * c, axis=-1, keepdims=True) + NORM_EPS)
    return c * inv, inv


def ln_back(up, m, inv, gain):
    s = up * gain
    a = jnp.mean(s, axis=-1, keepdims=True)
    b = jnp.mean(s * m, axis=-1, keepdims=True)
    return inv * (s - a - m * b), jnp.sum(up * m, axis=0, keepdims=True), jnp.sum(up, axis=0, keepdims=True)


class Block:
    def __init__(self, width, heads, size, hidden, first, table, col):
        self.width, self.heads, self.size, self.hidden, self.col = width, heads, size, hidden, col
        self.q, self.o, self.a, self.b = table[first:first + 4]
        self.part = heads // 2 * size
        self.per = 128 // size


def panel(w, t, mat, g, lo=0, num=16):
    rb, _, _, _, at, padded, _ = mat
    rows = pl.ds(pl.multiple_of(at + g * padded, 16), padded)
    v = w[t, lo:lo + num, rows, :] if isinstance(lo, int) else w[t, pl.ds(lo, num), rows, :]
    if padded > rb:
        v = v.astype(jnp.float32)[:, :rb].reshape(num * rb, 128).astype(jnp.bfloat16)
        return v
    return v.reshape(num * rb, 128)


def pair(w, mat, g):
    return jnp.concatenate([panel(w, 0, mat, g), panel(w, 1, mat, g)], axis=1)


def repeat(count, step, f):
    step = max(k for k in range(1, step + 1) if count % k == 0)

    def turn(i, _):
        for k in range(step):
            f(i * step + k)
        return 0

    if step == count:
        turn(0, 0)
    else:
        lax.fori_loop(0, count // step, turn, 0)


def pull(acc, up, w, mat, step):
    count = mat[1]
    step = max(k for k in range(1, step + 1) if count % k == 0)

    def part(i):
        gs = [i * step + k for k in range(step)]
        d = jnp.concatenate([up[:, lanes(o + g)] for g in gs for o in (0, count)], axis=1)
        return dot_nt(d, jnp.concatenate([pair(w, mat, g) for g in gs], axis=1))

    acc[...] = part(0)

    def turn(i, _):
        acc[...] += part(i)
        return 0

    lax.fori_loop(1, count // step, turn, 0)


def block_fwd(b, x, xo, w, gains, biases, same, n1, proj, p, att, ow, m1, i1, n2, m2, i2, act, slope,
              need, keep):
    cols = slice(b.col, b.col + b.width)
    m, inv = ln_parts(x[...])
    m1[...] = m
    i1[...] = jnp.broadcast_to(inv, i1.shape)
    n1[...] = (m * gains[0:1, cols] + biases[0:1, cols]).astype(jnp.bfloat16)
    keep(0)
    yield
    need(0)
    gq = b.q[1]

    def qkv(g):
        r = dot(n1[...], pair(w, b.q, g)).astype(jnp.bfloat16)
        proj[:, lanes(g)] = r[:, :128]
        proj[:, lanes(gq + g)] = r[:, 128:]

    repeat(gq, 9, qkv)
    yield
    np_ = b.part // 128
    lane = lax.broadcasted_iota(jnp.int32, (256, 128), 1)
    masks = [lane // b.size == i for i in range(b.per)]

    def heads(i, _):
        t, j = i // np_, i % np_
        q = proj[:, lanes(t * gq + j)]
        k = proj[:, lanes(t * gq + np_ + j)]
        v = proj[:, lanes(t * gq + 2 * np_ + j)]
        total = jnp.zeros((256, 128), jnp.float32)
        for h in range(b.per):
            z = dot_nt(jnp.where(masks[h], q, 0), k) * b.size ** (-0.5) + same
            e = jnp.exp(z - jnp.max(z, axis=-1, keepdims=True))
            s = e * (1.0 / jnp.sum(e, axis=-1, keepdims=True))
            p[i * b.per + h] = s
            total = total + dot(s.astype(jnp.bfloat16), jnp.where(masks[h], v, 0))
        att[:, lanes(i)] = total.astype(jnp.bfloat16)
        return 0

    lax.fori_loop(0, np_, heads, 0)
    yield
    lax.fori_loop(np_, 2 * np_, heads, 0)
    keep(1)
    yield
    need(1)
    for t in range(2):
        for g in range(b.width // 128):
            ow[t, :, g * 128:(g + 1) * 128] = panel(w, t, b.o, g)
    x1 = x[...] + dot(att[:, :b.part], ow[0]) + dot(att[:, b.part:], ow[1])
    xo[...] = x1
    m, inv = ln_parts(x1)
    m2[...] = m
    i2[...] = jnp.broadcast_to(inv, i2.shape)
    n2[...] = (m * gains[1:2, cols] + biases[1:2, cols]).astype(jnp.bfloat16)
    keep(2)
    yield
    need(2)
    ga = b.a[1]

    def up(g):
        h = dot(n2[...], pair(w, b.a, g))
        big = 0.5 * (1.0 + lax.erf(h * 0.7071067811865476))
        act_v = (h * big).astype(jnp.bfloat16)
        dens = big + h * (0.3989422804014327 * jnp.exp(-0.5 * h * h))
        act[:, lanes(g)] = act_v[:, :128]
        act[:, lanes(ga + g)] = act_v[:, 128:]
        slope[:, lanes(g)] = dens[:, :128]
        slope[:, lanes(ga + g)] = dens[:, 128:]

    repeat(ga, 12, up)
    keep(3)
    yield
    need(3)
    half = b.hidden // 2

    def down(g):
        w0 = jnp.concatenate([panel(w, 0, b.b, 2 * g), panel(w, 0, b.b, 2 * g + 1)], axis=1)
        w1 = jnp.concatenate([panel(w, 1, b.b, 2 * g), panel(w, 1, b.b, 2 * g + 1)], axis=1)
        xo[:, lanes(g, 256)] += dot(act[:, :half], w0) + dot(act[:, half:], w1)

    repeat(b.width // 256, 1, down)


def block_bwd(b, dr, w, gains, same, n1, proj, p, att, ow, m1, i1, n2, m2, i2, act, slope,
              r, dh, r1, dp_out, acc, da, norm_out, keep):
    cols = slice(b.col, b.col + b.width)
    r[...] = dr[...].astype(jnp.bfloat16)
    keep(3)
    half = b.hidden // 2
    rb = b.b[0]
    gb = b.width // 128
    num = 16

    def hidden(i, _):
        t, lo = i // (16 // num), (i % (16 // num)) * num
        wc = jnp.concatenate([panel(w, t, b.b, g, lo, num) for g in range(gb)], axis=1)
        at = lanes(i, num * rb)
        dh[:, at] = (dot_nt(r[...], wc) * slope[:, at]).astype(jnp.bfloat16)
        return 0

    lax.fori_loop(0, 2 * (16 // num), hidden, 0)
    keep(2)
    ga = b.a[1]
    pull(acc, dh, w, b.a, 12)
    dx, dg, db = ln_back(acc[...], m2[...], i2[:, :1], gains[1:2, cols])
    norm_out[1:2, cols] = dg
    norm_out[3:4, cols] = db
    dx1 = dr[...] + dx
    dr[...] = dx1
    r1[...] = dx1.astype(jnp.bfloat16)
    keep(1)
    for t in range(2):
        da[:, t * b.part:(t + 1) * b.part] = dot_nt(r1[...], ow[t]).astype(jnp.bfloat16)
    gq = b.q[1]
    np_ = b.part // 128
    lane = lax.broadcasted_iota(jnp.int32, (256, 128), 1)
    masks = [lane // b.size == i for i in range(b.per)]
    scale = b.size ** (-0.5)

    def heads(i, _):
        t, j = i // np_, i % np_
        q = proj[:, lanes(t * gq + j)]
        k = proj[:, lanes(t * gq + np_ + j)]
        v = proj[:, lanes(t * gq + 2 * np_ + j)]
        up_ = da[:, lanes(i)]
        dq = jnp.zeros((256, 128), jnp.float32)
        dk = jnp.zeros((256, 128), jnp.float32)
        dv = jnp.zeros((256, 128), jnp.float32)
        for h in range(b.per):
            s = p[i * b.per + h]
            u = jnp.where(masks[h], up_, 0)
            dp = dot_nt(u, v)
            dv = dv + dot_tn(s.astype(jnp.bfloat16), u)
            t1 = s * dp
            dz = (t1 - s * jnp.sum(t1, axis=-1, keepdims=True)).astype(jnp.bfloat16)
            dq = dq + dot(dz, jnp.where(masks[h], k, 0))
            dk = dk + dot_tn(dz, jnp.where(masks[h], q, 0))
        dp_out[:, lanes(t * gq + j)] = (dq * scale).astype(jnp.bfloat16)
        dp_out[:, lanes(t * gq + np_ + j)] = (dk * scale).astype(jnp.bfloat16)
        dp_out[:, lanes(t * gq + 2 * np_ + j)] = dv.astype(jnp.bfloat16)
        return 0

    lax.fori_loop(0, 2 * np_, heads, 0)
    keep(0)
    pull(acc, dp_out, w, b.q, 9)
    dx, dg, db = ln_back(acc[...], m1[...], i1[:, :1], gains[0:1, cols])
    norm_out[0:1, cols] = dg
    norm_out[2:3, cols] = db
    dr[...] = dr[...] + dx


ACTS = (DE, DE, DE, FFE, DE, DD, DD, DD, FFD)
GRADS = (3 * DE, DE, FFE, DE, DD, 3 * DD, DD, FFD, DD)


def lookup(pos, tab, cols):
    row = lax.broadcasted_iota(jnp.int32, (48, 256), 0)
    spots = [jnp.concatenate([pos[0, i:i + 1, :], pos[1, i:i + 1, :]], axis=1) for i in range(3)]
    hot = jnp.logical_or(jnp.logical_or(row == spots[0], row == spots[1] + 16), row == spots[2] + 32)
    hot = jnp.where(hot, 1.0, 0.0).astype(jnp.bfloat16)
    return sum(dot_tn(hot, tab[i, :, cols]) for i in range(3))


def tile_mask(tile):
    ids = tile[lax.axis_index("tensor")]
    tiles = jnp.where(lax.broadcasted_iota(jnp.int32, (16, 256), 0) == ids, 1.0, 0.0).astype(jnp.bfloat16)
    return (1.0 - dot_tn(tiles, tiles)) * MASK_FILL


FWD_ACTS = [((256, n), jnp.bfloat16) for n in (DE, DE, DE, FFE)]
FWD_KEPT = [((256, 3 * DE), jnp.bfloat16), ((HE, 256, 256), jnp.float32), ((2, DE // 2, DE), jnp.bfloat16),
            ((256, DE), jnp.float32), ((256, 128), jnp.float32), ((256, DE), jnp.float32), ((256, 128), jnp.float32),
            ((256, FFE), jnp.float32)]


def chain_kernel(table, pos, tile, gains, biases, cot, tab, x2, w_hbm, *refs):
    fwd_hbm, refs = refs[:8], refs[8:]
    dec, dx0, norm_out = refs[:3]
    kept_out = refs[3:17]
    kept = refs[17:31]
    low, n1d, ad, n2d, ud, dpe, r1e, dhe, re, dlow, dpd, r1d, dhd, rd = kept
    fwd, refs = refs[31:39], refs[39:]
    proj_e, pe, ow_e, m1e, i1e, m2e, i2e, se = fwd
    (w, pd, sd, proj_d, da_e, da_d, ow_d, m1d, m2d, i1d, i2d, y, acc_e, acc_d, w_sem, f_sem, out_sem) = refs
    enc_b = Block(DE, HE, HDE, FFE, 0, table, 0)
    dec_b = Block(DD, HD, HDD, FFD, 5, table, DE)
    em = table[4]

    def load(m):
        rows = pl.ds(table[m][4], table[m][1] * table[m][5])
        return pltpu.make_async_copy(w_hbm.at[:, :, rows], w.at[:, :, rows], w_sem.at[m])

    def fetch(i):
        return pltpu.make_async_copy(fwd_hbm[i], fwd[i], f_sem.at[i])

    def store(i):
        return pltpu.make_async_copy(kept[i], kept_out[i], out_sem.at[i])

    for m in (4, 5, 6, 7, 8, 3, 2, 1, 0):
        if m != 1:
            load(m).start()
    for i in range(8):
        fetch(i).start()
    same = tile_mask(tile)
    low[...] = x2[...].astype(jnp.bfloat16)
    store(0).start()
    load(4).wait()
    for g in range(2):
        v = dot(low[...], pair(w, em, g)).astype(jnp.bfloat16).astype(jnp.float32)
        y[:, g * 128:(g + 1) * 128] = v[:, :128]
        y[:, 256 + g * 128:256 + (g + 1) * 128] = v[:, 128:]
    y[...] += lookup(pos, tab, slice(DE, DE + DD))
    for _ in block_fwd(dec_b, y, dec, w, gains, biases, same, n1d, proj_d, pd, ad, ow_d, m1d, i1d, n2d, m2d, i2d, ud, sd,
                       lambda k: load(5 + k).wait(), lambda k: store(1 + k).start()):
        pass
    y[...] = cot[...]
    block_bwd(dec_b, y, w, gains, same, n1d, proj_d, pd, ad, ow_d, m1d, i1d, n2d, m2d, i2d, ud, sd,
              rd, dhd, r1d, dpd, acc_d, da_d, norm_out, lambda k: store(10 + k).start())
    dlow[...] = y[...].astype(jnp.bfloat16)
    store(9).start()
    for g in range(2):
        d = jnp.concatenate([dlow[:, g * 128:(g + 1) * 128], dlow[:, 256 + g * 128:256 + (g + 1) * 128]], axis=1)
        v = dot_nt(d, pair(w, em, g))
        if g == 0:
            dx0[...] = v
        else:
            dx0[...] += v
    for m in (3, 2, 0):
        load(m).wait()
    for i in range(8):
        fetch(i).wait()
    block_bwd(enc_b, dx0, w, gains, same, None, proj_e, pe, None, ow_e, m1e, i1e, None, m2e, i2e, None, se,
              re, dhe, r1e, dpe, acc_e, da_e, norm_out, lambda k: store(5 + k).start())
    for i in range(14):
        store(i).wait()


def chain(pos, tile, gains, biases, cot, full, x2, fwd, table):
    f32, bf16 = jnp.float32, jnp.bfloat16
    S = jax.ShapeDtypeStruct
    outs = [S((256, DD), f32), S((256, DE), f32), S((4, DE + DD), f32)]
    kept = [(256, n) for n in ACTS[4:] + GRADS]
    outs += [S(k, bf16) for k in kept]
    V = pltpu.VMEM
    scratch = [V(k, bf16) for k in kept] + [V(k, t) for k, t in FWD_KEPT] + [
        V((2, 16) + full.shape[-2:], bf16), V((HD, 256, 256), f32), V((256, FFD), f32),
        V((256, 3 * DD), bf16), V((256, DE), bf16), V((256, DD), bf16), V((2, DD // 2, DD), bf16),
        V((256, DD), f32), V((256, DD), f32), V((256, 128), f32), V((256, 128), f32),
        V((256, DD), f32), V((256, DE), f32), V((256, DD), f32),
        pltpu.SemaphoreType.DMA((9,)), pltpu.SemaphoreType.DMA((8,)), pltpu.SemaphoreType.DMA((14,))]
    vmem = pl.BlockSpec(memory_space=pltpu.VMEM)
    hbm = pl.BlockSpec(memory_space=pl.ANY)
    args = (pos, tile, gains, biases, cot, jnp.asarray(position_table()), x2,
            full.reshape(2, 16, full.shape[-2], 128), *fwd)
    return pl.pallas_call(
        partial(chain_kernel, table), out_shape=outs, in_specs=[vmem] * 7 + [hbm] * 9, out_specs=[vmem] * 3 + [hbm] * 14,
        scratch_shapes=scratch, compiler_params=pltpu.CompilerParams(vmem_limit_bytes=63 << 20), name="chain",
        cost_estimate=pl.CostEstimate(flops=8_000_000_000, bytes_accessed=40_000_000, transcendentals=3_000_000),
    )(*args)


def grad_panels(table, m, act, grad, turned, put):
    mat = table[m]
    rb, panels, padded = mat[0], mat[1], mat[5]
    count = act.shape[1]

    def turn(i):
        turned[pl.ds(pl.multiple_of(i * 128, 128), 128), :] = act[:, lanes(i)].T

    repeat(count // 128, 6, turn)

    def place(t, g, v):
        if padded > rb:
            v = v.reshape(16, rb, 128)
            v = jnp.concatenate([v, jnp.zeros((16, padded - rb, 128), jnp.float32)], axis=1).astype(jnp.bfloat16)
        else:
            v = v.astype(jnp.bfloat16).reshape(16, rb, 128)
        put(t, g, v)

    if m in BY_ROWS:
        half = count // 2

        def body(i):
            t, g = i // (panels // 2), i % (panels // 2)
            v = dot(turned[pl.ds(pl.multiple_of(t * half, 128), half), :], grad[:, lanes(g, 256)])
            place(t, 2 * g, v[:, :128])
            place(t, 2 * g + 1, v[:, 128:])

        repeat(panels, 6, body)
    else:
        def body(g):
            d = jnp.concatenate([grad[:, lanes(g)], grad[:, lanes(panels + g)]], axis=1)
            v = dot(turned[:count, :], d)
            place(0, g, v[:, :128])
            place(1, g, v[:, 128:])

        repeat(panels, 6, body)


class Wires:
    def __init__(self, place, sem):
        self.place, self.sem, self.used, self.waits = place, sem, 0, []

    def new(self, n=1):
        self.used += n
        assert self.used <= self.sem.shape[0], self.used
        return self.used - n

    def copy(self, k, src, dst, way):
        return pltpu.make_async_remote_copy(src_ref=src, dst_ref=dst, send_sem=self.sem.at[k], recv_sem=self.sem.at[k + 1],
                                            device_id=self.place.ids[way], device_id_type=MESH)

    def send(self, k, src, dst, way, cond=None):
        cp = self.copy(k, src, dst, way)
        when(cond, cp.start)
        self.waits.append((cond, cp))

    def land(self, k, dst, cond=None):
        when(cond, self.copy(k, dst, dst, "c").wait_recv)

    def drain(self):
        for cond, cp in self.waits:
            when(cond, cp.wait_send)


def edge_slots(order):
    slots, used, shared = {}, 0, {}
    for d, kids in sorted(spread(order).items()):
        for _, way in kids:
            if way in "xy" and order.index("z") < order.index(way):
                key = (way, d[1], d[2])
                if key not in shared:
                    shared[key] = used
                    used += 4
                slots[d, way] = (shared[key], 4)
            else:
                slots[d, way] = (used, 1)
                used += 1
    return slots, used


def beyond(p, way):
    return p.z < 3 if way == "z+" else p.z > 0 if way == "z-" else None


def reduce_events(p, w, order, own, half, bufs, ready, done):
    tree = spread(order)
    pair = {d: w.new(2) for d in tree}
    wire = {d: w.new(2) for d in tree}
    parent = {nd: (d, way) for d, t in tree.items() for nd, way in t}
    slots, _ = edge_slots(order)

    def buffer(up, way):
        first, n = slots[up, way]
        return bufs.at[first + p.z + up[0] if n > 1 else first]

    events = []
    far = sorted(tree, key=lambda d: (-hops(d), d))
    for d in far:
        def act(d=d):
            cond = p.there(d)

            def step():
                acc = own(d)
                ready(d)
                w.land(pair[d], half(d))
                add_rows(acc, half(d))
                for nd, way in tree[d]:
                    buf = buffer(d, way)

                    def take(buf=buf, nd=nd):
                        w.land(wire[nd], buf)
                        add_rows(acc, buf)
                    when(beyond(p, way), take)
            when(cond, step)
            if hops(d) == 0:
                done()
            else:
                up, way = parent[d]
                w.send(wire[d], own(d), buffer(up, way), BACK[way], cond)
        events.append(act)

    def share(give):
        for d in far:
            w.send(pair[d], give(d), half(d), "c", p.there(d))

    return events, share, far


def gather_events(p, w, order, first, at):
    tree = spread(order)
    pair = {d: w.new(2) for d in tree}
    wire = {d: w.new(2) for d in tree}
    events = []
    for d in sorted(tree, key=lambda d: (hops(d), d)):
        def act(d=d):
            cond = p.there(d)
            blk = at(d, p.c)
            if hops(d):
                w.land(wire[d], blk, cond)
                src = blk
            else:
                src = first
            for nd, way in tree[d]:
                w.send(wire[nd], src, blk, way, both(cond, beyond(p, way)))
            w.send(pair[d], src, blk, "c", cond)
        events.append(act)

    def finish():
        for d in tree:
            w.land(pair[d], at(d, 1 - p.c), p.there(d))

    return events, finish


def run_events(lists, order, extra=iter(()), every=8):
    assert sorted(order) == sorted(64 * g + i for g, acts in enumerate(lists) for i in range(len(acts)))
    for n, k in enumerate(order):
        if n % every == 0:
            next(extra, None)
        lists[k // 64][k % 64]()
    for _ in extra:
        pass


def group_span(table, mats):
    first, last = table[mats[0]], table[mats[-1]]
    units = last[3] + last[2] - first[3]
    return first[3], -(-units // 16) * 16, first[4], last[4] + last[1] * last[5] - first[4]


def units_to_panels(table, mats, units, flat, put):
    base, count = table[mats[0]][3], units.shape[0]
    for k in range(4):
        flat[pl.ds(k, count, stride=4), :] = units[:, 128 * k:128 * (k + 1)].astype(jnp.float32)
    for m in mats:
        rb, panels, n, first, _, padded, _ = table[m]
        for g in range(panels):
            v = flat[pl.ds(4 * (first - base) + g, rb, stride=panels), :]
            if padded > rb:
                v = jnp.concatenate([v, jnp.zeros((padded - rb, 128), jnp.float32)], axis=0)
            put(m, g, v.astype(jnp.bfloat16))


def panels_to_units(table, mats, take, flat, units):
    base, count = table[mats[0]][3], units.shape[0]
    used = 0
    for m in mats:
        rb, panels, n, first, _, padded, _ = table[m]
        for g in range(panels):
            flat[pl.ds(4 * (first - base) + g, rb, stride=panels), :] = take(m, g)[:rb]
        used = 4 * (first - base + n)
    if used < 4 * count:
        flat[used:4 * count, :] = jnp.zeros((4 * count - used, 128), jnp.float32)
    for k in range(4):
        units[:, 128 * k:128 * (k + 1)] = flat[pl.ds(k, count, stride=4), :].astype(jnp.bfloat16)


def encoder_steps(p, table, out, tok, pos, x, x2, tile, gains, biases, tab, fwd, fwd_out, wv, w_sem, fwd_sem, swapped, arrived):
    n1, att, n2, act, proj, prob, ow, m1, i1, m2, i2, slope = fwd

    def load(m):
        rows = pl.ds(table[m][4], table[m][1] * table[m][5])
        return pltpu.make_async_copy(out.at[:, :, :, :, rows], wv.at[:, :, :, :, rows], w_sem.at[m])

    def store(i):
        return pltpu.make_async_copy(fwd[i], fwd_out[i], fwd_sem.at[i])

    for f in swapped:
        f()
    x[...] = tok[...].reshape(256, DE).astype(jnp.float32) + lookup(pos, tab, slice(0, DE))
    same = tile_mask(tile)
    whole = wv.reshape(2, 16, wv.shape[-2], 128)
    block = block_fwd(Block(DE, HE, HDE, FFE, 0, table, 0), x, x2, whole, gains, biases, same, n1, proj, prob, att, ow, m1, i1, n2,
                      m2, i2, act, slope, lambda k: load(k).wait(), lambda k: store(k).start())
    next(block)
    yield
    for f in arrived[0]:
        f()
    load(0).start()
    load(1).start()
    yield
    for _ in range(4):
        next(block)
        yield
    for f in arrived[1]:
        f()
    load(2).start()
    yield
    next(block)
    yield
    for f in arrived[2]:
        f()
    load(3).start()
    yield
    for _ in block:
        pass
    for i in range(4, 12):
        store(i).start()
    yield
    for i in range(12):
        store(i).wait()


class Swap:
    def __init__(self, p, w, src, out, give, keep):
        self.p, self.w, self.src, self.out, self.give, self.keep = p, w, src, out, give, keep
        self.k, self.own = w.new(2), w.new()

    def local(self):
        return pltpu.make_async_copy(self.src.at[self.keep], self.out.at[self.p.x], self.w.sem.at[self.own])

    def start(self):
        self.w.send(self.k, self.src.at[self.give], self.out.at[self.p.x], "x")
        self.local().start()

    def finish(self):
        self.w.land(self.k, self.out.at[1 - self.p.x])
        self.local().wait()


def weights_kernel(table, groups, plan, parts, tok_in, pos_in, cot_in, tile, gains, biases, tab, *refs):
    n = len(groups)
    out, pos, cot, x2 = refs[:4]
    fwd_out, tok, x, fwd, wv, w_sem, fwd_sem = refs[4:16], refs[16], refs[17], refs[18:30], refs[30], refs[31], refs[32]
    rest = refs[33:]
    accs, halves, bufs, shards = (rest[i * n:(i + 1) * n] for i in range(4))
    flat, sem = rest[4 * n:]
    p = Place()
    p.greet(["c", "y", "x"])
    w = Wires(p, sem)
    swaps = [Swap(p, w, a, b, 1 - p.x, p.x) for a, b in ((tok_in, tok), (pos_in, pos), (cot_in, cot))]
    for s in swaps:
        s.start()
    lists, finishes = [], []
    for g, mats in enumerate(groups):
        u0, un, r0, rn = group_span(table, mats)
        acc, half, buf, shard = accs[g], halves[g], bufs[g], shards[g]
        own_sem = w.new()
        loads = {d: w.new() for d in spread(plan[0][g])}

        def own(d, acc=acc):
            return acc.at[p.at(d)[1:]]

        def other(d, half=half):
            return half.at[p.at(d)[1:]]

        def load(d, u0=u0, un=un, own=own, loads=loads):
            return pltpu.make_async_copy(parts.at[p.at(d)[1:] + (p.c, pl.ds(u0, un))], own(d), sem.at[loads[d]])

        def ready(d, load=load):
            load(d).wait()

        def done(mats=mats, acc=acc, shard=shard, r0=r0):
            def put(m, i, v):
                lo = table[m][4] - r0 + i * table[m][5]
                shard[lo:lo + table[m][5], :] = v
            units_to_panels(table, mats, acc.at[p.z, p.y], flat, put)

        ev, share, far = reduce_events(p, w, plan[0][g], own, other, buf, ready, done)

        def begin(load=load, share=share, far=far, u0=u0, un=un):
            share(lambda d: parts.at[p.at(d)[1:] + (1 - p.c, pl.ds(u0, un))])
            for d in far:
                when(p.there(d), load(d).start)

        def at(d, core, r0=r0, rn=rn):
            t, z, y = p.at(d)
            return out.at[t, z, y, core, pl.ds(r0, rn)]

        def local(shard=shard, r0=r0, rn=rn, own_sem=own_sem):
            return pltpu.make_async_copy(shard, out.at[p.x, p.z, p.y, p.c, pl.ds(r0, rn)], sem.at[own_sem])

        ag, finish = gather_events(p, w, plan[1][g], shard, at)

        def send_first(act=ag[0], local=local):
            act()
            local().start()

        lists.append([begin] + ev + [send_first] + ag[1:])
        finishes += [finish, lambda local=local: local().wait()]
    steps = encoder_steps(p, table, out, tok, pos, x, x2, tile, gains, biases, tab, fwd, fwd_out, wv, w_sem, fwd_sem,
                          [s.finish for s in swaps[:2]], [finishes[2 * k:2 * k + 2] for k in range(3)])
    lists.append([partial(next, steps, None)] * 11)
    run_events(lists, plan[2])
    for f in finishes[6:] + [swaps[2].finish]:
        f()
    w.drain()


def spread_weights(parts, tokens, pos, cot, tile, gains, biases, table, rows, groups, plan, ident):
    spans = [group_span(table, m) for m in groups]
    bf16 = jnp.bfloat16
    S = jax.ShapeDtypeStruct
    V = pltpu.VMEM
    fwd = FWD_ACTS + FWD_KEPT
    enc_rows = table[4][4]
    scratch = [V(tokens.shape, tokens.dtype), V((256, DE), jnp.float32)] + [V(k, t) for k, t in fwd]
    scratch += [V((2, 4, 2, 2, enc_rows, 128), bf16), pltpu.SemaphoreType.DMA((4,)), pltpu.SemaphoreType.DMA((12,))]
    scratch += [V((4, 2, s[1], 512), bf16) for s in spans] * 2
    scratch += [V((edge_slots(o)[1], s[1], 512), bf16) for s, o in zip(spans, plan[0])]
    scratch += [V((s[3], 128), bf16) for s in spans]
    scratch += [V((4 * max(s[1] for s in spans), 128), jnp.float32),
                pltpu.SemaphoreType.DMA((len(groups) * (1 + 5 * 14 + 4 * 28) + 9,))]
    hbm = pl.BlockSpec(memory_space=pl.ANY)
    vmem = pl.BlockSpec(memory_space=pltpu.VMEM)
    return pl.pallas_call(
        partial(weights_kernel, table, groups, plan),
        out_shape=[S((2, 4, 2, 2, rows, 128), bf16), S(pos.shape, pos.dtype), S(cot.shape, cot.dtype), S((256, DE), jnp.float32)]
        + [S(k, t) for k, t in fwd],
        in_specs=[hbm] * 4 + [vmem] * 4, out_specs=[hbm, vmem, hbm, vmem] + [hbm] * 12,
        scratch_shapes=scratch,
        compiler_params=pltpu.CompilerParams(collective_id=ident, has_side_effects=True, vmem_limit_bytes=63 << 20),
        name="spread_weights",
    )(parts, tokens, pos, cot, tile, gains, biases, jnp.asarray(position_table()))


def return_kernel(table, groups, plan, *refs):
    n = len(groups)
    kept_in, small_src, dec_in, dx_in, out, small_out, dec, dx = refs[:18], *refs[18:25]
    rest = refs[25:]
    kept, rest = rest[:18], rest[18:]
    acts, grads = kept[:9], kept[9:]
    sides, halves, bufs, units = (rest[i * n:(i + 1) * n] for i in range(4))
    flat, turned, mid, line, load_sem, sem = rest[4 * n:]

    def load(i):
        return pltpu.make_async_copy(kept_in[i], kept[i], load_sem.at[i])

    first = sorted(range(n), key=lambda g: plan[2].index(64 * g))
    for g in first:
        for m in groups[g]:
            load(m).start()
            load(9 + m).start()
    p = Place()
    p.greet(["c", "y", "x"])
    w = Wires(p, sem)
    swaps = [Swap(p, w, a, b, 1 - p.x, p.x) for a, b in ((dec_in, dec), (dx_in, dx))]
    swaps[0].start()
    lists, finishes = [], []
    for g, mats in enumerate(groups):
        u0, un, r0, rn = group_span(table, mats)
        side, half, buf, unit = sides[g], halves[g], bufs[g], units[g]
        own_sem = w.new()

        def own(d, side=side):
            return side.at[(p.c,) + p.at(d)]

        def other(d, half=half):
            return half.at[p.at(d)]

        def done(mats=mats, side=side, unit=unit, r0=r0):
            mine = side.at[p.c, p.x, p.z, p.y]

            def take(m, i):
                lo = table[m][4] - r0 + i * table[m][5]
                return mine[lo:lo + table[m][5], :].astype(jnp.float32)
            panels_to_units(table, mats, take, flat, unit)

        ev, share, far = reduce_events(p, w, plan[0][g], own, other, buf, lambda d: None, done)

        def begin(mats=mats, side=side, share=share, r0=r0):
            for m in mats:
                lo, padded = table[m][4] - r0, table[m][5]

                def put(t, i, v, lo=lo, padded=padded):
                    v = v.reshape(4, 2, 2, padded, 128)
                    rows = pl.ds(pl.multiple_of(lo + i * padded, 16), padded)
                    side[0, t, :, :, rows, :] = v[:, :, 0]
                    side[1, t, :, :, rows, :] = v[:, :, 1]
                load(m).wait()
                load(9 + m).wait()
                grad_panels(table, m, acts[m], grads[m], turned, put)
            share(lambda d: side.at[(1 - p.c,) + p.at(d)])

        def at(d, core, u0=u0, un=un):
            _, z, y = p.at(d)
            return out.at[z, y, core, pl.ds(u0, un)]

        def local(unit=unit, u0=u0, un=un, own_sem=own_sem):
            return pltpu.make_async_copy(unit, out.at[p.z, p.y, p.c, pl.ds(u0, un)], sem.at[own_sem])

        ag, finish = gather_events(p, w, plan[1][g], unit, at)

        def send_first(act=ag[0], local=local):
            act()
            local().start()

        lists.append([begin] + ev + [send_first] + ag[1:])
        finishes += [finish, lambda local=local: local().wait()]
    last = max(plan[2].index(64 * g + len(spread(plan[0][g]))) for g in range(n))
    g, i = plan[2][last] // 64, plan[2][last] % 64
    act = lists[g][i]

    def with_swaps():
        act()
        swaps[1].start()

    lists[g][i] = with_swaps
    run_events(lists, plan[2], total_steps(p, w, small_src, small_out, mid, line))
    for f in finishes + [s.finish for s in swaps]:
        f()
    w.drain()


def total_steps(p, w, src, out, mid, line):
    k = [w.new(2) for _ in range(9)]
    now = src
    for i, way in enumerate(("c", "x", "y")):
        w.send(k[i], now, mid.at[i], way)
        yield
        w.land(k[i], mid.at[i])
        nxt = mid.at[3 + i] if i < 2 else line.at[p.z]
        nxt[...] = now[...] + mid[i]
        now = nxt
    for i in range(4):
        lo, hi = jnp.maximum(p.z - i, 0), jnp.minimum(p.z + i, 3)
        if i > 0:
            w.land(k[2 + i], line.at[lo], p.z >= i)
            w.land(k[5 + i], line.at[hi], p.z + i <= 3)
        if i < 3:
            w.send(k[3 + i], line.at[lo], line.at[lo], "z+", jnp.logical_and(p.z >= i, p.z < 3))
            w.send(k[6 + i], line.at[hi], line.at[hi], "z-", jnp.logical_and(p.z + i <= 3, p.z > 0))
            yield
    out[...] = (line[0] + line[1]) + (line[2] + line[3])


def return_grads(kept, small, dec, dx, table, total_units, groups, plan, ident):
    spans = [group_span(table, m) for m in groups]
    bf16 = jnp.bfloat16
    S = jax.ShapeDtypeStruct
    V = pltpu.VMEM
    scratch = [V(v.shape, v.dtype) for v in kept]
    scratch += [V((2, 2, 4, 2, s[3], 128), bf16) for s in spans]
    scratch += [V((2, 4, 2, s[3], 128), bf16) for s in spans]
    scratch += [V((edge_slots(o)[1], s[3], 128), bf16) for s, o in zip(spans, plan[0])]
    scratch += [V((s[1], 512), bf16) for s in spans]
    scratch += [V((4 * max(s[1] for s in spans), 128), jnp.float32), V((FFE, 256), bf16),
                V((5,) + small.shape, small.dtype), V((4,) + small.shape, small.dtype), pltpu.SemaphoreType.DMA((18,)),
                pltpu.SemaphoreType.DMA((len(groups) * (1 + 4 * 14 + 4 * 28) + 24,))]
    vmem = pl.BlockSpec(memory_space=pltpu.VMEM)
    hbm = pl.BlockSpec(memory_space=pl.ANY)
    return pl.pallas_call(
        partial(return_kernel, table, groups, plan),
        out_shape=(S((4, 2, 2, total_units, 512), bf16), S(small.shape, small.dtype), S(dec.shape, dec.dtype), S(dx.shape, dx.dtype)),
        in_specs=[hbm] * 18 + [vmem, hbm, hbm], out_specs=(hbm, vmem, hbm, hbm),
        scratch_shapes=scratch,
        compiler_params=pltpu.CompilerParams(collective_id=ident, has_side_effects=True, vmem_limit_bytes=63 << 20),
        name="return_grads",
    )(*kept, small, dec, dx)


STEP_ROWS = 432


def update_kernel(place_s, place, spread, master, first, second, total, params, norm_first, norm_second,
                  new_master, new_first, new_second, new_norms, new_nf, new_ns):
    i = pl.program_id(0)

    @pl.when(i == 0)
    def _():
        new_norms[...], new_nf[...], new_ns[...] = adamw(params[...], total[...], norm_first[...], norm_second[...], 0.0, NORM_RATE)

    lane = lax.broadcasted_iota(jnp.int32, (16, 256), 1)
    row = lax.broadcasted_iota(jnp.int32, (16, 256), 0)
    for k in range(STEP_ROWS // 16):
        tiles = []
        for j in range(16):
            at = jnp.minimum(place_s[i * STEP_ROWS + 16 * k + j] >> 4, spread.shape[0] // 16 - 1)
            tiles.append(spread[pl.ds(pl.multiple_of(at * 16, 16), 16), :])
        here = slice(16 * k, 16 * k + 16)
        spot = place[here, :]
        used = jnp.logical_and(lane == row * 16 + (spot & 15), spot < spread.shape[0])
        grad = dot(jnp.where(used, 1.0, 0.0).astype(jnp.bfloat16), jnp.concatenate(tiles, axis=0))
        new_master[here, :], new_first[here, :], new_second[here, :] = adamw(
            master[here, :], grad, first[here, :], second[here, :], WEIGHT_DECAY, LEARN_RATE)


def update(place, spread, master, first, second, total, params, norm_first, norm_second):
    slots = master.shape[0]
    S = jax.ShapeDtypeStruct
    rows = pl.BlockSpec((STEP_ROWS, 512), lambda i, s: (i, 0))
    whole = lambda v: pl.BlockSpec(v.shape, lambda i, s: (0, 0), pipeline_mode=pl.Buffered(1))
    small = pl.BlockSpec(params.shape, lambda i, s: (0, 0))
    out = [S(master.shape, jnp.float32)] * 3 + [S(params.shape, jnp.float32)] * 3
    return pl.pallas_call(
        update_kernel, out_shape=out,
        grid_spec=pltpu.PrefetchScalarGridSpec(
            num_scalar_prefetch=1, grid=(slots // STEP_ROWS,),
            in_specs=[pl.BlockSpec((STEP_ROWS, 1), lambda i, s: (i, 0)), whole(spread), rows, rows, rows, small, small, small, small],
            out_specs=[rows] * 3 + [small] * 3),
        compiler_params=pltpu.CompilerParams(vmem_limit_bytes=62 << 20), name="update",
    )(place, lax.optimization_barrier(place)[:, None], spread, master, first, second, total, params, norm_first, norm_second)


def place_kernel(place_s, master, out, wide, staged, sem):
    count = wide.shape[0] // 64 - 1

    def clear(i, _):
        wide[pl.ds(pl.multiple_of(i * 64, 64), 64), :] = jnp.zeros((64, 512), jnp.float32)
        return 0

    lax.fori_loop(0, count, clear, 0)

    def turn(i, _):
        for j in range(16):
            wide[pl.ds(place_s[i * 16 + j], 1), :] = master[pl.ds(i * 16 + j, 1), :]
        return 0

    lax.fori_loop(0, master.shape[0] // 16, turn, 0)
    parts = 4
    part = count // parts * 64

    def copy(k):
        rows = pl.ds(pl.multiple_of(k * part, 64), part)
        return pltpu.make_async_copy(staged.at[rows], out.at[rows], sem.at[k])

    for k in range(parts):
        def narrow(i, _):
            rows = pl.ds(pl.multiple_of(k * part + i * 64, 64), 64)
            staged[rows, :] = wide[rows, :].astype(jnp.bfloat16)
            return 0

        lax.fori_loop(0, part // 64, narrow, 0)
        copy(k).start()
    for k in range(parts):
        copy(k).wait()


def place_blocks(place, master, rows):
    return pl.pallas_call(
        place_kernel, out_shape=jax.ShapeDtypeStruct((rows, 512), jnp.bfloat16),
        grid_spec=pltpu.PrefetchScalarGridSpec(
            num_scalar_prefetch=1, grid=(1,),
            in_specs=[pl.BlockSpec(master.shape, lambda i, s: (0, 0), pipeline_mode=pl.Buffered(1))],
            out_specs=pl.BlockSpec(memory_space=pl.ANY),
            scratch_shapes=[pltpu.VMEM((rows + 64, 512), jnp.float32), pltpu.VMEM((rows, 512), jnp.bfloat16), pltpu.SemaphoreType.DMA((4,))]),
        compiler_params=pltpu.CompilerParams(vmem_limit_bytes=60 << 20), name="place_blocks",
    )(place, master)


def sequence_device(tokens_in, positions, segment_ids, owners, master, first_moment, second_moment, norm_gains,
                    norm_biases, norm_first, norm_second, cotangent):
    shapes = weight_shapes(2)
    table, _, rows = layout(shapes, 16)
    unit, used = own_units(owners, lax.axis_index("dp"), master.shape[0])
    place = jnp.where(used, unit_places(unit, table, 16), 16 * SHARD_UNITS)
    parts = place_blocks(place, master, 16 * SHARD_UNITS)
    full, pos, cot, x2, *fwd = spread_weights(parts.reshape(4, 2, 2, SHARD_UNITS, 512), tokens_in, positions.transpose(1, 0, 2),
                                              cotangent, segment_ids, norm_gains, norm_biases, table, rows, GROUPS, PLAN_OUT, 1)
    kept = chain(pos, segment_ids, norm_gains, norm_biases, cot.reshape(256, DD), full, x2, fwd[4:], table)
    decoded, dx0, norms = kept[:3]
    spread_out, norm_total, decoded, dx0 = return_grads([*fwd[:4], *kept[3:]], norms, decoded.reshape(2, 128, DD), dx0.reshape(2, 128, DE), table,
                                                        SHARD_UNITS, GROUPS, PLAN_BACK, 2)
    norm_params = jnp.concatenate([norm_gains, norm_biases], axis=0)
    new_master, new_first, new_second, new_norms, norm_one_new, norm_two_new = update(
        place, spread_out.reshape(16 * SHARD_UNITS, 512), master, first_moment, second_moment, norm_total, norm_params, norm_first, norm_second)
    return (decoded, dx0, new_master, new_first, new_second, new_norms, norm_one_new, norm_two_new)


def solution(mesh):
    step = sequence_device if (mesh.shape["dp"], mesh.shape["tensor"]) == (16, 2) else per_device
    return jax.shard_map(
        step,
        mesh=mesh,
        in_specs=(
            P(None, ("dp", "tensor"), None),
            P(None, None, ("dp", "tensor")),
            P(None, "dp", None),
            P(),
            P("dp", "tensor"),
            P("dp", "tensor"),
            P("dp", "tensor"),
            P(),
            P(),
            P(),
            P(),
            P(None, ("dp", "tensor"), None),
        ),
        out_specs=(
            P(None, ("dp", "tensor"), None),
            P(None, ("dp", "tensor"), None),
            P("dp", "tensor"),
            P("dp", "tensor"),
            P("dp", "tensor"),
            P(),
            P(),
            P(),
        ),
        check_vma=False,
    )
```

```python
from functools import partial

import jax
import jax.numpy as jnp
import ml_dtypes
import numpy as np
from jax import lax
from jax.experimental import pallas as pl
from jax.experimental.pallas import tpu as pltpu
from jax.sharding import PartitionSpec as P

DE = 768
HE = 12
HDE = 64
FFE = 3072
DD = 512
HD = 16
HDD = 32
FFD = 2048
STEP = 10


NORM_EPS = 1e-06
BETA_ONE = 0.5
BETA_TWO = 0.5
LEARN_RATE = 0.03
NORM_RATE = 0.3
WEIGHT_DECAY = 0.05
ADAM_EPS = 1e-08
MASK_FILL = -1000000000.0


def sincos_part(coordinate, part_width):
    halfway = part_width // 2
    frequency = 1.0 / 10000.0 ** (jnp.arange(halfway, dtype=jnp.float32) / halfway)
    angles = coordinate.astype(jnp.float32)[:, None] * frequency[None, :]
    return jnp.concatenate([jnp.sin(angles), jnp.cos(angles)], axis=1)


def sincos_embed(positions, model_width):
    side_width = model_width // 16 * 6
    first_width = model_width - 2 * side_width
    return jnp.concatenate(
        [
            sincos_part(positions[0], first_width),
            sincos_part(positions[1], side_width),
            sincos_part(positions[2], side_width),
        ],
        axis=1,
    )


def slot_table(owners, devices, capacity):
    owner_ids = owners[:, 0]
    onehot = (owner_ids[:, None] == jnp.arange(devices, dtype=jnp.int32)[None, :]).astype(jnp.int32)
    before = jnp.cumsum(onehot, axis=0) - onehot
    owner_rank = jnp.sum(before * onehot, axis=1)
    return owner_ids * capacity + owner_rank


def weight_shapes(tensor_count):
    enc_heads = HE // tensor_count
    dec_heads = HD // tensor_count
    return [
        (DE, 3 * enc_heads * HDE),
        (enc_heads * HDE, DE),
        (DE, FFE // tensor_count),
        (FFE // tensor_count, DE),
        (DE, DD // tensor_count),
        (DD, 3 * dec_heads * HDD),
        (dec_heads * HDD, DD),
        (DD, FFD // tensor_count),
        (FFD // tensor_count, DD),
    ]


def split_flat(flat_vector, shapes):
    pieces = []
    offset = 0
    for matrix_shape in shapes:
        length = matrix_shape[0] * matrix_shape[1]
        pieces.append(flat_vector[offset : offset + length].reshape(matrix_shape))
        offset += length
    return pieces


def adamw(weights, gradient, moment_one, moment_two, decay_rate, step_rate):
    one_new = BETA_ONE * moment_one + (1.0 - BETA_ONE) * gradient
    two_new = BETA_TWO * moment_two + (1.0 - BETA_TWO) * gradient * gradient
    one_hat = one_new / (1.0 - BETA_ONE**STEP)
    two_hat = two_new / (1.0 - BETA_TWO**STEP)
    weights_new = weights - step_rate * (
        one_hat / (jnp.sqrt(two_hat) + ADAM_EPS) + decay_rate * weights
    )
    return (weights_new, one_new, two_new)


def norm_forward(values, gain_row, bias_row):
    center = values - jnp.mean(values, axis=-1, keepdims=True)
    spread = jnp.mean(center * center, axis=-1, keepdims=True)
    inverse = lax.rsqrt(spread + NORM_EPS)
    normed = center * inverse
    return (normed * gain_row + bias_row, (normed, inverse))


def norm_backward(upstream, stored, gain_row):
    normed, inverse = stored
    scaled = upstream * gain_row
    mean_one = jnp.mean(scaled, axis=-1, keepdims=True)
    mean_two = jnp.mean(scaled * normed, axis=-1, keepdims=True)
    return (
        inverse * (scaled - mean_one - normed * mean_two),
        jnp.sum(upstream * normed, axis=0),
        jnp.sum(upstream, axis=0),
    )


def inner_rows(left_side, right_side):
    return lax.dot_general(
        left_side, right_side, (((0,), (0,)), ((), ())), preferred_element_type=jnp.float32
    )


def times_transpose(left_side, right_side):
    return lax.dot_general(
        left_side, right_side, (((1,), (1,)), ((), ())), preferred_element_type=jnp.float32
    )


def gather_rows(values):
    return lax.all_gather(values, "tensor", axis=0, tiled=True)


def gather_grads(values):
    return lax.all_gather(values, "tensor", axis=0, tiled=True)


def branch_rows(values, weight):
    return lax.psum_scatter(
        jnp.dot(values, weight, preferred_element_type=jnp.float32).astype(jnp.bfloat16),
        "tensor",
        scatter_dimension=0,
        tiled=True,
    ).astype(jnp.float32)


def input_rows(values, weight):
    return lax.psum_scatter(
        times_transpose(values, weight).astype(jnp.bfloat16),
        "tensor",
        scatter_dimension=0,
        tiled=True,
    ).astype(jnp.float32)


def block_scores(queries, key_rows, mask_bias, block_start, block_rows, head_size):
    scores = jnp.einsum(
        "qhd,khd->hqk", queries, key_rows, preferred_element_type=jnp.float32
    ) * head_size ** (-0.5)
    return scores + mask_bias[None, block_start : block_start + block_rows]


def attention_forward(gathered, w_qkv, head_count, head_size, mask_bias):
    length = gathered.shape[0]
    projected = jnp.dot(gathered, w_qkv, preferred_element_type=jnp.float32).astype(jnp.bfloat16)
    projected = projected.reshape(length, 3, head_count, head_size)
    queries = projected[:, 0]
    key_rows = projected[:, 1]
    value_rows = projected[:, 2]
    block_rows = min(512, length)
    scores = block_scores(queries, key_rows, mask_bias, 0, block_rows, head_size)
    row_peak = jnp.max(scores, axis=-1, keepdims=True)
    row_total = row_peak + jnp.log(jnp.sum(jnp.exp(scores - row_peak), axis=-1, keepdims=True))
    weights = jnp.exp(scores - row_total).astype(jnp.bfloat16)
    outputs = jnp.einsum("hqk,khd->qhd", weights, value_rows, preferred_element_type=jnp.float32)
    totals = [row_total]
    attended = outputs.astype(jnp.bfloat16).reshape(length, head_count * head_size)
    return (attended, (queries, key_rows, value_rows, totals))


def attention_backward(upstream, w_out, attended, stored, head_count, head_size, mask_bias):
    queries, key_rows, value_rows, totals = stored
    length = upstream.shape[0]
    score_scale = head_size ** (-0.5)
    grad_out = inner_rows(attended, upstream)
    attended_grad = (
        times_transpose(upstream, w_out).astype(jnp.bfloat16).reshape(length, head_count, head_size)
    )
    block_rows = min(512, length)
    key_grads = jnp.zeros((length, head_count, head_size), jnp.float32)
    value_grads = jnp.zeros((length, head_count, head_size), jnp.float32)
    query_grads = []
    for number, block_start in enumerate(range(0, length, block_rows)):
        scores = block_scores(queries, key_rows, mask_bias, block_start, block_rows, head_size)
        weights = jnp.exp(scores - totals[number])
        value_grads = jnp.einsum(
            "hqk,qhd->khd",
            weights.astype(jnp.bfloat16),
            attended_grad,
            preferred_element_type=jnp.float32,
        )
        weight_grads = jnp.einsum(
            "qhd,khd->hqk", attended_grad, value_rows, preferred_element_type=jnp.float32
        )
        score_grads = (
            weights * (weight_grads - jnp.sum(weights * weight_grads, axis=-1, keepdims=True))
        ).astype(jnp.bfloat16)
        query_grads.append(
            jnp.einsum("hqk,khd->qhd", score_grads, key_rows, preferred_element_type=jnp.float32)
            * score_scale
        )
        key_grads = (
            jnp.einsum("hqk,qhd->khd", score_grads, queries, preferred_element_type=jnp.float32)
            * score_scale
        )
    projected_grad = jnp.stack([query_grads[0], key_grads, value_grads], axis=1)
    return (
        projected_grad.astype(jnp.bfloat16).reshape(length, 3 * head_count * head_size),
        grad_out,
    )


def block_forward(residual, matrices, gain_rows, bias_rows, head_count, head_size, mask_bias):
    w_qkv, w_out, w_in, w_down = matrices
    normed, norm_one = norm_forward(residual, gain_rows[0], bias_rows[0])
    gathered = gather_rows(normed.astype(jnp.bfloat16))
    attended, stored = attention_forward(gathered, w_qkv, head_count, head_size, mask_bias)
    middle = residual + branch_rows(attended, w_out)
    normed_two, norm_two = norm_forward(middle, gain_rows[1], bias_rows[1])
    gathered_two = gather_rows(normed_two.astype(jnp.bfloat16))
    hidden = jnp.dot(gathered_two, w_in, preferred_element_type=jnp.float32)
    active = jax.nn.gelu(hidden, approximate=False).astype(jnp.bfloat16)
    result = middle + branch_rows(active, w_down)
    return (result, (gathered, norm_one, attended, stored, gathered_two, norm_two, hidden, active))


def block_backward(upstream, matrices, gain_rows, saved_values, head_count, head_size, mask_bias):
    w_qkv, w_out, w_in, w_down = matrices
    gathered, norm_one, attended, stored, gathered_two, norm_two, hidden, active = saved_values
    down_full = gather_grads(upstream.astype(jnp.bfloat16))
    grad_down = inner_rows(active, down_full)
    active_grad = times_transpose(down_full, w_down)
    gelu_pull = jax.vjp(partial(jax.nn.gelu, approximate=False), hidden)[1]
    hidden_grad = gelu_pull(active_grad)[0].astype(jnp.bfloat16)
    grad_in = inner_rows(gathered_two, hidden_grad)
    normed_two_grad = input_rows(hidden_grad, w_in)
    middle_grad, gain_two, bias_two = norm_backward(normed_two_grad, norm_two, gain_rows[1])
    middle_grad = upstream + middle_grad
    middle_full = gather_grads(middle_grad.astype(jnp.bfloat16))
    projected_grad, grad_out = attention_backward(
        middle_full, w_out, attended, stored, head_count, head_size, mask_bias
    )
    grad_qkv = inner_rows(gathered, projected_grad)
    normed_grad = input_rows(projected_grad, w_qkv)
    input_grad, gain_one, bias_one = norm_backward(normed_grad, norm_one, gain_rows[0])
    return (
        middle_grad + input_grad,
        [grad_qkv, grad_out, grad_in, grad_down],
        (gain_one, gain_two, bias_one, bias_two),
    )


def embed_forward(residual, w_embed):
    residual_low = gather_rows(residual.astype(jnp.bfloat16))
    columns = jnp.dot(residual_low, w_embed, preferred_element_type=jnp.float32).astype(
        jnp.bfloat16
    )
    own_columns = lax.all_to_all(columns, "tensor", split_axis=0, concat_axis=1, tiled=True)
    return (own_columns.astype(jnp.float32), residual_low)


def embed_backward(upstream, residual_low, w_embed):
    columns = lax.all_to_all(
        upstream.astype(jnp.bfloat16), "tensor", split_axis=1, concat_axis=0, tiled=True
    )
    grad_embed = inner_rows(residual_low, columns)
    return (input_rows(columns, w_embed), grad_embed)


def slot_builder(gradients, unit_of_slot, unit_width):
    flat_units = jnp.concatenate([gradient.reshape(-1) for gradient in gradients]).reshape(
        -1, unit_width
    )
    unit_total = flat_units.shape[0]
    source = jnp.take(flat_units, jnp.clip(unit_of_slot, 0, unit_total - 1), axis=0)
    return jnp.where((unit_of_slot >= 0)[:, None], source, 0.0)


def per_device(
    tokens_in,
    positions,
    segment_ids,
    owners,
    master,
    first_moment,
    second_moment,
    norm_gains,
    norm_biases,
    norm_first,
    norm_second,
    cotangent,
):
    devices = lax.axis_size("dp")
    tensor_count = lax.axis_size("tensor")
    capacity = master.shape[0]
    unit_width = master.shape[1]
    unit_count = owners.shape[0]
    slot_index = slot_table(owners, devices, capacity)
    unit_of_slot = (
        jnp.full((devices * capacity,), -1, jnp.int32)
        .at[slot_index]
        .set(jnp.arange(unit_count, dtype=jnp.int32))
    )
    targets = unit_of_slot
    targets = jnp.where(targets < 0, unit_count, targets)
    placed = (
        jnp.zeros((unit_count, unit_width), jnp.bfloat16)
        .at[targets]
        .set(lax.all_gather(master.astype(jnp.bfloat16), "dp", axis=0, tiled=True), mode="drop")
    )
    shapes = weight_shapes(tensor_count)
    matrices = split_flat(placed.reshape(-1), shapes)
    encoder = matrices[0:4]
    w_embed = matrices[4]
    decoder = matrices[5:9]
    enc_heads = HE // tensor_count
    dec_heads = HD // tensor_count
    micro_count = tokens_in.shape[0]
    grad_sums = [jnp.zeros(matrix_shape, jnp.float32) for matrix_shape in shapes]
    norm_sums = jnp.zeros((4, DE + DD), jnp.float32)
    decoded_rows = []
    token_grads = []
    for micro_step in range(micro_count):
        tile_ids = segment_ids[micro_step, 0]
        mask_bias = jnp.where(tile_ids[:, None] == tile_ids[None, :], 0.0, MASK_FILL).astype(
            jnp.float32
        )
        position_now = positions[:, micro_step]
        residual = tokens_in[micro_step].astype(jnp.float32) + sincos_embed(position_now, DE)
        residual, enc_saved = block_forward(
            residual, encoder, norm_gains[:, :DE], norm_biases[:, :DE], enc_heads, HDE, mask_bias
        )
        residual, embed_low = embed_forward(residual, w_embed)
        residual = residual + sincos_embed(position_now, DD)
        residual, dec_saved = block_forward(
            residual, decoder, norm_gains[:, DE:], norm_biases[:, DE:], dec_heads, HDD, mask_bias
        )
        decoded_rows.append(residual)
        upstream, dec_grads, dec_norm = block_backward(
            cotangent[micro_step], decoder, norm_gains[:, DE:], dec_saved, dec_heads, HDD, mask_bias
        )
        upstream, grad_embed = embed_backward(upstream, embed_low, w_embed)
        upstream, enc_grads, enc_norm = block_backward(
            upstream, encoder, norm_gains[:, :DE], enc_saved, enc_heads, HDE, mask_bias
        )
        token_grads.append(upstream)
        step_grads = enc_grads + [grad_embed] + dec_grads
        step_norm = jnp.concatenate([jnp.stack(enc_norm), jnp.stack(dec_norm)], axis=1)
        grad_sums = [total_grad + new_grad for total_grad, new_grad in zip(grad_sums, step_grads)]
        norm_sums = norm_sums + step_norm
    reduced = lax.psum_scatter(
        slot_builder(grad_sums, unit_of_slot, unit_width), "dp", scatter_dimension=0, tiled=True
    )
    norm_total = lax.psum(norm_sums, ("dp", "tensor"))
    new_master, new_first, new_second = adamw(
        master, reduced, first_moment, second_moment, WEIGHT_DECAY, LEARN_RATE
    )
    norm_params = jnp.concatenate([norm_gains, norm_biases], axis=0)
    new_norms, norm_one_new, norm_two_new = adamw(
        norm_params, norm_total, norm_first, norm_second, 0.0, NORM_RATE
    )
    return (
        jnp.stack(decoded_rows),
        jnp.stack(token_grads),
        new_master,
        new_first,
        new_second,
        new_norms,
        norm_one_new,
        norm_two_new,
    )


MESH = pl.DeviceIdType.MESH
ALL = slice(None)


class Place:
    def __init__(self):
        self.d = lax.axis_index("dp")
        self.x = lax.axis_index("tensor")
        self.z = self.d // 4
        self.y = (self.d // 2) % 2
        self.c = self.d % 2
        self.ids = {
            "c": (self.d + 1 - 2 * self.c, self.x),
            "y": (self.d + 2 - 4 * self.y, self.x),
            "x": (self.d, 1 - self.x),
            "z+": (self.d + 4, self.x),
            "z-": (self.d - 4, self.x),
        }

    def greet(self, kinds):
        bar = pltpu.get_barrier_semaphore()
        for k in kinds:
            pl.semaphore_signal(bar, inc=1, device_id=self.ids[k], device_id_type=MESH)

        @pl.when(self.z < 3)
        def _():
            pl.semaphore_signal(bar, inc=1, device_id=self.ids["z+"], device_id_type=MESH)

        @pl.when(self.z > 0)
        def _():
            pl.semaphore_signal(bar, inc=1, device_id=self.ids["z-"], device_id_type=MESH)

        inner = jnp.where(jnp.logical_and(self.z > 0, self.z < 3), 1, 0)
        pl.semaphore_wait(bar, len(kinds) + 1 + inner)

    def there(self, disp):
        dz = disp[0]
        if dz == 0:
            return None
        return self.z + dz <= 3 if dz > 0 else self.z + dz >= 0

    def at(self, disp):
        dz, fy, fx = disp
        return (1 - self.x if fx else self.x, self.z + dz, 1 - self.y if fy else self.y)


def when(cond, f):
    if cond is None:
        f()
    else:
        pl.when(cond)(f)


def both(a, b):
    if a is None:
        return b
    if b is None:
        return a
    return jnp.logical_and(a, b)


def spread(order):
    out = {}
    todo = [((0, 0, 0), -1, 0)]
    while todo:
        (dz, fy, fx), last, way = todo.pop(0)
        nxt = []
        for i, a in enumerate(order):
            if i < last:
                continue
            if a == "z":
                for s in (1, -1):
                    if i == last and s != way:
                        continue
                    n = (dz - s, fy, fx)
                    if abs(n[0]) <= 3:
                        nxt.append((n, "z+" if s > 0 else "z-", i, s))
            elif i > last:
                n = (dz, 1, fx) if a == "y" else (dz, fy, 1)
                nxt.append((n, a, i, 0))
        out[(dz, fy, fx)] = [(n, w) for n, w, _, _ in nxt]
        todo += [(n, i, s) for n, _, i, s in nxt]
    return out


def hops(d):
    return abs(d[0]) + d[1] + d[2]


BACK = {"z+": "z-", "z-": "z+", "x": "x", "y": "y"}


def add_rows(acc, got, step=80):
    n = acc.shape[0]
    while n % step:
        step -= 16

    def body(i, _):
        r = pl.ds(pl.multiple_of(i * step, step), step)
        acc[r, :] = acc[r, :] + got[r, :]
        return 0

    lax.fori_loop(0, n // step, body, 0)


SHARD_UNITS = 656
PANEL = 128
GROUPS = ((0, 1), (2,), (3,), (4, 5, 6), (7, 8))

PLAN_OUT = (
    ("zy", "yz", "zy", "yz", "yz"),
    ("zyx", "zxy", "zyx", "yzx", "xzy"),
    (
        64, 65, 66, 0, 70, 1, 128, 2, 4, 5, 6, 137, 68, 3, 8, 9, 12, 7, 192, 130, 256, 140, 69, 10, 73, 129, 133, 136,
        13, 11, 74, 72, 67, 262, 14, 15, 71, 134, 131, 77, 132, 19, 76, 18, 75, 16, 320, 26, 135, 24, 138, 20, 78, 79,
        22, 141, 139, 195, 34, 257, 27, 81, 32, 193, 258, 25, 80, 35, 259, 83, 142, 143, 90, 30, 194, 266, 82, 196,
        39, 40, 144, 199, 84, 197, 260, 198, 263, 148, 147, 200, 261, 264, 31, 201, 202, 203, 98, 33, 29, 28, 42, 91,
        21, 155, 154, 36, 265, 204, 205, 269, 23, 268, 157, 267, 206, 164, 207, 86, 162, 17, 92, 103, 38, 88, 270, 37,
        271, 41, 210, 106, 161, 104, 96, 85, 99, 146, 150, 321, 322, 275, 160, 272, 211, 323, 273, 89, 153, 324, 100,
        101, 276, 208, 105, 168, 97, 165, 282, 217, 163, 218, 95, 209, 93, 87, 152, 214, 166, 325, 94, 151, 167, 102,
        280, 169, 290, 326, 277, 327, 159, 170, 225, 145, 221, 226, 216, 149, 156, 279, 158, 288, 212, 284, 328, 283,
        278, 228, 329, 295, 291, 213, 223, 219, 285, 232, 220, 330, 224, 296, 286, 292, 274, 289, 233, 230, 234, 229,
        281, 287, 222, 227, 231, 215, 294, 293, 298, 297,
    ),
)
PLAN_BACK = (
    ("zxy", "yzx", "zyx", "yzx", "xzy"),
    ("zy", "zy", "zy", "yz", "yz"),
    (
        256, 257, 258, 262, 261, 269, 64, 259, 67, 260, 65, 69, 263, 66, 78, 264, 271, 278, 276, 77, 270, 268, 267,
        71, 70, 275, 282, 85, 72, 266, 76, 265, 192, 82, 68, 199, 277, 73, 0, 84, 274, 74, 272, 5, 273, 80, 75, 279,
        6, 79, 13, 128, 204, 1, 281, 2, 12, 89, 283, 280, 11, 141, 129, 19, 8, 83, 4, 195, 86, 193, 87, 3, 134, 15, 7,
        81, 284, 285, 133, 88, 91, 14, 10, 197, 194, 90, 22, 196, 132, 286, 131, 201, 288, 287, 130, 16, 18, 21, 198,
        9, 92, 20, 205, 93, 291, 202, 200, 290, 136, 289, 143, 292, 26, 140, 208, 150, 206, 17, 94, 23, 135, 25, 212,
        213, 294, 95, 142, 203, 96, 24, 138, 148, 139, 207, 137, 211, 27, 214, 210, 100, 97, 295, 144, 215, 149, 104,
        146, 209, 147, 28, 29, 151, 218, 219, 217, 145, 154, 32, 101, 153, 106, 30, 216, 36, 155, 152, 296, 33, 220,
        105, 221, 293, 98, 156, 40, 157, 224, 31, 103, 298, 222, 160, 158, 223, 164, 102, 99, 228, 37, 161, 227, 165,
        41, 225, 168, 159, 226, 35, 42, 34, 229, 163, 297, 39, 231, 230, 232, 162, 167, 170, 234, 38, 166, 169, 233,
    ),
)


def layout(shapes, shards):
    table = []
    unit_at, row_at, flat_at = 0, 0, 0
    starts = [g[0] for g in GROUPS]
    for i, (rows, cols) in enumerate(shapes):
        if i in starts:
            unit_at = -(-unit_at // 16) * 16
        rb, panels = rows // shards, cols // PANEL
        units = rb * cols // 512
        padded = -(-rb // 16) * 16
        table.append((rb, panels, units, unit_at, row_at, padded, flat_at))
        unit_at += units
        row_at += padded * panels
        flat_at += units * shards
    return table, unit_at, row_at


def unit_places(units, table, shards):
    place = jnp.zeros_like(units)
    for _, _, n, first, _, _, lo in table:
        v = units - lo
        here = (v // n) * SHARD_UNITS + first + v % n
        place = jnp.where(v >= 0, here, place)
    return place


def own_units(owners, mine, capacity):
    count = owners.shape[0] // 128
    hit = (owners[:, 0] == mine).reshape(count, 128)
    lane = jnp.arange(128)
    tri = (lane[:, None] <= lane[None, :]).astype(jnp.bfloat16)
    within = jnp.dot(hit.astype(jnp.bfloat16), tri, preferred_element_type=jnp.float32)
    totals = within[:, 127].astype(jnp.int32)
    upto = jnp.sum(jnp.where(jnp.arange(count)[:, None] >= jnp.arange(count)[None, :], totals[None, :], 0), axis=1)
    slot = jnp.arange(capacity, dtype=jnp.int32)
    block = jnp.sum((upto[None, :] <= slot[:, None]).astype(jnp.int32), axis=1)
    pick = block[:, None] == jnp.arange(count)[None, :]
    before = jnp.sum(jnp.where(pick, (upto - totals)[None, :], 0), axis=1)
    row = jnp.dot(pick.astype(jnp.bfloat16), within.astype(jnp.bfloat16), preferred_element_type=jnp.float32)
    rank = (slot - before).astype(jnp.float32)
    at = jnp.sum((row <= rank[:, None]).astype(jnp.int32), axis=1)
    return block * 128 + at, slot < upto[count - 1]


BY_ROWS = (1, 3, 6, 8)


def position_table():
    cols = []
    for width in (DE, DD):
        side = width // 16 * 6
        parts = (width - 2 * side, side, side)
        tab = np.zeros((48, width), np.float64)
        col = 0
        for i, n in enumerate(parts):
            half = n // 2
            freq = 1.0 / 10000.0 ** (np.arange(half) / half)
            ang = np.arange(16)[:, None] * freq[None, :]
            tab[16 * i:16 * i + 16, col:col + n] = np.concatenate([np.sin(ang), np.cos(ang)], axis=1)
            col += n
        cols.append(tab)
    left = np.concatenate(cols, axis=1).astype(np.float32)
    terms = []
    for _ in range(3):
        terms.append(left.astype(ml_dtypes.bfloat16))
        left = left - terms[-1].astype(np.float32)
    return np.stack(terms)


def dot(a, b):
    return jnp.dot(a, b, preferred_element_type=jnp.float32)


def dot_nt(a, b):
    return lax.dot_general(a, b, (((1,), (1,)), ((), ())), preferred_element_type=jnp.float32)


def dot_tn(a, b):
    return lax.dot_general(a, b, (((0,), (0,)), ((), ())), preferred_element_type=jnp.float32)


def lanes(i, n=128):
    return pl.ds(pl.multiple_of(i * n, n), n)


def ln_parts(x):
    c = x - jnp.mean(x, axis=-1, keepdims=True)
    inv = lax.rsqrt(jnp.mean(c * c, axis=-1, keepdims=True) + NORM_EPS)
    return c * inv, inv


def ln_back(up, m, inv, gain):
    s = up * gain
    a = jnp.mean(s, axis=-1, keepdims=True)
    b = jnp.mean(s * m, axis=-1, keepdims=True)
    return inv * (s - a - m * b), jnp.sum(up * m, axis=0, keepdims=True), jnp.sum(up, axis=0, keepdims=True)


class Block:
    def __init__(self, width, heads, size, hidden, first, table, col):
        self.width, self.heads, self.size, self.hidden, self.col = width, heads, size, hidden, col
        self.q, self.o, self.a, self.b = table[first:first + 4]
        self.part = heads // 2 * size
        self.per = 128 // size


def panel(w, t, mat, g, lo=0, num=16):
    rb, _, _, _, at, padded, _ = mat
    rows = pl.ds(pl.multiple_of(at + g * padded, 16), padded)
    v = w[t, lo:lo + num, rows, :] if isinstance(lo, int) else w[t, pl.ds(lo, num), rows, :]
    if padded > rb:
        v = v.astype(jnp.float32)[:, :rb].reshape(num * rb, 128).astype(jnp.bfloat16)
        return v
    return v.reshape(num * rb, 128)


def pair(w, mat, g):
    return jnp.concatenate([panel(w, 0, mat, g), panel(w, 1, mat, g)], axis=1)


def repeat(count, step, f):
    step = max(k for k in range(1, step + 1) if count % k == 0)

    def turn(i, _):
        for k in range(step):
            f(i * step + k)
        return 0

    if step == count:
        turn(0, 0)
    else:
        lax.fori_loop(0, count // step, turn, 0)


def pull(acc, up, w, mat, step):
    count = mat[1]
    step = max(k for k in range(1, step + 1) if count % k == 0)

    def part(i):
        gs = [i * step + k for k in range(step)]
        d = jnp.concatenate([up[:, lanes(o + g)] for g in gs for o in (0, count)], axis=1)
        return dot_nt(d, jnp.concatenate([pair(w, mat, g) for g in gs], axis=1))

    acc[...] = part(0)

    def turn(i, _):
        acc[...] += part(i)
        return 0

    lax.fori_loop(1, count // step, turn, 0)


def block_fwd(b, x, xo, w, gains, biases, same, n1, proj, p, att, ow, m1, i1, n2, m2, i2, act, slope,
              need, keep):
    cols = slice(b.col, b.col + b.width)
    m, inv = ln_parts(x[...])
    m1[...] = m
    i1[...] = jnp.broadcast_to(inv, i1.shape)
    n1[...] = (m * gains[0:1, cols] + biases[0:1, cols]).astype(jnp.bfloat16)
    keep(0)
    yield
    need(0)
    gq = b.q[1]

    def qkv(g):
        r = dot(n1[...], pair(w, b.q, g)).astype(jnp.bfloat16)
        proj[:, lanes(g)] = r[:, :128]
        proj[:, lanes(gq + g)] = r[:, 128:]

    repeat(gq, 9, qkv)
    yield
    np_ = b.part // 128
    lane = lax.broadcasted_iota(jnp.int32, (256, 128), 1)
    masks = [lane // b.size == i for i in range(b.per)]

    def heads(i, _):
        t, j = i // np_, i % np_
        q = proj[:, lanes(t * gq + j)]
        k = proj[:, lanes(t * gq + np_ + j)]
        v = proj[:, lanes(t * gq + 2 * np_ + j)]
        total = jnp.zeros((256, 128), jnp.float32)
        for h in range(b.per):
            z = dot_nt(jnp.where(masks[h], q, 0), k) * b.size ** (-0.5) + same
            e = jnp.exp(z - jnp.max(z, axis=-1, keepdims=True))
            s = e * (1.0 / jnp.sum(e, axis=-1, keepdims=True))
            p[i * b.per + h] = s
            total = total + dot(s.astype(jnp.bfloat16), jnp.where(masks[h], v, 0))
        att[:, lanes(i)] = total.astype(jnp.bfloat16)
        return 0

    lax.fori_loop(0, np_, heads, 0)
    yield
    lax.fori_loop(np_, 2 * np_, heads, 0)
    keep(1)
    yield
    need(1)
    for t in range(2):
        for g in range(b.width // 128):
            ow[t, :, g * 128:(g + 1) * 128] = panel(w, t, b.o, g)
    x1 = x[...] + dot(att[:, :b.part], ow[0]) + dot(att[:, b.part:], ow[1])
    xo[...] = x1
    m, inv = ln_parts(x1)
    m2[...] = m
    i2[...] = jnp.broadcast_to(inv, i2.shape)
    n2[...] = (m * gains[1:2, cols] + biases[1:2, cols]).astype(jnp.bfloat16)
    keep(2)
    yield
    need(2)
    ga = b.a[1]

    def up(g):
        h = dot(n2[...], pair(w, b.a, g))
        big = 0.5 * (1.0 + lax.erf(h * 0.7071067811865476))
        act_v = (h * big).astype(jnp.bfloat16)
        dens = big + h * (0.3989422804014327 * jnp.exp(-0.5 * h * h))
        act[:, lanes(g)] = act_v[:, :128]
        act[:, lanes(ga + g)] = act_v[:, 128:]
        slope[:, lanes(g)] = dens[:, :128]
        slope[:, lanes(ga + g)] = dens[:, 128:]

    repeat(ga, 12, up)
    keep(3)
    yield
    need(3)
    half = b.hidden // 2

    def down(g):
        w0 = jnp.concatenate([panel(w, 0, b.b, 2 * g), panel(w, 0, b.b, 2 * g + 1)], axis=1)
        w1 = jnp.concatenate([panel(w, 1, b.b, 2 * g), panel(w, 1, b.b, 2 * g + 1)], axis=1)
        xo[:, lanes(g, 256)] += dot(act[:, :half], w0) + dot(act[:, half:], w1)

    repeat(b.width // 256, 1, down)


def block_bwd(b, dr, w, gains, same, n1, proj, p, att, ow, m1, i1, n2, m2, i2, act, slope,
              r, dh, r1, dp_out, acc, da, norm_out, keep):
    cols = slice(b.col, b.col + b.width)
    r[...] = dr[...].astype(jnp.bfloat16)
    keep(3)
    half = b.hidden // 2
    rb = b.b[0]
    gb = b.width // 128
    num = 16

    def hidden(i, _):
        t, lo = i // (16 // num), (i % (16 // num)) * num
        wc = jnp.concatenate([panel(w, t, b.b, g, lo, num) for g in range(gb)], axis=1)
        at = lanes(i, num * rb)
        dh[:, at] = (dot_nt(r[...], wc) * slope[:, at]).astype(jnp.bfloat16)
        return 0

    lax.fori_loop(0, 2 * (16 // num), hidden, 0)
    keep(2)
    ga = b.a[1]
    pull(acc, dh, w, b.a, 12)
    dx, dg, db = ln_back(acc[...], m2[...], i2[:, :1], gains[1:2, cols])
    norm_out[1:2, cols] = dg
    norm_out[3:4, cols] = db
    dx1 = dr[...] + dx
    dr[...] = dx1
    r1[...] = dx1.astype(jnp.bfloat16)
    keep(1)
    for t in range(2):
        da[:, t * b.part:(t + 1) * b.part] = dot_nt(r1[...], ow[t]).astype(jnp.bfloat16)
    gq = b.q[1]
    np_ = b.part // 128
    lane = lax.broadcasted_iota(jnp.int32, (256, 128), 1)
    masks = [lane // b.size == i for i in range(b.per)]
    scale = b.size ** (-0.5)

    def heads(i, _):
        t, j = i // np_, i % np_
        q = proj[:, lanes(t * gq + j)]
        k = proj[:, lanes(t * gq + np_ + j)]
        v = proj[:, lanes(t * gq + 2 * np_ + j)]
        up_ = da[:, lanes(i)]
        dq = jnp.zeros((256, 128), jnp.float32)
        dk = jnp.zeros((256, 128), jnp.float32)
        dv = jnp.zeros((256, 128), jnp.float32)
        for h in range(b.per):
            s = p[i * b.per + h]
            u = jnp.where(masks[h], up_, 0)
            dp = dot_nt(u, v)
            dv = dv + dot_tn(s.astype(jnp.bfloat16), u)
            t1 = s * dp
            dz = (t1 - s * jnp.sum(t1, axis=-1, keepdims=True)).astype(jnp.bfloat16)
            dq = dq + dot(dz, jnp.where(masks[h], k, 0))
            dk = dk + dot_tn(dz, jnp.where(masks[h], q, 0))
        dp_out[:, lanes(t * gq + j)] = (dq * scale).astype(jnp.bfloat16)
        dp_out[:, lanes(t * gq + np_ + j)] = (dk * scale).astype(jnp.bfloat16)
        dp_out[:, lanes(t * gq + 2 * np_ + j)] = dv.astype(jnp.bfloat16)
        return 0

    lax.fori_loop(0, 2 * np_, heads, 0)
    keep(0)
    pull(acc, dp_out, w, b.q, 9)
    dx, dg, db = ln_back(acc[...], m1[...], i1[:, :1], gains[0:1, cols])
    norm_out[0:1, cols] = dg
    norm_out[2:3, cols] = db
    dr[...] = dr[...] + dx


ACTS = (DE, DE, DE, FFE, DE, DD, DD, DD, FFD)
GRADS = (3 * DE, DE, FFE, DE, DD, 3 * DD, DD, FFD, DD)


def lookup(pos, tab, cols):
    row = lax.broadcasted_iota(jnp.int32, (48, 256), 0)
    spots = [jnp.concatenate([pos[0, i:i + 1, :], pos[1, i:i + 1, :]], axis=1) for i in range(3)]
    hot = jnp.logical_or(jnp.logical_or(row == spots[0], row == spots[1] + 16), row == spots[2] + 32)
    hot = jnp.where(hot, 1.0, 0.0).astype(jnp.bfloat16)
    return sum(dot_tn(hot, tab[i, :, cols]) for i in range(3))


def tile_mask(tile):
    ids = tile[lax.axis_index("tensor")]
    tiles = jnp.where(lax.broadcasted_iota(jnp.int32, (16, 256), 0) == ids, 1.0, 0.0).astype(jnp.bfloat16)
    return (1.0 - dot_tn(tiles, tiles)) * MASK_FILL


FWD_ACTS = [((256, n), jnp.bfloat16) for n in (DE, DE, DE, FFE)]
FWD_KEPT = [((256, 3 * DE), jnp.bfloat16), ((HE, 256, 256), jnp.float32), ((2, DE // 2, DE), jnp.bfloat16),
            ((256, DE), jnp.float32), ((256, 128), jnp.float32), ((256, DE), jnp.float32), ((256, 128), jnp.float32),
            ((256, FFE), jnp.float32)]


def chain_kernel(table, pos, tile, gains, biases, cot, tab, x2, w_hbm, *refs):
    fwd_hbm, refs = refs[:8], refs[8:]
    dec, dx0, norm_out = refs[:3]
    kept_out = refs[3:17]
    kept = refs[17:31]
    low, n1d, ad, n2d, ud, dpe, r1e, dhe, re, dlow, dpd, r1d, dhd, rd = kept
    fwd, refs = refs[31:39], refs[39:]
    proj_e, pe, ow_e, m1e, i1e, m2e, i2e, se = fwd
    (w, pd, sd, proj_d, da_e, da_d, ow_d, m1d, m2d, i1d, i2d, y, acc_e, acc_d, w_sem, f_sem, out_sem) = refs
    enc_b = Block(DE, HE, HDE, FFE, 0, table, 0)
    dec_b = Block(DD, HD, HDD, FFD, 5, table, DE)
    em = table[4]

    def load(m):
        rows = pl.ds(table[m][4], table[m][1] * table[m][5])
        return pltpu.make_async_copy(w_hbm.at[:, :, rows], w.at[:, :, rows], w_sem.at[m])

    def fetch(i):
        return pltpu.make_async_copy(fwd_hbm[i], fwd[i], f_sem.at[i])

    def store(i):
        return pltpu.make_async_copy(kept[i], kept_out[i], out_sem.at[i])

    for m in (4, 5, 6, 7, 8, 3, 2, 1, 0):
        if m != 1:
            load(m).start()
    for i in range(8):
        fetch(i).start()
    same = tile_mask(tile)
    low[...] = x2[...].astype(jnp.bfloat16)
    store(0).start()
    load(4).wait()
    for g in range(2):
        v = dot(low[...], pair(w, em, g)).astype(jnp.bfloat16).astype(jnp.float32)
        y[:, g * 128:(g + 1) * 128] = v[:, :128]
        y[:, 256 + g * 128:256 + (g + 1) * 128] = v[:, 128:]
    y[...] += lookup(pos, tab, slice(DE, DE + DD))
    for _ in block_fwd(dec_b, y, dec, w, gains, biases, same, n1d, proj_d, pd, ad, ow_d, m1d, i1d, n2d, m2d, i2d, ud, sd,
                       lambda k: load(5 + k).wait(), lambda k: store(1 + k).start()):
        pass
    y[...] = cot[...]
    block_bwd(dec_b, y, w, gains, same, n1d, proj_d, pd, ad, ow_d, m1d, i1d, n2d, m2d, i2d, ud, sd,
              rd, dhd, r1d, dpd, acc_d, da_d, norm_out, lambda k: store(10 + k).start())
    dlow[...] = y[...].astype(jnp.bfloat16)
    store(9).start()
    for g in range(2):
        d = jnp.concatenate([dlow[:, g * 128:(g + 1) * 128], dlow[:, 256 + g * 128:256 + (g + 1) * 128]], axis=1)
        v = dot_nt(d, pair(w, em, g))
        if g == 0:
            dx0[...] = v
        else:
            dx0[...] += v
    for m in (3, 2, 0):
        load(m).wait()
    for i in range(8):
        fetch(i).wait()
    block_bwd(enc_b, dx0, w, gains, same, None, proj_e, pe, None, ow_e, m1e, i1e, None, m2e, i2e, None, se,
              re, dhe, r1e, dpe, acc_e, da_e, norm_out, lambda k: store(5 + k).start())
    for i in range(14):
        store(i).wait()


def chain(pos, tile, gains, biases, cot, full, x2, fwd, table):
    f32, bf16 = jnp.float32, jnp.bfloat16
    S = jax.ShapeDtypeStruct
    outs = [S((256, DD), f32), S((256, DE), f32), S((4, DE + DD), f32)]
    kept = [(256, n) for n in ACTS[4:] + GRADS]
    outs += [S(k, bf16) for k in kept]
    V = pltpu.VMEM
    scratch = [V(k, bf16) for k in kept] + [V(k, t) for k, t in FWD_KEPT] + [
        V((2, 16) + full.shape[-2:], bf16), V((HD, 256, 256), f32), V((256, FFD), f32),
        V((256, 3 * DD), bf16), V((256, DE), bf16), V((256, DD), bf16), V((2, DD // 2, DD), bf16),
        V((256, DD), f32), V((256, DD), f32), V((256, 128), f32), V((256, 128), f32),
        V((256, DD), f32), V((256, DE), f32), V((256, DD), f32),
        pltpu.SemaphoreType.DMA((9,)), pltpu.SemaphoreType.DMA((8,)), pltpu.SemaphoreType.DMA((14,))]
    vmem = pl.BlockSpec(memory_space=pltpu.VMEM)
    hbm = pl.BlockSpec(memory_space=pl.ANY)
    args = (pos, tile, gains, biases, cot, jnp.asarray(position_table()), x2,
            full.reshape(2, 16, full.shape[-2], 128), *fwd)
    return pl.pallas_call(
        partial(chain_kernel, table), out_shape=outs, in_specs=[vmem] * 7 + [hbm] * 9, out_specs=[vmem] * 3 + [hbm] * 14,
        scratch_shapes=scratch, compiler_params=pltpu.CompilerParams(vmem_limit_bytes=63 << 20), name="chain",
        cost_estimate=pl.CostEstimate(flops=8_000_000_000, bytes_accessed=40_000_000, transcendentals=3_000_000),
    )(*args)


def grad_panels(table, m, act, grad, turned, put):
    mat = table[m]
    rb, panels, padded = mat[0], mat[1], mat[5]
    count = act.shape[1]

    def turn(i):
        turned[pl.ds(pl.multiple_of(i * 128, 128), 128), :] = act[:, lanes(i)].T

    repeat(count // 128, 6, turn)

    def place(t, g, v):
        if padded > rb:
            v = v.reshape(16, rb, 128)
            v = jnp.concatenate([v, jnp.zeros((16, padded - rb, 128), jnp.float32)], axis=1).astype(jnp.bfloat16)
        else:
            v = v.astype(jnp.bfloat16).reshape(16, rb, 128)
        put(t, g, v)

    if m in BY_ROWS:
        half = count // 2

        def body(i):
            t, g = i // (panels // 2), i % (panels // 2)
            v = dot(turned[pl.ds(pl.multiple_of(t * half, 128), half), :], grad[:, lanes(g, 256)])
            place(t, 2 * g, v[:, :128])
            place(t, 2 * g + 1, v[:, 128:])

        repeat(panels, 6, body)
    else:
        def body(g):
            d = jnp.concatenate([grad[:, lanes(g)], grad[:, lanes(panels + g)]], axis=1)
            v = dot(turned[:count, :], d)
            place(0, g, v[:, :128])
            place(1, g, v[:, 128:])

        repeat(panels, 6, body)


class Wires:
    def __init__(self, place, sem):
        self.place, self.sem, self.used, self.waits = place, sem, 0, []

    def new(self, n=1):
        self.used += n
        assert self.used <= self.sem.shape[0], self.used
        return self.used - n

    def copy(self, k, src, dst, way):
        return pltpu.make_async_remote_copy(src_ref=src, dst_ref=dst, send_sem=self.sem.at[k], recv_sem=self.sem.at[k + 1],
                                            device_id=self.place.ids[way], device_id_type=MESH)

    def send(self, k, src, dst, way, cond=None):
        cp = self.copy(k, src, dst, way)
        when(cond, cp.start)
        self.waits.append((cond, cp))

    def land(self, k, dst, cond=None):
        when(cond, self.copy(k, dst, dst, "c").wait_recv)

    def drain(self):
        for cond, cp in self.waits:
            when(cond, cp.wait_send)


def edge_slots(order):
    slots, used, shared = {}, 0, {}
    for d, kids in sorted(spread(order).items()):
        for _, way in kids:
            if way in "xy" and order.index("z") < order.index(way):
                key = (way, d[1], d[2])
                if key not in shared:
                    shared[key] = used
                    used += 4
                slots[d, way] = (shared[key], 4)
            else:
                slots[d, way] = (used, 1)
                used += 1
    return slots, used


def beyond(p, way):
    return p.z < 3 if way == "z+" else p.z > 0 if way == "z-" else None


def reduce_events(p, w, order, own, half, bufs, ready, done):
    tree = spread(order)
    pair = {d: w.new(2) for d in tree}
    wire = {d: w.new(2) for d in tree}
    parent = {nd: (d, way) for d, t in tree.items() for nd, way in t}
    slots, _ = edge_slots(order)

    def buffer(up, way):
        first, n = slots[up, way]
        return bufs.at[first + p.z + up[0] if n > 1 else first]

    events = []
    far = sorted(tree, key=lambda d: (-hops(d), d))
    for d in far:
        def act(d=d):
            cond = p.there(d)

            def step():
                acc = own(d)
                ready(d)
                w.land(pair[d], half(d))
                add_rows(acc, half(d))
                for nd, way in tree[d]:
                    buf = buffer(d, way)

                    def take(buf=buf, nd=nd):
                        w.land(wire[nd], buf)
                        add_rows(acc, buf)
                    when(beyond(p, way), take)
            when(cond, step)
            if hops(d) == 0:
                done()
            else:
                up, way = parent[d]
                w.send(wire[d], own(d), buffer(up, way), BACK[way], cond)
        events.append(act)

    def share(give):
        for d in far:
            w.send(pair[d], give(d), half(d), "c", p.there(d))

    return events, share, far


def gather_events(p, w, order, first, at):
    tree = spread(order)
    pair = {d: w.new(2) for d in tree}
    wire = {d: w.new(2) for d in tree}
    events = []
    for d in sorted(tree, key=lambda d: (hops(d), d)):
        def act(d=d):
            cond = p.there(d)
            blk = at(d, p.c)
            if hops(d):
                w.land(wire[d], blk, cond)
                src = blk
            else:
                src = first
            for nd, way in tree[d]:
                w.send(wire[nd], src, blk, way, both(cond, beyond(p, way)))
            w.send(pair[d], src, blk, "c", cond)
        events.append(act)

    def finish():
        for d in tree:
            w.land(pair[d], at(d, 1 - p.c), p.there(d))

    return events, finish


def run_events(lists, order, extra=iter(()), every=8):
    assert sorted(order) == sorted(64 * g + i for g, acts in enumerate(lists) for i in range(len(acts)))
    for n, k in enumerate(order):
        if n % every == 0:
            next(extra, None)
        lists[k // 64][k % 64]()
    for _ in extra:
        pass


def group_span(table, mats):
    first, last = table[mats[0]], table[mats[-1]]
    units = last[3] + last[2] - first[3]
    return first[3], -(-units // 16) * 16, first[4], last[4] + last[1] * last[5] - first[4]


def units_to_panels(table, mats, units, flat, put):
    base, count = table[mats[0]][3], units.shape[0]
    for k in range(4):
        flat[pl.ds(k, count, stride=4), :] = units[:, 128 * k:128 * (k + 1)].astype(jnp.float32)
    for m in mats:
        rb, panels, n, first, _, padded, _ = table[m]
        for g in range(panels):
            v = flat[pl.ds(4 * (first - base) + g, rb, stride=panels), :]
            if padded > rb:
                v = jnp.concatenate([v, jnp.zeros((padded - rb, 128), jnp.float32)], axis=0)
            put(m, g, v.astype(jnp.bfloat16))


def panels_to_units(table, mats, take, flat, units):
    base, count = table[mats[0]][3], units.shape[0]
    used = 0
    for m in mats:
        rb, panels, n, first, _, padded, _ = table[m]
        for g in range(panels):
            flat[pl.ds(4 * (first - base) + g, rb, stride=panels), :] = take(m, g)[:rb]
        used = 4 * (first - base + n)
    if used < 4 * count:
        flat[used:4 * count, :] = jnp.zeros((4 * count - used, 128), jnp.float32)
    for k in range(4):
        units[:, 128 * k:128 * (k + 1)] = flat[pl.ds(k, count, stride=4), :].astype(jnp.bfloat16)


def encoder_steps(p, table, out, tok, pos, x, x2, tile, gains, biases, tab, fwd, fwd_out, wv, w_sem, fwd_sem, swapped, arrived):
    n1, att, n2, act, proj, prob, ow, m1, i1, m2, i2, slope = fwd

    def load(m):
        rows = pl.ds(table[m][4], table[m][1] * table[m][5])
        return pltpu.make_async_copy(out.at[:, :, :, :, rows], wv.at[:, :, :, :, rows], w_sem.at[m])

    def store(i):
        return pltpu.make_async_copy(fwd[i], fwd_out[i], fwd_sem.at[i])

    def keep(k):
        for i in ((0, 7, 8), (1, 4, 5), (2, 6, 9, 10), (3, 11))[k]:
            store(i).start()

    for f in swapped:
        f()
    x[...] = tok[...].reshape(256, DE).astype(jnp.float32) + lookup(pos, tab, slice(0, DE))
    same = tile_mask(tile)
    whole = wv.reshape(2, 16, wv.shape[-2], 128)
    block = block_fwd(Block(DE, HE, HDE, FFE, 0, table, 0), x, x2, whole, gains, biases, same, n1, proj, prob, att, ow, m1, i1, n2,
                      m2, i2, act, slope, lambda k: load(k).wait(), keep)
    next(block)
    yield
    for f in arrived[0]:
        f()
    load(0).start()
    load(1).start()
    yield
    for _ in range(4):
        next(block)
        yield
    for f in arrived[1]:
        f()
    load(2).start()
    yield
    next(block)
    yield
    for f in arrived[2]:
        f()
    load(3).start()
    yield
    for _ in block:
        pass
    yield
    for i in range(12):
        store(i).wait()


class Swap:
    def __init__(self, p, w, src, out, give, keep):
        self.p, self.w, self.src, self.out, self.give, self.keep = p, w, src, out, give, keep
        self.k, self.own = w.new(2), w.new()

    def local(self):
        return pltpu.make_async_copy(self.src.at[self.keep], self.out.at[self.p.x], self.w.sem.at[self.own])

    def start(self):
        self.w.send(self.k, self.src.at[self.give], self.out.at[self.p.x], "x")
        self.local().start()

    def finish(self):
        self.w.land(self.k, self.out.at[1 - self.p.x])
        self.local().wait()


def weights_kernel(table, groups, plan, parts, tok_in, pos_in, cot_in, tile, gains, biases, tab, *refs):
    n = len(groups)
    out, pos, cot, x2 = refs[:4]
    fwd_out, tok, x, fwd, wv, w_sem, fwd_sem = refs[4:16], refs[16], refs[17], refs[18:30], refs[30], refs[31], refs[32]
    rest = refs[33:]
    accs, halves, bufs, shards = (rest[i * n:(i + 1) * n] for i in range(4))
    flat, sem = rest[4 * n:]
    p = Place()
    p.greet(["c", "y", "x"])
    w = Wires(p, sem)
    swaps = [Swap(p, w, a, b, 1 - p.x, p.x) for a, b in ((tok_in, tok), (pos_in, pos), (cot_in, cot))]
    for s in swaps:
        s.start()
    lists, finishes = [], []
    for g, mats in enumerate(groups):
        u0, un, r0, rn = group_span(table, mats)
        acc, half, buf, shard = accs[g], halves[g], bufs[g], shards[g]
        own_sem = w.new()
        loads = {d: w.new() for d in spread(plan[0][g])}

        def own(d, acc=acc):
            return acc.at[p.at(d)[1:]]

        def other(d, half=half):
            return half.at[p.at(d)[1:]]

        def load(d, u0=u0, un=un, own=own, loads=loads):
            return pltpu.make_async_copy(parts.at[p.at(d)[1:] + (p.c, pl.ds(u0, un))], own(d), sem.at[loads[d]])

        def ready(d, load=load):
            load(d).wait()

        def done(mats=mats, acc=acc, shard=shard, r0=r0):
            def put(m, i, v):
                lo = table[m][4] - r0 + i * table[m][5]
                shard[lo:lo + table[m][5], :] = v
            units_to_panels(table, mats, acc.at[p.z, p.y], flat, put)

        ev, share, far = reduce_events(p, w, plan[0][g], own, other, buf, ready, done)

        def begin(load=load, share=share, far=far, u0=u0, un=un):
            share(lambda d: parts.at[p.at(d)[1:] + (1 - p.c, pl.ds(u0, un))])
            for d in far:
                when(p.there(d), load(d).start)

        def at(d, core, r0=r0, rn=rn):
            t, z, y = p.at(d)
            return out.at[t, z, y, core, pl.ds(r0, rn)]

        def local(shard=shard, r0=r0, rn=rn, own_sem=own_sem):
            return pltpu.make_async_copy(shard, out.at[p.x, p.z, p.y, p.c, pl.ds(r0, rn)], sem.at[own_sem])

        ag, finish = gather_events(p, w, plan[1][g], shard, at)

        def send_first(act=ag[0], local=local):
            act()
            local().start()

        lists.append([begin] + ev + [send_first] + ag[1:])
        finishes += [finish, lambda local=local: local().wait()]
    steps = encoder_steps(p, table, out, tok, pos, x, x2, tile, gains, biases, tab, fwd, fwd_out, wv, w_sem, fwd_sem,
                          [s.finish for s in swaps[:2]], [finishes[2 * k:2 * k + 2] for k in range(3)])
    lists.append([partial(next, steps, None)] * 11)
    run_events(lists, plan[2])
    for f in finishes[6:] + [swaps[2].finish]:
        f()
    w.drain()


def spread_weights(parts, tokens, pos, cot, tile, gains, biases, table, rows, groups, plan, ident):
    spans = [group_span(table, m) for m in groups]
    bf16 = jnp.bfloat16
    S = jax.ShapeDtypeStruct
    V = pltpu.VMEM
    fwd = FWD_ACTS + FWD_KEPT
    enc_rows = table[4][4]
    scratch = [V(tokens.shape, tokens.dtype), V((256, DE), jnp.float32)] + [V(k, t) for k, t in fwd]
    scratch += [V((2, 4, 2, 2, enc_rows, 128), bf16), pltpu.SemaphoreType.DMA((4,)), pltpu.SemaphoreType.DMA((12,))]
    scratch += [V((4, 2, s[1], 512), bf16) for s in spans] * 2
    scratch += [V((edge_slots(o)[1], s[1], 512), bf16) for s, o in zip(spans, plan[0])]
    scratch += [V((s[3], 128), bf16) for s in spans]
    scratch += [V((4 * max(s[1] for s in spans), 128), jnp.float32),
                pltpu.SemaphoreType.DMA((len(groups) * (1 + 5 * 14 + 4 * 28) + 9,))]
    hbm = pl.BlockSpec(memory_space=pl.ANY)
    vmem = pl.BlockSpec(memory_space=pltpu.VMEM)
    return pl.pallas_call(
        partial(weights_kernel, table, groups, plan),
        out_shape=[S((2, 4, 2, 2, rows, 128), bf16), S(pos.shape, pos.dtype), S(cot.shape, cot.dtype), S((256, DE), jnp.float32)]
        + [S(k, t) for k, t in fwd],
        in_specs=[hbm] * 4 + [vmem] * 4, out_specs=[hbm, vmem, hbm, vmem] + [hbm] * 12,
        scratch_shapes=scratch,
        compiler_params=pltpu.CompilerParams(collective_id=ident, has_side_effects=True, vmem_limit_bytes=63 << 20),
        name="spread_weights",
    )(parts, tokens, pos, cot, tile, gains, biases, jnp.asarray(position_table()))


def return_kernel(table, groups, plan, *refs):
    n = len(groups)
    kept_in, small_src, dec_in, dx_in, out, small_out, dec, dx = refs[:18], *refs[18:25]
    rest = refs[25:]
    kept, rest = rest[:18], rest[18:]
    acts, grads = kept[:9], kept[9:]
    sides, halves, bufs, units = (rest[i * n:(i + 1) * n] for i in range(4))
    flat, turned, mid, line, load_sem, sem = rest[4 * n:]

    def load(i):
        return pltpu.make_async_copy(kept_in[i], kept[i], load_sem.at[i])

    first = sorted(range(n), key=lambda g: plan[2].index(64 * g))
    for g in first:
        for m in groups[g]:
            load(m).start()
            load(9 + m).start()
    p = Place()
    p.greet(["c", "y", "x"])
    w = Wires(p, sem)
    swaps = [Swap(p, w, a, b, 1 - p.x, p.x) for a, b in ((dec_in, dec), (dx_in, dx))]
    swaps[0].start()
    lists, finishes = [], []
    for g, mats in enumerate(groups):
        u0, un, r0, rn = group_span(table, mats)
        side, half, buf, unit = sides[g], halves[g], bufs[g], units[g]
        own_sem = w.new()

        def own(d, side=side):
            return side.at[(p.c,) + p.at(d)]

        def other(d, half=half):
            return half.at[p.at(d)]

        def done(mats=mats, side=side, unit=unit, r0=r0):
            mine = side.at[p.c, p.x, p.z, p.y]

            def take(m, i):
                lo = table[m][4] - r0 + i * table[m][5]
                return mine[lo:lo + table[m][5], :].astype(jnp.float32)
            panels_to_units(table, mats, take, flat, unit)

        ev, share, far = reduce_events(p, w, plan[0][g], own, other, buf, lambda d: None, done)

        def begin(mats=mats, side=side, share=share, r0=r0):
            for m in mats:
                lo, padded = table[m][4] - r0, table[m][5]

                def put(t, i, v, lo=lo, padded=padded):
                    v = v.reshape(4, 2, 2, padded, 128)
                    rows = pl.ds(pl.multiple_of(lo + i * padded, 16), padded)
                    side[0, t, :, :, rows, :] = v[:, :, 0]
                    side[1, t, :, :, rows, :] = v[:, :, 1]
                load(m).wait()
                load(9 + m).wait()
                grad_panels(table, m, acts[m], grads[m], turned, put)
            share(lambda d: side.at[(1 - p.c,) + p.at(d)])

        def at(d, core, u0=u0, un=un):
            _, z, y = p.at(d)
            return out.at[z, y, core, pl.ds(u0, un)]

        def local(unit=unit, u0=u0, un=un, own_sem=own_sem):
            return pltpu.make_async_copy(unit, out.at[p.z, p.y, p.c, pl.ds(u0, un)], sem.at[own_sem])

        ag, finish = gather_events(p, w, plan[1][g], unit, at)

        def send_first(act=ag[0], local=local):
            act()
            local().start()

        lists.append([begin] + ev + [send_first] + ag[1:])
        finishes += [finish, lambda local=local: local().wait()]
    last = max(plan[2].index(64 * g + len(spread(plan[0][g]))) for g in range(n))
    g, i = plan[2][last] // 64, plan[2][last] % 64
    act = lists[g][i]

    def with_swaps():
        act()
        swaps[1].start()

    lists[g][i] = with_swaps
    run_events(lists, plan[2], total_steps(p, w, small_src, small_out, mid, line))
    for f in finishes + [s.finish for s in swaps]:
        f()
    w.drain()


def total_steps(p, w, src, out, mid, line):
    k = [w.new(2) for _ in range(9)]
    now = src
    for i, way in enumerate(("c", "x", "y")):
        w.send(k[i], now, mid.at[i], way)
        yield
        w.land(k[i], mid.at[i])
        nxt = mid.at[3 + i] if i < 2 else line.at[p.z]
        nxt[...] = now[...] + mid[i]
        now = nxt
    for i in range(4):
        lo, hi = jnp.maximum(p.z - i, 0), jnp.minimum(p.z + i, 3)
        if i > 0:
            w.land(k[2 + i], line.at[lo], p.z >= i)
            w.land(k[5 + i], line.at[hi], p.z + i <= 3)
        if i < 3:
            w.send(k[3 + i], line.at[lo], line.at[lo], "z+", jnp.logical_and(p.z >= i, p.z < 3))
            w.send(k[6 + i], line.at[hi], line.at[hi], "z-", jnp.logical_and(p.z + i <= 3, p.z > 0))
            yield
    out[...] = (line[0] + line[1]) + (line[2] + line[3])


def return_grads(kept, small, dec, dx, table, total_units, groups, plan, ident):
    spans = [group_span(table, m) for m in groups]
    bf16 = jnp.bfloat16
    S = jax.ShapeDtypeStruct
    V = pltpu.VMEM
    scratch = [V(v.shape, v.dtype) for v in kept]
    scratch += [V((2, 2, 4, 2, s[3], 128), bf16) for s in spans]
    scratch += [V((2, 4, 2, s[3], 128), bf16) for s in spans]
    scratch += [V((edge_slots(o)[1], s[3], 128), bf16) for s, o in zip(spans, plan[0])]
    scratch += [V((s[1], 512), bf16) for s in spans]
    scratch += [V((4 * max(s[1] for s in spans), 128), jnp.float32), V((FFE, 256), bf16),
                V((5,) + small.shape, small.dtype), V((4,) + small.shape, small.dtype), pltpu.SemaphoreType.DMA((18,)),
                pltpu.SemaphoreType.DMA((len(groups) * (1 + 4 * 14 + 4 * 28) + 24,))]
    vmem = pl.BlockSpec(memory_space=pltpu.VMEM)
    hbm = pl.BlockSpec(memory_space=pl.ANY)
    return pl.pallas_call(
        partial(return_kernel, table, groups, plan),
        out_shape=(S((4, 2, 2, total_units, 512), bf16), S(small.shape, small.dtype), S(dec.shape, dec.dtype), S(dx.shape, dx.dtype)),
        in_specs=[hbm] * 18 + [vmem, hbm, hbm], out_specs=(hbm, vmem, hbm, hbm),
        scratch_shapes=scratch,
        compiler_params=pltpu.CompilerParams(collective_id=ident, has_side_effects=True, vmem_limit_bytes=63 << 20),
        name="return_grads",
    )(*kept, small, dec, dx)


STEP_ROWS = 432


def update_kernel(place_s, place, spread, master, first, second, total, params, norm_first, norm_second, *refs):
    passed, refs = refs[:2], refs[2:]
    new_master, new_first, new_second, new_norms, new_nf, new_ns = refs[:6]
    i = pl.program_id(0)
    copies = [pltpu.make_async_copy(a, b, refs[8].at[k]) for k, (a, b) in enumerate(zip(passed, refs[6:8]))]

    @pl.when(i == 0)
    def _():
        for c in copies:
            c.start()
        new_norms[...], new_nf[...], new_ns[...] = adamw(params[...], total[...], norm_first[...], norm_second[...], 0.0, NORM_RATE)

    lane = lax.broadcasted_iota(jnp.int32, (16, 256), 1)
    row = lax.broadcasted_iota(jnp.int32, (16, 256), 0)
    for k in range(STEP_ROWS // 16):
        tiles = []
        for j in range(16):
            at = jnp.minimum(place_s[i * STEP_ROWS + 16 * k + j] >> 4, spread.shape[0] // 16 - 1)
            tiles.append(spread[pl.ds(pl.multiple_of(at * 16, 16), 16), :])
        here = slice(16 * k, 16 * k + 16)
        spot = place[here, :]
        used = jnp.logical_and(lane == row * 16 + (spot & 15), spot < spread.shape[0])
        grad = dot(jnp.where(used, 1.0, 0.0).astype(jnp.bfloat16), jnp.concatenate(tiles, axis=0))
        new_master[here, :], new_first[here, :], new_second[here, :] = adamw(
            master[here, :], grad, first[here, :], second[here, :], WEIGHT_DECAY, LEARN_RATE)

    @pl.when(i == pl.num_programs(0) - 1)
    def _():
        for c in copies:
            c.wait()


def update(place, spread, master, first, second, total, params, norm_first, norm_second, passed):
    slots = master.shape[0]
    S = jax.ShapeDtypeStruct
    rows = pl.BlockSpec((STEP_ROWS, 512), lambda i, s: (i, 0))
    whole = lambda v: pl.BlockSpec(v.shape, lambda i, s: (0, 0), pipeline_mode=pl.Buffered(1))
    small = pl.BlockSpec(params.shape, lambda i, s: (0, 0))
    out = [S(master.shape, jnp.float32)] * 3 + [S(params.shape, jnp.float32)] * 3 + [S(v.shape, v.dtype) for v in passed]
    hbm = pl.BlockSpec(memory_space=pl.ANY)
    return pl.pallas_call(
        update_kernel, out_shape=out,
        grid_spec=pltpu.PrefetchScalarGridSpec(
            num_scalar_prefetch=1, grid=(slots // STEP_ROWS,),
            in_specs=[pl.BlockSpec((STEP_ROWS, 1), lambda i, s: (i, 0)), whole(spread), rows, rows, rows, small, small, small, small, hbm, hbm],
            out_specs=[rows] * 3 + [small] * 3 + [hbm, hbm], scratch_shapes=[pltpu.SemaphoreType.DMA((2,))]),
        compiler_params=pltpu.CompilerParams(vmem_limit_bytes=62 << 20), name="update",
    )(place, lax.optimization_barrier(place)[:, None], spread, master, first, second, total, params, norm_first, norm_second, *passed)


def place_kernel(place_s, master, out, wide, staged, sem):
    count = wide.shape[0] // 64 - 1

    def clear(i, _):
        wide[pl.ds(pl.multiple_of(i * 64, 64), 64), :] = jnp.zeros((64, 512), jnp.float32)
        return 0

    lax.fori_loop(0, count, clear, 0)

    def turn(i, _):
        for j in range(16):
            wide[pl.ds(place_s[i * 16 + j], 1), :] = master[pl.ds(i * 16 + j, 1), :]
        return 0

    lax.fori_loop(0, master.shape[0] // 16, turn, 0)
    parts = 4
    part = count // parts * 64

    def copy(k):
        rows = pl.ds(pl.multiple_of(k * part, 64), part)
        return pltpu.make_async_copy(staged.at[rows], out.at[rows], sem.at[k])

    for k in range(parts):
        def narrow(i, _):
            rows = pl.ds(pl.multiple_of(k * part + i * 64, 64), 64)
            staged[rows, :] = wide[rows, :].astype(jnp.bfloat16)
            return 0

        lax.fori_loop(0, part // 64, narrow, 0)
        copy(k).start()
    for k in range(parts):
        copy(k).wait()


def place_blocks(place, master, rows):
    return pl.pallas_call(
        place_kernel, out_shape=jax.ShapeDtypeStruct((rows, 512), jnp.bfloat16),
        grid_spec=pltpu.PrefetchScalarGridSpec(
            num_scalar_prefetch=1, grid=(1,),
            in_specs=[pl.BlockSpec(master.shape, lambda i, s: (0, 0), pipeline_mode=pl.Buffered(1))],
            out_specs=pl.BlockSpec(memory_space=pl.ANY),
            scratch_shapes=[pltpu.VMEM((rows + 64, 512), jnp.float32), pltpu.VMEM((rows, 512), jnp.bfloat16), pltpu.SemaphoreType.DMA((4,))]),
        compiler_params=pltpu.CompilerParams(vmem_limit_bytes=60 << 20), name="place_blocks",
    )(place, master)


def sequence_device(tokens_in, positions, segment_ids, owners, master, first_moment, second_moment, norm_gains,
                    norm_biases, norm_first, norm_second, cotangent):
    shapes = weight_shapes(2)
    table, _, rows = layout(shapes, 16)
    unit, used = own_units(owners, lax.axis_index("dp"), master.shape[0])
    place = jnp.where(used, unit_places(unit, table, 16), 16 * SHARD_UNITS)
    parts = place_blocks(place, master, 16 * SHARD_UNITS)
    full, pos, cot, x2, *fwd = spread_weights(parts.reshape(4, 2, 2, SHARD_UNITS, 512), tokens_in, positions.transpose(1, 0, 2),
                                              cotangent, segment_ids, norm_gains, norm_biases, table, rows, GROUPS, PLAN_OUT, 1)
    kept = chain(pos, segment_ids, norm_gains, norm_biases, cot.reshape(256, DD), full, x2, fwd[4:], table)
    decoded, dx0, norms = kept[:3]
    spread_out, norm_total, decoded, dx0 = return_grads([*fwd[:4], *kept[3:]], norms, decoded.reshape(2, 128, DD), dx0.reshape(2, 128, DE), table,
                                                        SHARD_UNITS, GROUPS, PLAN_BACK, 2)
    norm_params = jnp.concatenate([norm_gains, norm_biases], axis=0)
    new_master, new_first, new_second, new_norms, norm_one_new, norm_two_new, decoded, dx0 = update(
        place, spread_out.reshape(16 * SHARD_UNITS, 512), master, first_moment, second_moment, norm_total, norm_params, norm_first, norm_second,
        (decoded, dx0))
    return (decoded, dx0, new_master, new_first, new_second, new_norms, norm_one_new, norm_two_new)


def solution(mesh):
    step = sequence_device if (mesh.shape["dp"], mesh.shape["tensor"]) == (16, 2) else per_device
    return jax.shard_map(
        step,
        mesh=mesh,
        in_specs=(
            P(None, ("dp", "tensor"), None),
            P(None, None, ("dp", "tensor")),
            P(None, "dp", None),
            P(),
            P("dp", "tensor"),
            P("dp", "tensor"),
            P("dp", "tensor"),
            P(),
            P(),
            P(),
            P(),
            P(None, ("dp", "tensor"), None),
        ),
        out_specs=(
            P(None, ("dp", "tensor"), None),
            P(None, ("dp", "tensor"), None),
            P("dp", "tensor"),
            P("dp", "tensor"),
            P("dp", "tensor"),
            P(),
            P(),
            P(),
        ),
        check_vma=False,
    )
```

```python
from functools import partial

import jax
import jax.numpy as jnp
import ml_dtypes
import numpy as np
from jax import lax
from jax.experimental import pallas as pl
from jax.experimental.pallas import tpu as pltpu
from jax.sharding import PartitionSpec as P

DE = 768
HE = 12
HDE = 64
FFE = 3072
DD = 512
HD = 16
HDD = 32
FFD = 2048
STEP = 10


NORM_EPS = 1e-06
BETA_ONE = 0.5
BETA_TWO = 0.5
LEARN_RATE = 0.03
NORM_RATE = 0.3
WEIGHT_DECAY = 0.05
ADAM_EPS = 1e-08
MASK_FILL = -1000000000.0


def sincos_part(coordinate, part_width):
    halfway = part_width // 2
    frequency = 1.0 / 10000.0 ** (jnp.arange(halfway, dtype=jnp.float32) / halfway)
    angles = coordinate.astype(jnp.float32)[:, None] * frequency[None, :]
    return jnp.concatenate([jnp.sin(angles), jnp.cos(angles)], axis=1)


def sincos_embed(positions, model_width):
    side_width = model_width // 16 * 6
    first_width = model_width - 2 * side_width
    return jnp.concatenate(
        [
            sincos_part(positions[0], first_width),
            sincos_part(positions[1], side_width),
            sincos_part(positions[2], side_width),
        ],
        axis=1,
    )


def slot_table(owners, devices, capacity):
    owner_ids = owners[:, 0]
    onehot = (owner_ids[:, None] == jnp.arange(devices, dtype=jnp.int32)[None, :]).astype(jnp.int32)
    before = jnp.cumsum(onehot, axis=0) - onehot
    owner_rank = jnp.sum(before * onehot, axis=1)
    return owner_ids * capacity + owner_rank


def weight_shapes(tensor_count):
    enc_heads = HE // tensor_count
    dec_heads = HD // tensor_count
    return [
        (DE, 3 * enc_heads * HDE),
        (enc_heads * HDE, DE),
        (DE, FFE // tensor_count),
        (FFE // tensor_count, DE),
        (DE, DD // tensor_count),
        (DD, 3 * dec_heads * HDD),
        (dec_heads * HDD, DD),
        (DD, FFD // tensor_count),
        (FFD // tensor_count, DD),
    ]


def split_flat(flat_vector, shapes):
    pieces = []
    offset = 0
    for matrix_shape in shapes:
        length = matrix_shape[0] * matrix_shape[1]
        pieces.append(flat_vector[offset : offset + length].reshape(matrix_shape))
        offset += length
    return pieces


def adamw(weights, gradient, moment_one, moment_two, decay_rate, step_rate):
    one_new = BETA_ONE * moment_one + (1.0 - BETA_ONE) * gradient
    two_new = BETA_TWO * moment_two + (1.0 - BETA_TWO) * gradient * gradient
    one_hat = one_new / (1.0 - BETA_ONE**STEP)
    two_hat = two_new / (1.0 - BETA_TWO**STEP)
    weights_new = weights - step_rate * (
        one_hat / (jnp.sqrt(two_hat) + ADAM_EPS) + decay_rate * weights
    )
    return (weights_new, one_new, two_new)


def norm_forward(values, gain_row, bias_row):
    center = values - jnp.mean(values, axis=-1, keepdims=True)
    spread = jnp.mean(center * center, axis=-1, keepdims=True)
    inverse = lax.rsqrt(spread + NORM_EPS)
    normed = center * inverse
    return (normed * gain_row + bias_row, (normed, inverse))


def norm_backward(upstream, stored, gain_row):
    normed, inverse = stored
    scaled = upstream * gain_row
    mean_one = jnp.mean(scaled, axis=-1, keepdims=True)
    mean_two = jnp.mean(scaled * normed, axis=-1, keepdims=True)
    return (
        inverse * (scaled - mean_one - normed * mean_two),
        jnp.sum(upstream * normed, axis=0),
        jnp.sum(upstream, axis=0),
    )


def inner_rows(left_side, right_side):
    return lax.dot_general(
        left_side, right_side, (((0,), (0,)), ((), ())), preferred_element_type=jnp.float32
    )


def times_transpose(left_side, right_side):
    return lax.dot_general(
        left_side, right_side, (((1,), (1,)), ((), ())), preferred_element_type=jnp.float32
    )


def gather_rows(values):
    return lax.all_gather(values, "tensor", axis=0, tiled=True)


def gather_grads(values):
    return lax.all_gather(values, "tensor", axis=0, tiled=True)


def branch_rows(values, weight):
    return lax.psum_scatter(
        jnp.dot(values, weight, preferred_element_type=jnp.float32).astype(jnp.bfloat16),
        "tensor",
        scatter_dimension=0,
        tiled=True,
    ).astype(jnp.float32)


def input_rows(values, weight):
    return lax.psum_scatter(
        times_transpose(values, weight).astype(jnp.bfloat16),
        "tensor",
        scatter_dimension=0,
        tiled=True,
    ).astype(jnp.float32)


def block_scores(queries, key_rows, mask_bias, block_start, block_rows, head_size):
    scores = jnp.einsum(
        "qhd,khd->hqk", queries, key_rows, preferred_element_type=jnp.float32
    ) * head_size ** (-0.5)
    return scores + mask_bias[None, block_start : block_start + block_rows]


def attention_forward(gathered, w_qkv, head_count, head_size, mask_bias):
    length = gathered.shape[0]
    projected = jnp.dot(gathered, w_qkv, preferred_element_type=jnp.float32).astype(jnp.bfloat16)
    projected = projected.reshape(length, 3, head_count, head_size)
    queries = projected[:, 0]
    key_rows = projected[:, 1]
    value_rows = projected[:, 2]
    block_rows = min(512, length)
    scores = block_scores(queries, key_rows, mask_bias, 0, block_rows, head_size)
    row_peak = jnp.max(scores, axis=-1, keepdims=True)
    row_total = row_peak + jnp.log(jnp.sum(jnp.exp(scores - row_peak), axis=-1, keepdims=True))
    weights = jnp.exp(scores - row_total).astype(jnp.bfloat16)
    outputs = jnp.einsum("hqk,khd->qhd", weights, value_rows, preferred_element_type=jnp.float32)
    totals = [row_total]
    attended = outputs.astype(jnp.bfloat16).reshape(length, head_count * head_size)
    return (attended, (queries, key_rows, value_rows, totals))


def attention_backward(upstream, w_out, attended, stored, head_count, head_size, mask_bias):
    queries, key_rows, value_rows, totals = stored
    length = upstream.shape[0]
    score_scale = head_size ** (-0.5)
    grad_out = inner_rows(attended, upstream)
    attended_grad = (
        times_transpose(upstream, w_out).astype(jnp.bfloat16).reshape(length, head_count, head_size)
    )
    block_rows = min(512, length)
    key_grads = jnp.zeros((length, head_count, head_size), jnp.float32)
    value_grads = jnp.zeros((length, head_count, head_size), jnp.float32)
    query_grads = []
    for number, block_start in enumerate(range(0, length, block_rows)):
        scores = block_scores(queries, key_rows, mask_bias, block_start, block_rows, head_size)
        weights = jnp.exp(scores - totals[number])
        value_grads = jnp.einsum(
            "hqk,qhd->khd",
            weights.astype(jnp.bfloat16),
            attended_grad,
            preferred_element_type=jnp.float32,
        )
        weight_grads = jnp.einsum(
            "qhd,khd->hqk", attended_grad, value_rows, preferred_element_type=jnp.float32
        )
        score_grads = (
            weights * (weight_grads - jnp.sum(weights * weight_grads, axis=-1, keepdims=True))
        ).astype(jnp.bfloat16)
        query_grads.append(
            jnp.einsum("hqk,khd->qhd", score_grads, key_rows, preferred_element_type=jnp.float32)
            * score_scale
        )
        key_grads = (
            jnp.einsum("hqk,qhd->khd", score_grads, queries, preferred_element_type=jnp.float32)
            * score_scale
        )
    projected_grad = jnp.stack([query_grads[0], key_grads, value_grads], axis=1)
    return (
        projected_grad.astype(jnp.bfloat16).reshape(length, 3 * head_count * head_size),
        grad_out,
    )


def block_forward(residual, matrices, gain_rows, bias_rows, head_count, head_size, mask_bias):
    w_qkv, w_out, w_in, w_down = matrices
    normed, norm_one = norm_forward(residual, gain_rows[0], bias_rows[0])
    gathered = gather_rows(normed.astype(jnp.bfloat16))
    attended, stored = attention_forward(gathered, w_qkv, head_count, head_size, mask_bias)
    middle = residual + branch_rows(attended, w_out)
    normed_two, norm_two = norm_forward(middle, gain_rows[1], bias_rows[1])
    gathered_two = gather_rows(normed_two.astype(jnp.bfloat16))
    hidden = jnp.dot(gathered_two, w_in, preferred_element_type=jnp.float32)
    active = jax.nn.gelu(hidden, approximate=False).astype(jnp.bfloat16)
    result = middle + branch_rows(active, w_down)
    return (result, (gathered, norm_one, attended, stored, gathered_two, norm_two, hidden, active))


def block_backward(upstream, matrices, gain_rows, saved_values, head_count, head_size, mask_bias):
    w_qkv, w_out, w_in, w_down = matrices
    gathered, norm_one, attended, stored, gathered_two, norm_two, hidden, active = saved_values
    down_full = gather_grads(upstream.astype(jnp.bfloat16))
    grad_down = inner_rows(active, down_full)
    active_grad = times_transpose(down_full, w_down)
    gelu_pull = jax.vjp(partial(jax.nn.gelu, approximate=False), hidden)[1]
    hidden_grad = gelu_pull(active_grad)[0].astype(jnp.bfloat16)
    grad_in = inner_rows(gathered_two, hidden_grad)
    normed_two_grad = input_rows(hidden_grad, w_in)
    middle_grad, gain_two, bias_two = norm_backward(normed_two_grad, norm_two, gain_rows[1])
    middle_grad = upstream + middle_grad
    middle_full = gather_grads(middle_grad.astype(jnp.bfloat16))
    projected_grad, grad_out = attention_backward(
        middle_full, w_out, attended, stored, head_count, head_size, mask_bias
    )
    grad_qkv = inner_rows(gathered, projected_grad)
    normed_grad = input_rows(projected_grad, w_qkv)
    input_grad, gain_one, bias_one = norm_backward(normed_grad, norm_one, gain_rows[0])
    return (
        middle_grad + input_grad,
        [grad_qkv, grad_out, grad_in, grad_down],
        (gain_one, gain_two, bias_one, bias_two),
    )


def embed_forward(residual, w_embed):
    residual_low = gather_rows(residual.astype(jnp.bfloat16))
    columns = jnp.dot(residual_low, w_embed, preferred_element_type=jnp.float32).astype(
        jnp.bfloat16
    )
    own_columns = lax.all_to_all(columns, "tensor", split_axis=0, concat_axis=1, tiled=True)
    return (own_columns.astype(jnp.float32), residual_low)


def embed_backward(upstream, residual_low, w_embed):
    columns = lax.all_to_all(
        upstream.astype(jnp.bfloat16), "tensor", split_axis=1, concat_axis=0, tiled=True
    )
    grad_embed = inner_rows(residual_low, columns)
    return (input_rows(columns, w_embed), grad_embed)


def slot_builder(gradients, unit_of_slot, unit_width):
    flat_units = jnp.concatenate([gradient.reshape(-1) for gradient in gradients]).reshape(
        -1, unit_width
    )
    unit_total = flat_units.shape[0]
    source = jnp.take(flat_units, jnp.clip(unit_of_slot, 0, unit_total - 1), axis=0)
    return jnp.where((unit_of_slot >= 0)[:, None], source, 0.0)


def per_device(
    tokens_in,
    positions,
    segment_ids,
    owners,
    master,
    first_moment,
    second_moment,
    norm_gains,
    norm_biases,
    norm_first,
    norm_second,
    cotangent,
):
    devices = lax.axis_size("dp")
    tensor_count = lax.axis_size("tensor")
    capacity = master.shape[0]
    unit_width = master.shape[1]
    unit_count = owners.shape[0]
    slot_index = slot_table(owners, devices, capacity)
    unit_of_slot = (
        jnp.full((devices * capacity,), -1, jnp.int32)
        .at[slot_index]
        .set(jnp.arange(unit_count, dtype=jnp.int32))
    )
    targets = unit_of_slot
    targets = jnp.where(targets < 0, unit_count, targets)
    placed = (
        jnp.zeros((unit_count, unit_width), jnp.bfloat16)
        .at[targets]
        .set(lax.all_gather(master.astype(jnp.bfloat16), "dp", axis=0, tiled=True), mode="drop")
    )
    shapes = weight_shapes(tensor_count)
    matrices = split_flat(placed.reshape(-1), shapes)
    encoder = matrices[0:4]
    w_embed = matrices[4]
    decoder = matrices[5:9]
    enc_heads = HE // tensor_count
    dec_heads = HD // tensor_count
    micro_count = tokens_in.shape[0]
    grad_sums = [jnp.zeros(matrix_shape, jnp.float32) for matrix_shape in shapes]
    norm_sums = jnp.zeros((4, DE + DD), jnp.float32)
    decoded_rows = []
    token_grads = []
    for micro_step in range(micro_count):
        tile_ids = segment_ids[micro_step, 0]
        mask_bias = jnp.where(tile_ids[:, None] == tile_ids[None, :], 0.0, MASK_FILL).astype(
            jnp.float32
        )
        position_now = positions[:, micro_step]
        residual = tokens_in[micro_step].astype(jnp.float32) + sincos_embed(position_now, DE)
        residual, enc_saved = block_forward(
            residual, encoder, norm_gains[:, :DE], norm_biases[:, :DE], enc_heads, HDE, mask_bias
        )
        residual, embed_low = embed_forward(residual, w_embed)
        residual = residual + sincos_embed(position_now, DD)
        residual, dec_saved = block_forward(
            residual, decoder, norm_gains[:, DE:], norm_biases[:, DE:], dec_heads, HDD, mask_bias
        )
        decoded_rows.append(residual)
        upstream, dec_grads, dec_norm = block_backward(
            cotangent[micro_step], decoder, norm_gains[:, DE:], dec_saved, dec_heads, HDD, mask_bias
        )
        upstream, grad_embed = embed_backward(upstream, embed_low, w_embed)
        upstream, enc_grads, enc_norm = block_backward(
            upstream, encoder, norm_gains[:, :DE], enc_saved, enc_heads, HDE, mask_bias
        )
        token_grads.append(upstream)
        step_grads = enc_grads + [grad_embed] + dec_grads
        step_norm = jnp.concatenate([jnp.stack(enc_norm), jnp.stack(dec_norm)], axis=1)
        grad_sums = [total_grad + new_grad for total_grad, new_grad in zip(grad_sums, step_grads)]
        norm_sums = norm_sums + step_norm
    reduced = lax.psum_scatter(
        slot_builder(grad_sums, unit_of_slot, unit_width), "dp", scatter_dimension=0, tiled=True
    )
    norm_total = lax.psum(norm_sums, ("dp", "tensor"))
    new_master, new_first, new_second = adamw(
        master, reduced, first_moment, second_moment, WEIGHT_DECAY, LEARN_RATE
    )
    norm_params = jnp.concatenate([norm_gains, norm_biases], axis=0)
    new_norms, norm_one_new, norm_two_new = adamw(
        norm_params, norm_total, norm_first, norm_second, 0.0, NORM_RATE
    )
    return (
        jnp.stack(decoded_rows),
        jnp.stack(token_grads),
        new_master,
        new_first,
        new_second,
        new_norms,
        norm_one_new,
        norm_two_new,
    )


MESH = pl.DeviceIdType.MESH
ALL = slice(None)


class Place:
    def __init__(self):
        self.d = lax.axis_index("dp")
        self.x = lax.axis_index("tensor")
        self.z = self.d // 4
        self.y = (self.d // 2) % 2
        self.c = self.d % 2
        self.ids = {
            "c": (self.d + 1 - 2 * self.c, self.x),
            "y": (self.d + 2 - 4 * self.y, self.x),
            "x": (self.d, 1 - self.x),
            "z+": (self.d + 4, self.x),
            "z-": (self.d - 4, self.x),
        }

    def greet(self, kinds):
        bar = pltpu.get_barrier_semaphore()
        for k in kinds:
            pl.semaphore_signal(bar, inc=1, device_id=self.ids[k], device_id_type=MESH)

        @pl.when(self.z < 3)
        def _():
            pl.semaphore_signal(bar, inc=1, device_id=self.ids["z+"], device_id_type=MESH)

        @pl.when(self.z > 0)
        def _():
            pl.semaphore_signal(bar, inc=1, device_id=self.ids["z-"], device_id_type=MESH)

        inner = jnp.where(jnp.logical_and(self.z > 0, self.z < 3), 1, 0)
        pl.semaphore_wait(bar, len(kinds) + 1 + inner)

    def there(self, disp):
        dz = disp[0]
        if dz == 0:
            return None
        return self.z + dz <= 3 if dz > 0 else self.z + dz >= 0

    def at(self, disp):
        dz, fy, fx = disp
        return (1 - self.x if fx else self.x, self.z + dz, 1 - self.y if fy else self.y)


def when(cond, f):
    if cond is None:
        f()
    else:
        pl.when(cond)(f)


def both(a, b):
    if a is None:
        return b
    if b is None:
        return a
    return jnp.logical_and(a, b)


def spread(order):
    out = {}
    todo = [((0, 0, 0), -1, 0)]
    while todo:
        (dz, fy, fx), last, way = todo.pop(0)
        nxt = []
        for i, a in enumerate(order):
            if i < last:
                continue
            if a == "z":
                for s in (1, -1):
                    if i == last and s != way:
                        continue
                    n = (dz - s, fy, fx)
                    if abs(n[0]) <= 3:
                        nxt.append((n, "z+" if s > 0 else "z-", i, s))
            elif i > last:
                n = (dz, 1, fx) if a == "y" else (dz, fy, 1)
                nxt.append((n, a, i, 0))
        out[(dz, fy, fx)] = [(n, w) for n, w, _, _ in nxt]
        todo += [(n, i, s) for n, _, i, s in nxt]
    return out


def hops(d):
    return abs(d[0]) + d[1] + d[2]


BACK = {"z+": "z-", "z-": "z+", "x": "x", "y": "y"}


def add_rows(acc, got, step=80):
    n = acc.shape[0]
    while n % step:
        step -= 16

    def body(i, _):
        r = pl.ds(pl.multiple_of(i * step, step), step)
        acc[r, :] = acc[r, :] + got[r, :]
        return 0

    lax.fori_loop(0, n // step, body, 0)


SHARD_UNITS = 656
PANEL = 128
GROUPS = ((0, 1), (2,), (3,), (4, 5, 6), (7, 8))

PLAN_OUT = (
    ("zy", "yz", "zy", "yz", "yz"),
    ("zyx", "zxy", "zyx", "yzx", "xzy"),
    (
        64, 65, 66, 0, 70, 1, 128, 2, 4, 5, 6, 137, 68, 3, 8, 9, 12, 7, 192, 130, 256, 140, 69, 10, 73, 129, 133, 136,
        13, 11, 74, 72, 67, 262, 14, 15, 71, 134, 131, 77, 132, 19, 76, 18, 75, 16, 320, 26, 135, 24, 138, 20, 78, 79,
        22, 141, 139, 195, 34, 257, 27, 81, 32, 193, 258, 25, 80, 35, 259, 83, 142, 143, 90, 30, 194, 266, 82, 196,
        39, 40, 144, 199, 84, 197, 260, 198, 263, 148, 147, 200, 261, 264, 31, 201, 202, 203, 98, 33, 29, 28, 42, 91,
        21, 155, 154, 36, 265, 204, 205, 269, 23, 268, 157, 267, 206, 164, 207, 86, 162, 17, 92, 103, 38, 88, 270, 37,
        271, 41, 210, 106, 161, 104, 96, 85, 99, 146, 150, 321, 322, 275, 160, 272, 211, 323, 273, 89, 153, 324, 100,
        101, 276, 208, 105, 168, 97, 165, 282, 217, 163, 218, 95, 209, 93, 87, 152, 214, 166, 325, 94, 151, 167, 102,
        280, 169, 290, 326, 277, 327, 159, 170, 225, 145, 221, 226, 216, 149, 156, 279, 158, 288, 212, 284, 328, 283,
        278, 228, 329, 295, 291, 213, 223, 219, 285, 232, 220, 330, 224, 296, 286, 292, 274, 289, 233, 230, 234, 229,
        281, 287, 222, 227, 231, 215, 294, 293, 298, 297,
    ),
)
PLAN_BACK = (
    ("zxy", "yzx", "zyx", "yzx", "xzy"),
    ("zy", "zy", "zy", "yz", "yz"),
    (
        256, 257, 258, 262, 261, 269, 64, 259, 67, 260, 65, 69, 263, 66, 78, 264, 271, 278, 276, 77, 270, 268, 267,
        71, 70, 275, 282, 85, 72, 266, 76, 265, 192, 82, 68, 199, 277, 73, 0, 84, 274, 74, 272, 5, 273, 80, 75, 279,
        6, 79, 13, 128, 204, 1, 281, 2, 12, 89, 283, 280, 11, 141, 129, 19, 8, 83, 4, 195, 86, 193, 87, 3, 134, 15, 7,
        81, 284, 285, 133, 88, 91, 14, 10, 197, 194, 90, 22, 196, 132, 286, 131, 201, 288, 287, 130, 16, 18, 21, 198,
        9, 92, 20, 205, 93, 291, 202, 200, 290, 136, 289, 143, 292, 26, 140, 208, 150, 206, 17, 94, 23, 135, 25, 212,
        213, 294, 95, 142, 203, 96, 24, 138, 148, 139, 207, 137, 211, 27, 214, 210, 100, 97, 295, 144, 215, 149, 104,
        146, 209, 147, 28, 29, 151, 218, 219, 217, 145, 154, 32, 101, 153, 106, 30, 216, 36, 155, 152, 296, 33, 220,
        105, 221, 293, 98, 156, 40, 157, 224, 31, 103, 298, 222, 160, 158, 223, 164, 102, 99, 228, 37, 161, 227, 165,
        41, 225, 168, 159, 226, 35, 42, 34, 229, 163, 297, 39, 231, 230, 232, 162, 167, 170, 234, 38, 166, 169, 233,
    ),
)


def layout(shapes, shards):
    table = []
    unit_at, row_at, flat_at = 0, 0, 0
    starts = [g[0] for g in GROUPS]
    for i, (rows, cols) in enumerate(shapes):
        if i in starts:
            unit_at = -(-unit_at // 16) * 16
        rb, panels = rows // shards, cols // PANEL
        units = rb * cols // 512
        padded = -(-rb // 16) * 16
        table.append((rb, panels, units, unit_at, row_at, padded, flat_at))
        unit_at += units
        row_at += padded * panels
        flat_at += units * shards
    return table, unit_at, row_at


def unit_places(units, table, shards):
    place = jnp.zeros_like(units)
    for _, _, n, first, _, _, lo in table:
        v = units - lo
        here = (v // n) * SHARD_UNITS + first + v % n
        place = jnp.where(v >= 0, here, place)
    return place


def own_units(owners, mine, capacity):
    count = owners.shape[0] // 128
    hit = (owners[:, 0] == mine).reshape(count, 128)
    lane = jnp.arange(128)
    tri = (lane[:, None] <= lane[None, :]).astype(jnp.bfloat16)
    within = jnp.dot(hit.astype(jnp.bfloat16), tri, preferred_element_type=jnp.float32)
    totals = within[:, 127].astype(jnp.int32)
    upto = jnp.sum(jnp.where(jnp.arange(count)[:, None] >= jnp.arange(count)[None, :], totals[None, :], 0), axis=1)
    slot = jnp.arange(capacity, dtype=jnp.int32)
    block = jnp.sum((upto[None, :] <= slot[:, None]).astype(jnp.int32), axis=1)
    pick = block[:, None] == jnp.arange(count)[None, :]
    before = jnp.sum(jnp.where(pick, (upto - totals)[None, :], 0), axis=1)
    row = jnp.dot(pick.astype(jnp.bfloat16), within.astype(jnp.bfloat16), preferred_element_type=jnp.float32)
    rank = (slot - before).astype(jnp.float32)
    at = jnp.sum((row <= rank[:, None]).astype(jnp.int32), axis=1)
    return block * 128 + at, slot < upto[count - 1]


BY_ROWS = (1, 3, 6, 8)


def position_table():
    cols = []
    for width in (DE, DD):
        side = width // 16 * 6
        parts = (width - 2 * side, side, side)
        tab = np.zeros((48, width), np.float64)
        col = 0
        for i, n in enumerate(parts):
            half = n // 2
            freq = 1.0 / 10000.0 ** (np.arange(half) / half)
            ang = np.arange(16)[:, None] * freq[None, :]
            tab[16 * i:16 * i + 16, col:col + n] = np.concatenate([np.sin(ang), np.cos(ang)], axis=1)
            col += n
        cols.append(tab)
    left = np.concatenate(cols, axis=1).astype(np.float32)
    terms = []
    for _ in range(3):
        terms.append(left.astype(ml_dtypes.bfloat16))
        left = left - terms[-1].astype(np.float32)
    return np.stack(terms)


def dot(a, b):
    return jnp.dot(a, b, preferred_element_type=jnp.float32)


def dot_nt(a, b):
    return lax.dot_general(a, b, (((1,), (1,)), ((), ())), preferred_element_type=jnp.float32)


def dot_tn(a, b):
    return lax.dot_general(a, b, (((0,), (0,)), ((), ())), preferred_element_type=jnp.float32)


def lanes(i, n=128):
    return pl.ds(pl.multiple_of(i * n, n), n)


def ln_parts(x):
    c = x - jnp.mean(x, axis=-1, keepdims=True)
    inv = lax.rsqrt(jnp.mean(c * c, axis=-1, keepdims=True) + NORM_EPS)
    return c * inv, inv


def ln_back(up, m, inv, gain):
    s = up * gain
    a = jnp.mean(s, axis=-1, keepdims=True)
    b = jnp.mean(s * m, axis=-1, keepdims=True)
    return inv * (s - a - m * b), jnp.sum(up * m, axis=0, keepdims=True), jnp.sum(up, axis=0, keepdims=True)


class Block:
    def __init__(self, width, heads, size, hidden, first, table, col):
        self.width, self.heads, self.size, self.hidden, self.col = width, heads, size, hidden, col
        self.q, self.o, self.a, self.b = table[first:first + 4]
        self.part = heads // 2 * size
        self.per = 128 // size


def panel(w, t, mat, g, lo=0, num=16):
    rb, _, _, _, at, padded, _ = mat
    rows = pl.ds(pl.multiple_of(at + g * padded, 16), padded)
    v = w[t, lo:lo + num, rows, :] if isinstance(lo, int) else w[t, pl.ds(lo, num), rows, :]
    if padded > rb:
        v = v.astype(jnp.float32)[:, :rb].reshape(num * rb, 128).astype(jnp.bfloat16)
        return v
    return v.reshape(num * rb, 128)


def pair(w, mat, g):
    return jnp.concatenate([panel(w, 0, mat, g), panel(w, 1, mat, g)], axis=1)


def repeat(count, step, f):
    step = max(k for k in range(1, step + 1) if count % k == 0)

    def turn(i, _):
        for k in range(step):
            f(i * step + k)
        return 0

    if step == count:
        turn(0, 0)
    else:
        lax.fori_loop(0, count // step, turn, 0)


def pull(acc, up, w, mat, step):
    count = mat[1]
    step = max(k for k in range(1, step + 1) if count % k == 0)

    def part(i):
        gs = [i * step + k for k in range(step)]
        d = jnp.concatenate([up[:, lanes(o + g)] for g in gs for o in (0, count)], axis=1)
        return dot_nt(d, jnp.concatenate([pair(w, mat, g) for g in gs], axis=1))

    acc[...] = part(0)

    def turn(i, _):
        acc[...] += part(i)
        return 0

    lax.fori_loop(1, count // step, turn, 0)


def block_fwd(b, x, xo, w, gains, biases, same, n1, proj, p, att, ow, m1, i1, n2, m2, i2, act, slope,
              need, keep):
    cols = slice(b.col, b.col + b.width)
    m, inv = ln_parts(x[...])
    m1[...] = m
    i1[...] = jnp.broadcast_to(inv, i1.shape)
    n1[...] = (m * gains[0:1, cols] + biases[0:1, cols]).astype(jnp.bfloat16)
    keep(0)
    yield
    need(0)
    gq = b.q[1]

    def qkv(g):
        r = dot(n1[...], pair(w, b.q, g)).astype(jnp.bfloat16)
        proj[:, lanes(g)] = r[:, :128]
        proj[:, lanes(gq + g)] = r[:, 128:]

    repeat(gq, 9, qkv)
    yield
    np_ = b.part // 128
    lane = lax.broadcasted_iota(jnp.int32, (256, 128), 1)
    masks = [lane // b.size == i for i in range(b.per)]

    def heads(i, _):
        t, j = i // np_, i % np_
        q = proj[:, lanes(t * gq + j)]
        k = proj[:, lanes(t * gq + np_ + j)]
        v = proj[:, lanes(t * gq + 2 * np_ + j)]
        total = jnp.zeros((256, 128), jnp.float32)
        for h in range(b.per):
            z = dot_nt(jnp.where(masks[h], q, 0), k) * b.size ** (-0.5) + same
            e = jnp.exp(z - jnp.max(z, axis=-1, keepdims=True))
            s = e * (1.0 / jnp.sum(e, axis=-1, keepdims=True))
            p[i * b.per + h] = s
            total = total + dot(s.astype(jnp.bfloat16), jnp.where(masks[h], v, 0))
        att[:, lanes(i)] = total.astype(jnp.bfloat16)
        return 0

    lax.fori_loop(0, np_, heads, 0)
    yield
    lax.fori_loop(np_, 2 * np_, heads, 0)
    keep(1)
    yield
    need(1)
    for t in range(2):
        for g in range(b.width // 128):
            ow[t, :, g * 128:(g + 1) * 128] = panel(w, t, b.o, g)
    x1 = x[...] + dot(att[:, :b.part], ow[0]) + dot(att[:, b.part:], ow[1])
    xo[...] = x1
    m, inv = ln_parts(x1)
    m2[...] = m
    i2[...] = jnp.broadcast_to(inv, i2.shape)
    n2[...] = (m * gains[1:2, cols] + biases[1:2, cols]).astype(jnp.bfloat16)
    keep(2)
    yield
    need(2)
    ga = b.a[1]

    def up(g):
        h = dot(n2[...], pair(w, b.a, g))
        big = 0.5 * (1.0 + lax.erf(h * 0.7071067811865476))
        act_v = (h * big).astype(jnp.bfloat16)
        dens = big + h * (0.3989422804014327 * jnp.exp(-0.5 * h * h))
        act[:, lanes(g)] = act_v[:, :128]
        act[:, lanes(ga + g)] = act_v[:, 128:]
        slope[:, lanes(g)] = dens[:, :128]
        slope[:, lanes(ga + g)] = dens[:, 128:]

    repeat(ga, 12, up)
    keep(3)
    yield
    need(3)
    half = b.hidden // 2

    def down(g):
        w0 = jnp.concatenate([panel(w, 0, b.b, 2 * g), panel(w, 0, b.b, 2 * g + 1)], axis=1)
        w1 = jnp.concatenate([panel(w, 1, b.b, 2 * g), panel(w, 1, b.b, 2 * g + 1)], axis=1)
        xo[:, lanes(g, 256)] += dot(act[:, :half], w0) + dot(act[:, half:], w1)

    repeat(b.width // 256, 1, down)


def block_bwd(b, dr, w, gains, same, n1, proj, p, att, ow, m1, i1, n2, m2, i2, act, slope,
              r, dh, r1, dp_out, acc, da, norm_out, keep):
    cols = slice(b.col, b.col + b.width)
    r[...] = dr[...].astype(jnp.bfloat16)
    keep(3)
    half = b.hidden // 2
    rb = b.b[0]
    gb = b.width // 128
    num = 16

    def hidden(i, _):
        t, lo = i // (16 // num), (i % (16 // num)) * num
        wc = jnp.concatenate([panel(w, t, b.b, g, lo, num) for g in range(gb)], axis=1)
        at = lanes(i, num * rb)
        dh[:, at] = (dot_nt(r[...], wc) * slope[:, at]).astype(jnp.bfloat16)
        return 0

    lax.fori_loop(0, 2 * (16 // num), hidden, 0)
    keep(2)
    ga = b.a[1]
    pull(acc, dh, w, b.a, 12)
    dx, dg, db = ln_back(acc[...], m2[...], i2[:, :1], gains[1:2, cols])
    norm_out[1:2, cols] = dg
    norm_out[3:4, cols] = db
    dx1 = dr[...] + dx
    dr[...] = dx1
    r1[...] = dx1.astype(jnp.bfloat16)
    keep(1)
    for t in range(2):
        da[:, t * b.part:(t + 1) * b.part] = dot_nt(r1[...], ow[t]).astype(jnp.bfloat16)
    gq = b.q[1]
    np_ = b.part // 128
    lane = lax.broadcasted_iota(jnp.int32, (256, 128), 1)
    masks = [lane // b.size == i for i in range(b.per)]
    scale = b.size ** (-0.5)

    def heads(i, _):
        t, j = i // np_, i % np_
        q = proj[:, lanes(t * gq + j)]
        k = proj[:, lanes(t * gq + np_ + j)]
        v = proj[:, lanes(t * gq + 2 * np_ + j)]
        up_ = da[:, lanes(i)]
        dq = jnp.zeros((256, 128), jnp.float32)
        dk = jnp.zeros((256, 128), jnp.float32)
        dv = jnp.zeros((256, 128), jnp.float32)
        for h in range(b.per):
            s = p[i * b.per + h]
            u = jnp.where(masks[h], up_, 0)
            dp = dot_nt(u, v)
            dv = dv + dot_tn(s.astype(jnp.bfloat16), u)
            t1 = s * dp
            dz = (t1 - s * jnp.sum(t1, axis=-1, keepdims=True)).astype(jnp.bfloat16)
            dq = dq + dot(dz, jnp.where(masks[h], k, 0))
            dk = dk + dot_tn(dz, jnp.where(masks[h], q, 0))
        dp_out[:, lanes(t * gq + j)] = (dq * scale).astype(jnp.bfloat16)
        dp_out[:, lanes(t * gq + np_ + j)] = (dk * scale).astype(jnp.bfloat16)
        dp_out[:, lanes(t * gq + 2 * np_ + j)] = dv.astype(jnp.bfloat16)
        return 0

    lax.fori_loop(0, 2 * np_, heads, 0)
    keep(0)
    pull(acc, dp_out, w, b.q, 9)
    dx, dg, db = ln_back(acc[...], m1[...], i1[:, :1], gains[0:1, cols])
    norm_out[0:1, cols] = dg
    norm_out[2:3, cols] = db
    dr[...] = dr[...] + dx


ACTS = (DE, DE, DE, FFE, DE, DD, DD, DD, FFD)
GRADS = (3 * DE, DE, FFE, DE, DD, 3 * DD, DD, FFD, DD)


def lookup(pos, tab, cols):
    row = lax.broadcasted_iota(jnp.int32, (48, 256), 0)
    spots = [jnp.concatenate([pos[0, i:i + 1, :], pos[1, i:i + 1, :]], axis=1) for i in range(3)]
    hot = jnp.logical_or(jnp.logical_or(row == spots[0], row == spots[1] + 16), row == spots[2] + 32)
    hot = jnp.where(hot, 1.0, 0.0).astype(jnp.bfloat16)
    return sum(dot_tn(hot, tab[i, :, cols]) for i in range(3))


def tile_mask(tile):
    ids = tile[lax.axis_index("tensor")]
    tiles = jnp.where(lax.broadcasted_iota(jnp.int32, (16, 256), 0) == ids, 1.0, 0.0).astype(jnp.bfloat16)
    return (1.0 - dot_tn(tiles, tiles)) * MASK_FILL


FWD_ACTS = [((256, n), jnp.bfloat16) for n in (DE, DE, DE, FFE)]
FWD_KEPT = [((256, 3 * DE), jnp.bfloat16), ((HE, 256, 256), jnp.float32), ((2, DE // 2, DE), jnp.bfloat16),
            ((256, DE), jnp.float32), ((256, 128), jnp.float32), ((256, DE), jnp.float32), ((256, 128), jnp.float32),
            ((256, FFE), jnp.float32)]


def chain_kernel(table, pos, tile, gains, biases, cot, tab, x2, w_hbm, *refs):
    fwd_hbm, refs = refs[:8], refs[8:]
    dec, dx0, norm_out = refs[:3]
    kept_out = refs[3:17]
    kept = refs[17:31]
    low, n1d, ad, n2d, ud, dpe, r1e, dhe, re, dlow, dpd, r1d, dhd, rd = kept
    fwd, refs = refs[31:39], refs[39:]
    proj_e, pe, ow_e, m1e, i1e, m2e, i2e, se = fwd
    (w, pd, sd, proj_d, da_e, da_d, ow_d, m1d, m2d, i1d, i2d, y, acc_e, acc_d, w_sem, f_sem, out_sem) = refs
    enc_b = Block(DE, HE, HDE, FFE, 0, table, 0)
    dec_b = Block(DD, HD, HDD, FFD, 5, table, DE)
    em = table[4]

    def load(m):
        rows = pl.ds(table[m][4], table[m][1] * table[m][5])
        return pltpu.make_async_copy(w_hbm.at[:, :, rows], w.at[:, :, rows], w_sem.at[m])

    def fetch(i):
        return pltpu.make_async_copy(fwd_hbm[i], fwd[i], f_sem.at[i])

    def store(i):
        return pltpu.make_async_copy(kept[i], kept_out[i], out_sem.at[i])

    for m in (4, 5, 6, 7, 8, 3, 2, 1, 0):
        if m != 1:
            load(m).start()
    for i in range(8):
        fetch(i).start()
    same = tile_mask(tile)
    low[...] = x2[...].astype(jnp.bfloat16)
    store(0).start()
    load(4).wait()
    for g in range(2):
        v = dot(low[...], pair(w, em, g)).astype(jnp.bfloat16).astype(jnp.float32)
        y[:, g * 128:(g + 1) * 128] = v[:, :128]
        y[:, 256 + g * 128:256 + (g + 1) * 128] = v[:, 128:]
    y[...] += lookup(pos, tab, slice(DE, DE + DD))
    for _ in block_fwd(dec_b, y, dec, w, gains, biases, same, n1d, proj_d, pd, ad, ow_d, m1d, i1d, n2d, m2d, i2d, ud, sd,
                       lambda k: load(5 + k).wait(), lambda k: store(1 + k).start()):
        pass
    y[...] = cot[...]
    block_bwd(dec_b, y, w, gains, same, n1d, proj_d, pd, ad, ow_d, m1d, i1d, n2d, m2d, i2d, ud, sd,
              rd, dhd, r1d, dpd, acc_d, da_d, norm_out, lambda k: store(10 + k).start())
    dlow[...] = y[...].astype(jnp.bfloat16)
    store(9).start()
    for g in range(2):
        d = jnp.concatenate([dlow[:, g * 128:(g + 1) * 128], dlow[:, 256 + g * 128:256 + (g + 1) * 128]], axis=1)
        v = dot_nt(d, pair(w, em, g))
        if g == 0:
            dx0[...] = v
        else:
            dx0[...] += v
    for m in (3, 2, 0):
        load(m).wait()
    for i in range(8):
        fetch(i).wait()
    block_bwd(enc_b, dx0, w, gains, same, None, proj_e, pe, None, ow_e, m1e, i1e, None, m2e, i2e, None, se,
              re, dhe, r1e, dpe, acc_e, da_e, norm_out, lambda k: store(5 + k).start())
    for i in range(14):
        store(i).wait()


def chain(pos, tile, gains, biases, cot, full, x2, fwd, table):
    f32, bf16 = jnp.float32, jnp.bfloat16
    S = jax.ShapeDtypeStruct
    outs = [S((256, DD), f32), S((256, DE), f32), S((4, DE + DD), f32)]
    kept = [(256, n) for n in ACTS[4:] + GRADS]
    outs += [S(k, bf16) for k in kept]
    V = pltpu.VMEM
    scratch = [V(k, bf16) for k in kept] + [V(k, t) for k, t in FWD_KEPT] + [
        V((2, 16) + full.shape[-2:], bf16), V((HD, 256, 256), f32), V((256, FFD), f32),
        V((256, 3 * DD), bf16), V((256, DE), bf16), V((256, DD), bf16), V((2, DD // 2, DD), bf16),
        V((256, DD), f32), V((256, DD), f32), V((256, 128), f32), V((256, 128), f32),
        V((256, DD), f32), V((256, DE), f32), V((256, DD), f32),
        pltpu.SemaphoreType.DMA((9,)), pltpu.SemaphoreType.DMA((8,)), pltpu.SemaphoreType.DMA((14,))]
    vmem = pl.BlockSpec(memory_space=pltpu.VMEM)
    hbm = pl.BlockSpec(memory_space=pl.ANY)
    args = (pos, tile, gains, biases, cot, jnp.asarray(position_table()), x2,
            full.reshape(2, 16, full.shape[-2], 128), *fwd)
    return pl.pallas_call(
        partial(chain_kernel, table), out_shape=outs, in_specs=[vmem] * 7 + [hbm] * 9, out_specs=[vmem] * 3 + [hbm] * 14,
        scratch_shapes=scratch, compiler_params=pltpu.CompilerParams(vmem_limit_bytes=63 << 20), name="chain",
        cost_estimate=pl.CostEstimate(flops=8_000_000_000, bytes_accessed=40_000_000, transcendentals=3_000_000),
    )(*args)


def grad_panels(table, m, act, grad, turned, put):
    mat = table[m]
    rb, panels, padded = mat[0], mat[1], mat[5]
    count = act.shape[1]

    def turn(i):
        turned[pl.ds(pl.multiple_of(i * 128, 128), 128), :] = act[:, lanes(i)].T

    repeat(count // 128, 6, turn)

    def place(t, g, v):
        if padded > rb:
            v = v.reshape(16, rb, 128)
            v = jnp.concatenate([v, jnp.zeros((16, padded - rb, 128), jnp.float32)], axis=1).astype(jnp.bfloat16)
        else:
            v = v.astype(jnp.bfloat16).reshape(16, rb, 128)
        put(t, g, v)

    if m in BY_ROWS:
        half = count // 2

        def body(i):
            t, g = i // (panels // 2), i % (panels // 2)
            v = dot(turned[pl.ds(pl.multiple_of(t * half, 128), half), :], grad[:, lanes(g, 256)])
            place(t, 2 * g, v[:, :128])
            place(t, 2 * g + 1, v[:, 128:])

        repeat(panels, 6, body)
    else:
        def body(g):
            d = jnp.concatenate([grad[:, lanes(g)], grad[:, lanes(panels + g)]], axis=1)
            v = dot(turned[:count, :], d)
            place(0, g, v[:, :128])
            place(1, g, v[:, 128:])

        repeat(panels, 6, body)


class Wires:
    def __init__(self, place, sem):
        self.place, self.sem, self.used, self.waits = place, sem, 0, []

    def new(self, n=1):
        self.used += n
        assert self.used <= self.sem.shape[0], self.used
        return self.used - n

    def copy(self, k, src, dst, way):
        return pltpu.make_async_remote_copy(src_ref=src, dst_ref=dst, send_sem=self.sem.at[k], recv_sem=self.sem.at[k + 1],
                                            device_id=self.place.ids[way], device_id_type=MESH)

    def send(self, k, src, dst, way, cond=None):
        cp = self.copy(k, src, dst, way)
        when(cond, cp.start)
        self.waits.append((cond, cp))

    def land(self, k, dst, cond=None):
        when(cond, self.copy(k, dst, dst, "c").wait_recv)

    def drain(self):
        for cond, cp in self.waits:
            when(cond, cp.wait_send)


def edge_slots(order):
    slots, used, shared = {}, 0, {}
    for d, kids in sorted(spread(order).items()):
        for _, way in kids:
            if way in "xy" and order.index("z") < order.index(way):
                key = (way, d[1], d[2])
                if key not in shared:
                    shared[key] = used
                    used += 4
                slots[d, way] = (shared[key], 4)
            else:
                slots[d, way] = (used, 1)
                used += 1
    return slots, used


def beyond(p, way):
    return p.z < 3 if way == "z+" else p.z > 0 if way == "z-" else None


def reduce_events(p, w, order, own, half, bufs, ready, done):
    tree = spread(order)
    pair = {d: w.new(2) for d in tree}
    wire = {d: w.new(2) for d in tree}
    parent = {nd: (d, way) for d, t in tree.items() for nd, way in t}
    slots, _ = edge_slots(order)

    def buffer(up, way):
        first, n = slots[up, way]
        return bufs.at[first + p.z + up[0] if n > 1 else first]

    events = []
    far = sorted(tree, key=lambda d: (-hops(d), d))
    for d in far:
        def act(d=d):
            cond = p.there(d)

            def step():
                acc = own(d)
                ready(d)
                w.land(pair[d], half(d))
                add_rows(acc, half(d))
                for nd, way in tree[d]:
                    buf = buffer(d, way)

                    def take(buf=buf, nd=nd):
                        w.land(wire[nd], buf)
                        add_rows(acc, buf)
                    when(beyond(p, way), take)
            when(cond, step)
            if hops(d) == 0:
                done()
            else:
                up, way = parent[d]
                w.send(wire[d], own(d), buffer(up, way), BACK[way], cond)
        events.append(act)

    def share(give):
        for d in far:
            w.send(pair[d], give(d), half(d), "c", p.there(d))

    return events, share, far


def gather_events(p, w, order, first, at):
    tree = spread(order)
    pair = {d: w.new(2) for d in tree}
    wire = {d: w.new(2) for d in tree}
    events = []
    for d in sorted(tree, key=lambda d: (hops(d), d)):
        def act(d=d):
            cond = p.there(d)
            blk = at(d, p.c)
            if hops(d):
                w.land(wire[d], blk, cond)
                src = blk
            else:
                src = first
            for nd, way in tree[d]:
                w.send(wire[nd], src, blk, way, both(cond, beyond(p, way)))
            w.send(pair[d], src, blk, "c", cond)
        events.append(act)

    def finish():
        for d in tree:
            w.land(pair[d], at(d, 1 - p.c), p.there(d))

    return events, finish


def run_events(lists, order, extra=iter(()), every=8):
    assert sorted(order) == sorted(64 * g + i for g, acts in enumerate(lists) for i in range(len(acts)))
    for n, k in enumerate(order):
        if n % every == 0:
            next(extra, None)
        lists[k // 64][k % 64]()
    for _ in extra:
        pass


def group_span(table, mats):
    first, last = table[mats[0]], table[mats[-1]]
    units = last[3] + last[2] - first[3]
    return first[3], -(-units // 16) * 16, first[4], last[4] + last[1] * last[5] - first[4]


def units_to_panels(table, mats, units, flat, put):
    base, count = table[mats[0]][3], units.shape[0]
    for k in range(4):
        flat[pl.ds(k, count, stride=4), :] = units[:, 128 * k:128 * (k + 1)].astype(jnp.float32)
    for m in mats:
        rb, panels, n, first, _, padded, _ = table[m]
        for g in range(panels):
            v = flat[pl.ds(4 * (first - base) + g, rb, stride=panels), :]
            if padded > rb:
                v = jnp.concatenate([v, jnp.zeros((padded - rb, 128), jnp.float32)], axis=0)
            put(m, g, v.astype(jnp.bfloat16))


def panels_to_units(table, mats, take, flat, units):
    base, count = table[mats[0]][3], units.shape[0]
    used = 0
    for m in mats:
        rb, panels, n, first, _, padded, _ = table[m]
        for g in range(panels):
            flat[pl.ds(4 * (first - base) + g, rb, stride=panels), :] = take(m, g)[:rb]
        used = 4 * (first - base + n)
    if used < 4 * count:
        flat[used:4 * count, :] = jnp.zeros((4 * count - used, 128), jnp.float32)
    for k in range(4):
        units[:, 128 * k:128 * (k + 1)] = flat[pl.ds(k, count, stride=4), :].astype(jnp.bfloat16)


def encoder_steps(p, table, out, tok, pos, x, x2, tile, gains, biases, tab, fwd, fwd_out, wv, w_sem, fwd_sem, swapped, arrived):
    n1, att, n2, act, proj, prob, ow, m1, i1, m2, i2, slope = fwd

    def load(m):
        rows = pl.ds(table[m][4], table[m][1] * table[m][5])
        return pltpu.make_async_copy(out.at[:, :, :, :, rows], wv.at[:, :, :, :, rows], w_sem.at[m])

    def store(i):
        return pltpu.make_async_copy(fwd[i], fwd_out[i], fwd_sem.at[i])

    def keep(k):
        for i in ((0, 7, 8), (1, 4, 5), (2, 6, 9, 10), (3, 11))[k]:
            store(i).start()

    for f in swapped:
        f()
    x[...] = tok[...].reshape(256, DE).astype(jnp.float32) + lookup(pos, tab, slice(0, DE))
    same = tile_mask(tile)
    whole = wv.reshape(2, 16, wv.shape[-2], 128)
    block = block_fwd(Block(DE, HE, HDE, FFE, 0, table, 0), x, x2, whole, gains, biases, same, n1, proj, prob, att, ow, m1, i1, n2,
                      m2, i2, act, slope, lambda k: load(k).wait(), keep)
    next(block)
    yield
    for f in arrived[0]:
        f()
    load(0).start()
    load(1).start()
    yield
    for _ in range(4):
        next(block)
        yield
    for f in arrived[1]:
        f()
    load(2).start()
    yield
    next(block)
    yield
    for f in arrived[2]:
        f()
    load(3).start()
    yield
    for _ in block:
        pass
    yield
    for i in range(12):
        store(i).wait()


class Swap:
    def __init__(self, p, w, src, out, give, keep):
        self.p, self.w, self.src, self.out, self.give, self.keep = p, w, src, out, give, keep
        self.k, self.own = w.new(2), w.new()

    def local(self):
        return pltpu.make_async_copy(self.src.at[self.keep], self.out.at[self.p.x], self.w.sem.at[self.own])

    def start(self):
        self.w.send(self.k, self.src.at[self.give], self.out.at[self.p.x], "x")

    def finish(self):
        self.w.land(self.k, self.out.at[1 - self.p.x])
        self.local().wait()


def weights_kernel(table, groups, plan, parts, tok_in, pos_in, cot_in, tile, gains, biases, tab, *refs):
    n = len(groups)
    out, pos, cot, x2 = refs[:4]
    fwd_out, tok, x, fwd, wv, w_sem, fwd_sem = refs[4:16], refs[16], refs[17], refs[18:30], refs[30], refs[31], refs[32]
    rest = refs[33:]
    accs, halves, bufs, shards = (rest[i * n:(i + 1) * n] for i in range(4))
    flat, sem = rest[4 * n:]
    p = Place()
    p.greet(["c", "y", "x"])
    w = Wires(p, sem)
    swaps = [Swap(p, w, a, b, 1 - p.x, p.x) for a, b in ((tok_in, tok), (pos_in, pos), (cot_in, cot))]
    for s in swaps:
        s.start()
        s.local().start()
    lists, finishes = [], []
    for g, mats in enumerate(groups):
        u0, un, r0, rn = group_span(table, mats)
        acc, half, buf, shard = accs[g], halves[g], bufs[g], shards[g]
        own_sem = w.new()
        loads = {d: w.new() for d in spread(plan[0][g])}

        def own(d, acc=acc):
            return acc.at[p.at(d)[1:]]

        def other(d, half=half):
            return half.at[p.at(d)[1:]]

        def load(d, u0=u0, un=un, own=own, loads=loads):
            return pltpu.make_async_copy(parts.at[p.at(d)[1:] + (p.c, pl.ds(u0, un))], own(d), sem.at[loads[d]])

        def ready(d, load=load):
            load(d).wait()

        def done(mats=mats, acc=acc, shard=shard, r0=r0):
            def put(m, i, v):
                lo = table[m][4] - r0 + i * table[m][5]
                shard[lo:lo + table[m][5], :] = v
            units_to_panels(table, mats, acc.at[p.z, p.y], flat, put)

        ev, share, far = reduce_events(p, w, plan[0][g], own, other, buf, ready, done)

        def begin(load=load, share=share, far=far, u0=u0, un=un):
            share(lambda d: parts.at[p.at(d)[1:] + (1 - p.c, pl.ds(u0, un))])
            for d in far:
                when(p.there(d), load(d).start)

        def at(d, core, r0=r0, rn=rn):
            t, z, y = p.at(d)
            return out.at[t, z, y, core, pl.ds(r0, rn)]

        def local(shard=shard, r0=r0, rn=rn, own_sem=own_sem):
            return pltpu.make_async_copy(shard, out.at[p.x, p.z, p.y, p.c, pl.ds(r0, rn)], sem.at[own_sem])

        ag, finish = gather_events(p, w, plan[1][g], shard, at)

        def send_first(act=ag[0], local=local):
            act()
            local().start()

        lists.append([begin] + ev + [send_first] + ag[1:])
        finishes += [finish, lambda local=local: local().wait()]
    steps = encoder_steps(p, table, out, tok, pos, x, x2, tile, gains, biases, tab, fwd, fwd_out, wv, w_sem, fwd_sem,
                          [s.finish for s in swaps[:2]], [finishes[2 * k:2 * k + 2] for k in range(3)])
    lists.append([partial(next, steps, None)] * 11)
    run_events(lists, plan[2])
    for f in finishes[6:] + [swaps[2].finish]:
        f()
    w.drain()


def spread_weights(parts, tokens, pos, cot, tile, gains, biases, table, rows, groups, plan, ident):
    spans = [group_span(table, m) for m in groups]
    bf16 = jnp.bfloat16
    S = jax.ShapeDtypeStruct
    V = pltpu.VMEM
    fwd = FWD_ACTS + FWD_KEPT
    enc_rows = table[4][4]
    scratch = [V(tokens.shape, tokens.dtype), V((256, DE), jnp.float32)] + [V(k, t) for k, t in fwd]
    scratch += [V((2, 4, 2, 2, enc_rows, 128), bf16), pltpu.SemaphoreType.DMA((4,)), pltpu.SemaphoreType.DMA((12,))]
    scratch += [V((4, 2, s[1], 512), bf16) for s in spans] * 2
    scratch += [V((edge_slots(o)[1], s[1], 512), bf16) for s, o in zip(spans, plan[0])]
    scratch += [V((s[3], 128), bf16) for s in spans]
    scratch += [V((4 * max(s[1] for s in spans), 128), jnp.float32),
                pltpu.SemaphoreType.DMA((len(groups) * (1 + 5 * 14 + 4 * 28) + 9,))]
    hbm = pl.BlockSpec(memory_space=pl.ANY)
    vmem = pl.BlockSpec(memory_space=pltpu.VMEM)
    return pl.pallas_call(
        partial(weights_kernel, table, groups, plan),
        out_shape=[S((2, 4, 2, 2, rows, 128), bf16), S(pos.shape, pos.dtype), S(cot.shape, cot.dtype), S((256, DE), jnp.float32)]
        + [S(k, t) for k, t in fwd],
        in_specs=[hbm] * 4 + [vmem] * 4, out_specs=[hbm, vmem, hbm, vmem] + [hbm] * 12,
        scratch_shapes=scratch,
        compiler_params=pltpu.CompilerParams(collective_id=ident, has_side_effects=True, vmem_limit_bytes=63 << 20),
        name="spread_weights",
    )(parts, tokens, pos, cot, tile, gains, biases, jnp.asarray(position_table()))


def return_kernel(table, groups, plan, *refs):
    n = len(groups)
    kept_in, small_src, dec_in, dx_in, out, small_out, dec, dx = refs[:18], *refs[18:25]
    rest = refs[25:]
    kept, rest = rest[:18], rest[18:]
    acts, grads = kept[:9], kept[9:]
    sides, halves, bufs, units = (rest[i * n:(i + 1) * n] for i in range(4))
    flat, turned, mid, line, load_sem, sem = rest[4 * n:]

    def load(i):
        return pltpu.make_async_copy(kept_in[i], kept[i], load_sem.at[i])

    first = sorted(range(n), key=lambda g: plan[2].index(64 * g))
    for g in first:
        for m in groups[g]:
            load(m).start()
            load(9 + m).start()
    p = Place()
    p.greet(["c", "y", "x"])
    w = Wires(p, sem)
    swaps = [Swap(p, w, a, b, 1 - p.x, p.x) for a, b in ((dec_in, dec), (dx_in, dx))]
    for s in swaps:
        s.local().start()
    swaps[0].start()
    lists, finishes = [], []
    for g, mats in enumerate(groups):
        u0, un, r0, rn = group_span(table, mats)
        side, half, buf, unit = sides[g], halves[g], bufs[g], units[g]
        own_sem = w.new()

        def own(d, side=side):
            return side.at[(p.c,) + p.at(d)]

        def other(d, half=half):
            return half.at[p.at(d)]

        def done(mats=mats, side=side, unit=unit, r0=r0):
            mine = side.at[p.c, p.x, p.z, p.y]

            def take(m, i):
                lo = table[m][4] - r0 + i * table[m][5]
                return mine[lo:lo + table[m][5], :].astype(jnp.float32)
            panels_to_units(table, mats, take, flat, unit)

        ev, share, far = reduce_events(p, w, plan[0][g], own, other, buf, lambda d: None, done)

        def begin(mats=mats, side=side, share=share, r0=r0):
            for m in mats:
                lo, padded = table[m][4] - r0, table[m][5]

                def put(t, i, v, lo=lo, padded=padded):
                    v = v.reshape(4, 2, 2, padded, 128)
                    rows = pl.ds(pl.multiple_of(lo + i * padded, 16), padded)
                    side[0, t, :, :, rows, :] = v[:, :, 0]
                    side[1, t, :, :, rows, :] = v[:, :, 1]
                load(m).wait()
                load(9 + m).wait()
                grad_panels(table, m, acts[m], grads[m], turned, put)
            share(lambda d: side.at[(1 - p.c,) + p.at(d)])

        def at(d, core, u0=u0, un=un):
            _, z, y = p.at(d)
            return out.at[z, y, core, pl.ds(u0, un)]

        def local(unit=unit, u0=u0, un=un, own_sem=own_sem):
            return pltpu.make_async_copy(unit, out.at[p.z, p.y, p.c, pl.ds(u0, un)], sem.at[own_sem])

        ag, finish = gather_events(p, w, plan[1][g], unit, at)

        def send_first(act=ag[0], local=local):
            act()
            local().start()

        lists.append([begin] + ev + [send_first] + ag[1:])
        finishes += [finish, lambda local=local: local().wait()]
    last = max(plan[2].index(64 * g + len(spread(plan[0][g]))) for g in range(n))
    g, i = plan[2][last] // 64, plan[2][last] % 64
    act = lists[g][i]

    def with_swaps():
        act()
        swaps[1].start()

    lists[g][i] = with_swaps
    run_events(lists, plan[2], total_steps(p, w, small_src, small_out, mid, line))
    for f in finishes + [s.finish for s in swaps]:
        f()
    w.drain()


def total_steps(p, w, src, out, mid, line):
    k = [w.new(2) for _ in range(9)]
    now = src
    for i, way in enumerate(("c", "x", "y")):
        w.send(k[i], now, mid.at[i], way)
        yield
        w.land(k[i], mid.at[i])
        nxt = mid.at[3 + i] if i < 2 else line.at[p.z]
        nxt[...] = now[...] + mid[i]
        now = nxt
    for i in range(4):
        lo, hi = jnp.maximum(p.z - i, 0), jnp.minimum(p.z + i, 3)
        if i > 0:
            w.land(k[2 + i], line.at[lo], p.z >= i)
            w.land(k[5 + i], line.at[hi], p.z + i <= 3)
        if i < 3:
            w.send(k[3 + i], line.at[lo], line.at[lo], "z+", jnp.logical_and(p.z >= i, p.z < 3))
            w.send(k[6 + i], line.at[hi], line.at[hi], "z-", jnp.logical_and(p.z + i <= 3, p.z > 0))
            yield
    out[...] = (line[0] + line[1]) + (line[2] + line[3])


def return_grads(kept, small, dec, dx, table, total_units, groups, plan, ident):
    spans = [group_span(table, m) for m in groups]
    bf16 = jnp.bfloat16
    S = jax.ShapeDtypeStruct
    V = pltpu.VMEM
    scratch = [V(v.shape, v.dtype) for v in kept]
    scratch += [V((2, 2, 4, 2, s[3], 128), bf16) for s in spans]
    scratch += [V((2, 4, 2, s[3], 128), bf16) for s in spans]
    scratch += [V((edge_slots(o)[1], s[3], 128), bf16) for s, o in zip(spans, plan[0])]
    scratch += [V((s[1], 512), bf16) for s in spans]
    scratch += [V((4 * max(s[1] for s in spans), 128), jnp.float32), V((FFE, 256), bf16),
                V((5,) + small.shape, small.dtype), V((4,) + small.shape, small.dtype), pltpu.SemaphoreType.DMA((18,)),
                pltpu.SemaphoreType.DMA((len(groups) * (1 + 4 * 14 + 4 * 28) + 24,))]
    vmem = pl.BlockSpec(memory_space=pltpu.VMEM)
    hbm = pl.BlockSpec(memory_space=pl.ANY)
    return pl.pallas_call(
        partial(return_kernel, table, groups, plan),
        out_shape=(S((4, 2, 2, total_units, 512), bf16), S(small.shape, small.dtype), S(dec.shape, dec.dtype), S(dx.shape, dx.dtype)),
        in_specs=[hbm] * 18 + [vmem, hbm, hbm], out_specs=(hbm, vmem, hbm, hbm),
        scratch_shapes=scratch,
        compiler_params=pltpu.CompilerParams(collective_id=ident, has_side_effects=True, vmem_limit_bytes=63 << 20),
        name="return_grads",
    )(*kept, small, dec, dx)


STEP_ROWS = 432


def update_kernel(place_s, place, spread, master, first, second, total, params, norm_first, norm_second, *refs):
    passed, refs = refs[:2], refs[2:]
    new_master, new_first, new_second, new_norms, new_nf, new_ns = refs[:6]
    i = pl.program_id(0)

    @pl.when(i == 0)
    def _():
        for a, b in zip(passed, refs[6:8]):
            b[...] = a[...]
        new_norms[...], new_nf[...], new_ns[...] = adamw(params[...], total[...], norm_first[...], norm_second[...], 0.0, NORM_RATE)

    lane = lax.broadcasted_iota(jnp.int32, (16, 256), 1)
    row = lax.broadcasted_iota(jnp.int32, (16, 256), 0)
    for k in range(STEP_ROWS // 16):
        tiles = []
        for j in range(16):
            at = jnp.minimum(place_s[i * STEP_ROWS + 16 * k + j] >> 4, spread.shape[0] // 16 - 1)
            tiles.append(spread[pl.ds(pl.multiple_of(at * 16, 16), 16), :])
        here = slice(16 * k, 16 * k + 16)
        spot = place[here, :]
        used = jnp.logical_and(lane == row * 16 + (spot & 15), spot < spread.shape[0])
        grad = dot(jnp.where(used, 1.0, 0.0).astype(jnp.bfloat16), jnp.concatenate(tiles, axis=0))
        new_master[here, :], new_first[here, :], new_second[here, :] = adamw(
            master[here, :], grad, first[here, :], second[here, :], WEIGHT_DECAY, LEARN_RATE)


def update(place, spread, master, first, second, total, params, norm_first, norm_second, passed):
    slots = master.shape[0]
    S = jax.ShapeDtypeStruct
    rows = pl.BlockSpec((STEP_ROWS, 512), lambda i, s: (i, 0))
    whole = lambda v: pl.BlockSpec(v.shape, lambda i, s: (0, 0), pipeline_mode=pl.Buffered(1))
    small = pl.BlockSpec(params.shape, lambda i, s: (0, 0))
    out = [S(master.shape, jnp.float32)] * 3 + [S(params.shape, jnp.float32)] * 3 + [S(v.shape, v.dtype) for v in passed]
    both = [pl.BlockSpec(v.shape, lambda i, s: (0, 0, 0), pipeline_mode=pl.Buffered(1)) for v in passed]
    return pl.pallas_call(
        update_kernel, out_shape=out,
        grid_spec=pltpu.PrefetchScalarGridSpec(
            num_scalar_prefetch=1, grid=(slots // STEP_ROWS,),
            in_specs=[pl.BlockSpec((STEP_ROWS, 1), lambda i, s: (i, 0)), whole(spread), rows, rows, rows, small, small, small, small] + both,
            out_specs=[rows] * 3 + [small] * 3 + both),
        compiler_params=pltpu.CompilerParams(vmem_limit_bytes=62 << 20), name="update",
    )(place, lax.optimization_barrier(place)[:, None], spread, master, first, second, total, params, norm_first, norm_second, *passed)


def place_kernel(place_s, master, out, wide, staged, sem):
    count = wide.shape[0] // 64 - 1

    def clear(i, _):
        wide[pl.ds(pl.multiple_of(i * 64, 64), 64), :] = jnp.zeros((64, 512), jnp.float32)
        return 0

    lax.fori_loop(0, count, clear, 0)

    def turn(i, _):
        for j in range(16):
            wide[pl.ds(place_s[i * 16 + j], 1), :] = master[pl.ds(i * 16 + j, 1), :]
        return 0

    lax.fori_loop(0, master.shape[0] // 16, turn, 0)
    parts = 4
    part = count // parts * 64

    def copy(k):
        rows = pl.ds(pl.multiple_of(k * part, 64), part)
        return pltpu.make_async_copy(staged.at[rows], out.at[rows], sem.at[k])

    for k in range(parts):
        def narrow(i, _):
            rows = pl.ds(pl.multiple_of(k * part + i * 64, 64), 64)
            staged[rows, :] = wide[rows, :].astype(jnp.bfloat16)
            return 0

        lax.fori_loop(0, part // 64, narrow, 0)
        copy(k).start()
    for k in range(parts):
        copy(k).wait()


def place_blocks(place, master, rows):
    return pl.pallas_call(
        place_kernel, out_shape=jax.ShapeDtypeStruct((rows, 512), jnp.bfloat16),
        grid_spec=pltpu.PrefetchScalarGridSpec(
            num_scalar_prefetch=1, grid=(1,),
            in_specs=[pl.BlockSpec(master.shape, lambda i, s: (0, 0), pipeline_mode=pl.Buffered(1))],
            out_specs=pl.BlockSpec(memory_space=pl.ANY),
            scratch_shapes=[pltpu.VMEM((rows + 64, 512), jnp.float32), pltpu.VMEM((rows, 512), jnp.bfloat16), pltpu.SemaphoreType.DMA((4,))]),
        compiler_params=pltpu.CompilerParams(vmem_limit_bytes=60 << 20), name="place_blocks",
    )(place, master)


def sequence_device(tokens_in, positions, segment_ids, owners, master, first_moment, second_moment, norm_gains,
                    norm_biases, norm_first, norm_second, cotangent):
    shapes = weight_shapes(2)
    table, _, rows = layout(shapes, 16)
    unit, used = own_units(owners, lax.axis_index("dp"), master.shape[0])
    place = jnp.where(used, unit_places(unit, table, 16), 16 * SHARD_UNITS)
    parts = place_blocks(place, master, 16 * SHARD_UNITS)
    full, pos, cot, x2, *fwd = spread_weights(parts.reshape(4, 2, 2, SHARD_UNITS, 512), tokens_in, positions.transpose(1, 0, 2),
                                              cotangent, segment_ids, norm_gains, norm_biases, table, rows, GROUPS, PLAN_OUT, 1)
    kept = chain(pos, segment_ids, norm_gains, norm_biases, cot.reshape(256, DD), full, x2, fwd[4:], table)
    decoded, dx0, norms = kept[:3]
    spread_out, norm_total, decoded, dx0 = return_grads([*fwd[:4], *kept[3:]], norms, decoded.reshape(2, 128, DD), dx0.reshape(2, 128, DE), table,
                                                        SHARD_UNITS, GROUPS, PLAN_BACK, 2)
    norm_params = jnp.concatenate([norm_gains, norm_biases], axis=0)
    new_master, new_first, new_second, new_norms, norm_one_new, norm_two_new, decoded, dx0 = update(
        place, spread_out.reshape(16 * SHARD_UNITS, 512), master, first_moment, second_moment, norm_total, norm_params, norm_first, norm_second,
        (decoded, dx0))
    return (decoded, dx0, new_master, new_first, new_second, new_norms, norm_one_new, norm_two_new)


def solution(mesh):
    step = sequence_device if (mesh.shape["dp"], mesh.shape["tensor"]) == (16, 2) else per_device
    return jax.shard_map(
        step,
        mesh=mesh,
        in_specs=(
            P(None, ("dp", "tensor"), None),
            P(None, None, ("dp", "tensor")),
            P(None, "dp", None),
            P(),
            P("dp", "tensor"),
            P("dp", "tensor"),
            P("dp", "tensor"),
            P(),
            P(),
            P(),
            P(),
            P(None, ("dp", "tensor"), None),
        ),
        out_specs=(
            P(None, ("dp", "tensor"), None),
            P(None, ("dp", "tensor"), None),
            P("dp", "tensor"),
            P("dp", "tensor"),
            P("dp", "tensor"),
            P(),
            P(),
            P(),
        ),
        check_vma=False,
    )
```

```python
from functools import partial

import jax
import jax.numpy as jnp
import ml_dtypes
import numpy as np
from jax import lax
from jax.experimental import pallas as pl
from jax.experimental.pallas import tpu as pltpu
from jax.sharding import PartitionSpec as P

DE = 768
HE = 12
HDE = 64
FFE = 3072
DD = 512
HD = 16
HDD = 32
FFD = 2048
STEP = 10


NORM_EPS = 1e-06
BETA_ONE = 0.5
BETA_TWO = 0.5
LEARN_RATE = 0.03
NORM_RATE = 0.3
WEIGHT_DECAY = 0.05
ADAM_EPS = 1e-08
MASK_FILL = -1000000000.0


def sincos_part(coordinate, part_width):
    halfway = part_width // 2
    frequency = 1.0 / 10000.0 ** (jnp.arange(halfway, dtype=jnp.float32) / halfway)
    angles = coordinate.astype(jnp.float32)[:, None] * frequency[None, :]
    return jnp.concatenate([jnp.sin(angles), jnp.cos(angles)], axis=1)


def sincos_embed(positions, model_width):
    side_width = model_width // 16 * 6
    first_width = model_width - 2 * side_width
    return jnp.concatenate(
        [
            sincos_part(positions[0], first_width),
            sincos_part(positions[1], side_width),
            sincos_part(positions[2], side_width),
        ],
        axis=1,
    )


def slot_table(owners, devices, capacity):
    owner_ids = owners[:, 0]
    onehot = (owner_ids[:, None] == jnp.arange(devices, dtype=jnp.int32)[None, :]).astype(jnp.int32)
    before = jnp.cumsum(onehot, axis=0) - onehot
    owner_rank = jnp.sum(before * onehot, axis=1)
    return owner_ids * capacity + owner_rank


def weight_shapes(tensor_count):
    enc_heads = HE // tensor_count
    dec_heads = HD // tensor_count
    return [
        (DE, 3 * enc_heads * HDE),
        (enc_heads * HDE, DE),
        (DE, FFE // tensor_count),
        (FFE // tensor_count, DE),
        (DE, DD // tensor_count),
        (DD, 3 * dec_heads * HDD),
        (dec_heads * HDD, DD),
        (DD, FFD // tensor_count),
        (FFD // tensor_count, DD),
    ]


def split_flat(flat_vector, shapes):
    pieces = []
    offset = 0
    for matrix_shape in shapes:
        length = matrix_shape[0] * matrix_shape[1]
        pieces.append(flat_vector[offset : offset + length].reshape(matrix_shape))
        offset += length
    return pieces


def adamw(weights, gradient, moment_one, moment_two, decay_rate, step_rate):
    one_new = BETA_ONE * moment_one + (1.0 - BETA_ONE) * gradient
    two_new = BETA_TWO * moment_two + (1.0 - BETA_TWO) * gradient * gradient
    one_hat = one_new / (1.0 - BETA_ONE**STEP)
    two_hat = two_new / (1.0 - BETA_TWO**STEP)
    weights_new = weights - step_rate * (
        one_hat / (jnp.sqrt(two_hat) + ADAM_EPS) + decay_rate * weights
    )
    return (weights_new, one_new, two_new)


def norm_forward(values, gain_row, bias_row):
    center = values - jnp.mean(values, axis=-1, keepdims=True)
    spread = jnp.mean(center * center, axis=-1, keepdims=True)
    inverse = lax.rsqrt(spread + NORM_EPS)
    normed = center * inverse
    return (normed * gain_row + bias_row, (normed, inverse))


def norm_backward(upstream, stored, gain_row):
    normed, inverse = stored
    scaled = upstream * gain_row
    mean_one = jnp.mean(scaled, axis=-1, keepdims=True)
    mean_two = jnp.mean(scaled * normed, axis=-1, keepdims=True)
    return (
        inverse * (scaled - mean_one - normed * mean_two),
        jnp.sum(upstream * normed, axis=0),
        jnp.sum(upstream, axis=0),
    )


def inner_rows(left_side, right_side):
    return lax.dot_general(
        left_side, right_side, (((0,), (0,)), ((), ())), preferred_element_type=jnp.float32
    )


def times_transpose(left_side, right_side):
    return lax.dot_general(
        left_side, right_side, (((1,), (1,)), ((), ())), preferred_element_type=jnp.float32
    )


def gather_rows(values):
    return lax.all_gather(values, "tensor", axis=0, tiled=True)


def gather_grads(values):
    return lax.all_gather(values, "tensor", axis=0, tiled=True)


def branch_rows(values, weight):
    return lax.psum_scatter(
        jnp.dot(values, weight, preferred_element_type=jnp.float32).astype(jnp.bfloat16),
        "tensor",
        scatter_dimension=0,
        tiled=True,
    ).astype(jnp.float32)


def input_rows(values, weight):
    return lax.psum_scatter(
        times_transpose(values, weight).astype(jnp.bfloat16),
        "tensor",
        scatter_dimension=0,
        tiled=True,
    ).astype(jnp.float32)


def block_scores(queries, key_rows, mask_bias, block_start, block_rows, head_size):
    scores = jnp.einsum(
        "qhd,khd->hqk", queries, key_rows, preferred_element_type=jnp.float32
    ) * head_size ** (-0.5)
    return scores + mask_bias[None, block_start : block_start + block_rows]


def attention_forward(gathered, w_qkv, head_count, head_size, mask_bias):
    length = gathered.shape[0]
    projected = jnp.dot(gathered, w_qkv, preferred_element_type=jnp.float32).astype(jnp.bfloat16)
    projected = projected.reshape(length, 3, head_count, head_size)
    queries = projected[:, 0]
    key_rows = projected[:, 1]
    value_rows = projected[:, 2]
    block_rows = min(512, length)
    scores = block_scores(queries, key_rows, mask_bias, 0, block_rows, head_size)
    row_peak = jnp.max(scores, axis=-1, keepdims=True)
    row_total = row_peak + jnp.log(jnp.sum(jnp.exp(scores - row_peak), axis=-1, keepdims=True))
    weights = jnp.exp(scores - row_total).astype(jnp.bfloat16)
    outputs = jnp.einsum("hqk,khd->qhd", weights, value_rows, preferred_element_type=jnp.float32)
    totals = [row_total]
    attended = outputs.astype(jnp.bfloat16).reshape(length, head_count * head_size)
    return (attended, (queries, key_rows, value_rows, totals))


def attention_backward(upstream, w_out, attended, stored, head_count, head_size, mask_bias):
    queries, key_rows, value_rows, totals = stored
    length = upstream.shape[0]
    score_scale = head_size ** (-0.5)
    grad_out = inner_rows(attended, upstream)
    attended_grad = (
        times_transpose(upstream, w_out).astype(jnp.bfloat16).reshape(length, head_count, head_size)
    )
    block_rows = min(512, length)
    key_grads = jnp.zeros((length, head_count, head_size), jnp.float32)
    value_grads = jnp.zeros((length, head_count, head_size), jnp.float32)
    query_grads = []
    for number, block_start in enumerate(range(0, length, block_rows)):
        scores = block_scores(queries, key_rows, mask_bias, block_start, block_rows, head_size)
        weights = jnp.exp(scores - totals[number])
        value_grads = jnp.einsum(
            "hqk,qhd->khd",
            weights.astype(jnp.bfloat16),
            attended_grad,
            preferred_element_type=jnp.float32,
        )
        weight_grads = jnp.einsum(
            "qhd,khd->hqk", attended_grad, value_rows, preferred_element_type=jnp.float32
        )
        score_grads = (
            weights * (weight_grads - jnp.sum(weights * weight_grads, axis=-1, keepdims=True))
        ).astype(jnp.bfloat16)
        query_grads.append(
            jnp.einsum("hqk,khd->qhd", score_grads, key_rows, preferred_element_type=jnp.float32)
            * score_scale
        )
        key_grads = (
            jnp.einsum("hqk,qhd->khd", score_grads, queries, preferred_element_type=jnp.float32)
            * score_scale
        )
    projected_grad = jnp.stack([query_grads[0], key_grads, value_grads], axis=1)
    return (
        projected_grad.astype(jnp.bfloat16).reshape(length, 3 * head_count * head_size),
        grad_out,
    )


def block_forward(residual, matrices, gain_rows, bias_rows, head_count, head_size, mask_bias):
    w_qkv, w_out, w_in, w_down = matrices
    normed, norm_one = norm_forward(residual, gain_rows[0], bias_rows[0])
    gathered = gather_rows(normed.astype(jnp.bfloat16))
    attended, stored = attention_forward(gathered, w_qkv, head_count, head_size, mask_bias)
    middle = residual + branch_rows(attended, w_out)
    normed_two, norm_two = norm_forward(middle, gain_rows[1], bias_rows[1])
    gathered_two = gather_rows(normed_two.astype(jnp.bfloat16))
    hidden = jnp.dot(gathered_two, w_in, preferred_element_type=jnp.float32)
    active = jax.nn.gelu(hidden, approximate=False).astype(jnp.bfloat16)
    result = middle + branch_rows(active, w_down)
    return (result, (gathered, norm_one, attended, stored, gathered_two, norm_two, hidden, active))


def block_backward(upstream, matrices, gain_rows, saved_values, head_count, head_size, mask_bias):
    w_qkv, w_out, w_in, w_down = matrices
    gathered, norm_one, attended, stored, gathered_two, norm_two, hidden, active = saved_values
    down_full = gather_grads(upstream.astype(jnp.bfloat16))
    grad_down = inner_rows(active, down_full)
    active_grad = times_transpose(down_full, w_down)
    gelu_pull = jax.vjp(partial(jax.nn.gelu, approximate=False), hidden)[1]
    hidden_grad = gelu_pull(active_grad)[0].astype(jnp.bfloat16)
    grad_in = inner_rows(gathered_two, hidden_grad)
    normed_two_grad = input_rows(hidden_grad, w_in)
    middle_grad, gain_two, bias_two = norm_backward(normed_two_grad, norm_two, gain_rows[1])
    middle_grad = upstream + middle_grad
    middle_full = gather_grads(middle_grad.astype(jnp.bfloat16))
    projected_grad, grad_out = attention_backward(
        middle_full, w_out, attended, stored, head_count, head_size, mask_bias
    )
    grad_qkv = inner_rows(gathered, projected_grad)
    normed_grad = input_rows(projected_grad, w_qkv)
    input_grad, gain_one, bias_one = norm_backward(normed_grad, norm_one, gain_rows[0])
    return (
        middle_grad + input_grad,
        [grad_qkv, grad_out, grad_in, grad_down],
        (gain_one, gain_two, bias_one, bias_two),
    )


def embed_forward(residual, w_embed):
    residual_low = gather_rows(residual.astype(jnp.bfloat16))
    columns = jnp.dot(residual_low, w_embed, preferred_element_type=jnp.float32).astype(
        jnp.bfloat16
    )
    own_columns = lax.all_to_all(columns, "tensor", split_axis=0, concat_axis=1, tiled=True)
    return (own_columns.astype(jnp.float32), residual_low)


def embed_backward(upstream, residual_low, w_embed):
    columns = lax.all_to_all(
        upstream.astype(jnp.bfloat16), "tensor", split_axis=1, concat_axis=0, tiled=True
    )
    grad_embed = inner_rows(residual_low, columns)
    return (input_rows(columns, w_embed), grad_embed)


def slot_builder(gradients, unit_of_slot, unit_width):
    flat_units = jnp.concatenate([gradient.reshape(-1) for gradient in gradients]).reshape(
        -1, unit_width
    )
    unit_total = flat_units.shape[0]
    source = jnp.take(flat_units, jnp.clip(unit_of_slot, 0, unit_total - 1), axis=0)
    return jnp.where((unit_of_slot >= 0)[:, None], source, 0.0)


def per_device(
    tokens_in,
    positions,
    segment_ids,
    owners,
    master,
    first_moment,
    second_moment,
    norm_gains,
    norm_biases,
    norm_first,
    norm_second,
    cotangent,
):
    devices = lax.axis_size("dp")
    tensor_count = lax.axis_size("tensor")
    capacity = master.shape[0]
    unit_width = master.shape[1]
    unit_count = owners.shape[0]
    slot_index = slot_table(owners, devices, capacity)
    unit_of_slot = (
        jnp.full((devices * capacity,), -1, jnp.int32)
        .at[slot_index]
        .set(jnp.arange(unit_count, dtype=jnp.int32))
    )
    targets = unit_of_slot
    targets = jnp.where(targets < 0, unit_count, targets)
    placed = (
        jnp.zeros((unit_count, unit_width), jnp.bfloat16)
        .at[targets]
        .set(lax.all_gather(master.astype(jnp.bfloat16), "dp", axis=0, tiled=True), mode="drop")
    )
    shapes = weight_shapes(tensor_count)
    matrices = split_flat(placed.reshape(-1), shapes)
    encoder = matrices[0:4]
    w_embed = matrices[4]
    decoder = matrices[5:9]
    enc_heads = HE // tensor_count
    dec_heads = HD // tensor_count
    micro_count = tokens_in.shape[0]
    grad_sums = [jnp.zeros(matrix_shape, jnp.float32) for matrix_shape in shapes]
    norm_sums = jnp.zeros((4, DE + DD), jnp.float32)
    decoded_rows = []
    token_grads = []
    for micro_step in range(micro_count):
        tile_ids = segment_ids[micro_step, 0]
        mask_bias = jnp.where(tile_ids[:, None] == tile_ids[None, :], 0.0, MASK_FILL).astype(
            jnp.float32
        )
        position_now = positions[:, micro_step]
        residual = tokens_in[micro_step].astype(jnp.float32) + sincos_embed(position_now, DE)
        residual, enc_saved = block_forward(
            residual, encoder, norm_gains[:, :DE], norm_biases[:, :DE], enc_heads, HDE, mask_bias
        )
        residual, embed_low = embed_forward(residual, w_embed)
        residual = residual + sincos_embed(position_now, DD)
        residual, dec_saved = block_forward(
            residual, decoder, norm_gains[:, DE:], norm_biases[:, DE:], dec_heads, HDD, mask_bias
        )
        decoded_rows.append(residual)
        upstream, dec_grads, dec_norm = block_backward(
            cotangent[micro_step], decoder, norm_gains[:, DE:], dec_saved, dec_heads, HDD, mask_bias
        )
        upstream, grad_embed = embed_backward(upstream, embed_low, w_embed)
        upstream, enc_grads, enc_norm = block_backward(
            upstream, encoder, norm_gains[:, :DE], enc_saved, enc_heads, HDE, mask_bias
        )
        token_grads.append(upstream)
        step_grads = enc_grads + [grad_embed] + dec_grads
        step_norm = jnp.concatenate([jnp.stack(enc_norm), jnp.stack(dec_norm)], axis=1)
        grad_sums = [total_grad + new_grad for total_grad, new_grad in zip(grad_sums, step_grads)]
        norm_sums = norm_sums + step_norm
    reduced = lax.psum_scatter(
        slot_builder(grad_sums, unit_of_slot, unit_width), "dp", scatter_dimension=0, tiled=True
    )
    norm_total = lax.psum(norm_sums, ("dp", "tensor"))
    new_master, new_first, new_second = adamw(
        master, reduced, first_moment, second_moment, WEIGHT_DECAY, LEARN_RATE
    )
    norm_params = jnp.concatenate([norm_gains, norm_biases], axis=0)
    new_norms, norm_one_new, norm_two_new = adamw(
        norm_params, norm_total, norm_first, norm_second, 0.0, NORM_RATE
    )
    return (
        jnp.stack(decoded_rows),
        jnp.stack(token_grads),
        new_master,
        new_first,
        new_second,
        new_norms,
        norm_one_new,
        norm_two_new,
    )


MESH = pl.DeviceIdType.MESH
ALL = slice(None)


class Place:
    def __init__(self):
        self.d = lax.axis_index("dp")
        self.x = lax.axis_index("tensor")
        self.z = self.d // 4
        self.y = (self.d // 2) % 2
        self.c = self.d % 2
        self.ids = {
            "c": (self.d + 1 - 2 * self.c, self.x),
            "y": (self.d + 2 - 4 * self.y, self.x),
            "x": (self.d, 1 - self.x),
            "z+": (self.d + 4, self.x),
            "z-": (self.d - 4, self.x),
        }

    def greet(self, kinds):
        bar = pltpu.get_barrier_semaphore()
        for k in kinds:
            pl.semaphore_signal(bar, inc=1, device_id=self.ids[k], device_id_type=MESH)

        @pl.when(self.z < 3)
        def _():
            pl.semaphore_signal(bar, inc=1, device_id=self.ids["z+"], device_id_type=MESH)

        @pl.when(self.z > 0)
        def _():
            pl.semaphore_signal(bar, inc=1, device_id=self.ids["z-"], device_id_type=MESH)

        inner = jnp.where(jnp.logical_and(self.z > 0, self.z < 3), 1, 0)
        pl.semaphore_wait(bar, len(kinds) + 1 + inner)

    def there(self, disp):
        dz = disp[0]
        if dz == 0:
            return None
        return self.z + dz <= 3 if dz > 0 else self.z + dz >= 0

    def at(self, disp):
        dz, fy, fx = disp
        return (1 - self.x if fx else self.x, self.z + dz, 1 - self.y if fy else self.y)


def when(cond, f):
    if cond is None:
        f()
    else:
        pl.when(cond)(f)


def both(a, b):
    if a is None:
        return b
    if b is None:
        return a
    return jnp.logical_and(a, b)


def spread(order):
    out = {}
    todo = [((0, 0, 0), -1, 0)]
    while todo:
        (dz, fy, fx), last, way = todo.pop(0)
        nxt = []
        for i, a in enumerate(order):
            if i < last:
                continue
            if a == "z":
                for s in (1, -1):
                    if i == last and s != way:
                        continue
                    n = (dz - s, fy, fx)
                    if abs(n[0]) <= 3:
                        nxt.append((n, "z+" if s > 0 else "z-", i, s))
            elif i > last:
                n = (dz, 1, fx) if a == "y" else (dz, fy, 1)
                nxt.append((n, a, i, 0))
        out[(dz, fy, fx)] = [(n, w) for n, w, _, _ in nxt]
        todo += [(n, i, s) for n, _, i, s in nxt]
    return out


def hops(d):
    return abs(d[0]) + d[1] + d[2]


BACK = {"z+": "z-", "z-": "z+", "x": "x", "y": "y"}


def add_rows(acc, got, step=80):
    n = acc.shape[0]
    while n % step:
        step -= 16

    def body(i, _):
        r = pl.ds(pl.multiple_of(i * step, step), step)
        acc[r, :] = acc[r, :] + got[r, :]
        return 0

    lax.fori_loop(0, n // step, body, 0)


SHARD_UNITS = 656
PANEL = 128
GROUPS = ((0, 1), (2,), (3,), (4, 5, 6), (7, 8))

PLAN_OUT = (
    ("zy", "yz", "zy", "yz", "yz"),
    ("zyx", "zxy", "zyx", "yzx", "xzy"),
    (
        64, 65, 66, 0, 70, 1, 128, 2, 4, 5, 6, 137, 68, 3, 8, 9, 12, 7, 192, 130, 256, 140, 69, 10, 73, 129, 133, 136,
        13, 11, 74, 72, 67, 262, 14, 15, 71, 134, 131, 77, 132, 19, 76, 18, 75, 16, 320, 26, 135, 24, 138, 20, 78, 79,
        22, 141, 139, 195, 34, 257, 27, 81, 32, 193, 258, 25, 80, 35, 259, 83, 142, 143, 90, 30, 194, 266, 82, 196,
        39, 40, 144, 199, 84, 197, 260, 198, 263, 148, 147, 200, 261, 264, 31, 201, 202, 203, 98, 33, 29, 28, 42, 91,
        21, 155, 154, 36, 265, 204, 205, 269, 23, 268, 157, 267, 206, 164, 207, 86, 162, 17, 92, 103, 38, 88, 270, 37,
        271, 41, 210, 106, 161, 104, 96, 85, 99, 146, 150, 321, 322, 275, 160, 272, 211, 323, 273, 89, 153, 324, 100,
        101, 276, 208, 105, 168, 97, 165, 282, 217, 163, 218, 95, 209, 93, 87, 152, 214, 166, 325, 94, 151, 167, 102,
        280, 169, 290, 326, 277, 327, 159, 170, 225, 145, 221, 226, 216, 149, 156, 279, 158, 288, 212, 284, 328, 283,
        278, 228, 329, 295, 291, 213, 223, 219, 285, 232, 220, 330, 224, 296, 286, 292, 274, 289, 233, 230, 234, 229,
        281, 287, 222, 227, 231, 215, 294, 293, 298, 297,
    ),
)
PLAN_BACK = (
    ("zxy", "yzx", "zyx", "yzx", "xzy"),
    ("zy", "zy", "zy", "yz", "yz"),
    (
        256, 257, 258, 262, 261, 269, 64, 259, 67, 260, 65, 69, 263, 66, 78, 264, 271, 278, 276, 77, 270, 268, 267,
        71, 70, 275, 282, 85, 72, 266, 76, 265, 192, 82, 68, 199, 277, 73, 0, 84, 274, 74, 272, 5, 273, 80, 75, 279,
        6, 79, 13, 128, 204, 1, 281, 2, 12, 89, 283, 280, 11, 141, 129, 19, 8, 83, 4, 195, 86, 193, 87, 3, 134, 15, 7,
        81, 284, 285, 133, 88, 91, 14, 10, 197, 194, 90, 22, 196, 132, 286, 131, 201, 288, 287, 130, 16, 18, 21, 198,
        9, 92, 20, 205, 93, 291, 202, 200, 290, 136, 289, 143, 292, 26, 140, 208, 150, 206, 17, 94, 23, 135, 25, 212,
        213, 294, 95, 142, 203, 96, 24, 138, 148, 139, 207, 137, 211, 27, 214, 210, 100, 97, 295, 144, 215, 149, 104,
        146, 209, 147, 28, 29, 151, 218, 219, 217, 145, 154, 32, 101, 153, 106, 30, 216, 36, 155, 152, 296, 33, 220,
        105, 221, 293, 98, 156, 40, 157, 224, 31, 103, 298, 222, 160, 158, 223, 164, 102, 99, 228, 37, 161, 227, 165,
        41, 225, 168, 159, 226, 35, 42, 34, 229, 163, 297, 39, 231, 230, 232, 162, 167, 170, 234, 38, 166, 169, 233,
    ),
)


def layout(shapes, shards):
    table = []
    unit_at, row_at, flat_at = 0, 0, 0
    starts = [g[0] for g in GROUPS]
    for i, (rows, cols) in enumerate(shapes):
        if i in starts:
            unit_at = -(-unit_at // 16) * 16
        rb, panels = rows // shards, cols // PANEL
        units = rb * cols // 512
        padded = -(-rb // 16) * 16
        table.append((rb, panels, units, unit_at, row_at, padded, flat_at))
        unit_at += units
        row_at += padded * panels
        flat_at += units * shards
    return table, unit_at, row_at


def unit_places(units, table, shards):
    place = jnp.zeros_like(units)
    for _, _, n, first, _, _, lo in table:
        v = units - lo
        here = (v // n) * SHARD_UNITS + first + v % n
        place = jnp.where(v >= 0, here, place)
    return place


def own_units(owners, mine, capacity):
    count = owners.shape[0] // 128
    hit = (owners[:, 0] == mine).reshape(count, 128)
    lane = jnp.arange(128)
    tri = (lane[:, None] <= lane[None, :]).astype(jnp.bfloat16)
    within = jnp.dot(hit.astype(jnp.bfloat16), tri, preferred_element_type=jnp.float32)
    totals = within[:, 127].astype(jnp.int32)
    upto = jnp.sum(jnp.where(jnp.arange(count)[:, None] >= jnp.arange(count)[None, :], totals[None, :], 0), axis=1)
    slot = jnp.arange(capacity, dtype=jnp.int32)
    block = jnp.sum((upto[None, :] <= slot[:, None]).astype(jnp.int32), axis=1)
    pick = block[:, None] == jnp.arange(count)[None, :]
    before = jnp.sum(jnp.where(pick, (upto - totals)[None, :], 0), axis=1)
    row = jnp.dot(pick.astype(jnp.bfloat16), within.astype(jnp.bfloat16), preferred_element_type=jnp.float32)
    rank = (slot - before).astype(jnp.float32)
    at = jnp.sum((row <= rank[:, None]).astype(jnp.int32), axis=1)
    return block * 128 + at, slot < upto[count - 1]


BY_ROWS = (1, 3, 6, 8)


def position_table():
    cols = []
    for width in (DE, DD):
        side = width // 16 * 6
        parts = (width - 2 * side, side, side)
        tab = np.zeros((48, width), np.float64)
        col = 0
        for i, n in enumerate(parts):
            half = n // 2
            freq = 1.0 / 10000.0 ** (np.arange(half) / half)
            ang = np.arange(16)[:, None] * freq[None, :]
            tab[16 * i:16 * i + 16, col:col + n] = np.concatenate([np.sin(ang), np.cos(ang)], axis=1)
            col += n
        cols.append(tab)
    left = np.concatenate(cols, axis=1).astype(np.float32)
    terms = []
    for _ in range(3):
        terms.append(left.astype(ml_dtypes.bfloat16))
        left = left - terms[-1].astype(np.float32)
    return np.stack(terms)


def dot(a, b):
    return jnp.dot(a, b, preferred_element_type=jnp.float32)


def dot_nt(a, b):
    return lax.dot_general(a, b, (((1,), (1,)), ((), ())), preferred_element_type=jnp.float32)


def dot_tn(a, b):
    return lax.dot_general(a, b, (((0,), (0,)), ((), ())), preferred_element_type=jnp.float32)


def lanes(i, n=128):
    return pl.ds(pl.multiple_of(i * n, n), n)


def ln_parts(x):
    c = x - jnp.mean(x, axis=-1, keepdims=True)
    inv = lax.rsqrt(jnp.mean(c * c, axis=-1, keepdims=True) + NORM_EPS)
    return c * inv, inv


def ln_back(up, m, inv, gain):
    s = up * gain
    a = jnp.mean(s, axis=-1, keepdims=True)
    b = jnp.mean(s * m, axis=-1, keepdims=True)
    return inv * (s - a - m * b), jnp.sum(up * m, axis=0, keepdims=True), jnp.sum(up, axis=0, keepdims=True)


class Block:
    def __init__(self, width, heads, size, hidden, first, table, col):
        self.width, self.heads, self.size, self.hidden, self.col = width, heads, size, hidden, col
        self.q, self.o, self.a, self.b = table[first:first + 4]
        self.part = heads // 2 * size
        self.per = 128 // size


def panel(w, t, mat, g, lo=0, num=16):
    rb, _, _, _, at, padded, _ = mat
    rows = pl.ds(pl.multiple_of(at + g * padded, 16), padded)
    v = w[t, lo:lo + num, rows, :] if isinstance(lo, int) else w[t, pl.ds(lo, num), rows, :]
    if padded > rb:
        v = v.astype(jnp.float32)[:, :rb].reshape(num * rb, 128).astype(jnp.bfloat16)
        return v
    return v.reshape(num * rb, 128)


def pair(w, mat, g):
    return jnp.concatenate([panel(w, 0, mat, g), panel(w, 1, mat, g)], axis=1)


def repeat(count, step, f):
    step = max(k for k in range(1, step + 1) if count % k == 0)

    def turn(i, _):
        for k in range(step):
            f(i * step + k)
        return 0

    if step == count:
        turn(0, 0)
    else:
        lax.fori_loop(0, count // step, turn, 0)


def pull(acc, up, w, mat, step):
    count = mat[1]
    step = max(k for k in range(1, step + 1) if count % k == 0)

    def part(i):
        gs = [i * step + k for k in range(step)]
        d = jnp.concatenate([up[:, lanes(o + g)] for g in gs for o in (0, count)], axis=1)
        return dot_nt(d, jnp.concatenate([pair(w, mat, g) for g in gs], axis=1))

    acc[...] = part(0)

    def turn(i, _):
        acc[...] += part(i)
        return 0

    lax.fori_loop(1, count // step, turn, 0)


def block_fwd(b, x, xo, w, gains, biases, same, n1, proj, p, att, ow, m1, i1, n2, m2, i2, act, slope,
              need, keep):
    cols = slice(b.col, b.col + b.width)
    m, inv = ln_parts(x[...])
    m1[...] = m
    i1[...] = jnp.broadcast_to(inv, i1.shape)
    n1[...] = (m * gains[0:1, cols] + biases[0:1, cols]).astype(jnp.bfloat16)
    keep(0)
    yield
    need(0)
    gq = b.q[1]

    def qkv(g):
        r = dot(n1[...], pair(w, b.q, g)).astype(jnp.bfloat16)
        proj[:, lanes(g)] = r[:, :128]
        proj[:, lanes(gq + g)] = r[:, 128:]

    repeat(gq, 9, qkv)
    yield
    np_ = b.part // 128
    lane = lax.broadcasted_iota(jnp.int32, (256, 128), 1)
    masks = [lane // b.size == i for i in range(b.per)]

    def heads(i):
        t, j = i // np_, i % np_
        q = proj[:, lanes(t * gq + j)]
        k = proj[:, lanes(t * gq + np_ + j)]
        v = proj[:, lanes(t * gq + 2 * np_ + j)]
        total = jnp.zeros((256, 128), jnp.float32)
        for h in range(b.per):
            z = dot_nt(jnp.where(masks[h], q, 0), k) * b.size ** (-0.5) + same
            e = jnp.exp(z - jnp.max(z, axis=-1, keepdims=True))
            s = e * (1.0 / jnp.sum(e, axis=-1, keepdims=True))
            p[i * b.per + h] = s
            total = total + dot(s.astype(jnp.bfloat16), jnp.where(masks[h], v, 0))
        att[:, lanes(i)] = total.astype(jnp.bfloat16)

    repeat(np_, 3, heads)
    yield
    repeat(np_, 3, lambda i: heads(np_ + i))
    keep(1)
    yield
    need(1)
    for t in range(2):
        for g in range(b.width // 128):
            ow[t, :, g * 128:(g + 1) * 128] = panel(w, t, b.o, g)
    x1 = x[...] + dot(att[:, :b.part], ow[0]) + dot(att[:, b.part:], ow[1])
    xo[...] = x1
    m, inv = ln_parts(x1)
    m2[...] = m
    i2[...] = jnp.broadcast_to(inv, i2.shape)
    n2[...] = (m * gains[1:2, cols] + biases[1:2, cols]).astype(jnp.bfloat16)
    keep(2)
    yield
    need(2)
    ga = b.a[1]

    def up(g):
        h = dot(n2[...], pair(w, b.a, g))
        big = 0.5 * (1.0 + lax.erf(h * 0.7071067811865476))
        act_v = (h * big).astype(jnp.bfloat16)
        dens = big + h * (0.3989422804014327 * jnp.exp(-0.5 * h * h))
        act[:, lanes(g)] = act_v[:, :128]
        act[:, lanes(ga + g)] = act_v[:, 128:]
        slope[:, lanes(g)] = dens[:, :128]
        slope[:, lanes(ga + g)] = dens[:, 128:]

    repeat(ga, 12, up)
    keep(3)
    yield
    need(3)
    half = b.hidden // 2

    def down(g):
        w0 = jnp.concatenate([panel(w, 0, b.b, 2 * g), panel(w, 0, b.b, 2 * g + 1)], axis=1)
        w1 = jnp.concatenate([panel(w, 1, b.b, 2 * g), panel(w, 1, b.b, 2 * g + 1)], axis=1)
        xo[:, lanes(g, 256)] += dot(act[:, :half], w0) + dot(act[:, half:], w1)

    repeat(b.width // 256, 1, down)


def block_bwd(b, dr, w, gains, same, n1, proj, p, att, ow, m1, i1, n2, m2, i2, act, slope,
              r, dh, r1, dp_out, acc, da, norm_out, keep):
    cols = slice(b.col, b.col + b.width)
    r[...] = dr[...].astype(jnp.bfloat16)
    keep(3)
    half = b.hidden // 2
    rb = b.b[0]
    gb = b.width // 128
    num = 16

    def hidden(i, _):
        t, lo = i // (16 // num), (i % (16 // num)) * num
        wc = jnp.concatenate([panel(w, t, b.b, g, lo, num) for g in range(gb)], axis=1)
        at = lanes(i, num * rb)
        dh[:, at] = (dot_nt(r[...], wc) * slope[:, at]).astype(jnp.bfloat16)
        return 0

    lax.fori_loop(0, 2 * (16 // num), hidden, 0)
    keep(2)
    ga = b.a[1]
    pull(acc, dh, w, b.a, 12)
    dx, dg, db = ln_back(acc[...], m2[...], i2[:, :1], gains[1:2, cols])
    norm_out[1:2, cols] = dg
    norm_out[3:4, cols] = db
    dx1 = dr[...] + dx
    dr[...] = dx1
    r1[...] = dx1.astype(jnp.bfloat16)
    keep(1)
    for t in range(2):
        da[:, t * b.part:(t + 1) * b.part] = dot_nt(r1[...], ow[t]).astype(jnp.bfloat16)
    gq = b.q[1]
    np_ = b.part // 128
    lane = lax.broadcasted_iota(jnp.int32, (256, 128), 1)
    masks = [lane // b.size == i for i in range(b.per)]
    scale = b.size ** (-0.5)

    def heads(i):
        t, j = i // np_, i % np_
        q = proj[:, lanes(t * gq + j)]
        k = proj[:, lanes(t * gq + np_ + j)]
        v = proj[:, lanes(t * gq + 2 * np_ + j)]
        up_ = da[:, lanes(i)]
        dq = jnp.zeros((256, 128), jnp.float32)
        dk = jnp.zeros((256, 128), jnp.float32)
        dv = jnp.zeros((256, 128), jnp.float32)
        for h in range(b.per):
            s = p[i * b.per + h]
            u = jnp.where(masks[h], up_, 0)
            dp = dot_nt(u, v)
            dv = dv + dot_tn(s.astype(jnp.bfloat16), u)
            t1 = s * dp
            dz = (t1 - s * jnp.sum(t1, axis=-1, keepdims=True)).astype(jnp.bfloat16)
            dq = dq + dot(dz, jnp.where(masks[h], k, 0))
            dk = dk + dot_tn(dz, jnp.where(masks[h], q, 0))
        dp_out[:, lanes(t * gq + j)] = (dq * scale).astype(jnp.bfloat16)
        dp_out[:, lanes(t * gq + np_ + j)] = (dk * scale).astype(jnp.bfloat16)
        dp_out[:, lanes(t * gq + 2 * np_ + j)] = dv.astype(jnp.bfloat16)

    repeat(2 * np_, 2, heads)
    keep(0)
    pull(acc, dp_out, w, b.q, 9)
    dx, dg, db = ln_back(acc[...], m1[...], i1[:, :1], gains[0:1, cols])
    norm_out[0:1, cols] = dg
    norm_out[2:3, cols] = db
    dr[...] = dr[...] + dx


ACTS = (DE, DE, DE, FFE, DE, DD, DD, DD, FFD)
GRADS = (3 * DE, DE, FFE, DE, DD, 3 * DD, DD, FFD, DD)


def lookup(pos, tab, cols):
    row = lax.broadcasted_iota(jnp.int32, (48, 256), 0)
    spots = [jnp.concatenate([pos[0, i:i + 1, :], pos[1, i:i + 1, :]], axis=1) for i in range(3)]
    hot = jnp.logical_or(jnp.logical_or(row == spots[0], row == spots[1] + 16), row == spots[2] + 32)
    hot = jnp.where(hot, 1.0, 0.0).astype(jnp.bfloat16)
    return sum(dot_tn(hot, tab[i, :, cols]) for i in range(3))


def tile_mask(tile):
    ids = tile[lax.axis_index("tensor")]
    tiles = jnp.where(lax.broadcasted_iota(jnp.int32, (16, 256), 0) == ids, 1.0, 0.0).astype(jnp.bfloat16)
    return (1.0 - dot_tn(tiles, tiles)) * MASK_FILL


FWD_ACTS = [((256, n), jnp.bfloat16) for n in (DE, DE, DE, FFE)]
FWD_KEPT = [((256, 3 * DE), jnp.bfloat16), ((HE, 256, 256), jnp.float32), ((2, DE // 2, DE), jnp.bfloat16),
            ((256, DE), jnp.float32), ((256, 128), jnp.float32), ((256, DE), jnp.float32), ((256, 128), jnp.float32),
            ((256, FFE), jnp.float32)]


def chain_kernel(table, pos, tile, gains, biases, cot, tab, x2, w_hbm, *refs):
    fwd_hbm, refs = refs[:8], refs[8:]
    dec, dx0, norm_out = refs[:3]
    kept_out = refs[3:17]
    kept = refs[17:31]
    low, n1d, ad, n2d, ud, dpe, r1e, dhe, re, dlow, dpd, r1d, dhd, rd = kept
    fwd, refs = refs[31:39], refs[39:]
    proj_e, pe, ow_e, m1e, i1e, m2e, i2e, se = fwd
    (w, pd, sd, proj_d, da_e, da_d, ow_d, m1d, m2d, i1d, i2d, y, acc_e, acc_d, w_sem, f_sem, out_sem) = refs
    enc_b = Block(DE, HE, HDE, FFE, 0, table, 0)
    dec_b = Block(DD, HD, HDD, FFD, 5, table, DE)
    em = table[4]

    def load(m):
        rows = pl.ds(table[m][4], table[m][1] * table[m][5])
        return pltpu.make_async_copy(w_hbm.at[:, :, rows], w.at[:, :, rows], w_sem.at[m])

    def fetch(i):
        return pltpu.make_async_copy(fwd_hbm[i], fwd[i], f_sem.at[i])

    def store(i):
        return pltpu.make_async_copy(kept[i], kept_out[i], out_sem.at[i])

    for m in (4, 5, 6, 7, 8, 3, 2, 1, 0):
        if m != 1:
            load(m).start()
    for i in range(8):
        fetch(i).start()
    same = tile_mask(tile)
    low[...] = x2[...].astype(jnp.bfloat16)
    store(0).start()
    load(4).wait()
    for g in range(2):
        v = dot(low[...], pair(w, em, g)).astype(jnp.bfloat16).astype(jnp.float32)
        y[:, g * 128:(g + 1) * 128] = v[:, :128]
        y[:, 256 + g * 128:256 + (g + 1) * 128] = v[:, 128:]
    y[...] += lookup(pos, tab, slice(DE, DE + DD))
    for _ in block_fwd(dec_b, y, dec, w, gains, biases, same, n1d, proj_d, pd, ad, ow_d, m1d, i1d, n2d, m2d, i2d, ud, sd,
                       lambda k: load(5 + k).wait(), lambda k: store(1 + k).start()):
        pass
    y[...] = cot[...]
    block_bwd(dec_b, y, w, gains, same, n1d, proj_d, pd, ad, ow_d, m1d, i1d, n2d, m2d, i2d, ud, sd,
              rd, dhd, r1d, dpd, acc_d, da_d, norm_out, lambda k: store(10 + k).start())
    dlow[...] = y[...].astype(jnp.bfloat16)
    store(9).start()
    for g in range(2):
        d = jnp.concatenate([dlow[:, g * 128:(g + 1) * 128], dlow[:, 256 + g * 128:256 + (g + 1) * 128]], axis=1)
        v = dot_nt(d, pair(w, em, g))
        if g == 0:
            dx0[...] = v
        else:
            dx0[...] += v
    for m in (3, 2, 0):
        load(m).wait()
    for i in range(8):
        fetch(i).wait()
    block_bwd(enc_b, dx0, w, gains, same, None, proj_e, pe, None, ow_e, m1e, i1e, None, m2e, i2e, None, se,
              re, dhe, r1e, dpe, acc_e, da_e, norm_out, lambda k: store(5 + k).start())
    for i in range(14):
        store(i).wait()


def chain(pos, tile, gains, biases, cot, full, x2, fwd, table):
    f32, bf16 = jnp.float32, jnp.bfloat16
    S = jax.ShapeDtypeStruct
    outs = [S((256, DD), f32), S((256, DE), f32), S((4, DE + DD), f32)]
    kept = [(256, n) for n in ACTS[4:] + GRADS]
    outs += [S(k, bf16) for k in kept]
    V = pltpu.VMEM
    scratch = [V(k, bf16) for k in kept] + [V(k, t) for k, t in FWD_KEPT] + [
        V((2, 16) + full.shape[-2:], bf16), V((HD, 256, 256), f32), V((256, FFD), f32),
        V((256, 3 * DD), bf16), V((256, DE), bf16), V((256, DD), bf16), V((2, DD // 2, DD), bf16),
        V((256, DD), f32), V((256, DD), f32), V((256, 128), f32), V((256, 128), f32),
        V((256, DD), f32), V((256, DE), f32), V((256, DD), f32),
        pltpu.SemaphoreType.DMA((9,)), pltpu.SemaphoreType.DMA((8,)), pltpu.SemaphoreType.DMA((14,))]
    vmem = pl.BlockSpec(memory_space=pltpu.VMEM)
    hbm = pl.BlockSpec(memory_space=pl.ANY)
    args = (pos, tile, gains, biases, cot, jnp.asarray(position_table()), x2,
            full.reshape(2, 16, full.shape[-2], 128), *fwd)
    return pl.pallas_call(
        partial(chain_kernel, table), out_shape=outs, in_specs=[vmem] * 7 + [hbm] * 9, out_specs=[vmem] * 3 + [hbm] * 14,
        scratch_shapes=scratch, compiler_params=pltpu.CompilerParams(vmem_limit_bytes=63 << 20), name="chain",
        cost_estimate=pl.CostEstimate(flops=8_000_000_000, bytes_accessed=40_000_000, transcendentals=3_000_000),
    )(*args)


def grad_panels(table, m, act, grad, turned, put):
    mat = table[m]
    rb, panels, padded = mat[0], mat[1], mat[5]
    count = act.shape[1]

    def turn(i):
        turned[pl.ds(pl.multiple_of(i * 128, 128), 128), :] = act[:, lanes(i)].T

    repeat(count // 128, 6, turn)

    def place(t, g, v):
        if padded > rb:
            v = v.reshape(16, rb, 128)
            v = jnp.concatenate([v, jnp.zeros((16, padded - rb, 128), jnp.float32)], axis=1).astype(jnp.bfloat16)
        else:
            v = v.astype(jnp.bfloat16).reshape(16, rb, 128)
        put(t, g, v)

    if m in BY_ROWS:
        half = count // 2

        def body(i):
            t, g = i // (panels // 2), i % (panels // 2)
            v = dot(turned[pl.ds(pl.multiple_of(t * half, 128), half), :], grad[:, lanes(g, 256)])
            place(t, 2 * g, v[:, :128])
            place(t, 2 * g + 1, v[:, 128:])

        repeat(panels, 6, body)
    else:
        def body(g):
            d = jnp.concatenate([grad[:, lanes(g)], grad[:, lanes(panels + g)]], axis=1)
            v = dot(turned[:count, :], d)
            place(0, g, v[:, :128])
            place(1, g, v[:, 128:])

        repeat(panels, 6, body)


class Wires:
    def __init__(self, place, sem):
        self.place, self.sem, self.used, self.waits = place, sem, 0, []

    def new(self, n=1):
        self.used += n
        assert self.used <= self.sem.shape[0], self.used
        return self.used - n

    def copy(self, k, src, dst, way):
        return pltpu.make_async_remote_copy(src_ref=src, dst_ref=dst, send_sem=self.sem.at[k], recv_sem=self.sem.at[k + 1],
                                            device_id=self.place.ids[way], device_id_type=MESH)

    def send(self, k, src, dst, way, cond=None):
        cp = self.copy(k, src, dst, way)
        when(cond, cp.start)
        self.waits.append((cond, cp))

    def land(self, k, dst, cond=None):
        when(cond, self.copy(k, dst, dst, "c").wait_recv)

    def drain(self):
        for cond, cp in self.waits:
            when(cond, cp.wait_send)


def edge_slots(order):
    slots, used, shared = {}, 0, {}
    for d, kids in sorted(spread(order).items()):
        for _, way in kids:
            if way in "xy" and order.index("z") < order.index(way):
                key = (way, d[1], d[2])
                if key not in shared:
                    shared[key] = used
                    used += 4
                slots[d, way] = (shared[key], 4)
            else:
                slots[d, way] = (used, 1)
                used += 1
    return slots, used


def beyond(p, way):
    return p.z < 3 if way == "z+" else p.z > 0 if way == "z-" else None


def reduce_events(p, w, order, own, half, bufs, ready, done):
    tree = spread(order)
    pair = {d: w.new(2) for d in tree}
    wire = {d: w.new(2) for d in tree}
    parent = {nd: (d, way) for d, t in tree.items() for nd, way in t}
    slots, _ = edge_slots(order)

    def buffer(up, way):
        first, n = slots[up, way]
        return bufs.at[first + p.z + up[0] if n > 1 else first]

    events = []
    far = sorted(tree, key=lambda d: (-hops(d), d))
    for d in far:
        def act(d=d):
            cond = p.there(d)

            def step():
                acc = own(d)
                ready(d)
                w.land(pair[d], half(d))
                add_rows(acc, half(d))
                for nd, way in tree[d]:
                    buf = buffer(d, way)

                    def take(buf=buf, nd=nd):
                        w.land(wire[nd], buf)
                        add_rows(acc, buf)
                    when(beyond(p, way), take)
            when(cond, step)
            if hops(d) == 0:
                done()
            else:
                up, way = parent[d]
                w.send(wire[d], own(d), buffer(up, way), BACK[way], cond)
        events.append(act)

    def share(give):
        for d in far:
            w.send(pair[d], give(d), half(d), "c", p.there(d))

    return events, share, far


def gather_events(p, w, order, first, at):
    tree = spread(order)
    pair = {d: w.new(2) for d in tree}
    wire = {d: w.new(2) for d in tree}
    events = []
    for d in sorted(tree, key=lambda d: (hops(d), d)):
        def act(d=d):
            cond = p.there(d)
            blk = at(d, p.c)
            if hops(d):
                w.land(wire[d], blk, cond)
                src = blk
            else:
                src = first
            for nd, way in tree[d]:
                w.send(wire[nd], src, blk, way, both(cond, beyond(p, way)))
            w.send(pair[d], src, blk, "c", cond)
        events.append(act)

    def finish():
        for d in tree:
            w.land(pair[d], at(d, 1 - p.c), p.there(d))

    return events, finish


def run_events(lists, order, extra=iter(()), every=8):
    assert sorted(order) == sorted(64 * g + i for g, acts in enumerate(lists) for i in range(len(acts)))
    for n, k in enumerate(order):
        if n % every == 0:
            next(extra, None)
        lists[k // 64][k % 64]()
    for _ in extra:
        pass


def group_span(table, mats):
    first, last = table[mats[0]], table[mats[-1]]
    units = last[3] + last[2] - first[3]
    return first[3], -(-units // 16) * 16, first[4], last[4] + last[1] * last[5] - first[4]


def units_to_panels(table, mats, units, flat, put):
    base, count = table[mats[0]][3], units.shape[0]
    for k in range(4):
        flat[pl.ds(k, count, stride=4), :] = units[:, 128 * k:128 * (k + 1)].astype(jnp.float32)
    for m in mats:
        rb, panels, n, first, _, padded, _ = table[m]
        for g in range(panels):
            v = flat[pl.ds(4 * (first - base) + g, rb, stride=panels), :]
            if padded > rb:
                v = jnp.concatenate([v, jnp.zeros((padded - rb, 128), jnp.float32)], axis=0)
            put(m, g, v.astype(jnp.bfloat16))


def panels_to_units(table, mats, take, flat, units):
    base, count = table[mats[0]][3], units.shape[0]
    used = 0
    for m in mats:
        rb, panels, n, first, _, padded, _ = table[m]
        for g in range(panels):
            flat[pl.ds(4 * (first - base) + g, rb, stride=panels), :] = take(m, g)[:rb]
        used = 4 * (first - base + n)
    if used < 4 * count:
        flat[used:4 * count, :] = jnp.zeros((4 * count - used, 128), jnp.float32)
    for k in range(4):
        units[:, 128 * k:128 * (k + 1)] = flat[pl.ds(k, count, stride=4), :].astype(jnp.bfloat16)


def encoder_steps(p, table, out, tok, pos, x, x2, tile, gains, biases, tab, fwd, fwd_out, wv, w_sem, fwd_sem, swapped, arrived):
    n1, att, n2, act, proj, prob, ow, m1, i1, m2, i2, slope = fwd

    def load(m):
        rows = pl.ds(table[m][4], table[m][1] * table[m][5])
        return pltpu.make_async_copy(out.at[:, :, :, :, rows], wv.at[:, :, :, :, rows], w_sem.at[m])

    def store(i):
        return pltpu.make_async_copy(fwd[i], fwd_out[i], fwd_sem.at[i])

    def keep(k):
        for i in ((0, 7, 8), (1, 4, 5), (2, 6, 9, 10), (3, 11))[k]:
            store(i).start()

    for f in swapped:
        f()
    x[...] = tok[...].reshape(256, DE).astype(jnp.float32) + lookup(pos, tab, slice(0, DE))
    same = tile_mask(tile)
    whole = wv.reshape(2, 16, wv.shape[-2], 128)
    block = block_fwd(Block(DE, HE, HDE, FFE, 0, table, 0), x, x2, whole, gains, biases, same, n1, proj, prob, att, ow, m1, i1, n2,
                      m2, i2, act, slope, lambda k: load(k).wait(), keep)
    next(block)
    yield
    for f in arrived[0]:
        f()
    load(0).start()
    load(1).start()
    yield
    for _ in range(4):
        next(block)
        yield
    for f in arrived[1]:
        f()
    load(2).start()
    yield
    next(block)
    yield
    for f in arrived[2]:
        f()
    load(3).start()
    yield
    for _ in block:
        pass
    yield
    for i in range(12):
        store(i).wait()


class Swap:
    def __init__(self, p, w, src, out, give, keep):
        self.p, self.w, self.src, self.out, self.give, self.keep = p, w, src, out, give, keep
        self.k, self.own = w.new(2), w.new()

    def local(self):
        return pltpu.make_async_copy(self.src.at[self.keep], self.out.at[self.p.x], self.w.sem.at[self.own])

    def start(self):
        self.w.send(self.k, self.src.at[self.give], self.out.at[self.p.x], "x")

    def finish(self):
        self.w.land(self.k, self.out.at[1 - self.p.x])
        self.local().wait()


def weights_kernel(table, groups, plan, parts, tok_in, pos_in, cot_in, tile, gains, biases, tab, *refs):
    n = len(groups)
    out, pos, cot, x2 = refs[:4]
    fwd_out, tok, x, fwd, wv, w_sem, fwd_sem = refs[4:16], refs[16], refs[17], refs[18:30], refs[30], refs[31], refs[32]
    rest = refs[33:]
    accs, halves, bufs, shards = (rest[i * n:(i + 1) * n] for i in range(4))
    flat, sem = rest[4 * n:]
    p = Place()
    p.greet(["c", "y", "x"])
    w = Wires(p, sem)
    swaps = [Swap(p, w, a, b, 1 - p.x, p.x) for a, b in ((tok_in, tok), (pos_in, pos), (cot_in, cot))]
    for s in swaps:
        s.start()
        s.local().start()
    lists, finishes = [], []
    for g, mats in enumerate(groups):
        u0, un, r0, rn = group_span(table, mats)
        acc, half, buf, shard = accs[g], halves[g], bufs[g], shards[g]
        own_sem = w.new()
        loads = {d: w.new() for d in spread(plan[0][g])}

        def own(d, acc=acc):
            return acc.at[p.at(d)[1:]]

        def other(d, half=half):
            return half.at[p.at(d)[1:]]

        def load(d, u0=u0, un=un, own=own, loads=loads):
            return pltpu.make_async_copy(parts.at[p.at(d)[1:] + (p.c, pl.ds(u0, un))], own(d), sem.at[loads[d]])

        def ready(d, load=load):
            load(d).wait()

        def done(mats=mats, acc=acc, shard=shard, r0=r0):
            def put(m, i, v):
                lo = table[m][4] - r0 + i * table[m][5]
                shard[lo:lo + table[m][5], :] = v
            units_to_panels(table, mats, acc.at[p.z, p.y], flat, put)

        ev, share, far = reduce_events(p, w, plan[0][g], own, other, buf, ready, done)

        def begin(load=load, share=share, far=far, u0=u0, un=un):
            share(lambda d: parts.at[p.at(d)[1:] + (1 - p.c, pl.ds(u0, un))])
            for d in far:
                when(p.there(d), load(d).start)

        def at(d, core, r0=r0, rn=rn):
            t, z, y = p.at(d)
            return out.at[t, z, y, core, pl.ds(r0, rn)]

        def local(shard=shard, r0=r0, rn=rn, own_sem=own_sem):
            return pltpu.make_async_copy(shard, out.at[p.x, p.z, p.y, p.c, pl.ds(r0, rn)], sem.at[own_sem])

        ag, finish = gather_events(p, w, plan[1][g], shard, at)

        def send_first(act=ag[0], local=local):
            act()
            local().start()

        lists.append([begin] + ev + [send_first] + ag[1:])
        finishes += [finish, lambda local=local: local().wait()]
    steps = encoder_steps(p, table, out, tok, pos, x, x2, tile, gains, biases, tab, fwd, fwd_out, wv, w_sem, fwd_sem,
                          [s.finish for s in swaps[:2]], [finishes[2 * k:2 * k + 2] for k in range(3)])
    lists.append([partial(next, steps, None)] * 11)
    run_events(lists, plan[2])
    for f in finishes[6:] + [swaps[2].finish]:
        f()
    w.drain()


def spread_weights(parts, tokens, pos, cot, tile, gains, biases, table, rows, groups, plan, ident):
    spans = [group_span(table, m) for m in groups]
    bf16 = jnp.bfloat16
    S = jax.ShapeDtypeStruct
    V = pltpu.VMEM
    fwd = FWD_ACTS + FWD_KEPT
    enc_rows = table[4][4]
    scratch = [V(tokens.shape, tokens.dtype), V((256, DE), jnp.float32)] + [V(k, t) for k, t in fwd]
    scratch += [V((2, 4, 2, 2, enc_rows, 128), bf16), pltpu.SemaphoreType.DMA((4,)), pltpu.SemaphoreType.DMA((12,))]
    scratch += [V((4, 2, s[1], 512), bf16) for s in spans] * 2
    scratch += [V((edge_slots(o)[1], s[1], 512), bf16) for s, o in zip(spans, plan[0])]
    scratch += [V((s[3], 128), bf16) for s in spans]
    scratch += [V((4 * max(s[1] for s in spans), 128), jnp.float32),
                pltpu.SemaphoreType.DMA((len(groups) * (1 + 5 * 14 + 4 * 28) + 9,))]
    hbm = pl.BlockSpec(memory_space=pl.ANY)
    vmem = pl.BlockSpec(memory_space=pltpu.VMEM)
    return pl.pallas_call(
        partial(weights_kernel, table, groups, plan),
        out_shape=[S((2, 4, 2, 2, rows, 128), bf16), S(pos.shape, pos.dtype), S(cot.shape, cot.dtype), S((256, DE), jnp.float32)]
        + [S(k, t) for k, t in fwd],
        in_specs=[hbm] * 4 + [vmem] * 4, out_specs=[hbm, vmem, hbm, vmem] + [hbm] * 12,
        scratch_shapes=scratch,
        compiler_params=pltpu.CompilerParams(collective_id=ident, has_side_effects=True, vmem_limit_bytes=63 << 20),
        name="spread_weights",
    )(parts, tokens, pos, cot, tile, gains, biases, jnp.asarray(position_table()))


def return_kernel(table, groups, plan, *refs):
    n = len(groups)
    kept_in, small_src, dec_in, dx_in, out, small_out, dec, dx = refs[:18], *refs[18:25]
    rest = refs[25:]
    kept, rest = rest[:18], rest[18:]
    acts, grads = kept[:9], kept[9:]
    sides, halves, bufs, units = (rest[i * n:(i + 1) * n] for i in range(4))
    flat, turned, mid, line, load_sem, sem = rest[4 * n:]

    def load(i):
        return pltpu.make_async_copy(kept_in[i], kept[i], load_sem.at[i])

    first = sorted(range(n), key=lambda g: plan[2].index(64 * g))
    for g in first:
        for m in groups[g]:
            load(m).start()
            load(9 + m).start()
    p = Place()
    p.greet(["c", "y", "x"])
    w = Wires(p, sem)
    swaps = [Swap(p, w, a, b, 1 - p.x, p.x) for a, b in ((dec_in, dec), (dx_in, dx))]
    for s in swaps:
        s.local().start()
    swaps[0].start()
    lists, finishes = [], []
    for g, mats in enumerate(groups):
        u0, un, r0, rn = group_span(table, mats)
        side, half, buf, unit = sides[g], halves[g], bufs[g], units[g]
        own_sem = w.new()

        def own(d, side=side):
            return side.at[(p.c,) + p.at(d)]

        def other(d, half=half):
            return half.at[p.at(d)]

        def done(mats=mats, side=side, unit=unit, r0=r0):
            mine = side.at[p.c, p.x, p.z, p.y]

            def take(m, i):
                lo = table[m][4] - r0 + i * table[m][5]
                return mine[lo:lo + table[m][5], :].astype(jnp.float32)
            panels_to_units(table, mats, take, flat, unit)

        ev, share, far = reduce_events(p, w, plan[0][g], own, other, buf, lambda d: None, done)

        def begin(mats=mats, side=side, share=share, r0=r0):
            for m in mats:
                lo, padded = table[m][4] - r0, table[m][5]

                def put(t, i, v, lo=lo, padded=padded):
                    v = v.reshape(4, 2, 2, padded, 128)
                    rows = pl.ds(pl.multiple_of(lo + i * padded, 16), padded)
                    side[0, t, :, :, rows, :] = v[:, :, 0]
                    side[1, t, :, :, rows, :] = v[:, :, 1]
                load(m).wait()
                load(9 + m).wait()
                grad_panels(table, m, acts[m], grads[m], turned, put)
            share(lambda d: side.at[(1 - p.c,) + p.at(d)])

        def at(d, core, u0=u0, un=un):
            _, z, y = p.at(d)
            return out.at[z, y, core, pl.ds(u0, un)]

        def local(unit=unit, u0=u0, un=un, own_sem=own_sem):
            return pltpu.make_async_copy(unit, out.at[p.z, p.y, p.c, pl.ds(u0, un)], sem.at[own_sem])

        ag, finish = gather_events(p, w, plan[1][g], unit, at)

        def send_first(act=ag[0], local=local):
            act()
            local().start()

        lists.append([begin] + ev + [send_first] + ag[1:])
        finishes += [finish, lambda local=local: local().wait()]
    last = max(plan[2].index(64 * g + len(spread(plan[0][g]))) for g in range(n))
    g, i = plan[2][last] // 64, plan[2][last] % 64
    act = lists[g][i]

    def with_swaps():
        act()
        swaps[1].start()

    lists[g][i] = with_swaps
    run_events(lists, plan[2], total_steps(p, w, small_src, small_out, mid, line))
    for f in finishes + [s.finish for s in swaps]:
        f()
    w.drain()


def total_steps(p, w, src, out, mid, line):
    k = [w.new(2) for _ in range(9)]
    now = src
    for i, way in enumerate(("c", "x", "y")):
        w.send(k[i], now, mid.at[i], way)
        yield
        w.land(k[i], mid.at[i])
        nxt = mid.at[3 + i] if i < 2 else line.at[p.z]
        nxt[...] = now[...] + mid[i]
        now = nxt
    for i in range(4):
        lo, hi = jnp.maximum(p.z - i, 0), jnp.minimum(p.z + i, 3)
        if i > 0:
            w.land(k[2 + i], line.at[lo], p.z >= i)
            w.land(k[5 + i], line.at[hi], p.z + i <= 3)
        if i < 3:
            w.send(k[3 + i], line.at[lo], line.at[lo], "z+", jnp.logical_and(p.z >= i, p.z < 3))
            w.send(k[6 + i], line.at[hi], line.at[hi], "z-", jnp.logical_and(p.z + i <= 3, p.z > 0))
            yield
    out[...] = (line[0] + line[1]) + (line[2] + line[3])


def return_grads(kept, small, dec, dx, table, total_units, groups, plan, ident):
    spans = [group_span(table, m) for m in groups]
    bf16 = jnp.bfloat16
    S = jax.ShapeDtypeStruct
    V = pltpu.VMEM
    scratch = [V(v.shape, v.dtype) for v in kept]
    scratch += [V((2, 2, 4, 2, s[3], 128), bf16) for s in spans]
    scratch += [V((2, 4, 2, s[3], 128), bf16) for s in spans]
    scratch += [V((edge_slots(o)[1], s[3], 128), bf16) for s, o in zip(spans, plan[0])]
    scratch += [V((s[1], 512), bf16) for s in spans]
    scratch += [V((4 * max(s[1] for s in spans), 128), jnp.float32), V((FFE, 256), bf16),
                V((5,) + small.shape, small.dtype), V((4,) + small.shape, small.dtype), pltpu.SemaphoreType.DMA((18,)),
                pltpu.SemaphoreType.DMA((len(groups) * (1 + 4 * 14 + 4 * 28) + 24,))]
    vmem = pl.BlockSpec(memory_space=pltpu.VMEM)
    hbm = pl.BlockSpec(memory_space=pl.ANY)
    return pl.pallas_call(
        partial(return_kernel, table, groups, plan),
        out_shape=(S((4, 2, 2, total_units, 512), bf16), S(small.shape, small.dtype), S(dec.shape, dec.dtype), S(dx.shape, dx.dtype)),
        in_specs=[hbm] * 18 + [vmem, hbm, hbm], out_specs=(hbm, vmem, hbm, hbm),
        scratch_shapes=scratch,
        compiler_params=pltpu.CompilerParams(collective_id=ident, has_side_effects=True, vmem_limit_bytes=63 << 20),
        name="return_grads",
    )(*kept, small, dec, dx)


STEP_ROWS = 432


def update_kernel(place, spread, master, first, second, total, params, norm_first, norm_second, *refs):
    passed, refs = refs[:2], refs[2:]
    new_master, new_first, new_second, new_norms, new_nf, new_ns = refs[:6]
    i = pl.program_id(0)

    @pl.when(i == 0)
    def _():
        for a, b in zip(passed, refs[6:8]):
            b[...] = a[...]
        new_norms[...], new_nf[...], new_ns[...] = adamw(params[...], total[...], norm_first[...], norm_second[...], 0.0, NORM_RATE)

    lane = lax.broadcasted_iota(jnp.int32, (16, 128), 1)
    row = lax.broadcasted_iota(jnp.int32, (16, 128), 0)
    for k in range(STEP_ROWS // 16):
        tiles, spot = [], jnp.full((16, 128), -1, jnp.int32)
        for j in range(16):
            at = place[i * STEP_ROWS + 16 * k + j]
            tile = jnp.minimum(at >> 4, spread.shape[0] // 16 - 1)
            tiles.append(spread[pl.ds(pl.multiple_of(tile * 16, 16), 16), :])
            spot = jnp.where(row == j, jnp.where(at < spread.shape[0], 16 * j + (at & 15), -1), spot)
        here = slice(16 * k, 16 * k + 16)
        pick = jnp.concatenate([jnp.where(lane == spot, 1.0, 0.0), jnp.where(lane + 128 == spot, 1.0, 0.0)], axis=1)
        grad = dot(pick.astype(jnp.bfloat16), jnp.concatenate(tiles, axis=0))
        new_master[here, :], new_first[here, :], new_second[here, :] = adamw(
            master[here, :], grad, first[here, :], second[here, :], WEIGHT_DECAY, LEARN_RATE)


def update(place, spread, master, first, second, total, params, norm_first, norm_second, passed):
    slots = master.shape[0]
    S = jax.ShapeDtypeStruct
    rows = pl.BlockSpec((STEP_ROWS, 512), lambda i, s: (i, 0))
    whole = lambda v: pl.BlockSpec(v.shape, lambda i, s: (0, 0), pipeline_mode=pl.Buffered(1))
    small = pl.BlockSpec(params.shape, lambda i, s: (0, 0))
    out = [S(master.shape, jnp.float32)] * 3 + [S(params.shape, jnp.float32)] * 3 + [S(v.shape, v.dtype) for v in passed]
    both = [pl.BlockSpec(v.shape, lambda i, s: (0, 0, 0), pipeline_mode=pl.Buffered(1)) for v in passed]
    return pl.pallas_call(
        update_kernel, out_shape=out,
        grid_spec=pltpu.PrefetchScalarGridSpec(
            num_scalar_prefetch=1, grid=(slots // STEP_ROWS,),
            in_specs=[whole(spread), rows, rows, rows, small, small, small, small] + both,
            out_specs=[rows] * 3 + [small] * 3 + both),
        compiler_params=pltpu.CompilerParams(vmem_limit_bytes=62 << 20), name="update",
    )(place, spread, master, first, second, total, params, norm_first, norm_second, *passed)


def place_kernel(place_s, master, out, wide, staged, sem):
    count = wide.shape[0] // 64 - 1

    def clear(i, _):
        wide[pl.ds(pl.multiple_of(i * 64, 64), 64), :] = jnp.zeros((64, 512), jnp.float32)
        return 0

    lax.fori_loop(0, count, clear, 0)

    def turn(i, _):
        for j in range(16):
            wide[pl.ds(place_s[i * 16 + j], 1), :] = master[pl.ds(i * 16 + j, 1), :]
        return 0

    lax.fori_loop(0, master.shape[0] // 16, turn, 0)
    parts = 4
    part = count // parts * 64

    def copy(k):
        rows = pl.ds(pl.multiple_of(k * part, 64), part)
        return pltpu.make_async_copy(staged.at[rows], out.at[rows], sem.at[k])

    for k in range(parts):
        def narrow(i, _):
            rows = pl.ds(pl.multiple_of(k * part + i * 64, 64), 64)
            staged[rows, :] = wide[rows, :].astype(jnp.bfloat16)
            return 0

        lax.fori_loop(0, part // 64, narrow, 0)
        copy(k).start()
    for k in range(parts):
        copy(k).wait()


def place_blocks(place, master, rows):
    return pl.pallas_call(
        place_kernel, out_shape=jax.ShapeDtypeStruct((rows, 512), jnp.bfloat16),
        grid_spec=pltpu.PrefetchScalarGridSpec(
            num_scalar_prefetch=1, grid=(1,),
            in_specs=[pl.BlockSpec(master.shape, lambda i, s: (0, 0), pipeline_mode=pl.Buffered(1))],
            out_specs=pl.BlockSpec(memory_space=pl.ANY),
            scratch_shapes=[pltpu.VMEM((rows + 64, 512), jnp.float32), pltpu.VMEM((rows, 512), jnp.bfloat16), pltpu.SemaphoreType.DMA((4,))]),
        compiler_params=pltpu.CompilerParams(vmem_limit_bytes=60 << 20), name="place_blocks",
    )(place, master)


def sequence_device(tokens_in, positions, segment_ids, owners, master, first_moment, second_moment, norm_gains,
                    norm_biases, norm_first, norm_second, cotangent):
    shapes = weight_shapes(2)
    table, _, rows = layout(shapes, 16)
    unit, used = own_units(owners, lax.axis_index("dp"), master.shape[0])
    place = jnp.where(used, unit_places(unit, table, 16), 16 * SHARD_UNITS)
    parts = place_blocks(place, master, 16 * SHARD_UNITS)
    full, pos, cot, x2, *fwd = spread_weights(parts.reshape(4, 2, 2, SHARD_UNITS, 512), tokens_in, positions.transpose(1, 0, 2),
                                              cotangent, segment_ids, norm_gains, norm_biases, table, rows, GROUPS, PLAN_OUT, 1)
    kept = chain(pos, segment_ids, norm_gains, norm_biases, cot.reshape(256, DD), full, x2, fwd[4:], table)
    decoded, dx0, norms = kept[:3]
    spread_out, norm_total, decoded, dx0 = return_grads([*fwd[:4], *kept[3:]], norms, decoded.reshape(2, 128, DD), dx0.reshape(2, 128, DE), table,
                                                        SHARD_UNITS, GROUPS, PLAN_BACK, 2)
    norm_params = jnp.concatenate([norm_gains, norm_biases], axis=0)
    new_master, new_first, new_second, new_norms, norm_one_new, norm_two_new, decoded, dx0 = update(
        place, spread_out.reshape(16 * SHARD_UNITS, 512), master, first_moment, second_moment, norm_total, norm_params, norm_first, norm_second,
        (decoded, dx0))
    return (decoded, dx0, new_master, new_first, new_second, new_norms, norm_one_new, norm_two_new)


def solution(mesh):
    step = sequence_device if (mesh.shape["dp"], mesh.shape["tensor"]) == (16, 2) else per_device
    return jax.shard_map(
        step,
        mesh=mesh,
        in_specs=(
            P(None, ("dp", "tensor"), None),
            P(None, None, ("dp", "tensor")),
            P(None, "dp", None),
            P(),
            P("dp", "tensor"),
            P("dp", "tensor"),
            P("dp", "tensor"),
            P(),
            P(),
            P(),
            P(),
            P(None, ("dp", "tensor"), None),
        ),
        out_specs=(
            P(None, ("dp", "tensor"), None),
            P(None, ("dp", "tensor"), None),
            P("dp", "tensor"),
            P("dp", "tensor"),
            P("dp", "tensor"),
            P(),
            P(),
            P(),
        ),
        check_vma=False,
    )
```

```python
from functools import partial

import jax
import jax.numpy as jnp
import ml_dtypes
import numpy as np
from jax import lax
from jax.experimental import pallas as pl
from jax.experimental.pallas import tpu as pltpu
from jax.sharding import PartitionSpec as P

DE = 768
HE = 12
HDE = 64
FFE = 3072
DD = 512
HD = 16
HDD = 32
FFD = 2048
STEP = 10


NORM_EPS = 1e-06
BETA_ONE = 0.5
BETA_TWO = 0.5
LEARN_RATE = 0.03
NORM_RATE = 0.3
WEIGHT_DECAY = 0.05
ADAM_EPS = 1e-08
MASK_FILL = -1000000000.0


def sincos_part(coordinate, part_width):
    halfway = part_width // 2
    frequency = 1.0 / 10000.0 ** (jnp.arange(halfway, dtype=jnp.float32) / halfway)
    angles = coordinate.astype(jnp.float32)[:, None] * frequency[None, :]
    return jnp.concatenate([jnp.sin(angles), jnp.cos(angles)], axis=1)


def sincos_embed(positions, model_width):
    side_width = model_width // 16 * 6
    first_width = model_width - 2 * side_width
    return jnp.concatenate(
        [
            sincos_part(positions[0], first_width),
            sincos_part(positions[1], side_width),
            sincos_part(positions[2], side_width),
        ],
        axis=1,
    )


def slot_table(owners, devices, capacity):
    owner_ids = owners[:, 0]
    onehot = (owner_ids[:, None] == jnp.arange(devices, dtype=jnp.int32)[None, :]).astype(jnp.int32)
    before = jnp.cumsum(onehot, axis=0) - onehot
    owner_rank = jnp.sum(before * onehot, axis=1)
    return owner_ids * capacity + owner_rank


def weight_shapes(tensor_count):
    enc_heads = HE // tensor_count
    dec_heads = HD // tensor_count
    return [
        (DE, 3 * enc_heads * HDE),
        (enc_heads * HDE, DE),
        (DE, FFE // tensor_count),
        (FFE // tensor_count, DE),
        (DE, DD // tensor_count),
        (DD, 3 * dec_heads * HDD),
        (dec_heads * HDD, DD),
        (DD, FFD // tensor_count),
        (FFD // tensor_count, DD),
    ]


def split_flat(flat_vector, shapes):
    pieces = []
    offset = 0
    for matrix_shape in shapes:
        length = matrix_shape[0] * matrix_shape[1]
        pieces.append(flat_vector[offset : offset + length].reshape(matrix_shape))
        offset += length
    return pieces


def adamw(weights, gradient, moment_one, moment_two, decay_rate, step_rate):
    one_new = BETA_ONE * moment_one + (1.0 - BETA_ONE) * gradient
    two_new = BETA_TWO * moment_two + (1.0 - BETA_TWO) * gradient * gradient
    one_hat = one_new / (1.0 - BETA_ONE**STEP)
    two_hat = two_new / (1.0 - BETA_TWO**STEP)
    weights_new = weights - step_rate * (
        one_hat / (jnp.sqrt(two_hat) + ADAM_EPS) + decay_rate * weights
    )
    return (weights_new, one_new, two_new)


def norm_forward(values, gain_row, bias_row):
    center = values - jnp.mean(values, axis=-1, keepdims=True)
    spread = jnp.mean(center * center, axis=-1, keepdims=True)
    inverse = lax.rsqrt(spread + NORM_EPS)
    normed = center * inverse
    return (normed * gain_row + bias_row, (normed, inverse))


def norm_backward(upstream, stored, gain_row):
    normed, inverse = stored
    scaled = upstream * gain_row
    mean_one = jnp.mean(scaled, axis=-1, keepdims=True)
    mean_two = jnp.mean(scaled * normed, axis=-1, keepdims=True)
    return (
        inverse * (scaled - mean_one - normed * mean_two),
        jnp.sum(upstream * normed, axis=0),
        jnp.sum(upstream, axis=0),
    )


def inner_rows(left_side, right_side):
    return lax.dot_general(
        left_side, right_side, (((0,), (0,)), ((), ())), preferred_element_type=jnp.float32
    )


def times_transpose(left_side, right_side):
    return lax.dot_general(
        left_side, right_side, (((1,), (1,)), ((), ())), preferred_element_type=jnp.float32
    )


def gather_rows(values):
    return lax.all_gather(values, "tensor", axis=0, tiled=True)


def gather_grads(values):
    return lax.all_gather(values, "tensor", axis=0, tiled=True)


def branch_rows(values, weight):
    return lax.psum_scatter(
        jnp.dot(values, weight, preferred_element_type=jnp.float32).astype(jnp.bfloat16),
        "tensor",
        scatter_dimension=0,
        tiled=True,
    ).astype(jnp.float32)


def input_rows(values, weight):
    return lax.psum_scatter(
        times_transpose(values, weight).astype(jnp.bfloat16),
        "tensor",
        scatter_dimension=0,
        tiled=True,
    ).astype(jnp.float32)


def block_scores(queries, key_rows, mask_bias, block_start, block_rows, head_size):
    scores = jnp.einsum(
        "qhd,khd->hqk", queries, key_rows, preferred_element_type=jnp.float32
    ) * head_size ** (-0.5)
    return scores + mask_bias[None, block_start : block_start + block_rows]


def attention_forward(gathered, w_qkv, head_count, head_size, mask_bias):
    length = gathered.shape[0]
    projected = jnp.dot(gathered, w_qkv, preferred_element_type=jnp.float32).astype(jnp.bfloat16)
    projected = projected.reshape(length, 3, head_count, head_size)
    queries = projected[:, 0]
    key_rows = projected[:, 1]
    value_rows = projected[:, 2]
    block_rows = min(512, length)
    scores = block_scores(queries, key_rows, mask_bias, 0, block_rows, head_size)
    row_peak = jnp.max(scores, axis=-1, keepdims=True)
    row_total = row_peak + jnp.log(jnp.sum(jnp.exp(scores - row_peak), axis=-1, keepdims=True))
    weights = jnp.exp(scores - row_total).astype(jnp.bfloat16)
    outputs = jnp.einsum("hqk,khd->qhd", weights, value_rows, preferred_element_type=jnp.float32)
    totals = [row_total]
    attended = outputs.astype(jnp.bfloat16).reshape(length, head_count * head_size)
    return (attended, (queries, key_rows, value_rows, totals))


def attention_backward(upstream, w_out, attended, stored, head_count, head_size, mask_bias):
    queries, key_rows, value_rows, totals = stored
    length = upstream.shape[0]
    score_scale = head_size ** (-0.5)
    grad_out = inner_rows(attended, upstream)
    attended_grad = (
        times_transpose(upstream, w_out).astype(jnp.bfloat16).reshape(length, head_count, head_size)
    )
    block_rows = min(512, length)
    key_grads = jnp.zeros((length, head_count, head_size), jnp.float32)
    value_grads = jnp.zeros((length, head_count, head_size), jnp.float32)
    query_grads = []
    for number, block_start in enumerate(range(0, length, block_rows)):
        scores = block_scores(queries, key_rows, mask_bias, block_start, block_rows, head_size)
        weights = jnp.exp(scores - totals[number])
        value_grads = jnp.einsum(
            "hqk,qhd->khd",
            weights.astype(jnp.bfloat16),
            attended_grad,
            preferred_element_type=jnp.float32,
        )
        weight_grads = jnp.einsum(
            "qhd,khd->hqk", attended_grad, value_rows, preferred_element_type=jnp.float32
        )
        score_grads = (
            weights * (weight_grads - jnp.sum(weights * weight_grads, axis=-1, keepdims=True))
        ).astype(jnp.bfloat16)
        query_grads.append(
            jnp.einsum("hqk,khd->qhd", score_grads, key_rows, preferred_element_type=jnp.float32)
            * score_scale
        )
        key_grads = (
            jnp.einsum("hqk,qhd->khd", score_grads, queries, preferred_element_type=jnp.float32)
            * score_scale
        )
    projected_grad = jnp.stack([query_grads[0], key_grads, value_grads], axis=1)
    return (
        projected_grad.astype(jnp.bfloat16).reshape(length, 3 * head_count * head_size),
        grad_out,
    )


def block_forward(residual, matrices, gain_rows, bias_rows, head_count, head_size, mask_bias):
    w_qkv, w_out, w_in, w_down = matrices
    normed, norm_one = norm_forward(residual, gain_rows[0], bias_rows[0])
    gathered = gather_rows(normed.astype(jnp.bfloat16))
    attended, stored = attention_forward(gathered, w_qkv, head_count, head_size, mask_bias)
    middle = residual + branch_rows(attended, w_out)
    normed_two, norm_two = norm_forward(middle, gain_rows[1], bias_rows[1])
    gathered_two = gather_rows(normed_two.astype(jnp.bfloat16))
    hidden = jnp.dot(gathered_two, w_in, preferred_element_type=jnp.float32)
    active = jax.nn.gelu(hidden, approximate=False).astype(jnp.bfloat16)
    result = middle + branch_rows(active, w_down)
    return (result, (gathered, norm_one, attended, stored, gathered_two, norm_two, hidden, active))


def block_backward(upstream, matrices, gain_rows, saved_values, head_count, head_size, mask_bias):
    w_qkv, w_out, w_in, w_down = matrices
    gathered, norm_one, attended, stored, gathered_two, norm_two, hidden, active = saved_values
    down_full = gather_grads(upstream.astype(jnp.bfloat16))
    grad_down = inner_rows(active, down_full)
    active_grad = times_transpose(down_full, w_down)
    gelu_pull = jax.vjp(partial(jax.nn.gelu, approximate=False), hidden)[1]
    hidden_grad = gelu_pull(active_grad)[0].astype(jnp.bfloat16)
    grad_in = inner_rows(gathered_two, hidden_grad)
    normed_two_grad = input_rows(hidden_grad, w_in)
    middle_grad, gain_two, bias_two = norm_backward(normed_two_grad, norm_two, gain_rows[1])
    middle_grad = upstream + middle_grad
    middle_full = gather_grads(middle_grad.astype(jnp.bfloat16))
    projected_grad, grad_out = attention_backward(
        middle_full, w_out, attended, stored, head_count, head_size, mask_bias
    )
    grad_qkv = inner_rows(gathered, projected_grad)
    normed_grad = input_rows(projected_grad, w_qkv)
    input_grad, gain_one, bias_one = norm_backward(normed_grad, norm_one, gain_rows[0])
    return (
        middle_grad + input_grad,
        [grad_qkv, grad_out, grad_in, grad_down],
        (gain_one, gain_two, bias_one, bias_two),
    )


def embed_forward(residual, w_embed):
    residual_low = gather_rows(residual.astype(jnp.bfloat16))
    columns = jnp.dot(residual_low, w_embed, preferred_element_type=jnp.float32).astype(
        jnp.bfloat16
    )
    own_columns = lax.all_to_all(columns, "tensor", split_axis=0, concat_axis=1, tiled=True)
    return (own_columns.astype(jnp.float32), residual_low)


def embed_backward(upstream, residual_low, w_embed):
    columns = lax.all_to_all(
        upstream.astype(jnp.bfloat16), "tensor", split_axis=1, concat_axis=0, tiled=True
    )
    grad_embed = inner_rows(residual_low, columns)
    return (input_rows(columns, w_embed), grad_embed)


def slot_builder(gradients, unit_of_slot, unit_width):
    flat_units = jnp.concatenate([gradient.reshape(-1) for gradient in gradients]).reshape(
        -1, unit_width
    )
    unit_total = flat_units.shape[0]
    source = jnp.take(flat_units, jnp.clip(unit_of_slot, 0, unit_total - 1), axis=0)
    return jnp.where((unit_of_slot >= 0)[:, None], source, 0.0)


def per_device(
    tokens_in,
    positions,
    segment_ids,
    owners,
    master,
    first_moment,
    second_moment,
    norm_gains,
    norm_biases,
    norm_first,
    norm_second,
    cotangent,
):
    devices = lax.axis_size("dp")
    tensor_count = lax.axis_size("tensor")
    capacity = master.shape[0]
    unit_width = master.shape[1]
    unit_count = owners.shape[0]
    slot_index = slot_table(owners, devices, capacity)
    unit_of_slot = (
        jnp.full((devices * capacity,), -1, jnp.int32)
        .at[slot_index]
        .set(jnp.arange(unit_count, dtype=jnp.int32))
    )
    targets = unit_of_slot
    targets = jnp.where(targets < 0, unit_count, targets)
    placed = (
        jnp.zeros((unit_count, unit_width), jnp.bfloat16)
        .at[targets]
        .set(lax.all_gather(master.astype(jnp.bfloat16), "dp", axis=0, tiled=True), mode="drop")
    )
    shapes = weight_shapes(tensor_count)
    matrices = split_flat(placed.reshape(-1), shapes)
    encoder = matrices[0:4]
    w_embed = matrices[4]
    decoder = matrices[5:9]
    enc_heads = HE // tensor_count
    dec_heads = HD // tensor_count
    micro_count = tokens_in.shape[0]
    grad_sums = [jnp.zeros(matrix_shape, jnp.float32) for matrix_shape in shapes]
    norm_sums = jnp.zeros((4, DE + DD), jnp.float32)
    decoded_rows = []
    token_grads = []
    for micro_step in range(micro_count):
        tile_ids = segment_ids[micro_step, 0]
        mask_bias = jnp.where(tile_ids[:, None] == tile_ids[None, :], 0.0, MASK_FILL).astype(
            jnp.float32
        )
        position_now = positions[:, micro_step]
        residual = tokens_in[micro_step].astype(jnp.float32) + sincos_embed(position_now, DE)
        residual, enc_saved = block_forward(
            residual, encoder, norm_gains[:, :DE], norm_biases[:, :DE], enc_heads, HDE, mask_bias
        )
        residual, embed_low = embed_forward(residual, w_embed)
        residual = residual + sincos_embed(position_now, DD)
        residual, dec_saved = block_forward(
            residual, decoder, norm_gains[:, DE:], norm_biases[:, DE:], dec_heads, HDD, mask_bias
        )
        decoded_rows.append(residual)
        upstream, dec_grads, dec_norm = block_backward(
            cotangent[micro_step], decoder, norm_gains[:, DE:], dec_saved, dec_heads, HDD, mask_bias
        )
        upstream, grad_embed = embed_backward(upstream, embed_low, w_embed)
        upstream, enc_grads, enc_norm = block_backward(
            upstream, encoder, norm_gains[:, :DE], enc_saved, enc_heads, HDE, mask_bias
        )
        token_grads.append(upstream)
        step_grads = enc_grads + [grad_embed] + dec_grads
        step_norm = jnp.concatenate([jnp.stack(enc_norm), jnp.stack(dec_norm)], axis=1)
        grad_sums = [total_grad + new_grad for total_grad, new_grad in zip(grad_sums, step_grads)]
        norm_sums = norm_sums + step_norm
    reduced = lax.psum_scatter(
        slot_builder(grad_sums, unit_of_slot, unit_width), "dp", scatter_dimension=0, tiled=True
    )
    norm_total = lax.psum(norm_sums, ("dp", "tensor"))
    new_master, new_first, new_second = adamw(
        master, reduced, first_moment, second_moment, WEIGHT_DECAY, LEARN_RATE
    )
    norm_params = jnp.concatenate([norm_gains, norm_biases], axis=0)
    new_norms, norm_one_new, norm_two_new = adamw(
        norm_params, norm_total, norm_first, norm_second, 0.0, NORM_RATE
    )
    return (
        jnp.stack(decoded_rows),
        jnp.stack(token_grads),
        new_master,
        new_first,
        new_second,
        new_norms,
        norm_one_new,
        norm_two_new,
    )


MESH = pl.DeviceIdType.MESH
ALL = slice(None)


class Place:
    def __init__(self):
        self.d = lax.axis_index("dp")
        self.x = lax.axis_index("tensor")
        self.z = self.d // 4
        self.y = (self.d // 2) % 2
        self.c = self.d % 2
        self.ids = {
            "c": (self.d + 1 - 2 * self.c, self.x),
            "y": (self.d + 2 - 4 * self.y, self.x),
            "x": (self.d, 1 - self.x),
            "z+": (self.d + 4, self.x),
            "z-": (self.d - 4, self.x),
        }

    def greet(self, kinds):
        bar = pltpu.get_barrier_semaphore()
        for k in kinds:
            pl.semaphore_signal(bar, inc=1, device_id=self.ids[k], device_id_type=MESH)

        @pl.when(self.z < 3)
        def _():
            pl.semaphore_signal(bar, inc=1, device_id=self.ids["z+"], device_id_type=MESH)

        @pl.when(self.z > 0)
        def _():
            pl.semaphore_signal(bar, inc=1, device_id=self.ids["z-"], device_id_type=MESH)

        inner = jnp.where(jnp.logical_and(self.z > 0, self.z < 3), 1, 0)
        pl.semaphore_wait(bar, len(kinds) + 1 + inner)

    def there(self, disp):
        dz = disp[0]
        if dz == 0:
            return None
        return self.z + dz <= 3 if dz > 0 else self.z + dz >= 0

    def at(self, disp):
        dz, fy, fx = disp
        return (1 - self.x if fx else self.x, self.z + dz, 1 - self.y if fy else self.y)


def when(cond, f):
    if cond is None:
        f()
    else:
        pl.when(cond)(f)


def both(a, b):
    if a is None:
        return b
    if b is None:
        return a
    return jnp.logical_and(a, b)


def spread(order):
    out = {}
    todo = [((0, 0, 0), -1, 0)]
    while todo:
        (dz, fy, fx), last, way = todo.pop(0)
        nxt = []
        for i, a in enumerate(order):
            if i < last:
                continue
            if a == "z":
                for s in (1, -1):
                    if i == last and s != way:
                        continue
                    n = (dz - s, fy, fx)
                    if abs(n[0]) <= 3:
                        nxt.append((n, "z+" if s > 0 else "z-", i, s))
            elif i > last:
                n = (dz, 1, fx) if a == "y" else (dz, fy, 1)
                nxt.append((n, a, i, 0))
        out[(dz, fy, fx)] = [(n, w) for n, w, _, _ in nxt]
        todo += [(n, i, s) for n, _, i, s in nxt]
    return out


def hops(d):
    return abs(d[0]) + d[1] + d[2]


BACK = {"z+": "z-", "z-": "z+", "x": "x", "y": "y"}


def add_rows(acc, got, step=80):
    n = acc.shape[0]
    while n % step:
        step -= 16

    def body(i, _):
        r = pl.ds(pl.multiple_of(i * step, step), step)
        acc[r, :] = acc[r, :] + got[r, :]
        return 0

    lax.fori_loop(0, n // step, body, 0)


SHARD_UNITS = 656
PANEL = 128
GROUPS = ((0, 1), (2,), (3,), (4, 5, 6), (7, 8))

PLAN_OUT = (
    ("zy", "yz", "zy", "yz", "yz"),
    ("zyx", "zxy", "zyx", "yzx", "xzy"),
    (
        64, 65, 66, 0, 70, 1, 128, 2, 4, 5, 6, 137, 68, 3, 8, 9, 12, 7, 192, 130, 256, 140, 69, 10, 73, 129, 133, 136,
        13, 11, 74, 72, 67, 262, 14, 15, 71, 134, 131, 77, 132, 19, 76, 18, 75, 16, 320, 26, 135, 24, 138, 20, 78, 79,
        22, 141, 139, 195, 34, 257, 27, 81, 32, 193, 258, 25, 80, 35, 259, 83, 142, 143, 90, 30, 194, 266, 82, 196,
        39, 40, 144, 199, 84, 197, 260, 198, 263, 148, 147, 200, 261, 264, 31, 201, 202, 203, 98, 33, 29, 28, 42, 91,
        21, 155, 154, 36, 265, 204, 205, 269, 23, 268, 157, 267, 206, 164, 207, 86, 162, 17, 92, 103, 38, 88, 270, 37,
        271, 41, 210, 106, 161, 104, 96, 85, 99, 146, 150, 321, 322, 275, 160, 272, 211, 323, 273, 89, 153, 324, 100,
        101, 276, 208, 105, 168, 97, 165, 282, 217, 163, 218, 95, 209, 93, 87, 152, 214, 166, 325, 94, 151, 167, 102,
        280, 169, 290, 326, 277, 327, 159, 170, 225, 145, 221, 226, 216, 149, 156, 279, 158, 288, 212, 284, 328, 283,
        278, 228, 329, 295, 291, 213, 223, 219, 285, 232, 220, 330, 224, 296, 286, 292, 274, 289, 233, 230, 234, 229,
        281, 287, 222, 227, 231, 215, 294, 293, 298, 297,
    ),
)
PLAN_BACK = (
    ("zxy", "yzx", "zyx", "yzx", "xzy"),
    ("zy", "zy", "zy", "yz", "yz"),
    (
        256, 257, 258, 262, 261, 269, 64, 259, 67, 260, 65, 69, 263, 66, 78, 264, 271, 278, 276, 77, 270, 268, 267,
        71, 70, 275, 282, 85, 72, 266, 76, 265, 192, 82, 68, 199, 277, 73, 0, 84, 274, 74, 272, 5, 273, 80, 75, 279,
        6, 79, 13, 128, 204, 1, 281, 2, 12, 89, 283, 280, 11, 141, 129, 19, 8, 83, 4, 195, 86, 193, 87, 3, 134, 15, 7,
        81, 284, 285, 133, 88, 91, 14, 10, 197, 194, 90, 22, 196, 132, 286, 131, 201, 288, 287, 130, 16, 18, 21, 198,
        9, 92, 20, 205, 93, 291, 202, 200, 290, 136, 289, 143, 292, 26, 140, 208, 150, 206, 17, 94, 23, 135, 25, 212,
        213, 294, 95, 142, 203, 96, 24, 138, 148, 139, 207, 137, 211, 27, 214, 210, 100, 97, 295, 144, 215, 149, 104,
        146, 209, 147, 28, 29, 151, 218, 219, 217, 145, 154, 32, 101, 153, 106, 30, 216, 36, 155, 152, 296, 33, 220,
        105, 221, 293, 98, 156, 40, 157, 224, 31, 103, 298, 222, 160, 158, 223, 164, 102, 99, 228, 37, 161, 227, 165,
        41, 225, 168, 159, 226, 35, 42, 34, 229, 163, 297, 39, 231, 230, 232, 162, 167, 170, 234, 38, 166, 169, 233,
    ),
)


def layout(shapes, shards):
    table = []
    unit_at, row_at, flat_at = 0, 0, 0
    starts = [g[0] for g in GROUPS]
    for i, (rows, cols) in enumerate(shapes):
        if i in starts:
            unit_at = -(-unit_at // 16) * 16
        rb, panels = rows // shards, cols // PANEL
        units = rb * cols // 512
        table.append((rb, panels, units, unit_at, row_at, rb, flat_at))
        unit_at += units
        row_at += rb * panels
        flat_at += units * shards
    return table, unit_at, row_at


def unit_places(units, table, shards):
    place = jnp.zeros_like(units)
    for _, _, n, first, _, _, lo in table:
        v = units - lo
        here = (v // n) * SHARD_UNITS + first + v % n
        place = jnp.where(v >= 0, here, place)
    return place


def own_units(owners, mine, capacity):
    count = owners.shape[0] // 128
    hit = (owners[:, 0] == mine).reshape(count, 128)
    lane = jnp.arange(128)
    tri = (lane[:, None] <= lane[None, :]).astype(jnp.bfloat16)
    within = jnp.dot(hit.astype(jnp.bfloat16), tri, preferred_element_type=jnp.float32)
    totals = within[:, 127].astype(jnp.int32)
    upto = jnp.sum(jnp.where(jnp.arange(count)[:, None] >= jnp.arange(count)[None, :], totals[None, :], 0), axis=1)
    slot = jnp.arange(capacity, dtype=jnp.int32)
    block = jnp.sum((upto[None, :] <= slot[:, None]).astype(jnp.int32), axis=1)
    pick = block[:, None] == jnp.arange(count)[None, :]
    before = jnp.sum(jnp.where(pick, (upto - totals)[None, :], 0), axis=1)
    row = jnp.dot(pick.astype(jnp.bfloat16), within.astype(jnp.bfloat16), preferred_element_type=jnp.float32)
    rank = (slot - before).astype(jnp.float32)
    at = jnp.sum((row <= rank[:, None]).astype(jnp.int32), axis=1)
    return block * 128 + at, slot < upto[count - 1]


BY_ROWS = (1, 3, 6, 8)


def position_table():
    cols = []
    for width in (DE, DD):
        side = width // 16 * 6
        parts = (width - 2 * side, side, side)
        tab = np.zeros((48, width), np.float64)
        col = 0
        for i, n in enumerate(parts):
            half = n // 2
            freq = 1.0 / 10000.0 ** (np.arange(half) / half)
            ang = np.arange(16)[:, None] * freq[None, :]
            tab[16 * i:16 * i + 16, col:col + n] = np.concatenate([np.sin(ang), np.cos(ang)], axis=1)
            col += n
        cols.append(tab)
    left = np.concatenate(cols, axis=1).astype(np.float32)
    terms = []
    for _ in range(3):
        terms.append(left.astype(ml_dtypes.bfloat16))
        left = left - terms[-1].astype(np.float32)
    return np.stack(terms)


def dot(a, b):
    return jnp.dot(a, b, preferred_element_type=jnp.float32)


def dot_nt(a, b):
    return lax.dot_general(a, b, (((1,), (1,)), ((), ())), preferred_element_type=jnp.float32)


def dot_tn(a, b):
    return lax.dot_general(a, b, (((0,), (0,)), ((), ())), preferred_element_type=jnp.float32)


def lanes(i, n=128):
    return pl.ds(pl.multiple_of(i * n, n), n)


def ln_parts(x):
    c = x - jnp.mean(x, axis=-1, keepdims=True)
    inv = lax.rsqrt(jnp.mean(c * c, axis=-1, keepdims=True) + NORM_EPS)
    return c * inv, inv


def ln_back(up, m, inv, gain):
    s = up * gain
    a = jnp.mean(s, axis=-1, keepdims=True)
    b = jnp.mean(s * m, axis=-1, keepdims=True)
    return inv * (s - a - m * b), jnp.sum(up * m, axis=0, keepdims=True), jnp.sum(up, axis=0, keepdims=True)


class Block:
    def __init__(self, width, heads, size, hidden, first, table, col):
        self.width, self.heads, self.size, self.hidden, self.col = width, heads, size, hidden, col
        self.q, self.o, self.a, self.b = table[first:first + 4]
        self.part = heads // 2 * size
        self.per = 128 // size


def panel(w, t, mat, g, lo=0, num=16):
    rb, _, _, _, at, _, _ = mat
    if rb % 16:
        v = w[t, lo:lo + num, at + g // 2 * 2 * rb:at + (g // 2 + 1) * 2 * rb, :].astype(jnp.float32)
        return v[:, g % 2 * rb:(g % 2 + 1) * rb].reshape(num * rb, 128).astype(jnp.bfloat16)
    rows = pl.ds(pl.multiple_of(at + g * rb, 16), rb)
    v = w[t, lo:lo + num, rows, :] if isinstance(lo, int) else w[t, pl.ds(lo, num), rows, :]
    return v.reshape(num * rb, 128)


def pair(w, mat, g):
    return jnp.concatenate([panel(w, 0, mat, g), panel(w, 1, mat, g)], axis=1)


def repeat(count, step, f):
    step = max(k for k in range(1, step + 1) if count % k == 0)

    def turn(i, _):
        for k in range(step):
            f(i * step + k)
        return 0

    if step == count:
        turn(0, 0)
    else:
        lax.fori_loop(0, count // step, turn, 0)


def pull(acc, up, w, mat, step):
    count = mat[1]
    step = max(k for k in range(1, step + 1) if count % k == 0)

    def part(i):
        gs = [i * step + k for k in range(step)]
        d = jnp.concatenate([up[:, lanes(o + g)] for g in gs for o in (0, count)], axis=1)
        return dot_nt(d, jnp.concatenate([pair(w, mat, g) for g in gs], axis=1))

    acc[...] = part(0)

    def turn(i, _):
        acc[...] += part(i)
        return 0

    lax.fori_loop(1, count // step, turn, 0)


def block_fwd(b, x, xo, w, gains, biases, same, n1, proj, p, att, ow, m1, i1, n2, m2, i2, act, slope,
              need, keep):
    cols = slice(b.col, b.col + b.width)
    m, inv = ln_parts(x[...])
    m1[...] = m
    i1[...] = jnp.broadcast_to(inv, i1.shape)
    n1[...] = (m * gains[0:1, cols] + biases[0:1, cols]).astype(jnp.bfloat16)
    keep(0)
    yield
    need(0)
    gq = b.q[1]

    def qkv(g):
        r = dot(n1[...], pair(w, b.q, g)).astype(jnp.bfloat16)
        proj[:, lanes(g)] = r[:, :128]
        proj[:, lanes(gq + g)] = r[:, 128:]

    repeat(gq, 9, qkv)
    yield
    np_ = b.part // 128
    lane = lax.broadcasted_iota(jnp.int32, (256, 128), 1)
    masks = [lane // b.size == i for i in range(b.per)]

    def heads(i):
        t, j = i // np_, i % np_
        q = proj[:, lanes(t * gq + j)]
        k = proj[:, lanes(t * gq + np_ + j)]
        v = proj[:, lanes(t * gq + 2 * np_ + j)]
        total = jnp.zeros((256, 128), jnp.float32)
        for h in range(b.per):
            z = dot_nt(jnp.where(masks[h], q, 0), k) * b.size ** (-0.5) + same
            e = jnp.exp(z - jnp.max(z, axis=-1, keepdims=True))
            s = e * (1.0 / jnp.sum(e, axis=-1, keepdims=True))
            p[i * b.per + h] = s
            total = total + dot(s.astype(jnp.bfloat16), jnp.where(masks[h], v, 0))
        att[:, lanes(i)] = total.astype(jnp.bfloat16)

    repeat(np_, 3, heads)
    yield
    repeat(np_, 3, lambda i: heads(np_ + i))
    keep(1)
    yield
    need(1)
    for t in range(2):
        for g in range(b.width // 128):
            ow[t, :, g * 128:(g + 1) * 128] = panel(w, t, b.o, g)
    x1 = x[...] + dot(att[:, :b.part], ow[0]) + dot(att[:, b.part:], ow[1])
    xo[...] = x1
    m, inv = ln_parts(x1)
    m2[...] = m
    i2[...] = jnp.broadcast_to(inv, i2.shape)
    n2[...] = (m * gains[1:2, cols] + biases[1:2, cols]).astype(jnp.bfloat16)
    keep(2)
    yield
    need(2)
    ga = b.a[1]

    def up(g):
        h = dot(n2[...], pair(w, b.a, g))
        big = 0.5 * (1.0 + lax.erf(h * 0.7071067811865476))
        act_v = (h * big).astype(jnp.bfloat16)
        dens = big + h * (0.3989422804014327 * jnp.exp(-0.5 * h * h))
        act[:, lanes(g)] = act_v[:, :128]
        act[:, lanes(ga + g)] = act_v[:, 128:]
        slope[:, lanes(g)] = dens[:, :128]
        slope[:, lanes(ga + g)] = dens[:, 128:]

    repeat(ga, 12, up)
    keep(3)
    yield
    need(3)
    half = b.hidden // 2

    def down(g):
        w0 = jnp.concatenate([panel(w, 0, b.b, 2 * g), panel(w, 0, b.b, 2 * g + 1)], axis=1)
        w1 = jnp.concatenate([panel(w, 1, b.b, 2 * g), panel(w, 1, b.b, 2 * g + 1)], axis=1)
        xo[:, lanes(g, 256)] += dot(act[:, :half], w0) + dot(act[:, half:], w1)

    repeat(b.width // 256, 1, down)


def block_bwd(b, dr, w, gains, same, n1, proj, p, att, ow, m1, i1, n2, m2, i2, act, slope,
              r, dh, r1, dp_out, acc, da, norm_out, keep):
    cols = slice(b.col, b.col + b.width)
    r[...] = dr[...].astype(jnp.bfloat16)
    keep(3)
    half = b.hidden // 2
    rb = b.b[0]
    gb = b.width // 128
    num = 16

    def hidden(i, _):
        t, lo = i // (16 // num), (i % (16 // num)) * num
        wc = jnp.concatenate([panel(w, t, b.b, g, lo, num) for g in range(gb)], axis=1)
        at = lanes(i, num * rb)
        dh[:, at] = (dot_nt(r[...], wc) * slope[:, at]).astype(jnp.bfloat16)
        return 0

    lax.fori_loop(0, 2 * (16 // num), hidden, 0)
    keep(2)
    ga = b.a[1]
    pull(acc, dh, w, b.a, 12)
    dx, dg, db = ln_back(acc[...], m2[...], i2[:, :1], gains[1:2, cols])
    norm_out[1:2, cols] = dg
    norm_out[3:4, cols] = db
    dx1 = dr[...] + dx
    dr[...] = dx1
    r1[...] = dx1.astype(jnp.bfloat16)
    keep(1)
    for t in range(2):
        da[:, t * b.part:(t + 1) * b.part] = dot_nt(r1[...], ow[t]).astype(jnp.bfloat16)
    gq = b.q[1]
    np_ = b.part // 128
    lane = lax.broadcasted_iota(jnp.int32, (256, 128), 1)
    masks = [lane // b.size == i for i in range(b.per)]
    scale = b.size ** (-0.5)

    def heads(i):
        t, j = i // np_, i % np_
        q = proj[:, lanes(t * gq + j)]
        k = proj[:, lanes(t * gq + np_ + j)]
        v = proj[:, lanes(t * gq + 2 * np_ + j)]
        up_ = da[:, lanes(i)]
        dq = jnp.zeros((256, 128), jnp.float32)
        dk = jnp.zeros((256, 128), jnp.float32)
        dv = jnp.zeros((256, 128), jnp.float32)
        for h in range(b.per):
            s = p[i * b.per + h]
            u = jnp.where(masks[h], up_, 0)
            dp = dot_nt(u, v)
            dv = dv + dot_tn(s.astype(jnp.bfloat16), u)
            t1 = s * dp
            dz = (t1 - s * jnp.sum(t1, axis=-1, keepdims=True)).astype(jnp.bfloat16)
            dq = dq + dot(dz, jnp.where(masks[h], k, 0))
            dk = dk + dot_tn(dz, jnp.where(masks[h], q, 0))
        dp_out[:, lanes(t * gq + j)] = (dq * scale).astype(jnp.bfloat16)
        dp_out[:, lanes(t * gq + np_ + j)] = (dk * scale).astype(jnp.bfloat16)
        dp_out[:, lanes(t * gq + 2 * np_ + j)] = dv.astype(jnp.bfloat16)

    repeat(2 * np_, 2, heads)
    keep(0)
    pull(acc, dp_out, w, b.q, 9)
    dx, dg, db = ln_back(acc[...], m1[...], i1[:, :1], gains[0:1, cols])
    norm_out[0:1, cols] = dg
    norm_out[2:3, cols] = db
    dr[...] = dr[...] + dx


ACTS = (DE, DE, DE, FFE, DE, DD, DD, DD, FFD)
GRADS = (3 * DE, DE, FFE, DE, DD, 3 * DD, DD, FFD, DD)


def lookup(pos, tab, cols):
    row = lax.broadcasted_iota(jnp.int32, (48, 256), 0)
    spots = [jnp.concatenate([pos[0, i:i + 1, :], pos[1, i:i + 1, :]], axis=1) for i in range(3)]
    hot = jnp.logical_or(jnp.logical_or(row == spots[0], row == spots[1] + 16), row == spots[2] + 32)
    hot = jnp.where(hot, 1.0, 0.0).astype(jnp.bfloat16)
    return sum(dot_tn(hot, tab[i, :, cols]) for i in range(3))


def tile_mask(tile):
    ids = tile[lax.axis_index("tensor")]
    tiles = jnp.where(lax.broadcasted_iota(jnp.int32, (16, 256), 0) == ids, 1.0, 0.0).astype(jnp.bfloat16)
    return (1.0 - dot_tn(tiles, tiles)) * MASK_FILL


FWD_ACTS = [((256, n), jnp.bfloat16) for n in (DE, DE, DE, FFE)]
FWD_KEPT = [((256, 3 * DE), jnp.bfloat16), ((HE, 256, 256), jnp.float32), ((2, DE // 2, DE), jnp.bfloat16),
            ((256, DE), jnp.float32), ((256, 128), jnp.float32), ((256, DE), jnp.float32), ((256, 128), jnp.float32),
            ((256, FFE), jnp.float32)]


def chain_kernel(table, pos, tile, gains, biases, cot, tab, x2, w_hbm, *refs):
    fwd_hbm, refs = refs[:8], refs[8:]
    dec, dx0, norm_out = refs[:3]
    kept_out = refs[3:17]
    kept = refs[17:31]
    low, n1d, ad, n2d, ud, dpe, r1e, dhe, re, dlow, dpd, r1d, dhd, rd = kept
    fwd, refs = refs[31:39], refs[39:]
    proj_e, pe, ow_e, m1e, i1e, m2e, i2e, se = fwd
    (w, pd, sd, proj_d, da_e, da_d, ow_d, m1d, m2d, i1d, i2d, y, acc_e, acc_d, w_sem, f_sem, out_sem) = refs
    enc_b = Block(DE, HE, HDE, FFE, 0, table, 0)
    dec_b = Block(DD, HD, HDD, FFD, 5, table, DE)
    em = table[4]

    def load(m):
        rows = pl.ds(table[m][4], table[m][1] * table[m][5])
        return pltpu.make_async_copy(w_hbm.at[:, :, rows], w.at[:, :, rows], w_sem.at[m])

    def fetch(i):
        return pltpu.make_async_copy(fwd_hbm[i], fwd[i], f_sem.at[i])

    def store(i):
        return pltpu.make_async_copy(kept[i], kept_out[i], out_sem.at[i])

    for m in (4, 5, 6, 7, 8, 3, 2, 1, 0):
        if m != 1:
            load(m).start()
    for i in range(8):
        fetch(i).start()
    same = tile_mask(tile)
    low[...] = x2[...].astype(jnp.bfloat16)
    store(0).start()
    load(4).wait()
    for g in range(2):
        v = dot(low[...], pair(w, em, g)).astype(jnp.bfloat16).astype(jnp.float32)
        y[:, g * 128:(g + 1) * 128] = v[:, :128]
        y[:, 256 + g * 128:256 + (g + 1) * 128] = v[:, 128:]
    y[...] += lookup(pos, tab, slice(DE, DE + DD))
    for _ in block_fwd(dec_b, y, dec, w, gains, biases, same, n1d, proj_d, pd, ad, ow_d, m1d, i1d, n2d, m2d, i2d, ud, sd,
                       lambda k: load(5 + k).wait(), lambda k: store(1 + k).start()):
        pass
    y[...] = cot[...]
    block_bwd(dec_b, y, w, gains, same, n1d, proj_d, pd, ad, ow_d, m1d, i1d, n2d, m2d, i2d, ud, sd,
              rd, dhd, r1d, dpd, acc_d, da_d, norm_out, lambda k: store(10 + k).start())
    dlow[...] = y[...].astype(jnp.bfloat16)
    store(9).start()
    for g in range(2):
        d = jnp.concatenate([dlow[:, g * 128:(g + 1) * 128], dlow[:, 256 + g * 128:256 + (g + 1) * 128]], axis=1)
        v = dot_nt(d, pair(w, em, g))
        if g == 0:
            dx0[...] = v
        else:
            dx0[...] += v
    for m in (3, 2, 0):
        load(m).wait()
    for i in range(8):
        fetch(i).wait()
    block_bwd(enc_b, dx0, w, gains, same, None, proj_e, pe, None, ow_e, m1e, i1e, None, m2e, i2e, None, se,
              re, dhe, r1e, dpe, acc_e, da_e, norm_out, lambda k: store(5 + k).start())
    for i in range(14):
        store(i).wait()


def chain(pos, tile, gains, biases, cot, full, x2, fwd, table):
    f32, bf16 = jnp.float32, jnp.bfloat16
    S = jax.ShapeDtypeStruct
    outs = [S((256, DD), f32), S((256, DE), f32), S((4, DE + DD), f32)]
    kept = [(256, n) for n in ACTS[4:] + GRADS]
    outs += [S(k, bf16) for k in kept]
    V = pltpu.VMEM
    scratch = [V(k, bf16) for k in kept] + [V(k, t) for k, t in FWD_KEPT] + [
        V((2, 16) + full.shape[-2:], bf16), V((HD, 256, 256), f32), V((256, FFD), f32),
        V((256, 3 * DD), bf16), V((256, DE), bf16), V((256, DD), bf16), V((2, DD // 2, DD), bf16),
        V((256, DD), f32), V((256, DD), f32), V((256, 128), f32), V((256, 128), f32),
        V((256, DD), f32), V((256, DE), f32), V((256, DD), f32),
        pltpu.SemaphoreType.DMA((9,)), pltpu.SemaphoreType.DMA((8,)), pltpu.SemaphoreType.DMA((14,))]
    vmem = pl.BlockSpec(memory_space=pltpu.VMEM)
    hbm = pl.BlockSpec(memory_space=pl.ANY)
    args = (pos, tile, gains, biases, cot, jnp.asarray(position_table()), x2,
            full.reshape(2, 16, full.shape[-2], 128), *fwd)
    return pl.pallas_call(
        partial(chain_kernel, table), out_shape=outs, in_specs=[vmem] * 7 + [hbm] * 9, out_specs=[vmem] * 3 + [hbm] * 14,
        scratch_shapes=scratch, compiler_params=pltpu.CompilerParams(vmem_limit_bytes=63 << 20), name="chain",
        cost_estimate=pl.CostEstimate(flops=8_000_000_000, bytes_accessed=40_000_000, transcendentals=3_000_000),
    )(*args)


def grad_panels(table, m, act, grad, turned, put):
    mat = table[m]
    rb, panels, padded = mat[0], mat[1], mat[5]
    count = act.shape[1]

    def turn(i):
        turned[pl.ds(pl.multiple_of(i * 128, 128), 128), :] = act[:, lanes(i)].T

    repeat(count // 128, 6, turn)

    def place(t, g, v):
        put(t, g, v.astype(jnp.bfloat16).reshape(16, rb, 128))

    if m in BY_ROWS:
        half = count // 2

        def body(i):
            t, g = i // (panels // 2), i % (panels // 2)
            v = dot(turned[pl.ds(pl.multiple_of(t * half, 128), half), :], grad[:, lanes(g, 256)])
            if rb % 16:
                v = jnp.concatenate([v[:, :128].reshape(16, rb, 128), v[:, 128:].reshape(16, rb, 128)], axis=1)
                put(t, 2 * g, v.astype(jnp.bfloat16))
                return
            place(t, 2 * g, v[:, :128])
            place(t, 2 * g + 1, v[:, 128:])

        repeat(panels, 6, body)
    else:
        def body(g):
            d = jnp.concatenate([grad[:, lanes(g)], grad[:, lanes(panels + g)]], axis=1)
            v = dot(turned[:count, :], d)
            place(0, g, v[:, :128])
            place(1, g, v[:, 128:])

        repeat(panels, 6, body)


class Wires:
    def __init__(self, place, sem):
        self.place, self.sem, self.used, self.waits = place, sem, 0, []

    def new(self, n=1):
        self.used += n
        assert self.used <= self.sem.shape[0], self.used
        return self.used - n

    def copy(self, k, src, dst, way):
        return pltpu.make_async_remote_copy(src_ref=src, dst_ref=dst, send_sem=self.sem.at[k], recv_sem=self.sem.at[k + 1],
                                            device_id=self.place.ids[way], device_id_type=MESH)

    def send(self, k, src, dst, way, cond=None):
        cp = self.copy(k, src, dst, way)
        when(cond, cp.start)
        self.waits.append((cond, cp))

    def land(self, k, dst, cond=None):
        when(cond, self.copy(k, dst, dst, "c").wait_recv)

    def drain(self):
        for cond, cp in self.waits:
            when(cond, cp.wait_send)


def edge_slots(order):
    slots, used, shared = {}, 0, {}
    for d, kids in sorted(spread(order).items()):
        for _, way in kids:
            if way in "xy" and order.index("z") < order.index(way):
                key = (way, d[1], d[2])
                if key not in shared:
                    shared[key] = used
                    used += 4
                slots[d, way] = (shared[key], 4)
            else:
                slots[d, way] = (used, 1)
                used += 1
    return slots, used


def beyond(p, way):
    return p.z < 3 if way == "z+" else p.z > 0 if way == "z-" else None


def reduce_events(p, w, order, own, half, bufs, ready, done):
    tree = spread(order)
    pair = {d: w.new(2) for d in tree}
    wire = {d: w.new(2) for d in tree}
    parent = {nd: (d, way) for d, t in tree.items() for nd, way in t}
    slots, _ = edge_slots(order)

    def buffer(up, way):
        first, n = slots[up, way]
        return bufs.at[first + p.z + up[0] if n > 1 else first]

    events = []
    far = sorted(tree, key=lambda d: (-hops(d), d))
    for d in far:
        def act(d=d):
            cond = p.there(d)

            def step():
                acc = own(d)
                ready(d)
                w.land(pair[d], half(d))
                add_rows(acc, half(d))
                for nd, way in tree[d]:
                    buf = buffer(d, way)

                    def take(buf=buf, nd=nd):
                        w.land(wire[nd], buf)
                        add_rows(acc, buf)
                    when(beyond(p, way), take)
            when(cond, step)
            if hops(d) == 0:
                done()
            else:
                up, way = parent[d]
                w.send(wire[d], own(d), buffer(up, way), BACK[way], cond)
        events.append(act)

    def share(give):
        for d in far:
            w.send(pair[d], give(d), half(d), "c", p.there(d))

    return events, share, far


def gather_events(p, w, order, first, at):
    tree = spread(order)
    pair = {d: w.new(2) for d in tree}
    wire = {d: w.new(2) for d in tree}
    events = []
    for d in sorted(tree, key=lambda d: (hops(d), d)):
        def act(d=d):
            cond = p.there(d)
            blk = at(d, p.c)
            if hops(d):
                w.land(wire[d], blk, cond)
                src = blk
            else:
                src = first
            for nd, way in tree[d]:
                w.send(wire[nd], src, blk, way, both(cond, beyond(p, way)))
            w.send(pair[d], src, blk, "c", cond)
        events.append(act)

    def finish():
        for d in tree:
            w.land(pair[d], at(d, 1 - p.c), p.there(d))

    return events, finish


def run_events(lists, order, extra=iter(()), every=8):
    assert sorted(order) == sorted(64 * g + i for g, acts in enumerate(lists) for i in range(len(acts)))
    for n, k in enumerate(order):
        if n % every == 0:
            next(extra, None)
        lists[k // 64][k % 64]()
    for _ in extra:
        pass


def group_span(table, mats):
    first, last = table[mats[0]], table[mats[-1]]
    units = last[3] + last[2] - first[3]
    return first[3], -(-units // 16) * 16, first[4], last[4] + last[1] * last[5] - first[4]


def units_to_panels(table, mats, units, flat, put):
    base, count = table[mats[0]][3], units.shape[0]
    for k in range(4):
        flat[pl.ds(k, count, stride=4), :] = units[:, 128 * k:128 * (k + 1)].astype(jnp.float32)
    for m in mats:
        rb, panels, n, first, _, padded, _ = table[m]
        n = 2 if rb % 16 else 1
        for g in range(0, panels, n):
            v = [flat[pl.ds(4 * (first - base) + g + k, rb, stride=panels), :] for k in range(n)]
            put(m, g, jnp.concatenate(v, axis=0).astype(jnp.bfloat16))


def panels_to_units(table, mats, take, flat, units):
    base, count = table[mats[0]][3], units.shape[0]
    used = 0
    for m in mats:
        rb, panels, n, first, _, padded, _ = table[m]
        many = 2 if rb % 16 else 1
        for g in range(0, panels, many):
            v = take(m, g, many)
            for k in range(many):
                flat[pl.ds(4 * (first - base) + g + k, rb, stride=panels), :] = v[k * rb:(k + 1) * rb]
        used = 4 * (first - base + n)
    if used < 4 * count:
        flat[used:4 * count, :] = jnp.zeros((4 * count - used, 128), jnp.float32)
    for k in range(4):
        units[:, 128 * k:128 * (k + 1)] = flat[pl.ds(k, count, stride=4), :].astype(jnp.bfloat16)


def encoder_steps(p, table, out, tok, pos, x, x2, tile, gains, biases, tab, fwd, fwd_out, wv, w_sem, fwd_sem, swapped, arrived):
    n1, att, n2, act, proj, prob, ow, m1, i1, m2, i2, slope = fwd

    def load(m):
        rows = pl.ds(table[m][4], table[m][1] * table[m][5])
        return pltpu.make_async_copy(out.at[:, :, :, :, rows], wv.at[:, :, :, :, rows], w_sem.at[m])

    def store(i):
        return pltpu.make_async_copy(fwd[i], fwd_out[i], fwd_sem.at[i])

    def keep(k):
        for i in ((0, 7, 8), (1, 4, 5), (2, 6, 9, 10), (3, 11))[k]:
            store(i).start()

    for f in swapped:
        f()
    x[...] = tok[...].reshape(256, DE).astype(jnp.float32) + lookup(pos, tab, slice(0, DE))
    same = tile_mask(tile)
    whole = wv.reshape(2, 16, wv.shape[-2], 128)
    block = block_fwd(Block(DE, HE, HDE, FFE, 0, table, 0), x, x2, whole, gains, biases, same, n1, proj, prob, att, ow, m1, i1, n2,
                      m2, i2, act, slope, lambda k: load(k).wait(), keep)
    next(block)
    yield
    for f in arrived[0]:
        f()
    load(0).start()
    load(1).start()
    yield
    for _ in range(4):
        next(block)
        yield
    for f in arrived[1]:
        f()
    load(2).start()
    yield
    next(block)
    yield
    for f in arrived[2]:
        f()
    load(3).start()
    yield
    for _ in block:
        pass
    yield
    for i in range(12):
        store(i).wait()


class Swap:
    def __init__(self, p, w, src, out, give, keep):
        self.p, self.w, self.src, self.out, self.give, self.keep = p, w, src, out, give, keep
        self.k, self.own = w.new(2), w.new()

    def local(self):
        return pltpu.make_async_copy(self.src.at[self.keep], self.out.at[self.p.x], self.w.sem.at[self.own])

    def start(self):
        self.w.send(self.k, self.src.at[self.give], self.out.at[self.p.x], "x")

    def finish(self):
        self.w.land(self.k, self.out.at[1 - self.p.x])
        self.local().wait()


def weights_kernel(table, groups, plan, parts, tok_in, pos_in, cot_in, tile, gains, biases, tab, *refs):
    n = len(groups)
    out, pos, cot, x2 = refs[:4]
    fwd_out, tok, x, fwd, wv, w_sem, fwd_sem = refs[4:16], refs[16], refs[17], refs[18:30], refs[30], refs[31], refs[32]
    rest = refs[33:]
    accs, halves, bufs, shards = (rest[i * n:(i + 1) * n] for i in range(4))
    flat, sem = rest[4 * n:]
    p = Place()
    p.greet(["c", "y", "x"])
    w = Wires(p, sem)
    swaps = [Swap(p, w, a, b, 1 - p.x, p.x) for a, b in ((tok_in, tok), (pos_in, pos), (cot_in, cot))]
    for s in swaps:
        s.start()
        s.local().start()
    lists, finishes = [], []
    for g, mats in enumerate(groups):
        u0, un, r0, rn = group_span(table, mats)
        acc, half, buf, shard = accs[g], halves[g], bufs[g], shards[g]
        own_sem = w.new()
        loads = {d: w.new() for d in spread(plan[0][g])}

        def own(d, acc=acc):
            return acc.at[p.at(d)[1:]]

        def other(d, half=half):
            return half.at[p.at(d)[1:]]

        def load(d, u0=u0, un=un, own=own, loads=loads):
            return pltpu.make_async_copy(parts.at[p.at(d)[1:] + (p.c, pl.ds(u0, un))], own(d), sem.at[loads[d]])

        def ready(d, load=load):
            load(d).wait()

        def done(mats=mats, acc=acc, shard=shard, r0=r0):
            def put(m, i, v):
                lo = table[m][4] - r0 + i * table[m][5]
                shard[lo:lo + v.shape[0], :] = v
            units_to_panels(table, mats, acc.at[p.z, p.y], flat, put)

        ev, share, far = reduce_events(p, w, plan[0][g], own, other, buf, ready, done)

        def begin(load=load, share=share, far=far, u0=u0, un=un):
            share(lambda d: parts.at[p.at(d)[1:] + (1 - p.c, pl.ds(u0, un))])
            for d in far:
                when(p.there(d), load(d).start)

        def at(d, core, r0=r0, rn=rn):
            t, z, y = p.at(d)
            return out.at[t, z, y, core, pl.ds(r0, rn)]

        def local(shard=shard, r0=r0, rn=rn, own_sem=own_sem):
            return pltpu.make_async_copy(shard, out.at[p.x, p.z, p.y, p.c, pl.ds(r0, rn)], sem.at[own_sem])

        ag, finish = gather_events(p, w, plan[1][g], shard, at)

        def send_first(act=ag[0], local=local):
            act()
            local().start()

        lists.append([begin] + ev + [send_first] + ag[1:])
        finishes += [finish, lambda local=local: local().wait()]
    steps = encoder_steps(p, table, out, tok, pos, x, x2, tile, gains, biases, tab, fwd, fwd_out, wv, w_sem, fwd_sem,
                          [s.finish for s in swaps[:2]], [finishes[2 * k:2 * k + 2] for k in range(3)])
    lists.append([partial(next, steps, None)] * 11)
    run_events(lists, plan[2])
    for f in finishes[6:] + [swaps[2].finish]:
        f()
    w.drain()


def spread_weights(parts, tokens, pos, cot, tile, gains, biases, table, rows, groups, plan, ident):
    spans = [group_span(table, m) for m in groups]
    bf16 = jnp.bfloat16
    S = jax.ShapeDtypeStruct
    V = pltpu.VMEM
    fwd = FWD_ACTS + FWD_KEPT
    enc_rows = table[4][4]
    scratch = [V(tokens.shape, tokens.dtype), V((256, DE), jnp.float32)] + [V(k, t) for k, t in fwd]
    scratch += [V((2, 4, 2, 2, enc_rows, 128), bf16), pltpu.SemaphoreType.DMA((4,)), pltpu.SemaphoreType.DMA((12,))]
    scratch += [V((4, 2, s[1], 512), bf16) for s in spans] * 2
    scratch += [V((edge_slots(o)[1], s[1], 512), bf16) for s, o in zip(spans, plan[0])]
    scratch += [V((s[3], 128), bf16) for s in spans]
    scratch += [V((4 * max(s[1] for s in spans), 128), jnp.float32),
                pltpu.SemaphoreType.DMA((len(groups) * (1 + 5 * 14 + 4 * 28) + 9,))]
    hbm = pl.BlockSpec(memory_space=pl.ANY)
    vmem = pl.BlockSpec(memory_space=pltpu.VMEM)
    return pl.pallas_call(
        partial(weights_kernel, table, groups, plan),
        out_shape=[S((2, 4, 2, 2, rows, 128), bf16), S(pos.shape, pos.dtype), S(cot.shape, cot.dtype), S((256, DE), jnp.float32)]
        + [S(k, t) for k, t in fwd],
        in_specs=[hbm] * 4 + [vmem] * 4, out_specs=[hbm, vmem, hbm, vmem] + [hbm] * 12,
        scratch_shapes=scratch,
        compiler_params=pltpu.CompilerParams(collective_id=ident, has_side_effects=True, vmem_limit_bytes=63 << 20),
        name="spread_weights",
    )(parts, tokens, pos, cot, tile, gains, biases, jnp.asarray(position_table()))


def return_kernel(table, groups, plan, *refs):
    n = len(groups)
    kept_in, small_src, dec_in, dx_in, out, small_out, dec, dx = refs[:18], *refs[18:25]
    rest = refs[25:]
    kept, rest = rest[:18], rest[18:]
    acts, grads = kept[:9], kept[9:]
    sides, halves, bufs, units = (rest[i * n:(i + 1) * n] for i in range(4))
    flat, turned, mid, line, load_sem, sem = rest[4 * n:]

    def load(i):
        return pltpu.make_async_copy(kept_in[i], kept[i], load_sem.at[i])

    first = sorted(range(n), key=lambda g: plan[2].index(64 * g))
    for g in first:
        for m in groups[g]:
            load(m).start()
            load(9 + m).start()
    p = Place()
    p.greet(["c", "y", "x"])
    w = Wires(p, sem)
    swaps = [Swap(p, w, a, b, 1 - p.x, p.x) for a, b in ((dec_in, dec), (dx_in, dx))]
    for s in swaps:
        s.local().start()
    swaps[0].start()
    lists, finishes = [], []
    for g, mats in enumerate(groups):
        u0, un, r0, rn = group_span(table, mats)
        side, half, buf, unit = sides[g], halves[g], bufs[g], units[g]
        own_sem = w.new()

        def own(d, side=side):
            return side.at[(p.c,) + p.at(d)]

        def other(d, half=half):
            return half.at[p.at(d)]

        def done(mats=mats, side=side, unit=unit, r0=r0):
            mine = side.at[p.c, p.x, p.z, p.y]

            def take(m, i, many):
                lo = table[m][4] - r0 + i * table[m][5]
                return mine[lo:lo + many * table[m][5], :].astype(jnp.float32)
            panels_to_units(table, mats, take, flat, unit)

        ev, share, far = reduce_events(p, w, plan[0][g], own, other, buf, lambda d: None, done)

        def begin(mats=mats, side=side, share=share, r0=r0):
            for m in mats:
                lo, padded = table[m][4] - r0, table[m][5]

                def put(t, i, v, lo=lo, padded=padded):
                    v = v.reshape(4, 2, 2, v.shape[1], 128)
                    rows = pl.ds(pl.multiple_of(lo + i * padded, 16), v.shape[3])
                    side[0, t, :, :, rows, :] = v[:, :, 0]
                    side[1, t, :, :, rows, :] = v[:, :, 1]
                load(m).wait()
                load(9 + m).wait()
                grad_panels(table, m, acts[m], grads[m], turned, put)
            share(lambda d: side.at[(1 - p.c,) + p.at(d)])

        def at(d, core, u0=u0, un=un):
            _, z, y = p.at(d)
            return out.at[z, y, core, pl.ds(u0, un)]

        def local(unit=unit, u0=u0, un=un, own_sem=own_sem):
            return pltpu.make_async_copy(unit, out.at[p.z, p.y, p.c, pl.ds(u0, un)], sem.at[own_sem])

        ag, finish = gather_events(p, w, plan[1][g], unit, at)

        def send_first(act=ag[0], local=local):
            act()
            local().start()

        lists.append([begin] + ev + [send_first] + ag[1:])
        finishes += [finish, lambda local=local: local().wait()]
    last = max(plan[2].index(64 * g + len(spread(plan[0][g]))) for g in range(n))
    g, i = plan[2][last] // 64, plan[2][last] % 64
    act = lists[g][i]

    def with_swaps():
        act()
        swaps[1].start()

    lists[g][i] = with_swaps
    run_events(lists, plan[2], total_steps(p, w, small_src, small_out, mid, line))
    for f in finishes + [s.finish for s in swaps]:
        f()
    w.drain()


def total_steps(p, w, src, out, mid, line):
    k = [w.new(2) for _ in range(9)]
    now = src
    for i, way in enumerate(("c", "x", "y")):
        w.send(k[i], now, mid.at[i], way)
        yield
        w.land(k[i], mid.at[i])
        nxt = mid.at[3 + i] if i < 2 else line.at[p.z]
        nxt[...] = now[...] + mid[i]
        now = nxt
    for i in range(4):
        lo, hi = jnp.maximum(p.z - i, 0), jnp.minimum(p.z + i, 3)
        if i > 0:
            w.land(k[2 + i], line.at[lo], p.z >= i)
            w.land(k[5 + i], line.at[hi], p.z + i <= 3)
        if i < 3:
            w.send(k[3 + i], line.at[lo], line.at[lo], "z+", jnp.logical_and(p.z >= i, p.z < 3))
            w.send(k[6 + i], line.at[hi], line.at[hi], "z-", jnp.logical_and(p.z + i <= 3, p.z > 0))
            yield
    out[...] = (line[0] + line[1]) + (line[2] + line[3])


def return_grads(kept, small, dec, dx, table, total_units, groups, plan, ident):
    spans = [group_span(table, m) for m in groups]
    bf16 = jnp.bfloat16
    S = jax.ShapeDtypeStruct
    V = pltpu.VMEM
    scratch = [V(v.shape, v.dtype) for v in kept]
    scratch += [V((2, 2, 4, 2, s[3], 128), bf16) for s in spans]
    scratch += [V((2, 4, 2, s[3], 128), bf16) for s in spans]
    scratch += [V((edge_slots(o)[1], s[3], 128), bf16) for s, o in zip(spans, plan[0])]
    scratch += [V((s[1], 512), bf16) for s in spans]
    scratch += [V((4 * max(s[1] for s in spans), 128), jnp.float32), V((FFE, 256), bf16),
                V((5,) + small.shape, small.dtype), V((4,) + small.shape, small.dtype), pltpu.SemaphoreType.DMA((18,)),
                pltpu.SemaphoreType.DMA((len(groups) * (1 + 4 * 14 + 4 * 28) + 24,))]
    vmem = pl.BlockSpec(memory_space=pltpu.VMEM)
    hbm = pl.BlockSpec(memory_space=pl.ANY)
    return pl.pallas_call(
        partial(return_kernel, table, groups, plan),
        out_shape=(S((4, 2, 2, total_units, 512), bf16), S(small.shape, small.dtype), S(dec.shape, dec.dtype), S(dx.shape, dx.dtype)),
        in_specs=[hbm] * 18 + [vmem, hbm, hbm], out_specs=(hbm, vmem, hbm, hbm),
        scratch_shapes=scratch,
        compiler_params=pltpu.CompilerParams(collective_id=ident, has_side_effects=True, vmem_limit_bytes=63 << 20),
        name="return_grads",
    )(*kept, small, dec, dx)


STEP_ROWS = 432


def update_kernel(place, spread, master, first, second, total, gains, biases, norm_first, norm_second, *refs):
    passed, refs = refs[:2], refs[2:]
    new_master, new_first, new_second, new_norms, new_nf, new_ns = refs[:6]
    i = pl.program_id(0)

    @pl.when(i == 0)
    def _():
        for a, b in zip(passed, refs[6:8]):
            b[...] = a[...]
        for v, r in ((gains, slice(0, 2)), (biases, slice(2, 4))):
            new_norms[r, :], new_nf[r, :], new_ns[r, :] = adamw(v[...], total[r, :], norm_first[r, :], norm_second[r, :], 0.0, NORM_RATE)

    lane = lax.broadcasted_iota(jnp.int32, (16, 128), 1)
    row = lax.broadcasted_iota(jnp.int32, (16, 128), 0)
    for k in range(STEP_ROWS // 16):
        tiles, spot = [], jnp.full((16, 128), -1, jnp.int32)
        for j in range(16):
            at = place[i * STEP_ROWS + 16 * k + j]
            tile = jnp.minimum(at >> 4, spread.shape[0] // 16 - 1)
            tiles.append(spread[pl.ds(pl.multiple_of(tile * 16, 16), 16), :])
            spot = jnp.where(row == j, jnp.where(at < spread.shape[0], 16 * j + (at & 15), -1), spot)
        here = slice(16 * k, 16 * k + 16)
        pick = jnp.concatenate([jnp.where(lane == spot, 1.0, 0.0), jnp.where(lane + 128 == spot, 1.0, 0.0)], axis=1)
        grad = dot(pick.astype(jnp.bfloat16), jnp.concatenate(tiles, axis=0))
        new_master[here, :], new_first[here, :], new_second[here, :] = adamw(
            master[here, :], grad, first[here, :], second[here, :], WEIGHT_DECAY, LEARN_RATE)


def update(place, spread, master, first, second, total, gains, biases, norm_first, norm_second, passed):
    slots = master.shape[0]
    S = jax.ShapeDtypeStruct
    rows = pl.BlockSpec((STEP_ROWS, 512), lambda i, s: (i, 0))
    whole = lambda v: pl.BlockSpec(v.shape, lambda i, s: (0, 0), pipeline_mode=pl.Buffered(1))
    small = pl.BlockSpec(total.shape, lambda i, s: (0, 0))
    pair_of = pl.BlockSpec(gains.shape, lambda i, s: (0, 0))
    out = [S(master.shape, jnp.float32)] * 3 + [S(total.shape, jnp.float32)] * 3 + [S(v.shape, v.dtype) for v in passed]
    both = [pl.BlockSpec(v.shape, lambda i, s: (0, 0, 0), pipeline_mode=pl.Buffered(1)) for v in passed]
    return pl.pallas_call(
        update_kernel, out_shape=out,
        grid_spec=pltpu.PrefetchScalarGridSpec(
            num_scalar_prefetch=1, grid=(slots // STEP_ROWS,),
            in_specs=[whole(spread), rows, rows, rows, small, pair_of, pair_of, small, small] + both,
            out_specs=[rows] * 3 + [small] * 3 + both),
        compiler_params=pltpu.CompilerParams(vmem_limit_bytes=62 << 20), name="update",
    )(place, spread, master, first, second, total, gains, biases, norm_first, norm_second, *passed)


def place_kernel(place_s, master, out, wide, staged, sem):
    count = wide.shape[0] // 64 - 1

    def clear(i, _):
        wide[pl.ds(pl.multiple_of(i * 64, 64), 64), :] = jnp.zeros((64, 512), jnp.float32)
        return 0

    lax.fori_loop(0, count, clear, 0)

    def turn(i, _):
        for j in range(16):
            wide[pl.ds(place_s[i * 16 + j], 1), :] = master[pl.ds(i * 16 + j, 1), :]
        return 0

    lax.fori_loop(0, master.shape[0] // 16, turn, 0)
    parts = 4
    part = count // parts * 64

    def copy(k):
        rows = pl.ds(pl.multiple_of(k * part, 64), part)
        return pltpu.make_async_copy(staged.at[rows], out.at[rows], sem.at[k])

    for k in range(parts):
        def narrow(i, _):
            rows = pl.ds(pl.multiple_of(k * part + i * 64, 64), 64)
            staged[rows, :] = wide[rows, :].astype(jnp.bfloat16)
            return 0

        lax.fori_loop(0, part // 64, narrow, 0)
        copy(k).start()
    for k in range(parts):
        copy(k).wait()


def place_blocks(place, master, rows):
    return pl.pallas_call(
        place_kernel, out_shape=jax.ShapeDtypeStruct((rows, 512), jnp.bfloat16),
        grid_spec=pltpu.PrefetchScalarGridSpec(
            num_scalar_prefetch=1, grid=(1,),
            in_specs=[pl.BlockSpec(master.shape, lambda i, s: (0, 0), pipeline_mode=pl.Buffered(1))],
            out_specs=pl.BlockSpec(memory_space=pl.ANY),
            scratch_shapes=[pltpu.VMEM((rows + 64, 512), jnp.float32), pltpu.VMEM((rows, 512), jnp.bfloat16), pltpu.SemaphoreType.DMA((4,))]),
        compiler_params=pltpu.CompilerParams(vmem_limit_bytes=60 << 20), name="place_blocks",
    )(place, master)


def sequence_device(tokens_in, positions, segment_ids, owners, master, first_moment, second_moment, norm_gains,
                    norm_biases, norm_first, norm_second, cotangent):
    shapes = weight_shapes(2)
    table, _, rows = layout(shapes, 16)
    unit, used = own_units(owners, lax.axis_index("dp"), master.shape[0])
    place = jnp.where(used, unit_places(unit, table, 16), 16 * SHARD_UNITS)
    parts = place_blocks(place, master, 16 * SHARD_UNITS)
    full, pos, cot, x2, *fwd = spread_weights(parts.reshape(4, 2, 2, SHARD_UNITS, 512), tokens_in, positions.transpose(1, 0, 2),
                                              cotangent, segment_ids, norm_gains, norm_biases, table, rows, GROUPS, PLAN_OUT, 1)
    kept = chain(pos, segment_ids, norm_gains, norm_biases, cot.reshape(256, DD), full, x2, fwd[4:], table)
    decoded, dx0, norms = kept[:3]
    spread_out, norm_total, decoded, dx0 = return_grads([*fwd[:4], *kept[3:]], norms, decoded.reshape(2, 128, DD), dx0.reshape(2, 128, DE), table,
                                                        SHARD_UNITS, GROUPS, PLAN_BACK, 2)
    new_master, new_first, new_second, new_norms, norm_one_new, norm_two_new, decoded, dx0 = update(
        place, spread_out.reshape(16 * SHARD_UNITS, 512), master, first_moment, second_moment, norm_total, norm_gains, norm_biases, norm_first, norm_second,
        (decoded, dx0))
    return (decoded, dx0, new_master, new_first, new_second, new_norms, norm_one_new, norm_two_new)


def solution(mesh):
    step = sequence_device if (mesh.shape["dp"], mesh.shape["tensor"]) == (16, 2) else per_device
    return jax.shard_map(
        step,
        mesh=mesh,
        in_specs=(
            P(None, ("dp", "tensor"), None),
            P(None, None, ("dp", "tensor")),
            P(None, "dp", None),
            P(),
            P("dp", "tensor"),
            P("dp", "tensor"),
            P("dp", "tensor"),
            P(),
            P(),
            P(),
            P(),
            P(None, ("dp", "tensor"), None),
        ),
        out_specs=(
            P(None, ("dp", "tensor"), None),
            P(None, ("dp", "tensor"), None),
            P("dp", "tensor"),
            P("dp", "tensor"),
            P("dp", "tensor"),
            P(),
            P(),
            P(),
        ),
        check_vma=False,
    )
```

```python
from functools import partial

import jax
import jax.numpy as jnp
import ml_dtypes
import numpy as np
from jax import lax
from jax.experimental import pallas as pl
from jax.experimental.pallas import tpu as pltpu
from jax.sharding import PartitionSpec as P

DE = 768
HE = 12
HDE = 64
FFE = 3072
DD = 512
HD = 16
HDD = 32
FFD = 2048
STEP = 10


NORM_EPS = 1e-06
BETA_ONE = 0.5
BETA_TWO = 0.5
LEARN_RATE = 0.03
NORM_RATE = 0.3
WEIGHT_DECAY = 0.05
ADAM_EPS = 1e-08
MASK_FILL = -1000000000.0


def sincos_part(coordinate, part_width):
    halfway = part_width // 2
    frequency = 1.0 / 10000.0 ** (jnp.arange(halfway, dtype=jnp.float32) / halfway)
    angles = coordinate.astype(jnp.float32)[:, None] * frequency[None, :]
    return jnp.concatenate([jnp.sin(angles), jnp.cos(angles)], axis=1)


def sincos_embed(positions, model_width):
    side_width = model_width // 16 * 6
    first_width = model_width - 2 * side_width
    return jnp.concatenate(
        [
            sincos_part(positions[0], first_width),
            sincos_part(positions[1], side_width),
            sincos_part(positions[2], side_width),
        ],
        axis=1,
    )


def slot_table(owners, devices, capacity):
    owner_ids = owners[:, 0]
    onehot = (owner_ids[:, None] == jnp.arange(devices, dtype=jnp.int32)[None, :]).astype(jnp.int32)
    before = jnp.cumsum(onehot, axis=0) - onehot
    owner_rank = jnp.sum(before * onehot, axis=1)
    return owner_ids * capacity + owner_rank


def weight_shapes(tensor_count):
    enc_heads = HE // tensor_count
    dec_heads = HD // tensor_count
    return [
        (DE, 3 * enc_heads * HDE),
        (enc_heads * HDE, DE),
        (DE, FFE // tensor_count),
        (FFE // tensor_count, DE),
        (DE, DD // tensor_count),
        (DD, 3 * dec_heads * HDD),
        (dec_heads * HDD, DD),
        (DD, FFD // tensor_count),
        (FFD // tensor_count, DD),
    ]


def split_flat(flat_vector, shapes):
    pieces = []
    offset = 0
    for matrix_shape in shapes:
        length = matrix_shape[0] * matrix_shape[1]
        pieces.append(flat_vector[offset : offset + length].reshape(matrix_shape))
        offset += length
    return pieces


def adamw(weights, gradient, moment_one, moment_two, decay_rate, step_rate):
    one_new = BETA_ONE * moment_one + (1.0 - BETA_ONE) * gradient
    two_new = BETA_TWO * moment_two + (1.0 - BETA_TWO) * gradient * gradient
    one_hat = one_new / (1.0 - BETA_ONE**STEP)
    two_hat = two_new / (1.0 - BETA_TWO**STEP)
    weights_new = weights - step_rate * (
        one_hat / (jnp.sqrt(two_hat) + ADAM_EPS) + decay_rate * weights
    )
    return (weights_new, one_new, two_new)


def norm_forward(values, gain_row, bias_row):
    center = values - jnp.mean(values, axis=-1, keepdims=True)
    spread = jnp.mean(center * center, axis=-1, keepdims=True)
    inverse = lax.rsqrt(spread + NORM_EPS)
    normed = center * inverse
    return (normed * gain_row + bias_row, (normed, inverse))


def norm_backward(upstream, stored, gain_row):
    normed, inverse = stored
    scaled = upstream * gain_row
    mean_one = jnp.mean(scaled, axis=-1, keepdims=True)
    mean_two = jnp.mean(scaled * normed, axis=-1, keepdims=True)
    return (
        inverse * (scaled - mean_one - normed * mean_two),
        jnp.sum(upstream * normed, axis=0),
        jnp.sum(upstream, axis=0),
    )


def inner_rows(left_side, right_side):
    return lax.dot_general(
        left_side, right_side, (((0,), (0,)), ((), ())), preferred_element_type=jnp.float32
    )


def times_transpose(left_side, right_side):
    return lax.dot_general(
        left_side, right_side, (((1,), (1,)), ((), ())), preferred_element_type=jnp.float32
    )


def gather_rows(values):
    return lax.all_gather(values, "tensor", axis=0, tiled=True)


def gather_grads(values):
    return lax.all_gather(values, "tensor", axis=0, tiled=True)


def branch_rows(values, weight):
    return lax.psum_scatter(
        jnp.dot(values, weight, preferred_element_type=jnp.float32).astype(jnp.bfloat16),
        "tensor",
        scatter_dimension=0,
        tiled=True,
    ).astype(jnp.float32)


def input_rows(values, weight):
    return lax.psum_scatter(
        times_transpose(values, weight).astype(jnp.bfloat16),
        "tensor",
        scatter_dimension=0,
        tiled=True,
    ).astype(jnp.float32)


def block_scores(queries, key_rows, mask_bias, block_start, block_rows, head_size):
    scores = jnp.einsum(
        "qhd,khd->hqk", queries, key_rows, preferred_element_type=jnp.float32
    ) * head_size ** (-0.5)
    return scores + mask_bias[None, block_start : block_start + block_rows]


def attention_forward(gathered, w_qkv, head_count, head_size, mask_bias):
    length = gathered.shape[0]
    projected = jnp.dot(gathered, w_qkv, preferred_element_type=jnp.float32).astype(jnp.bfloat16)
    projected = projected.reshape(length, 3, head_count, head_size)
    queries = projected[:, 0]
    key_rows = projected[:, 1]
    value_rows = projected[:, 2]
    block_rows = min(512, length)
    scores = block_scores(queries, key_rows, mask_bias, 0, block_rows, head_size)
    row_peak = jnp.max(scores, axis=-1, keepdims=True)
    row_total = row_peak + jnp.log(jnp.sum(jnp.exp(scores - row_peak), axis=-1, keepdims=True))
    weights = jnp.exp(scores - row_total).astype(jnp.bfloat16)
    outputs = jnp.einsum("hqk,khd->qhd", weights, value_rows, preferred_element_type=jnp.float32)
    totals = [row_total]
    attended = outputs.astype(jnp.bfloat16).reshape(length, head_count * head_size)
    return (attended, (queries, key_rows, value_rows, totals))


def attention_backward(upstream, w_out, attended, stored, head_count, head_size, mask_bias):
    queries, key_rows, value_rows, totals = stored
    length = upstream.shape[0]
    score_scale = head_size ** (-0.5)
    grad_out = inner_rows(attended, upstream)
    attended_grad = (
        times_transpose(upstream, w_out).astype(jnp.bfloat16).reshape(length, head_count, head_size)
    )
    block_rows = min(512, length)
    key_grads = jnp.zeros((length, head_count, head_size), jnp.float32)
    value_grads = jnp.zeros((length, head_count, head_size), jnp.float32)
    query_grads = []
    for number, block_start in enumerate(range(0, length, block_rows)):
        scores = block_scores(queries, key_rows, mask_bias, block_start, block_rows, head_size)
        weights = jnp.exp(scores - totals[number])
        value_grads = jnp.einsum(
            "hqk,qhd->khd",
            weights.astype(jnp.bfloat16),
            attended_grad,
            preferred_element_type=jnp.float32,
        )
        weight_grads = jnp.einsum(
            "qhd,khd->hqk", attended_grad, value_rows, preferred_element_type=jnp.float32
        )
        score_grads = (
            weights * (weight_grads - jnp.sum(weights * weight_grads, axis=-1, keepdims=True))
        ).astype(jnp.bfloat16)
        query_grads.append(
            jnp.einsum("hqk,khd->qhd", score_grads, key_rows, preferred_element_type=jnp.float32)
            * score_scale
        )
        key_grads = (
            jnp.einsum("hqk,qhd->khd", score_grads, queries, preferred_element_type=jnp.float32)
            * score_scale
        )
    projected_grad = jnp.stack([query_grads[0], key_grads, value_grads], axis=1)
    return (
        projected_grad.astype(jnp.bfloat16).reshape(length, 3 * head_count * head_size),
        grad_out,
    )


def block_forward(residual, matrices, gain_rows, bias_rows, head_count, head_size, mask_bias):
    w_qkv, w_out, w_in, w_down = matrices
    normed, norm_one = norm_forward(residual, gain_rows[0], bias_rows[0])
    gathered = gather_rows(normed.astype(jnp.bfloat16))
    attended, stored = attention_forward(gathered, w_qkv, head_count, head_size, mask_bias)
    middle = residual + branch_rows(attended, w_out)
    normed_two, norm_two = norm_forward(middle, gain_rows[1], bias_rows[1])
    gathered_two = gather_rows(normed_two.astype(jnp.bfloat16))
    hidden = jnp.dot(gathered_two, w_in, preferred_element_type=jnp.float32)
    active = jax.nn.gelu(hidden, approximate=False).astype(jnp.bfloat16)
    result = middle + branch_rows(active, w_down)
    return (result, (gathered, norm_one, attended, stored, gathered_two, norm_two, hidden, active))


def block_backward(upstream, matrices, gain_rows, saved_values, head_count, head_size, mask_bias):
    w_qkv, w_out, w_in, w_down = matrices
    gathered, norm_one, attended, stored, gathered_two, norm_two, hidden, active = saved_values
    down_full = gather_grads(upstream.astype(jnp.bfloat16))
    grad_down = inner_rows(active, down_full)
    active_grad = times_transpose(down_full, w_down)
    gelu_pull = jax.vjp(partial(jax.nn.gelu, approximate=False), hidden)[1]
    hidden_grad = gelu_pull(active_grad)[0].astype(jnp.bfloat16)
    grad_in = inner_rows(gathered_two, hidden_grad)
    normed_two_grad = input_rows(hidden_grad, w_in)
    middle_grad, gain_two, bias_two = norm_backward(normed_two_grad, norm_two, gain_rows[1])
    middle_grad = upstream + middle_grad
    middle_full = gather_grads(middle_grad.astype(jnp.bfloat16))
    projected_grad, grad_out = attention_backward(
        middle_full, w_out, attended, stored, head_count, head_size, mask_bias
    )
    grad_qkv = inner_rows(gathered, projected_grad)
    normed_grad = input_rows(projected_grad, w_qkv)
    input_grad, gain_one, bias_one = norm_backward(normed_grad, norm_one, gain_rows[0])
    return (
        middle_grad + input_grad,
        [grad_qkv, grad_out, grad_in, grad_down],
        (gain_one, gain_two, bias_one, bias_two),
    )


def embed_forward(residual, w_embed):
    residual_low = gather_rows(residual.astype(jnp.bfloat16))
    columns = jnp.dot(residual_low, w_embed, preferred_element_type=jnp.float32).astype(
        jnp.bfloat16
    )
    own_columns = lax.all_to_all(columns, "tensor", split_axis=0, concat_axis=1, tiled=True)
    return (own_columns.astype(jnp.float32), residual_low)


def embed_backward(upstream, residual_low, w_embed):
    columns = lax.all_to_all(
        upstream.astype(jnp.bfloat16), "tensor", split_axis=1, concat_axis=0, tiled=True
    )
    grad_embed = inner_rows(residual_low, columns)
    return (input_rows(columns, w_embed), grad_embed)


def slot_builder(gradients, unit_of_slot, unit_width):
    flat_units = jnp.concatenate([gradient.reshape(-1) for gradient in gradients]).reshape(
        -1, unit_width
    )
    unit_total = flat_units.shape[0]
    source = jnp.take(flat_units, jnp.clip(unit_of_slot, 0, unit_total - 1), axis=0)
    return jnp.where((unit_of_slot >= 0)[:, None], source, 0.0)


def per_device(
    tokens_in,
    positions,
    segment_ids,
    owners,
    master,
    first_moment,
    second_moment,
    norm_gains,
    norm_biases,
    norm_first,
    norm_second,
    cotangent,
):
    devices = lax.axis_size("dp")
    tensor_count = lax.axis_size("tensor")
    capacity = master.shape[0]
    unit_width = master.shape[1]
    unit_count = owners.shape[0]
    slot_index = slot_table(owners, devices, capacity)
    unit_of_slot = (
        jnp.full((devices * capacity,), -1, jnp.int32)
        .at[slot_index]
        .set(jnp.arange(unit_count, dtype=jnp.int32))
    )
    targets = unit_of_slot
    targets = jnp.where(targets < 0, unit_count, targets)
    placed = (
        jnp.zeros((unit_count, unit_width), jnp.bfloat16)
        .at[targets]
        .set(lax.all_gather(master.astype(jnp.bfloat16), "dp", axis=0, tiled=True), mode="drop")
    )
    shapes = weight_shapes(tensor_count)
    matrices = split_flat(placed.reshape(-1), shapes)
    encoder = matrices[0:4]
    w_embed = matrices[4]
    decoder = matrices[5:9]
    enc_heads = HE // tensor_count
    dec_heads = HD // tensor_count
    micro_count = tokens_in.shape[0]
    grad_sums = [jnp.zeros(matrix_shape, jnp.float32) for matrix_shape in shapes]
    norm_sums = jnp.zeros((4, DE + DD), jnp.float32)
    decoded_rows = []
    token_grads = []
    for micro_step in range(micro_count):
        tile_ids = segment_ids[micro_step, 0]
        mask_bias = jnp.where(tile_ids[:, None] == tile_ids[None, :], 0.0, MASK_FILL).astype(
            jnp.float32
        )
        position_now = positions[:, micro_step]
        residual = tokens_in[micro_step].astype(jnp.float32) + sincos_embed(position_now, DE)
        residual, enc_saved = block_forward(
            residual, encoder, norm_gains[:, :DE], norm_biases[:, :DE], enc_heads, HDE, mask_bias
        )
        residual, embed_low = embed_forward(residual, w_embed)
        residual = residual + sincos_embed(position_now, DD)
        residual, dec_saved = block_forward(
            residual, decoder, norm_gains[:, DE:], norm_biases[:, DE:], dec_heads, HDD, mask_bias
        )
        decoded_rows.append(residual)
        upstream, dec_grads, dec_norm = block_backward(
            cotangent[micro_step], decoder, norm_gains[:, DE:], dec_saved, dec_heads, HDD, mask_bias
        )
        upstream, grad_embed = embed_backward(upstream, embed_low, w_embed)
        upstream, enc_grads, enc_norm = block_backward(
            upstream, encoder, norm_gains[:, :DE], enc_saved, enc_heads, HDE, mask_bias
        )
        token_grads.append(upstream)
        step_grads = enc_grads + [grad_embed] + dec_grads
        step_norm = jnp.concatenate([jnp.stack(enc_norm), jnp.stack(dec_norm)], axis=1)
        grad_sums = [total_grad + new_grad for total_grad, new_grad in zip(grad_sums, step_grads)]
        norm_sums = norm_sums + step_norm
    reduced = lax.psum_scatter(
        slot_builder(grad_sums, unit_of_slot, unit_width), "dp", scatter_dimension=0, tiled=True
    )
    norm_total = lax.psum(norm_sums, ("dp", "tensor"))
    new_master, new_first, new_second = adamw(
        master, reduced, first_moment, second_moment, WEIGHT_DECAY, LEARN_RATE
    )
    norm_params = jnp.concatenate([norm_gains, norm_biases], axis=0)
    new_norms, norm_one_new, norm_two_new = adamw(
        norm_params, norm_total, norm_first, norm_second, 0.0, NORM_RATE
    )
    return (
        jnp.stack(decoded_rows),
        jnp.stack(token_grads),
        new_master,
        new_first,
        new_second,
        new_norms,
        norm_one_new,
        norm_two_new,
    )


MESH = pl.DeviceIdType.MESH
ALL = slice(None)


class Place:
    def __init__(self):
        self.d = lax.axis_index("dp")
        self.x = lax.axis_index("tensor")
        self.z = self.d // 4
        self.y = (self.d // 2) % 2
        self.c = self.d % 2
        self.ids = {
            "c": (self.d + 1 - 2 * self.c, self.x),
            "y": (self.d + 2 - 4 * self.y, self.x),
            "x": (self.d, 1 - self.x),
            "z+": (self.d + 4, self.x),
            "z-": (self.d - 4, self.x),
        }

    def greet(self, kinds):
        bar = pltpu.get_barrier_semaphore()
        for k in kinds:
            pl.semaphore_signal(bar, inc=1, device_id=self.ids[k], device_id_type=MESH)

        @pl.when(self.z < 3)
        def _():
            pl.semaphore_signal(bar, inc=1, device_id=self.ids["z+"], device_id_type=MESH)

        @pl.when(self.z > 0)
        def _():
            pl.semaphore_signal(bar, inc=1, device_id=self.ids["z-"], device_id_type=MESH)

        inner = jnp.where(jnp.logical_and(self.z > 0, self.z < 3), 1, 0)
        pl.semaphore_wait(bar, len(kinds) + 1 + inner)

    def there(self, disp):
        dz = disp[0]
        if dz == 0:
            return None
        return self.z + dz <= 3 if dz > 0 else self.z + dz >= 0

    def at(self, disp):
        dz, fy, fx = disp
        return (1 - self.x if fx else self.x, self.z + dz, 1 - self.y if fy else self.y)


def when(cond, f):
    if cond is None:
        f()
    else:
        pl.when(cond)(f)


def both(a, b):
    if a is None:
        return b
    if b is None:
        return a
    return jnp.logical_and(a, b)


def spread(order):
    out = {}
    todo = [((0, 0, 0), -1, 0)]
    while todo:
        (dz, fy, fx), last, way = todo.pop(0)
        nxt = []
        for i, a in enumerate(order):
            if i < last:
                continue
            if a == "z":
                for s in (1, -1):
                    if i == last and s != way:
                        continue
                    n = (dz - s, fy, fx)
                    if abs(n[0]) <= 3:
                        nxt.append((n, "z+" if s > 0 else "z-", i, s))
            elif i > last:
                n = (dz, 1, fx) if a == "y" else (dz, fy, 1)
                nxt.append((n, a, i, 0))
        out[(dz, fy, fx)] = [(n, w) for n, w, _, _ in nxt]
        todo += [(n, i, s) for n, _, i, s in nxt]
    return out


def hops(d):
    return abs(d[0]) + d[1] + d[2]


BACK = {"z+": "z-", "z-": "z+", "x": "x", "y": "y"}


def add_rows(acc, got, step=80):
    n = acc.shape[0]
    while n % step:
        step -= 16

    def body(i, _):
        r = pl.ds(pl.multiple_of(i * step, step), step)
        acc[r, :] = acc[r, :] + got[r, :]
        return 0

    lax.fori_loop(0, n // step, body, 0)


SHARD_UNITS = 656
PANEL = 128
GROUPS = ((0, 1), (2,), (3,), (4, 5, 6), (7, 8))

PLAN_OUT = (
    ("zy", "yz", "zy", "yz", "yz"),
    ("zyx", "zxy", "zyx", "yzx", "xzy"),
    (
        64, 65, 66, 0, 70, 1, 128, 2, 4, 5, 6, 137, 68, 3, 8, 9, 12, 7, 192, 130, 256, 140, 69, 10, 73, 129, 133, 136,
        13, 11, 74, 72, 67, 262, 14, 15, 71, 134, 131, 77, 132, 19, 76, 18, 75, 16, 320, 26, 135, 24, 138, 20, 78, 79,
        22, 141, 139, 195, 34, 257, 27, 81, 32, 193, 258, 25, 80, 35, 259, 83, 142, 143, 90, 30, 194, 266, 82, 196,
        39, 40, 144, 199, 84, 197, 260, 198, 263, 148, 147, 200, 261, 264, 31, 201, 202, 203, 98, 33, 29, 28, 42, 91,
        21, 155, 154, 36, 265, 204, 205, 269, 23, 268, 157, 267, 206, 164, 207, 86, 162, 17, 92, 103, 38, 88, 270, 37,
        271, 41, 210, 106, 161, 104, 96, 85, 99, 146, 150, 321, 322, 275, 160, 272, 211, 323, 273, 89, 153, 324, 100,
        101, 276, 208, 105, 168, 97, 165, 282, 217, 163, 218, 95, 209, 93, 87, 152, 214, 166, 325, 94, 151, 167, 102,
        280, 169, 290, 326, 277, 327, 159, 170, 225, 145, 221, 226, 216, 149, 156, 279, 158, 288, 212, 284, 328, 283,
        278, 228, 329, 295, 291, 213, 223, 219, 285, 232, 220, 330, 224, 296, 286, 292, 274, 289, 233, 230, 234, 229,
        281, 287, 222, 227, 231, 215, 294, 293, 298, 297,
    ),
)
PLAN_BACK = (
    ("zxy", "yzx", "zyx", "yzx", "xzy"),
    ("zy", "zy", "zy", "yz", "yz"),
    (
        256, 257, 258, 262, 261, 269, 64, 259, 67, 260, 65, 69, 263, 66, 78, 264, 271, 278, 276, 77, 270, 268, 267,
        71, 70, 275, 282, 85, 72, 266, 76, 265, 192, 82, 68, 199, 277, 73, 0, 84, 274, 74, 272, 5, 273, 80, 75, 279,
        6, 79, 13, 128, 204, 1, 281, 2, 12, 89, 283, 280, 11, 141, 129, 19, 8, 83, 4, 195, 86, 193, 87, 3, 134, 15, 7,
        81, 284, 285, 133, 88, 91, 14, 10, 197, 194, 90, 22, 196, 132, 286, 131, 201, 288, 287, 130, 16, 18, 21, 198,
        9, 92, 20, 205, 93, 291, 202, 200, 290, 136, 289, 143, 292, 26, 140, 208, 150, 206, 17, 94, 23, 135, 25, 212,
        213, 294, 95, 142, 203, 96, 24, 138, 148, 139, 207, 137, 211, 27, 214, 210, 100, 97, 295, 144, 215, 149, 104,
        146, 209, 147, 28, 29, 151, 218, 219, 217, 145, 154, 32, 101, 153, 106, 30, 216, 36, 155, 152, 296, 33, 220,
        105, 221, 293, 98, 156, 40, 157, 224, 31, 103, 298, 222, 160, 158, 223, 164, 102, 99, 228, 37, 161, 227, 165,
        41, 225, 168, 159, 226, 35, 42, 34, 229, 163, 297, 39, 231, 230, 232, 162, 167, 170, 234, 38, 166, 169, 233,
    ),
)


def layout(shapes, shards):
    table = []
    unit_at, row_at, flat_at = 0, 0, 0
    starts = [g[0] for g in GROUPS]
    for i, (rows, cols) in enumerate(shapes):
        if i in starts:
            unit_at = -(-unit_at // 16) * 16
        rb, panels = rows // shards, cols // PANEL
        units = rb * cols // 512
        table.append((rb, panels, units, unit_at, row_at, rb, flat_at))
        unit_at += units
        row_at += rb * panels
        flat_at += units * shards
    return table, unit_at, row_at


def unit_places(units, table, shards):
    place = jnp.zeros_like(units)
    for _, _, n, first, _, _, lo in table:
        v = units - lo
        here = (v // n) * SHARD_UNITS + first + v % n
        place = jnp.where(v >= 0, here, place)
    return place


def own_units(owners, mine, capacity):
    count = owners.shape[0] // 128
    hit = (owners[:, 0] == mine).reshape(count, 128)
    lane = jnp.arange(128)
    tri = (lane[:, None] <= lane[None, :]).astype(jnp.bfloat16)
    within = jnp.dot(hit.astype(jnp.bfloat16), tri, preferred_element_type=jnp.float32)
    totals = within[:, 127].astype(jnp.int32)
    upto = jnp.sum(jnp.where(jnp.arange(count)[:, None] >= jnp.arange(count)[None, :], totals[None, :], 0), axis=1)
    slot = jnp.arange(capacity, dtype=jnp.int32)
    block = jnp.sum((upto[None, :] <= slot[:, None]).astype(jnp.int32), axis=1)
    pick = block[:, None] == jnp.arange(count)[None, :]
    before = jnp.sum(jnp.where(pick, (upto - totals)[None, :], 0), axis=1)
    row = jnp.dot(pick.astype(jnp.bfloat16), within.astype(jnp.bfloat16), preferred_element_type=jnp.float32)
    rank = (slot - before).astype(jnp.float32)
    at = jnp.sum((row <= rank[:, None]).astype(jnp.int32), axis=1)
    return block * 128 + at, slot < upto[count - 1]


BY_ROWS = (1, 3, 6, 8)


def position_table():
    cols = []
    for width in (DE, DD):
        side = width // 16 * 6
        parts = (width - 2 * side, side, side)
        tab = np.zeros((48, width), np.float64)
        col = 0
        for i, n in enumerate(parts):
            half = n // 2
            freq = 1.0 / 10000.0 ** (np.arange(half) / half)
            ang = np.arange(16)[:, None] * freq[None, :]
            tab[16 * i:16 * i + 16, col:col + n] = np.concatenate([np.sin(ang), np.cos(ang)], axis=1)
            col += n
        cols.append(tab)
    left = np.concatenate(cols, axis=1).astype(np.float32)
    terms = []
    for _ in range(3):
        terms.append(left.astype(ml_dtypes.bfloat16))
        left = left - terms[-1].astype(np.float32)
    return np.stack(terms)


def dot(a, b):
    return jnp.dot(a, b, preferred_element_type=jnp.float32)


def dot_nt(a, b):
    return lax.dot_general(a, b, (((1,), (1,)), ((), ())), preferred_element_type=jnp.float32)


def dot_tn(a, b):
    return lax.dot_general(a, b, (((0,), (0,)), ((), ())), preferred_element_type=jnp.float32)


def lanes(i, n=128):
    return pl.ds(pl.multiple_of(i * n, n), n)


def ln_parts(x):
    c = x - jnp.mean(x, axis=-1, keepdims=True)
    inv = lax.rsqrt(jnp.mean(c * c, axis=-1, keepdims=True) + NORM_EPS)
    return c * inv, inv


def ln_back(up, m, inv, gain):
    s = up * gain
    a = jnp.mean(s, axis=-1, keepdims=True)
    b = jnp.mean(s * m, axis=-1, keepdims=True)
    return inv * (s - a - m * b), jnp.sum(up * m, axis=0, keepdims=True), jnp.sum(up, axis=0, keepdims=True)


class Block:
    def __init__(self, width, heads, size, hidden, first, table, col):
        self.width, self.heads, self.size, self.hidden, self.col = width, heads, size, hidden, col
        self.q, self.o, self.a, self.b = table[first:first + 4]
        self.part = heads // 2 * size
        self.per = 128 // size


def panel(w, t, mat, g, lo=0, num=16):
    rb, _, _, _, at, _, _ = mat
    if rb % 16:
        v = w[t, lo:lo + num, at + g // 2 * 2 * rb:at + (g // 2 + 1) * 2 * rb, :].astype(jnp.float32)
        return v[:, g % 2 * rb:(g % 2 + 1) * rb].reshape(num * rb, 128).astype(jnp.bfloat16)
    rows = pl.ds(pl.multiple_of(at + g * rb, 16), rb)
    v = w[t, lo:lo + num, rows, :] if isinstance(lo, int) else w[t, pl.ds(lo, num), rows, :]
    return v.reshape(num * rb, 128)


def pair(w, mat, g):
    return jnp.concatenate([panel(w, 0, mat, g), panel(w, 1, mat, g)], axis=1)


def repeat(count, step, f):
    step = max(k for k in range(1, step + 1) if count % k == 0)

    def turn(i, _):
        for k in range(step):
            f(i * step + k)
        return 0

    if step == count:
        turn(0, 0)
    else:
        lax.fori_loop(0, count // step, turn, 0)


def pull(acc, up, w, mat, step):
    count = mat[1]
    step = max(k for k in range(1, step + 1) if count % k == 0)

    def part(i):
        gs = [i * step + k for k in range(step)]
        d = jnp.concatenate([up[:, lanes(o + g)] for g in gs for o in (0, count)], axis=1)
        return dot_nt(d, jnp.concatenate([pair(w, mat, g) for g in gs], axis=1))

    acc[...] = part(0)

    def turn(i, _):
        acc[...] += part(i)
        return 0

    lax.fori_loop(1, count // step, turn, 0)


def block_fwd(b, x, xo, w, gains, biases, same, n1, proj, p, att, ow, m1, i1, n2, m2, i2, act, slope,
              need, keep):
    cols = slice(b.col, b.col + b.width)
    m, inv = ln_parts(x[...])
    m1[...] = m
    i1[...] = jnp.broadcast_to(inv, i1.shape)
    n1[...] = (m * gains[0:1, cols] + biases[0:1, cols]).astype(jnp.bfloat16)
    keep(0)
    yield
    need(0)
    gq = b.q[1]

    def qkv(g):
        r = dot(n1[...], pair(w, b.q, g)).astype(jnp.bfloat16)
        proj[:, lanes(g)] = r[:, :128]
        proj[:, lanes(gq + g)] = r[:, 128:]

    repeat(gq, 9, qkv)
    yield
    np_ = b.part // 128
    lane = lax.broadcasted_iota(jnp.int32, (256, 128), 1)
    masks = [lane // b.size == i for i in range(b.per)]

    def heads(i):
        t, j = i // np_, i % np_
        q = proj[:, lanes(t * gq + j)]
        k = proj[:, lanes(t * gq + np_ + j)]
        v = proj[:, lanes(t * gq + 2 * np_ + j)]
        total = jnp.zeros((256, 128), jnp.float32)
        for h in range(b.per):
            z = dot_nt(jnp.where(masks[h], q, 0), k) * b.size ** (-0.5) + same
            e = jnp.exp(z - jnp.max(z, axis=-1, keepdims=True))
            s = e * (1.0 / jnp.sum(e, axis=-1, keepdims=True))
            p[i * b.per + h] = s
            total = total + dot(s.astype(jnp.bfloat16), jnp.where(masks[h], v, 0))
        att[:, lanes(i)] = total.astype(jnp.bfloat16)

    repeat(np_, 3, heads)
    yield
    repeat(np_, 3, lambda i: heads(np_ + i))
    keep(1)
    yield
    need(1)
    for t in range(2):
        for g in range(b.width // 128):
            ow[t, :, g * 128:(g + 1) * 128] = panel(w, t, b.o, g)
    x1 = x[...] + dot(att[:, :b.part], ow[0]) + dot(att[:, b.part:], ow[1])
    xo[...] = x1
    m, inv = ln_parts(x1)
    m2[...] = m
    i2[...] = jnp.broadcast_to(inv, i2.shape)
    n2[...] = (m * gains[1:2, cols] + biases[1:2, cols]).astype(jnp.bfloat16)
    keep(2)
    yield
    need(2)
    ga = b.a[1]

    def up(g):
        h = dot(n2[...], pair(w, b.a, g))
        big = 0.5 * (1.0 + lax.erf(h * 0.7071067811865476))
        act_v = (h * big).astype(jnp.bfloat16)
        dens = big + h * (0.3989422804014327 * jnp.exp(-0.5 * h * h))
        act[:, lanes(g)] = act_v[:, :128]
        act[:, lanes(ga + g)] = act_v[:, 128:]
        slope[:, lanes(g)] = dens[:, :128]
        slope[:, lanes(ga + g)] = dens[:, 128:]

    repeat(ga, 12, up)
    keep(3)
    yield
    need(3)
    half = b.hidden // 2

    def down(g):
        w0 = jnp.concatenate([panel(w, 0, b.b, 2 * g), panel(w, 0, b.b, 2 * g + 1)], axis=1)
        w1 = jnp.concatenate([panel(w, 1, b.b, 2 * g), panel(w, 1, b.b, 2 * g + 1)], axis=1)
        xo[:, lanes(g, 256)] += dot(act[:, :half], w0) + dot(act[:, half:], w1)

    repeat(b.width // 256, 1, down)


def block_bwd(b, dr, w, gains, same, n1, proj, p, att, ow, m1, i1, n2, m2, i2, act, slope,
              r, dh, r1, dp_out, acc, da, norm_out, keep):
    cols = slice(b.col, b.col + b.width)
    r[...] = dr[...].astype(jnp.bfloat16)
    keep(3)
    half = b.hidden // 2
    rb = b.b[0]
    gb = b.width // 128
    num = 16

    def hidden(i, _):
        t, lo = i // (16 // num), (i % (16 // num)) * num
        wc = jnp.concatenate([panel(w, t, b.b, g, lo, num) for g in range(gb)], axis=1)
        at = lanes(i, num * rb)
        dh[:, at] = (dot_nt(r[...], wc) * slope[:, at]).astype(jnp.bfloat16)
        return 0

    lax.fori_loop(0, 2 * (16 // num), hidden, 0)
    keep(2)
    ga = b.a[1]
    pull(acc, dh, w, b.a, 12)
    dx, dg, db = ln_back(acc[...], m2[...], i2[:, :1], gains[1:2, cols])
    norm_out[1:2, cols] = dg
    norm_out[3:4, cols] = db
    dx1 = dr[...] + dx
    dr[...] = dx1
    r1[...] = dx1.astype(jnp.bfloat16)
    keep(1)
    for t in range(2):
        da[:, t * b.part:(t + 1) * b.part] = dot_nt(r1[...], ow[t]).astype(jnp.bfloat16)
    gq = b.q[1]
    np_ = b.part // 128
    lane = lax.broadcasted_iota(jnp.int32, (256, 128), 1)
    masks = [lane // b.size == i for i in range(b.per)]
    scale = b.size ** (-0.5)

    def heads(i):
        t, j = i // np_, i % np_
        q = proj[:, lanes(t * gq + j)]
        k = proj[:, lanes(t * gq + np_ + j)]
        v = proj[:, lanes(t * gq + 2 * np_ + j)]
        up_ = da[:, lanes(i)]
        dq = jnp.zeros((256, 128), jnp.float32)
        dk = jnp.zeros((256, 128), jnp.float32)
        dv = jnp.zeros((256, 128), jnp.float32)
        for h in range(b.per):
            s = p[i * b.per + h]
            u = jnp.where(masks[h], up_, 0)
            dp = dot_nt(u, v)
            dv = dv + dot_tn(s.astype(jnp.bfloat16), u)
            t1 = s * dp
            dz = (t1 - s * jnp.sum(t1, axis=-1, keepdims=True)).astype(jnp.bfloat16)
            dq = dq + dot(dz, jnp.where(masks[h], k, 0))
            dk = dk + dot_tn(dz, jnp.where(masks[h], q, 0))
        dp_out[:, lanes(t * gq + j)] = (dq * scale).astype(jnp.bfloat16)
        dp_out[:, lanes(t * gq + np_ + j)] = (dk * scale).astype(jnp.bfloat16)
        dp_out[:, lanes(t * gq + 2 * np_ + j)] = dv.astype(jnp.bfloat16)

    repeat(2 * np_, 6, heads)
    keep(0)
    pull(acc, dp_out, w, b.q, 9)
    dx, dg, db = ln_back(acc[...], m1[...], i1[:, :1], gains[0:1, cols])
    norm_out[0:1, cols] = dg
    norm_out[2:3, cols] = db
    dr[...] = dr[...] + dx


ACTS = (DE, DE, DE, FFE, DE, DD, DD, DD, FFD)
GRADS = (3 * DE, DE, FFE, DE, DD, 3 * DD, DD, FFD, DD)


def lookup(pos, tab, cols):
    row = lax.broadcasted_iota(jnp.int32, (48, 256), 0)
    spots = [jnp.concatenate([pos[0, i], pos[1, i]], axis=1) for i in range(3)]
    hot = jnp.logical_or(jnp.logical_or(row == spots[0], row == spots[1] + 16), row == spots[2] + 32)
    hot = jnp.where(hot, 1.0, 0.0).astype(jnp.bfloat16)
    return sum(dot_tn(hot, tab[i, :, cols]) for i in range(3))


def tile_mask(tile):
    ids = tile[lax.axis_index("tensor")]
    tiles = jnp.where(lax.broadcasted_iota(jnp.int32, (16, 256), 0) == ids, 1.0, 0.0).astype(jnp.bfloat16)
    return (1.0 - dot_tn(tiles, tiles)) * MASK_FILL


FWD_ACTS = [((256, n), jnp.bfloat16) for n in (DE, DE, DE, FFE)]
FWD_KEPT = [((256, 3 * DE), jnp.bfloat16), ((HE, 256, 256), jnp.float32), ((2, DE // 2, DE), jnp.bfloat16),
            ((256, DE), jnp.float32), ((256, 128), jnp.float32), ((256, DE), jnp.float32), ((256, 128), jnp.float32),
            ((256, FFE), jnp.float32)]


def chain_kernel(table, pos, tile, gains, biases, cot, tab, x2, w_hbm, *refs):
    fwd_hbm, refs = refs[:8], refs[8:]
    dec, dx0, norm_out = refs[:3]
    kept_out = refs[3:17]
    kept = refs[17:31]
    low, n1d, ad, n2d, ud, dpe, r1e, dhe, re, dlow, dpd, r1d, dhd, rd = kept
    fwd, refs = refs[31:39], refs[39:]
    proj_e, pe, ow_e, m1e, i1e, m2e, i2e, se = fwd
    (w, pd, sd, proj_d, da_e, da_d, ow_d, m1d, m2d, i1d, i2d, y, acc_e, acc_d, w_sem, f_sem, out_sem) = refs
    enc_b = Block(DE, HE, HDE, FFE, 0, table, 0)
    dec_b = Block(DD, HD, HDD, FFD, 5, table, DE)
    em = table[4]

    def load(m):
        rows = pl.ds(table[m][4], table[m][1] * table[m][5])
        return pltpu.make_async_copy(w_hbm.at[:, :, rows], w.at[:, :, rows], w_sem.at[m])

    def fetch(i):
        return pltpu.make_async_copy(fwd_hbm[i], fwd[i], f_sem.at[i])

    def store(i):
        return pltpu.make_async_copy(kept[i], kept_out[i], out_sem.at[i])

    for m in (4, 5, 6, 7, 8, 3, 2, 1, 0):
        if m != 1:
            load(m).start()
    for i in range(8):
        fetch(i).start()
    same = tile_mask(tile)
    low[...] = x2[...].astype(jnp.bfloat16)
    store(0).start()
    load(4).wait()
    for g in range(2):
        v = dot(low[...], pair(w, em, g)).astype(jnp.bfloat16).astype(jnp.float32)
        y[:, g * 128:(g + 1) * 128] = v[:, :128]
        y[:, 256 + g * 128:256 + (g + 1) * 128] = v[:, 128:]
    y[...] += lookup(pos, tab, slice(DE, DE + DD))
    for _ in block_fwd(dec_b, y, dec, w, gains, biases, same, n1d, proj_d, pd, ad, ow_d, m1d, i1d, n2d, m2d, i2d, ud, sd,
                       lambda k: load(5 + k).wait(), lambda k: store(1 + k).start()):
        pass
    y[...] = cot[...]
    block_bwd(dec_b, y, w, gains, same, n1d, proj_d, pd, ad, ow_d, m1d, i1d, n2d, m2d, i2d, ud, sd,
              rd, dhd, r1d, dpd, acc_d, da_d, norm_out, lambda k: store(10 + k).start())
    dlow[...] = y[...].astype(jnp.bfloat16)
    store(9).start()
    for g in range(2):
        d = jnp.concatenate([dlow[:, g * 128:(g + 1) * 128], dlow[:, 256 + g * 128:256 + (g + 1) * 128]], axis=1)
        v = dot_nt(d, pair(w, em, g))
        if g == 0:
            dx0[...] = v
        else:
            dx0[...] += v
    for m in (3, 2, 0):
        load(m).wait()
    for i in range(8):
        fetch(i).wait()
    block_bwd(enc_b, dx0, w, gains, same, None, proj_e, pe, None, ow_e, m1e, i1e, None, m2e, i2e, None, se,
              re, dhe, r1e, dpe, acc_e, da_e, norm_out, lambda k: store(5 + k).start())
    for i in range(14):
        store(i).wait()


def chain(pos, tile, gains, biases, cot, full, x2, fwd, table):
    f32, bf16 = jnp.float32, jnp.bfloat16
    S = jax.ShapeDtypeStruct
    outs = [S((256, DD), f32), S((256, DE), f32), S((4, DE + DD), f32)]
    kept = [(256, n) for n in ACTS[4:] + GRADS]
    outs += [S(k, bf16) for k in kept]
    V = pltpu.VMEM
    scratch = [V(k, bf16) for k in kept] + [V(k, t) for k, t in FWD_KEPT] + [
        V((2, 16) + full.shape[-2:], bf16), V((HD, 256, 256), f32), V((256, FFD), f32),
        V((256, 3 * DD), bf16), V((256, DE), bf16), V((256, DD), bf16), V((2, DD // 2, DD), bf16),
        V((256, DD), f32), V((256, DD), f32), V((256, 128), f32), V((256, 128), f32),
        V((256, DD), f32), V((256, DE), f32), V((256, DD), f32),
        pltpu.SemaphoreType.DMA((9,)), pltpu.SemaphoreType.DMA((8,)), pltpu.SemaphoreType.DMA((14,))]
    vmem = pl.BlockSpec(memory_space=pltpu.VMEM)
    hbm = pl.BlockSpec(memory_space=pl.ANY)
    args = (pos, tile, gains, biases, cot, jnp.asarray(position_table()), x2,
            full.reshape(2, 16, full.shape[-2], 128), *fwd)
    return pl.pallas_call(
        partial(chain_kernel, table), out_shape=outs, in_specs=[vmem] * 7 + [hbm] * 9, out_specs=[vmem] * 3 + [hbm] * 14,
        scratch_shapes=scratch, compiler_params=pltpu.CompilerParams(vmem_limit_bytes=63 << 20), name="chain",
        cost_estimate=pl.CostEstimate(flops=8_000_000_000, bytes_accessed=40_000_000, transcendentals=3_000_000),
    )(*args)


def grad_panels(table, m, act, grad, turned, put):
    mat = table[m]
    rb, panels, padded = mat[0], mat[1], mat[5]
    count = act.shape[1]

    def turn(i):
        turned[pl.ds(pl.multiple_of(i * 128, 128), 128), :] = act[:, lanes(i)].T

    repeat(count // 128, 6, turn)

    def place(t, g, v):
        put(t, g, v.astype(jnp.bfloat16).reshape(16, rb, 128))

    if m in BY_ROWS:
        half = count // 2

        def body(i):
            t, g = i // (panels // 2), i % (panels // 2)
            v = dot(turned[pl.ds(pl.multiple_of(t * half, 128), half), :], grad[:, lanes(g, 256)])
            if rb % 16:
                v = jnp.concatenate([v[:, :128].reshape(16, rb, 128), v[:, 128:].reshape(16, rb, 128)], axis=1)
                put(t, 2 * g, v.astype(jnp.bfloat16))
                return
            place(t, 2 * g, v[:, :128])
            place(t, 2 * g + 1, v[:, 128:])

        repeat(panels, 6, body)
    else:
        def body(g):
            d = jnp.concatenate([grad[:, lanes(g)], grad[:, lanes(panels + g)]], axis=1)
            v = dot(turned[:count, :], d)
            place(0, g, v[:, :128])
            place(1, g, v[:, 128:])

        repeat(panels, 6, body)


class Wires:
    def __init__(self, place, sem):
        self.place, self.sem, self.used, self.waits = place, sem, 0, []

    def new(self, n=1):
        self.used += n
        assert self.used <= self.sem.shape[0], self.used
        return self.used - n

    def copy(self, k, src, dst, way):
        return pltpu.make_async_remote_copy(src_ref=src, dst_ref=dst, send_sem=self.sem.at[k], recv_sem=self.sem.at[k + 1],
                                            device_id=self.place.ids[way], device_id_type=MESH)

    def send(self, k, src, dst, way, cond=None):
        cp = self.copy(k, src, dst, way)
        when(cond, cp.start)
        self.waits.append((cond, cp))

    def land(self, k, dst, cond=None):
        when(cond, self.copy(k, dst, dst, "c").wait_recv)

    def drain(self):
        for cond, cp in self.waits:
            when(cond, cp.wait_send)


def edge_slots(order):
    slots, used, shared = {}, 0, {}
    for d, kids in sorted(spread(order).items()):
        for _, way in kids:
            if way in "xy" and order.index("z") < order.index(way):
                key = (way, d[1], d[2])
                if key not in shared:
                    shared[key] = used
                    used += 4
                slots[d, way] = (shared[key], 4)
            else:
                slots[d, way] = (used, 1)
                used += 1
    return slots, used


def beyond(p, way):
    return p.z < 3 if way == "z+" else p.z > 0 if way == "z-" else None


def reduce_events(p, w, order, own, half, bufs, ready, done):
    tree = spread(order)
    pair = {d: w.new(2) for d in tree}
    wire = {d: w.new(2) for d in tree}
    parent = {nd: (d, way) for d, t in tree.items() for nd, way in t}
    slots, _ = edge_slots(order)

    def buffer(up, way):
        first, n = slots[up, way]
        return bufs.at[first + p.z + up[0] if n > 1 else first]

    events = []
    far = sorted(tree, key=lambda d: (-hops(d), d))
    for d in far:
        def act(d=d):
            cond = p.there(d)

            def step():
                acc = own(d)
                ready(d)
                w.land(pair[d], half(d))
                add_rows(acc, half(d))
                for nd, way in tree[d]:
                    buf = buffer(d, way)

                    def take(buf=buf, nd=nd):
                        w.land(wire[nd], buf)
                        add_rows(acc, buf)
                    when(beyond(p, way), take)
            when(cond, step)
            if hops(d) == 0:
                done()
            else:
                up, way = parent[d]
                w.send(wire[d], own(d), buffer(up, way), BACK[way], cond)
        events.append(act)

    def share(give):
        for d in far:
            w.send(pair[d], give(d), half(d), "c", p.there(d))

    return events, share, far


def gather_events(p, w, order, first, at):
    tree = spread(order)
    pair = {d: w.new(2) for d in tree}
    wire = {d: w.new(2) for d in tree}
    events = []
    for d in sorted(tree, key=lambda d: (hops(d), d)):
        def act(d=d):
            cond = p.there(d)
            blk = at(d, p.c)
            if hops(d):
                w.land(wire[d], blk, cond)
                src = blk
            else:
                src = first
            for nd, way in tree[d]:
                w.send(wire[nd], src, blk, way, both(cond, beyond(p, way)))
            w.send(pair[d], src, blk, "c", cond)
        events.append(act)

    def finish():
        for d in tree:
            w.land(pair[d], at(d, 1 - p.c), p.there(d))

    return events, finish


def run_events(lists, order, extra=iter(()), every=8):
    assert sorted(order) == sorted(64 * g + i for g, acts in enumerate(lists) for i in range(len(acts)))
    for n, k in enumerate(order):
        if n % every == 0:
            next(extra, None)
        lists[k // 64][k % 64]()
    for _ in extra:
        pass


def group_span(table, mats):
    first, last = table[mats[0]], table[mats[-1]]
    units = last[3] + last[2] - first[3]
    return first[3], -(-units // 16) * 16, first[4], last[4] + last[1] * last[5] - first[4]


def units_to_panels(table, mats, units, flat, put):
    base, count = table[mats[0]][3], units.shape[0]
    for k in range(4):
        flat[pl.ds(k, count, stride=4), :] = units[:, 128 * k:128 * (k + 1)].astype(jnp.float32)
    for m in mats:
        rb, panels, n, first, _, padded, _ = table[m]
        n = 2 if rb % 16 else 1
        for g in range(0, panels, n):
            v = [flat[pl.ds(4 * (first - base) + g + k, rb, stride=panels), :] for k in range(n)]
            put(m, g, jnp.concatenate(v, axis=0).astype(jnp.bfloat16))


def panels_to_units(table, mats, take, flat, units):
    base, count = table[mats[0]][3], units.shape[0]
    used = 0
    for m in mats:
        rb, panels, n, first, _, padded, _ = table[m]
        many = 2 if rb % 16 else 1
        for g in range(0, panels, many):
            v = take(m, g, many)
            for k in range(many):
                flat[pl.ds(4 * (first - base) + g + k, rb, stride=panels), :] = v[k * rb:(k + 1) * rb]
        used = 4 * (first - base + n)
    if used < 4 * count:
        flat[used:4 * count, :] = jnp.zeros((4 * count - used, 128), jnp.float32)
    for k in range(4):
        units[:, 128 * k:128 * (k + 1)] = flat[pl.ds(k, count, stride=4), :].astype(jnp.bfloat16)


def encoder_steps(p, table, out, tok, pos, x, x2, tile, gains, biases, tab, fwd, fwd_out, wv, w_sem, fwd_sem, swapped, arrived):
    n1, att, n2, act, proj, prob, ow, m1, i1, m2, i2, slope = fwd

    def load(m):
        rows = pl.ds(table[m][4], table[m][1] * table[m][5])
        return pltpu.make_async_copy(out.at[:, :, :, :, rows], wv.at[:, :, :, :, rows], w_sem.at[m])

    def store(i):
        return pltpu.make_async_copy(fwd[i], fwd_out[i], fwd_sem.at[i])

    def keep(k):
        for i in ((0, 7, 8), (1, 4, 5), (2, 6, 9, 10), (3, 11))[k]:
            store(i).start()

    for f in swapped:
        f()
    x[...] = tok[...].reshape(256, DE).astype(jnp.float32) + lookup(pos, tab, slice(0, DE))
    same = tile_mask(tile)
    whole = wv.reshape(2, 16, wv.shape[-2], 128)
    block = block_fwd(Block(DE, HE, HDE, FFE, 0, table, 0), x, x2, whole, gains, biases, same, n1, proj, prob, att, ow, m1, i1, n2,
                      m2, i2, act, slope, lambda k: load(k).wait(), keep)
    next(block)
    yield
    for f in arrived[0]:
        f()
    load(0).start()
    load(1).start()
    yield
    for _ in range(4):
        next(block)
        yield
    for f in arrived[1]:
        f()
    load(2).start()
    yield
    next(block)
    yield
    for f in arrived[2]:
        f()
    load(3).start()
    yield
    for _ in block:
        pass
    yield
    for i in range(12):
        store(i).wait()


class Swap:
    def __init__(self, p, w, src, out, give, keep):
        self.p, self.w, self.src, self.out, self.give, self.keep = p, w, src, out, give, keep
        self.k, self.own = w.new(2), w.new()

    def local(self):
        return pltpu.make_async_copy(self.src.at[self.keep], self.out.at[self.p.x], self.w.sem.at[self.own])

    def start(self):
        self.w.send(self.k, self.src.at[self.give], self.out.at[self.p.x], "x")

    def finish(self):
        self.w.land(self.k, self.out.at[1 - self.p.x])
        self.local().wait()


def weights_kernel(table, groups, plan, parts, tok_in, pos_in, cot_in, tile, gains, biases, tab, *refs):
    n = len(groups)
    out, pos, cot, x2 = refs[:4]
    fwd_out, tok, x, fwd, wv, w_sem, fwd_sem = refs[4:16], refs[16], refs[17], refs[18:30], refs[30], refs[31], refs[32]
    rest = refs[33:]
    accs, halves, bufs, shards = (rest[i * n:(i + 1) * n] for i in range(4))
    flat, sem = rest[4 * n:]
    p = Place()
    p.greet(["c", "y", "x"])
    w = Wires(p, sem)
    swaps = [Swap(p, w, tok_in, tok, 1 - p.x, p.x), Swap(p, w, pos_in, pos, (ALL, 1 - p.x), (ALL, p.x)),
             Swap(p, w, cot_in, cot, 1 - p.x, p.x)]
    for s in swaps:
        s.start()
        s.local().start()
    lists, finishes = [], []
    for g, mats in enumerate(groups):
        u0, un, r0, rn = group_span(table, mats)
        acc, half, buf, shard = accs[g], halves[g], bufs[g], shards[g]
        own_sem = w.new()
        loads = {d: w.new() for d in spread(plan[0][g])}

        def own(d, acc=acc):
            return acc.at[p.at(d)[1:]]

        def other(d, half=half):
            return half.at[p.at(d)[1:]]

        def load(d, u0=u0, un=un, own=own, loads=loads):
            return pltpu.make_async_copy(parts.at[p.at(d)[1:] + (p.c, pl.ds(u0, un))], own(d), sem.at[loads[d]])

        def ready(d, load=load):
            load(d).wait()

        def done(mats=mats, acc=acc, shard=shard, r0=r0):
            def put(m, i, v):
                lo = table[m][4] - r0 + i * table[m][5]
                shard[lo:lo + v.shape[0], :] = v
            units_to_panels(table, mats, acc.at[p.z, p.y], flat, put)

        ev, share, far = reduce_events(p, w, plan[0][g], own, other, buf, ready, done)

        def begin(load=load, share=share, far=far, u0=u0, un=un):
            share(lambda d: parts.at[p.at(d)[1:] + (1 - p.c, pl.ds(u0, un))])
            for d in far:
                when(p.there(d), load(d).start)

        def at(d, core, r0=r0, rn=rn):
            t, z, y = p.at(d)
            return out.at[t, z, y, core, pl.ds(r0, rn)]

        def local(shard=shard, r0=r0, rn=rn, own_sem=own_sem):
            return pltpu.make_async_copy(shard, out.at[p.x, p.z, p.y, p.c, pl.ds(r0, rn)], sem.at[own_sem])

        ag, finish = gather_events(p, w, plan[1][g], shard, at)

        def send_first(act=ag[0], local=local):
            act()
            local().start()

        lists.append([begin] + ev + [send_first] + ag[1:])
        finishes += [finish, lambda local=local: local().wait()]
    steps = encoder_steps(p, table, out, tok, pos, x, x2, tile, gains, biases, tab, fwd, fwd_out, wv, w_sem, fwd_sem,
                          [s.finish for s in swaps[:2]], [finishes[2 * k:2 * k + 2] for k in range(3)])
    lists.append([partial(next, steps, None)] * 11)
    run_events(lists, plan[2])
    for f in finishes[6:] + [swaps[2].finish]:
        f()
    w.drain()


def spread_weights(parts, tokens, pos, cot, tile, gains, biases, table, rows, groups, plan, ident):
    spans = [group_span(table, m) for m in groups]
    bf16 = jnp.bfloat16
    S = jax.ShapeDtypeStruct
    V = pltpu.VMEM
    fwd = FWD_ACTS + FWD_KEPT
    enc_rows = table[4][4]
    scratch = [V(tokens.shape, tokens.dtype), V((256, DE), jnp.float32)] + [V(k, t) for k, t in fwd]
    scratch += [V((2, 4, 2, 2, enc_rows, 128), bf16), pltpu.SemaphoreType.DMA((4,)), pltpu.SemaphoreType.DMA((12,))]
    scratch += [V((4, 2, s[1], 512), bf16) for s in spans] * 2
    scratch += [V((edge_slots(o)[1], s[1], 512), bf16) for s, o in zip(spans, plan[0])]
    scratch += [V((s[3], 128), bf16) for s in spans]
    scratch += [V((4 * max(s[1] for s in spans), 128), jnp.float32),
                pltpu.SemaphoreType.DMA((len(groups) * (1 + 5 * 14 + 4 * 28) + 9,))]
    hbm = pl.BlockSpec(memory_space=pl.ANY)
    vmem = pl.BlockSpec(memory_space=pltpu.VMEM)
    return pl.pallas_call(
        partial(weights_kernel, table, groups, plan),
        out_shape=[S((2, 4, 2, 2, rows, 128), bf16), S((2, 3, 1, 128), pos.dtype), S(cot.shape, cot.dtype), S((256, DE), jnp.float32)]
        + [S(k, t) for k, t in fwd],
        in_specs=[hbm] * 4 + [vmem] * 4, out_specs=[hbm, vmem, hbm, vmem] + [hbm] * 12,
        scratch_shapes=scratch,
        compiler_params=pltpu.CompilerParams(collective_id=ident, has_side_effects=True, vmem_limit_bytes=63 << 20),
        name="spread_weights",
    )(parts, tokens, pos, cot, tile, gains, biases, jnp.asarray(position_table()))


def return_kernel(table, groups, plan, *refs):
    n = len(groups)
    kept_in, small_src, dec_in, dx_in, out, small_out, dec, dx = refs[:18], *refs[18:25]
    rest = refs[25:]
    kept, rest = rest[:18], rest[18:]
    acts, grads = kept[:9], kept[9:]
    sides, halves, bufs, units = (rest[i * n:(i + 1) * n] for i in range(4))
    flat, turned, mid, line, load_sem, sem = rest[4 * n:]

    def load(i):
        return pltpu.make_async_copy(kept_in[i], kept[i], load_sem.at[i])

    first = sorted(range(n), key=lambda g: plan[2].index(64 * g))
    for g in first:
        for m in groups[g]:
            load(m).start()
            load(9 + m).start()
    p = Place()
    p.greet(["c", "y", "x"])
    w = Wires(p, sem)
    swaps = [Swap(p, w, a, b, 1 - p.x, p.x) for a, b in ((dec_in, dec), (dx_in, dx))]
    for s in swaps:
        s.local().start()
    swaps[0].start()
    lists, finishes = [], []
    for g, mats in enumerate(groups):
        u0, un, r0, rn = group_span(table, mats)
        side, half, buf, unit = sides[g], halves[g], bufs[g], units[g]
        own_sem = w.new()

        def own(d, side=side):
            return side.at[(p.c,) + p.at(d)]

        def other(d, half=half):
            return half.at[p.at(d)]

        def done(mats=mats, side=side, unit=unit, r0=r0):
            mine = side.at[p.c, p.x, p.z, p.y]

            def take(m, i, many):
                lo = table[m][4] - r0 + i * table[m][5]
                return mine[lo:lo + many * table[m][5], :].astype(jnp.float32)
            panels_to_units(table, mats, take, flat, unit)

        ev, share, far = reduce_events(p, w, plan[0][g], own, other, buf, lambda d: None, done)

        def begin(mats=mats, side=side, share=share, r0=r0):
            for m in mats:
                lo, padded = table[m][4] - r0, table[m][5]

                def put(t, i, v, lo=lo, padded=padded):
                    v = v.reshape(4, 2, 2, v.shape[1], 128)
                    rows = pl.ds(pl.multiple_of(lo + i * padded, 16), v.shape[3])
                    side[0, t, :, :, rows, :] = v[:, :, 0]
                    side[1, t, :, :, rows, :] = v[:, :, 1]
                load(m).wait()
                load(9 + m).wait()
                grad_panels(table, m, acts[m], grads[m], turned, put)
            share(lambda d: side.at[(1 - p.c,) + p.at(d)])

        def at(d, core, u0=u0, un=un):
            _, z, y = p.at(d)
            return out.at[z, y, core, pl.ds(u0, un)]

        def local(unit=unit, u0=u0, un=un, own_sem=own_sem):
            return pltpu.make_async_copy(unit, out.at[p.z, p.y, p.c, pl.ds(u0, un)], sem.at[own_sem])

        ag, finish = gather_events(p, w, plan[1][g], unit, at)

        def send_first(act=ag[0], local=local):
            act()
            local().start()

        lists.append([begin] + ev + [send_first] + ag[1:])
        finishes += [finish, lambda local=local: local().wait()]
    last = max(plan[2].index(64 * g + len(spread(plan[0][g]))) for g in range(n))
    g, i = plan[2][last] // 64, plan[2][last] % 64
    act = lists[g][i]

    def with_swaps():
        act()
        swaps[1].start()

    lists[g][i] = with_swaps
    run_events(lists, plan[2], total_steps(p, w, small_src, small_out, mid, line))
    for f in finishes + [s.finish for s in swaps]:
        f()
    w.drain()


def total_steps(p, w, src, out, mid, line):
    k = [w.new(2) for _ in range(9)]
    now = src
    for i, way in enumerate(("c", "x", "y")):
        w.send(k[i], now, mid.at[i], way)
        yield
        w.land(k[i], mid.at[i])
        nxt = mid.at[3 + i] if i < 2 else line.at[p.z]
        nxt[...] = now[...] + mid[i]
        now = nxt
    for i in range(4):
        lo, hi = jnp.maximum(p.z - i, 0), jnp.minimum(p.z + i, 3)
        if i > 0:
            w.land(k[2 + i], line.at[lo], p.z >= i)
            w.land(k[5 + i], line.at[hi], p.z + i <= 3)
        if i < 3:
            w.send(k[3 + i], line.at[lo], line.at[lo], "z+", jnp.logical_and(p.z >= i, p.z < 3))
            w.send(k[6 + i], line.at[hi], line.at[hi], "z-", jnp.logical_and(p.z + i <= 3, p.z > 0))
            yield
    out[...] = (line[0] + line[1]) + (line[2] + line[3])


def return_grads(kept, small, dec, dx, table, total_units, groups, plan, ident):
    spans = [group_span(table, m) for m in groups]
    bf16 = jnp.bfloat16
    S = jax.ShapeDtypeStruct
    V = pltpu.VMEM
    scratch = [V(v.shape, v.dtype) for v in kept]
    scratch += [V((2, 2, 4, 2, s[3], 128), bf16) for s in spans]
    scratch += [V((2, 4, 2, s[3], 128), bf16) for s in spans]
    scratch += [V((edge_slots(o)[1], s[3], 128), bf16) for s, o in zip(spans, plan[0])]
    scratch += [V((s[1], 512), bf16) for s in spans]
    scratch += [V((4 * max(s[1] for s in spans), 128), jnp.float32), V((FFE, 256), bf16),
                V((5,) + small.shape, small.dtype), V((4,) + small.shape, small.dtype), pltpu.SemaphoreType.DMA((18,)),
                pltpu.SemaphoreType.DMA((len(groups) * (1 + 4 * 14 + 4 * 28) + 24,))]
    vmem = pl.BlockSpec(memory_space=pltpu.VMEM)
    hbm = pl.BlockSpec(memory_space=pl.ANY)
    return pl.pallas_call(
        partial(return_kernel, table, groups, plan),
        out_shape=(S((4, 2, 2, total_units, 512), bf16), S(small.shape, small.dtype), S(dec.shape, dec.dtype), S(dx.shape, dx.dtype)),
        in_specs=[hbm] * 18 + [vmem, hbm, hbm], out_specs=(hbm, vmem, hbm, hbm),
        scratch_shapes=scratch,
        compiler_params=pltpu.CompilerParams(collective_id=ident, has_side_effects=True, vmem_limit_bytes=63 << 20),
        name="return_grads",
    )(*kept, small, dec, dx)


STEP_ROWS = 432


def update_kernel(place, spread, master, first, second, total, gains, biases, norm_first, norm_second, *refs):
    passed, refs = refs[:2], refs[2:]
    new_master, new_first, new_second, new_norms, new_nf, new_ns = refs[:6]
    i = pl.program_id(0)

    @pl.when(i == 0)
    def _():
        for a, b in zip(passed, refs[6:8]):
            b[...] = a[...]
        for v, r in ((gains, slice(0, 2)), (biases, slice(2, 4))):
            new_norms[r, :], new_nf[r, :], new_ns[r, :] = adamw(v[...], total[r, :], norm_first[r, :], norm_second[r, :], 0.0, NORM_RATE)

    lane = lax.broadcasted_iota(jnp.int32, (16, 128), 1)
    row = lax.broadcasted_iota(jnp.int32, (16, 128), 0)
    for k in range(STEP_ROWS // 16):
        tiles, spot = [], jnp.full((16, 128), -1, jnp.int32)
        for j in range(16):
            at = place[i * STEP_ROWS + 16 * k + j]
            tile = jnp.minimum(at >> 4, spread.shape[0] // 16 - 1)
            tiles.append(spread[pl.ds(pl.multiple_of(tile * 16, 16), 16), :])
            spot = jnp.where(row == j, jnp.where(at < spread.shape[0], 16 * j + (at & 15), -1), spot)
        here = slice(16 * k, 16 * k + 16)
        pick = jnp.concatenate([jnp.where(lane == spot, 1.0, 0.0), jnp.where(lane + 128 == spot, 1.0, 0.0)], axis=1)
        grad = dot(pick.astype(jnp.bfloat16), jnp.concatenate(tiles, axis=0))
        new_master[here, :], new_first[here, :], new_second[here, :] = adamw(
            master[here, :], grad, first[here, :], second[here, :], WEIGHT_DECAY, LEARN_RATE)


def update(place, spread, master, first, second, total, gains, biases, norm_first, norm_second, passed):
    slots = master.shape[0]
    S = jax.ShapeDtypeStruct
    rows = pl.BlockSpec((STEP_ROWS, 512), lambda i, s: (i, 0))
    whole = lambda v: pl.BlockSpec(v.shape, lambda i, s: (0, 0), pipeline_mode=pl.Buffered(1))
    small = pl.BlockSpec(total.shape, lambda i, s: (0, 0))
    pair_of = pl.BlockSpec(gains.shape, lambda i, s: (0, 0))
    out = [S(master.shape, jnp.float32)] * 3 + [S(total.shape, jnp.float32)] * 3 + [S(v.shape, v.dtype) for v in passed]
    both = [pl.BlockSpec(v.shape, lambda i, s: (0, 0, 0), pipeline_mode=pl.Buffered(1)) for v in passed]
    return pl.pallas_call(
        update_kernel, out_shape=out,
        grid_spec=pltpu.PrefetchScalarGridSpec(
            num_scalar_prefetch=1, grid=(slots // STEP_ROWS,),
            in_specs=[whole(spread), rows, rows, rows, small, pair_of, pair_of, small, small] + both,
            out_specs=[rows] * 3 + [small] * 3 + both),
        compiler_params=pltpu.CompilerParams(vmem_limit_bytes=62 << 20), name="update",
    )(place, spread, master, first, second, total, gains, biases, norm_first, norm_second, *passed)


def place_kernel(place_s, master, out, wide, staged, sem):
    count = wide.shape[0] // 64 - 1

    def clear(i, _):
        wide[pl.ds(pl.multiple_of(i * 64, 64), 64), :] = jnp.zeros((64, 512), jnp.float32)
        return 0

    lax.fori_loop(0, count, clear, 0)

    def turn(i, _):
        for j in range(16):
            wide[pl.ds(place_s[i * 16 + j], 1), :] = master[pl.ds(i * 16 + j, 1), :]
        return 0

    lax.fori_loop(0, master.shape[0] // 16, turn, 0)
    parts = 4
    part = count // parts * 64

    def copy(k):
        rows = pl.ds(pl.multiple_of(k * part, 64), part)
        return pltpu.make_async_copy(staged.at[rows], out.at[rows], sem.at[k])

    for k in range(parts):
        def narrow(i, _):
            rows = pl.ds(pl.multiple_of(k * part + i * 64, 64), 64)
            staged[rows, :] = wide[rows, :].astype(jnp.bfloat16)
            return 0

        lax.fori_loop(0, part // 64, narrow, 0)
        copy(k).start()
    for k in range(parts):
        copy(k).wait()


def place_blocks(place, master, rows):
    return pl.pallas_call(
        place_kernel, out_shape=jax.ShapeDtypeStruct((rows, 512), jnp.bfloat16),
        grid_spec=pltpu.PrefetchScalarGridSpec(
            num_scalar_prefetch=1, grid=(1,),
            in_specs=[pl.BlockSpec(master.shape, lambda i, s: (0, 0), pipeline_mode=pl.Buffered(1))],
            out_specs=pl.BlockSpec(memory_space=pl.ANY),
            scratch_shapes=[pltpu.VMEM((rows + 64, 512), jnp.float32), pltpu.VMEM((rows, 512), jnp.bfloat16), pltpu.SemaphoreType.DMA((4,))]),
        compiler_params=pltpu.CompilerParams(vmem_limit_bytes=60 << 20), name="place_blocks",
    )(place, master)


def sequence_device(tokens_in, positions, segment_ids, owners, master, first_moment, second_moment, norm_gains,
                    norm_biases, norm_first, norm_second, cotangent):
    shapes = weight_shapes(2)
    table, _, rows = layout(shapes, 16)
    unit, used = own_units(owners, lax.axis_index("dp"), master.shape[0])
    place = jnp.where(used, unit_places(unit, table, 16), 16 * SHARD_UNITS)
    parts = place_blocks(place, master, 16 * SHARD_UNITS)
    full, pos, cot, x2, *fwd = spread_weights(parts.reshape(4, 2, 2, SHARD_UNITS, 512), tokens_in, positions[:, :, None],
                                              cotangent, segment_ids, norm_gains, norm_biases, table, rows, GROUPS, PLAN_OUT, 1)
    kept = chain(pos, segment_ids, norm_gains, norm_biases, cot.reshape(256, DD), full, x2, fwd[4:], table)
    decoded, dx0, norms = kept[:3]
    spread_out, norm_total, decoded, dx0 = return_grads([*fwd[:4], *kept[3:]], norms, decoded.reshape(2, 128, DD), dx0.reshape(2, 128, DE), table,
                                                        SHARD_UNITS, GROUPS, PLAN_BACK, 2)
    new_master, new_first, new_second, new_norms, norm_one_new, norm_two_new, decoded, dx0 = update(
        place, spread_out.reshape(16 * SHARD_UNITS, 512), master, first_moment, second_moment, norm_total, norm_gains, norm_biases, norm_first, norm_second,
        (decoded, dx0))
    return (decoded, dx0, new_master, new_first, new_second, new_norms, norm_one_new, norm_two_new)


def solution(mesh):
    step = sequence_device if (mesh.shape["dp"], mesh.shape["tensor"]) == (16, 2) else per_device
    return jax.shard_map(
        step,
        mesh=mesh,
        in_specs=(
            P(None, ("dp", "tensor"), None),
            P(None, None, ("dp", "tensor")),
            P(None, "dp", None),
            P(),
            P("dp", "tensor"),
            P("dp", "tensor"),
            P("dp", "tensor"),
            P(),
            P(),
            P(),
            P(),
            P(None, ("dp", "tensor"), None),
        ),
        out_specs=(
            P(None, ("dp", "tensor"), None),
            P(None, ("dp", "tensor"), None),
            P("dp", "tensor"),
            P("dp", "tensor"),
            P("dp", "tensor"),
            P(),
            P(),
            P(),
        ),
        check_vma=False,
    )
```

```python
from functools import partial

import jax
import jax.numpy as jnp
import ml_dtypes
import numpy as np
from jax import lax
from jax.experimental import pallas as pl
from jax.experimental.pallas import tpu as pltpu
from jax.sharding import PartitionSpec as P

DE = 768
HE = 12
HDE = 64
FFE = 3072
DD = 512
HD = 16
HDD = 32
FFD = 2048
STEP = 10


NORM_EPS = 1e-06
BETA_ONE = 0.5
BETA_TWO = 0.5
LEARN_RATE = 0.03
NORM_RATE = 0.3
WEIGHT_DECAY = 0.05
ADAM_EPS = 1e-08
MASK_FILL = -1000000000.0


def sincos_part(coordinate, part_width):
    halfway = part_width // 2
    frequency = 1.0 / 10000.0 ** (jnp.arange(halfway, dtype=jnp.float32) / halfway)
    angles = coordinate.astype(jnp.float32)[:, None] * frequency[None, :]
    return jnp.concatenate([jnp.sin(angles), jnp.cos(angles)], axis=1)


def sincos_embed(positions, model_width):
    side_width = model_width // 16 * 6
    first_width = model_width - 2 * side_width
    return jnp.concatenate(
        [
            sincos_part(positions[0], first_width),
            sincos_part(positions[1], side_width),
            sincos_part(positions[2], side_width),
        ],
        axis=1,
    )


def slot_table(owners, devices, capacity):
    owner_ids = owners[:, 0]
    onehot = (owner_ids[:, None] == jnp.arange(devices, dtype=jnp.int32)[None, :]).astype(jnp.int32)
    before = jnp.cumsum(onehot, axis=0) - onehot
    owner_rank = jnp.sum(before * onehot, axis=1)
    return owner_ids * capacity + owner_rank


def weight_shapes(tensor_count):
    enc_heads = HE // tensor_count
    dec_heads = HD // tensor_count
    return [
        (DE, 3 * enc_heads * HDE),
        (enc_heads * HDE, DE),
        (DE, FFE // tensor_count),
        (FFE // tensor_count, DE),
        (DE, DD // tensor_count),
        (DD, 3 * dec_heads * HDD),
        (dec_heads * HDD, DD),
        (DD, FFD // tensor_count),
        (FFD // tensor_count, DD),
    ]


def split_flat(flat_vector, shapes):
    pieces = []
    offset = 0
    for matrix_shape in shapes:
        length = matrix_shape[0] * matrix_shape[1]
        pieces.append(flat_vector[offset : offset + length].reshape(matrix_shape))
        offset += length
    return pieces


def adamw(weights, gradient, moment_one, moment_two, decay_rate, step_rate):
    one_new = BETA_ONE * moment_one + (1.0 - BETA_ONE) * gradient
    two_new = BETA_TWO * moment_two + (1.0 - BETA_TWO) * gradient * gradient
    one_hat = one_new / (1.0 - BETA_ONE**STEP)
    two_hat = two_new / (1.0 - BETA_TWO**STEP)
    weights_new = weights - step_rate * (
        one_hat / (jnp.sqrt(two_hat) + ADAM_EPS) + decay_rate * weights
    )
    return (weights_new, one_new, two_new)


def norm_forward(values, gain_row, bias_row):
    center = values - jnp.mean(values, axis=-1, keepdims=True)
    spread = jnp.mean(center * center, axis=-1, keepdims=True)
    inverse = lax.rsqrt(spread + NORM_EPS)
    normed = center * inverse
    return (normed * gain_row + bias_row, (normed, inverse))


def norm_backward(upstream, stored, gain_row):
    normed, inverse = stored
    scaled = upstream * gain_row
    mean_one = jnp.mean(scaled, axis=-1, keepdims=True)
    mean_two = jnp.mean(scaled * normed, axis=-1, keepdims=True)
    return (
        inverse * (scaled - mean_one - normed * mean_two),
        jnp.sum(upstream * normed, axis=0),
        jnp.sum(upstream, axis=0),
    )


def inner_rows(left_side, right_side):
    return lax.dot_general(
        left_side, right_side, (((0,), (0,)), ((), ())), preferred_element_type=jnp.float32
    )


def times_transpose(left_side, right_side):
    return lax.dot_general(
        left_side, right_side, (((1,), (1,)), ((), ())), preferred_element_type=jnp.float32
    )


def gather_rows(values):
    return lax.all_gather(values, "tensor", axis=0, tiled=True)


def gather_grads(values):
    return lax.all_gather(values, "tensor", axis=0, tiled=True)


def branch_rows(values, weight):
    return lax.psum_scatter(
        jnp.dot(values, weight, preferred_element_type=jnp.float32).astype(jnp.bfloat16),
        "tensor",
        scatter_dimension=0,
        tiled=True,
    ).astype(jnp.float32)


def input_rows(values, weight):
    return lax.psum_scatter(
        times_transpose(values, weight).astype(jnp.bfloat16),
        "tensor",
        scatter_dimension=0,
        tiled=True,
    ).astype(jnp.float32)


def block_scores(queries, key_rows, mask_bias, block_start, block_rows, head_size):
    scores = jnp.einsum(
        "qhd,khd->hqk", queries, key_rows, preferred_element_type=jnp.float32
    ) * head_size ** (-0.5)
    return scores + mask_bias[None, block_start : block_start + block_rows]


def attention_forward(gathered, w_qkv, head_count, head_size, mask_bias):
    length = gathered.shape[0]
    projected = jnp.dot(gathered, w_qkv, preferred_element_type=jnp.float32).astype(jnp.bfloat16)
    projected = projected.reshape(length, 3, head_count, head_size)
    queries = projected[:, 0]
    key_rows = projected[:, 1]
    value_rows = projected[:, 2]
    block_rows = min(512, length)
    scores = block_scores(queries, key_rows, mask_bias, 0, block_rows, head_size)
    row_peak = jnp.max(scores, axis=-1, keepdims=True)
    row_total = row_peak + jnp.log(jnp.sum(jnp.exp(scores - row_peak), axis=-1, keepdims=True))
    weights = jnp.exp(scores - row_total).astype(jnp.bfloat16)
    outputs = jnp.einsum("hqk,khd->qhd", weights, value_rows, preferred_element_type=jnp.float32)
    totals = [row_total]
    attended = outputs.astype(jnp.bfloat16).reshape(length, head_count * head_size)
    return (attended, (queries, key_rows, value_rows, totals))


def attention_backward(upstream, w_out, attended, stored, head_count, head_size, mask_bias):
    queries, key_rows, value_rows, totals = stored
    length = upstream.shape[0]
    score_scale = head_size ** (-0.5)
    grad_out = inner_rows(attended, upstream)
    attended_grad = (
        times_transpose(upstream, w_out).astype(jnp.bfloat16).reshape(length, head_count, head_size)
    )
    block_rows = min(512, length)
    key_grads = jnp.zeros((length, head_count, head_size), jnp.float32)
    value_grads = jnp.zeros((length, head_count, head_size), jnp.float32)
    query_grads = []
    for number, block_start in enumerate(range(0, length, block_rows)):
        scores = block_scores(queries, key_rows, mask_bias, block_start, block_rows, head_size)
        weights = jnp.exp(scores - totals[number])
        value_grads = jnp.einsum(
            "hqk,qhd->khd",
            weights.astype(jnp.bfloat16),
            attended_grad,
            preferred_element_type=jnp.float32,
        )
        weight_grads = jnp.einsum(
            "qhd,khd->hqk", attended_grad, value_rows, preferred_element_type=jnp.float32
        )
        score_grads = (
            weights * (weight_grads - jnp.sum(weights * weight_grads, axis=-1, keepdims=True))
        ).astype(jnp.bfloat16)
        query_grads.append(
            jnp.einsum("hqk,khd->qhd", score_grads, key_rows, preferred_element_type=jnp.float32)
            * score_scale
        )
        key_grads = (
            jnp.einsum("hqk,qhd->khd", score_grads, queries, preferred_element_type=jnp.float32)
            * score_scale
        )
    projected_grad = jnp.stack([query_grads[0], key_grads, value_grads], axis=1)
    return (
        projected_grad.astype(jnp.bfloat16).reshape(length, 3 * head_count * head_size),
        grad_out,
    )


def block_forward(residual, matrices, gain_rows, bias_rows, head_count, head_size, mask_bias):
    w_qkv, w_out, w_in, w_down = matrices
    normed, norm_one = norm_forward(residual, gain_rows[0], bias_rows[0])
    gathered = gather_rows(normed.astype(jnp.bfloat16))
    attended, stored = attention_forward(gathered, w_qkv, head_count, head_size, mask_bias)
    middle = residual + branch_rows(attended, w_out)
    normed_two, norm_two = norm_forward(middle, gain_rows[1], bias_rows[1])
    gathered_two = gather_rows(normed_two.astype(jnp.bfloat16))
    hidden = jnp.dot(gathered_two, w_in, preferred_element_type=jnp.float32)
    active = jax.nn.gelu(hidden, approximate=False).astype(jnp.bfloat16)
    result = middle + branch_rows(active, w_down)
    return (result, (gathered, norm_one, attended, stored, gathered_two, norm_two, hidden, active))


def block_backward(upstream, matrices, gain_rows, saved_values, head_count, head_size, mask_bias):
    w_qkv, w_out, w_in, w_down = matrices
    gathered, norm_one, attended, stored, gathered_two, norm_two, hidden, active = saved_values
    down_full = gather_grads(upstream.astype(jnp.bfloat16))
    grad_down = inner_rows(active, down_full)
    active_grad = times_transpose(down_full, w_down)
    gelu_pull = jax.vjp(partial(jax.nn.gelu, approximate=False), hidden)[1]
    hidden_grad = gelu_pull(active_grad)[0].astype(jnp.bfloat16)
    grad_in = inner_rows(gathered_two, hidden_grad)
    normed_two_grad = input_rows(hidden_grad, w_in)
    middle_grad, gain_two, bias_two = norm_backward(normed_two_grad, norm_two, gain_rows[1])
    middle_grad = upstream + middle_grad
    middle_full = gather_grads(middle_grad.astype(jnp.bfloat16))
    projected_grad, grad_out = attention_backward(
        middle_full, w_out, attended, stored, head_count, head_size, mask_bias
    )
    grad_qkv = inner_rows(gathered, projected_grad)
    normed_grad = input_rows(projected_grad, w_qkv)
    input_grad, gain_one, bias_one = norm_backward(normed_grad, norm_one, gain_rows[0])
    return (
        middle_grad + input_grad,
        [grad_qkv, grad_out, grad_in, grad_down],
        (gain_one, gain_two, bias_one, bias_two),
    )


def embed_forward(residual, w_embed):
    residual_low = gather_rows(residual.astype(jnp.bfloat16))
    columns = jnp.dot(residual_low, w_embed, preferred_element_type=jnp.float32).astype(
        jnp.bfloat16
    )
    own_columns = lax.all_to_all(columns, "tensor", split_axis=0, concat_axis=1, tiled=True)
    return (own_columns.astype(jnp.float32), residual_low)


def embed_backward(upstream, residual_low, w_embed):
    columns = lax.all_to_all(
        upstream.astype(jnp.bfloat16), "tensor", split_axis=1, concat_axis=0, tiled=True
    )
    grad_embed = inner_rows(residual_low, columns)
    return (input_rows(columns, w_embed), grad_embed)


def slot_builder(gradients, unit_of_slot, unit_width):
    flat_units = jnp.concatenate([gradient.reshape(-1) for gradient in gradients]).reshape(
        -1, unit_width
    )
    unit_total = flat_units.shape[0]
    source = jnp.take(flat_units, jnp.clip(unit_of_slot, 0, unit_total - 1), axis=0)
    return jnp.where((unit_of_slot >= 0)[:, None], source, 0.0)


def per_device(
    tokens_in,
    positions,
    segment_ids,
    owners,
    master,
    first_moment,
    second_moment,
    norm_gains,
    norm_biases,
    norm_first,
    norm_second,
    cotangent,
):
    devices = lax.axis_size("dp")
    tensor_count = lax.axis_size("tensor")
    capacity = master.shape[0]
    unit_width = master.shape[1]
    unit_count = owners.shape[0]
    slot_index = slot_table(owners, devices, capacity)
    unit_of_slot = (
        jnp.full((devices * capacity,), -1, jnp.int32)
        .at[slot_index]
        .set(jnp.arange(unit_count, dtype=jnp.int32))
    )
    targets = unit_of_slot
    targets = jnp.where(targets < 0, unit_count, targets)
    placed = (
        jnp.zeros((unit_count, unit_width), jnp.bfloat16)
        .at[targets]
        .set(lax.all_gather(master.astype(jnp.bfloat16), "dp", axis=0, tiled=True), mode="drop")
    )
    shapes = weight_shapes(tensor_count)
    matrices = split_flat(placed.reshape(-1), shapes)
    encoder = matrices[0:4]
    w_embed = matrices[4]
    decoder = matrices[5:9]
    enc_heads = HE // tensor_count
    dec_heads = HD // tensor_count
    micro_count = tokens_in.shape[0]
    grad_sums = [jnp.zeros(matrix_shape, jnp.float32) for matrix_shape in shapes]
    norm_sums = jnp.zeros((4, DE + DD), jnp.float32)
    decoded_rows = []
    token_grads = []
    for micro_step in range(micro_count):
        tile_ids = segment_ids[micro_step, 0]
        mask_bias = jnp.where(tile_ids[:, None] == tile_ids[None, :], 0.0, MASK_FILL).astype(
            jnp.float32
        )
        position_now = positions[:, micro_step]
        residual = tokens_in[micro_step].astype(jnp.float32) + sincos_embed(position_now, DE)
        residual, enc_saved = block_forward(
            residual, encoder, norm_gains[:, :DE], norm_biases[:, :DE], enc_heads, HDE, mask_bias
        )
        residual, embed_low = embed_forward(residual, w_embed)
        residual = residual + sincos_embed(position_now, DD)
        residual, dec_saved = block_forward(
            residual, decoder, norm_gains[:, DE:], norm_biases[:, DE:], dec_heads, HDD, mask_bias
        )
        decoded_rows.append(residual)
        upstream, dec_grads, dec_norm = block_backward(
            cotangent[micro_step], decoder, norm_gains[:, DE:], dec_saved, dec_heads, HDD, mask_bias
        )
        upstream, grad_embed = embed_backward(upstream, embed_low, w_embed)
        upstream, enc_grads, enc_norm = block_backward(
            upstream, encoder, norm_gains[:, :DE], enc_saved, enc_heads, HDE, mask_bias
        )
        token_grads.append(upstream)
        step_grads = enc_grads + [grad_embed] + dec_grads
        step_norm = jnp.concatenate([jnp.stack(enc_norm), jnp.stack(dec_norm)], axis=1)
        grad_sums = [total_grad + new_grad for total_grad, new_grad in zip(grad_sums, step_grads)]
        norm_sums = norm_sums + step_norm
    reduced = lax.psum_scatter(
        slot_builder(grad_sums, unit_of_slot, unit_width), "dp", scatter_dimension=0, tiled=True
    )
    norm_total = lax.psum(norm_sums, ("dp", "tensor"))
    new_master, new_first, new_second = adamw(
        master, reduced, first_moment, second_moment, WEIGHT_DECAY, LEARN_RATE
    )
    norm_params = jnp.concatenate([norm_gains, norm_biases], axis=0)
    new_norms, norm_one_new, norm_two_new = adamw(
        norm_params, norm_total, norm_first, norm_second, 0.0, NORM_RATE
    )
    return (
        jnp.stack(decoded_rows),
        jnp.stack(token_grads),
        new_master,
        new_first,
        new_second,
        new_norms,
        norm_one_new,
        norm_two_new,
    )


MESH = pl.DeviceIdType.MESH
ALL = slice(None)


class Place:
    def __init__(self):
        self.d = lax.axis_index("dp")
        self.x = lax.axis_index("tensor")
        self.z = self.d // 4
        self.y = (self.d // 2) % 2
        self.c = self.d % 2
        self.ids = {
            "c": (self.d + 1 - 2 * self.c, self.x),
            "y": (self.d + 2 - 4 * self.y, self.x),
            "x": (self.d, 1 - self.x),
            "z+": (self.d + 4, self.x),
            "z-": (self.d - 4, self.x),
        }

    def greet(self, kinds):
        bar = pltpu.get_barrier_semaphore()
        for k in kinds:
            pl.semaphore_signal(bar, inc=1, device_id=self.ids[k], device_id_type=MESH)

        @pl.when(self.z < 3)
        def _():
            pl.semaphore_signal(bar, inc=1, device_id=self.ids["z+"], device_id_type=MESH)

        @pl.when(self.z > 0)
        def _():
            pl.semaphore_signal(bar, inc=1, device_id=self.ids["z-"], device_id_type=MESH)

        inner = jnp.where(jnp.logical_and(self.z > 0, self.z < 3), 1, 0)
        pl.semaphore_wait(bar, len(kinds) + 1 + inner)

    def there(self, disp):
        dz = disp[0]
        if dz == 0:
            return None
        return self.z + dz <= 3 if dz > 0 else self.z + dz >= 0

    def at(self, disp):
        dz, fy, fx = disp
        return (1 - self.x if fx else self.x, self.z + dz, 1 - self.y if fy else self.y)


def when(cond, f):
    if cond is None:
        f()
    else:
        pl.when(cond)(f)


def both(a, b):
    if a is None:
        return b
    if b is None:
        return a
    return jnp.logical_and(a, b)


def spread(order):
    out = {}
    todo = [((0, 0, 0), -1, 0)]
    while todo:
        (dz, fy, fx), last, way = todo.pop(0)
        nxt = []
        for i, a in enumerate(order):
            if i < last:
                continue
            if a == "z":
                for s in (1, -1):
                    if i == last and s != way:
                        continue
                    n = (dz - s, fy, fx)
                    if abs(n[0]) <= 3:
                        nxt.append((n, "z+" if s > 0 else "z-", i, s))
            elif i > last:
                n = (dz, 1, fx) if a == "y" else (dz, fy, 1)
                nxt.append((n, a, i, 0))
        out[(dz, fy, fx)] = [(n, w) for n, w, _, _ in nxt]
        todo += [(n, i, s) for n, _, i, s in nxt]
    return out


def hops(d):
    return abs(d[0]) + d[1] + d[2]


BACK = {"z+": "z-", "z-": "z+", "x": "x", "y": "y"}


def add_rows(acc, got, step=80):
    n = acc.shape[0]
    while n % step:
        step -= 16

    def body(i, _):
        r = pl.ds(pl.multiple_of(i * step, step), step)
        acc[r, :] = acc[r, :] + got[r, :]
        return 0

    lax.fori_loop(0, n // step, body, 0)


SHARD_UNITS = 656
PANEL = 128
GROUPS = ((0, 1), (2,), (3,), (4, 5, 6), (7, 8))

PLAN_OUT = (
    ("zy", "yz", "zy", "yz", "yz"),
    ("zyx", "zxy", "zyx", "yzx", "xzy"),
    (
        64, 65, 66, 0, 70, 1, 128, 2, 4, 5, 6, 137, 68, 3, 8, 9, 12, 7, 192, 130, 256, 140, 69, 10, 73, 129, 133, 136,
        13, 11, 74, 72, 67, 262, 14, 15, 71, 134, 131, 77, 132, 19, 76, 18, 75, 16, 320, 26, 135, 24, 138, 20, 78, 79,
        22, 141, 139, 195, 34, 257, 27, 81, 32, 193, 258, 25, 80, 35, 259, 83, 142, 143, 90, 30, 194, 266, 82, 196,
        39, 40, 144, 199, 84, 197, 260, 198, 263, 148, 147, 200, 261, 264, 31, 201, 202, 203, 98, 33, 29, 28, 42, 91,
        21, 155, 154, 36, 265, 204, 205, 269, 23, 268, 157, 267, 206, 164, 207, 86, 162, 17, 92, 103, 38, 88, 270, 37,
        271, 41, 210, 106, 161, 104, 96, 85, 99, 146, 150, 321, 322, 275, 160, 272, 211, 323, 273, 89, 153, 324, 100,
        101, 276, 208, 105, 168, 97, 165, 282, 217, 163, 218, 95, 209, 93, 87, 152, 214, 166, 325, 94, 151, 167, 102,
        280, 169, 290, 326, 277, 327, 159, 170, 225, 145, 221, 226, 216, 149, 156, 279, 158, 288, 212, 284, 328, 283,
        278, 228, 329, 295, 291, 213, 223, 219, 285, 232, 220, 330, 224, 296, 286, 292, 274, 289, 233, 230, 234, 229,
        281, 287, 222, 227, 231, 215, 294, 293, 298, 297,
    ),
)
PLAN_BACK = (
    ("zxy", "yzx", "zyx", "yzx", "xzy"),
    ("zy", "zy", "zy", "yz", "yz"),
    (
        256, 257, 258, 262, 261, 269, 64, 259, 67, 260, 65, 69, 263, 66, 78, 264, 271, 278, 276, 77, 270, 268, 267,
        71, 70, 275, 282, 85, 72, 266, 76, 265, 192, 82, 68, 199, 277, 73, 0, 84, 274, 74, 272, 5, 273, 80, 75, 279,
        6, 79, 13, 128, 204, 1, 281, 2, 12, 89, 283, 280, 11, 141, 129, 19, 8, 83, 4, 195, 86, 193, 87, 3, 134, 15, 7,
        81, 284, 285, 133, 88, 91, 14, 10, 197, 194, 90, 22, 196, 132, 286, 131, 201, 288, 287, 130, 16, 18, 21, 198,
        9, 92, 20, 205, 93, 291, 202, 200, 290, 136, 289, 143, 292, 26, 140, 208, 150, 206, 17, 94, 23, 135, 25, 212,
        213, 294, 95, 142, 203, 96, 24, 138, 148, 139, 207, 137, 211, 27, 214, 210, 100, 97, 295, 144, 215, 149, 104,
        146, 209, 147, 28, 29, 151, 218, 219, 217, 145, 154, 32, 101, 153, 106, 30, 216, 36, 155, 152, 296, 33, 220,
        105, 221, 293, 98, 156, 40, 157, 224, 31, 103, 298, 222, 160, 158, 223, 164, 102, 99, 228, 37, 161, 227, 165,
        41, 225, 168, 159, 226, 35, 42, 34, 229, 163, 297, 39, 231, 230, 232, 162, 167, 170, 234, 38, 166, 169, 233,
    ),
)


def layout(shapes, shards):
    table = []
    unit_at, row_at, flat_at = 0, 0, 0
    starts = [g[0] for g in GROUPS]
    for i, (rows, cols) in enumerate(shapes):
        if i in starts:
            unit_at = -(-unit_at // 16) * 16
        rb, panels = rows // shards, cols // PANEL
        units = rb * cols // 512
        table.append((rb, panels, units, unit_at, row_at, rb, flat_at))
        unit_at += units
        row_at += rb * panels
        flat_at += units * shards
    return table, unit_at, row_at


def unit_places(units, table, shards):
    place = jnp.zeros_like(units)
    for _, _, n, first, _, _, lo in table:
        v = units - lo
        here = (v // n) * SHARD_UNITS + first + v % n
        place = jnp.where(v >= 0, here, place)
    return place


def own_units(owners, mine, capacity):
    count = owners.shape[0] // 128
    hit = (owners[:, 0] == mine).reshape(count, 128)
    lane = jnp.arange(128)
    tri = (lane[:, None] <= lane[None, :]).astype(jnp.bfloat16)
    within = jnp.dot(hit.astype(jnp.bfloat16), tri, preferred_element_type=jnp.float32)
    totals = within[:, 127].astype(jnp.int32)
    upto = jnp.sum(jnp.where(jnp.arange(count)[:, None] >= jnp.arange(count)[None, :], totals[None, :], 0), axis=1)
    slot = jnp.arange(capacity, dtype=jnp.int32)
    block = jnp.sum((upto[None, :] <= slot[:, None]).astype(jnp.int32), axis=1)
    pick = block[:, None] == jnp.arange(count)[None, :]
    before = jnp.sum(jnp.where(pick, (upto - totals)[None, :], 0), axis=1)
    row = jnp.dot(pick.astype(jnp.bfloat16), within.astype(jnp.bfloat16), preferred_element_type=jnp.float32)
    rank = (slot - before).astype(jnp.float32)
    at = jnp.sum((row <= rank[:, None]).astype(jnp.int32), axis=1)
    return block * 128 + at, slot < upto[count - 1]


BY_ROWS = (1, 3, 6, 8)


def position_table():
    cols = []
    for width in (DE, DD):
        side = width // 16 * 6
        parts = (width - 2 * side, side, side)
        tab = np.zeros((48, width), np.float64)
        col = 0
        for i, n in enumerate(parts):
            half = n // 2
            freq = 1.0 / 10000.0 ** (np.arange(half) / half)
            ang = np.arange(16)[:, None] * freq[None, :]
            tab[16 * i:16 * i + 16, col:col + n] = np.concatenate([np.sin(ang), np.cos(ang)], axis=1)
            col += n
        cols.append(tab)
    left = np.concatenate(cols, axis=1).astype(np.float32)
    terms = []
    for _ in range(3):
        terms.append(left.astype(ml_dtypes.bfloat16))
        left = left - terms[-1].astype(np.float32)
    return np.stack(terms)


def dot(a, b):
    return jnp.dot(a, b, preferred_element_type=jnp.float32)


def dot_nt(a, b):
    return lax.dot_general(a, b, (((1,), (1,)), ((), ())), preferred_element_type=jnp.float32)


def dot_tn(a, b):
    return lax.dot_general(a, b, (((0,), (0,)), ((), ())), preferred_element_type=jnp.float32)


def lanes(i, n=128):
    return pl.ds(pl.multiple_of(i * n, n), n)


def ln_parts(x):
    c = x - jnp.mean(x, axis=-1, keepdims=True)
    inv = lax.rsqrt(jnp.mean(c * c, axis=-1, keepdims=True) + NORM_EPS)
    return c * inv, inv


def ln_back(up, m, inv, gain):
    s = up * gain
    a = jnp.mean(s, axis=-1, keepdims=True)
    b = jnp.mean(s * m, axis=-1, keepdims=True)
    return inv * (s - a - m * b), jnp.sum(up * m, axis=0, keepdims=True), jnp.sum(up, axis=0, keepdims=True)


class Block:
    def __init__(self, width, heads, size, hidden, first, table, col):
        self.width, self.heads, self.size, self.hidden, self.col = width, heads, size, hidden, col
        self.q, self.o, self.a, self.b = table[first:first + 4]
        self.part = heads // 2 * size
        self.per = 128 // size


def panel(w, t, mat, g, lo=0, num=16):
    rb, _, _, _, at, _, _ = mat
    if rb % 16:
        v = w[t, lo:lo + num, at + g // 2 * 2 * rb:at + (g // 2 + 1) * 2 * rb, :].astype(jnp.float32)
        return v[:, g % 2 * rb:(g % 2 + 1) * rb].reshape(num * rb, 128).astype(jnp.bfloat16)
    rows = pl.ds(pl.multiple_of(at + g * rb, 16), rb)
    v = w[t, lo:lo + num, rows, :] if isinstance(lo, int) else w[t, pl.ds(lo, num), rows, :]
    return v.reshape(num * rb, 128)


def pair(w, mat, g):
    return jnp.concatenate([panel(w, 0, mat, g), panel(w, 1, mat, g)], axis=1)


def repeat(count, step, f):
    step = max(k for k in range(1, step + 1) if count % k == 0)

    def turn(i, _):
        for k in range(step):
            f(i * step + k)
        return 0

    if step == count:
        turn(0, 0)
    else:
        lax.fori_loop(0, count // step, turn, 0)


def pull(acc, up, w, mat, step):
    count = mat[1]
    step = max(k for k in range(1, step + 1) if count % k == 0)

    def part(i):
        gs = [i * step + k for k in range(step)]
        d = jnp.concatenate([up[:, lanes(o + g)] for g in gs for o in (0, count)], axis=1)
        return dot_nt(d, jnp.concatenate([pair(w, mat, g) for g in gs], axis=1))

    acc[...] = part(0)

    def turn(i, _):
        acc[...] += part(i)
        return 0

    lax.fori_loop(1, count // step, turn, 0)


def block_fwd(b, x, xo, w, gains, biases, same, n1, proj, p, att, ow, m1, i1, n2, m2, i2, act, slope,
              need, keep):
    cols = slice(b.col, b.col + b.width)
    m, inv = ln_parts(x[...])
    m1[...] = m
    i1[...] = jnp.broadcast_to(inv, i1.shape)
    n1[...] = (m * gains[0:1, cols] + biases[0:1, cols]).astype(jnp.bfloat16)
    keep(0)
    yield
    need(0)
    gq = b.q[1]

    def qkv(g):
        r = dot(n1[...], pair(w, b.q, g)).astype(jnp.bfloat16)
        proj[:, lanes(g)] = r[:, :128]
        proj[:, lanes(gq + g)] = r[:, 128:]

    repeat(gq, 9, qkv)
    yield
    np_ = b.part // 128
    lane = lax.broadcasted_iota(jnp.int32, (256, 128), 1)
    masks = [lane // b.size == i for i in range(b.per)]

    def heads(i):
        t, j = i // np_, i % np_
        q = proj[:, lanes(t * gq + j)]
        k = proj[:, lanes(t * gq + np_ + j)]
        v = proj[:, lanes(t * gq + 2 * np_ + j)]
        total = jnp.zeros((256, 128), jnp.float32)
        for h in range(b.per):
            z = dot_nt(jnp.where(masks[h], q, 0), k) * b.size ** (-0.5) + same
            e = jnp.exp(z - jnp.max(z, axis=-1, keepdims=True))
            s = e * (1.0 / jnp.sum(e, axis=-1, keepdims=True))
            p[i * b.per + h] = s
            total = total + dot(s.astype(jnp.bfloat16), jnp.where(masks[h], v, 0))
        att[:, lanes(i)] = total.astype(jnp.bfloat16)

    repeat(np_, 3, heads)
    yield
    repeat(np_, 3, lambda i: heads(np_ + i))
    keep(1)
    yield
    need(1)
    for t in range(2):
        for g in range(b.width // 128):
            ow[t, :, g * 128:(g + 1) * 128] = panel(w, t, b.o, g)
    x1 = x[...] + dot(att[:, :b.part], ow[0]) + dot(att[:, b.part:], ow[1])
    xo[...] = x1
    m, inv = ln_parts(x1)
    m2[...] = m
    i2[...] = jnp.broadcast_to(inv, i2.shape)
    n2[...] = (m * gains[1:2, cols] + biases[1:2, cols]).astype(jnp.bfloat16)
    keep(2)
    yield
    need(2)
    ga = b.a[1]

    def up(g):
        h = dot(n2[...], pair(w, b.a, g))
        big = 0.5 * (1.0 + lax.erf(h * 0.7071067811865476))
        act_v = (h * big).astype(jnp.bfloat16)
        dens = big + h * (0.3989422804014327 * jnp.exp(-0.5 * h * h))
        act[:, lanes(g)] = act_v[:, :128]
        act[:, lanes(ga + g)] = act_v[:, 128:]
        slope[:, lanes(g)] = dens[:, :128]
        slope[:, lanes(ga + g)] = dens[:, 128:]

    repeat(ga, 12, up)
    keep(3)
    yield
    need(3)
    half = b.hidden // 2

    def down(g):
        w0 = jnp.concatenate([panel(w, 0, b.b, 2 * g), panel(w, 0, b.b, 2 * g + 1)], axis=1)
        w1 = jnp.concatenate([panel(w, 1, b.b, 2 * g), panel(w, 1, b.b, 2 * g + 1)], axis=1)
        xo[:, lanes(g, 256)] += dot(act[:, :half], w0) + dot(act[:, half:], w1)

    repeat(b.width // 256, 1, down)


def block_bwd(b, dr, w, gains, same, n1, proj, p, att, ow, m1, i1, n2, m2, i2, act, slope,
              r, dh, r1, dp_out, acc, da, norm_out, keep):
    cols = slice(b.col, b.col + b.width)
    r[...] = dr[...].astype(jnp.bfloat16)
    keep(3)
    half = b.hidden // 2
    rb = b.b[0]
    gb = b.width // 128
    num = 16

    def hidden(i, _):
        t, lo = i // (16 // num), (i % (16 // num)) * num
        wc = jnp.concatenate([panel(w, t, b.b, g, lo, num) for g in range(gb)], axis=1)
        at = lanes(i, num * rb)
        dh[:, at] = (dot_nt(r[...], wc) * slope[:, at]).astype(jnp.bfloat16)
        return 0

    lax.fori_loop(0, 2 * (16 // num), hidden, 0)
    keep(2)
    ga = b.a[1]
    pull(acc, dh, w, b.a, 12)
    dx, dg, db = ln_back(acc[...], m2[...], i2[:, :1], gains[1:2, cols])
    norm_out[1:2, cols] = dg
    norm_out[3:4, cols] = db
    dx1 = dr[...] + dx
    dr[...] = dx1
    r1[...] = dx1.astype(jnp.bfloat16)
    keep(1)
    for t in range(2):
        da[:, t * b.part:(t + 1) * b.part] = dot_nt(r1[...], ow[t]).astype(jnp.bfloat16)
    gq = b.q[1]
    np_ = b.part // 128
    lane = lax.broadcasted_iota(jnp.int32, (256, 128), 1)
    masks = [lane // b.size == i for i in range(b.per)]
    scale = b.size ** (-0.5)

    def heads(i):
        t, j = i // np_, i % np_
        q = proj[:, lanes(t * gq + j)]
        k = proj[:, lanes(t * gq + np_ + j)]
        v = proj[:, lanes(t * gq + 2 * np_ + j)]
        up_ = da[:, lanes(i)]
        dq = jnp.zeros((256, 128), jnp.float32)
        dk = jnp.zeros((256, 128), jnp.float32)
        dv = jnp.zeros((256, 128), jnp.float32)
        for h in range(b.per):
            s = p[i * b.per + h]
            u = jnp.where(masks[h], up_, 0)
            dp = dot_nt(u, v)
            dv = dv + dot_tn(s.astype(jnp.bfloat16), u)
            t1 = s * dp
            dz = (t1 - s * jnp.sum(t1, axis=-1, keepdims=True)).astype(jnp.bfloat16)
            dq = dq + dot(dz, jnp.where(masks[h], k, 0))
            dk = dk + dot_tn(dz, jnp.where(masks[h], q, 0))
        dp_out[:, lanes(t * gq + j)] = (dq * scale).astype(jnp.bfloat16)
        dp_out[:, lanes(t * gq + np_ + j)] = (dk * scale).astype(jnp.bfloat16)
        dp_out[:, lanes(t * gq + 2 * np_ + j)] = dv.astype(jnp.bfloat16)

    repeat(2 * np_, 6, heads)
    keep(0)
    pull(acc, dp_out, w, b.q, 9)
    dx, dg, db = ln_back(acc[...], m1[...], i1[:, :1], gains[0:1, cols])
    norm_out[0:1, cols] = dg
    norm_out[2:3, cols] = db
    dr[...] = dr[...] + dx


ACTS = (DE, DE, DE, FFE, DE, DD, DD, DD, FFD)
GRADS = (3 * DE, DE, FFE, DE, DD, 3 * DD, DD, FFD, DD)


def lookup(pos, tab, cols):
    row = lax.broadcasted_iota(jnp.int32, (48, 256), 0)
    spots = [jnp.concatenate([pos[0, i], pos[1, i]], axis=1) for i in range(3)]
    hot = jnp.logical_or(jnp.logical_or(row == spots[0], row == spots[1] + 16), row == spots[2] + 32)
    hot = jnp.where(hot, 1.0, 0.0).astype(jnp.bfloat16)
    return sum(dot_tn(hot, tab[i, :, cols]) for i in range(3))


def tile_mask(tile):
    ids = tile[lax.axis_index("tensor")]
    tiles = jnp.where(lax.broadcasted_iota(jnp.int32, (16, 256), 0) == ids, 1.0, 0.0).astype(jnp.bfloat16)
    return (1.0 - dot_tn(tiles, tiles)) * MASK_FILL


FWD_ACTS = [((256, n), jnp.bfloat16) for n in (DE, DE, DE, FFE)]
FWD_KEPT = [((256, 3 * DE), jnp.bfloat16), ((HE, 256, 256), jnp.float32), ((2, DE // 2, DE), jnp.bfloat16),
            ((256, DE), jnp.float32), ((256, 128), jnp.float32), ((256, DE), jnp.float32), ((256, 128), jnp.float32),
            ((256, FFE), jnp.float32)]


def chain_kernel(table, pos, tile, gains, biases, cot, tab, x2, w_hbm, *refs):
    fwd_hbm, refs = refs[:8], refs[8:]
    dec, dx0, norm_out = refs[:3]
    kept_out = refs[3:17]
    kept = refs[17:31]
    low, n1d, ad, n2d, ud, dpe, r1e, dhe, re, dlow, dpd, r1d, dhd, rd = kept
    fwd, refs = refs[31:39], refs[39:]
    proj_e, pe, ow_e, m1e, i1e, m2e, i2e, se = fwd
    (w, pd, sd, proj_d, da_e, da_d, ow_d, m1d, m2d, i1d, i2d, y, acc_e, acc_d, w_sem, f_sem, out_sem) = refs
    enc_b = Block(DE, HE, HDE, FFE, 0, table, 0)
    dec_b = Block(DD, HD, HDD, FFD, 5, table, DE)
    em = table[4]

    def load(m):
        rows = pl.ds(table[m][4], table[m][1] * table[m][5])
        return pltpu.make_async_copy(w_hbm.at[:, :, rows], w.at[:, :, rows], w_sem.at[m])

    def fetch(i):
        return pltpu.make_async_copy(fwd_hbm[i], fwd[i], f_sem.at[i])

    def store(i):
        return pltpu.make_async_copy(kept[i], kept_out[i], out_sem.at[i])

    for m in (4, 5, 6, 7, 8, 3, 2, 1, 0):
        if m != 1:
            load(m).start()
    for i in range(8):
        fetch(i).start()
    same = tile_mask(tile)
    low[...] = x2[...].astype(jnp.bfloat16)
    store(0).start()
    load(4).wait()
    for g in range(2):
        v = dot(low[...], pair(w, em, g)).astype(jnp.bfloat16).astype(jnp.float32)
        y[:, g * 128:(g + 1) * 128] = v[:, :128]
        y[:, 256 + g * 128:256 + (g + 1) * 128] = v[:, 128:]
    y[...] += lookup(pos, tab, slice(DE, DE + DD))
    for _ in block_fwd(dec_b, y, dec, w, gains, biases, same, n1d, proj_d, pd, ad, ow_d, m1d, i1d, n2d, m2d, i2d, ud, sd,
                       lambda k: load(5 + k).wait(), lambda k: store(1 + k).start()):
        pass
    y[...] = cot[...]
    block_bwd(dec_b, y, w, gains, same, n1d, proj_d, pd, ad, ow_d, m1d, i1d, n2d, m2d, i2d, ud, sd,
              rd, dhd, r1d, dpd, acc_d, da_d, norm_out, lambda k: store(10 + k).start())
    dlow[...] = y[...].astype(jnp.bfloat16)
    store(9).start()
    for g in range(2):
        d = jnp.concatenate([dlow[:, g * 128:(g + 1) * 128], dlow[:, 256 + g * 128:256 + (g + 1) * 128]], axis=1)
        v = dot_nt(d, pair(w, em, g))
        if g == 0:
            dx0[...] = v
        else:
            dx0[...] += v
    for m in (3, 2, 0):
        load(m).wait()
    for i in range(8):
        fetch(i).wait()
    block_bwd(enc_b, dx0, w, gains, same, None, proj_e, pe, None, ow_e, m1e, i1e, None, m2e, i2e, None, se,
              re, dhe, r1e, dpe, acc_e, da_e, norm_out, lambda k: store(5 + k).start())
    for i in range(14):
        store(i).wait()


def chain(pos, tile, gains, biases, cot, full, x2, fwd, table):
    f32, bf16 = jnp.float32, jnp.bfloat16
    S = jax.ShapeDtypeStruct
    outs = [S((256, DD), f32), S((256, DE), f32), S((4, DE + DD), f32)]
    kept = [(256, n) for n in ACTS[4:] + GRADS]
    outs += [S(k, bf16) for k in kept]
    V = pltpu.VMEM
    scratch = [V(k, bf16) for k in kept] + [V(k, t) for k, t in FWD_KEPT] + [
        V((2, 16) + full.shape[-2:], bf16), V((HD, 256, 256), f32), V((256, FFD), f32),
        V((256, 3 * DD), bf16), V((256, DE), bf16), V((256, DD), bf16), V((2, DD // 2, DD), bf16),
        V((256, DD), f32), V((256, DD), f32), V((256, 128), f32), V((256, 128), f32),
        V((256, DD), f32), V((256, DE), f32), V((256, DD), f32),
        pltpu.SemaphoreType.DMA((9,)), pltpu.SemaphoreType.DMA((8,)), pltpu.SemaphoreType.DMA((14,))]
    vmem = pl.BlockSpec(memory_space=pltpu.VMEM)
    hbm = pl.BlockSpec(memory_space=pl.ANY)
    args = (pos, tile, gains, biases, cot, jnp.asarray(position_table()), x2,
            full.reshape(2, 16, full.shape[-2], 128), *fwd)
    return pl.pallas_call(
        partial(chain_kernel, table), out_shape=outs, in_specs=[vmem] * 7 + [hbm] * 9, out_specs=[vmem] * 3 + [hbm] * 14,
        scratch_shapes=scratch, compiler_params=pltpu.CompilerParams(vmem_limit_bytes=63 << 20), name="chain",
        cost_estimate=pl.CostEstimate(flops=8_000_000_000, bytes_accessed=40_000_000, transcendentals=3_000_000),
    )(*args)


def grad_panels(table, m, act, grad, turned, put):
    mat = table[m]
    rb, panels, padded = mat[0], mat[1], mat[5]
    count = act.shape[1]

    def turn(i):
        turned[pl.ds(pl.multiple_of(i * 128, 128), 128), :] = act[:, lanes(i)].T

    repeat(count // 128, 6, turn)

    def place(t, g, v):
        put(t, g, v.astype(jnp.bfloat16).reshape(16, rb, 128))

    if m in BY_ROWS:
        half = count // 2

        def body(i):
            t, g = i // (panels // 2), i % (panels // 2)
            v = dot(turned[pl.ds(pl.multiple_of(t * half, 128), half), :], grad[:, lanes(g, 256)])
            if rb % 16:
                v = jnp.concatenate([v[:, :128].reshape(16, rb, 128), v[:, 128:].reshape(16, rb, 128)], axis=1)
                put(t, 2 * g, v.astype(jnp.bfloat16))
                return
            place(t, 2 * g, v[:, :128])
            place(t, 2 * g + 1, v[:, 128:])

        repeat(panels, 6, body)
    else:
        def body(g):
            d = jnp.concatenate([grad[:, lanes(g)], grad[:, lanes(panels + g)]], axis=1)
            v = dot(turned[:count, :], d)
            place(0, g, v[:, :128])
            place(1, g, v[:, 128:])

        repeat(panels, 6, body)


class Wires:
    def __init__(self, place, sem):
        self.place, self.sem, self.used, self.waits = place, sem, 0, []

    def new(self, n=1):
        self.used += n
        assert self.used <= self.sem.shape[0], self.used
        return self.used - n

    def copy(self, k, src, dst, way):
        return pltpu.make_async_remote_copy(src_ref=src, dst_ref=dst, send_sem=self.sem.at[k], recv_sem=self.sem.at[k + 1],
                                            device_id=self.place.ids[way], device_id_type=MESH)

    def send(self, k, src, dst, way, cond=None):
        cp = self.copy(k, src, dst, way)
        when(cond, cp.start)
        self.waits.append((cond, cp))

    def land(self, k, dst, cond=None):
        when(cond, self.copy(k, dst, dst, "c").wait_recv)

    def drain(self):
        for cond, cp in self.waits:
            when(cond, cp.wait_send)


def edge_slots(order):
    slots, used, shared = {}, 0, {}
    for d, kids in sorted(spread(order).items()):
        for _, way in kids:
            if way in "xy" and order.index("z") < order.index(way):
                key = (way, d[1], d[2])
                if key not in shared:
                    shared[key] = used
                    used += 4
                slots[d, way] = (shared[key], 4)
            else:
                slots[d, way] = (used, 1)
                used += 1
    return slots, used


def beyond(p, way):
    return p.z < 3 if way == "z+" else p.z > 0 if way == "z-" else None


def reduce_events(p, w, order, own, half, bufs, ready, done):
    tree = spread(order)
    pair = {d: w.new(2) for d in tree}
    wire = {d: w.new(2) for d in tree}
    parent = {nd: (d, way) for d, t in tree.items() for nd, way in t}
    slots, _ = edge_slots(order)

    def buffer(up, way):
        first, n = slots[up, way]
        return bufs.at[first + p.z + up[0] if n > 1 else first]

    events = []
    far = sorted(tree, key=lambda d: (-hops(d), d))
    for d in far:
        def act(d=d):
            cond = p.there(d)

            def step():
                acc = own(d)
                ready(d)
                w.land(pair[d], half(d))
                add_rows(acc, half(d))
                for nd, way in tree[d]:
                    buf = buffer(d, way)

                    def take(buf=buf, nd=nd):
                        w.land(wire[nd], buf)
                        add_rows(acc, buf)
                    when(beyond(p, way), take)
            when(cond, step)
            if hops(d) == 0:
                done()
            else:
                up, way = parent[d]
                w.send(wire[d], own(d), buffer(up, way), BACK[way], cond)
        events.append(act)

    def share(give):
        for d in far:
            w.send(pair[d], give(d), half(d), "c", p.there(d))

    return events, share, far


def gather_events(p, w, order, first, at):
    tree = spread(order)
    pair = {d: w.new(2) for d in tree}
    wire = {d: w.new(2) for d in tree}
    events = []
    for d in sorted(tree, key=lambda d: (hops(d), d)):
        def act(d=d):
            cond = p.there(d)
            blk = at(d, p.c)
            if hops(d):
                w.land(wire[d], blk, cond)
                src = blk
            else:
                src = first
            for nd, way in tree[d]:
                w.send(wire[nd], src, blk, way, both(cond, beyond(p, way)))
            w.send(pair[d], src, blk, "c", cond)
        events.append(act)

    def finish():
        for d in tree:
            w.land(pair[d], at(d, 1 - p.c), p.there(d))

    return events, finish


def run_events(lists, order, extra=iter(()), every=8):
    assert sorted(order) == sorted(64 * g + i for g, acts in enumerate(lists) for i in range(len(acts)))
    for n, k in enumerate(order):
        if n % every == 0:
            next(extra, None)
        lists[k // 64][k % 64]()
    for _ in extra:
        pass


def group_span(table, mats):
    first, last = table[mats[0]], table[mats[-1]]
    units = last[3] + last[2] - first[3]
    return first[3], -(-units // 16) * 16, first[4], last[4] + last[1] * last[5] - first[4]


def units_to_panels(table, mats, units, flat, put):
    base, count = table[mats[0]][3], units.shape[0]
    for k in range(4):
        flat[pl.ds(k, count, stride=4), :] = units[:, 128 * k:128 * (k + 1)].astype(jnp.float32)
    for m in mats:
        rb, panels, n, first, _, padded, _ = table[m]
        n = 2 if rb % 16 else 1
        for g in range(0, panels, n):
            v = [flat[pl.ds(4 * (first - base) + g + k, rb, stride=panels), :] for k in range(n)]
            put(m, g, jnp.concatenate(v, axis=0).astype(jnp.bfloat16))


def panels_to_units(table, mats, take, flat, units):
    base, count = table[mats[0]][3], units.shape[0]
    used = 0
    for m in mats:
        rb, panels, n, first, _, padded, _ = table[m]
        many = 2 if rb % 16 else 1
        for g in range(0, panels, many):
            v = take(m, g, many)
            for k in range(many):
                flat[pl.ds(4 * (first - base) + g + k, rb, stride=panels), :] = v[k * rb:(k + 1) * rb]
        used = 4 * (first - base + n)
    if used < 4 * count:
        flat[used:4 * count, :] = jnp.zeros((4 * count - used, 128), jnp.float32)
    for k in range(4):
        units[:, 128 * k:128 * (k + 1)] = flat[pl.ds(k, count, stride=4), :].astype(jnp.bfloat16)


def encoder_steps(p, table, out, tok, pos, x, x2, tile, gains, biases, tab, fwd, fwd_out, wv, w_sem, fwd_sem, swapped, arrived):
    n1, att, n2, act, proj, prob, ow, m1, i1, m2, i2, slope = fwd

    def load(m):
        rows = pl.ds(table[m][4], table[m][1] * table[m][5])
        return pltpu.make_async_copy(out.at[:, :, :, :, rows], wv.at[:, :, :, :, rows], w_sem.at[m])

    def store(i):
        return pltpu.make_async_copy(fwd[i], fwd_out[i], fwd_sem.at[i])

    def keep(k):
        for i in ((0, 7, 8), (1, 4, 5), (2, 6, 9, 10), (3, 11))[k]:
            store(i).start()

    for f in swapped:
        f()
    x[...] = tok[...].reshape(256, DE).astype(jnp.float32) + lookup(pos, tab, slice(0, DE))
    same = tile_mask(tile)
    whole = wv.reshape(2, 16, wv.shape[-2], 128)
    block = block_fwd(Block(DE, HE, HDE, FFE, 0, table, 0), x, x2, whole, gains, biases, same, n1, proj, prob, att, ow, m1, i1, n2,
                      m2, i2, act, slope, lambda k: load(k).wait(), keep)
    next(block)
    yield
    for f in arrived[0]:
        f()
    load(0).start()
    load(1).start()
    yield
    for _ in range(4):
        next(block)
        yield
    for f in arrived[1]:
        f()
    load(2).start()
    yield
    next(block)
    yield
    for f in arrived[2]:
        f()
    load(3).start()
    yield
    for _ in block:
        pass
    yield
    for i in range(12):
        store(i).wait()


class Swap:
    def __init__(self, p, w, src, out, give, keep):
        self.p, self.w, self.src, self.out, self.give, self.keep = p, w, src, out, give, keep
        self.k, self.own = w.new(2), w.new()

    def local(self):
        return pltpu.make_async_copy(self.src.at[self.keep], self.out.at[self.p.x], self.w.sem.at[self.own])

    def start(self):
        self.w.send(self.k, self.src.at[self.give], self.out.at[self.p.x], "x")

    def finish(self):
        self.w.land(self.k, self.out.at[1 - self.p.x])
        self.local().wait()


def weights_kernel(table, groups, plan, parts, tok_in, pos_in, cot_in, tile, gains, biases, tab, *refs):
    n = len(groups)
    out, pos, cot, x2 = refs[:4]
    fwd_out, tok, x, fwd, wv, w_sem, fwd_sem = refs[4:16], refs[16], refs[17], refs[18:30], refs[30], refs[31], refs[32]
    rest = refs[33:]
    accs, halves, bufs, shards = (rest[i * n:(i + 1) * n] for i in range(4))
    flat, sem = rest[4 * n:]
    p = Place()
    p.greet(["c", "y", "x"])
    w = Wires(p, sem)
    swaps = [Swap(p, w, tok_in, tok, 1 - p.x, p.x), Swap(p, w, pos_in, pos, (ALL, 1 - p.x), (ALL, p.x)),
             Swap(p, w, cot_in, cot, 1 - p.x, p.x)]
    for s in swaps:
        s.start()
        s.local().start()
    lists, finishes = [], []
    for g, mats in enumerate(groups):
        u0, un, r0, rn = group_span(table, mats)
        acc, half, buf, shard = accs[g], halves[g], bufs[g], shards[g]
        own_sem = w.new()
        loads = {d: w.new() for d in spread(plan[0][g])}

        def own(d, acc=acc):
            return acc.at[p.at(d)[1:]]

        def other(d, half=half):
            return half.at[p.at(d)[1:]]

        def load(d, u0=u0, un=un, own=own, loads=loads):
            return pltpu.make_async_copy(parts.at[p.at(d)[1:] + (p.c, pl.ds(u0, un))], own(d), sem.at[loads[d]])

        def ready(d, load=load):
            load(d).wait()

        def done(mats=mats, acc=acc, shard=shard, r0=r0):
            def put(m, i, v):
                lo = table[m][4] - r0 + i * table[m][5]
                shard[lo:lo + v.shape[0], :] = v
            units_to_panels(table, mats, acc.at[p.z, p.y], flat, put)

        ev, share, far = reduce_events(p, w, plan[0][g], own, other, buf, ready, done)

        def begin(load=load, share=share, far=far, u0=u0, un=un):
            share(lambda d: parts.at[p.at(d)[1:] + (1 - p.c, pl.ds(u0, un))])
            for d in far:
                when(p.there(d), load(d).start)

        def at(d, core, r0=r0, rn=rn):
            t, z, y = p.at(d)
            return out.at[t, z, y, core, pl.ds(r0, rn)]

        def local(shard=shard, r0=r0, rn=rn, own_sem=own_sem):
            return pltpu.make_async_copy(shard, out.at[p.x, p.z, p.y, p.c, pl.ds(r0, rn)], sem.at[own_sem])

        ag, finish = gather_events(p, w, plan[1][g], shard, at)

        def send_first(act=ag[0], local=local):
            act()
            local().start()

        lists.append([begin] + ev + [send_first] + ag[1:])
        finishes += [finish, lambda local=local: local().wait()]
    steps = encoder_steps(p, table, out, tok, pos, x, x2, tile, gains, biases, tab, fwd, fwd_out, wv, w_sem, fwd_sem,
                          [s.finish for s in swaps[:2]], [finishes[2 * k:2 * k + 2] for k in range(3)])
    lists.append([partial(next, steps, None)] * 11)
    run_events(lists, plan[2])
    for f in finishes[6:] + [swaps[2].finish]:
        f()
    w.drain()


def spread_weights(parts, tokens, pos, cot, tile, gains, biases, table, rows, groups, plan, ident):
    spans = [group_span(table, m) for m in groups]
    bf16 = jnp.bfloat16
    S = jax.ShapeDtypeStruct
    V = pltpu.VMEM
    fwd = FWD_ACTS + FWD_KEPT
    enc_rows = table[4][4]
    scratch = [V(tokens.shape, tokens.dtype), V((256, DE), jnp.float32)] + [V(k, t) for k, t in fwd]
    scratch += [V((2, 4, 2, 2, enc_rows, 128), bf16), pltpu.SemaphoreType.DMA((4,)), pltpu.SemaphoreType.DMA((12,))]
    scratch += [V((4, 2, s[1], 512), bf16) for s in spans] * 2
    scratch += [V((edge_slots(o)[1], s[1], 512), bf16) for s, o in zip(spans, plan[0])]
    scratch += [V((s[3], 128), bf16) for s in spans]
    scratch += [V((4 * max(s[1] for s in spans), 128), jnp.float32),
                pltpu.SemaphoreType.DMA((len(groups) * (1 + 5 * 14 + 4 * 28) + 9,))]
    hbm = pl.BlockSpec(memory_space=pl.ANY)
    vmem = pl.BlockSpec(memory_space=pltpu.VMEM)
    return pl.pallas_call(
        partial(weights_kernel, table, groups, plan),
        out_shape=[S((2, 4, 2, 2, rows, 128), bf16), S((2, 3, 1, 128), pos.dtype), S(cot.shape, cot.dtype), S((256, DE), jnp.float32)]
        + [S(k, t) for k, t in fwd],
        in_specs=[hbm] * 4 + [vmem] * 4, out_specs=[hbm, vmem, hbm, vmem] + [hbm] * 12,
        scratch_shapes=scratch,
        compiler_params=pltpu.CompilerParams(collective_id=ident, has_side_effects=True, vmem_limit_bytes=63 << 20),
        name="spread_weights",
    )(parts, tokens, pos, cot, tile, gains, biases, jnp.asarray(position_table()))


def return_kernel(table, groups, plan, *refs):
    n = len(groups)
    kept_in, small_src, dec_in, dx_in, out, small_out, dec, dx = refs[:18], *refs[18:25]
    rest = refs[25:]
    kept, rest = rest[:18], rest[18:]
    acts, grads = kept[:9], kept[9:]
    sides, halves, bufs, units = (rest[i * n:(i + 1) * n] for i in range(4))
    flat, turned, mid, line, load_sem, sem = rest[4 * n:]

    def load(i):
        return pltpu.make_async_copy(kept_in[i], kept[i], load_sem.at[i])

    first = sorted(range(n), key=lambda g: plan[2].index(64 * g))
    for g in first:
        for m in groups[g]:
            load(m).start()
            load(9 + m).start()
    p = Place()
    p.greet(["c", "y", "x"])
    w = Wires(p, sem)
    swaps = [Swap(p, w, a, b, 1 - p.x, p.x) for a, b in ((dec_in, dec), (dx_in, dx))]
    for s in swaps:
        s.local().start()
    swaps[0].start()
    lists, finishes = [], []
    for g, mats in enumerate(groups):
        u0, un, r0, rn = group_span(table, mats)
        side, half, buf, unit = sides[g], halves[g], bufs[g], units[g]
        own_sem = w.new()

        def own(d, side=side):
            return side.at[(p.c,) + p.at(d)]

        def other(d, half=half):
            return half.at[p.at(d)]

        def done(mats=mats, side=side, unit=unit, r0=r0):
            mine = side.at[p.c, p.x, p.z, p.y]

            def take(m, i, many):
                lo = table[m][4] - r0 + i * table[m][5]
                return mine[lo:lo + many * table[m][5], :].astype(jnp.float32)
            panels_to_units(table, mats, take, flat, unit)

        ev, share, far = reduce_events(p, w, plan[0][g], own, other, buf, lambda d: None, done)

        def begin(mats=mats, side=side, share=share, r0=r0):
            for m in mats:
                lo, padded = table[m][4] - r0, table[m][5]

                def put(t, i, v, lo=lo, padded=padded):
                    v = v.reshape(4, 2, 2, v.shape[1], 128)
                    rows = pl.ds(pl.multiple_of(lo + i * padded, 16), v.shape[3])
                    side[0, t, :, :, rows, :] = v[:, :, 0]
                    side[1, t, :, :, rows, :] = v[:, :, 1]
                load(m).wait()
                load(9 + m).wait()
                grad_panels(table, m, acts[m], grads[m], turned, put)
            share(lambda d: side.at[(1 - p.c,) + p.at(d)])

        def at(d, core, u0=u0, un=un):
            _, z, y = p.at(d)
            return out.at[z, y, core, pl.ds(u0, un)]

        def local(unit=unit, u0=u0, un=un, own_sem=own_sem):
            return pltpu.make_async_copy(unit, out.at[p.z, p.y, p.c, pl.ds(u0, un)], sem.at[own_sem])

        ag, finish = gather_events(p, w, plan[1][g], unit, at)

        def send_first(act=ag[0], local=local):
            act()
            local().start()

        lists.append([begin] + ev + [send_first] + ag[1:])
        finishes += [finish, lambda local=local: local().wait()]
    last = max(plan[2].index(64 * g + len(spread(plan[0][g]))) for g in range(n))
    g, i = plan[2][last] // 64, plan[2][last] % 64
    act = lists[g][i]

    def with_swaps():
        act()
        swaps[1].start()

    lists[g][i] = with_swaps
    run_events(lists, plan[2], total_steps(p, w, small_src, small_out, mid, line))
    for f in finishes + [s.finish for s in swaps]:
        f()
    w.drain()


def total_steps(p, w, src, out, mid, line):
    k = [w.new(2) for _ in range(9)]
    now = src
    for i, way in enumerate(("c", "x", "y")):
        w.send(k[i], now, mid.at[i], way)
        yield
        w.land(k[i], mid.at[i])
        nxt = mid.at[3 + i] if i < 2 else line.at[p.z]
        nxt[...] = now[...] + mid[i]
        now = nxt
    for i in range(4):
        lo, hi = jnp.maximum(p.z - i, 0), jnp.minimum(p.z + i, 3)
        if i > 0:
            w.land(k[2 + i], line.at[lo], p.z >= i)
            w.land(k[5 + i], line.at[hi], p.z + i <= 3)
        if i < 3:
            w.send(k[3 + i], line.at[lo], line.at[lo], "z+", jnp.logical_and(p.z >= i, p.z < 3))
            w.send(k[6 + i], line.at[hi], line.at[hi], "z-", jnp.logical_and(p.z + i <= 3, p.z > 0))
            yield
    out[...] = (line[0] + line[1]) + (line[2] + line[3])


def return_grads(kept, small, dec, dx, table, total_units, groups, plan, ident):
    spans = [group_span(table, m) for m in groups]
    bf16 = jnp.bfloat16
    S = jax.ShapeDtypeStruct
    V = pltpu.VMEM
    scratch = [V(v.shape, v.dtype) for v in kept]
    scratch += [V((2, 2, 4, 2, s[3], 128), bf16) for s in spans]
    scratch += [V((2, 4, 2, s[3], 128), bf16) for s in spans]
    scratch += [V((edge_slots(o)[1], s[3], 128), bf16) for s, o in zip(spans, plan[0])]
    scratch += [V((s[1], 512), bf16) for s in spans]
    scratch += [V((4 * max(s[1] for s in spans), 128), jnp.float32), V((FFE, 256), bf16),
                V((5,) + small.shape, small.dtype), V((4,) + small.shape, small.dtype), pltpu.SemaphoreType.DMA((18,)),
                pltpu.SemaphoreType.DMA((len(groups) * (1 + 4 * 14 + 4 * 28) + 24,))]
    vmem = pl.BlockSpec(memory_space=pltpu.VMEM)
    hbm = pl.BlockSpec(memory_space=pl.ANY)
    return pl.pallas_call(
        partial(return_kernel, table, groups, plan),
        out_shape=(S((4, 2, 2, total_units, 512), bf16), S(small.shape, small.dtype), S(dec.shape, dec.dtype), S(dx.shape, dx.dtype)),
        in_specs=[hbm] * 18 + [vmem, hbm, hbm], out_specs=(hbm, vmem, hbm, hbm),
        scratch_shapes=scratch,
        compiler_params=pltpu.CompilerParams(collective_id=ident, has_side_effects=True, vmem_limit_bytes=63 << 20),
        name="return_grads",
    )(*kept, small, dec, dx)


STEP_ROWS = 432


def update_kernel(place, spread, master, first, second, total, gains, biases, norm_first, norm_second, *refs):
    passed, refs = refs[:2], refs[2:]
    new_master, new_first, new_second, new_norms, new_nf, new_ns = refs[:6]
    i = pl.program_id(0)

    @pl.when(i == 0)
    def _():
        for a, b in zip(passed, refs[6:8]):
            b[...] = a[...]
        for v, r in ((gains, slice(0, 2)), (biases, slice(2, 4))):
            new_norms[r, :], new_nf[r, :], new_ns[r, :] = adamw(v[...], total[r, :], norm_first[r, :], norm_second[r, :], 0.0, NORM_RATE)

    lane = lax.broadcasted_iota(jnp.int32, (16, 128), 1)
    row = lax.broadcasted_iota(jnp.int32, (16, 128), 0)
    for k in range(STEP_ROWS // 16):
        tiles, spot = [], jnp.full((16, 128), -1, jnp.int32)
        for j in range(16):
            at = place[i * STEP_ROWS + 16 * k + j]
            tile = jnp.minimum(at >> 4, spread.shape[0] // 16 - 1)
            tiles.append(spread[pl.ds(pl.multiple_of(tile * 16, 16), 16), :])
            spot = jnp.where(row == j, jnp.where(at < spread.shape[0], 16 * j + (at & 15), -1), spot)
        here = slice(16 * k, 16 * k + 16)
        pick = jnp.concatenate([jnp.where(lane == spot, 1.0, 0.0), jnp.where(lane + 128 == spot, 1.0, 0.0)], axis=1)
        grad = dot(pick.astype(jnp.bfloat16), jnp.concatenate(tiles, axis=0))
        new_master[here, :], new_first[here, :], new_second[here, :] = adamw(
            master[here, :], grad, first[here, :], second[here, :], WEIGHT_DECAY, LEARN_RATE)


def update(place, spread, master, first, second, total, gains, biases, norm_first, norm_second, passed):
    slots = master.shape[0]
    S = jax.ShapeDtypeStruct
    rows = pl.BlockSpec((STEP_ROWS, 512), lambda i, s: (i, 0))
    whole = lambda v: pl.BlockSpec(v.shape, lambda i, s: (0, 0), pipeline_mode=pl.Buffered(1))
    small = pl.BlockSpec(total.shape, lambda i, s: (0, 0))
    pair_of = pl.BlockSpec(gains.shape, lambda i, s: (0, 0))
    out = [S(master.shape, jnp.float32)] * 3 + [S(total.shape, jnp.float32)] * 3 + [S(v.shape, v.dtype) for v in passed]
    both = [pl.BlockSpec(v.shape, lambda i, s: (0, 0, 0), pipeline_mode=pl.Buffered(1)) for v in passed]
    return pl.pallas_call(
        update_kernel, out_shape=out,
        grid_spec=pltpu.PrefetchScalarGridSpec(
            num_scalar_prefetch=1, grid=(slots // STEP_ROWS,),
            in_specs=[whole(spread), rows, rows, rows, small, pair_of, pair_of, small, small] + both,
            out_specs=[rows] * 3 + [small] * 3 + both),
        compiler_params=pltpu.CompilerParams(vmem_limit_bytes=62 << 20), name="update",
    )(place, spread, master, first, second, total, gains, biases, norm_first, norm_second, *passed)


def place_kernel(place_s, master, out, wide, staged, sem):
    count = wide.shape[0] // 64 - 1

    def clear(i, _):
        wide[pl.ds(pl.multiple_of(i * 64, 64), 64), :] = jnp.zeros((64, 512), jnp.float32)
        return 0

    lax.fori_loop(0, count, clear, 0)

    def turn(i, _):
        for j in range(48):
            wide[pl.ds(place_s[i * 48 + j], 1), :] = master[pl.ds(i * 48 + j, 1), :]
        return 0

    lax.fori_loop(0, master.shape[0] // 48, turn, 0)
    parts = 4
    part = count // parts * 64

    def copy(k):
        rows = pl.ds(pl.multiple_of(k * part, 64), part)
        return pltpu.make_async_copy(staged.at[rows], out.at[rows], sem.at[k])

    for k in range(parts):
        def narrow(i, _):
            rows = pl.ds(pl.multiple_of(k * part + i * 64, 64), 64)
            staged[rows, :] = wide[rows, :].astype(jnp.bfloat16)
            return 0

        lax.fori_loop(0, part // 64, narrow, 0)
        copy(k).start()
    for k in range(parts):
        copy(k).wait()


def place_blocks(place, master, rows):
    return pl.pallas_call(
        place_kernel, out_shape=jax.ShapeDtypeStruct((rows, 512), jnp.bfloat16),
        grid_spec=pltpu.PrefetchScalarGridSpec(
            num_scalar_prefetch=1, grid=(1,),
            in_specs=[pl.BlockSpec(master.shape, lambda i, s: (0, 0), pipeline_mode=pl.Buffered(1))],
            out_specs=pl.BlockSpec(memory_space=pl.ANY),
            scratch_shapes=[pltpu.VMEM((rows + 64, 512), jnp.float32), pltpu.VMEM((rows, 512), jnp.bfloat16), pltpu.SemaphoreType.DMA((4,))]),
        compiler_params=pltpu.CompilerParams(vmem_limit_bytes=60 << 20), name="place_blocks",
    )(place, master)


def sequence_device(tokens_in, positions, segment_ids, owners, master, first_moment, second_moment, norm_gains,
                    norm_biases, norm_first, norm_second, cotangent):
    shapes = weight_shapes(2)
    table, _, rows = layout(shapes, 16)
    unit, used = own_units(owners, lax.axis_index("dp"), master.shape[0])
    place = jnp.where(used, unit_places(unit, table, 16), 16 * SHARD_UNITS)
    parts = place_blocks(place, master, 16 * SHARD_UNITS)
    full, pos, cot, x2, *fwd = spread_weights(parts.reshape(4, 2, 2, SHARD_UNITS, 512), tokens_in, positions[:, :, None],
                                              cotangent, segment_ids, norm_gains, norm_biases, table, rows, GROUPS, PLAN_OUT, 1)
    kept = chain(pos, segment_ids, norm_gains, norm_biases, cot.reshape(256, DD), full, x2, fwd[4:], table)
    decoded, dx0, norms = kept[:3]
    spread_out, norm_total, decoded, dx0 = return_grads([*fwd[:4], *kept[3:]], norms, decoded.reshape(2, 128, DD), dx0.reshape(2, 128, DE), table,
                                                        SHARD_UNITS, GROUPS, PLAN_BACK, 2)
    new_master, new_first, new_second, new_norms, norm_one_new, norm_two_new, decoded, dx0 = update(
        place, spread_out.reshape(16 * SHARD_UNITS, 512), master, first_moment, second_moment, norm_total, norm_gains, norm_biases, norm_first, norm_second,
        (decoded, dx0))
    return (decoded, dx0, new_master, new_first, new_second, new_norms, norm_one_new, norm_two_new)


def solution(mesh):
    step = sequence_device if (mesh.shape["dp"], mesh.shape["tensor"]) == (16, 2) else per_device
    return jax.shard_map(
        step,
        mesh=mesh,
        in_specs=(
            P(None, ("dp", "tensor"), None),
            P(None, None, ("dp", "tensor")),
            P(None, "dp", None),
            P(),
            P("dp", "tensor"),
            P("dp", "tensor"),
            P("dp", "tensor"),
            P(),
            P(),
            P(),
            P(),
            P(None, ("dp", "tensor"), None),
        ),
        out_specs=(
            P(None, ("dp", "tensor"), None),
            P(None, ("dp", "tensor"), None),
            P("dp", "tensor"),
            P("dp", "tensor"),
            P("dp", "tensor"),
            P(),
            P(),
            P(),
        ),
        check_vma=False,
    )
```
